32 devices in a mesh: dp: 8 (over z, x), blk: 4 (over y, core).
Axes of the slice: x: 2, y: 2, z: 4, core: 2. Of those that a mesh axis runs over, the one named last changes fastest.
Arguments:
- inputs: bfloat16 [16, 1024, 512], P('dp', 'blk'), may hold values from -16 to 16
- w_query: bfloat16 [512, 512], replicated, may hold values from -0.03125 to 0.03125
- w_key: bfloat16 [512, 512], replicated, may hold values from -0.25 to 0.25
- w_value: bfloat16 [512, 512], replicated, may hold values from -0.25 to 0.25
- w_out: bfloat16 [512, 512], replicated, may hold values from -4 to 4
- w_in: bfloat16 [512, 2048], replicated, may hold values from -0.25 to 0.25
- w_back: bfloat16 [2048, 512], replicated, may hold values from -0.125 to 0.125
- norm1_gain: float32 [512], replicated, may hold values from 0.1 to 1.9
- norm2_gain: float32 [512], replicated, may hold values from 0.1 to 1.9
- final_gain: float32 [512], replicated, may hold values from 0.1 to 1.9
- bias_table: float32 [32, 8], replicated, may hold values from -4 to 4
- bucket_table: int32 [2047], replicated, may hold values from 0 to 31
- prefix_len: int32 [16], P('dp'), may hold values from 5 to 40
- pad_len: int32 [16], P('dp'), may hold values from 0 to 255
- pooled_grad: float32 [16, 512], P('dp'), may hold values from -8 to 8
Outputs:
- pooled: float32 [16, 512], P('dp')
- input_grad: bfloat16 [16, 1024, 512], P('dp', 'blk')
- query_grad: float32 [512, 512], replicated
- key_grad: float32 [512, 512], replicated
- value_grad: float32 [512, 512], replicated
- out_grad: float32 [512, 512], replicated
- in_grad: float32 [512, 2048], replicated
- back_grad: float32 [2048, 512], replicated
- norm1_grad: float32 [512], replicated
- norm2_grad: float32 [512], replicated
- final_grad: float32 [512], replicated
- bias_grad: float32 [32, 8], replicated
The draws below stay inside these ranges and needn't reach their ends.
Inputs may be any that keep to these rules, and one draw needn't show every extreme that they name: `bucket_table`: entry r is the bucket of the offset r - 1023, key position minus query position.
All inputs are finite; a program needn't handle non-finite values.
Results may differ from the reference program's by a relative error of at most 0.03.
Values may be sent and summed in bfloat16 or wider, within the bound.
No kernel may reach another device: no remote copies, remote signals or barrier semaphores. Data moves between devices by JAX's collectives and lax.ppermute only.
A program may use at most 192 MiB of HBM per device.

```python
import math
import jax
import jax.numpy as jnp
from jax import lax

D = 512
HEADS = 8
HEAD_DIM = 64
FF = 2048
BUCKETS = 32
LENGTH = 1024
DOCUMENTS = 16


def draw_inputs(key, part):
    common = jax.random.normal(jax.random.fold_in(key, 11), (DOCUMENTS, 1, D), jnp.float32)
    place = jnp.arange(LENGTH, dtype=jnp.float32) / (LENGTH - 1)
    noise = jax.random.normal(jax.random.fold_in(key, 12), (DOCUMENTS, LENGTH, D), jnp.float32)
    weighting = 0.3 * 10.0 ** place
    result = noise + weighting[None, :, None] * common
    return jnp.clip(result, -16.0, 16.0).astype(jnp.bfloat16)


def place_ends(values, own_key, least, top_value):
    dims = values.shape
    spot = [jax.random.randint(jax.random.fold_in(own_key, axis), (), 0, dims[axis]) for axis in range(len(dims))]
    values = values.at[tuple(spot)].set(least)
    longest = dims.index(max(dims))
    spot[longest] = (spot[longest] + 1) % dims[longest]
    return values.at[tuple(spot)].set(top_value)


def with_spikes(array, stream_key, source, target, blocks, factor):
    def block_of(position):
        return (jnp.arange(array.shape[position]) // (array.shape[position] // blocks)).reshape((-1,) + (1,) * (array.ndim - 1 - position))

    first = jax.random.permutation(stream_key, blocks)[block_of(target)]
    far = (block_of(target) + blocks // 2) % blocks
    return jnp.where((block_of(source) == first) | (block_of(source) == far), factor * array, array)


def levels(rng, extent, shards, least, high):
    def one(axis_at, parts):
        heights = jax.random.uniform(jax.random.fold_in(jax.random.fold_in(rng, 6), axis_at), (parts,), jnp.float32, least / len(shards), high / len(shards))
        return jnp.repeat(jnp.exp(heights), extent[axis_at] // parts).reshape((-1,) + (1,) * (len(extent) - axis_at - 1))

    factor_of = one(*shards[0])
    for cut in shards[1:]:
        factor_of = factor_of * one(*cut)
    return factor_of


def centred(key, shape, deviation, limit, shards=(), kind=jnp.bfloat16):
    values = deviation * jax.random.normal(key, shape, jnp.float32)
    if shards:
        values = values * levels(key, shape, shards, -0.22, 0.18)
    return jnp.clip(values, -limit, limit).astype(kind)


def bell_draw_with(key, dims, spread, reach, shards, heavy, held_as=jnp.bfloat16):
    values = spread * jax.random.normal(key, dims, jnp.float32)
    if shards:
        values = values * levels(key, dims, shards, -0.22, 0.18)
    return jnp.clip(with_spikes(values, jax.random.fold_in(key, 3), *heavy), -reach, reach).astype(held_as)


def setup_inputs(seed: int = 0) -> dict:
    splits = jax.random.split(jax.random.key(seed), 16)
    return {
        "inputs": draw_inputs(jax.random.fold_in(splits[15], 71), 0),
        "w_query": centred(splits[1], (D, D), (D * HEAD_DIM) ** -0.5, 0.03125),
        "w_key": centred(splits[2], (D, D), D ** -0.5, 0.25),
        "w_value": centred(splits[3], (D, D), D ** -0.5, 0.25),
        "w_out": centred(splits[4], (D, D), (max(D // 256, 1)) ** -0.5, 4.0),
        "w_in": centred(splits[5], (D, FF), D ** -0.5, 0.25),
        "w_back": centred(splits[6], (FF, D), FF ** -0.5, 0.125),
        "norm1_gain": jnp.clip(1.0 + 0.18 * jax.random.normal(splits[7], (D,), jnp.float32), 0.1, 1.9),
        "norm2_gain": jnp.clip(1.0 + 0.18 * jax.random.normal(splits[8], (D,), jnp.float32), 0.1, 1.9),
        "final_gain": jnp.clip(1.0 + 0.18 * jax.random.normal(splits[9], (D,), jnp.float32), 0.1, 1.9),
        "bias_table": centred(splits[10], (BUCKETS, HEADS), 1.0, 4.0, (), jnp.float32),
        "bucket_table": place_ends(jax.random.randint(splits[11], (2 * LENGTH - 1,), 0, BUCKETS), jax.random.fold_in(splits[11], 1), 0, BUCKETS - 1).astype(jnp.int32),
        "prefix_len": place_ends(jax.random.randint(splits[12], (DOCUMENTS,), 5, 41), jax.random.fold_in(splits[12], 1), 5, 40).astype(jnp.int32),
        "pad_len": place_ends(jax.random.randint(splits[13], (DOCUMENTS,), 0, LENGTH // 4), jax.random.fold_in(splits[13], 1), 0, (LENGTH // 4) - 1).astype(jnp.int32),
        "pooled_grad": bell_draw_with(splits[14], (DOCUMENTS, D), 1.0, 8.0, ((0, 8),), (0, 1, 8, 2.0), jnp.float32),
    }


@jax.custom_vjp
def low(v):
    return lax.optimization_barrier(v.astype(jnp.bfloat16)).astype(jnp.float32)

@jax.custom_vjp
def low_back(v):
    return v

def low_keep(v):
    return (low(v), None)

def low_pass(kept, grad):
    return (grad,)

def back_keep(v):
    return (v, None)

def back_low(kept, grad):
    return (low(grad),)
low.defvjp(low_keep, low_pass)
low_back.defvjp(back_keep, back_low)
EPS = 1e-06
NEG = -1000000000.0
HIGH = lax.Precision.HIGHEST

def rms_norm(values, gain):
    return values * lax.rsqrt(lax.optimization_barrier(jnp.mean(values * values, axis=-1, keepdims=True)) + EPS) * gain

def attend_block(query_block, first_row, keys, values, offset_bias, key_live):
    row_count = query_block.shape[0]
    scores = jnp.einsum('ihe,jhe->hij', query_block, keys, precision=HIGH)
    places = jnp.arange(LENGTH, dtype=jnp.int32)
    relative = places[None, :] - (first_row + jnp.arange(row_count, dtype=jnp.int32))[:, None] + (LENGTH - 1)
    scores = scores + jnp.take(offset_bias, relative, axis=1)
    scores = jnp.where(key_live[None, None, :], scores, NEG)
    scores = low_back(scores)
    softmax_p = jax.nn.softmax(scores, axis=-1)
    return jnp.einsum('hij,jhe->ihe', low(softmax_p), values, precision=HIGH)

def document(params, tokens, prefix, padding, bucket_table):
    w_query, w_key, w_value, w_out, w_in, w_back, gain_one, gain_two, gain_end, bias_table = params
    hidden = low(rms_norm(tokens, gain_one))
    query = low(low_back(jnp.dot(hidden, w_query, precision=HIGH)))
    keys = low(low_back(jnp.dot(hidden, w_key, precision=HIGH)))
    values = low(low_back(jnp.dot(hidden, w_value, precision=HIGH)))
    offset_bias = bias_table[bucket_table].T
    places = jnp.arange(LENGTH, dtype=jnp.int32)
    key_live = places < LENGTH - padding
    span_rows = math.gcd(LENGTH, 512)
    pieces = LENGTH // span_rows
    query_blocks = query.reshape(pieces, span_rows, HEADS, HEAD_DIM)
    starts = jnp.arange(pieces, dtype=jnp.int32) * span_rows
    key_heads = keys.reshape(LENGTH, HEADS, HEAD_DIM)
    value_heads = values.reshape(LENGTH, HEADS, HEAD_DIM)
    stepper = jax.checkpoint(attend_block)
    attended = lax.map(lambda member: stepper(member[0], member[1], key_heads, value_heads, offset_bias, key_live), (query_blocks, starts))
    attended = low(low_back(attended.reshape(LENGTH, D)))
    mixed = tokens + low_back(jnp.dot(attended, w_out, precision=HIGH))
    inner = low(rms_norm(mixed, gain_two))
    lifted = jnp.dot(inner, w_in, precision=HIGH)
    active = low(low_back(jnp.where(lifted > 0, lifted, 0.0)))
    result = mixed + low_back(jnp.dot(active, w_back, precision=HIGH))
    final = rms_norm(result, gain_end)
    live = (places >= prefix) & (places < LENGTH - padding)
    summed = lax.optimization_barrier(jnp.sum(jnp.where(live[:, None], final, 0.0), axis=0))
    return summed / (LENGTH - padding - prefix).astype(jnp.float32)

def reference(inputs, w_query, w_key, w_value, w_out, w_in, w_back, norm1_gain, norm2_gain, final_gain, bias_table, bucket_table, prefix_len, pad_len, pooled_grad):
    params = (w_query.astype(jnp.float32), w_key.astype(jnp.float32), w_value.astype(jnp.float32), w_out.astype(jnp.float32), w_in.astype(jnp.float32), w_back.astype(jnp.float32), norm1_gain, norm2_gain, final_gain, bias_table)

    def step(running, member):
        tokens, prefix, padding, cotangent = member
        pooled_row, pull = jax.vjp(lambda weights, rows_in: document(weights, rows_in, prefix, padding, bucket_table), params, tokens.astype(jnp.float32))
        grad_params, grad_tokens = pull(cotangent)
        running = jax.tree.map(lambda left, right: left + right, running, grad_params)
        return (running, (pooled_row, grad_tokens.astype(jnp.bfloat16)))
    zeros = jax.tree.map(jnp.zeros_like, params)
    totals, (pooled, input_grad) = lax.scan(step, zeros, (inputs, prefix_len, pad_len, pooled_grad))
    return (pooled, input_grad, totals[0], totals[1], totals[2], totals[3], totals[4], totals[5], totals[6], totals[7], totals[8], totals[9])
```

```python
import jax, jax.numpy as jnp
from jax import lax
from jax.experimental import pallas as pl
from jax.experimental.pallas import tpu as pltpu
from jax.sharding import PartitionSpec as P

F32, BF16 = jnp.float32, jnp.bfloat16
NEG = -1000000000.0
NT = (((1,), (1,)), ((), ()))
TN = (((0,), (0,)), ((), ()))
NN = (((1,), (0,)), ((), ()))

def dot(a, b, dims=NN):
    return lax.dot_general(a, b, dims, preferred_element_type=F32)

def skew(row, width, dtype=F32):
    return pltpu.roll(jnp.broadcast_to(row, (128, width)), width - 127, 1, stride=1, stride_axis=0)

def fwd_kernel(info, ql, qr, kl, kr, vl, vr, table, out, expo, inv, bias, scores):
    limit = info[0]
    lane = lax.broadcasted_iota(jnp.int32, (1, 128), 1)
    kref = [(kl, 0), (kl, 256), (kr, 0), (kr, 256)]
    vref = [(vl, 0), (vl, 256), (vr, 0), (vr, 256)]
    starts = [info[1 + b] for b in range(4)]
    parts = [[], []]
    for head in range(2):
        mine = (lane < 64) if head == 0 else (lane >= 64)
        spare = lane == (64 if head == 0 else 0)
        bias[...] = skew(table[head : head + 1, :], bias.shape[1])
        keys, vals = [], []
        for b in range(4):
            ref, at = kref[b]
            place = starts[b] + lax.broadcasted_iota(jnp.int32, (256, 1), 0)
            gate = jnp.where(place < limit, 0.0, NEG)
            edge = jnp.where(spare, gate, 0.0)
            keys.append(jnp.where(mine, ref[at : at + 256, :].astype(F32), edge).astype(BF16))
            ref, at = vref[b]
            vals.append(jnp.where(mine, ref[at : at + 256, :].astype(F32), jnp.where(spare, 1.0, 0.0)).astype(BF16))
        for chunk in range(2):
            q = (ql, qr)[chunk][...].astype(F32)
            q = jnp.where(mine, q, jnp.where(spare, 1.0, 0.0)).astype(BF16)
            begin = starts[2 * chunk]
            peak = None
            for b in range(4):
                s = dot(q, keys[b], NT)
                at = starts[b] - begin + 896
                lo = bias[:, pl.ds(pl.multiple_of(at, 128), 256)]
                hi = bias[:, pl.ds(pl.multiple_of(at - 128, 128), 256)]
                s = s + jnp.concatenate([lo, hi], axis=0)
                scores[:, b * 256 : (b + 1) * 256] = s
                top = jnp.maximum(s[:, :128], s[:, 128:])
                peak = top if peak is None else jnp.maximum(peak, top)
            peak = jnp.max(peak, axis=1, keepdims=True)
            acc = None
            for b in range(4):
                e = jnp.exp(scores[:, b * 256 : (b + 1) * 256] - peak).astype(BF16)
                expo[head, chunk * 256 : (chunk + 1) * 256, b * 256 : (b + 1) * 256] = e
                part = dot(e, vals[b])
                acc = part if acc is None else acc + part
            total = acc[:, 64:65] if head == 0 else acc[:, 0:1]
            parts[chunk].append((acc, 1.0 / total))
    for chunk in range(2):
        (a0, i0), (a1, i1) = parts[chunk]
        scale = jnp.where(lane < 64, i0, i1)
        rows = slice(chunk * 256, (chunk + 1) * 256)
        out[rows, :] = (jnp.where(lane < 64, a0, a1) * scale).astype(BF16)
        inv[rows, :] = scale

def attention(info, ql, qr, kl, kr, vl, vr, table):
    d = ql.shape[1]
    pairs = d // 128
    col = lambda rows: pl.BlockSpec((rows, 128), lambda g: (0, g))
    return pl.pallas_call(
        fwd_kernel,
        grid=(pairs,),
        in_specs=[pl.BlockSpec(memory_space=pltpu.SMEM), col(256), col(256), col(512), col(512), col(512), col(512),
                  pl.BlockSpec((None, 2, 2048), lambda g: (g, 0, 0))],
        out_specs=[col(512), pl.BlockSpec((2, 512, 1024), lambda g: (g, 0, 0)), col(512)],
        out_shape=[jax.ShapeDtypeStruct((512, d), BF16), jax.ShapeDtypeStruct((2 * pairs, 512, 1024), BF16),
                   jax.ShapeDtypeStruct((512, d), F32)],
        scratch_shapes=[pltpu.VMEM((128, 2048), F32), pltpu.VMEM((256, 1024), F32)],
        name="attn_fwd",
    )(info, ql, qr, kl, kr, vl, vr, table)

def bwd_kernel(info, ql, qr, kl, kr, vl, vr, gout, out, inv, expo, dq, dk, dv, diag, acc, tmp):
    lane = lax.broadcasted_iota(jnp.int32, (1, 128), 1)
    kref = [(kl, 0), (kl, 256), (kr, 0), (kr, 256)]
    vref = [(vl, 0), (vl, 256), (vr, 0), (vr, 256)]
    starts = [info[1 + b] for b in range(4)]
    scaled = gout[...].astype(F32) * inv[...]
    prod = scaled * out[...].astype(F32)
    gkeys = [None] * 4
    gvals = [None] * 4
    dqs = [None, None]
    for head in range(2):
        mine = (lane < 64) if head == 0 else (lane >= 64)
        base = 64 if head == 0 else 0
        delta = jnp.sum(jnp.where(mine, prod, 0.0), axis=1, keepdims=True)
        high = delta.astype(BF16).astype(F32)
        gaug = jnp.where(mine, scaled, jnp.where(lane == base, high, jnp.where(lane == base + 1, delta - high, 0.0))).astype(BF16)
        gplain = jnp.where(mine, scaled, 0.0).astype(BF16)
        minus = jnp.where((lane == base) | (lane == base + 1), -1.0, 0.0)
        acc[...] = jnp.zeros_like(acc)
        vals, keys = [], []
        for b in range(4):
            ref, at = vref[b]
            vals.append(jnp.where(mine, ref[at : at + 256, :].astype(F32), minus).astype(BF16))
            ref, at = kref[b]
            keys.append(jnp.where(mine, ref[at : at + 256, :].astype(F32), 0.0).astype(BF16))
        for chunk in range(2):
            rows = slice(chunk * 256, (chunk + 1) * 256)
            q = jnp.where(mine, (ql, qr)[chunk][...].astype(F32), 0.0).astype(BF16)
            begin = starts[2 * chunk]
            for b in range(4):
                e = expo[head, rows, b * 256 : (b + 1) * 256]
                ds = dot(gaug[rows], vals[b], NT) * e.astype(F32)
                at = starts[b] - begin + 896
                lo = pl.ds(pl.multiple_of(at, 128), 256)
                hi = pl.ds(pl.multiple_of(at - 128, 128), 256)
                acc[:, lo] += ds[:128]
                acc[:, hi] += ds[128:]
                ds = ds.astype(BF16)
                part = dot(ds, keys[b])
                dqs[chunk] = part if dqs[chunk] is None else dqs[chunk] + part
                part = dot(q, ds, TN)
                gkeys[b] = part if gkeys[b] is None else gkeys[b] + part
                part = dot(gplain[rows], e, TN)
                gvals[b] = part if gvals[b] is None else gvals[b] + part
        rest = acc[...]
        n = 64
        while n >= 8:
            rest = rest[:n] + pltpu.roll(rest[n:], 2048 - n, 1)
            n //= 2
        line = rest[7:8]
        for r in range(6, -1, -1):
            line = rest[r : r + 1] + pltpu.roll(line, 2047, 1)
        diag[head : head + 1, :] = pltpu.roll(line, 127, 1)
    for chunk in range(2):
        dq[chunk * 256 : (chunk + 1) * 256, :] = dqs[chunk].astype(BF16)
    for b in range(4):
        dk[b * 256 : (b + 1) * 256, :] = gkeys[b].T.astype(BF16)
        dv[b * 256 : (b + 1) * 256, :] = gvals[b].T.astype(BF16)

def attention_grads(info, ql, qr, kl, kr, vl, vr, gout, out, inv, expo):
    d = ql.shape[1]
    pairs = d // 128
    col = lambda rows: pl.BlockSpec((rows, 128), lambda g: (0, g))
    return pl.pallas_call(
        bwd_kernel,
        grid=(pairs,),
        in_specs=[pl.BlockSpec(memory_space=pltpu.SMEM), col(256), col(256), col(512), col(512), col(512), col(512),
                  col(512), col(512), col(512), pl.BlockSpec((2, 512, 1024), lambda g: (g, 0, 0))],
        out_specs=[col(512), col(1024), col(1024), pl.BlockSpec((None, 2, 2048), lambda g: (g, 0, 0))],
        out_shape=[jax.ShapeDtypeStruct((512, d), BF16), jax.ShapeDtypeStruct((1024, d), BF16),
                   jax.ShapeDtypeStruct((1024, d), BF16), jax.ShapeDtypeStruct((pairs, 2, 2048), F32)],
        scratch_shapes=[pltpu.VMEM((128, 2048), F32), pltpu.VMEM((8, 128), F32)],
        name="attn_bwd",
    )(info, ql, qr, kl, kr, vl, vr, gout, out, inv, expo)

BUCKETS = 32
EPS = 1e-06

def rms_scale(values):
    return lax.rsqrt(jnp.mean(values * values, axis=-1, keepdims=True) + EPS)

def norm_back(grad_out, values, scale, gain):
    weighted = grad_out * gain
    inner = jnp.mean(weighted * values, axis=-1, keepdims=True)
    grad_in = scale * weighted - scale * scale * scale * values * inner
    return grad_in, jnp.sum(grad_out * values * scale, axis=0)

def exchange(value, axis, bit):
    size = lax.axis_size(axis)
    return lax.ppermute(value, axis, [(i, i ^ bit) for i in range(size)])

def side(axis, bit):
    return (lax.axis_index(axis) // bit) % 2

def reduce_halves(value, steps):
    for axis, bit in steps:
        half = value.shape[0] // 2
        mine = side(axis, bit)
        keep = lax.dynamic_slice_in_dim(value, mine * half, half, 0)
        send = lax.dynamic_slice_in_dim(value, (1 - mine) * half, half, 0)
        value = (keep.astype(F32) + exchange(send, axis, bit).astype(F32)).astype(BF16)
    return value

def gather_halves(value, steps):
    for axis, bit in reversed(steps):
        other = exchange(value, axis, bit)
        mine = side(axis, bit)
        value = jnp.where(mine == 0, jnp.concatenate([value, other]), jnp.concatenate([other, value]))
    return value

def plans():
    bits = [("dp", 1 << b) for b in range(lax.axis_size("dp").bit_length() - 1)]
    near, rest = bits[0], bits[1:]
    y = ("blk", 2)
    return [[y, near] + rest, [near] + rest + [y], rest + [y, near]]

def reduce_all(value, cuts):
    core = [("blk", 1)]
    value = reduce_halves(value, core)
    at, pieces = 0, []
    for rows, steps in zip(cuts, plans()):
        if rows:
            piece = lax.slice_in_dim(value, at, at + rows, axis=0)
            pieces.append(gather_halves(reduce_halves(piece, steps), steps))
        at += rows
    return gather_halves(jnp.concatenate(pieces), core)

def reduce_small(value):
    for axis in ("blk", "dp"):
        for b in range(lax.axis_size(axis).bit_length() - 1):
            value = value + exchange(value, axis, 1 << b)
    return value

def mm(a, b, dims=NN):
    return lax.dot_general(a, b, dims, preferred_element_type=F32)

def local(inputs, w_query, w_key, w_value, w_out, w_in, w_back, norm1_gain, norm2_gain, final_gain, bias_table, bucket_table, prefix_len, pad_len, pooled_grad):
    rows, width = inputs.shape[1:]
    place = lax.axis_index("blk")
    length = rows * lax.axis_size("blk")
    doc, core = place // 2, place % 2
    block = [doc * 2 + core, doc * 2 + 1 - core, (1 - doc) * 2 + core, (1 - doc) * 2 + 1 - core]
    near = lax.dynamic_index_in_dim(inputs, doc, 0, keepdims=False)
    far = exchange(lax.dynamic_index_in_dim(inputs, 1 - doc, 0, keepdims=False), "blk", 2)
    near_other = exchange(near, "blk", 1)
    far_other = exchange(far, "blk", 1)
    limit = length - lax.dynamic_index_in_dim(pad_len, doc, 0, keepdims=False)
    prefix = lax.dynamic_index_in_dim(prefix_len, doc, 0, keepdims=False)
    count = (limit - prefix).astype(F32)
    cotangent = lax.dynamic_index_in_dim(pooled_grad, doc, 0, keepdims=True)
    info = jnp.stack([limit] + [b * rows for b in block]).astype(jnp.int32)
    picker = (jnp.arange(BUCKETS, dtype=jnp.int32)[:, None] == bucket_table[None, :]).astype(F32)
    picker = jnp.pad(picker, ((0, 0), (0, 1)))
    table = lax.dot_general(bias_table, picker, TN, precision=lax.Precision.HIGHEST)
    table = table.reshape(-1, 2, picker.shape[1])

    def front(raw, own):
        tokens = raw.astype(F32)
        scale = rms_scale(tokens)
        hidden = (tokens * scale * norm1_gain).astype(BF16)
        return hidden, mm(hidden[:own], w_query).astype(BF16), mm(hidden, w_key).astype(BF16), mm(hidden, w_value).astype(BF16)

    hid_l, q_l, k_l, v_l = front(jnp.concatenate([near, near_other]), rows)
    hid_r, q_r, k_r, v_r = front(jnp.concatenate([far, far_other]), rows)
    attended, expo, inverse = attention(info, q_l, q_r, k_l, k_r, v_l, v_r, table)

    raw = jnp.concatenate([near, far])
    tokens = raw.astype(F32)
    mixed = tokens + mm(attended, w_out)
    scale_two = rms_scale(mixed)
    inner = (mixed * scale_two * norm2_gain).astype(BF16)
    lifted = mm(inner, w_in)
    active = jnp.maximum(lifted, 0.0).astype(BF16)
    result = mixed + mm(active, w_back)
    scale_end = rms_scale(result)
    spots = jnp.concatenate([block[0] * rows + jnp.arange(rows), block[2] * rows + jnp.arange(rows)])
    live = ((spots >= prefix) & (spots < limit)).astype(F32)[:, None]
    pool_part = jnp.sum(result * scale_end * final_gain * live, axis=0, keepdims=True)
    pool_mine = (pool_part + exchange(pool_part, "blk", 1)) / count
    pool_other = exchange(pool_mine, "blk", 2)
    pooled = jnp.where(doc == 0, jnp.concatenate([pool_mine, pool_other]), jnp.concatenate([pool_other, pool_mine]))

    grad_final = live * (cotangent / count)
    grad_result, grad_end = norm_back(grad_final, result, scale_end, final_gain)
    grad_branch = grad_result.astype(BF16)
    grad_back_w = mm(active, grad_branch, TN)
    grad_lifted = jnp.where(active > 0, mm(grad_branch, w_back, NT).astype(BF16), jnp.zeros_like(active))
    grad_in_t = mm(grad_lifted, inner, TN)
    big = reduce_all(jnp.concatenate([grad_back_w.astype(BF16), grad_in_t.astype(BF16)]), (768, 768, 512))
    grad_inner = mm(grad_lifted, w_in, NT)
    grad_through, grad_two = norm_back(grad_inner, mixed, scale_two, norm2_gain)
    grad_mixed = grad_result + grad_through
    grad_att_out = grad_mixed.astype(BF16)
    grad_out_w = mm(attended, grad_att_out, TN)
    grad_attended = mm(grad_att_out, w_out, NT).astype(BF16)
    dq, dk, dv, offsets = attention_grads(info, q_l, q_r, k_l, k_r, v_l, v_r, grad_attended, attended, inverse, expo)
    grad_bias = lax.dot_general(picker, offsets.reshape(-1, picker.shape[1]), NT, precision=lax.Precision.HIGHEST)
    own = jnp.concatenate([hid_l[:rows], hid_r[:rows]])
    everyone = jnp.concatenate([hid_l, hid_r])
    grad_q_w = mm(own, dq, TN)
    grad_k_w = mm(everyone, dk, TN)
    grad_v_w = mm(everyone, dv, TN)
    rest = reduce_all(jnp.concatenate([g.astype(BF16) for g in (grad_out_w, grad_q_w, grad_k_w, grad_v_w)]), (384, 384, 256))
    through_kv = mm(dk, w_key, NT) + mm(dv, w_value, NT)
    through_kv = through_kv.reshape(2, 2, rows, width)
    sent = exchange(through_kv[:, 1].reshape(2 * rows, width).astype(BF16), "blk", 1).astype(F32)
    grad_hidden = mm(dq, w_query, NT) + through_kv[:, 0].reshape(2 * rows, width) + sent
    grad_norm, grad_one = norm_back(grad_hidden, tokens, rms_scale(tokens), norm1_gain)
    input_grad = (grad_mixed + grad_norm).astype(BF16)
    away = exchange(input_grad[rows:], "blk", 2)
    home = input_grad[:rows]
    input_grad = jnp.where(doc == 0, jnp.stack([home, away]), jnp.stack([away, home]))
    small = jnp.concatenate([jnp.stack([grad_one, grad_two, grad_end]), jnp.pad(grad_bias.reshape(1, -1), ((0, 0), (0, width - grad_bias.size)))])
    small = reduce_small(small)
    split = w_in.shape[1]
    grads = [rest[i * width : (i + 1) * width].astype(F32) for i in range(4)]
    return (
        pooled,
        input_grad,
        grads[1],
        grads[2],
        grads[3],
        grads[0],
        big[split:].astype(F32).T,
        big[:split].astype(F32),
        small[0],
        small[1],
        small[2],
        small[3, : grad_bias.size].reshape(grad_bias.shape),
    )

def solution(mesh):
    data = P("dp", "blk", None)
    placed = (data,) + (P(),) * 11 + (P("dp"), P("dp"), P("dp", None))
    return jax.shard_map(local, mesh=mesh, in_specs=placed, out_specs=(P("dp", None), data) + (P(),) * 10, check_vma=False)
```

```python
import jax, jax.numpy as jnp
from jax import lax
from jax.experimental import pallas as pl
from jax.experimental.pallas import tpu as pltpu
from jax.sharding import PartitionSpec as P

F32, BF16 = jnp.float32, jnp.bfloat16
NEG = -1000000000.0
NT = (((1,), (1,)), ((), ()))
TN = (((0,), (0,)), ((), ()))
NN = (((1,), (0,)), ((), ()))

def dot(a, b, dims=NN):
    return lax.dot_general(a, b, dims, preferred_element_type=F32)

def skew(row, width, dtype=F32):
    return pltpu.roll(jnp.broadcast_to(row, (128, width)), width - 127, 1, stride=1, stride_axis=0)

def fwd_kernel(info, ql, qr, kl, kr, vl, vr, table, out, expo, inv, bias, scores):
    limit = info[0]
    lane = lax.broadcasted_iota(jnp.int32, (1, 128), 1)
    kref = [(kl, 0), (kl, 256), (kr, 0), (kr, 256)]
    vref = [(vl, 0), (vl, 256), (vr, 0), (vr, 256)]
    starts = [info[1 + b] for b in range(4)]
    parts = [[], []]
    for head in range(2):
        mine = (lane < 64) if head == 0 else (lane >= 64)
        spare = lane == (64 if head == 0 else 0)
        bias[...] = skew(table[head : head + 1, :], bias.shape[1])
        keys, vals = [], []
        for b in range(4):
            ref, at = kref[b]
            place = starts[b] + lax.broadcasted_iota(jnp.int32, (256, 1), 0)
            gate = jnp.where(place < limit, 0.0, NEG)
            edge = jnp.where(spare, gate, 0.0)
            keys.append(jnp.where(mine, ref[at : at + 256, :].astype(F32), edge).astype(BF16))
            ref, at = vref[b]
            vals.append(jnp.where(mine, ref[at : at + 256, :].astype(F32), jnp.where(spare, 1.0, 0.0)).astype(BF16))
        for chunk in range(2):
            q = (ql, qr)[chunk][...].astype(F32)
            q = jnp.where(mine, q, jnp.where(spare, 1.0, 0.0)).astype(BF16)
            begin = starts[2 * chunk]
            peak = None
            for b in range(4):
                s = dot(q, keys[b], NT)
                at = starts[b] - begin + 896
                lo = bias[:, pl.ds(pl.multiple_of(at, 128), 256)]
                hi = bias[:, pl.ds(pl.multiple_of(at - 128, 128), 256)]
                s = s + jnp.concatenate([lo, hi], axis=0)
                scores[:, b * 256 : (b + 1) * 256] = s
                top = jnp.maximum(s[:, :128], s[:, 128:])
                peak = top if peak is None else jnp.maximum(peak, top)
            peak = jnp.max(peak, axis=1, keepdims=True)
            acc = None
            for b in range(4):
                e = jnp.exp(scores[:, b * 256 : (b + 1) * 256] - peak).astype(BF16)
                expo[head, chunk * 256 : (chunk + 1) * 256, b * 256 : (b + 1) * 256] = e
                part = dot(e, vals[b])
                acc = part if acc is None else acc + part
            total = acc[:, 64:65] if head == 0 else acc[:, 0:1]
            parts[chunk].append((acc, 1.0 / total))
    for chunk in range(2):
        (a0, i0), (a1, i1) = parts[chunk]
        scale = jnp.where(lane < 64, i0, i1)
        rows = slice(chunk * 256, (chunk + 1) * 256)
        out[rows, :] = (jnp.where(lane < 64, a0, a1) * scale).astype(BF16)
        inv[rows, :] = scale

def attention(info, ql, qr, kl, kr, vl, vr, table):
    d = ql.shape[1]
    pairs = d // 128
    col = lambda rows: pl.BlockSpec((rows, 128), lambda g: (0, g))
    return pl.pallas_call(
        fwd_kernel,
        grid=(pairs,),
        in_specs=[pl.BlockSpec(memory_space=pltpu.SMEM), col(256), col(256), col(512), col(512), col(512), col(512),
                  pl.BlockSpec((None, 2, 2048), lambda g: (g, 0, 0))],
        out_specs=[col(512), pl.BlockSpec((2, 512, 1024), lambda g: (g, 0, 0)), col(512)],
        out_shape=[jax.ShapeDtypeStruct((512, d), BF16), jax.ShapeDtypeStruct((2 * pairs, 512, 1024), BF16),
                   jax.ShapeDtypeStruct((512, d), F32)],
        scratch_shapes=[pltpu.VMEM((128, 2048), F32), pltpu.VMEM((256, 1024), F32)],
        name="attn_fwd",
    )(info, ql, qr, kl, kr, vl, vr, table)

def bwd_kernel(info, ql, qr, kl, kr, vl, vr, gout, out, inv, expo, dq, dk, dv, diag, acc):
    lane = lax.broadcasted_iota(jnp.int32, (1, 128), 1)
    kref = [(kl, 0), (kl, 256), (kr, 0), (kr, 256)]
    vref = [(vl, 0), (vl, 256), (vr, 0), (vr, 256)]
    starts = [info[1 + b] for b in range(4)]
    scaled = gout[...].astype(F32) * inv[...]
    prod = scaled * out[...].astype(F32)
    gkeys = [None] * 4
    gvals = [None] * 4
    dqs = [None, None]
    for head in range(2):
        mine = (lane < 64) if head == 0 else (lane >= 64)
        base = 64 if head == 0 else 0
        delta = jnp.sum(jnp.where(mine, prod, 0.0), axis=1, keepdims=True)
        high = delta.astype(BF16).astype(F32)
        gaug = jnp.where(mine, scaled, jnp.where(lane == base, high, jnp.where(lane == base + 1, delta - high, 0.0))).astype(BF16)
        gplain = jnp.where(mine, scaled, 0.0).astype(BF16)
        minus = jnp.where((lane == base) | (lane == base + 1), -1.0, 0.0)
        acc[...] = jnp.zeros_like(acc)
        vals, keys = [], []
        for b in range(4):
            ref, at = vref[b]
            vals.append(jnp.where(mine, ref[at : at + 256, :].astype(F32), minus).astype(BF16))
            ref, at = kref[b]
            keys.append(jnp.where(mine, ref[at : at + 256, :].astype(F32), 0.0).astype(BF16))
        for chunk in range(2):
            rows = slice(chunk * 256, (chunk + 1) * 256)
            q = jnp.where(mine, (ql, qr)[chunk][...].astype(F32), 0.0).astype(BF16)
            begin = starts[2 * chunk]
            for b in range(4):
                e = expo[head, rows, b * 256 : (b + 1) * 256]
                ds = dot(gaug[rows], vals[b], NT) * e.astype(F32)
                at = starts[b] - begin + 896
                lo = pl.ds(pl.multiple_of(at, 128), 256)
                hi = pl.ds(pl.multiple_of(at - 128, 128), 256)
                acc[:, lo] += ds[:128]
                acc[:, hi] += ds[128:]
                ds = ds.astype(BF16)
                part = dot(ds, keys[b])
                dqs[chunk] = part if dqs[chunk] is None else dqs[chunk] + part
                part = dot(q, ds, TN)
                gkeys[b] = part if gkeys[b] is None else gkeys[b] + part
                part = dot(gplain[rows], e, TN)
                gvals[b] = part if gvals[b] is None else gvals[b] + part
        rest = acc[...]
        n = 64
        while n >= 8:
            rest = rest[:n] + pltpu.roll(rest[n:], 2048 - n, 1)
            n //= 2
        line = rest[7:8]
        for r in range(6, -1, -1):
            line = rest[r : r + 1] + pltpu.roll(line, 2047, 1)
        diag[head : head + 1, :] = pltpu.roll(line, 127, 1)
    for chunk in range(2):
        dq[chunk * 256 : (chunk + 1) * 256, :] = dqs[chunk].astype(BF16)
    for b in range(4):
        dk[b * 256 : (b + 1) * 256, :] = gkeys[b].T.astype(BF16)
        dv[b * 256 : (b + 1) * 256, :] = gvals[b].T.astype(BF16)

def attention_grads(info, ql, qr, kl, kr, vl, vr, gout, out, inv, expo, first, pairs):
    d = pairs * 128
    col = lambda rows: pl.BlockSpec((rows, 128), lambda g: (0, first + g))
    made = lambda rows: pl.BlockSpec((rows, 128), lambda g: (0, g))
    return pl.pallas_call(
        bwd_kernel,
        grid=(pairs,),
        in_specs=[pl.BlockSpec(memory_space=pltpu.SMEM), col(256), col(256), col(512), col(512), col(512), col(512),
                  col(512), col(512), col(512), pl.BlockSpec((2, 512, 1024), lambda g: (first + g, 0, 0))],
        out_specs=[made(512), made(1024), made(1024), pl.BlockSpec((None, 2, 2048), lambda g: (g, 0, 0))],
        out_shape=[jax.ShapeDtypeStruct((512, d), BF16), jax.ShapeDtypeStruct((1024, d), BF16),
                   jax.ShapeDtypeStruct((1024, d), BF16), jax.ShapeDtypeStruct((pairs, 2, 2048), F32)],
        scratch_shapes=[pltpu.VMEM((128, 2048), F32)],
        name="attn_bwd",
    )(info, ql, qr, kl, kr, vl, vr, gout, out, inv, expo)

BUCKETS = 32
EPS = 1e-06

def rms_scale(values):
    return lax.rsqrt(jnp.mean(values * values, axis=-1, keepdims=True) + EPS)

def norm_back(grad_out, values, scale, gain):
    weighted = grad_out * gain
    inner = jnp.mean(weighted * values, axis=-1, keepdims=True)
    grad_in = scale * weighted - scale * scale * scale * values * inner
    return grad_in, jnp.sum(grad_out * values * scale, axis=0)

def project_kernel(mine, other, wq, wk, wv, gain, hidden, query, keys, values):
    rows = mine.shape[0]
    for part, raw in enumerate((mine, other)):
        tokens = raw[...].astype(F32)
        hidden[part * rows : (part + 1) * rows, :] = (tokens * rms_scale(tokens) * gain[...]).astype(BF16)
    h = hidden[...]
    query[...] = dot(h[:rows], wq[...]).astype(BF16)
    keys[...] = dot(h, wk[...]).astype(BF16)
    values[...] = dot(h, wv[...]).astype(BF16)

def project(mine, other, wq, wk, wv, gain):
    rows, width = mine.shape
    shape = lambda n: jax.ShapeDtypeStruct((n, width), BF16)
    return pl.pallas_call(
        project_kernel,
        out_shape=[shape(2 * rows), shape(rows), shape(2 * rows), shape(2 * rows)],
        name="project",
    )(mine, other, wq, wk, wv, gain)

def exchange(value, axis, bit):
    size = lax.axis_size(axis)
    return lax.ppermute(value, axis, [(i, i ^ bit) for i in range(size)])

def side(move):
    axis, bit = move
    return (lax.axis_index(axis) // bit) % 2

def halves(value, move):
    half = value.shape[1] // 2
    mine = side(move)
    return lax.dynamic_slice_in_dim(value, mine * half, half, 1), lax.dynamic_slice_in_dim(value, (1 - mine) * half, half, 1)

def add(keep, got):
    return (keep.astype(F32) + got.astype(F32)).astype(BF16)

def join(value, got, move):
    return jnp.where(side(move) == 0, jnp.concatenate([value, got], 1), jnp.concatenate([got, value], 1))

def scatter(values, moves, extra=None):
    split = [halves(v, m) for v, m in zip(values, moves)]
    sends = [s for _, s in split]
    width = sends[0].shape[2]
    if extra is not None:
        count = sends[0].shape[0] * sends[0].shape[1]
        sends[0] = jnp.concatenate([sends[0].reshape(count, width), extra])
    def finish(got):
        got = list(got)
        new = None
        if extra is not None:
            new = add(extra, got[0][count:])
            got[0] = got[0][:count].reshape(split[0][1].shape)
        out = [add(k, g) for (k, _), g in zip(split, got)]
        return out if extra is None else (out, new)
    return list(zip(sends, moves)), finish

def gather(values, moves):
    return list(zip(values, moves)), lambda got: [join(v, g, m) for v, g, m in zip(values, got, moves)]

def phase(parts, token, work=None):
    sends = [s for moves, _ in parts for s, _ in moves]
    moves = [m for moves, _ in parts for _, m in moves]
    token, sends = lax.optimization_barrier((token, sends))
    got = [exchange(s, *m) for s, m in zip(sends, moves)]
    result = None
    if work is not None:
        result, token = work(token)
    token, got = lax.optimization_barrier((token, got))
    outs, at = [], 0
    for part, finish in parts:
        outs.append(finish(got[at : at + len(part)]))
        at += len(part)
    return outs, token, result

def mm(a, b, dims=NN):
    return lax.dot_general(a, b, dims, preferred_element_type=F32)

def pairwise(value):
    half = value.shape[1] // 2
    return [value[:, :half], value[:, half:]]

def local(inputs, w_query, w_key, w_value, w_out, w_in, w_back, norm1_gain, norm2_gain, final_gain, bias_table, bucket_table, prefix_len, pad_len, pooled_grad):
    rows, width = inputs.shape[1:]
    place = lax.axis_index("blk")
    length = rows * lax.axis_size("blk")
    doc, core = place // 2, place % 2
    block = [doc * 2 + core, doc * 2 + 1 - core, (1 - doc) * 2 + core, (1 - doc) * 2 + 1 - core]
    near = lax.dynamic_index_in_dim(inputs, doc, 0, keepdims=False)
    far = exchange(lax.dynamic_index_in_dim(inputs, 1 - doc, 0, keepdims=False), "blk", 2)
    near_other = exchange(near, "blk", 1)
    far_other = exchange(far, "blk", 1)
    limit = length - lax.dynamic_index_in_dim(pad_len, doc, 0, keepdims=False)
    prefix = lax.dynamic_index_in_dim(prefix_len, doc, 0, keepdims=False)
    count = (limit - prefix).astype(F32)
    cotangent = lax.dynamic_index_in_dim(pooled_grad, doc, 0, keepdims=True)
    slot = jnp.arange(8, dtype=jnp.int32)
    info = jnp.where(slot == 0, limit, 0)
    for i, b in enumerate(block):
        info = jnp.where(slot == i + 1, b * rows, info)
    picker = (jnp.arange(BUCKETS, dtype=jnp.int32)[:, None] == bucket_table[None, :]).astype(F32)
    picker = jnp.pad(picker, ((0, 0), (0, 1)))
    table = lax.dot_general(bias_table, picker, TN, precision=lax.Precision.HIGHEST)
    table = table.reshape(-1, 2, picker.shape[1])

    gain_row = norm1_gain[None, :]
    hid_l, q_l, k_l, v_l = project(near, near_other, w_query, w_key, w_value, gain_row)
    hid_r, q_r, k_r, v_r = project(far, far_other, w_query, w_key, w_value, gain_row)
    attended, expo, inverse = attention(info, q_l, q_r, k_l, k_r, v_l, v_r, table)

    tokens = jnp.concatenate([near, far]).astype(F32)
    mixed = tokens + mm(attended, w_out)
    scale_two = rms_scale(mixed)
    inner = (mixed * scale_two * norm2_gain).astype(BF16)
    lifted = mm(inner, w_in)
    active = jnp.maximum(lifted, 0.0).astype(BF16)
    result = mixed + mm(active, w_back)
    scale_end = rms_scale(result)
    spots = jnp.concatenate([block[0] * rows + jnp.arange(rows), block[2] * rows + jnp.arange(rows)])
    live = ((spots >= prefix) & (spots < limit)).astype(F32)[:, None]
    pool_part = jnp.sum(result * scale_end * final_gain * live, axis=0, keepdims=True)

    grad_final = live * (cotangent / count)
    grad_result, grad_end = norm_back(grad_final, result, scale_end, final_gain)
    grad_branch = grad_result.astype(BF16)
    grad_back_w = mm(active, grad_branch, TN).astype(BF16)
    grad_lifted = jnp.where(active > 0, mm(grad_branch, w_back, NT).astype(BF16), jnp.zeros_like(active))
    folds = w_in.shape[1] // width
    grad_in_w = jnp.concatenate([mm(inner, grad_lifted[:, i * width : (i + 1) * width], TN).astype(BF16) for i in range(folds)])
    big = jnp.concatenate([grad_back_w, grad_in_w])[None]

    c = ("blk", 1)
    y = ("blk", 2)
    bits = [("dp", 1 << b) for b in range(lax.axis_size("dp").bit_length() - 1)]
    x, line = bits[0], bits[1:]

    def middle(token):
        grad_inner = mm(grad_lifted, w_in, NT)
        grad_through, grad_two = norm_back(grad_inner, mixed, scale_two, norm2_gain)
        grad_mixed = grad_result + grad_through
        grad_att_out = grad_mixed.astype(BF16)
        grad_out_w = mm(attended, grad_att_out, TN).astype(BF16)
        grad_attended = mm(grad_att_out, w_out, NT).astype(BF16)
        return (grad_mixed, grad_two, grad_out_w, grad_attended), token

    (big,), token, (grad_mixed, grad_two, grad_out_w, grad_attended) = phase([scatter([big], [c])], info, middle)
    big = big[0]

    def back(first, grad_attended):
        def work(token):
            made = attention_grads(token, q_l, q_r, k_l, k_r, v_l, v_r, grad_attended, attended, inverse, expo, first, 2)
            token, last = lax.optimization_barrier((token, made[3]))
            return list(made[:3]) + [last], token
        return work

    own = jnp.concatenate([hid_l[:rows], hid_r[:rows]])
    everyone = jnp.concatenate([hid_l, hid_r])
    (big,), token, made_a = phase([scatter(pairwise(big), [y, x])], token, back(0, grad_attended))
    (big,), token, made_b = phase([scatter(big, [x, y])], token, back(2, grad_attended))
    big = jnp.concatenate(big)
    dq, dk, dv = (jnp.concatenate([a, b], axis=1) for a, b in zip(made_a[:3], made_b[:3]))
    offsets = jnp.concatenate([made_a[3], made_b[3]]).reshape(-1, picker.shape[1])

    def weights(token):
        token, near_dq = lax.optimization_barrier((token, dq))
        grad_bias = lax.dot_general(picker, offsets, NT, precision=lax.Precision.HIGHEST)
        made = [mm(own, near_dq, TN), mm(everyone, dk, TN), mm(everyone, dv, TN)]
        rest = jnp.concatenate([grad_out_w] + [g.astype(BF16) for g in made])[None]
        through_kv = mm(dk, w_key, NT) + mm(dv, w_value, NT)
        through_q = mm(near_dq, w_query, NT)
        raw = jnp.concatenate([near, near_other, far, far_other]).astype(F32)
        scaled = raw * rms_scale(raw)
        near_scaled = jnp.concatenate([scaled[:rows], scaled[2 * rows : 3 * rows]])
        grad_one = jnp.sum(through_kv * scaled, axis=0) + jnp.sum(through_q * near_scaled, axis=0)
        small = jnp.concatenate([grad_one[None], grad_two[None], grad_end[None], jnp.pad(grad_bias.reshape(1, -1), ((0, 0), (0, width - grad_bias.size)))])
        small = jnp.pad(small, ((0, 12), (0, 0))).astype(BF16)
        through_kv = through_kv.reshape(2, 2, rows, width)
        keep = through_q + through_kv[:, 0].reshape(2 * rows, width)
        send = through_kv[:, 1].reshape(2 * rows, width).astype(BF16)
        return (rest, small, keep, send), token

    (big,), token, (rest, small, grad_hidden, sent) = phase([scatter([big], [line[0]])], token, weights)
    hand = ([(sent, c)], lambda got: got[0])
    (big, (rest, small), came), token, _ = phase([scatter(big, [line[1]]), scatter([rest], [c], small), hand], token)
    for step in line[2:]:
        (big,), token, _ = phase([scatter(big, [step])], token)

    def ending(token):
        token, kept = lax.optimization_barrier((token, grad_hidden))
        grad_norm, _ = norm_back(kept + came.astype(F32), tokens, rms_scale(tokens), norm1_gain)
        return (grad_mixed + grad_norm).astype(BF16), token

    for step in reversed(line[2:]):
        (big,), token, _ = phase([gather(big, [step])], token)
    (big, (rest, small)), token, input_grad = phase([gather(big, [line[1]]), scatter(pairwise(rest[0]), [y, x], small)], token, ending)
    away = ([(input_grad[rows:], y)], lambda got: got[0])
    (big, (rest, small), away), token, _ = phase([gather(big, [line[0]]), scatter(rest, [x, y], small), away], token)
    rest = jnp.concatenate(rest)
    big = [big[0][:1], big[0][1:]]
    pool = ([(pool_part, c)], lambda got: got[0])
    (big, (rest, small), pool_got), token, _ = phase([gather(big, [x, y]), scatter([rest], [line[0]], small), pool], token)
    pool_mine = (pool_part + pool_got) / count
    pool = ([(pool_mine, y)], lambda got: got[0])
    (big, (rest, small), pool_other), token, _ = phase([gather(big, [y, x]), scatter(rest, [line[1]], small), pool], token)
    for step in line[2:]:
        ((rest, small),), token, _ = phase([scatter(rest, [step], small)], token)
    for step in reversed(line[2:]):
        (rest,), token, _ = phase([gather(rest, [step])], token)
    big = [jnp.concatenate(big, 1)]
    (big, rest), token, _ = phase([gather(big, [c]), gather(rest, [line[1]])], token)

    def convert(token):
        token, value = lax.optimization_barrier((token, big[0][0]))
        split = w_back.shape[0]
        first = value[:split].astype(F32)
        second = value[split:].reshape(folds, width, width).swapaxes(0, 1).reshape(width, folds * width).astype(F32)
        return (first, second), token

    (rest,), token, (out_back, out_in) = phase([gather(rest, [line[0]])], token, convert)
    rest = [rest[0][:1], rest[0][1:]]
    (rest,), token, _ = phase([gather(rest, [x, y])], token)
    (rest,), token, _ = phase([gather(rest, [y, x])], token)
    (rest,), token, _ = phase([gather([jnp.concatenate(rest, 1)], [c])], token)
    grads = [rest[0][0, i * width : (i + 1) * width].astype(F32) for i in range(4)]
    pooled = jnp.where(doc == 0, jnp.concatenate([pool_mine, pool_other]), jnp.concatenate([pool_other, pool_mine]))
    home = input_grad[:rows]
    input_grad = jnp.where(doc == 0, jnp.stack([home, away]), jnp.stack([away, home]))
    small = small.astype(F32)
    return (
        pooled,
        input_grad,
        grads[1],
        grads[2],
        grads[3],
        grads[0],
        out_in,
        out_back,
        small[0],
        small[1],
        small[2],
        small[3, : bias_table.size].reshape(bias_table.shape),
    )

def solution(mesh):
    data = P("dp", "blk", None)
    placed = (data,) + (P(),) * 11 + (P("dp"), P("dp"), P("dp", None))
    return jax.shard_map(local, mesh=mesh, in_specs=placed, out_specs=(P("dp", None), data) + (P(),) * 10, check_vma=False)
```

```python
import jax, jax.numpy as jnp
from jax import lax
from jax.experimental import pallas as pl
from jax.experimental.pallas import tpu as pltpu
from jax.sharding import PartitionSpec as P

F32, BF16 = jnp.float32, jnp.bfloat16
NEG = -1000000000.0
NT = (((1,), (1,)), ((), ()))
TN = (((0,), (0,)), ((), ()))
NN = (((1,), (0,)), ((), ()))

def dot(a, b, dims=NN):
    return lax.dot_general(a, b, dims, preferred_element_type=F32)

def skew(row, width, dtype=F32):
    return pltpu.roll(jnp.broadcast_to(row, (128, width)), width - 127, 1, stride=1, stride_axis=0)

def fwd_kernel(info, ql, qr, kl, kr, vl, vr, table, out, expo, inv, bias, scores):
    limit = info[0]
    lane = lax.broadcasted_iota(jnp.int32, (1, 128), 1)
    kref = [(kl, 0), (kl, 256), (kr, 0), (kr, 256)]
    vref = [(vl, 0), (vl, 256), (vr, 0), (vr, 256)]
    starts = [info[1 + b] for b in range(4)]
    parts = [[], []]
    for head in range(2):
        mine = (lane < 64) if head == 0 else (lane >= 64)
        spare = lane == (64 if head == 0 else 0)
        bias[...] = skew(table[head : head + 1, :], bias.shape[1])
        keys, vals = [], []
        for b in range(4):
            ref, at = kref[b]
            place = starts[b] + lax.broadcasted_iota(jnp.int32, (256, 1), 0)
            gate = jnp.where(place < limit, 0.0, NEG)
            edge = jnp.where(spare, gate, 0.0)
            keys.append(jnp.where(mine, ref[at : at + 256, :].astype(F32), edge).astype(BF16))
            ref, at = vref[b]
            vals.append(jnp.where(mine, ref[at : at + 256, :].astype(F32), jnp.where(spare, 1.0, 0.0)).astype(BF16))
        for chunk in range(2):
            q = (ql, qr)[chunk][...].astype(F32)
            q = jnp.where(mine, q, jnp.where(spare, 1.0, 0.0)).astype(BF16)
            begin = starts[2 * chunk]
            peak = None
            for b in range(4):
                s = dot(q, keys[b], NT)
                at = starts[b] - begin + 896
                lo = bias[:, pl.ds(pl.multiple_of(at, 128), 256)]
                hi = bias[:, pl.ds(pl.multiple_of(at - 128, 128), 256)]
                s = s + jnp.concatenate([lo, hi], axis=0)
                scores[:, b * 256 : (b + 1) * 256] = s
                top = jnp.maximum(s[:, :128], s[:, 128:])
                peak = top if peak is None else jnp.maximum(peak, top)
            peak = jnp.max(peak, axis=1, keepdims=True)
            acc = None
            for b in range(4):
                e = jnp.exp(scores[:, b * 256 : (b + 1) * 256] - peak).astype(BF16)
                expo[head, chunk * 256 : (chunk + 1) * 256, b * 256 : (b + 1) * 256] = e
                part = dot(e, vals[b])
                acc = part if acc is None else acc + part
            total = acc[:, 64:65] if head == 0 else acc[:, 0:1]
            parts[chunk].append((acc, 1.0 / total))
    for chunk in range(2):
        (a0, i0), (a1, i1) = parts[chunk]
        scale = jnp.where(lane < 64, i0, i1)
        rows = slice(chunk * 256, (chunk + 1) * 256)
        out[rows, :] = (jnp.where(lane < 64, a0, a1) * scale).astype(BF16)
        inv[rows, :] = scale

def attention(info, ql, qr, kl, kr, vl, vr, table):
    d = ql.shape[1]
    pairs = d // 128
    col = lambda rows: pl.BlockSpec((rows, 128), lambda g: (0, g))
    return pl.pallas_call(
        fwd_kernel,
        grid=(pairs,),
        in_specs=[pl.BlockSpec(memory_space=pltpu.SMEM), col(256), col(256), col(512), col(512), col(512), col(512),
                  pl.BlockSpec((None, 2, 2048), lambda g: (g, 0, 0))],
        out_specs=[col(512), pl.BlockSpec((2, 512, 1024), lambda g: (g, 0, 0)), col(512)],
        out_shape=[jax.ShapeDtypeStruct((512, d), BF16), jax.ShapeDtypeStruct((2 * pairs, 512, 1024), BF16),
                   jax.ShapeDtypeStruct((512, d), F32)],
        scratch_shapes=[pltpu.VMEM((128, 2048), F32), pltpu.VMEM((256, 1024), F32)],
        name="attn_fwd",
    )(info, ql, qr, kl, kr, vl, vr, table)

def bwd_kernel(info, ql, qr, kl, kr, vl, vr, gout, out, inv, expo, dq, dk, dv, diag, acc):
    lane = lax.broadcasted_iota(jnp.int32, (1, 128), 1)
    kref = [(kl, 0), (kl, 256), (kr, 0), (kr, 256)]
    vref = [(vl, 0), (vl, 256), (vr, 0), (vr, 256)]
    starts = [info[1 + b] for b in range(4)]
    scaled = gout[...].astype(F32) * inv[...]
    prod = scaled * out[...].astype(F32)
    gkeys = [None] * 4
    gvals = [None] * 4
    dqs = [None, None]
    for head in range(2):
        mine = (lane < 64) if head == 0 else (lane >= 64)
        base = 64 if head == 0 else 0
        delta = jnp.sum(jnp.where(mine, prod, 0.0), axis=1, keepdims=True)
        high = delta.astype(BF16).astype(F32)
        gaug = jnp.where(mine, scaled, jnp.where(lane == base, high, jnp.where(lane == base + 1, delta - high, 0.0))).astype(BF16)
        gplain = jnp.where(mine, scaled, 0.0).astype(BF16)
        minus = jnp.where((lane == base) | (lane == base + 1), -1.0, 0.0)
        acc[...] = jnp.zeros_like(acc)
        vals, keys = [], []
        for b in range(4):
            ref, at = vref[b]
            vals.append(jnp.where(mine, ref[at : at + 256, :].astype(F32), minus).astype(BF16))
            ref, at = kref[b]
            keys.append(jnp.where(mine, ref[at : at + 256, :].astype(F32), 0.0).astype(BF16))
        for chunk in range(2):
            rows = slice(chunk * 256, (chunk + 1) * 256)
            q = jnp.where(mine, (ql, qr)[chunk][...].astype(F32), 0.0).astype(BF16)
            begin = starts[2 * chunk]
            for b in range(4):
                e = expo[head, rows, b * 256 : (b + 1) * 256]
                ds = dot(gaug[rows], vals[b], NT) * e.astype(F32)
                at = starts[b] - begin + 896
                lo = pl.ds(pl.multiple_of(at, 128), 256)
                hi = pl.ds(pl.multiple_of(at - 128, 128), 256)
                acc[:, lo] += ds[:128]
                acc[:, hi] += ds[128:]
                ds = ds.astype(BF16)
                part = dot(ds, keys[b])
                dqs[chunk] = part if dqs[chunk] is None else dqs[chunk] + part
                part = dot(q, ds, TN)
                gkeys[b] = part if gkeys[b] is None else gkeys[b] + part
                part = dot(gplain[rows], e, TN)
                gvals[b] = part if gvals[b] is None else gvals[b] + part
        rest = acc[...]
        n = 64
        while n >= 8:
            rest = rest[:n] + pltpu.roll(rest[n:], 2048 - n, 1)
            n //= 2
        line = rest[7:8]
        for r in range(6, -1, -1):
            line = rest[r : r + 1] + pltpu.roll(line, 2047, 1)
        diag[head : head + 1, :] = pltpu.roll(line, 127, 1)
    for chunk in range(2):
        dq[chunk * 256 : (chunk + 1) * 256, :] = dqs[chunk].astype(BF16)
    for b in range(4):
        dk[b * 256 : (b + 1) * 256, :] = gkeys[b].T.astype(BF16)
        dv[b * 256 : (b + 1) * 256, :] = gvals[b].T.astype(BF16)

def attention_grads(info, ql, qr, kl, kr, vl, vr, gout, out, inv, expo):
    d = ql.shape[1]
    pairs = d // 128
    col = lambda rows: pl.BlockSpec((rows, 128), lambda g: (0, g))
    return pl.pallas_call(
        bwd_kernel,
        grid=(pairs,),
        in_specs=[pl.BlockSpec(memory_space=pltpu.SMEM), col(256), col(256), col(512), col(512), col(512), col(512),
                  col(512), col(512), col(512), pl.BlockSpec((2, 512, 1024), lambda g: (g, 0, 0))],
        out_specs=[col(512), col(1024), col(1024), pl.BlockSpec((None, 2, 2048), lambda g: (g, 0, 0))],
        out_shape=[jax.ShapeDtypeStruct((512, d), BF16), jax.ShapeDtypeStruct((1024, d), BF16),
                   jax.ShapeDtypeStruct((1024, d), BF16), jax.ShapeDtypeStruct((pairs, 2, 2048), F32)],
        scratch_shapes=[pltpu.VMEM((128, 2048), F32)],
        name="attn_bwd",
    )(info, ql, qr, kl, kr, vl, vr, gout, out, inv, expo)

BUCKETS = 32
EPS = 1e-06
CORE, ROW, NEAR_X = 1, 2, 4

def rms_scale(values):
    return lax.rsqrt(jnp.mean(values * values, axis=-1, keepdims=True) + EPS)

def norm_back(grad_out, values, scale, gain):
    weighted = grad_out * gain
    inner = jnp.mean(weighted * values, axis=-1, keepdims=True)
    grad_in = scale * weighted - scale * scale * scale * values * inner
    return grad_in, jnp.sum(grad_out * values * scale, axis=0, keepdims=True)

def two_terms(value):
    high = value.astype(BF16)
    low = (value - high.astype(F32)).astype(BF16)
    fill = jnp.zeros((8 - value.shape[0], value.shape[1]), BF16)
    return jnp.concatenate([high, fill, low, fill])

def one_value(terms, count):
    return terms[:count].astype(F32) + terms[8 : 8 + count].astype(F32)

def project_kernel(mine, other, wq, wk, wv, gain, hidden, query, keys, values):
    rows = mine.shape[0]
    for part, raw in enumerate((mine, other)):
        tokens = raw[...].astype(F32)
        hidden[part * rows : (part + 1) * rows, :] = (tokens * rms_scale(tokens) * gain[...]).astype(BF16)
    h = hidden[...]
    query[...] = dot(h[:rows], wq[...]).astype(BF16)
    keys[...] = dot(h, wk[...]).astype(BF16)
    values[...] = dot(h, wv[...]).astype(BF16)

def project(mine, other, wq, wk, wv, gain):
    rows, width = mine.shape
    shape = lambda n: jax.ShapeDtypeStruct((n, width), BF16)
    return pl.pallas_call(
        project_kernel,
        out_shape=[shape(2 * rows), shape(rows), shape(2 * rows), shape(2 * rows)],
        name="project",
    )(mine, other, wq, wk, wv, gain)

def dense_kernel(info, near, far, attended, wo, win, wback, gain2, gain3, cot, keep, send, slopes, mixed, steep, rows, active, turned):
    count, width = near.shape
    hidden = win.shape[1]
    for part, raw in enumerate((near, far)):
        spot = slice(part * count, (part + 1) * count)
        mixed[spot, :] = raw[...].astype(F32) + dot(attended[spot, :], wo[...])
    values = mixed[...]
    inner = (values * rms_scale(values) * gain2[...]).astype(BF16)
    turned[...] = inner.T
    total = values
    for at in range(0, hidden, 512):
        lifted = jnp.maximum(dot(inner, win[:, at : at + 512]), 0.0).astype(BF16)
        active[:, at : at + 512] = lifted
        total = total + dot(lifted, wback[at : at + 512, :])
    scale = rms_scale(total)
    place = lax.broadcasted_iota(jnp.int32, (2 * count, 1), 0)
    place = jnp.where(place < count, place + info[1], place + (info[3] - count))
    live = jnp.where((place >= info[5]) & (place < info[0]), 1.0, 0.0)
    pool = jnp.sum(total * scale * gain3[...] * live, axis=0, keepdims=True)
    slope, grad_end = norm_back(live * cot[...], total, scale, gain3[...])
    steep[...] = slope
    rows[...] = jnp.concatenate([pool, grad_end, jnp.zeros((6, width), F32)])
    low = slope.astype(BF16)
    for at in range(0, hidden, 512):
        through = dot(low, wback[at : at + 512, :], NT).astype(BF16)
        slopes[:, at : at + 512] = jnp.where(active[:, at : at + 512] > 0, through, jnp.zeros_like(through))
    mine = info[6] & 15

    def backs(to):
        @pl.loop(0, hidden // 256)
        def _(pair):
            made = dot(active[:, pl.ds(pl.multiple_of(pair * 256, 256), 256)], low, TN).astype(BF16)
            for b in range(2):
                to[(2 * pair + b) ^ mine] = jnp.concatenate([made[b * 128 : (b + 1) * 128, q * 128 : (q + 1) * 128] for q in range(4)])

    def ins(to):
        @pl.loop(0, hidden // 256)
        def _(pair):
            made = dot(turned[...], slopes[:, pl.ds(pl.multiple_of(pair * 256, 256), 256)]).astype(BF16)
            for b in range(2):
                to[(2 * pair + b) ^ mine] = made[:, b * 128 : (b + 1) * 128]

    @pl.when(info[7] == 0)
    def _():
        ins(send)
        backs(keep)

    @pl.when(info[7] == 1)
    def _():
        backs(send)
        ins(keep)

def dense(info, near, far, attended, wo, win, wback, gain2, gain3, cot):
    count, width = near.shape
    hidden = win.shape[1]
    smem, vmem = pl.BlockSpec(memory_space=pltpu.SMEM), pl.BlockSpec(memory_space=pltpu.VMEM)
    shape = jax.ShapeDtypeStruct
    return pl.pallas_call(
        dense_kernel,
        in_specs=[smem] + [vmem] * 9,
        out_specs=[vmem] * 6,
        out_shape=[shape((16, width, 128), BF16), shape((16, width, 128), BF16), shape((2 * count, hidden), BF16),
                   shape((2 * count, width), F32), shape((2 * count, width), F32), shape((8, width), F32)],
        scratch_shapes=[pltpu.VMEM((2 * count, hidden), BF16), pltpu.VMEM((width, 2 * count), BF16)],
        name="dense",
    )(info, near, far, attended, wo, win, wback, gain2, gain3, cot)

def through_kernel(info, slopes, win, mixed, steep, attended, wo, gain2, grad_mixed, grad_out, grad_attended, rows):
    width = mixed.shape[1]
    grad_inner = None
    for at in range(0, slopes.shape[1], 512):
        part = dot(slopes[:, at : at + 512], win[:, at : at + 512], NT)
        grad_inner = part if grad_inner is None else grad_inner + part
    values = mixed[...]
    more, grad_two = norm_back(grad_inner, values, rms_scale(values), gain2[...])
    total = steep[...] + more
    grad_mixed[...] = total
    low = total.astype(BF16)
    grad_attended[...] = dot(low, wo[...], NT).astype(BF16)
    grad_out[...] = dot(attended[...], low, TN).astype(BF16)
    rows[...] = jnp.concatenate([grad_two, jnp.zeros((7, width), F32)])

def through(info, slopes, win, mixed, steep, attended, wo, gain2):
    n, width = mixed.shape
    smem, vmem = pl.BlockSpec(memory_space=pltpu.SMEM), pl.BlockSpec(memory_space=pltpu.VMEM)
    shape = jax.ShapeDtypeStruct
    return pl.pallas_call(
        through_kernel,
        in_specs=[smem] + [vmem] * 7,
        out_specs=[vmem] * 4,
        out_shape=[shape((n, width), F32), shape((width, width), BF16), shape((n, width), BF16), shape((8, width), F32)],
        name="through",
    )(info, slopes, win, mixed, steep, attended, wo, gain2)

def weights_kernel(info, hid_l, hid_r, near, near_other, far, far_other, dq, dk, dv, grad_out, wq, wk, wv, dense_rows, keep, send, stay, leave, rows, made):
    count, width = near.shape
    made[0:width, :] = grad_out[...]
    made[width : 2 * width, :] = (dot(hid_l[:count, :], dq[:count, :], TN) + dot(hid_r[:count, :], dq[count:, :], TN)).astype(BF16)
    for at, grads in ((2 * width, dk), (3 * width, dv)):
        made[at : at + width, :] = (dot(hid_l[...], grads[: 2 * count, :], TN) + dot(hid_r[...], grads[2 * count :, :], TN)).astype(BF16)
    mine = info[6]
    size = made.shape[0] // 32

    @pl.loop(0, 16)
    def _(r):
        keep[r] = made[pl.ds(pl.multiple_of((r ^ mine) * size, size), size), :]
        send[r] = made[pl.ds(pl.multiple_of(((r + 16) ^ mine) * size, size), size), :]

    gain = jnp.zeros((1, width), F32)
    for b, raw in enumerate((near, near_other, far, far_other)):
        spot = slice(b * count, (b + 1) * count)
        grad = dot(dk[spot, :], wk[...], NT) + dot(dv[spot, :], wv[...], NT)
        half = slice((b // 2) * count, (b // 2 + 1) * count)
        if b % 2 == 0:
            grad = grad + dot(dq[half, :], wq[...], NT)
            stay[half, :] = grad
        else:
            leave[half, :] = grad.astype(BF16)
        tokens = raw[...].astype(F32)
        gain = gain + jnp.sum(grad * (tokens * rms_scale(tokens)), axis=0, keepdims=True)
    leave[2 * count :, :] = two_terms(dense_rows[0:1, :])
    rows[...] = jnp.concatenate([gain, jnp.zeros((7, width), F32)])

def weights(info, hid_l, hid_r, near, near_other, far, far_other, dq, dk, dv, grad_out, wq, wk, wv, dense_rows):
    count, width = near.shape
    smem, vmem = pl.BlockSpec(memory_space=pltpu.SMEM), pl.BlockSpec(memory_space=pltpu.VMEM)
    shape = jax.ShapeDtypeStruct
    size = 4 * width // 32
    return pl.pallas_call(
        weights_kernel,
        in_specs=[smem] + [vmem] * 14,
        out_specs=[vmem] * 5,
        out_shape=[shape((16, size, width), BF16), shape((16, size, width), BF16), shape((2 * count, width), F32),
                   shape((2 * count + 16, width), BF16), shape((8, width), F32)],
        scratch_shapes=[pltpu.VMEM((4 * width, width), BF16)],
        name="weights",
    )(info, hid_l, hid_r, near, near_other, far, far_other, dq, dk, dv, grad_out, wq, wk, wv, dense_rows)

def ending_kernel(info, stay, came, near, far, grad_mixed, gain, dense_rows, home, away):
    count, width = near.shape
    for part, raw in enumerate((near, far)):
        spot = slice(part * count, (part + 1) * count)
        tokens = raw[...].astype(F32)
        grad = stay[spot, :] + came[spot, :].astype(F32)
        more, _ = norm_back(grad, tokens, rms_scale(tokens), gain[...])
        value = (grad_mixed[spot, :] + more).astype(BF16)
        if part == 0:
            home[:count, :] = value
        else:
            away[:count, :] = value
    alive = (info[0] - info[5]).astype(F32)
    pool = two_terms((dense_rows[0:1, :] + one_value(came[2 * count :, :], 1)) / alive)
    home[count:, :] = pool
    away[count:, :] = pool

def ending(info, stay, came, near, far, grad_mixed, gain, dense_rows):
    count, width = near.shape
    smem, vmem = pl.BlockSpec(memory_space=pltpu.SMEM), pl.BlockSpec(memory_space=pltpu.VMEM)
    shape = jax.ShapeDtypeStruct((count + 16, width), BF16)
    return pl.pallas_call(
        ending_kernel, in_specs=[smem] + [vmem] * 7, out_specs=[vmem] * 2, out_shape=[shape, shape], name="ending"
    )(info, stay, came, near, far, grad_mixed, gain, dense_rows)

def place_kernel(info, *refs):
    parts, (back, front) = refs[:8], refs[8:]
    mine = info[6] & 15

    def backs(half):
        for i in range(4):
            for j in range(4):
                to = (4 * i + j) ^ mine
                for q in range(4):
                    back[pl.ds(pl.multiple_of(to * 128, 128), 128), q * 128 : (q + 1) * 128] = half[i][j, q * 128 : (q + 1) * 128, :].astype(F32)

    def ins(half):
        for i in range(4):
            for j in range(4):
                to = (4 * i + j) ^ mine
                front[:, pl.ds(pl.multiple_of(to * 128, 128), 128)] = half[i][j].astype(F32)

    @pl.when(info[7] == 0)
    def _():
        backs(parts[:4])
        ins(parts[4:])

    @pl.when(info[7] == 1)
    def _():
        ins(parts[:4])
        backs(parts[4:])

def place(info, parts, width):
    hidden = 16 * 128
    smem, vmem = pl.BlockSpec(memory_space=pltpu.SMEM), pl.BlockSpec(memory_space=pltpu.VMEM)
    shape = jax.ShapeDtypeStruct
    return pl.pallas_call(
        place_kernel, in_specs=[smem] + [vmem] * 8, out_specs=[vmem] * 2,
        out_shape=[shape((hidden, width), F32), shape((width, hidden), F32)], name="place",
    )(info, *parts)

def sort_kernel(info, *refs):
    parts, made = refs[:8], refs[8:]
    size, width = parts[0].shape[1:]
    per = width // size
    mine = info[6]

    for half in range(2):
        for top in range(2):
            @pl.when(((mine >> 4) ^ half) == top)
            def _(half=half, top=top):
                for i in range(4):
                    for j in range(4):
                        to = ((4 * i + j) ^ mine) & 15
                        value = parts[4 * half + i][j].astype(F32)
                        spot = pl.ds(pl.multiple_of((to % per) * size, size), size)

                        @pl.when(to < per)
                        def _():
                            made[2 * top][spot, :] = value

                        @pl.when(to >= per)
                        def _():
                            made[2 * top + 1][spot, :] = value

def sort(info, parts, width):
    smem, vmem = pl.BlockSpec(memory_space=pltpu.SMEM), pl.BlockSpec(memory_space=pltpu.VMEM)
    shape = jax.ShapeDtypeStruct((width, width), F32)
    return pl.pallas_call(
        sort_kernel, in_specs=[smem] + [vmem] * 8, out_specs=[vmem] * 4, out_shape=[shape] * 4, name="sort"
    )(info, *parts)

def exchange(value, bits):
    size = lax.axis_size("dp") * lax.axis_size("blk")
    return lax.ppermute(value, ("dp", "blk"), [(i, i ^ bits) for i in range(size)])

def wait(*values):
    return lax.optimization_barrier(values)

def added(*terms):
    total = terms[0].astype(F32)
    for term in terms[1:]:
        total = total + term.astype(F32)
    return total.astype(BF16)

def local(inputs, w_query, w_key, w_value, w_out, w_in, w_back, norm1_gain, norm2_gain, final_gain, bias_table, bucket_table, prefix_len, pad_len, pooled_grad):
    rows, width = inputs.shape[1:]
    spot, far_off = lax.axis_index("blk"), lax.axis_index("dp")
    length = rows * lax.axis_size("blk")
    doc, core = spot // 2, spot % 2
    block = [doc * 2 + core, doc * 2 + 1 - core, (1 - doc) * 2 + core, (1 - doc) * 2 + 1 - core]
    line = [8, 16]
    further = [32 << b for b in range((lax.axis_size("dp") // 8).bit_length() - 1)]
    piece = core * 16 + doc * 4 + (far_off % 2) * 8 + (far_off // 2) % 4
    near = lax.dynamic_index_in_dim(inputs, doc, 0, keepdims=False)
    far = exchange(lax.dynamic_index_in_dim(inputs, 1 - doc, 0, keepdims=False), ROW)
    near_other = exchange(near, CORE)
    far_other = exchange(far, CORE)
    limit = length - lax.dynamic_index_in_dim(pad_len, doc, 0, keepdims=False)
    prefix = lax.dynamic_index_in_dim(prefix_len, doc, 0, keepdims=False)
    cot = lax.dynamic_index_in_dim(pooled_grad, doc, 0, keepdims=True) / (limit - prefix).astype(F32)
    slot = jnp.arange(8, dtype=jnp.int32)
    info = jnp.where(slot == 0, limit, 0)
    for i, value in enumerate([b * rows for b in block] + [prefix, piece, core]):
        info = jnp.where(slot == i + 1, value, info)
    picker = (jnp.arange(BUCKETS, dtype=jnp.int32)[:, None] == bucket_table[None, :]).astype(F32)
    picker = jnp.pad(picker, ((0, 0), (0, 1)))
    table = lax.dot_general(bias_table, picker, TN, precision=lax.Precision.HIGHEST)
    table = table.reshape(-1, 2, picker.shape[1])

    gain1, gain2, gain3 = norm1_gain[None, :], norm2_gain[None, :], final_gain[None, :]
    hid_l, q_l, k_l, v_l = project(near, near_other, w_query, w_key, w_value, gain1)
    hid_r, q_r, k_r, v_r = project(far, far_other, w_query, w_key, w_value, gain1)
    attended, expo, inverse = attention(info, q_l, q_r, k_l, k_r, v_l, v_r, table)
    keep, send, slopes, mixed, steep, dense_rows = dense(info, near, far, attended, w_out, w_in, w_back, gain2, gain3, cot)

    xy = [ROW, NEAR_X, ROW ^ NEAR_X]
    zz = [line[0], line[1], line[0] ^ line[1]]

    token, send = wait(info, send)
    got = exchange(send, CORE)
    grad_mixed, grad_out_w, grad_attended, through_rows = through(token, slopes, w_in, mixed, steep, attended, w_out, gain2)
    token, through_rows, got = wait(token, through_rows, got)

    sends = [added(keep[4 * k : 4 * k + 4], got[4 * k : 4 * k + 4]) for k in (1, 2, 3)]
    token, sends = wait(token, sends)
    came = [exchange(s, m) for s, m in zip(sends, xy)]
    dq, dk, dv, offsets = attention_grads(token, q_l, q_r, k_l, k_r, v_l, v_r, grad_attended, attended, inverse, expo)
    rest_keep, rest_send, stay, leave, first_rows = weights(
        token, hid_l, hid_r, near, near_other, far, far_other, dq, dk, dv, grad_out_w, w_query, w_key, w_value, dense_rows)
    grad_bias = lax.dot_general(picker, offsets.reshape(-1, picker.shape[1]), NT, precision=lax.Precision.HIGHEST)
    grad_bias = jnp.pad(grad_bias.reshape(1, -1), ((0, 0), (0, width - grad_bias.size)))
    small = jnp.concatenate([first_rows[:1], through_rows[:1], dense_rows[1:2], grad_bias])
    token, first_rows, came = wait(token, first_rows, came)

    lines = [added(keep[k], got[k], *[c[k] for c in came]) for k in range(4)]
    first = jnp.concatenate([rest_send.reshape(-1, width), two_terms(small)])
    token, lines, leave, first = wait(token, lines, leave, first)
    took = [exchange(lines[k + 1], m) for k, m in enumerate(zz)]
    rest_got = exchange(first, CORE)
    hidden_got = exchange(leave, CORE)
    token, took, rest_got, hidden_got = wait(token, took, rest_got, hidden_got)
    whole = added(lines[0], *took)
    for bit in further:
        whole = added(whole, exchange(whole, bit))

    count = rest_keep.shape[0] * rest_keep.shape[1]
    small = small + one_value(rest_got[count:], 4)
    rest_got = rest_got[:count].reshape(rest_keep.shape)
    terms = two_terms(small)
    sends = [jnp.concatenate([added(rest_keep[4 * k : 4 * k + 4], rest_got[4 * k : 4 * k + 4]).reshape(-1, width), terms]) for k in (1, 2, 3)]
    token, whole, sends = wait(token, whole, sends)
    back_line = [exchange(whole, m) for m in zz]
    rest_came = [exchange(s, m) for s, m in zip(sends, xy)]
    home, away = ending(token, stay, hidden_got, near, far, grad_mixed, gain1, dense_rows)
    token, back_line, rest_came, away = wait(token, back_line, rest_came, away)

    quarter = jnp.stack([whole] + back_line)
    count = count // 4
    for part in rest_came:
        small = small + one_value(part[count:], 4)
    rest_came = [part[:count].reshape((4,) + rest_keep.shape[1:]) for part in rest_came]
    terms = two_terms(small)
    lines = [added(rest_keep[k], rest_got[k], *[c[k] for c in rest_came]) for k in range(4)]
    sends = [jnp.concatenate([lines[k], terms]) for k in (1, 2, 3)]
    token, quarter, sends, away = wait(token, quarter, sends, away)
    quarters = [exchange(quarter, m) for m in xy]
    took = [exchange(s, m) for s, m in zip(sends, zz)]
    away_got = exchange(away, ROW)
    token, took = wait(token, took)
    count = count // 4
    for part in took:
        small = small + one_value(part[count:], 4)
    rest = added(lines[0], *[part[:count] for part in took])
    for bit in further:
        rest = added(rest, exchange(rest, bit))
        small = small + exchange(small, bit)
    token, rest = wait(token, rest)
    back_line = [exchange(rest, m) for m in zz]
    token, back_line = wait(token, back_line)
    rest_quarter = jnp.stack([rest] + back_line)

    token, rest_quarter = wait(token, rest_quarter)
    rest_quarters = [exchange(rest_quarter, m) for m in xy]
    token, quarters, away_got = wait(token, quarters, away_got)
    mine = [quarter] + quarters
    others = [exchange(value, CORE) for value in mine]
    token, others = wait(token, others)
    out_back, out_in = place(token, mine + others, width)
    token, out_back, rest_quarters = wait(token, out_back, rest_quarters)
    mine = [rest_quarter] + rest_quarters
    others = [exchange(value, CORE) for value in mine]
    out_out, out_query, out_key, out_value = sort(info, mine + others, width)

    pool_mine, pool_other = one_value(home[rows:], 1), one_value(away_got[rows:], 1)
    pooled = jnp.where(doc == 0, jnp.concatenate([pool_mine, pool_other]), jnp.concatenate([pool_other, pool_mine]))
    home, away_got = home[:rows], away_got[:rows]
    input_grad = jnp.where(doc == 0, jnp.stack([home, away_got]), jnp.stack([away_got, home]))
    return (
        pooled,
        input_grad,
        out_query,
        out_key,
        out_value,
        out_out,
        out_in,
        out_back,
        small[0],
        small[1],
        small[2],
        small[3, : bias_table.size].reshape(bias_table.shape),
    )

def solution(mesh):
    data = P("dp", "blk", None)
    placed = (data,) + (P(),) * 11 + (P("dp"), P("dp"), P("dp", None))
    return jax.shard_map(local, mesh=mesh, in_specs=placed, out_specs=(P("dp", None), data) + (P(),) * 10, check_vma=False)
```

```python
import functools
import jax, jax.numpy as jnp
from jax import lax
from jax.experimental import pallas as pl
from jax.experimental.pallas import tpu as pltpu
from jax.sharding import PartitionSpec as P

F32, BF16 = jnp.float32, jnp.bfloat16
NEG = -1000000000.0
NT = (((1,), (1,)), ((), ()))
TN = (((0,), (0,)), ((), ()))
NN = (((1,), (0,)), ((), ()))

def dot(a, b, dims=NN):
    return lax.dot_general(a, b, dims, preferred_element_type=F32)

def skew(row, width, dtype=F32):
    return pltpu.roll(jnp.broadcast_to(row, (128, width)), width - 127, 1, stride=1, stride_axis=0)

def fwd_kernel(info, ql, qr, kl, kr, vl, vr, table, out, expo, inv, bias, scores):
    limit = info[0]
    lane = lax.broadcasted_iota(jnp.int32, (1, 128), 1)
    kref = [(kl, 0), (kl, 256), (kr, 0), (kr, 256)]
    vref = [(vl, 0), (vl, 256), (vr, 0), (vr, 256)]
    starts = [info[1 + b] for b in range(4)]
    parts = [[], []]
    for head in range(2):
        mine = (lane < 64) if head == 0 else (lane >= 64)
        spare = lane == (64 if head == 0 else 0)
        bias[...] = skew(table[head : head + 1, :], bias.shape[1])
        keys, vals = [], []
        for b in range(4):
            ref, at = kref[b]
            place = starts[b] + lax.broadcasted_iota(jnp.int32, (256, 1), 0)
            gate = jnp.where(place < limit, 0.0, NEG)
            edge = jnp.where(spare, gate, 0.0)
            keys.append(jnp.where(mine, ref[at : at + 256, :].astype(F32), edge).astype(BF16))
            ref, at = vref[b]
            vals.append(jnp.where(mine, ref[at : at + 256, :].astype(F32), jnp.where(spare, 1.0, 0.0)).astype(BF16))
        for chunk in range(2):
            q = (ql, qr)[chunk][...].astype(F32)
            q = jnp.where(mine, q, jnp.where(spare, 1.0, 0.0)).astype(BF16)
            begin = starts[2 * chunk]
            peak = None
            for b in range(4):
                s = dot(q, keys[b], NT)
                at = starts[b] - begin + 896
                lo = bias[:, pl.ds(pl.multiple_of(at, 128), 256)]
                hi = bias[:, pl.ds(pl.multiple_of(at - 128, 128), 256)]
                s = s + jnp.concatenate([lo, hi], axis=0)
                scores[:, b * 256 : (b + 1) * 256] = s
                top = jnp.maximum(s[:, :128], s[:, 128:])
                peak = top if peak is None else jnp.maximum(peak, top)
            peak = jnp.max(peak, axis=1, keepdims=True)
            acc = None
            for b in range(4):
                e = jnp.exp(scores[:, b * 256 : (b + 1) * 256] - peak).astype(BF16)
                expo[head, chunk * 256 : (chunk + 1) * 256, b * 256 : (b + 1) * 256] = e
                part = dot(e, vals[b])
                acc = part if acc is None else acc + part
            total = acc[:, 64:65] if head == 0 else acc[:, 0:1]
            parts[chunk].append((acc, 1.0 / total))
    for chunk in range(2):
        (a0, i0), (a1, i1) = parts[chunk]
        scale = jnp.where(lane < 64, i0, i1)
        rows = slice(chunk * 256, (chunk + 1) * 256)
        out[rows, :] = (jnp.where(lane < 64, a0, a1) * scale).astype(BF16)
        inv[rows, :] = scale

def attention(info, ql, qr, kl, kr, vl, vr, table):
    d = ql.shape[1]
    pairs = d // 128
    col = lambda rows: pl.BlockSpec((rows, 128), lambda g: (0, g))
    return pl.pallas_call(
        fwd_kernel,
        grid=(pairs,),
        in_specs=[pl.BlockSpec(memory_space=pltpu.SMEM), col(256), col(256), col(512), col(512), col(512), col(512),
                  pl.BlockSpec((None, 2, 2048), lambda g: (g, 0, 0))],
        out_specs=[col(512), pl.BlockSpec((2, 512, 1024), lambda g: (g, 0, 0)), col(512)],
        out_shape=[jax.ShapeDtypeStruct((512, d), BF16), jax.ShapeDtypeStruct((2 * pairs, 512, 1024), BF16),
                   jax.ShapeDtypeStruct((512, d), F32)],
        scratch_shapes=[pltpu.VMEM((128, 2048), F32), pltpu.VMEM((256, 1024), F32)],
        name="attn_fwd",
    )(info, ql, qr, kl, kr, vl, vr, table)

def bwd_kernel(info, ql, qr, kl, kr, vl, vr, gout, out, inv, expo, dq, dk, dv, diag, acc):
    lane = lax.broadcasted_iota(jnp.int32, (1, 128), 1)
    kref = [(kl, 0), (kl, 256), (kr, 0), (kr, 256)]
    vref = [(vl, 0), (vl, 256), (vr, 0), (vr, 256)]
    starts = [info[1 + b] for b in range(4)]
    scaled = gout[...].astype(F32) * inv[...]
    prod = scaled * out[...].astype(F32)
    gkeys = [None] * 4
    gvals = [None] * 4
    dqs = [None, None]
    for head in range(2):
        mine = (lane < 64) if head == 0 else (lane >= 64)
        base = 64 if head == 0 else 0
        delta = jnp.sum(jnp.where(mine, prod, 0.0), axis=1, keepdims=True)
        high = delta.astype(BF16).astype(F32)
        gaug = jnp.where(mine, scaled, jnp.where(lane == base, high, jnp.where(lane == base + 1, delta - high, 0.0))).astype(BF16)
        gplain = jnp.where(mine, scaled, 0.0).astype(BF16)
        minus = jnp.where((lane == base) | (lane == base + 1), -1.0, 0.0)
        acc[...] = jnp.zeros_like(acc)
        vals, keys = [], []
        for b in range(4):
            ref, at = vref[b]
            vals.append(jnp.where(mine, ref[at : at + 256, :].astype(F32), minus).astype(BF16))
            ref, at = kref[b]
            keys.append(jnp.where(mine, ref[at : at + 256, :].astype(F32), 0.0).astype(BF16))
        for chunk in range(2):
            rows = slice(chunk * 256, (chunk + 1) * 256)
            q = jnp.where(mine, (ql, qr)[chunk][...].astype(F32), 0.0).astype(BF16)
            begin = starts[2 * chunk]
            for b in range(4):
                e = expo[head, rows, b * 256 : (b + 1) * 256]
                ds = dot(gaug[rows], vals[b], NT) * e.astype(F32)
                at = starts[b] - begin + 896
                lo = pl.ds(pl.multiple_of(at, 128), 256)
                hi = pl.ds(pl.multiple_of(at - 128, 128), 256)
                acc[:, lo] += ds[:128]
                acc[:, hi] += ds[128:]
                ds = ds.astype(BF16)
                part = dot(ds, keys[b])
                dqs[chunk] = part if dqs[chunk] is None else dqs[chunk] + part
                part = dot(q, ds, TN)
                gkeys[b] = part if gkeys[b] is None else gkeys[b] + part
                part = dot(gplain[rows], e, TN)
                gvals[b] = part if gvals[b] is None else gvals[b] + part
        rest = acc[...]
        n = 64
        while n >= 8:
            rest = rest[:n] + pltpu.roll(rest[n:], 2048 - n, 1)
            n //= 2
        line = rest[7:8]
        for r in range(6, -1, -1):
            line = rest[r : r + 1] + pltpu.roll(line, 2047, 1)
        diag[head : head + 1, :] = pltpu.roll(line, 127, 1)
    for chunk in range(2):
        dq[chunk * 256 : (chunk + 1) * 256, :] = dqs[chunk].astype(BF16)
    for b in range(4):
        dk[b * 256 : (b + 1) * 256, :] = gkeys[b].T.astype(BF16)
        dv[b * 256 : (b + 1) * 256, :] = gvals[b].T.astype(BF16)

def attention_grads(info, ql, qr, kl, kr, vl, vr, gout, out, inv, expo):
    d = ql.shape[1]
    pairs = d // 128
    col = lambda rows: pl.BlockSpec((rows, 128), lambda g: (0, g))
    return pl.pallas_call(
        bwd_kernel,
        grid=(pairs,),
        in_specs=[pl.BlockSpec(memory_space=pltpu.SMEM), col(256), col(256), col(512), col(512), col(512), col(512),
                  col(512), col(512), col(512), pl.BlockSpec((2, 512, 1024), lambda g: (g, 0, 0))],
        out_specs=[col(512), col(1024), col(1024), pl.BlockSpec((None, 2, 2048), lambda g: (g, 0, 0))],
        out_shape=[jax.ShapeDtypeStruct((512, d), BF16), jax.ShapeDtypeStruct((1024, d), BF16),
                   jax.ShapeDtypeStruct((1024, d), BF16), jax.ShapeDtypeStruct((pairs, 2, 2048), F32)],
        scratch_shapes=[pltpu.VMEM((128, 2048), F32)],
        name="attn_bwd",
    )(info, ql, qr, kl, kr, vl, vr, gout, out, inv, expo)

BUCKETS = 32
EPS = 1e-06
CORE, ROW, NEAR_X = 1, 2, 4

def rms_scale(values):
    return lax.rsqrt(jnp.mean(values * values, axis=-1, keepdims=True) + EPS)

def norm_back(grad_out, values, scale, gain):
    weighted = grad_out * gain
    inner = jnp.mean(weighted * values, axis=-1, keepdims=True)
    grad_in = scale * weighted - scale * scale * scale * values * inner
    return grad_in, jnp.sum(grad_out * values * scale, axis=0, keepdims=True)

def two_terms(value):
    high = value.astype(BF16)
    return jnp.concatenate([high, (value - high.astype(F32)).astype(BF16)])

def one_value(terms):
    return terms[:16].astype(F32) + terms[16:32].astype(F32)

def rows_of(*values):
    count = sum(v.shape[0] for v in values)
    return jnp.concatenate(list(values) + [jnp.zeros((16 - count, values[0].shape[1]), F32)])

def project_kernel(mine, other, wq, wk, wv, gain, hidden, query, keys, values):
    rows = mine.shape[0]
    for part, raw in enumerate((mine, other)):
        tokens = raw[...].astype(F32)
        hidden[part * rows : (part + 1) * rows, :] = (tokens * rms_scale(tokens) * gain[...]).astype(BF16)
    h = hidden[...]
    query[...] = dot(h[:rows], wq[...]).astype(BF16)
    keys[...] = dot(h, wk[...]).astype(BF16)
    values[...] = dot(h, wv[...]).astype(BF16)

def project(mine, other, wq, wk, wv, gain):
    rows, width = mine.shape
    shape = lambda n: jax.ShapeDtypeStruct((n, width), BF16)
    return pl.pallas_call(
        project_kernel,
        out_shape=[shape(2 * rows), shape(rows), shape(2 * rows), shape(2 * rows)],
        name="project",
    )(mine, other, wq, wk, wv, gain)

def dense_kernel(info, near, far, attended, wo, win, wback, gain2, gain3, cot, keep, send, slopes, mixed, steep, rows, active, turned):
    count, width = near.shape
    hidden = win.shape[1]
    for part, raw in enumerate((near, far)):
        spot = slice(part * count, (part + 1) * count)
        mixed[spot, :] = raw[...].astype(F32) + dot(attended[spot, :], wo[...])
    values = mixed[...]
    inner = (values * rms_scale(values) * gain2[...]).astype(BF16)
    turned[...] = inner.T
    total = values
    for at in range(0, hidden, 512):
        lifted = jnp.maximum(dot(inner, win[:, at : at + 512]), 0.0).astype(BF16)
        active[:, at : at + 512] = lifted
        total = total + dot(lifted, wback[at : at + 512, :])
    scale = rms_scale(total)
    place = lax.broadcasted_iota(jnp.int32, (2 * count, 1), 0)
    place = jnp.where(place < count, place + info[1], place + (info[3] - count))
    live = jnp.where((place >= info[5]) & (place < info[0]), 1.0, 0.0)
    pool = jnp.sum(total * scale * gain3[...] * live, axis=0, keepdims=True)
    slope, grad_end = norm_back(live * cot[...], total, scale, gain3[...])
    steep[...] = slope
    rows[...] = jnp.concatenate([pool, grad_end, jnp.zeros((6, width), F32)])
    low = slope.astype(BF16)
    for at in range(0, hidden, 512):
        through = dot(low, wback[at : at + 512, :], NT).astype(BF16)
        slopes[:, at : at + 512] = jnp.where(active[:, at : at + 512] > 0, through, jnp.zeros_like(through))
    mine = info[6] & 15

    def backs(to):
        @pl.loop(0, hidden // 256)
        def _(pair):
            made = dot(active[:, pl.ds(pl.multiple_of(pair * 256, 256), 256)], low, TN).astype(BF16)
            for b in range(2):
                to[(2 * pair + b) ^ mine] = jnp.concatenate([made[b * 128 : (b + 1) * 128, q * 128 : (q + 1) * 128] for q in range(4)])

    def ins(to):
        @pl.loop(0, hidden // 256)
        def _(pair):
            made = dot(turned[...], slopes[:, pl.ds(pl.multiple_of(pair * 256, 256), 256)]).astype(BF16)
            for b in range(2):
                to[(2 * pair + b) ^ mine] = made[:, b * 128 : (b + 1) * 128]

    @pl.when(info[7] == 0)
    def _():
        ins(send)
        backs(keep)

    @pl.when(info[7] == 1)
    def _():
        backs(send)
        ins(keep)

def dense(info, near, far, attended, wo, win, wback, gain2, gain3, cot):
    count, width = near.shape
    hidden = win.shape[1]
    smem, vmem = pl.BlockSpec(memory_space=pltpu.SMEM), pl.BlockSpec(memory_space=pltpu.VMEM)
    shape = jax.ShapeDtypeStruct
    return pl.pallas_call(
        dense_kernel,
        in_specs=[smem] + [vmem] * 9,
        out_specs=[vmem] * 6,
        out_shape=[shape((16, width, 128), BF16), shape((16, width, 128), BF16), shape((2 * count, hidden), BF16),
                   shape((2 * count, width), F32), shape((2 * count, width), F32), shape((8, width), F32)],
        scratch_shapes=[pltpu.VMEM((2 * count, hidden), BF16), pltpu.VMEM((width, 2 * count), BF16)],
        name="dense",
    )(info, near, far, attended, wo, win, wback, gain2, gain3, cot)

def through_kernel(info, slopes, win, mixed, steep, attended, wo, gain2, grad_mixed, grad_out, grad_attended, rows):
    width = mixed.shape[1]
    grad_inner = None
    for at in range(0, slopes.shape[1], 512):
        part = dot(slopes[:, at : at + 512], win[:, at : at + 512], NT)
        grad_inner = part if grad_inner is None else grad_inner + part
    values = mixed[...]
    more, grad_two = norm_back(grad_inner, values, rms_scale(values), gain2[...])
    total = steep[...] + more
    grad_mixed[...] = total
    low = total.astype(BF16)
    grad_attended[...] = dot(low, wo[...], NT).astype(BF16)
    grad_out[...] = dot(attended[...], low, TN).astype(BF16)
    rows[...] = jnp.concatenate([grad_two, jnp.zeros((7, width), F32)])

def through(info, slopes, win, mixed, steep, attended, wo, gain2):
    n, width = mixed.shape
    smem, vmem = pl.BlockSpec(memory_space=pltpu.SMEM), pl.BlockSpec(memory_space=pltpu.VMEM)
    shape = jax.ShapeDtypeStruct
    return pl.pallas_call(
        through_kernel,
        in_specs=[smem] + [vmem] * 7,
        out_specs=[vmem] * 4,
        out_shape=[shape((n, width), F32), shape((width, width), BF16), shape((n, width), BF16), shape((8, width), F32)],
        name="through",
    )(info, slopes, win, mixed, steep, attended, wo, gain2)

def weights_kernel(info, hid_l, hid_r, near, near_other, far, far_other, dq, dk, dv, grad_out, wq, wk, wv, dense_rows, through_rows, offsets, buckets, keep, send, stay, leave, small, made):
    count, width = near.shape
    made[0:width, :] = grad_out[...]
    made[width : 2 * width, :] = (dot(hid_l[:count, :], dq[:count, :], TN) + dot(hid_r[:count, :], dq[count:, :], TN)).astype(BF16)
    for at, grads in ((2 * width, dk), (3 * width, dv)):
        made[at : at + width, :] = (dot(hid_l[...], grads[: 2 * count, :], TN) + dot(hid_r[...], grads[2 * count :, :], TN)).astype(BF16)
    mine = info[6]
    size = made.shape[0] // 32

    @pl.loop(0, 16)
    def _(r):
        keep[r] = made[pl.ds(pl.multiple_of((r ^ mine) * size, size), size), :]
        send[pl.ds(pl.multiple_of(r * size, size), size), :] = made[pl.ds(pl.multiple_of(((r + 16) ^ mine) * size, size), size), :]

    gain = jnp.zeros((1, width), F32)
    for b, raw in enumerate((near, near_other, far, far_other)):
        spot = slice(b * count, (b + 1) * count)
        grad = dot(dk[spot, :], wk[...], NT) + dot(dv[spot, :], wv[...], NT)
        half = slice((b // 2) * count, (b // 2 + 1) * count)
        if b % 2 == 0:
            grad = grad + dot(dq[half, :], wq[...], NT)
            stay[half, :] = grad
        else:
            leave[half, :] = grad.astype(BF16)
        tokens = raw[...].astype(F32)
        gain = gain + jnp.sum(grad * (tokens * rms_scale(tokens)), axis=0, keepdims=True)
    leave[2 * count :, :] = two_terms(rows_of(dense_rows[0:1, :]))
    picker = jnp.where(lax.broadcasted_iota(jnp.int32, (width, 1), 0) == buckets[...], 1.0, 0.0).astype(BF16)
    lines = jnp.concatenate([offsets[g] for g in range(offsets.shape[0])])
    bias = None
    for _ in range(3):
        part = lines.astype(BF16)
        lines = lines - part.astype(F32)
        bias = dot(part, picker, NT) if bias is None else bias + dot(part, picker, NT)
    sums = jnp.concatenate([gain, through_rows[0:1, :], dense_rows[1:2, :], jnp.zeros((5, width), F32), bias])
    small[...] = sums
    send[16 * size :, :] = two_terms(sums)

def weights(info, hid_l, hid_r, near, near_other, far, far_other, dq, dk, dv, grad_out, wq, wk, wv, dense_rows, through_rows, offsets, buckets):
    count, width = near.shape
    smem, vmem = pl.BlockSpec(memory_space=pltpu.SMEM), pl.BlockSpec(memory_space=pltpu.VMEM)
    shape = jax.ShapeDtypeStruct
    size = 4 * width // 32
    return pl.pallas_call(
        weights_kernel,
        in_specs=[smem] + [vmem] * 17,
        out_specs=[vmem] * 5,
        out_shape=[shape((16, size, width), BF16), shape((16 * size + 32, width), BF16), shape((2 * count, width), F32),
                   shape((2 * count + 32, width), BF16), shape((16, width), F32)],
        scratch_shapes=[pltpu.VMEM((4 * width, width), BF16)],
        name="weights",
    )(info, hid_l, hid_r, near, near_other, far, far_other, dq, dk, dv, grad_out, wq, wk, wv, dense_rows, through_rows, offsets, buckets)

def ending_kernel(info, stay, came, near, far, grad_mixed, gain, dense_rows, home, away):
    count, width = near.shape
    for part, raw in enumerate((near, far)):
        spot = slice(part * count, (part + 1) * count)
        tokens = raw[...].astype(F32)
        grad = stay[spot, :] + came[spot, :].astype(F32)
        more, _ = norm_back(grad, tokens, rms_scale(tokens), gain[...])
        value = (grad_mixed[spot, :] + more).astype(BF16)
        if part == 0:
            home[:count, :] = value
        else:
            away[:count, :] = value
    alive = (info[0] - info[5]).astype(F32)
    pool = two_terms((rows_of(dense_rows[0:1, :]) + one_value(came[2 * count :, :])) / alive)
    home[count:, :] = pool
    away[count:, :] = pool

def ending(info, stay, came, near, far, grad_mixed, gain, dense_rows):
    count, width = near.shape
    smem, vmem = pl.BlockSpec(memory_space=pltpu.SMEM), pl.BlockSpec(memory_space=pltpu.VMEM)
    shape = jax.ShapeDtypeStruct((count + 32, width), BF16)
    return pl.pallas_call(
        ending_kernel, in_specs=[smem] + [vmem] * 7, out_specs=[vmem] * 2, out_shape=[shape, shape], name="ending"
    )(info, stay, came, near, far, grad_mixed, gain, dense_rows)

def place_kernel(half, info, *refs):
    parts, (back, front), (tall, sems) = refs[:4], refs[-4:-2], refs[-2:]
    mine = info[6] & 15

    @pl.when(info[7] == half)
    def _():
        copies = []
        for r in range(16):
            to = pl.ds(pl.multiple_of((r ^ mine) * 128, 128), 128)
            for q in range(4):
                tall[r, :128, q * 128 : (q + 1) * 128] = parts[r // 4][r % 4, q * 128 : (q + 1) * 128, :].astype(F32)
            copies.append(pltpu.make_async_copy(tall.at[r, :128, :], back.at[to, :], sems.at[r]))
            copies[-1].start()
        for copy in copies:
            copy.wait()

    @pl.when(info[7] != half)
    def _():
        copies = []
        for r in range(16):
            to = pl.ds(pl.multiple_of((r ^ mine) * 128, 128), 128)
            tall[r, :, :128] = parts[r // 4][r % 4].astype(F32)
            copies.append(pltpu.make_async_copy(tall.at[r, :, :128], front.at[:, to], sems.at[r]))
            copies[-1].start()
        for copy in copies:
            copy.wait()

def place(info, half, parts, made, width):
    smem, vmem, free = (pl.BlockSpec(memory_space=m) for m in (pltpu.SMEM, pltpu.VMEM, pl.ANY))
    shape = jax.ShapeDtypeStruct
    return pl.pallas_call(
        functools.partial(place_kernel, half),
        in_specs=[smem] + [vmem] * 4 + [free] * len(made),
        out_specs=[free] * 2,
        out_shape=[shape((16 * 128, width), F32), shape((width, 16 * 128), F32)],
        scratch_shapes=[pltpu.VMEM((16, width, width), F32), pltpu.SemaphoreType.DMA((16,))],
        input_output_aliases={5 + i: i for i in range(len(made))},
        name="place",
    )(info, *parts, *made)

def sort_kernel(half, info, *refs):
    parts, made, (tall, sems) = refs[:4], refs[-6:-2], refs[-2:]
    size = parts[0].shape[1]
    per = tall.shape[1] // size
    mine = info[6] & 15
    for r in range(16):
        to = r ^ mine
        tall[to // per, pl.ds(pl.multiple_of((to % per) * size, size), size), :] = parts[r // 4][r % 4].astype(F32)
    for top in range(2):
        @pl.when((info[7] ^ half) == top)
        def _(top=top):
            copies = [pltpu.make_async_copy(tall.at[w], made[2 * top + w], sems.at[w]) for w in range(2)]
            for copy in copies:
                copy.start()
            for copy in copies:
                copy.wait()

def sort(info, half, parts, made, width):
    smem, vmem, free = (pl.BlockSpec(memory_space=m) for m in (pltpu.SMEM, pltpu.VMEM, pl.ANY))
    shape = jax.ShapeDtypeStruct((width, width), F32)
    return pl.pallas_call(
        functools.partial(sort_kernel, half),
        in_specs=[smem] + [vmem] * 4 + [free] * len(made),
        out_specs=[free] * 4,
        out_shape=[shape] * 4,
        scratch_shapes=[pltpu.VMEM((2, width, width), F32), pltpu.SemaphoreType.DMA((2,))],
        input_output_aliases={5 + i: i for i in range(len(made))},
        name="sort",
    )(info, *parts, *made)

def mix_kernel(*refs):
    ins, outs = refs[: -4], refs[-4:]
    for k in range(4):
        outs[k][...] = added(*[term[k] for term in ins])

def mix(terms):
    block = terms[0].shape[1:]
    spec = pl.BlockSpec((4,) + block, lambda i: (0,) * (1 + len(block)))
    out = pl.BlockSpec(block, lambda i: (0,) * len(block))
    return pl.pallas_call(
        mix_kernel, grid=(1,), in_specs=[spec] * len(terms), out_specs=[out] * 4,
        out_shape=[jax.ShapeDtypeStruct(block, BF16)] * 4, name="mix",
    )(*terms)

def exchange(value, bits):
    size = lax.axis_size("dp") * lax.axis_size("blk")
    return lax.ppermute(value, ("dp", "blk"), [(i, i ^ bits) for i in range(size)])

def wait(*values):
    return lax.optimization_barrier(values)

def added(*terms):
    total = terms[0].astype(F32)
    for term in terms[1:]:
        total = total + term.astype(F32)
    return total.astype(BF16)

def local(inputs, w_query, w_key, w_value, w_out, w_in, w_back, norm1_gain, norm2_gain, final_gain, bias_table, bucket_table, prefix_len, pad_len, pooled_grad):
    rows, width = inputs.shape[1:]
    spot, far_off = lax.axis_index("blk"), lax.axis_index("dp")
    length = rows * lax.axis_size("blk")
    doc, core = spot // 2, spot % 2
    block = [doc * 2 + core, doc * 2 + 1 - core, (1 - doc) * 2 + core, (1 - doc) * 2 + 1 - core]
    line = [8, 16]
    further = [32 << b for b in range((lax.axis_size("dp") // 8).bit_length() - 1)]
    piece = core * 16 + doc * 4 + (far_off % 2) * 8 + (far_off // 2) % 4
    near = jnp.where(doc == 0, inputs[0], inputs[1])
    far_send = jnp.where(doc == 0, inputs[1], inputs[0])
    near, far_send = wait(near, far_send)
    far = exchange(far_send, ROW)
    near_other = exchange(near, CORE)
    limit = length - jnp.where(doc == 0, pad_len[0], pad_len[1])
    prefix = jnp.where(doc == 0, prefix_len[0], prefix_len[1])
    cot = jnp.where(doc == 0, pooled_grad[:1], pooled_grad[1:]) / (limit - prefix).astype(F32)
    slot = jnp.arange(8, dtype=jnp.int32)
    info = jnp.where(slot == 0, limit, 0)
    for i, value in enumerate([b * rows for b in block] + [prefix, piece, core]):
        info = jnp.where(slot == i + 1, value, info)
    buckets = jnp.pad(bucket_table, (0, 1), constant_values=-1)[None, :]
    picker = (jnp.arange(BUCKETS, dtype=jnp.int32)[:, None] == buckets).astype(F32)
    table = lax.dot_general(bias_table, picker, TN, precision=lax.Precision.HIGHEST)
    table = table.reshape(-1, 2, picker.shape[1])

    gain1, gain2, gain3 = norm1_gain[None, :], norm2_gain[None, :], final_gain[None, :]
    hid_l, q_l, k_l, v_l = project(near, near_other, w_query, w_key, w_value, gain1)
    far, q_l, info, table, cot, buckets = wait(far, q_l, info, table, cot, buckets)
    far_other = exchange(far, CORE)
    hid_r, q_r, k_r, v_r = project(far, far_other, w_query, w_key, w_value, gain1)
    attended, expo, inverse = attention(info, q_l, q_r, k_l, k_r, v_l, v_r, table)
    keep, send, slopes, mixed, steep, dense_rows = dense(info, near, far, attended, w_out, w_in, w_back, gain2, gain3, cot)

    xy = [ROW, NEAR_X, ROW ^ NEAR_X]
    zz = [line[0], line[1], line[0] ^ line[1]]

    token, send = wait(info, send)
    got = exchange(send, CORE)
    grad_mixed, grad_out_w, grad_attended, through_rows = through(token, slopes, w_in, mixed, steep, attended, w_out, gain2)
    token, through_rows, got = wait(token, through_rows, got)

    sends = [added(keep[4 * k : 4 * k + 4], got[4 * k : 4 * k + 4]) for k in (3, 1, 2)]
    came = [exchange(s, m) for s, m in zip(sends, (xy[2], xy[0], xy[1]))]
    token, sends = wait(token, sends)
    dq, dk, dv, offsets = attention_grads(token, q_l, q_r, k_l, k_r, v_l, v_r, grad_attended, attended, inverse, expo)
    rest_keep, rest_send, stay, leave, small = weights(
        token, hid_l, hid_r, near, near_other, far, far_other, dq, dk, dv, grad_out_w, w_query, w_key, w_value, dense_rows,
        through_rows, offsets, buckets)
    token, small, rest_send, leave, came = wait(token, small, rest_send, leave, came)

    rest_got = exchange(rest_send, CORE)
    hidden_got = exchange(leave, CORE)
    lines = mix([keep, got] + list(came))
    token, lines = wait(token, lines)
    took = [exchange(lines[k + 1], m) for k, m in enumerate(zz)]
    token, rest_got, hidden_got = wait(token, rest_got, hidden_got)

    count = rest_keep.shape[0] * rest_keep.shape[1]
    small = small + one_value(rest_got[count:])
    rest_got = rest_got[:count].reshape(rest_keep.shape)
    terms = two_terms(small)
    sends = [jnp.concatenate([added(rest_keep[4 * k : 4 * k + 4], rest_got[4 * k : 4 * k + 4]).reshape(-1, width), terms]) for k in (1, 2, 3)]
    token, sends = wait(token, sends)
    rest_came = [exchange(s, m) for s, m in zip(sends, xy)]
    home, away = ending(token, stay, hidden_got, near, far, grad_mixed, gain1, dense_rows)
    token, took, away = wait(token, took, away)

    whole = added(lines[0], *took)
    for bit in further:
        whole = added(whole, exchange(whole, bit))
    token, whole = wait(token, whole)
    back_line = [exchange(whole, m) for m in zz]
    away_got = exchange(away, ROW)
    token, rest_came = wait(token, rest_came)

    count = count // 4
    for part in rest_came:
        small = small + one_value(part[count:])
    rest_came = [part[:count].reshape((4,) + rest_keep.shape[1:]) for part in rest_came]
    terms = two_terms(small)
    lines = [added(rest_keep[k], rest_got[k], *[c[k] for c in rest_came]) for k in range(4)]
    sends = [jnp.concatenate([lines[k], terms]) for k in (1, 2, 3)]
    token, sends = wait(token, sends)
    took = [exchange(s, m) for s, m in zip(sends, zz)]
    token, back_line = wait(token, back_line)

    quarter = jnp.stack([whole] + back_line)
    token, quarter = wait(token, quarter)
    quarters = [exchange(quarter, m) for m in xy]
    token, took = wait(token, took)

    count = count // 4
    for part in took:
        small = small + one_value(part[count:])
    rest = added(lines[0], *[part[:count] for part in took])
    for bit in further:
        rest = added(rest, exchange(rest, bit))
        small = small + exchange(small, bit)
    token, rest = wait(token, rest)
    back_line = [exchange(rest, m) for m in zz]
    token, back_line = wait(token, back_line)
    rest_quarter = jnp.stack([rest] + back_line)
    token, rest_quarter = wait(token, rest_quarter)
    rest_quarters = [exchange(rest_quarter, m) for m in xy]

    token, quarters = wait(token, quarters)
    mine = [quarter] + quarters
    others = [exchange(value, CORE) for value in mine]
    out_big = place(token, 0, mine, [], width)
    token, out_big, others = wait(token, out_big, others)
    out_back, out_in = place(token, 1, others, out_big, width)
    token, out_back, out_in, rest_quarters, away_got = wait(token, out_back, out_in, rest_quarters, away_got)
    mine = [rest_quarter] + rest_quarters
    others = [exchange(value, CORE) for value in mine]
    out_rest = sort(token, 0, mine, [], width)
    token, out_rest, others = wait(token, out_rest, others)
    out_out, out_query, out_key, out_value = sort(token, 1, others, out_rest, width)

    pool_mine, pool_other = one_value(home[rows:])[:1], one_value(away_got[rows:])[:1]
    pooled = jnp.where(doc == 0, jnp.concatenate([pool_mine, pool_other]), jnp.concatenate([pool_other, pool_mine]))
    home, away_got = home[:rows], away_got[:rows]
    input_grad = jnp.where(doc == 0, jnp.stack([home, away_got]), jnp.stack([away_got, home]))
    return (
        pooled,
        input_grad,
        out_query,
        out_key,
        out_value,
        out_out,
        out_in,
        out_back,
        small[0],
        small[1],
        small[2],
        small[8:, :BUCKETS].T,
    )

def solution(mesh):
    data = P("dp", "blk", None)
    placed = (data,) + (P(),) * 11 + (P("dp"), P("dp"), P("dp", None))
    return jax.shard_map(local, mesh=mesh, in_specs=placed, out_specs=(P("dp", None), data) + (P(),) * 10, check_vma=False)
```

```python
import functools
import jax, jax.numpy as jnp
from jax import lax
from jax.experimental import pallas as pl
from jax.experimental.pallas import tpu as pltpu
from jax.sharding import PartitionSpec as P

F32, BF16 = jnp.float32, jnp.bfloat16
NEG = -1000000000.0
NT = (((1,), (1,)), ((), ()))
TN = (((0,), (0,)), ((), ()))
NN = (((1,), (0,)), ((), ()))

def dot(a, b, dims=NN):
    return lax.dot_general(a, b, dims, preferred_element_type=F32)

def skew(row, width, dtype=F32):
    return pltpu.roll(jnp.broadcast_to(row, (128, width)), width - 127, 1, stride=1, stride_axis=0)


BUCKETS = 32
EPS = 1e-06
CORE, ROW, NEAR_X = 1, 2, 4

def rms_scale(values):
    return lax.rsqrt(jnp.mean(values * values, axis=-1, keepdims=True) + EPS)

def norm_back(grad_out, values, scale, gain):
    weighted = grad_out * gain
    inner = jnp.mean(weighted * values, axis=-1, keepdims=True)
    grad_in = scale * weighted - scale * scale * scale * values * inner
    return grad_in, jnp.sum(grad_out * values * scale, axis=0, keepdims=True)

def two_terms(value):
    high = value.astype(BF16)
    return jnp.concatenate([high, (value - high.astype(F32)).astype(BF16)])

def one_value(terms):
    return terms[:16].astype(F32) + terms[16:32].astype(F32)

def rows_of(*values):
    count = sum(v.shape[0] for v in values)
    return jnp.concatenate(list(values) + [jnp.zeros((16 - count, values[0].shape[1]), F32)])

def prepare_kernel(ids, pads, prefixes, mine, other, wq, wk, wv, gain, bias, buckets, hidden, query, keys, values, lines, info):
    rows = mine.shape[0]
    info[0] = 4 * rows - pads[ids[6]]
    info[5] = prefixes[ids[6]]
    for to, at in enumerate((0, 1, 2, 3)):
        info[1 + to] = ids[at]
    for to, at in enumerate((4, 5, 6)):
        info[6 + to] = ids[at]
    for part, raw in enumerate((mine, other)):
        tokens = raw[...].astype(F32)
        hidden[part * rows : (part + 1) * rows, :] = (tokens * rms_scale(tokens) * gain[...]).astype(BF16)
    h = hidden[...]
    query[...] = dot(h[:rows], wq[...]).astype(BF16)
    keys[...] = dot(h, wk[...]).astype(BF16)
    values[...] = dot(h, wv[...]).astype(BF16)
    picker = jnp.where(lax.broadcasted_iota(jnp.int32, (bias.shape[0], 1), 0) == buckets[...], 1.0, 0.0).astype(BF16)
    left, total = bias[...], None
    for _ in range(3):
        part = left.astype(BF16)
        left = left - part.astype(F32)
        made = dot(part, picker, TN)
        total = made if total is None else total + made
    lines[...] = jnp.zeros_like(lines)
    lines[:, : buckets.shape[1]] = total

def prepare(ids, pads, prefixes, mine, other, wq, wk, wv, gain, bias, buckets):
    rows, width = mine.shape
    span = buckets.shape[1] + 1
    heads = bias.shape[1]
    shape = lambda n: jax.ShapeDtypeStruct((n, width), BF16)
    smem, vmem = pl.BlockSpec(memory_space=pltpu.SMEM), pl.BlockSpec(memory_space=pltpu.VMEM)
    return pl.pallas_call(
        prepare_kernel,
        in_specs=[smem] * 3 + [vmem] * 8,
        out_specs=[vmem] * 5 + [smem],
        out_shape=[shape(2 * rows), shape(rows), shape(2 * rows), shape(2 * rows),
                   jax.ShapeDtypeStruct((heads, span), F32), jax.ShapeDtypeStruct((16,), jnp.int32)],
        name="prepare",
    )(ids, pads, prefixes, mine, other, wq, wk, wv, gain, bias, buckets)

def swap_in(to, hidden, index, mine, made, columns):
    for b in range(2):
        if columns:
            to[(2 * index + b) ^ mine] = made[:, b * 128 : (b + 1) * 128]
        else:
            to[(2 * index + b) ^ mine] = jnp.concatenate([made[b * 128 : (b + 1) * 128, q * 128 : (q + 1) * 128] for q in range(4)])

def back_pieces(to, active, low, mine):
    @pl.loop(0, active.shape[1] // 256)
    def _(pair):
        made = dot(active[:, pl.ds(pl.multiple_of(pair * 256, 256), 256)], low, TN).astype(BF16)
        swap_in(to, active.shape[1], pair, mine, made, False)

def in_pieces(to, slopes, turned, mine):
    @pl.loop(0, slopes.shape[1] // 256)
    def _(pair):
        made = dot(turned, slopes[:, pl.ds(pl.multiple_of(pair * 256, 256), 256)]).astype(BF16)
        swap_in(to, slopes.shape[1], pair, mine, made, True)

def front_kernel(info, far, far_other, near, q_l, k_l, v_l, lines, wq, wk, wv, gain1, gain2, gain3, cots, wo_h, win_h, wback_h,
                 hid_o, q_o, k_o, v_o, expo_o, inv_o, att_o, send_o, active_o, slopes_o, turned_o, mixed_o, steep_o, rows,
                 hid, qs, ks, vs, inv, att, send, active, slopes, turned, mixed, steep, wo, win, wback, expo, scores, skewed, edges, sems):
    count, width = near.shape
    hidden = win.shape[1]
    step = pl.program_id(0)
    late = [pltpu.make_async_copy(a, b, sems.at[i]) for i, (a, b) in enumerate(((wo_h, wo), (win_h, win), (wback_h, wback)))]
    early = [pltpu.make_async_copy(a, b, sems.at[3 + i]) for i, (a, b) in enumerate(((hid, hid_o), (qs, q_o), (ks, k_o), (vs, v_o)))]
    dense = [pltpu.make_async_copy(a, b, sems.at[7 + i]) for i, (a, b) in enumerate((
        (inv, inv_o), (att, att_o), (mixed, mixed_o), (turned, turned_o), (active, active_o), (steep, steep_o), (slopes, slopes_o), (send, send_o)))]
    kept = lambda g: pltpu.make_async_copy(expo, expo_o.at[pl.ds(2 * g, 2)], sems.at[15])

    @pl.when(step == 0)
    def _():
        for copy in late:
            copy.start()
        for part, raw in enumerate((far, far_other)):
            tokens = raw[...].astype(F32)
            hid[part * count : (part + 1) * count, :] = (tokens * rms_scale(tokens) * gain1[...]).astype(BF16)
        h = hid[...]
        qs[...] = dot(h[:count], wq[...]).astype(BF16)
        ks[...] = dot(h, wk[...]).astype(BF16)
        vs[...] = dot(h, wv[...]).astype(BF16)
        for copy in early:
            copy.start()
        column = lax.broadcasted_iota(jnp.int32, (1, 128), 1)
        for b in range(4):
            place = info[1 + b] + lax.broadcasted_iota(jnp.int32, (count, 1), 0)
            gate = jnp.where(place < info[0], 0.0, NEG)
            for head in range(2):
                edges[head, b * count : (b + 1) * count, :] = jnp.where(column == (64 if head == 0 else 0), gate, 0.0).astype(BF16)

    @pl.when(step > 0)
    def _():
        kept(step - 1).wait()

    cols = pl.ds(pl.multiple_of(step * 128, 128), 128)
    lane = lax.broadcasted_iota(jnp.int32, (1, 128), 1)
    first = lane < 64
    limit = info[0]
    starts = [info[1 + b] for b in range(4)]
    keys = [k_l[:count, :], k_l[count:, :], ks[:count, cols], ks[count:, cols]]
    values = jnp.concatenate([v_l[...], vs[:, cols]])
    query = jnp.concatenate([q_l[...], qs[:, cols]])
    made = []
    for head in range(2):
        mine = jnp.where(first if head == 0 else lane >= 64, 1.0, 0.0).astype(BF16)
        one = jnp.where(lane == (64 if head == 0 else 0), 1.0, 0.0).astype(BF16)
        q = query * mine + one
        v = values * mine + one
        skewed[head] = skew(lines[pl.ds(2 * step + head, 1), :], lines.shape[1])
        for b in range(4):
            s = dot(q, keys[b] * mine + edges[head, b * count : (b + 1) * count, :], NT)
            for r in range(4):
                at = starts[b] - starts[2 * (r // 2)] + 896 - 128 * (r % 2)
                part = s[r * 128 : (r + 1) * 128] + skewed[head, :, pl.ds(pl.multiple_of(at, 128), 256)]
                scores[head, r * 128 : (r + 1) * 128, b * 256 : (b + 1) * 256] = part
        for r in range(4):
            rs = slice(r * 128, (r + 1) * 128)
            value = scores[head, rs, :]
            top = jnp.max(value, axis=1, keepdims=True)
            expo[head, rs, :] = jnp.exp(value - top).astype(BF16)
        acc = dot(expo[head], v)
        made.append((acc, 1.0 / (acc[:, 64:65] if head == 0 else acc[:, 0:1])))
    (a0, i0), (a1, i1) = made
    scale = jnp.where(first, i0, i1)
    att[:, cols] = (jnp.where(first, a0, a1) * scale).astype(BF16)
    inv[:, cols] = scale
    kept(step).start()

    @pl.when(step == 3)
    def _():
        for copy in late:
            copy.wait()
        dense[0].start()
        dense[1].start()
        for part, raw in enumerate((near, far)):
            spot = slice(part * count, (part + 1) * count)
            mixed[spot, :] = raw[...].astype(F32) + dot(att[spot, :], wo[...])
        dense[2].start()
        values = mixed[...]
        inner = (values * rms_scale(values) * gain2[...]).astype(BF16)
        turned[...] = inner.T
        dense[3].start()
        total = values
        for at in range(0, hidden, 512):
            lifted = jnp.maximum(dot(inner, win[:, at : at + 512]), 0.0).astype(BF16)
            active[:, at : at + 512] = lifted
            total = total + dot(lifted, wback[at : at + 512, :])
        dense[4].start()
        scale = rms_scale(total)
        place = lax.broadcasted_iota(jnp.int32, (2 * count, 1), 0)
        place = jnp.where(place < count, place + info[1], place + (info[3] - count))
        live = jnp.where((place >= info[5]) & (place < limit), 1.0, 0.0)
        pool = jnp.sum(total * scale * gain3[...] * live, axis=0, keepdims=True)
        cot = jnp.where(info[8] == 0, cots[0:1, :], cots[1:2, :]) / (limit - info[5]).astype(F32)
        slope, grad_end = norm_back(live * cot, total, scale, gain3[...])
        steep[...] = slope
        dense[5].start()
        rows[...] = jnp.concatenate([pool, grad_end, jnp.zeros((6, width), F32)])
        low = slope.astype(BF16)
        for at in range(0, hidden, 512):
            through = dot(low, wback[at : at + 512, :], NT).astype(BF16)
            slopes[:, at : at + 512] = jnp.where(active[:, at : at + 512] > 0, through, jnp.zeros_like(through))
        dense[6].start()
        mine = info[6] & 15

        @pl.when(info[7] == 0)
        def _():
            in_pieces(send, slopes, turned[...], mine)

        @pl.when(info[7] == 1)
        def _():
            back_pieces(send, active, steep[...].astype(BF16), mine)

        dense[7].start()
        for copy in early + dense:
            copy.wait()
        kept(step).wait()

def front(info, far, far_other, near, q_l, k_l, v_l, lines, wq, wk, wv, gain1, gain2, gain3, cots, wo, win, wback):
    count, width = near.shape
    hidden = win.shape[1]
    heads, span = lines.shape
    shape = jax.ShapeDtypeStruct
    smem, free = pl.BlockSpec(memory_space=pltpu.SMEM), pl.BlockSpec(memory_space=pl.ANY)
    whole = lambda *dims: pl.BlockSpec(dims, lambda g: (0,) * len(dims))
    col = lambda n: pl.BlockSpec((n, 128), lambda g: (0, g))
    outs = [shape((2 * count, width), BF16), shape((count, width), BF16), shape((2 * count, width), BF16), shape((2 * count, width), BF16),
            shape((heads, 2 * count, 4 * count), BF16), shape((2 * count, width), F32), shape((2 * count, width), BF16),
            shape((16, width, 128), BF16), shape((2 * count, hidden), BF16), shape((2 * count, hidden), BF16),
            shape((width, 2 * count), BF16), shape((2 * count, width), F32), shape((2 * count, width), F32)]
    return pl.pallas_call(
        front_kernel,
        grid=(heads // 2,),
        in_specs=[smem, whole(count, width), whole(count, width), whole(count, width), col(count), col(2 * count), col(2 * count),
                  whole(heads, span)] + [whole(width, width)] * 3 + [whole(1, width)] * 3
                 + [whole(2, width)] + [free] * 3,
        out_specs=[free] * 13 + [whole(8, width)],
        out_shape=outs + [shape((8, width), F32)],
        scratch_shapes=[pltpu.VMEM(o.shape, o.dtype) for o in outs[:4] + outs[5:]]
                       + [pltpu.VMEM(wo.shape, BF16), pltpu.VMEM(win.shape, BF16), pltpu.VMEM(wback.shape, BF16),
                          pltpu.VMEM((2, 2 * count, 4 * count), BF16), pltpu.VMEM((2, 2 * count, 4 * count), F32),
                          pltpu.VMEM((2, 128, span), F32), pltpu.VMEM((2, 4 * count, 128), BF16), pltpu.SemaphoreType.DMA((16,))],
        name="front",
    )(info, far, far_other, near, q_l, k_l, v_l, lines, wq, wk, wv, gain1, gain2, gain3, cots, wo, win, wback)

def through_kernel(info, slopes_h, win_h, mixed_h, steep_h, wo_h, att_h, active_h, turned_h, gain2, keep, grad_mixed, grad_out, grad_attended, rows,
                   slopes, win, mixed, steep, wo, att, active, turned, sems):
    hidden, width = slopes.shape[1], mixed.shape[1]
    chunks = []
    for i, at in enumerate(range(0, hidden, 512)):
        for a, b, s in ((slopes_h, slopes, i), (win_h, win, 4 + i)):
            chunks.append(pltpu.make_async_copy(a.at[:, at : at + 512], b.at[:, at : at + 512], sems.at[s]))
    copies = [pltpu.make_async_copy(a, b, sems.at[8 + i]) for i, (a, b) in enumerate((
        (mixed_h, mixed), (steep_h, steep), (wo_h, wo), (att_h, att), (active_h, active), (turned_h, turned)))]
    for copy in chunks + copies:
        copy.start()
    grad_inner = None
    for i, at in enumerate(range(0, hidden, 512)):
        chunks[2 * i].wait()
        chunks[2 * i + 1].wait()
        part = dot(slopes[:, at : at + 512], win[:, at : at + 512], NT)
        grad_inner = part if grad_inner is None else grad_inner + part
    copies[0].wait()
    copies[1].wait()
    values = mixed[...]
    more, grad_two = norm_back(grad_inner, values, rms_scale(values), gain2[...])
    total = steep[...] + more
    grad_mixed[...] = total
    low = total.astype(BF16)
    copies[2].wait()
    grad_attended[...] = dot(low, wo[...], NT).astype(BF16)
    copies[3].wait()
    grad_out[...] = dot(att[...], low, TN).astype(BF16)
    rows[...] = jnp.concatenate([grad_two, jnp.zeros((7, width), F32)])
    copies[4].wait()
    copies[5].wait()
    mine = info[6] & 15

    @pl.when(info[7] == 0)
    def _():
        back_pieces(keep, active, steep[...].astype(BF16), mine)

    @pl.when(info[7] == 1)
    def _():
        in_pieces(keep, slopes, turned[...], mine)

def through(info, slopes, win, mixed, steep, wo, att, active, turned, gain2):
    n, width = mixed.shape
    smem, vmem, free = (pl.BlockSpec(memory_space=m) for m in (pltpu.SMEM, pltpu.VMEM, pl.ANY))
    shape = jax.ShapeDtypeStruct
    given = (slopes, win, mixed, steep, wo, att, active, turned)
    return pl.pallas_call(
        through_kernel,
        in_specs=[smem] + [free] * 8 + [vmem],
        out_specs=[vmem] * 5,
        out_shape=[shape((16, width, 128), BF16), shape((n, width), F32), shape((width, width), BF16), shape((n, width), BF16), shape((8, width), F32)],
        scratch_shapes=[pltpu.VMEM(g.shape, g.dtype) for g in given] + [pltpu.SemaphoreType.DMA((14,))],
        name="through",
    )(info, *given, gain2)

CLASS = {(0, 0): 0, (1, 2): 0, (0, 1): 1, (1, 3): 1, (0, 2): 2, (0, 3): 3, (1, 0): 4, (1, 1): 5}

def back_kernel(info, ql, qr, kl, kr, vl, vr, gout, out, inv, expo, buckets, dense_rows, through_rows,
                hid_l_h, hid_r_h, near_h, near_other_h, far_h, far_other_h, wq_h, wk_h, wv_h, grad_out_h,
                keep_o, send_o, stay_o, leave_o, small,
                hid_l, hid_r, near, near_other, far, far_other, wq, wk, wv, made,
                keep, send, stay, leave, dq, dk, dv, offsets, sums, acc, slopes, sems):
    count, width = near.shape
    step = pl.program_id(0)
    pairs = width // 128
    late = [pltpu.make_async_copy(a, b, sems.at[i]) for i, (a, b) in enumerate((
        (hid_l_h, hid_l), (hid_r_h, hid_r), (near_h, near), (near_other_h, near_other), (far_h, far), (far_other_h, far_other),
        (wq_h, wq), (wk_h, wk), (wv_h, wv), (grad_out_h, made.at[0:width])))]
    done = [pltpu.make_async_copy(a, b, sems.at[10 + i]) for i, (a, b) in enumerate(((send, send_o), (keep, keep_o), (leave, leave_o), (stay, stay_o)))]

    @pl.when(step == 0)
    def _():
        for copy in late:
            copy.start()

    cols = pl.ds(pl.multiple_of(step * 128, 128), 128)
    lane = lax.broadcasted_iota(jnp.int32, (1, 128), 1)
    starts = [info[1 + b] for b in range(4)]
    keys = jnp.concatenate([kl[...], kr[...]])
    values = jnp.concatenate([vl[...], vr[...]])
    query = jnp.concatenate([ql[...], qr[...]])
    scaled = gout[...].astype(F32) * inv[...]
    prod = scaled * out[...].astype(F32)
    low = scaled.astype(BF16)
    query_t, low_t = query.T, low.T
    grads_q, grads_k, grads_v = None, [], []
    for head in range(2):
        mine = (lane < 64) if head == 0 else (lane >= 64)
        base = 64 if head == 0 else 0
        pick = jnp.where(mine, 1.0, 0.0).astype(BF16)
        delta = jnp.sum(jnp.where(mine, prod, 0.0), axis=1, keepdims=True)
        high = delta.astype(BF16).astype(F32)
        extra = jnp.where(lane == base, high, jnp.where(lane == base + 1, delta - high, 0.0)).astype(BF16)
        grad = low * pick + extra
        minus = jnp.where((lane == base) | (lane == base + 1), -1.0, 0.0).astype(BF16)
        for b in range(4):
            spot = slice(b * count, (b + 1) * count)
            ds = dot(grad, values[spot] * pick + minus, NT) * expo[head, :, spot].astype(F32)
            slopes[head, :, spot] = ds.astype(BF16)
            for chunk in range(2):
                upper, lower = (ds[chunk * count + r * 128 : chunk * count + (r + 1) * 128] for r in range(2))
                group = CLASS[chunk, b]
                block = jnp.concatenate([lower[:, :128], lower[:, 128:] + upper[:, :128], upper[:, 128:]], axis=1)
                if (chunk, b) in ((1, 2), (1, 3)):
                    block = block + sums[head, group]
                sums[head, group] = block
        part = dot(slopes[head], keys * pick)
        grads_q = part if grads_q is None else grads_q + part
        half = slice(head * 64, (head + 1) * 64)
        grads_k.append(dot(query_t[half], slopes[head]))
        grads_v.append(dot(low_t[half], expo[head]))
    dq[:, cols] = grads_q.astype(BF16)
    dk[:, cols] = jnp.concatenate(grads_k).astype(BF16).T
    dv[:, cols] = jnp.concatenate(grads_v).astype(BF16).T
    for head in range(2):
        acc[head] = jnp.zeros(acc.shape[1:], F32)
        for (chunk, b), group in CLASS.items():
            if (chunk, b) not in ((1, 2), (1, 3)):
                at = starts[b] - starts[2 * chunk] + 768
                to = pl.ds(pl.multiple_of(at, 128), 384)
                acc[head, :, to] += sums[head, group]
        rest = acc[head]
        n = 64
        while n >= 8:
            rest = rest[:n] + pltpu.roll(rest[n:], 2048 - n, 1)
            n //= 2
        line = rest[7:8]
        for r in range(6, -1, -1):
            line = rest[r : r + 1] + pltpu.roll(line, 2047, 1)
        offsets[pl.ds(2 * step + head, 1), :] = pltpu.roll(line, 127, 1)

    @pl.when(step == pairs - 1)
    def _():
        for copy in late:
            copy.wait()
        made[width : 2 * width, :] = (dot(hid_l[:count, :], dq[:count, :], TN) + dot(hid_r[:count, :], dq[count:, :], TN)).astype(BF16)
        for at, grads in ((2 * width, dk), (3 * width, dv)):
            made[at : at + width, :] = (dot(hid_l[...], grads[: 2 * count, :], TN) + dot(hid_r[...], grads[2 * count :, :], TN)).astype(BF16)
        me = info[6]
        size = made.shape[0] // 32

        @pl.loop(0, 16)
        def _(r):
            keep[r] = made[pl.ds(pl.multiple_of((r ^ me) * size, size), size), :]
            send[pl.ds(pl.multiple_of(r * size, size), size), :] = made[pl.ds(pl.multiple_of(((r + 16) ^ me) * size, size), size), :]

        gain = jnp.zeros((1, width), F32)
        for b, raw in enumerate((near, near_other, far, far_other)):
            spot = slice(b * count, (b + 1) * count)
            grad = dot(dk[spot, :], wk[...], NT) + dot(dv[spot, :], wv[...], NT)
            half = slice((b // 2) * count, (b // 2 + 1) * count)
            if b % 2 == 0:
                grad = grad + dot(dq[half, :], wq[...], NT)
                stay[half, :] = grad
            else:
                leave[half, :] = grad.astype(BF16)
            tokens = raw[...].astype(F32)
            gain = gain + jnp.sum(grad * (tokens * rms_scale(tokens)), axis=0, keepdims=True)
        leave[2 * count :, :] = two_terms(rows_of(dense_rows[0:1, :]))
        picker = jnp.where(lax.broadcasted_iota(jnp.int32, (128, 1), 0) == buckets[...], 1.0, 0.0).astype(BF16)
        left = offsets[...][:, : buckets.shape[1]]
        bias = None
        for _ in range(3):
            part = left.astype(BF16)
            left = left - part.astype(F32)
            bias = dot(part, picker, NT) if bias is None else bias + dot(part, picker, NT)
        bias = jnp.concatenate([bias, jnp.zeros((bias.shape[0], width - 128), F32)], axis=1)
        total = jnp.concatenate([gain, through_rows[0:1, :], dense_rows[1:2, :], jnp.zeros((5, width), F32), bias])
        small[...] = total
        send[16 * size :, :] = two_terms(total)
        for copy in done:
            copy.start()
        for copy in done:
            copy.wait()

def back(info, ql, qr, kl, kr, vl, vr, gout, out, inv, expo, buckets, dense_rows, through_rows,
         hid_l, hid_r, near, near_other, far, far_other, wq, wk, wv, grad_out):
    count, width = near.shape
    smem, free = pl.BlockSpec(memory_space=pltpu.SMEM), pl.BlockSpec(memory_space=pl.ANY)
    whole = lambda *dims: pl.BlockSpec(dims, lambda g: (0,) * len(dims))
    col = lambda n: pl.BlockSpec((n, 128), lambda g: (0, g))
    shape = jax.ShapeDtypeStruct
    size = 4 * width // 32
    outs = [shape((16, size, width), BF16), shape((16 * size + 32, width), BF16), shape((2 * count, width), F32), shape((2 * count + 32, width), BF16)]
    given = (hid_l, hid_r, near, near_other, far, far_other, wq, wk, wv)
    return pl.pallas_call(
        back_kernel,
        grid=(width // 128,),
        in_specs=[smem, col(count), col(count)] + [col(2 * count)] * 7 + [pl.BlockSpec((2, 2 * count, 4 * count), lambda g: (g, 0, 0)),
                  whole(*buckets.shape), whole(8, width), whole(8, width)] + [free] * 10,
        out_specs=[free] * 4 + [whole(16, width)],
        out_shape=outs + [shape((16, width), F32)],
        scratch_shapes=[pltpu.VMEM(g.shape, BF16) for g in given] + [pltpu.VMEM((4 * width, width), BF16)]
                       + [pltpu.VMEM(o.shape, o.dtype) for o in outs]
                       + [pltpu.VMEM((2 * count, width), BF16), pltpu.VMEM((4 * count, width), BF16), pltpu.VMEM((4 * count, width), BF16),
                          pltpu.VMEM((8, 2048), F32), pltpu.VMEM((2, 6, 128, 384), F32), pltpu.VMEM((2, 128, 2048), F32),
                          pltpu.VMEM((2, 2 * count, 4 * count), BF16), pltpu.SemaphoreType.DMA((14,))],
        name="back",
    )(info, ql, qr, kl, kr, vl, vr, gout, out, inv, expo, buckets, dense_rows, through_rows, *given, grad_out)

def ending_kernel(info, stay, came, near, far, grad_mixed, gain, dense_rows, home, away):
    count, width = near.shape
    for part, raw in enumerate((near, far)):
        spot = slice(part * count, (part + 1) * count)
        tokens = raw[...].astype(F32)
        grad = stay[spot, :] + came[spot, :].astype(F32)
        more, _ = norm_back(grad, tokens, rms_scale(tokens), gain[...])
        value = (grad_mixed[spot, :] + more).astype(BF16)
        if part == 0:
            home[:count, :] = value
        else:
            away[:count, :] = value
    alive = (info[0] - info[5]).astype(F32)
    pool = two_terms((rows_of(dense_rows[0:1, :]) + one_value(came[2 * count :, :])) / alive)
    home[count:, :] = pool
    away[count:, :] = pool

def ending(info, stay, came, near, far, grad_mixed, gain, dense_rows):
    count, width = near.shape
    smem, vmem = pl.BlockSpec(memory_space=pltpu.SMEM), pl.BlockSpec(memory_space=pltpu.VMEM)
    shape = jax.ShapeDtypeStruct((count + 32, width), BF16)
    return pl.pallas_call(
        ending_kernel, in_specs=[smem] + [vmem] * 7, out_specs=[vmem] * 2, out_shape=[shape, shape], name="ending"
    )(info, stay, came, near, far, grad_mixed, gain, dense_rows)

def place_kernel(half, info, *refs):
    parts, (back, front), (tall, sems) = refs[:4], refs[-4:-2], refs[-2:]
    mine = info[6] & 15

    @pl.when(info[7] == half)
    def _():
        copies = []
        for r in range(16):
            to = pl.ds(pl.multiple_of((r ^ mine) * 128, 128), 128)
            for q in range(4):
                tall[r, :128, q * 128 : (q + 1) * 128] = parts[r // 4][r % 4, q * 128 : (q + 1) * 128, :].astype(F32)
            copies.append(pltpu.make_async_copy(tall.at[r, :128, :], back.at[to, :], sems.at[r]))
            copies[-1].start()
        for copy in copies:
            copy.wait()

    @pl.when(info[7] != half)
    def _():
        copies = []
        for r in range(16):
            to = pl.ds(pl.multiple_of((r ^ mine) * 128, 128), 128)
            tall[r, :, :128] = parts[r // 4][r % 4].astype(F32)
            copies.append(pltpu.make_async_copy(tall.at[r, :, :128], front.at[:, to], sems.at[r]))
            copies[-1].start()
        for copy in copies:
            copy.wait()

def place(info, half, parts, made, width):
    smem, vmem, free = (pl.BlockSpec(memory_space=m) for m in (pltpu.SMEM, pltpu.VMEM, pl.ANY))
    shape = jax.ShapeDtypeStruct
    return pl.pallas_call(
        functools.partial(place_kernel, half),
        in_specs=[smem] + [vmem] * 4 + [free] * len(made),
        out_specs=[free] * 2,
        out_shape=[shape((16 * 128, width), F32), shape((width, 16 * 128), F32)],
        scratch_shapes=[pltpu.VMEM((16, width, width), F32), pltpu.SemaphoreType.DMA((16,))],
        input_output_aliases={5 + i: i for i in range(len(made))},
        name="place",
    )(info, *parts, *made)

def sort_kernel(half, info, *refs):
    parts, made, (tall, sems) = refs[:4], refs[-6:-2], refs[-2:]
    size = parts[0].shape[1]
    per = tall.shape[1] // size
    mine = info[6] & 15
    for r in range(16):
        to = r ^ mine
        tall[to // per, pl.ds(pl.multiple_of((to % per) * size, size), size), :] = parts[r // 4][r % 4].astype(F32)
    for top in range(2):
        @pl.when((info[7] ^ half) == top)
        def _(top=top):
            copies = [pltpu.make_async_copy(tall.at[w], made[2 * top + w], sems.at[w]) for w in range(2)]
            for copy in copies:
                copy.start()
            for copy in copies:
                copy.wait()

def sort(info, half, parts, made, width):
    smem, vmem, free = (pl.BlockSpec(memory_space=m) for m in (pltpu.SMEM, pltpu.VMEM, pl.ANY))
    shape = jax.ShapeDtypeStruct((width, width), F32)
    return pl.pallas_call(
        functools.partial(sort_kernel, half),
        in_specs=[smem] + [vmem] * 4 + [free] * len(made),
        out_specs=[free] * 4,
        out_shape=[shape] * 4,
        scratch_shapes=[pltpu.VMEM((2, width, width), F32), pltpu.SemaphoreType.DMA((2,))],
        input_output_aliases={5 + i: i for i in range(len(made))},
        name="sort",
    )(info, *parts, *made)

def mix_kernel(*refs):
    ins, outs = refs[: -4], refs[-4:]
    for k in range(4):
        outs[k][...] = added(*[term[k] for term in ins])

def mix(terms):
    block = terms[0].shape[1:]
    spec = pl.BlockSpec((4,) + block, lambda i: (0,) * (1 + len(block)))
    out = pl.BlockSpec(block, lambda i: (0,) * len(block))
    return pl.pallas_call(
        mix_kernel, grid=(1,), in_specs=[spec] * len(terms), out_specs=[out] * 4,
        out_shape=[jax.ShapeDtypeStruct(block, BF16)] * 4, name="mix",
    )(*terms)

def exchange(value, bits):
    size = lax.axis_size("dp") * lax.axis_size("blk")
    return lax.ppermute(value, ("dp", "blk"), [(i, i ^ bits) for i in range(size)])

def wait(*values):
    return lax.optimization_barrier(values)

def added(*terms):
    total = terms[0].astype(F32)
    for term in terms[1:]:
        total = total + term.astype(F32)
    return total.astype(BF16)

def local(inputs, w_query, w_key, w_value, w_out, w_in, w_back, norm1_gain, norm2_gain, final_gain, bias_table, bucket_table, prefix_len, pad_len, pooled_grad):
    rows, width = inputs.shape[1:]
    spot, far_off = lax.axis_index("blk"), lax.axis_index("dp")
    doc, core = spot // 2, spot % 2
    block = [doc * 2 + core, doc * 2 + 1 - core, (1 - doc) * 2 + core, (1 - doc) * 2 + 1 - core]
    line = [8, 16]
    further = [32 << b for b in range((lax.axis_size("dp") // 8).bit_length() - 1)]
    piece = core * 16 + doc * 4 + (far_off % 2) * 8 + (far_off // 2) % 4
    near = jnp.where(doc == 0, inputs[0], inputs[1])
    far_send = jnp.where(doc == 0, inputs[1], inputs[0])
    near, far_send = wait(near, far_send)
    far = exchange(far_send, ROW)
    near_other = exchange(near, CORE)
    slot = jnp.arange(8, dtype=jnp.int32)
    ids = jnp.zeros_like(slot)
    for i, value in enumerate([b * rows for b in block] + [piece, core, doc]):
        ids = jnp.where(slot == i, value, ids)
    gain1, gain2, gain3 = norm1_gain[None, :], norm2_gain[None, :], final_gain[None, :]
    buckets = bucket_table[None, :]
    hid_l, q_l, k_l, v_l, lines, info = prepare(ids, pad_len, prefix_len, near, near_other, w_query, w_key, w_value, gain1, bias_table, buckets)
    far, info = wait(far, info)
    far_other = exchange(far, CORE)
    (hid_r, q_r, k_r, v_r, expo, inverse, attended, send, active, slopes, turned, mixed, steep, dense_rows) = front(
        info, far, far_other, near, q_l, k_l, v_l, lines, w_query, w_key, w_value, gain1, gain2, gain3, pooled_grad, w_out, w_in, w_back)

    xy = [ROW, NEAR_X, ROW ^ NEAR_X]
    zz = [line[0], line[1], line[0] ^ line[1]]

    token, send = wait(info, send)
    got = exchange(send, CORE)
    keep, grad_mixed, grad_out_w, grad_attended, through_rows = through(token, slopes, w_in, mixed, steep, w_out, attended, active, turned, gain2)
    token, through_rows, got = wait(token, through_rows, got)

    sends = [added(keep[4 * k : 4 * k + 4], got[4 * k : 4 * k + 4]) for k in (3, 1, 2)]
    came = [exchange(s, m) for s, m in zip(sends, (xy[2], xy[0], xy[1]))]
    token, sends = wait(token, sends)
    rest_keep, rest_send, stay, leave, small = back(
        token, q_l, q_r, k_l, k_r, v_l, v_r, grad_attended, attended, inverse, expo, buckets, dense_rows, through_rows,
        hid_l, hid_r, near, near_other, far, far_other, w_query, w_key, w_value, grad_out_w)
    token, small, rest_send, leave, came = wait(token, small, rest_send, leave, came)

    rest_got = exchange(rest_send, CORE)
    hidden_got = exchange(leave, CORE)
    lines = mix([keep, got] + list(came))
    token, lines = wait(token, lines)
    took = [exchange(lines[k + 1], m) for k, m in enumerate(zz)]
    token, rest_got, hidden_got = wait(token, rest_got, hidden_got)

    count = rest_keep.shape[0] * rest_keep.shape[1]
    small = small + one_value(rest_got[count:])
    rest_got = rest_got[:count].reshape(rest_keep.shape)
    terms = two_terms(small)
    sends = [jnp.concatenate([added(rest_keep[4 * k : 4 * k + 4], rest_got[4 * k : 4 * k + 4]).reshape(-1, width), terms]) for k in (1, 2, 3)]
    token, sends = wait(token, sends)
    rest_came = [exchange(s, m) for s, m in zip(sends, xy)]
    home, away = ending(token, stay, hidden_got, near, far, grad_mixed, gain1, dense_rows)
    token, took, away = wait(token, took, away)

    whole = added(lines[0], *took)
    for bit in further:
        whole = added(whole, exchange(whole, bit))
    token, whole = wait(token, whole)
    back_line = [exchange(whole, m) for m in zz]
    away_got = exchange(away, ROW)
    token, rest_came = wait(token, rest_came)

    count = count // 4
    for part in rest_came:
        small = small + one_value(part[count:])
    rest_came = [part[:count].reshape((4,) + rest_keep.shape[1:]) for part in rest_came]
    terms = two_terms(small)
    lines = [added(rest_keep[k], rest_got[k], *[c[k] for c in rest_came]) for k in range(4)]
    sends = [jnp.concatenate([lines[k], terms]) for k in (1, 2, 3)]
    token, sends = wait(token, sends)
    took = [exchange(s, m) for s, m in zip(sends, zz)]
    token, back_line = wait(token, back_line)

    quarter = jnp.stack([whole] + back_line)
    token, quarter = wait(token, quarter)
    quarters = [exchange(quarter, m) for m in xy]
    token, took = wait(token, took)

    count = count // 4
    for part in took:
        small = small + one_value(part[count:])
    rest = added(lines[0], *[part[:count] for part in took])
    for bit in further:
        rest = added(rest, exchange(rest, bit))
        small = small + exchange(small, bit)
    token, rest = wait(token, rest)
    back_line = [exchange(rest, m) for m in zz]
    token, back_line = wait(token, back_line)
    rest_quarter = jnp.stack([rest] + back_line)
    token, rest_quarter = wait(token, rest_quarter)
    rest_quarters = [exchange(rest_quarter, m) for m in xy]

    token, quarters = wait(token, quarters)
    mine = [quarter] + quarters
    others = [exchange(value, CORE) for value in mine]
    out_big = place(token, 0, mine, [], width)
    token, out_big, others = wait(token, out_big, others)
    out_back, out_in = place(token, 1, others, out_big, width)
    token, out_back, out_in, rest_quarters, away_got = wait(token, out_back, out_in, rest_quarters, away_got)
    mine = [rest_quarter] + rest_quarters
    others = [exchange(value, CORE) for value in mine]
    out_rest = sort(token, 0, mine, [], width)
    token, out_rest, others = wait(token, out_rest, others)
    out_out, out_query, out_key, out_value = sort(token, 1, others, out_rest, width)

    pool_mine, pool_other = one_value(home[rows:])[:1], one_value(away_got[rows:])[:1]
    pooled = jnp.where(doc == 0, jnp.concatenate([pool_mine, pool_other]), jnp.concatenate([pool_other, pool_mine]))
    home, away_got = home[:rows], away_got[:rows]
    input_grad = jnp.where(doc == 0, jnp.stack([home, away_got]), jnp.stack([away_got, home]))
    return (
        pooled,
        input_grad,
        out_query,
        out_key,
        out_value,
        out_out,
        out_in,
        out_back,
        small[0],
        small[1],
        small[2],
        small[8:, :BUCKETS].T,
    )

def solution(mesh):
    data = P("dp", "blk", None)
    placed = (data,) + (P(),) * 11 + (P("dp"), P("dp"), P("dp", None))
    return jax.shard_map(local, mesh=mesh, in_specs=placed, out_specs=(P("dp", None), data) + (P(),) * 10, check_vma=False)
```

```python
import functools
import jax, jax.numpy as jnp
from jax import lax
from jax.experimental import pallas as pl
from jax.experimental.pallas import tpu as pltpu
from jax.sharding import PartitionSpec as P

F32, BF16 = jnp.float32, jnp.bfloat16
NEG = -1000000000.0
NT = (((1,), (1,)), ((), ()))
TN = (((0,), (0,)), ((), ()))
NN = (((1,), (0,)), ((), ()))

def dot(a, b, dims=NN):
    return lax.dot_general(a, b, dims, preferred_element_type=F32)

def skew(row, width, dtype=F32):
    return pltpu.roll(jnp.broadcast_to(row, (128, width)), width - 127, 1, stride=1, stride_axis=0)


BUCKETS = 32
EPS = 1e-06
CORE, ROW, NEAR_X = 1, 2, 4

def rms_scale(values):
    return lax.rsqrt(jnp.mean(values * values, axis=-1, keepdims=True) + EPS)

def norm_back(grad_out, values, scale, gain):
    weighted = grad_out * gain
    inner = jnp.mean(weighted * values, axis=-1, keepdims=True)
    grad_in = scale * weighted - scale * scale * scale * values * inner
    return grad_in, jnp.sum(grad_out * values * scale, axis=0, keepdims=True)

def two_terms(value):
    high = value.astype(BF16)
    return jnp.concatenate([high, (value - high.astype(F32)).astype(BF16)])

def one_value(terms):
    return terms[:16].astype(F32) + terms[16:32].astype(F32)

def rows_of(*values):
    count = sum(v.shape[0] for v in values)
    return jnp.concatenate(list(values) + [jnp.zeros((16 - count, values[0].shape[1]), F32)])

def prepare_kernel(ids, pads, prefixes, mine, other, wq, wk, wv, gain, bias, buckets, hidden, query, keys, values, lines, info):
    rows = mine.shape[0]
    info[0] = 4 * rows - pads[ids[6]]
    info[5] = prefixes[ids[6]]
    for to, at in enumerate((0, 1, 2, 3)):
        info[1 + to] = ids[at]
    for to, at in enumerate((4, 5, 6)):
        info[6 + to] = ids[at]
    for part, raw in enumerate((mine, other)):
        tokens = raw[...].astype(F32)
        hidden[part * rows : (part + 1) * rows, :] = (tokens * rms_scale(tokens) * gain[...]).astype(BF16)
    h = hidden[...]
    query[...] = dot(h[:rows], wq[...]).astype(BF16)
    keys[...] = dot(h, wk[...]).astype(BF16)
    values[...] = dot(h, wv[...]).astype(BF16)
    picker = jnp.where(lax.broadcasted_iota(jnp.int32, (bias.shape[0], 1), 0) == buckets[...], 1.0, 0.0).astype(BF16)
    left, total = bias[...], None
    for _ in range(3):
        part = left.astype(BF16)
        left = left - part.astype(F32)
        made = dot(part, picker, TN)
        total = made if total is None else total + made
    lines[...] = jnp.zeros_like(lines)
    lines[:, : buckets.shape[1]] = total

def prepare(ids, pads, prefixes, mine, other, wq, wk, wv, gain, bias, buckets):
    rows, width = mine.shape
    span = buckets.shape[1] + 1
    heads = bias.shape[1]
    shape = lambda n: jax.ShapeDtypeStruct((n, width), BF16)
    smem, vmem = pl.BlockSpec(memory_space=pltpu.SMEM), pl.BlockSpec(memory_space=pltpu.VMEM)
    return pl.pallas_call(
        prepare_kernel,
        in_specs=[smem] * 3 + [vmem] * 8,
        out_specs=[vmem] * 5 + [smem],
        out_shape=[shape(2 * rows), shape(rows), shape(2 * rows), shape(2 * rows),
                   jax.ShapeDtypeStruct((heads, span), F32), jax.ShapeDtypeStruct((16,), jnp.int32)],
        name="prepare",
    )(ids, pads, prefixes, mine, other, wq, wk, wv, gain, bias, buckets)

def back_pieces(to, active, low, mine):
    @pl.loop(0, active.shape[1] // 512)
    def _(group):
        made = dot(active[:, pl.ds(pl.multiple_of(group * 512, 512), 512)], low, TN).astype(BF16)
        for b in range(4):
            rows = made[b * 128 : (b + 1) * 128]
            to[(4 * group + b) ^ mine] = jnp.concatenate([rows[:, q * 128 : (q + 1) * 128] for q in range(4)])

def in_pieces(to, slopes, turned, mine):
    @pl.loop(0, slopes.shape[1] // 512)
    def _(group):
        made = dot(turned, slopes[:, pl.ds(pl.multiple_of(group * 512, 512), 512)]).astype(BF16)
        for b in range(4):
            to[(4 * group + b) ^ mine] = made[:, b * 128 : (b + 1) * 128]

def front_kernel(info, far, far_other, near, q_l, k_l, v_l, lines, wq, wk, wv, gain1, gain2, gain3, cots, wo_h, win_h, wback_h,
                 hid_o, q_o, k_o, v_o, expo_o, inv_o, att_o, send_o, active_o, slopes_o, turned_o, mixed_o, steep_o, rows,
                 hid, qs, ks, vs, inv, att, send, active, slopes, turned, mixed, steep, wo, win, wback, expo, scores, skewed, edges, sems):
    count, width = near.shape
    hidden = win.shape[1]
    step = pl.program_id(0)
    late = [pltpu.make_async_copy(a, b, sems.at[i]) for i, (a, b) in enumerate(((wo_h, wo), (win_h, win), (wback_h, wback)))]
    early = [pltpu.make_async_copy(a, b, sems.at[3 + i]) for i, (a, b) in enumerate(((hid, hid_o), (qs, q_o), (ks, k_o), (vs, v_o)))]
    dense = [pltpu.make_async_copy(a, b, sems.at[7 + i]) for i, (a, b) in enumerate((
        (inv, inv_o), (att, att_o), (mixed, mixed_o), (turned, turned_o), (active, active_o), (steep, steep_o), (slopes, slopes_o), (send, send_o)))]
    kept = lambda g: pltpu.make_async_copy(expo, expo_o.at[pl.ds(2 * g, 2)], sems.at[15])

    @pl.when(step == 0)
    def _():
        for copy in late:
            copy.start()
        for part, raw in enumerate((far, far_other)):
            tokens = raw[...].astype(F32)
            hid[part * count : (part + 1) * count, :] = (tokens * rms_scale(tokens) * gain1[...]).astype(BF16)
        h = hid[...]
        qs[...] = dot(h[:count], wq[...]).astype(BF16)
        ks[...] = dot(h, wk[...]).astype(BF16)
        vs[...] = dot(h, wv[...]).astype(BF16)
        for copy in early:
            copy.start()
        column = lax.broadcasted_iota(jnp.int32, (1, 128), 1)
        for b in range(4):
            place = info[1 + b] + lax.broadcasted_iota(jnp.int32, (count, 1), 0)
            gate = jnp.where(place < info[0], 0.0, NEG)
            for head in range(2):
                edges[head, b * count : (b + 1) * count, :] = jnp.where(column == (64 if head == 0 else 0), gate, 0.0).astype(BF16)

    @pl.when(step > 0)
    def _():
        kept(step - 1).wait()

    cols = pl.ds(pl.multiple_of(step * 128, 128), 128)
    lane = lax.broadcasted_iota(jnp.int32, (1, 128), 1)
    first = lane < 64
    limit = info[0]
    starts = [info[1 + b] for b in range(4)]
    keys = [k_l[:count, :], k_l[count:, :], ks[:count, cols], ks[count:, cols]]
    values = jnp.concatenate([v_l[...], vs[:, cols]])
    query = jnp.concatenate([q_l[...], qs[:, cols]])
    made = []
    for head in range(2):
        mine = jnp.where(first if head == 0 else lane >= 64, 1.0, 0.0).astype(BF16)
        one = jnp.where(lane == (64 if head == 0 else 0), 1.0, 0.0).astype(BF16)
        q = query * mine + one
        v = values * mine + one
        skewed[head] = skew(lines[pl.ds(2 * step + head, 1), :], lines.shape[1])
        for b in range(4):
            s = dot(q, keys[b] * mine + edges[head, b * count : (b + 1) * count, :], NT)
            for r in range(4):
                at = starts[b] - starts[2 * (r // 2)] + 896 - 128 * (r % 2)
                part = s[r * 128 : (r + 1) * 128] + skewed[head, :, pl.ds(pl.multiple_of(at, 128), 256)]
                scores[head, r * 128 : (r + 1) * 128, b * 256 : (b + 1) * 256] = part
        for r in range(4):
            rs = slice(r * 128, (r + 1) * 128)
            value = scores[head, rs, :]
            top = jnp.max(value, axis=1, keepdims=True)
            expo[head, rs, :] = jnp.exp(value - top).astype(BF16)
        acc = dot(expo[head], v)
        made.append((acc, 1.0 / (acc[:, 64:65] if head == 0 else acc[:, 0:1])))
    (a0, i0), (a1, i1) = made
    scale = jnp.where(first, i0, i1)
    att[:, cols] = (jnp.where(first, a0, a1) * scale).astype(BF16)
    inv[:, cols] = scale
    kept(step).start()

    @pl.when(step == 3)
    def _():
        for copy in late:
            copy.wait()
        dense[0].start()
        dense[1].start()
        for part, raw in enumerate((near, far)):
            spot = slice(part * count, (part + 1) * count)
            mixed[spot, :] = raw[...].astype(F32) + dot(att[spot, :], wo[...])
        dense[2].start()
        values = mixed[...]
        inner = (values * rms_scale(values) * gain2[...]).astype(BF16)
        turned[...] = inner.T
        dense[3].start()
        total = values
        for at in range(0, hidden, 512):
            lifted = jnp.maximum(dot(inner, win[:, at : at + 512]), 0.0).astype(BF16)
            active[:, at : at + 512] = lifted
            total = total + dot(lifted, wback[at : at + 512, :])
        dense[4].start()
        scale = rms_scale(total)
        place = lax.broadcasted_iota(jnp.int32, (2 * count, 1), 0)
        place = jnp.where(place < count, place + info[1], place + (info[3] - count))
        live = jnp.where((place >= info[5]) & (place < limit), 1.0, 0.0)
        pool = jnp.sum(total * scale * gain3[...] * live, axis=0, keepdims=True)
        cot = jnp.where(info[8] == 0, cots[0:1, :], cots[1:2, :]) / (limit - info[5]).astype(F32)
        slope, grad_end = norm_back(live * cot, total, scale, gain3[...])
        steep[...] = slope
        dense[5].start()
        rows[...] = jnp.concatenate([pool, grad_end, jnp.zeros((6, width), F32)])
        low = slope.astype(BF16)
        for at in range(0, hidden, 512):
            through = dot(low, wback[at : at + 512, :], NT).astype(BF16)
            slopes[:, at : at + 512] = jnp.where(active[:, at : at + 512] > 0, through, jnp.zeros_like(through))
        dense[6].start()
        mine = info[6] & 15

        @pl.when(info[7] == 0)
        def _():
            in_pieces(send, slopes, turned[...], mine)

        @pl.when(info[7] == 1)
        def _():
            back_pieces(send, active, steep[...].astype(BF16), mine)

        dense[7].start()
        for copy in early + dense:
            copy.wait()
        kept(step).wait()

def front(info, far, far_other, near, q_l, k_l, v_l, lines, wq, wk, wv, gain1, gain2, gain3, cots, wo, win, wback):
    count, width = near.shape
    hidden = win.shape[1]
    heads, span = lines.shape
    shape = jax.ShapeDtypeStruct
    smem, free = pl.BlockSpec(memory_space=pltpu.SMEM), pl.BlockSpec(memory_space=pl.ANY)
    whole = lambda *dims: pl.BlockSpec(dims, lambda g: (0,) * len(dims))
    col = lambda n: pl.BlockSpec((n, 128), lambda g: (0, g))
    outs = [shape((2 * count, width), BF16), shape((count, width), BF16), shape((2 * count, width), BF16), shape((2 * count, width), BF16),
            shape((heads, 2 * count, 4 * count), BF16), shape((2 * count, width), F32), shape((2 * count, width), BF16),
            shape((16, width, 128), BF16), shape((2 * count, hidden), BF16), shape((2 * count, hidden), BF16),
            shape((width, 2 * count), BF16), shape((2 * count, width), F32), shape((2 * count, width), F32)]
    return pl.pallas_call(
        front_kernel,
        grid=(heads // 2,),
        in_specs=[smem, whole(count, width), whole(count, width), whole(count, width), col(count), col(2 * count), col(2 * count),
                  whole(heads, span)] + [whole(width, width)] * 3 + [whole(1, width)] * 3
                 + [whole(2, width)] + [free] * 3,
        out_specs=[free] * 13 + [whole(8, width)],
        out_shape=outs + [shape((8, width), F32)],
        scratch_shapes=[pltpu.VMEM(o.shape, o.dtype) for o in outs[:4] + outs[5:]]
                       + [pltpu.VMEM(wo.shape, BF16), pltpu.VMEM(win.shape, BF16), pltpu.VMEM(wback.shape, BF16),
                          pltpu.VMEM((2, 2 * count, 4 * count), BF16), pltpu.VMEM((2, 2 * count, 4 * count), F32),
                          pltpu.VMEM((2, 128, span), F32), pltpu.VMEM((2, 4 * count, 128), BF16), pltpu.SemaphoreType.DMA((16,))],
        name="front",
    )(info, far, far_other, near, q_l, k_l, v_l, lines, wq, wk, wv, gain1, gain2, gain3, cots, wo, win, wback)

def through_kernel(info, slopes_h, win_h, mixed_h, steep_h, wo_h, att_h, active_h, turned_h, gain2,
                   keep, grad_mixed_o, grad_attended_o, grad_out_o, rows,
                   slopes, win, mixed, steep, wo, att, active, turned, grad_mixed, grad_attended, grad_out, sems):
    hidden, width = slopes.shape[1], mixed.shape[1]
    chunks = []
    for i, at in enumerate(range(0, hidden, 512)):
        for a, b, s in ((slopes_h, slopes, i), (win_h, win, 4 + i)):
            chunks.append(pltpu.make_async_copy(a.at[:, at : at + 512], b.at[:, at : at + 512], sems.at[s]))
    copies = [pltpu.make_async_copy(a, b, sems.at[8 + i]) for i, (a, b) in enumerate((
        (mixed_h, mixed), (steep_h, steep), (wo_h, wo), (att_h, att), (active_h, active), (turned_h, turned)))]
    outs = [pltpu.make_async_copy(a, b, sems.at[14 + i]) for i, (a, b) in enumerate((
        (grad_mixed, grad_mixed_o), (grad_attended, grad_attended_o), (grad_out, grad_out_o)))]
    for copy in chunks + copies[:4]:
        copy.start()

    @pl.when(info[7] == 0)
    def _():
        copies[4].start()

    @pl.when(info[7] == 1)
    def _():
        copies[5].start()

    grad_inner = None
    for i, at in enumerate(range(0, hidden, 512)):
        chunks[2 * i].wait()
        chunks[2 * i + 1].wait()
        part = dot(slopes[:, at : at + 512], win[:, at : at + 512], NT)
        grad_inner = part if grad_inner is None else grad_inner + part
    copies[0].wait()
    copies[1].wait()
    values = mixed[...]
    more, grad_two = norm_back(grad_inner, values, rms_scale(values), gain2[...])
    total = steep[...] + more
    grad_mixed[...] = total
    outs[0].start()
    low = total.astype(BF16)
    copies[2].wait()
    grad_attended[...] = dot(low, wo[...], NT).astype(BF16)
    outs[1].start()
    copies[3].wait()
    grad_out[...] = dot(att[...], low, TN).astype(BF16)
    outs[2].start()
    rows[...] = jnp.concatenate([grad_two, jnp.zeros((7, width), F32)])
    mine = info[6] & 15

    @pl.when(info[7] == 0)
    def _():
        copies[4].wait()
        back_pieces(keep, active, steep[...].astype(BF16), mine)

    @pl.when(info[7] == 1)
    def _():
        copies[5].wait()
        in_pieces(keep, slopes, turned[...], mine)

    for copy in outs:
        copy.wait()

def through(info, slopes, win, mixed, steep, wo, att, active, turned, gain2):
    n, width = mixed.shape
    smem, vmem, free = (pl.BlockSpec(memory_space=m) for m in (pltpu.SMEM, pltpu.VMEM, pl.ANY))
    shape = jax.ShapeDtypeStruct
    given = (slopes, win, mixed, steep, wo, att, active, turned)
    outs = [shape((n, width), F32), shape((n, width), BF16), shape((width, width), BF16)]
    return pl.pallas_call(
        through_kernel,
        in_specs=[smem] + [free] * 8 + [vmem],
        out_specs=[vmem] + [free] * 3 + [vmem],
        out_shape=[shape((16, width, 128), BF16)] + outs + [shape((8, width), F32)],
        scratch_shapes=[pltpu.VMEM(g.shape, g.dtype) for g in given] + [pltpu.VMEM(o.shape, o.dtype) for o in outs] + [pltpu.SemaphoreType.DMA((17,))],
        name="through",
    )(info, *given, gain2)

CLASS = {(0, 0): 0, (1, 2): 0, (0, 1): 1, (1, 3): 1, (0, 2): 2, (0, 3): 3, (1, 0): 4, (1, 1): 5}

def back_kernel(info, ql, qr, kl, kr, vl, vr, gout, out, inv, expo, buckets, dense_rows, through_rows,
                hid_l_h, hid_r_h, near_h, near_other_h, far_h, far_other_h, wq_h, wk_h, wv_h, grad_out_h,
                keep_o, send_o, stay_o, leave_o, small,
                hid_l, hid_r, near, near_other, far, far_other, wq, wk, wv, made,
                keep, send, stay, leave, dq, dk, dv, offsets, sums, acc, slopes, sems):
    count, width = near.shape
    step = pl.program_id(0)
    pairs = width // 128
    late = [pltpu.make_async_copy(a, b, sems.at[i]) for i, (a, b) in enumerate((
        (hid_l_h, hid_l), (hid_r_h, hid_r), (near_h, near), (near_other_h, near_other), (far_h, far), (far_other_h, far_other),
        (wq_h, wq), (wk_h, wk), (wv_h, wv), (grad_out_h, made.at[0:width])))]
    done = [pltpu.make_async_copy(a, b, sems.at[10 + i]) for i, (a, b) in enumerate(((send, send_o), (keep, keep_o), (leave, leave_o), (stay, stay_o)))]

    @pl.when(step == 0)
    def _():
        for copy in late:
            copy.start()

    cols = pl.ds(pl.multiple_of(step * 128, 128), 128)
    lane = lax.broadcasted_iota(jnp.int32, (1, 128), 1)
    starts = [info[1 + b] for b in range(4)]
    keys = jnp.concatenate([kl[...], kr[...]])
    values = jnp.concatenate([vl[...], vr[...]])
    query = jnp.concatenate([ql[...], qr[...]])
    scaled = gout[...].astype(F32) * inv[...]
    prod = scaled * out[...].astype(F32)
    low = scaled.astype(BF16)
    query_t, low_t = query.T, low.T
    grads_q, grads_k, grads_v = None, [], []
    for head in range(2):
        mine = (lane < 64) if head == 0 else (lane >= 64)
        base = 64 if head == 0 else 0
        pick = jnp.where(mine, 1.0, 0.0).astype(BF16)
        delta = jnp.sum(jnp.where(mine, prod, 0.0), axis=1, keepdims=True)
        high = delta.astype(BF16).astype(F32)
        extra = jnp.where(lane == base, high, jnp.where(lane == base + 1, delta - high, 0.0)).astype(BF16)
        grad = low * pick + extra
        minus = jnp.where((lane == base) | (lane == base + 1), -1.0, 0.0).astype(BF16)
        for b in range(4):
            spot = slice(b * count, (b + 1) * count)
            ds = dot(grad, values[spot] * pick + minus, NT) * expo[head, :, spot].astype(F32)
            slopes[head, :, spot] = ds.astype(BF16)
            for chunk in range(2):
                upper, lower = (ds[chunk * count + r * 128 : chunk * count + (r + 1) * 128] for r in range(2))
                group = CLASS[chunk, b]
                block = jnp.concatenate([lower[:, :128], lower[:, 128:] + upper[:, :128], upper[:, 128:]], axis=1)
                if (chunk, b) in ((1, 2), (1, 3)):
                    block = block + sums[head, group]
                sums[head, group] = block
        part = dot(slopes[head], keys * pick)
        grads_q = part if grads_q is None else grads_q + part
        half = slice(head * 64, (head + 1) * 64)
        grads_k.append(dot(query_t[half], slopes[head]))
        grads_v.append(dot(low_t[half], expo[head]))
    dq[:, cols] = grads_q.astype(BF16)
    dk[:, cols] = jnp.concatenate(grads_k).astype(BF16).T
    dv[:, cols] = jnp.concatenate(grads_v).astype(BF16).T
    for head in range(2):
        acc[head] = jnp.zeros(acc.shape[1:], F32)
        for (chunk, b), group in CLASS.items():
            if (chunk, b) not in ((1, 2), (1, 3)):
                at = starts[b] - starts[2 * chunk] + 768
                to = pl.ds(pl.multiple_of(at, 128), 384)
                acc[head, :, to] += sums[head, group]
        rest = acc[head]
        n = 64
        while n >= 8:
            rest = rest[:n] + pltpu.roll(rest[n:], 2048 - n, 1)
            n //= 2
        line = rest[7:8]
        for r in range(6, -1, -1):
            line = rest[r : r + 1] + pltpu.roll(line, 2047, 1)
        offsets[pl.ds(2 * step + head, 1), :] = pltpu.roll(line, 127, 1)

    @pl.when(step == pairs - 1)
    def _():
        for copy in late:
            copy.wait()
        made[width : 2 * width, :] = (dot(hid_l[:count, :], dq[:count, :], TN) + dot(hid_r[:count, :], dq[count:, :], TN)).astype(BF16)
        for at, grads in ((2 * width, dk), (3 * width, dv)):
            made[at : at + width, :] = (dot(hid_l[...], grads[: 2 * count, :], TN) + dot(hid_r[...], grads[2 * count :, :], TN)).astype(BF16)
        me = info[6]
        size = made.shape[0] // 32

        @pl.loop(0, 16)
        def _(r):
            keep[r] = made[pl.ds(pl.multiple_of((r ^ me) * size, size), size), :]
            send[pl.ds(pl.multiple_of(r * size, size), size), :] = made[pl.ds(pl.multiple_of(((r + 16) ^ me) * size, size), size), :]

        gain = jnp.zeros((1, width), F32)
        for b, raw in enumerate((near, near_other, far, far_other)):
            spot = slice(b * count, (b + 1) * count)
            grad = dot(dk[spot, :], wk[...], NT) + dot(dv[spot, :], wv[...], NT)
            half = slice((b // 2) * count, (b // 2 + 1) * count)
            if b % 2 == 0:
                grad = grad + dot(dq[half, :], wq[...], NT)
                stay[half, :] = grad
            else:
                leave[half, :] = grad.astype(BF16)
            tokens = raw[...].astype(F32)
            gain = gain + jnp.sum(grad * (tokens * rms_scale(tokens)), axis=0, keepdims=True)
        leave[2 * count :, :] = two_terms(rows_of(dense_rows[0:1, :]))
        picker = jnp.where(lax.broadcasted_iota(jnp.int32, (128, 1), 0) == buckets[...], 1.0, 0.0).astype(BF16)
        left = offsets[...][:, : buckets.shape[1]]
        bias = None
        for _ in range(3):
            part = left.astype(BF16)
            left = left - part.astype(F32)
            bias = dot(part, picker, NT) if bias is None else bias + dot(part, picker, NT)
        bias = jnp.concatenate([bias, jnp.zeros((bias.shape[0], width - 128), F32)], axis=1)
        total = jnp.concatenate([gain, through_rows[0:1, :], dense_rows[1:2, :], jnp.zeros((5, width), F32), bias])
        small[...] = total
        send[16 * size :, :] = two_terms(total)
        for copy in done:
            copy.start()
        for copy in done:
            copy.wait()

def back(info, ql, qr, kl, kr, vl, vr, gout, out, inv, expo, buckets, dense_rows, through_rows,
         hid_l, hid_r, near, near_other, far, far_other, wq, wk, wv, grad_out):
    count, width = near.shape
    smem, free = pl.BlockSpec(memory_space=pltpu.SMEM), pl.BlockSpec(memory_space=pl.ANY)
    whole = lambda *dims: pl.BlockSpec(dims, lambda g: (0,) * len(dims))
    col = lambda n: pl.BlockSpec((n, 128), lambda g: (0, g))
    shape = jax.ShapeDtypeStruct
    size = 4 * width // 32
    outs = [shape((16, size, width), BF16), shape((16 * size + 32, width), BF16), shape((2 * count, width), F32), shape((2 * count + 32, width), BF16)]
    given = (hid_l, hid_r, near, near_other, far, far_other, wq, wk, wv)
    return pl.pallas_call(
        back_kernel,
        grid=(width // 128,),
        in_specs=[smem, col(count), col(count)] + [col(2 * count)] * 7 + [pl.BlockSpec((2, 2 * count, 4 * count), lambda g: (g, 0, 0)),
                  whole(*buckets.shape), whole(8, width), whole(8, width)] + [free] * 10,
        out_specs=[free] * 4 + [whole(16, width)],
        out_shape=outs + [shape((16, width), F32)],
        scratch_shapes=[pltpu.VMEM(g.shape, BF16) for g in given] + [pltpu.VMEM((4 * width, width), BF16)]
                       + [pltpu.VMEM(o.shape, o.dtype) for o in outs]
                       + [pltpu.VMEM((2 * count, width), BF16), pltpu.VMEM((4 * count, width), BF16), pltpu.VMEM((4 * count, width), BF16),
                          pltpu.VMEM((8, 2048), F32), pltpu.VMEM((2, 6, 128, 384), F32), pltpu.VMEM((2, 128, 2048), F32),
                          pltpu.VMEM((2, 2 * count, 4 * count), BF16), pltpu.SemaphoreType.DMA((14,))],
        name="back",
    )(info, ql, qr, kl, kr, vl, vr, gout, out, inv, expo, buckets, dense_rows, through_rows, *given, grad_out)

def ending_kernel(info, stay, came, near, far, grad_mixed, gain, dense_rows, home, away):
    count, width = near.shape
    for part, raw in enumerate((near, far)):
        spot = slice(part * count, (part + 1) * count)
        tokens = raw[...].astype(F32)
        grad = stay[spot, :] + came[spot, :].astype(F32)
        more, _ = norm_back(grad, tokens, rms_scale(tokens), gain[...])
        value = (grad_mixed[spot, :] + more).astype(BF16)
        if part == 0:
            home[:count, :] = value
        else:
            away[:count, :] = value
    alive = (info[0] - info[5]).astype(F32)
    pool = two_terms((rows_of(dense_rows[0:1, :]) + one_value(came[2 * count :, :])) / alive)
    home[count:, :] = pool
    away[count:, :] = pool

def ending(info, stay, came, near, far, grad_mixed, gain, dense_rows):
    count, width = near.shape
    smem, vmem = pl.BlockSpec(memory_space=pltpu.SMEM), pl.BlockSpec(memory_space=pltpu.VMEM)
    shape = jax.ShapeDtypeStruct((count + 32, width), BF16)
    return pl.pallas_call(
        ending_kernel, in_specs=[smem] + [vmem] * 7, out_specs=[vmem] * 2, out_shape=[shape, shape], name="ending"
    )(info, stay, came, near, far, grad_mixed, gain, dense_rows)

def place_kernel(firsts, info, *refs):
    parts, (back, front, rows, columns, sems) = refs[: len(firsts)], refs[-5:]
    pieces = [(part, i, first + i) for part, first in zip(parts, firsts) for i in range(part.shape[0])]
    mine = info[6] & 15
    for side in range(2):
        @pl.when(info[7] == side)
        def _(side=side):
            copies = []
            for n, (part, i, r) in enumerate(pieces):
                to = pl.ds(pl.multiple_of(((r & 15) ^ mine) * 128, 128), 128)
                if (r >= 16) == (side == 1):
                    for q in range(4):
                        rows[n, :, q * 128 : (q + 1) * 128] = part[i, q * 128 : (q + 1) * 128, :].astype(F32)
                    copies.append(pltpu.make_async_copy(rows.at[n], back.at[to, :], sems.at[n]))
                else:
                    columns[n] = part[i].astype(F32)
                    copies.append(pltpu.make_async_copy(columns.at[n], front.at[:, to], sems.at[n]))
                copies[-1].start()
            for copy in copies:
                copy.wait()

def place(info, parts, made, width):
    smem, vmem, free = (pl.BlockSpec(memory_space=m) for m in (pltpu.SMEM, pltpu.VMEM, pl.ANY))
    shape = jax.ShapeDtypeStruct
    count = sum(p.shape[0] for _, p in parts)
    return pl.pallas_call(
        functools.partial(place_kernel, [first for first, _ in parts]),
        in_specs=[smem] + [vmem] * len(parts) + [free] * len(made),
        out_specs=[free] * 2,
        out_shape=[shape((16 * 128, width), F32), shape((width, 16 * 128), F32)],
        scratch_shapes=[pltpu.VMEM((count, 128, width), F32), pltpu.VMEM((count, width, 128), F32), pltpu.SemaphoreType.DMA((count,))],
        input_output_aliases={1 + len(parts) + i: i for i in range(len(made))},
        name="place",
    )(info, *[p for _, p in parts], *made)

def sort_kernel(firsts, info, *refs):
    parts, made, (tall, sems) = refs[: len(firsts)], refs[-6:-2], refs[-2:]
    pieces = [(part, i, first + i) for part, first in zip(parts, firsts) for i in range(part.shape[0])]
    size = parts[0].shape[1]
    mine = info[6]
    for n, (part, i, r) in enumerate(pieces):
        tall[n] = part[i].astype(F32)
    for top in range(4):
        @pl.when((mine >> 3) == top)
        def _(top=top):
            copies = []
            for n, (part, i, r) in enumerate(pieces):
                to = pl.ds(pl.multiple_of(((r ^ mine) & 7) * size, size), size)
                copies.append(pltpu.make_async_copy(tall.at[n], made[top ^ (r >> 3)].at[to, :], sems.at[n]))
                copies[-1].start()
            for copy in copies:
                copy.wait()

def sort(info, parts, made, width):
    smem, vmem, free = (pl.BlockSpec(memory_space=m) for m in (pltpu.SMEM, pltpu.VMEM, pl.ANY))
    shape = jax.ShapeDtypeStruct((width, width), F32)
    count = sum(p.shape[0] for _, p in parts)
    return pl.pallas_call(
        functools.partial(sort_kernel, [first for first, _ in parts]),
        in_specs=[smem] + [vmem] * len(parts) + [free] * len(made),
        out_specs=[free] * 4,
        out_shape=[shape] * 4,
        scratch_shapes=[pltpu.VMEM((count,) + parts[0][1].shape[1:], F32), pltpu.SemaphoreType.DMA((count,))],
        input_output_aliases={1 + len(parts) + i: i for i in range(len(made))},
        name="sort",
    )(info, *[p for _, p in parts], *made)

def spread_kernel(keep, got, out):
    out[...] = added(keep[...], got[...])

def spread(keep, got, k):
    block = (1,) + keep.shape[1:]
    spec = pl.BlockSpec(block, lambda i: (4 * k + i, 0, 0))
    return pl.pallas_call(
        spread_kernel, grid=(4,), in_specs=[spec, spec], out_specs=pl.BlockSpec(block, lambda i: (i, 0, 0)),
        out_shape=jax.ShapeDtypeStruct((4,) + keep.shape[1:], BF16), name="spread",
    )(keep, got)

def mix_kernel(*refs):
    ins, outs = refs[: -4], refs[-4:]
    for k in range(4):
        outs[k][...] = added(*[term[k] for term in ins])

def mix(terms):
    block = terms[0].shape[1:]
    spec = pl.BlockSpec((4,) + block, lambda i: (0,) * (1 + len(block)))
    out = pl.BlockSpec(block, lambda i: (0,) * len(block))
    return pl.pallas_call(
        mix_kernel, grid=(1,), in_specs=[spec] * len(terms), out_specs=[out] * 4,
        out_shape=[jax.ShapeDtypeStruct(block, BF16)] * 4, name="mix",
    )(*terms)

def exchange(value, bits):
    size = lax.axis_size("dp") * lax.axis_size("blk")
    return lax.ppermute(value, ("dp", "blk"), [(i, i ^ bits) for i in range(size)])

def wait(*values):
    return lax.optimization_barrier(values)

def added(*terms):
    total = terms[0].astype(F32)
    for term in terms[1:]:
        total = total + term.astype(F32)
    return total.astype(BF16)

def local(inputs, w_query, w_key, w_value, w_out, w_in, w_back, norm1_gain, norm2_gain, final_gain, bias_table, bucket_table, prefix_len, pad_len, pooled_grad):
    rows, width = inputs.shape[1:]
    spot, far_off = lax.axis_index("blk"), lax.axis_index("dp")
    doc, core = spot // 2, spot % 2
    block = [doc * 2 + core, doc * 2 + 1 - core, (1 - doc) * 2 + core, (1 - doc) * 2 + 1 - core]
    line = [8, 16]
    further = [32 << b for b in range((lax.axis_size("dp") // 8).bit_length() - 1)]
    piece = core * 16 + doc * 4 + (far_off % 2) * 8 + (far_off // 2) % 4
    near = jnp.where(doc == 0, inputs[0], inputs[1])
    far_send = jnp.where(doc == 0, inputs[1], inputs[0])
    near, far_send = wait(near, far_send)
    far = exchange(far_send, ROW)
    near_other = exchange(near, CORE)
    slot = jnp.arange(8, dtype=jnp.int32)
    ids = jnp.zeros_like(slot)
    for i, value in enumerate([b * rows for b in block] + [piece, core, doc]):
        ids = jnp.where(slot == i, value, ids)
    gain1, gain2, gain3 = norm1_gain[None, :], norm2_gain[None, :], final_gain[None, :]
    buckets = bucket_table[None, :]
    hid_l, q_l, k_l, v_l, lines, info = prepare(ids, pad_len, prefix_len, near, near_other, w_query, w_key, w_value, gain1, bias_table, buckets)
    far, info = wait(far, info)
    far_other = exchange(far, CORE)
    (hid_r, q_r, k_r, v_r, expo, inverse, attended, send, active, slopes, turned, mixed, steep, dense_rows) = front(
        info, far, far_other, near, q_l, k_l, v_l, lines, w_query, w_key, w_value, gain1, gain2, gain3, pooled_grad, w_out, w_in, w_back)

    xy = [ROW, NEAR_X, ROW ^ NEAR_X]
    zz = [line[0], line[1], line[0] ^ line[1]]

    token, send = wait(info, send)
    got = exchange(send, CORE)
    keep, grad_mixed, grad_attended, grad_out_w, through_rows = through(token, slopes, w_in, mixed, steep, w_out, attended, active, turned, gain2)
    token, through_rows, got = wait(token, through_rows, got)

    sends = [spread(keep, got, k) for k in (3, 1, 2)]
    came = [exchange(s, m) for s, m in zip(sends, (xy[2], xy[0], xy[1]))]
    token, sends = wait(token, sends)
    rest_keep, rest_send, stay, leave, small = back(
        token, q_l, q_r, k_l, k_r, v_l, v_r, grad_attended, attended, inverse, expo, buckets, dense_rows, through_rows,
        hid_l, hid_r, near, near_other, far, far_other, w_query, w_key, w_value, grad_out_w)
    token, small, rest_send, leave, came = wait(token, small, rest_send, leave, came)

    rest_got = exchange(rest_send, CORE)
    hidden_got = exchange(leave, CORE)
    lines = mix([keep, got] + list(came))
    token, lines = wait(token, lines)
    took = [exchange(lines[k + 1], m) for k, m in enumerate(zz)]
    token, rest_got, hidden_got = wait(token, rest_got, hidden_got)

    count = rest_keep.shape[0] * rest_keep.shape[1]
    small = small + one_value(rest_got[count:])
    rest_got = rest_got[:count].reshape(rest_keep.shape)
    terms = two_terms(small)
    sends = [jnp.concatenate([added(rest_keep[4 * k : 4 * k + 4], rest_got[4 * k : 4 * k + 4]).reshape(-1, width), terms]) for k in (1, 2, 3)]
    token, sends = wait(token, sends)
    rest_came = [exchange(s, m) for s, m in zip(sends, xy)]
    home, away = ending(token, stay, hidden_got, near, far, grad_mixed, gain1, dense_rows)
    token, took, away = wait(token, took, away)

    whole = added(lines[0], *took)
    for bit in further:
        whole = added(whole, exchange(whole, bit))
    token, whole = wait(token, whole)
    back_line = [exchange(whole, m) for m in zz]
    away_got = exchange(away, ROW)
    token, rest_came = wait(token, rest_came)

    count = count // 4
    for part in rest_came:
        small = small + one_value(part[count:])
    rest_came = [part[:count].reshape((4,) + rest_keep.shape[1:]) for part in rest_came]
    terms = two_terms(small)
    lines = [added(rest_keep[k], rest_got[k], *[c[k] for c in rest_came]) for k in range(4)]
    sends = [jnp.concatenate([lines[k], terms]) for k in (1, 2, 3)]
    token, sends = wait(token, sends)
    took = [exchange(s, m) for s, m in zip(sends, zz)]
    token, back_line = wait(token, back_line)

    quarter = jnp.stack([whole] + back_line)
    token, quarter, away_got = wait(token, quarter, away_got)
    from_y, from_x = exchange(quarter, ROW), exchange(quarter, NEAR_X)
    token, took = wait(token, took)

    count = count // 4
    for part in took:
        small = small + one_value(part[count:])
    rest = added(lines[0], *[part[:count] for part in took])
    for bit in further:
        rest = added(rest, exchange(rest, bit))
        small = small + exchange(small, bit)
    token, rest = wait(token, rest)
    back_line = [exchange(rest, m) for m in zz]
    token, back_line, from_y, from_x = wait(token, back_line, from_y, from_x)
    fourth = jnp.stack([rest] + back_line)

    sends = [from_x[:2], from_y[2:], fourth, fourth]
    token, sends = wait(token, sends)
    far_a, far_b, fourth_y, fourth_x = (exchange(s, m) for s, m in zip(sends, (ROW, NEAR_X, ROW, NEAR_X)))
    grads = place(token, [(0, quarter), (4, from_y), (8, from_x)], [], width)
    token, grads, quarter, from_y, from_x = wait(token, grads, quarter, from_y, from_x)
    others = [exchange(value, CORE) for value in (quarter, from_y, from_x)]
    token, grads, others, far_a, far_b, fourth_y, fourth_x = wait(token, grads, others, far_a, far_b, fourth_y, fourth_x)

    sends = [fourth_x[:2], fourth_y[2:], far_a, far_b]
    token, sends = wait(token, sends)
    last_a, last_b, other_a, other_b = (exchange(s, m) for s, m in zip(sends, (ROW, NEAR_X, CORE, CORE)))
    grads = place(token, [(12, far_a), (14, far_b), (16, others[0]), (20, others[1]), (24, others[2])], grads, width)
    token, grads, fourth, fourth_y, fourth_x = wait(token, grads, fourth, fourth_y, fourth_x)
    pair = [exchange(value, CORE) for value in (fourth, fourth_y, fourth_x)]
    token, grads, last_a, last_b, other_a, other_b, pair = wait(token, grads, last_a, last_b, other_a, other_b, pair)

    ends = [exchange(last_a, CORE), exchange(last_b, CORE)]
    made = sort(token, [(0, fourth), (4, fourth_y), (8, fourth_x), (12, last_a), (14, last_b), (16, pair[0]), (20, pair[1]), (24, pair[2])], [], width)
    out_back, out_in = place(token, [(28, other_a), (30, other_b)], grads, width)
    token, made, ends = wait(token, made, ends)
    out_out, out_query, out_key, out_value = sort(token, [(28, ends[0]), (30, ends[1])], made, width)

    pool_mine, pool_other = one_value(home[rows:])[:1], one_value(away_got[rows:])[:1]
    pooled = jnp.where(doc == 0, jnp.concatenate([pool_mine, pool_other]), jnp.concatenate([pool_other, pool_mine]))
    home, away_got = home[:rows], away_got[:rows]
    input_grad = jnp.where(doc == 0, jnp.stack([home, away_got]), jnp.stack([away_got, home]))
    return (
        pooled,
        input_grad,
        out_query,
        out_key,
        out_value,
        out_out,
        out_in,
        out_back,
        small[0],
        small[1],
        small[2],
        small[8:, :BUCKETS].T,
    )

def solution(mesh):
    data = P("dp", "blk", None)
    placed = (data,) + (P(),) * 11 + (P("dp"), P("dp"), P("dp", None))
    return jax.shard_map(local, mesh=mesh, in_specs=placed, out_specs=(P("dp", None), data) + (P(),) * 10, check_vma=False)
```

```python
import functools
import jax, jax.numpy as jnp
from jax import lax
from jax.experimental import pallas as pl
from jax.experimental.pallas import tpu as pltpu
from jax.sharding import PartitionSpec as P

F32, BF16 = jnp.float32, jnp.bfloat16
NEG = -1000000000.0
NT = (((1,), (1,)), ((), ()))
TN = (((0,), (0,)), ((), ()))
NN = (((1,), (0,)), ((), ()))

def dot(a, b, dims=NN):
    return lax.dot_general(a, b, dims, preferred_element_type=F32)

def skew(row, width, dtype=F32):
    return pltpu.roll(jnp.broadcast_to(row, (128, width)), width - 127, 1, stride=1, stride_axis=0)


BUCKETS = 32
EPS = 1e-06
CORE, ROW, NEAR_X = 1, 2, 4

def rms_scale(values):
    return lax.rsqrt(jnp.mean(values * values, axis=-1, keepdims=True) + EPS)

def norm_back(grad_out, values, scale, gain):
    weighted = grad_out * gain
    inner = jnp.mean(weighted * values, axis=-1, keepdims=True)
    grad_in = scale * weighted - scale * scale * scale * values * inner
    return grad_in, jnp.sum(grad_out * values * scale, axis=0, keepdims=True)

def two_terms(value):
    high = value.astype(BF16)
    return jnp.concatenate([high, (value - high.astype(F32)).astype(BF16)])

def one_value(terms):
    return terms[:16].astype(F32) + terms[16:32].astype(F32)

def rows_of(*values):
    count = sum(v.shape[0] for v in values)
    return jnp.concatenate(list(values) + [jnp.zeros((16 - count, values[0].shape[1]), F32)])

def prepare_kernel(ids, pads, prefixes, mine, other, wq, wk, wv, gain, bias, buckets, hidden, query, keys, values, lines, info):
    rows = mine.shape[0]
    info[0] = 4 * rows - pads[ids[6]]
    info[5] = prefixes[ids[6]]
    for to, at in enumerate((0, 1, 2, 3)):
        info[1 + to] = ids[at]
    for to, at in enumerate((4, 5, 6)):
        info[6 + to] = ids[at]
    for part, raw in enumerate((mine, other)):
        tokens = raw[...].astype(F32)
        hidden[part * rows : (part + 1) * rows, :] = (tokens * rms_scale(tokens) * gain[...]).astype(BF16)
    h = hidden[...]
    query[...] = dot(h[:rows], wq[...]).astype(BF16)
    keys[...] = dot(h, wk[...]).astype(BF16)
    values[...] = dot(h, wv[...]).astype(BF16)
    picker = jnp.where(lax.broadcasted_iota(jnp.int32, (bias.shape[0], 1), 0) == buckets[...], 1.0, 0.0).astype(BF16)
    left, total = bias[...], None
    for _ in range(3):
        part = left.astype(BF16)
        left = left - part.astype(F32)
        made = dot(part, picker, TN)
        total = made if total is None else total + made
    lines[...] = jnp.zeros_like(lines)
    lines[:, : buckets.shape[1]] = total

def prepare(ids, pads, prefixes, mine, other, wq, wk, wv, gain, bias, buckets):
    rows, width = mine.shape
    span = buckets.shape[1] + 1
    heads = bias.shape[1]
    shape = lambda n: jax.ShapeDtypeStruct((n, width), BF16)
    smem, vmem = pl.BlockSpec(memory_space=pltpu.SMEM), pl.BlockSpec(memory_space=pltpu.VMEM)
    return pl.pallas_call(
        prepare_kernel,
        in_specs=[smem] * 3 + [vmem] * 8,
        out_specs=[vmem] * 5 + [smem],
        out_shape=[shape(2 * rows), shape(rows), shape(2 * rows), shape(2 * rows),
                   jax.ShapeDtypeStruct((heads, span), F32), jax.ShapeDtypeStruct((16,), jnp.int32)],
        name="prepare",
    )(ids, pads, prefixes, mine, other, wq, wk, wv, gain, bias, buckets)

def back_pieces(to, active, low, mine):
    @pl.loop(0, active.shape[1] // 512)
    def _(group):
        made = dot(active[:, pl.ds(pl.multiple_of(group * 512, 512), 512)], low, TN).astype(BF16)
        for b in range(4):
            rows = made[b * 128 : (b + 1) * 128]
            to[(4 * group + b) ^ mine] = jnp.concatenate([rows[:, q * 128 : (q + 1) * 128] for q in range(4)])

def in_pieces(to, slopes, turned, mine):
    @pl.loop(0, slopes.shape[1] // 512)
    def _(group):
        made = dot(turned, slopes[:, pl.ds(pl.multiple_of(group * 512, 512), 512)]).astype(BF16)
        for b in range(4):
            to[(4 * group + b) ^ mine] = made[:, b * 128 : (b + 1) * 128]

def front_kernel(info, far, far_other, near, q_l, k_l, v_l, lines, wq, wk, wv, gain1, gain2, gain3, cots, wo_h, win_h, wback_h,
                 hid_o, q_o, k_o, v_o, expo_o, inv_o, att_o, send_o, active_o, slopes_o, turned_o, mixed_o, steep_o, rows,
                 hid, qs, ks, vs, inv, att, send, active, slopes, turned, mixed, steep, wo, win, wback, expo, scores, skewed, edges, sems):
    count, width = near.shape
    hidden = win.shape[1]
    step = pl.program_id(0)
    late = [pltpu.make_async_copy(a, b, sems.at[i]) for i, (a, b) in enumerate(((wo_h, wo), (win_h, win), (wback_h, wback)))]
    early = [pltpu.make_async_copy(a, b, sems.at[3 + i]) for i, (a, b) in enumerate(((hid, hid_o), (qs, q_o), (ks, k_o), (vs, v_o)))]
    dense = [pltpu.make_async_copy(a, b, sems.at[7 + i]) for i, (a, b) in enumerate((
        (inv, inv_o), (att, att_o), (mixed, mixed_o), (turned, turned_o), (active, active_o), (steep, steep_o), (slopes, slopes_o), (send, send_o)))]
    kept = lambda g: pltpu.make_async_copy(expo, expo_o.at[pl.ds(2 * g, 2)], sems.at[15])

    @pl.when(step == 0)
    def _():
        for copy in late:
            copy.start()
        for part, raw in enumerate((far, far_other)):
            tokens = raw[...].astype(F32)
            hid[part * count : (part + 1) * count, :] = (tokens * rms_scale(tokens) * gain1[...]).astype(BF16)
        h = hid[...]
        qs[...] = dot(h[:count], wq[...]).astype(BF16)
        ks[...] = dot(h, wk[...]).astype(BF16)
        vs[...] = dot(h, wv[...]).astype(BF16)
        for copy in early:
            copy.start()
        column = lax.broadcasted_iota(jnp.int32, (1, 128), 1)
        for b in range(4):
            place = info[1 + b] + lax.broadcasted_iota(jnp.int32, (count, 1), 0)
            gate = jnp.where(place < info[0], 0.0, NEG)
            for head in range(2):
                edges[head, b * count : (b + 1) * count, :] = jnp.where(column == (64 if head == 0 else 0), gate, 0.0).astype(BF16)

    @pl.when(step > 0)
    def _():
        kept(step - 1).wait()

    cols = pl.ds(pl.multiple_of(step * 128, 128), 128)
    lane = lax.broadcasted_iota(jnp.int32, (1, 128), 1)
    first = lane < 64
    limit = info[0]
    starts = [info[1 + b] for b in range(4)]
    keys = [k_l[:count, :], k_l[count:, :], ks[:count, cols], ks[count:, cols]]
    values = jnp.concatenate([v_l[...], vs[:, cols]])
    query = jnp.concatenate([q_l[...], qs[:, cols]])
    made = []
    for head in range(2):
        mine = jnp.where(first if head == 0 else lane >= 64, 1.0, 0.0).astype(BF16)
        one = jnp.where(lane == (64 if head == 0 else 0), 1.0, 0.0).astype(BF16)
        q = query * mine + one
        v = values * mine + one
        skewed[head] = skew(lines[pl.ds(2 * step + head, 1), :], lines.shape[1])
        for b in range(4):
            s = dot(q, keys[b] * mine + edges[head, b * count : (b + 1) * count, :], NT)
            for r in range(4):
                at = starts[b] - starts[2 * (r // 2)] + 896 - 128 * (r % 2)
                part = s[r * 128 : (r + 1) * 128] + skewed[head, :, pl.ds(pl.multiple_of(at, 128), 256)]
                scores[head, r * 128 : (r + 1) * 128, b * 256 : (b + 1) * 256] = part
        for r in range(4):
            rs = slice(r * 128, (r + 1) * 128)
            value = scores[head, rs, :]
            top = jnp.max(value, axis=1, keepdims=True)
            expo[head, rs, :] = jnp.exp(value - top).astype(BF16)
        acc = dot(expo[head], v)
        made.append((acc, 1.0 / (acc[:, 64:65] if head == 0 else acc[:, 0:1])))
    (a0, i0), (a1, i1) = made
    scale = jnp.where(first, i0, i1)
    att[:, cols] = (jnp.where(first, a0, a1) * scale).astype(BF16)
    inv[:, cols] = scale
    kept(step).start()

    @pl.when(step == 3)
    def _():
        for copy in late:
            copy.wait()
        dense[0].start()
        dense[1].start()
        for part, raw in enumerate((near, far)):
            spot = slice(part * count, (part + 1) * count)
            mixed[spot, :] = raw[...].astype(F32) + dot(att[spot, :], wo[...])
        dense[2].start()
        values = mixed[...]
        inner = (values * rms_scale(values) * gain2[...]).astype(BF16)
        turned[...] = inner.T
        dense[3].start()
        total = values
        for at in range(0, hidden, 512):
            lifted = jnp.maximum(dot(inner, win[:, at : at + 512]), 0.0).astype(BF16)
            active[:, at : at + 512] = lifted
            total = total + dot(lifted, wback[at : at + 512, :])
        dense[4].start()
        scale = rms_scale(total)
        place = lax.broadcasted_iota(jnp.int32, (2 * count, 1), 0)
        place = jnp.where(place < count, place + info[1], place + (info[3] - count))
        live = jnp.where((place >= info[5]) & (place < limit), 1.0, 0.0)
        pool = jnp.sum(total * scale * gain3[...] * live, axis=0, keepdims=True)
        cot = jnp.where(info[8] == 0, cots[0:1, :], cots[1:2, :]) / (limit - info[5]).astype(F32)
        slope, grad_end = norm_back(live * cot, total, scale, gain3[...])
        steep[...] = slope
        dense[5].start()
        rows[...] = jnp.concatenate([pool, grad_end, jnp.zeros((6, width), F32)])
        low = slope.astype(BF16)
        for at in range(0, hidden, 512):
            through = dot(low, wback[at : at + 512, :], NT).astype(BF16)
            slopes[:, at : at + 512] = jnp.where(active[:, at : at + 512] > 0, through, jnp.zeros_like(through))
        dense[6].start()
        mine = info[6] & 15

        @pl.when(info[7] == 0)
        def _():
            in_pieces(send, slopes, turned[...], mine)

        @pl.when(info[7] == 1)
        def _():
            back_pieces(send, active, steep[...].astype(BF16), mine)

        dense[7].start()
        for copy in early + dense:
            copy.wait()
        kept(step).wait()

def front(info, far, far_other, near, q_l, k_l, v_l, lines, wq, wk, wv, gain1, gain2, gain3, cots, wo, win, wback):
    count, width = near.shape
    hidden = win.shape[1]
    heads, span = lines.shape
    shape = jax.ShapeDtypeStruct
    smem, free = pl.BlockSpec(memory_space=pltpu.SMEM), pl.BlockSpec(memory_space=pl.ANY)
    whole = lambda *dims: pl.BlockSpec(dims, lambda g: (0,) * len(dims))
    col = lambda n: pl.BlockSpec((n, 128), lambda g: (0, g))
    outs = [shape((2 * count, width), BF16), shape((count, width), BF16), shape((2 * count, width), BF16), shape((2 * count, width), BF16),
            shape((heads, 2 * count, 4 * count), BF16), shape((2 * count, width), F32), shape((2 * count, width), BF16),
            shape((16, width, 128), BF16), shape((2 * count, hidden), BF16), shape((2 * count, hidden), BF16),
            shape((width, 2 * count), BF16), shape((2 * count, width), F32), shape((2 * count, width), F32)]
    return pl.pallas_call(
        front_kernel,
        grid=(heads // 2,),
        in_specs=[smem, whole(count, width), whole(count, width), whole(count, width), col(count), col(2 * count), col(2 * count),
                  whole(heads, span)] + [whole(width, width)] * 3 + [whole(1, width)] * 3
                 + [whole(2, width)] + [free] * 3,
        out_specs=[free] * 13 + [whole(8, width)],
        out_shape=outs + [shape((8, width), F32)],
        scratch_shapes=[pltpu.VMEM(o.shape, o.dtype) for o in outs[:4] + outs[5:]]
                       + [pltpu.VMEM(wo.shape, BF16), pltpu.VMEM(win.shape, BF16), pltpu.VMEM(wback.shape, BF16),
                          pltpu.VMEM((2, 2 * count, 4 * count), BF16), pltpu.VMEM((2, 2 * count, 4 * count), F32),
                          pltpu.VMEM((2, 128, span), F32), pltpu.VMEM((2, 4 * count, 128), BF16), pltpu.SemaphoreType.DMA((16,))],
        name="front",
    )(info, far, far_other, near, q_l, k_l, v_l, lines, wq, wk, wv, gain1, gain2, gain3, cots, wo, win, wback)

def through_kernel(info, slopes_h, win_h, mixed_h, steep_h, wo_h, att_h, gain2, grad_mixed_o, grad_attended_o, grad_out_o, rows,
                   slopes, win, mixed, steep, wo, att, grad_mixed, grad_attended, grad_out, sems):
    hidden, width = slopes.shape[1], mixed.shape[1]
    chunks = []
    for i, at in enumerate(range(0, hidden, 512)):
        for a, b, s in ((slopes_h, slopes, i), (win_h, win, 4 + i)):
            chunks.append(pltpu.make_async_copy(a.at[:, at : at + 512], b.at[:, at : at + 512], sems.at[s]))
    copies = [pltpu.make_async_copy(a, b, sems.at[8 + i]) for i, (a, b) in enumerate((
        (mixed_h, mixed), (steep_h, steep), (wo_h, wo), (att_h, att)))]
    outs = [pltpu.make_async_copy(a, b, sems.at[12 + i]) for i, (a, b) in enumerate((
        (grad_mixed, grad_mixed_o), (grad_attended, grad_attended_o), (grad_out, grad_out_o)))]
    for copy in chunks + copies:
        copy.start()
    grad_inner = None
    for i, at in enumerate(range(0, hidden, 512)):
        chunks[2 * i].wait()
        chunks[2 * i + 1].wait()
        part = dot(slopes[:, at : at + 512], win[:, at : at + 512], NT)
        grad_inner = part if grad_inner is None else grad_inner + part
    copies[0].wait()
    copies[1].wait()
    values = mixed[...]
    more, grad_two = norm_back(grad_inner, values, rms_scale(values), gain2[...])
    total = steep[...] + more
    grad_mixed[...] = total
    outs[0].start()
    low = total.astype(BF16)
    copies[2].wait()
    grad_attended[...] = dot(low, wo[...], NT).astype(BF16)
    outs[1].start()
    copies[3].wait()
    grad_out[...] = dot(att[...], low, TN).astype(BF16)
    outs[2].start()
    rows[...] = jnp.concatenate([grad_two, jnp.zeros((7, width), F32)])
    for copy in outs:
        copy.wait()

def through(info, slopes, win, mixed, steep, wo, att, gain2):
    n, width = mixed.shape
    smem, vmem, free = (pl.BlockSpec(memory_space=m) for m in (pltpu.SMEM, pltpu.VMEM, pl.ANY))
    shape = jax.ShapeDtypeStruct
    given = (slopes, win, mixed, steep, wo, att)
    outs = [shape((n, width), F32), shape((n, width), BF16), shape((width, width), BF16)]
    return pl.pallas_call(
        through_kernel,
        in_specs=[smem] + [free] * 6 + [vmem],
        out_specs=[free] * 3 + [vmem],
        out_shape=outs + [shape((8, width), F32)],
        scratch_shapes=[pltpu.VMEM(g.shape, g.dtype) for g in given] + [pltpu.VMEM(o.shape, o.dtype) for o in outs] + [pltpu.SemaphoreType.DMA((15,))],
        name="through",
    )(info, *given, gain2)

def meet_kernel(info, got_h, active_h, slopes_h, turned_h, steep_h, *refs):
    outs, (got, chunk, turned, steep, blocks, sems) = refs[:4], refs[4:]
    order = (3, 1, 2, 0)
    high, lowest = (info[6] & 15) >> 2, info[6] & 3
    load = [pltpu.make_async_copy(got_h.at[4 * k : 4 * k + 4], got.at[k], sems.at[k]) for k in range(4)]
    save = [pltpu.make_async_copy(blocks.at[k], outs[k], sems.at[4 + k]) for k in range(4)]

    def columns(source, k):
        at = pl.ds(pl.multiple_of((k ^ high) * 512, 512), 512)
        return pltpu.make_async_copy(source.at[:, at], chunk.at[k], sems.at[8 + k])

    for side, source in ((0, active_h), (1, slopes_h)):
        @pl.when(info[7] == side)
        def _(side=side, source=source):
            extra = pltpu.make_async_copy(*((steep_h, steep) if side == 0 else (turned_h, turned)), sems.at[12])
            extra.start()
            for k in order:
                columns(source, k).start()
                load[k].start()
            extra.wait()
            low = steep[...].astype(BF16) if side == 0 else turned[...]
            for k in order:
                columns(source, k).wait()
                made = dot(chunk[k], low, TN) if side == 0 else dot(low, chunk[k])
                load[k].wait()
                for b in range(4):
                    piece = made[:, b * 128 : (b + 1) * 128]
                    if side == 0:
                        piece = made[b * 128 : (b + 1) * 128]
                        piece = jnp.concatenate([piece[:, q * 128 : (q + 1) * 128] for q in range(4)])
                    to = b ^ lowest
                    blocks[k, to] = (piece + got[k, to].astype(F32)).astype(BF16)
                save[k].start()

    for copy in save:
        copy.wait()

def meet(info, got, active, slopes, turned, steep):
    smem, free = pl.BlockSpec(memory_space=pltpu.SMEM), pl.BlockSpec(memory_space=pl.ANY)
    block = (4,) + got.shape[1:]
    n, width = steep.shape
    return pl.pallas_call(
        meet_kernel,
        in_specs=[smem] + [free] * 5,
        out_specs=[free] * 4,
        out_shape=[jax.ShapeDtypeStruct(block, BF16)] * 4,
        scratch_shapes=[pltpu.VMEM((4,) + block, BF16), pltpu.VMEM((4, n, 512), BF16), pltpu.VMEM(turned.shape, BF16), pltpu.VMEM(steep.shape, F32),
                        pltpu.VMEM((4,) + block, BF16), pltpu.SemaphoreType.DMA((13,))],
        name="meet",
    )(info, got, active, slopes, turned, steep)

CLASS = {(0, 0): 0, (1, 2): 0, (0, 1): 1, (1, 3): 1, (0, 2): 2, (0, 3): 3, (1, 0): 4, (1, 1): 5}

def back_kernel(info, ql, qr, kl, kr, vl, vr, gout, out, inv, expo, buckets, dense_rows, through_rows,
                hid_l_h, hid_r_h, near_h, near_other_h, far_h, far_other_h, wq_h, wk_h, wv_h, grad_out_h,
                keep_o, send_o, stay_o, leave_o, small,
                hid_l, hid_r, near, near_other, far, far_other, wq, wk, wv, made,
                keep, send, stay, leave, dq, dk, dv, offsets, sums, acc, slopes, sems):
    count, width = near.shape
    step = pl.program_id(0)
    pairs = width // 128
    late = [pltpu.make_async_copy(a, b, sems.at[i]) for i, (a, b) in enumerate((
        (hid_l_h, hid_l), (hid_r_h, hid_r), (near_h, near), (near_other_h, near_other), (far_h, far), (far_other_h, far_other),
        (wq_h, wq), (wk_h, wk), (wv_h, wv), (grad_out_h, made.at[0:width])))]
    done = [pltpu.make_async_copy(a, b, sems.at[10 + i]) for i, (a, b) in enumerate(((send, send_o), (keep, keep_o), (leave, leave_o), (stay, stay_o)))]

    @pl.when(step == 0)
    def _():
        for copy in late:
            copy.start()

    cols = pl.ds(pl.multiple_of(step * 128, 128), 128)
    lane = lax.broadcasted_iota(jnp.int32, (1, 128), 1)
    starts = [info[1 + b] for b in range(4)]
    keys = jnp.concatenate([kl[...], kr[...]])
    values = jnp.concatenate([vl[...], vr[...]])
    query = jnp.concatenate([ql[...], qr[...]])
    scaled = gout[...].astype(F32) * inv[...]
    prod = scaled * out[...].astype(F32)
    low = scaled.astype(BF16)
    query_t, low_t = query.T, low.T
    grads_q, grads_k, grads_v = None, [], []
    for head in range(2):
        mine = (lane < 64) if head == 0 else (lane >= 64)
        base = 64 if head == 0 else 0
        pick = jnp.where(mine, 1.0, 0.0).astype(BF16)
        delta = jnp.sum(jnp.where(mine, prod, 0.0), axis=1, keepdims=True)
        high = delta.astype(BF16).astype(F32)
        extra = jnp.where(lane == base, high, jnp.where(lane == base + 1, delta - high, 0.0)).astype(BF16)
        grad = low * pick + extra
        minus = jnp.where((lane == base) | (lane == base + 1), -1.0, 0.0).astype(BF16)
        for b in range(4):
            spot = slice(b * count, (b + 1) * count)
            ds = dot(grad, values[spot] * pick + minus, NT) * expo[head, :, spot].astype(F32)
            slopes[head, :, spot] = ds.astype(BF16)
            for chunk in range(2):
                upper, lower = (ds[chunk * count + r * 128 : chunk * count + (r + 1) * 128] for r in range(2))
                group = CLASS[chunk, b]
                block = jnp.concatenate([lower[:, :128], lower[:, 128:] + upper[:, :128], upper[:, 128:]], axis=1)
                if (chunk, b) in ((1, 2), (1, 3)):
                    block = block + sums[head, group]
                sums[head, group] = block
        part = dot(slopes[head], keys * pick)
        grads_q = part if grads_q is None else grads_q + part
        half = slice(head * 64, (head + 1) * 64)
        grads_k.append(dot(query_t[half], slopes[head]))
        grads_v.append(dot(low_t[half], expo[head]))
    dq[:, cols] = grads_q.astype(BF16)
    dk[:, cols] = jnp.concatenate(grads_k).astype(BF16).T
    dv[:, cols] = jnp.concatenate(grads_v).astype(BF16).T
    for head in range(2):
        acc[head] = jnp.zeros(acc.shape[1:], F32)
        for (chunk, b), group in CLASS.items():
            if (chunk, b) not in ((1, 2), (1, 3)):
                at = starts[b] - starts[2 * chunk] + 768
                to = pl.ds(pl.multiple_of(at, 128), 384)
                acc[head, :, to] += sums[head, group]
        rest = acc[head]
        n = 64
        while n >= 8:
            rest = rest[:n] + pltpu.roll(rest[n:], 2048 - n, 1)
            n //= 2
        line = rest[7:8]
        for r in range(6, -1, -1):
            line = rest[r : r + 1] + pltpu.roll(line, 2047, 1)
        offsets[pl.ds(2 * step + head, 1), :] = pltpu.roll(line, 127, 1)

    @pl.when(step == pairs - 1)
    def _():
        for copy in late:
            copy.wait()
        made[width : 2 * width, :] = (dot(hid_l[:count, :], dq[:count, :], TN) + dot(hid_r[:count, :], dq[count:, :], TN)).astype(BF16)
        for at, grads in ((2 * width, dk), (3 * width, dv)):
            made[at : at + width, :] = (dot(hid_l[...], grads[: 2 * count, :], TN) + dot(hid_r[...], grads[2 * count :, :], TN)).astype(BF16)
        me = info[6]
        size = made.shape[0] // 32

        @pl.loop(0, 16)
        def _(r):
            keep[r] = made[pl.ds(pl.multiple_of((r ^ me) * size, size), size), :]
            send[pl.ds(pl.multiple_of(r * size, size), size), :] = made[pl.ds(pl.multiple_of(((r + 16) ^ me) * size, size), size), :]

        gain = jnp.zeros((1, width), F32)
        for b, raw in enumerate((near, near_other, far, far_other)):
            spot = slice(b * count, (b + 1) * count)
            grad = dot(dk[spot, :], wk[...], NT) + dot(dv[spot, :], wv[...], NT)
            half = slice((b // 2) * count, (b // 2 + 1) * count)
            if b % 2 == 0:
                grad = grad + dot(dq[half, :], wq[...], NT)
                stay[half, :] = grad
            else:
                leave[half, :] = grad.astype(BF16)
            tokens = raw[...].astype(F32)
            gain = gain + jnp.sum(grad * (tokens * rms_scale(tokens)), axis=0, keepdims=True)
        leave[2 * count :, :] = two_terms(rows_of(dense_rows[0:1, :]))
        picker = jnp.where(lax.broadcasted_iota(jnp.int32, (128, 1), 0) == buckets[...], 1.0, 0.0).astype(BF16)
        left = offsets[...][:, : buckets.shape[1]]
        bias = None
        for _ in range(3):
            part = left.astype(BF16)
            left = left - part.astype(F32)
            bias = dot(part, picker, NT) if bias is None else bias + dot(part, picker, NT)
        bias = jnp.concatenate([bias, jnp.zeros((bias.shape[0], width - 128), F32)], axis=1)
        total = jnp.concatenate([gain, through_rows[0:1, :], dense_rows[1:2, :], jnp.zeros((5, width), F32), bias])
        small[...] = total
        send[16 * size :, :] = two_terms(total)
        for copy in done:
            copy.start()
        for copy in done:
            copy.wait()

def back(info, ql, qr, kl, kr, vl, vr, gout, out, inv, expo, buckets, dense_rows, through_rows,
         hid_l, hid_r, near, near_other, far, far_other, wq, wk, wv, grad_out):
    count, width = near.shape
    smem, free = pl.BlockSpec(memory_space=pltpu.SMEM), pl.BlockSpec(memory_space=pl.ANY)
    whole = lambda *dims: pl.BlockSpec(dims, lambda g: (0,) * len(dims))
    col = lambda n: pl.BlockSpec((n, 128), lambda g: (0, g))
    shape = jax.ShapeDtypeStruct
    size = 4 * width // 32
    outs = [shape((16, size, width), BF16), shape((16 * size + 32, width), BF16), shape((2 * count, width), F32), shape((2 * count + 32, width), BF16)]
    given = (hid_l, hid_r, near, near_other, far, far_other, wq, wk, wv)
    return pl.pallas_call(
        back_kernel,
        grid=(width // 128,),
        in_specs=[smem, col(count), col(count)] + [col(2 * count)] * 7 + [pl.BlockSpec((2, 2 * count, 4 * count), lambda g: (g, 0, 0)),
                  whole(*buckets.shape), whole(8, width), whole(8, width)] + [free] * 10,
        out_specs=[free] * 4 + [whole(16, width)],
        out_shape=outs + [shape((16, width), F32)],
        scratch_shapes=[pltpu.VMEM(g.shape, BF16) for g in given] + [pltpu.VMEM((4 * width, width), BF16)]
                       + [pltpu.VMEM(o.shape, o.dtype) for o in outs]
                       + [pltpu.VMEM((2 * count, width), BF16), pltpu.VMEM((4 * count, width), BF16), pltpu.VMEM((4 * count, width), BF16),
                          pltpu.VMEM((8, 2048), F32), pltpu.VMEM((2, 6, 128, 384), F32), pltpu.VMEM((2, 128, 2048), F32),
                          pltpu.VMEM((2, 2 * count, 4 * count), BF16), pltpu.SemaphoreType.DMA((14,))],
        name="back",
    )(info, ql, qr, kl, kr, vl, vr, gout, out, inv, expo, buckets, dense_rows, through_rows, *given, grad_out)

def ending_kernel(info, stay, came, near, far, grad_mixed, gain, dense_rows, home, away):
    count, width = near.shape
    for part, raw in enumerate((near, far)):
        spot = slice(part * count, (part + 1) * count)
        tokens = raw[...].astype(F32)
        grad = stay[spot, :] + came[spot, :].astype(F32)
        more, _ = norm_back(grad, tokens, rms_scale(tokens), gain[...])
        value = (grad_mixed[spot, :] + more).astype(BF16)
        if part == 0:
            home[:count, :] = value
        else:
            away[:count, :] = value
    alive = (info[0] - info[5]).astype(F32)
    pool = two_terms((rows_of(dense_rows[0:1, :]) + one_value(came[2 * count :, :])) / alive)
    home[count:, :] = pool
    away[count:, :] = pool

def ending(info, stay, came, near, far, grad_mixed, gain, dense_rows):
    count, width = near.shape
    smem, vmem = pl.BlockSpec(memory_space=pltpu.SMEM), pl.BlockSpec(memory_space=pltpu.VMEM)
    shape = jax.ShapeDtypeStruct((count + 32, width), BF16)
    return pl.pallas_call(
        ending_kernel, in_specs=[smem] + [vmem] * 7, out_specs=[vmem] * 2, out_shape=[shape, shape], name="ending"
    )(info, stay, came, near, far, grad_mixed, gain, dense_rows)

def place_kernel(firsts, info, *refs):
    count = len(firsts)
    given, (back, front), parts, (rows, columns, sems) = refs[:count], refs[-5 - count : -3 - count], refs[-3 - count : -3], refs[-3:]
    load = [pltpu.make_async_copy(a, b, sems.at[i]) for i, (a, b) in enumerate(zip(given, parts))]
    for copy in load:
        copy.start()
    mine = info[6] & 15
    for side in range(2):
        @pl.when(info[7] == side)
        def _(side=side):
            copies, n = [], 0
            for part, first, ready in zip(parts, firsts, load):
                ready.wait()
                for i in range(part.shape[0]):
                    r = first + i
                    to = pl.ds(pl.multiple_of(((r & 15) ^ mine) * 128, 128), 128)
                    if (r >= 16) == (side == 1):
                        for q in range(4):
                            rows[n, :, q * 128 : (q + 1) * 128] = part[i, q * 128 : (q + 1) * 128, :].astype(F32)
                        copies.append(pltpu.make_async_copy(rows.at[n], back.at[to, :], sems.at[count + n]))
                    else:
                        columns[n] = part[i].astype(F32)
                        copies.append(pltpu.make_async_copy(columns.at[n], front.at[:, to], sems.at[count + n]))
                    copies[-1].start()
                    n += 1
            for copy in copies:
                copy.wait()

def place(info, parts, made, width):
    smem, free = pl.BlockSpec(memory_space=pltpu.SMEM), pl.BlockSpec(memory_space=pl.ANY)
    shape = jax.ShapeDtypeStruct
    count = sum(p.shape[0] for _, p in parts)
    return pl.pallas_call(
        functools.partial(place_kernel, [first for first, _ in parts]),
        in_specs=[smem] + [free] * (len(parts) + len(made)),
        out_specs=[free] * 2,
        out_shape=[shape((16 * 128, width), F32), shape((width, 16 * 128), F32)],
        scratch_shapes=[pltpu.VMEM(p.shape, BF16) for _, p in parts]
                       + [pltpu.VMEM((count, 128, width), F32), pltpu.VMEM((count, width, 128), F32), pltpu.SemaphoreType.DMA((len(parts) + count,))],
        input_output_aliases={1 + len(parts) + i: i for i in range(len(made))},
        name="place",
    )(info, *[p for _, p in parts], *made)

def sort_kernel(firsts, info, *refs):
    count = len(firsts)
    given, made, parts, (tall, sems) = refs[:count], refs[-6 - count : -2 - count], refs[-2 - count : -2], refs[-2:]
    load = [pltpu.make_async_copy(a, b, sems.at[i]) for i, (a, b) in enumerate(zip(given, parts))]
    for copy in load:
        copy.start()
    size = parts[0].shape[1]
    mine = info[6]
    pieces = []
    for part, first, ready in zip(parts, firsts, load):
        ready.wait()
        for i in range(part.shape[0]):
            tall[len(pieces)] = part[i].astype(F32)
            pieces.append(first + i)
    for top in range(4):
        @pl.when((mine >> 3) == top)
        def _(top=top):
            copies = []
            for n, r in enumerate(pieces):
                to = pl.ds(pl.multiple_of(((r ^ mine) & 7) * size, size), size)
                copies.append(pltpu.make_async_copy(tall.at[n], made[top ^ (r >> 3)].at[to, :], sems.at[count + n]))
                copies[-1].start()
            for copy in copies:
                copy.wait()

def sort(info, parts, made, width):
    smem, free = pl.BlockSpec(memory_space=pltpu.SMEM), pl.BlockSpec(memory_space=pl.ANY)
    shape = jax.ShapeDtypeStruct((width, width), F32)
    count = sum(p.shape[0] for _, p in parts)
    return pl.pallas_call(
        functools.partial(sort_kernel, [first for first, _ in parts]),
        in_specs=[smem] + [free] * (len(parts) + len(made)),
        out_specs=[free] * 4,
        out_shape=[shape] * 4,
        scratch_shapes=[pltpu.VMEM(p.shape, BF16) for _, p in parts]
                       + [pltpu.VMEM((count,) + parts[0][1].shape[1:], F32), pltpu.SemaphoreType.DMA((len(parts) + count,))],
        input_output_aliases={1 + len(parts) + i: i for i in range(len(made))},
        name="sort",
    )(info, *[p for _, p in parts], *made)

def mix_kernel(*refs):
    given, outs, terms, (sums, sems) = refs[:4], refs[4:8], refs[8:12], refs[12:]
    order = (3, 1, 2, 0)
    load = {(t, k): pltpu.make_async_copy(given[t].at[k], terms[t].at[k], sems.at[4 * t + k]) for k in order for t in range(4)}
    save = {k: pltpu.make_async_copy(sums.at[k], outs[k], sems.at[16 + k]) for k in order}
    for copy in load.values():
        copy.start()
    for k in order:
        for t in range(4):
            load[t, k].wait()
        sums[k] = added(*[term[k] for term in terms])
        save[k].start()
    for copy in save.values():
        copy.wait()

def mix(terms):
    block = terms[0].shape[1:]
    free = pl.BlockSpec(memory_space=pl.ANY)
    return pl.pallas_call(
        mix_kernel, in_specs=[free] * 4, out_specs=[free] * 4, out_shape=[jax.ShapeDtypeStruct(block, BF16)] * 4,
        scratch_shapes=[pltpu.VMEM((4,) + block, BF16)] * 5 + [pltpu.SemaphoreType.DMA((20,))], name="mix",
    )(*terms)

def exchange(value, bits):
    size = lax.axis_size("dp") * lax.axis_size("blk")
    return lax.ppermute(value, ("dp", "blk"), [(i, i ^ bits) for i in range(size)])

def wait(*values):
    return lax.optimization_barrier(values)

def added(*terms):
    total = terms[0].astype(F32)
    for term in terms[1:]:
        total = total + term.astype(F32)
    return total.astype(BF16)

def local(inputs, w_query, w_key, w_value, w_out, w_in, w_back, norm1_gain, norm2_gain, final_gain, bias_table, bucket_table, prefix_len, pad_len, pooled_grad):
    rows, width = inputs.shape[1:]
    spot, far_off = lax.axis_index("blk"), lax.axis_index("dp")
    doc, core = spot // 2, spot % 2
    block = [doc * 2 + core, doc * 2 + 1 - core, (1 - doc) * 2 + core, (1 - doc) * 2 + 1 - core]
    line = [8, 16]
    further = [32 << b for b in range((lax.axis_size("dp") // 8).bit_length() - 1)]
    piece = core * 16 + doc * 4 + (far_off % 2) * 8 + (far_off // 2) % 4
    near = jnp.where(doc == 0, inputs[0], inputs[1])
    far_send = jnp.where(doc == 0, inputs[1], inputs[0])
    near, far_send = wait(near, far_send)
    far = exchange(far_send, ROW)
    near_other = exchange(near, CORE)
    slot = jnp.arange(8, dtype=jnp.int32)
    ids = jnp.zeros_like(slot)
    for i, value in enumerate([b * rows for b in block] + [piece, core, doc]):
        ids = jnp.where(slot == i, value, ids)
    gain1, gain2, gain3 = norm1_gain[None, :], norm2_gain[None, :], final_gain[None, :]
    buckets = bucket_table[None, :]
    hid_l, q_l, k_l, v_l, lines, info = prepare(ids, pad_len, prefix_len, near, near_other, w_query, w_key, w_value, gain1, bias_table, buckets)
    far, info = wait(far, info)
    far_other = exchange(far, CORE)
    (hid_r, q_r, k_r, v_r, expo, inverse, attended, send, active, slopes, turned, mixed, steep, dense_rows) = front(
        info, far, far_other, near, q_l, k_l, v_l, lines, w_query, w_key, w_value, gain1, gain2, gain3, pooled_grad, w_out, w_in, w_back)

    xy = [ROW, NEAR_X, ROW ^ NEAR_X]
    zz = [line[0], line[1], line[0] ^ line[1]]

    token, send = wait(info, send)
    got = exchange(send, CORE)
    grad_mixed, grad_attended, grad_out_w, through_rows = through(token, slopes, w_in, mixed, steep, w_out, attended, gain2)
    token, through_rows, got = wait(token, through_rows, got)
    stays, *sends = meet(token, got, active, slopes, turned, steep)

    token, sends = wait(token, sends)
    came = [exchange(s, m) for s, m in zip(sends, xy)]
    rest_keep, rest_send, stay, leave, small = back(
        token, q_l, q_r, k_l, k_r, v_l, v_r, grad_attended, attended, inverse, expo, buckets, dense_rows, through_rows,
        hid_l, hid_r, near, near_other, far, far_other, w_query, w_key, w_value, grad_out_w)
    token, small, rest_send, leave, came = wait(token, small, rest_send, leave, came)

    rest_got = exchange(rest_send, CORE)
    hidden_got = exchange(leave, CORE)
    lines = mix([stays] + list(came))
    token, lines = wait(token, lines)
    took = [exchange(lines[k + 1], m) for k, m in enumerate(zz)]
    token, rest_got, hidden_got = wait(token, rest_got, hidden_got)

    count = rest_keep.shape[0] * rest_keep.shape[1]
    small = small + one_value(rest_got[count:])
    rest_got = rest_got[:count].reshape(rest_keep.shape)
    terms = two_terms(small)
    sends = [jnp.concatenate([added(rest_keep[4 * k : 4 * k + 4], rest_got[4 * k : 4 * k + 4]).reshape(-1, width), terms]) for k in (1, 2, 3)]
    token, sends = wait(token, sends)
    rest_came = [exchange(s, m) for s, m in zip(sends, xy)]
    home, away = ending(token, stay, hidden_got, near, far, grad_mixed, gain1, dense_rows)
    token, took, away = wait(token, took, away)

    whole = added(lines[0], *took)
    for bit in further:
        whole = added(whole, exchange(whole, bit))
    token, whole = wait(token, whole)
    back_line = [exchange(whole, m) for m in zz]
    away_got = exchange(away, ROW)
    token, rest_came = wait(token, rest_came)

    count = count // 4
    for part in rest_came:
        small = small + one_value(part[count:])
    rest_came = [part[:count].reshape((4,) + rest_keep.shape[1:]) for part in rest_came]
    piece = count // 4
    lines = added(rest_keep[:4], rest_got[:4], *rest_came).reshape(-1, width)
    send = jnp.concatenate([lines[2 * piece :], two_terms(small)])
    token, send = wait(token, send)
    took = exchange(send, line[1])
    token, took = wait(token, took)
    small = small + one_value(took[2 * piece :])
    lines = added(lines[: 2 * piece], took[: 2 * piece])
    send = jnp.concatenate([lines[piece:], two_terms(small)])
    token, send, back_line, away_got = wait(token, send, back_line, away_got)
    took = exchange(send, line[0])

    quarter = jnp.stack([whole] + back_line)
    token, quarter = wait(token, quarter)
    from_y, from_x = exchange(quarter, ROW), exchange(quarter, NEAR_X)
    token, took = wait(token, took)

    small = small + one_value(took[piece:])
    rest = added(lines[:piece], took[:piece])
    for bit in further:
        rest = added(rest, exchange(rest, bit))
        small = small + exchange(small, bit)
    token, rest = wait(token, rest)
    rest_back = [exchange(rest, m) for m in zz]
    token, rest_back, from_y, from_x = wait(token, rest_back, from_y, from_x)
    fourth = jnp.stack([rest] + rest_back)

    sends = [from_x[:2], from_y[2:], fourth, fourth]
    token, sends, quarter = wait(token, sends, quarter)
    far_a, far_b, fourth_y, fourth_x = (exchange(s, m) for s, m in zip(sends, (ROW, NEAR_X, ROW, NEAR_X)))
    other = exchange(quarter, CORE)
    near_pair = jnp.concatenate([from_y, from_x])
    grads = place(token, [(0, quarter), (4, from_y), (8, from_x)], [], width)
    token, grads, other, near_pair, far_a, far_b, fourth_y, fourth_x = wait(token, grads, other, near_pair, far_a, far_b, fourth_y, fourth_x)

    sends = [fourth_x[:2], fourth_y[2:], near_pair, jnp.concatenate([far_a, far_b]), jnp.concatenate([fourth, fourth_y, fourth_x])]
    token, sends = wait(token, sends)
    last_a, last_b, other_near, other_far, pair = (exchange(s, m) for s, m in zip(sends, (ROW, NEAR_X, CORE, CORE, CORE)))
    grads = place(token, [(12, far_a), (14, far_b), (16, other)], grads, width)
    token, grads, last_a, last_b, other_near, other_far, pair = wait(token, grads, last_a, last_b, other_near, other_far, pair)

    ends = exchange(jnp.concatenate([last_a, last_b]), CORE)
    made = sort(token, [(0, fourth), (4, fourth_y), (8, fourth_x), (12, last_a), (14, last_b), (16, pair)], [], width)
    out_back, out_in = place(token, [(20, other_near), (28, other_far)], grads, width)
    token, made, ends = wait(token, made, ends)
    out_out, out_query, out_key, out_value = sort(token, [(28, ends)], made, width)

    pool_mine, pool_other = one_value(home[rows:])[:1], one_value(away_got[rows:])[:1]
    pooled = jnp.where(doc == 0, jnp.concatenate([pool_mine, pool_other]), jnp.concatenate([pool_other, pool_mine]))
    home, away_got = home[:rows], away_got[:rows]
    input_grad = jnp.where(doc == 0, jnp.stack([home, away_got]), jnp.stack([away_got, home]))
    return (
        pooled,
        input_grad,
        out_query,
        out_key,
        out_value,
        out_out,
        out_in,
        out_back,
        small[0],
        small[1],
        small[2],
        small[8:, :BUCKETS].T,
    )

def solution(mesh):
    data = P("dp", "blk", None)
    placed = (data,) + (P(),) * 11 + (P("dp"), P("dp"), P("dp", None))
    return jax.shard_map(local, mesh=mesh, in_specs=placed, out_specs=(P("dp", None), data) + (P(),) * 10, check_vma=False)
```

```python
import functools
import jax, jax.numpy as jnp
from jax import lax
from jax.experimental import pallas as pl
from jax.experimental.pallas import tpu as pltpu
from jax.sharding import PartitionSpec as P

F32, BF16 = jnp.float32, jnp.bfloat16
NEG = -1000000000.0
NT = (((1,), (1,)), ((), ()))
TN = (((0,), (0,)), ((), ()))
NN = (((1,), (0,)), ((), ()))

def dot(a, b, dims=NN):
    return lax.dot_general(a, b, dims, preferred_element_type=F32)

def skew(row, width, dtype=F32):
    return pltpu.roll(jnp.broadcast_to(row, (128, width)), width - 127, 1, stride=1, stride_axis=0)


BUCKETS = 32
EPS = 1e-06
CORE, ROW, NEAR_X = 1, 2, 4

def rms_scale(values):
    return lax.rsqrt(jnp.mean(values * values, axis=-1, keepdims=True) + EPS)

def norm_back(grad_out, values, scale, gain):
    weighted = grad_out * gain
    inner = jnp.mean(weighted * values, axis=-1, keepdims=True)
    grad_in = scale * weighted - scale * scale * scale * values * inner
    return grad_in, jnp.sum(grad_out * values * scale, axis=0, keepdims=True)

def two_terms(value):
    high = value.astype(BF16)
    return jnp.concatenate([high, (value - high.astype(F32)).astype(BF16)])

def one_value(terms):
    return terms[:16].astype(F32) + terms[16:32].astype(F32)

def rows_of(*values):
    count = sum(v.shape[0] for v in values)
    return jnp.concatenate(list(values) + [jnp.zeros((16 - count, values[0].shape[1]), F32)])

def prepare_kernel(ids, pads, prefixes, mine, other, wq, wk, wv, gain, bias, buckets, hidden, query, keys, values, lines, info):
    rows = mine.shape[0]
    info[0] = 4 * rows - pads[ids[6]]
    info[5] = prefixes[ids[6]]
    for to, at in enumerate((0, 1, 2, 3)):
        info[1 + to] = ids[at]
    for to, at in enumerate((4, 5, 6)):
        info[6 + to] = ids[at]
    for part, raw in enumerate((mine, other)):
        tokens = raw[...].astype(F32)
        hidden[part * rows : (part + 1) * rows, :] = (tokens * rms_scale(tokens) * gain[...]).astype(BF16)
    h = hidden[...]
    query[...] = dot(h[:rows], wq[...]).astype(BF16)
    keys[...] = dot(h, wk[...]).astype(BF16)
    values[...] = dot(h, wv[...]).astype(BF16)
    picker = jnp.where(lax.broadcasted_iota(jnp.int32, (bias.shape[0], 1), 0) == buckets[...], 1.0, 0.0).astype(BF16)
    left, total = bias[...], None
    for _ in range(3):
        part = left.astype(BF16)
        left = left - part.astype(F32)
        made = dot(part, picker, TN)
        total = made if total is None else total + made
    lines[...] = jnp.zeros_like(lines)
    lines[:, : buckets.shape[1]] = total

def prepare(ids, pads, prefixes, mine, other, wq, wk, wv, gain, bias, buckets):
    rows, width = mine.shape
    span = buckets.shape[1] + 1
    heads = bias.shape[1]
    shape = lambda n: jax.ShapeDtypeStruct((n, width), BF16)
    smem, vmem = pl.BlockSpec(memory_space=pltpu.SMEM), pl.BlockSpec(memory_space=pltpu.VMEM)
    return pl.pallas_call(
        prepare_kernel,
        in_specs=[smem] * 3 + [vmem] * 8,
        out_specs=[vmem] * 5 + [smem],
        out_shape=[shape(2 * rows), shape(rows), shape(2 * rows), shape(2 * rows),
                   jax.ShapeDtypeStruct((heads, span), F32), jax.ShapeDtypeStruct((16,), jnp.int32)],
        name="prepare", compiler_params=pltpu.CompilerParams(vmem_limit_bytes=14 << 20),
    )(ids, pads, prefixes, mine, other, wq, wk, wv, gain, bias, buckets)

def back_pieces(to, active, low, mine):
    @pl.loop(0, active.shape[1] // 512)
    def _(group):
        made = dot(active[:, pl.ds(pl.multiple_of(group * 512, 512), 512)], low, TN).astype(BF16)
        for b in range(4):
            rows = made[b * 128 : (b + 1) * 128]
            to[(4 * group + b) ^ mine] = jnp.concatenate([rows[:, q * 128 : (q + 1) * 128] for q in range(4)])

def in_pieces(to, slopes, turned, mine):
    @pl.loop(0, slopes.shape[1] // 512)
    def _(group):
        made = dot(turned, slopes[:, pl.ds(pl.multiple_of(group * 512, 512), 512)]).astype(BF16)
        for b in range(4):
            to[(4 * group + b) ^ mine] = made[:, b * 128 : (b + 1) * 128]

def front_kernel(info, far, far_other, near, q_l, k_l, v_l, lines, wq, wk, wv, gain1, gain2, gain3, cots, wo_h, win_h, wback_h,
                 hid_o, q_o, k_o, v_o, expo_o, inv_o, att_o, send_o, active_o, slopes_o, turned_o, mixed_o, steep_o, rows,
                 hid, qs, ks, vs, inv, att, send, active, slopes, turned, mixed, steep, wo, win, wback, expo, scores, skewed, edges, sems):
    count, width = near.shape
    hidden = win.shape[1]
    step = pl.program_id(0)
    late = [pltpu.make_async_copy(a, b, sems.at[i]) for i, (a, b) in enumerate(((wo_h, wo), (win_h, win), (wback_h, wback)))]
    early = [pltpu.make_async_copy(a, b, sems.at[3 + i]) for i, (a, b) in enumerate(((hid, hid_o), (qs, q_o), (ks, k_o), (vs, v_o)))]
    dense = [pltpu.make_async_copy(a, b, sems.at[7 + i]) for i, (a, b) in enumerate((
        (inv, inv_o), (att, att_o), (mixed, mixed_o), (turned, turned_o), (active, active_o), (steep, steep_o), (slopes, slopes_o), (send, send_o)))]
    kept = lambda g: pltpu.make_async_copy(expo, expo_o.at[pl.ds(2 * g, 2)], sems.at[15])

    @pl.when(step == 0)
    def _():
        for copy in late:
            copy.start()
        for part, raw in enumerate((far, far_other)):
            tokens = raw[...].astype(F32)
            hid[part * count : (part + 1) * count, :] = (tokens * rms_scale(tokens) * gain1[...]).astype(BF16)
        h = hid[...]
        qs[...] = dot(h[:count], wq[...]).astype(BF16)
        ks[...] = dot(h, wk[...]).astype(BF16)
        vs[...] = dot(h, wv[...]).astype(BF16)
        for copy in early:
            copy.start()
        column = lax.broadcasted_iota(jnp.int32, (1, 128), 1)
        for b in range(4):
            place = info[1 + b] + lax.broadcasted_iota(jnp.int32, (count, 1), 0)
            gate = jnp.where(place < info[0], 0.0, NEG)
            for head in range(2):
                edges[head, b * count : (b + 1) * count, :] = jnp.where(column == (64 if head == 0 else 0), gate, 0.0).astype(BF16)

    @pl.when(step > 0)
    def _():
        kept(step - 1).wait()

    cols = pl.ds(pl.multiple_of(step * 128, 128), 128)
    lane = lax.broadcasted_iota(jnp.int32, (1, 128), 1)
    first = lane < 64
    limit = info[0]
    starts = [info[1 + b] for b in range(4)]
    keys = [k_l[:count, :], k_l[count:, :], ks[:count, cols], ks[count:, cols]]
    values = jnp.concatenate([v_l[...], vs[:, cols]])
    query = jnp.concatenate([q_l[...], qs[:, cols]])
    made = []
    for head in range(2):
        mine = jnp.where(first if head == 0 else lane >= 64, 1.0, 0.0).astype(BF16)
        one = jnp.where(lane == (64 if head == 0 else 0), 1.0, 0.0).astype(BF16)
        q = query * mine + one
        v = values * mine + one
        skewed[head] = skew(lines[pl.ds(2 * step + head, 1), :], lines.shape[1])
        for b in range(4):
            s = dot(q, keys[b] * mine + edges[head, b * count : (b + 1) * count, :], NT)
            for r in range(4):
                at = starts[b] - starts[2 * (r // 2)] + 896 - 128 * (r % 2)
                part = s[r * 128 : (r + 1) * 128] + skewed[head, :, pl.ds(pl.multiple_of(at, 128), 256)]
                scores[head, r * 128 : (r + 1) * 128, b * 256 : (b + 1) * 256] = part
        for r in range(4):
            rs = slice(r * 128, (r + 1) * 128)
            value = scores[head, rs, :]
            top = jnp.max(value, axis=1, keepdims=True)
            expo[head, rs, :] = jnp.exp(value - top).astype(BF16)
        acc = dot(expo[head], v)
        made.append((acc, 1.0 / (acc[:, 64:65] if head == 0 else acc[:, 0:1])))
    (a0, i0), (a1, i1) = made
    scale = jnp.where(first, i0, i1)
    att[:, cols] = (jnp.where(first, a0, a1) * scale).astype(BF16)
    inv[:, cols] = scale
    kept(step).start()

    @pl.when(step == 3)
    def _():
        for copy in late:
            copy.wait()
        dense[0].start()
        dense[1].start()
        for part, raw in enumerate((near, far)):
            spot = slice(part * count, (part + 1) * count)
            mixed[spot, :] = raw[...].astype(F32) + dot(att[spot, :], wo[...])
        dense[2].start()
        values = mixed[...]
        inner = (values * rms_scale(values) * gain2[...]).astype(BF16)
        turned[...] = inner.T
        dense[3].start()
        total = values
        for at in range(0, hidden, 512):
            lifted = jnp.maximum(dot(inner, win[:, at : at + 512]), 0.0).astype(BF16)
            active[:, at : at + 512] = lifted
            total = total + dot(lifted, wback[at : at + 512, :])
        dense[4].start()
        scale = rms_scale(total)
        place = lax.broadcasted_iota(jnp.int32, (2 * count, 1), 0)
        place = jnp.where(place < count, place + info[1], place + (info[3] - count))
        live = jnp.where((place >= info[5]) & (place < limit), 1.0, 0.0)
        pool = jnp.sum(total * scale * gain3[...] * live, axis=0, keepdims=True)
        cot = jnp.where(info[8] == 0, cots[0:1, :], cots[1:2, :]) / (limit - info[5]).astype(F32)
        slope, grad_end = norm_back(live * cot, total, scale, gain3[...])
        steep[...] = slope
        dense[5].start()
        rows[...] = jnp.concatenate([pool, grad_end, jnp.zeros((6, width), F32)])
        low = slope.astype(BF16)
        for at in range(0, hidden, 512):
            through = dot(low, wback[at : at + 512, :], NT).astype(BF16)
            slopes[:, at : at + 512] = jnp.where(active[:, at : at + 512] > 0, through, jnp.zeros_like(through))
        dense[6].start()
        mine = info[6] & 15

        @pl.when(info[7] == 0)
        def _():
            in_pieces(send, slopes, turned[...], mine)

        @pl.when(info[7] == 1)
        def _():
            back_pieces(send, active, steep[...].astype(BF16), mine)

        dense[7].start()
        for copy in early + dense:
            copy.wait()
        kept(step).wait()

def front(info, far, far_other, near, q_l, k_l, v_l, lines, wq, wk, wv, gain1, gain2, gain3, cots, wo, win, wback):
    count, width = near.shape
    hidden = win.shape[1]
    heads, span = lines.shape
    shape = jax.ShapeDtypeStruct
    smem, free = pl.BlockSpec(memory_space=pltpu.SMEM), pl.BlockSpec(memory_space=pl.ANY)
    whole = lambda *dims: pl.BlockSpec(dims, lambda g: (0,) * len(dims))
    col = lambda n: pl.BlockSpec((n, 128), lambda g: (0, g))
    outs = [shape((2 * count, width), BF16), shape((count, width), BF16), shape((2 * count, width), BF16), shape((2 * count, width), BF16),
            shape((heads, 2 * count, 4 * count), BF16), shape((2 * count, width), F32), shape((2 * count, width), BF16),
            shape((16, width, 128), BF16), shape((2 * count, hidden), BF16), shape((2 * count, hidden), BF16),
            shape((width, 2 * count), BF16), shape((2 * count, width), F32), shape((2 * count, width), F32)]
    return pl.pallas_call(
        front_kernel,
        grid=(heads // 2,),
        in_specs=[smem, whole(count, width), whole(count, width), whole(count, width), col(count), col(2 * count), col(2 * count),
                  whole(heads, span)] + [whole(width, width)] * 3 + [whole(1, width)] * 3
                 + [whole(2, width)] + [free] * 3,
        out_specs=[free] * 13 + [whole(8, width)],
        out_shape=outs + [shape((8, width), F32)],
        scratch_shapes=[pltpu.VMEM(o.shape, o.dtype) for o in outs[:4] + outs[5:]]
                       + [pltpu.VMEM(wo.shape, BF16), pltpu.VMEM(win.shape, BF16), pltpu.VMEM(wback.shape, BF16),
                          pltpu.VMEM((2, 2 * count, 4 * count), BF16), pltpu.VMEM((2, 2 * count, 4 * count), F32),
                          pltpu.VMEM((2, 128, span), F32), pltpu.VMEM((2, 4 * count, 128), BF16), pltpu.SemaphoreType.DMA((16,))],
        name="front", compiler_params=pltpu.CompilerParams(vmem_limit_bytes=50 << 20),
    )(info, far, far_other, near, q_l, k_l, v_l, lines, wq, wk, wv, gain1, gain2, gain3, cots, wo, win, wback)

def through_kernel(info, slopes_h, win_h, mixed_h, steep_h, wo_h, att_h, gain2, grad_mixed_o, grad_attended_o, grad_out_o, rows,
                   slopes, win, mixed, steep, wo, att, grad_mixed, grad_attended, grad_out, sems):
    hidden, width = slopes.shape[1], mixed.shape[1]
    chunks = []
    for i, at in enumerate(range(0, hidden, 512)):
        for a, b, s in ((slopes_h, slopes, i), (win_h, win, 4 + i)):
            chunks.append(pltpu.make_async_copy(a.at[:, at : at + 512], b.at[:, at : at + 512], sems.at[s]))
    copies = [pltpu.make_async_copy(a, b, sems.at[8 + i]) for i, (a, b) in enumerate((
        (mixed_h, mixed), (steep_h, steep), (wo_h, wo), (att_h, att)))]
    outs = [pltpu.make_async_copy(a, b, sems.at[12 + i]) for i, (a, b) in enumerate((
        (grad_mixed, grad_mixed_o), (grad_attended, grad_attended_o), (grad_out, grad_out_o)))]
    for copy in chunks + copies:
        copy.start()
    grad_inner = None
    for i, at in enumerate(range(0, hidden, 512)):
        chunks[2 * i].wait()
        chunks[2 * i + 1].wait()
        part = dot(slopes[:, at : at + 512], win[:, at : at + 512], NT)
        grad_inner = part if grad_inner is None else grad_inner + part
    copies[0].wait()
    copies[1].wait()
    values = mixed[...]
    more, grad_two = norm_back(grad_inner, values, rms_scale(values), gain2[...])
    total = steep[...] + more
    grad_mixed[...] = total
    outs[0].start()
    low = total.astype(BF16)
    copies[2].wait()
    grad_attended[...] = dot(low, wo[...], NT).astype(BF16)
    outs[1].start()
    copies[3].wait()
    grad_out[...] = dot(att[...], low, TN).astype(BF16)
    outs[2].start()
    rows[...] = jnp.concatenate([grad_two, jnp.zeros((7, width), F32)])
    for copy in outs:
        copy.wait()

def through(info, slopes, win, mixed, steep, wo, att, gain2):
    n, width = mixed.shape
    smem, vmem, free = (pl.BlockSpec(memory_space=m) for m in (pltpu.SMEM, pltpu.VMEM, pl.ANY))
    shape = jax.ShapeDtypeStruct
    given = (slopes, win, mixed, steep, wo, att)
    outs = [shape((n, width), F32), shape((n, width), BF16), shape((width, width), BF16)]
    return pl.pallas_call(
        through_kernel,
        in_specs=[smem] + [free] * 6 + [vmem],
        out_specs=[free] * 3 + [vmem],
        out_shape=outs + [shape((8, width), F32)],
        scratch_shapes=[pltpu.VMEM(g.shape, g.dtype) for g in given] + [pltpu.VMEM(o.shape, o.dtype) for o in outs] + [pltpu.SemaphoreType.DMA((15,))],
        name="through", compiler_params=pltpu.CompilerParams(vmem_limit_bytes=16 << 20),
    )(info, *given, gain2)

def meet_kernel(info, got_h, active_h, slopes_h, turned_h, steep_h, *refs):
    outs, (got, chunk, turned, steep, blocks, sems) = refs[:4], refs[4:]
    order = (3, 1, 2, 0)
    high, lowest = (info[6] & 15) >> 2, info[6] & 3
    load = [pltpu.make_async_copy(got_h.at[4 * k : 4 * k + 4], got.at[k], sems.at[k]) for k in range(4)]
    save = [pltpu.make_async_copy(blocks.at[k], outs[k], sems.at[4 + k]) for k in range(4)]

    def columns(source, k):
        at = pl.ds(pl.multiple_of((k ^ high) * 512, 512), 512)
        return pltpu.make_async_copy(source.at[:, at], chunk.at[k], sems.at[8 + k])

    for side, source in ((0, active_h), (1, slopes_h)):
        @pl.when(info[7] == side)
        def _(side=side, source=source):
            extra = pltpu.make_async_copy(*((steep_h, steep) if side == 0 else (turned_h, turned)), sems.at[12])
            extra.start()
            for k in order:
                columns(source, k).start()
                load[k].start()
            extra.wait()
            low = steep[...].astype(BF16) if side == 0 else turned[...]
            for k in order:
                columns(source, k).wait()
                made = dot(chunk[k], low, TN) if side == 0 else dot(low, chunk[k])
                load[k].wait()
                for b in range(4):
                    piece = made[:, b * 128 : (b + 1) * 128]
                    if side == 0:
                        piece = made[b * 128 : (b + 1) * 128]
                        piece = jnp.concatenate([piece[:, q * 128 : (q + 1) * 128] for q in range(4)])
                    to = b ^ lowest
                    blocks[k, to] = (piece + got[k, to].astype(F32)).astype(BF16)
                save[k].start()

    for copy in save:
        copy.wait()

def meet(info, got, active, slopes, turned, steep):
    smem, free = pl.BlockSpec(memory_space=pltpu.SMEM), pl.BlockSpec(memory_space=pl.ANY)
    block = (4,) + got.shape[1:]
    n, width = steep.shape
    return pl.pallas_call(
        meet_kernel,
        in_specs=[smem] + [free] * 5,
        out_specs=[free] * 4,
        out_shape=[jax.ShapeDtypeStruct(block, BF16)] * 4,
        scratch_shapes=[pltpu.VMEM((4,) + block, BF16), pltpu.VMEM((4, n, 512), BF16), pltpu.VMEM(turned.shape, BF16), pltpu.VMEM(steep.shape, F32),
                        pltpu.VMEM((4,) + block, BF16), pltpu.SemaphoreType.DMA((13,))],
        name="meet", compiler_params=pltpu.CompilerParams(vmem_limit_bytes=20 << 20),
    )(info, got, active, slopes, turned, steep)

CLASS = {(0, 0): 0, (1, 2): 0, (0, 1): 1, (1, 3): 1, (0, 2): 2, (0, 3): 3, (1, 0): 4, (1, 1): 5}

def back_kernel(info, ql, qr, kl, kr, vl, vr, gout, out, inv, expo, buckets, dense_rows, through_rows,
                hid_l_h, hid_r_h, near_h, near_other_h, far_h, far_other_h, wq_h, wk_h, wv_h, grad_out_h,
                keep_o, send_o, stay_o, leave_o, small,
                hid_l, hid_r, near, near_other, far, far_other, wq, wk, wv, made,
                keep, send, stay, leave, dq, dk, dv, offsets, sums, acc, slopes, sems):
    count, width = near.shape
    step = pl.program_id(0)
    pairs = width // 128
    late = [pltpu.make_async_copy(a, b, sems.at[i]) for i, (a, b) in enumerate((
        (hid_l_h, hid_l), (hid_r_h, hid_r), (near_h, near), (near_other_h, near_other), (far_h, far), (far_other_h, far_other),
        (wq_h, wq), (wk_h, wk), (wv_h, wv), (grad_out_h, made.at[0:width])))]
    done = [pltpu.make_async_copy(a, b, sems.at[10 + i]) for i, (a, b) in enumerate(((send, send_o), (keep, keep_o), (leave, leave_o), (stay, stay_o)))]

    @pl.when(step == 0)
    def _():
        for copy in late:
            copy.start()

    cols = pl.ds(pl.multiple_of(step * 128, 128), 128)
    lane = lax.broadcasted_iota(jnp.int32, (1, 128), 1)
    starts = [info[1 + b] for b in range(4)]
    keys = jnp.concatenate([kl[...], kr[...]])
    values = jnp.concatenate([vl[...], vr[...]])
    query = jnp.concatenate([ql[...], qr[...]])
    scaled = gout[...].astype(F32) * inv[...]
    prod = scaled * out[...].astype(F32)
    low = scaled.astype(BF16)
    query_t, low_t = query.T, low.T
    grads_q, grads_k, grads_v = None, [], []
    for head in range(2):
        mine = (lane < 64) if head == 0 else (lane >= 64)
        base = 64 if head == 0 else 0
        pick = jnp.where(mine, 1.0, 0.0).astype(BF16)
        delta = jnp.sum(jnp.where(mine, prod, 0.0), axis=1, keepdims=True)
        high = delta.astype(BF16).astype(F32)
        extra = jnp.where(lane == base, high, jnp.where(lane == base + 1, delta - high, 0.0)).astype(BF16)
        grad = low * pick + extra
        minus = jnp.where((lane == base) | (lane == base + 1), -1.0, 0.0).astype(BF16)
        for b in range(4):
            spot = slice(b * count, (b + 1) * count)
            ds = dot(grad, values[spot] * pick + minus, NT) * expo[head, :, spot].astype(F32)
            slopes[head, :, spot] = ds.astype(BF16)
            for chunk in range(2):
                upper, lower = (ds[chunk * count + r * 128 : chunk * count + (r + 1) * 128] for r in range(2))
                group = CLASS[chunk, b]
                block = jnp.concatenate([lower[:, :128], lower[:, 128:] + upper[:, :128], upper[:, 128:]], axis=1)
                if (chunk, b) in ((1, 2), (1, 3)):
                    block = block + sums[head, group]
                sums[head, group] = block
        part = dot(slopes[head], keys * pick)
        grads_q = part if grads_q is None else grads_q + part
        half = slice(head * 64, (head + 1) * 64)
        grads_k.append(dot(query_t[half], slopes[head]))
        grads_v.append(dot(low_t[half], expo[head]))
    dq[:, cols] = grads_q.astype(BF16)
    dk[:, cols] = jnp.concatenate(grads_k).astype(BF16).T
    dv[:, cols] = jnp.concatenate(grads_v).astype(BF16).T
    for head in range(2):
        acc[head] = jnp.zeros(acc.shape[1:], F32)
        for (chunk, b), group in CLASS.items():
            if (chunk, b) not in ((1, 2), (1, 3)):
                at = starts[b] - starts[2 * chunk] + 768
                to = pl.ds(pl.multiple_of(at, 128), 384)
                acc[head, :, to] += sums[head, group]
        rest = acc[head]
        n = 64
        while n >= 8:
            rest = rest[:n] + pltpu.roll(rest[n:], 2048 - n, 1)
            n //= 2
        line = rest[7:8]
        for r in range(6, -1, -1):
            line = rest[r : r + 1] + pltpu.roll(line, 2047, 1)
        offsets[pl.ds(2 * step + head, 1), :] = pltpu.roll(line, 127, 1)

    @pl.when(step == pairs - 1)
    def _():
        for copy in late:
            copy.wait()
        made[width : 2 * width, :] = (dot(hid_l[:count, :], dq[:count, :], TN) + dot(hid_r[:count, :], dq[count:, :], TN)).astype(BF16)
        for at, grads in ((2 * width, dk), (3 * width, dv)):
            made[at : at + width, :] = (dot(hid_l[...], grads[: 2 * count, :], TN) + dot(hid_r[...], grads[2 * count :, :], TN)).astype(BF16)
        me = info[6]
        size = made.shape[0] // 32

        @pl.loop(0, 16)
        def _(r):
            keep[r] = made[pl.ds(pl.multiple_of((r ^ me) * size, size), size), :]
            send[pl.ds(pl.multiple_of(r * size, size), size), :] = made[pl.ds(pl.multiple_of(((r + 16) ^ me) * size, size), size), :]

        gain = jnp.zeros((1, width), F32)
        for b, raw in enumerate((near, near_other, far, far_other)):
            spot = slice(b * count, (b + 1) * count)
            grad = dot(dk[spot, :], wk[...], NT) + dot(dv[spot, :], wv[...], NT)
            half = slice((b // 2) * count, (b // 2 + 1) * count)
            if b % 2 == 0:
                grad = grad + dot(dq[half, :], wq[...], NT)
                stay[half, :] = grad
            else:
                leave[half, :] = grad.astype(BF16)
            tokens = raw[...].astype(F32)
            gain = gain + jnp.sum(grad * (tokens * rms_scale(tokens)), axis=0, keepdims=True)
        leave[2 * count :, :] = two_terms(rows_of(dense_rows[0:1, :]))
        picker = jnp.where(lax.broadcasted_iota(jnp.int32, (128, 1), 0) == buckets[...], 1.0, 0.0).astype(BF16)
        left = offsets[...][:, : buckets.shape[1]]
        bias = None
        for _ in range(3):
            part = left.astype(BF16)
            left = left - part.astype(F32)
            bias = dot(part, picker, NT) if bias is None else bias + dot(part, picker, NT)
        bias = jnp.concatenate([bias, jnp.zeros((bias.shape[0], width - 128), F32)], axis=1)
        total = jnp.concatenate([gain, through_rows[0:1, :], dense_rows[1:2, :], jnp.zeros((5, width), F32), bias])
        small[...] = total
        send[16 * size :, :] = two_terms(total)
        for copy in done:
            copy.start()
        for copy in done:
            copy.wait()

def back(info, ql, qr, kl, kr, vl, vr, gout, out, inv, expo, buckets, dense_rows, through_rows,
         hid_l, hid_r, near, near_other, far, far_other, wq, wk, wv, grad_out):
    count, width = near.shape
    smem, free = pl.BlockSpec(memory_space=pltpu.SMEM), pl.BlockSpec(memory_space=pl.ANY)
    whole = lambda *dims: pl.BlockSpec(dims, lambda g: (0,) * len(dims))
    col = lambda n: pl.BlockSpec((n, 128), lambda g: (0, g))
    shape = jax.ShapeDtypeStruct
    size = 4 * width // 32
    outs = [shape((16, size, width), BF16), shape((16 * size + 32, width), BF16), shape((2 * count, width), F32), shape((2 * count + 32, width), BF16)]
    given = (hid_l, hid_r, near, near_other, far, far_other, wq, wk, wv)
    return pl.pallas_call(
        back_kernel,
        grid=(width // 128,),
        in_specs=[smem, col(count), col(count)] + [col(2 * count)] * 7 + [pl.BlockSpec((2, 2 * count, 4 * count), lambda g: (g, 0, 0)),
                  whole(*buckets.shape), whole(8, width), whole(8, width)] + [free] * 10,
        out_specs=[free] * 4 + [whole(16, width)],
        out_shape=outs + [shape((16, width), F32)],
        scratch_shapes=[pltpu.VMEM(g.shape, BF16) for g in given] + [pltpu.VMEM((4 * width, width), BF16)]
                       + [pltpu.VMEM(o.shape, o.dtype) for o in outs]
                       + [pltpu.VMEM((2 * count, width), BF16), pltpu.VMEM((4 * count, width), BF16), pltpu.VMEM((4 * count, width), BF16),
                          pltpu.VMEM((8, 2048), F32), pltpu.VMEM((2, 6, 128, 384), F32), pltpu.VMEM((2, 128, 2048), F32),
                          pltpu.VMEM((2, 2 * count, 4 * count), BF16), pltpu.SemaphoreType.DMA((14,))],
        name="back", compiler_params=pltpu.CompilerParams(vmem_limit_bytes=44 << 20),
    )(info, ql, qr, kl, kr, vl, vr, gout, out, inv, expo, buckets, dense_rows, through_rows, *given, grad_out)

def ending_kernel(info, stay, came, near, far, grad_mixed, gain, dense_rows, home, away):
    count, width = near.shape
    for part, raw in enumerate((near, far)):
        spot = slice(part * count, (part + 1) * count)
        tokens = raw[...].astype(F32)
        grad = stay[spot, :] + came[spot, :].astype(F32)
        more, _ = norm_back(grad, tokens, rms_scale(tokens), gain[...])
        value = (grad_mixed[spot, :] + more).astype(BF16)
        if part == 0:
            home[:count, :] = value
        else:
            away[:count, :] = value
    alive = (info[0] - info[5]).astype(F32)
    pool = two_terms((rows_of(dense_rows[0:1, :]) + one_value(came[2 * count :, :])) / alive)
    home[count:, :] = pool
    away[count:, :] = pool

def ending(info, stay, came, near, far, grad_mixed, gain, dense_rows):
    count, width = near.shape
    smem, vmem = pl.BlockSpec(memory_space=pltpu.SMEM), pl.BlockSpec(memory_space=pltpu.VMEM)
    shape = jax.ShapeDtypeStruct((count + 32, width), BF16)
    return pl.pallas_call(
        ending_kernel, in_specs=[smem] + [vmem] * 7, out_specs=[vmem] * 2, out_shape=[shape, shape], name="ending", compiler_params=pltpu.CompilerParams(vmem_limit_bytes=10 << 20)
    )(info, stay, came, near, far, grad_mixed, gain, dense_rows)

def place_kernel(firsts, info, *refs):
    count = len(firsts)
    given, (back, front), parts, (rows, columns, sems) = refs[:count], refs[-5 - count : -3 - count], refs[-3 - count : -3], refs[-3:]
    load = [pltpu.make_async_copy(a, b, sems.at[i]) for i, (a, b) in enumerate(zip(given, parts))]
    for copy in load:
        copy.start()
    mine = info[6] & 15
    for side in range(2):
        @pl.when(info[7] == side)
        def _(side=side):
            copies, n = [], 0
            for part, first, ready in zip(parts, firsts, load):
                ready.wait()
                for i in range(part.shape[0]):
                    r = first + i
                    to = pl.ds(pl.multiple_of(((r & 15) ^ mine) * 128, 128), 128)
                    if (r >= 16) == (side == 1):
                        for q in range(4):
                            rows[n, :, q * 128 : (q + 1) * 128] = part[i, q * 128 : (q + 1) * 128, :].astype(F32)
                        copies.append(pltpu.make_async_copy(rows.at[n], back.at[to, :], sems.at[count + n]))
                    else:
                        columns[n] = part[i].astype(F32)
                        copies.append(pltpu.make_async_copy(columns.at[n], front.at[:, to], sems.at[count + n]))
                    copies[-1].start()
                    n += 1
            for copy in copies:
                copy.wait()

def place(info, parts, made, width):
    smem, free = pl.BlockSpec(memory_space=pltpu.SMEM), pl.BlockSpec(memory_space=pl.ANY)
    shape = jax.ShapeDtypeStruct
    count = sum(p.shape[0] for _, p in parts)
    return pl.pallas_call(
        functools.partial(place_kernel, [first for first, _ in parts]),
        in_specs=[smem] + [free] * (len(parts) + len(made)),
        out_specs=[free] * 2,
        out_shape=[shape((16 * 128, width), F32), shape((width, 16 * 128), F32)],
        scratch_shapes=[pltpu.VMEM(p.shape, BF16) for _, p in parts]
                       + [pltpu.VMEM((count, 128, width), F32), pltpu.VMEM((count, width, 128), F32), pltpu.SemaphoreType.DMA((len(parts) + count,))],
        input_output_aliases={1 + len(parts) + i: i for i in range(len(made))},
        name="place", compiler_params=pltpu.CompilerParams(vmem_limit_bytes=24 << 20),
    )(info, *[p for _, p in parts], *made)

def sort_kernel(firsts, info, *refs):
    count = len(firsts)
    given, made, parts, (tall, sems) = refs[:count], refs[-6 - count : -2 - count], refs[-2 - count : -2], refs[-2:]
    load = [pltpu.make_async_copy(a, b, sems.at[i]) for i, (a, b) in enumerate(zip(given, parts))]
    for copy in load:
        copy.start()
    size = parts[0].shape[1]
    mine = info[6]
    pieces = []
    for part, first, ready in zip(parts, firsts, load):
        ready.wait()
        for i in range(part.shape[0]):
            tall[len(pieces)] = part[i].astype(F32)
            pieces.append(first + i)
    for top in range(4):
        @pl.when((mine >> 3) == top)
        def _(top=top):
            copies = []
            for n, r in enumerate(pieces):
                to = pl.ds(pl.multiple_of(((r ^ mine) & 7) * size, size), size)
                copies.append(pltpu.make_async_copy(tall.at[n], made[top ^ (r >> 3)].at[to, :], sems.at[count + n]))
                copies[-1].start()
            for copy in copies:
                copy.wait()

def sort(info, parts, made, width):
    smem, free = pl.BlockSpec(memory_space=pltpu.SMEM), pl.BlockSpec(memory_space=pl.ANY)
    shape = jax.ShapeDtypeStruct((width, width), F32)
    count = sum(p.shape[0] for _, p in parts)
    return pl.pallas_call(
        functools.partial(sort_kernel, [first for first, _ in parts]),
        in_specs=[smem] + [free] * (len(parts) + len(made)),
        out_specs=[free] * 4,
        out_shape=[shape] * 4,
        scratch_shapes=[pltpu.VMEM(p.shape, BF16) for _, p in parts]
                       + [pltpu.VMEM((count,) + parts[0][1].shape[1:], F32), pltpu.SemaphoreType.DMA((len(parts) + count,))],
        input_output_aliases={1 + len(parts) + i: i for i in range(len(made))},
        name="sort", compiler_params=pltpu.CompilerParams(vmem_limit_bytes=12 << 20),
    )(info, *[p for _, p in parts], *made)

def mix_kernel(*refs):
    given, outs, terms, (sums, sems) = refs[:4], refs[4:8], refs[8:12], refs[12:]
    order = (3, 1, 2, 0)
    load = {(t, k): pltpu.make_async_copy(given[t].at[k], terms[t].at[k], sems.at[4 * t + k]) for k in order for t in range(4)}
    save = {k: pltpu.make_async_copy(sums.at[k], outs[k], sems.at[16 + k]) for k in order}
    for copy in load.values():
        copy.start()
    for k in order:
        for t in range(4):
            load[t, k].wait()
        sums[k] = added(*[term[k] for term in terms])
        save[k].start()
    for copy in save.values():
        copy.wait()

def mix(terms):
    block = terms[0].shape[1:]
    free = pl.BlockSpec(memory_space=pl.ANY)
    return pl.pallas_call(
        mix_kernel, in_specs=[free] * 4, out_specs=[free] * 4, out_shape=[jax.ShapeDtypeStruct(block, BF16)] * 4,
        scratch_shapes=[pltpu.VMEM((4,) + block, BF16)] * 5 + [pltpu.SemaphoreType.DMA((20,))], name="mix", compiler_params=pltpu.CompilerParams(vmem_limit_bytes=10 << 20),
    )(*terms)

def exchange(value, bits):
    size = lax.axis_size("dp") * lax.axis_size("blk")
    return lax.ppermute(value, ("dp", "blk"), [(i, i ^ bits) for i in range(size)])

def wait(*values):
    return lax.optimization_barrier(values)

def added(*terms):
    total = terms[0].astype(F32)
    for term in terms[1:]:
        total = total + term.astype(F32)
    return total.astype(BF16)

def local(inputs, w_query, w_key, w_value, w_out, w_in, w_back, norm1_gain, norm2_gain, final_gain, bias_table, bucket_table, prefix_len, pad_len, pooled_grad):
    rows, width = inputs.shape[1:]
    spot, far_off = lax.axis_index("blk"), lax.axis_index("dp")
    doc, core = spot // 2, spot % 2
    block = [doc * 2 + core, doc * 2 + 1 - core, (1 - doc) * 2 + core, (1 - doc) * 2 + 1 - core]
    line = [8, 16]
    further = [32 << b for b in range((lax.axis_size("dp") // 8).bit_length() - 1)]
    piece = core * 16 + doc * 4 + (far_off % 2) * 8 + (far_off // 2) % 4
    near = jnp.where(doc == 0, inputs[0], inputs[1])
    far_send = jnp.where(doc == 0, inputs[1], inputs[0])
    near, far_send = wait(near, far_send)
    far = exchange(far_send, ROW)
    near_other = exchange(near, CORE)
    slot = jnp.arange(8, dtype=jnp.int32)
    ids = jnp.zeros_like(slot)
    for i, value in enumerate([b * rows for b in block] + [piece, core, doc]):
        ids = jnp.where(slot == i, value, ids)
    gain1, gain2, gain3 = norm1_gain[None, :], norm2_gain[None, :], final_gain[None, :]
    buckets = bucket_table[None, :]
    hid_l, q_l, k_l, v_l, lines, info = prepare(ids, pad_len, prefix_len, near, near_other, w_query, w_key, w_value, gain1, bias_table, buckets)
    far, info = wait(far, info)
    far_other = exchange(far, CORE)
    (hid_r, q_r, k_r, v_r, expo, inverse, attended, send, active, slopes, turned, mixed, steep, dense_rows) = front(
        info, far, far_other, near, q_l, k_l, v_l, lines, w_query, w_key, w_value, gain1, gain2, gain3, pooled_grad, w_out, w_in, w_back)

    xy = [ROW, NEAR_X, ROW ^ NEAR_X]
    zz = [line[0], line[1], line[0] ^ line[1]]

    token, send = wait(info, send)
    got = exchange(send, CORE)
    grad_mixed, grad_attended, grad_out_w, through_rows = through(token, slopes, w_in, mixed, steep, w_out, attended, gain2)
    token, through_rows, got = wait(token, through_rows, got)
    stays, *sends = meet(token, got, active, slopes, turned, steep)

    token, sends = wait(token, sends)
    came = [exchange(s, m) for s, m in zip(sends, xy)]
    rest_keep, rest_send, stay, leave, small = back(
        token, q_l, q_r, k_l, k_r, v_l, v_r, grad_attended, attended, inverse, expo, buckets, dense_rows, through_rows,
        hid_l, hid_r, near, near_other, far, far_other, w_query, w_key, w_value, grad_out_w)
    token, small, rest_send, leave, came = wait(token, small, rest_send, leave, came)

    rest_got = exchange(rest_send, CORE)
    hidden_got = exchange(leave, CORE)
    lines = mix([stays] + list(came))
    token, lines = wait(token, lines)
    took = [exchange(lines[k + 1], m) for k, m in enumerate(zz)]
    token, rest_got, hidden_got = wait(token, rest_got, hidden_got)

    count = rest_keep.shape[0] * rest_keep.shape[1]
    small = small + one_value(rest_got[count:])
    rest_got = rest_got[:count].reshape(rest_keep.shape)
    terms = two_terms(small)
    sends = [jnp.concatenate([added(rest_keep[4 * k : 4 * k + 4], rest_got[4 * k : 4 * k + 4]).reshape(-1, width), terms]) for k in (1, 2, 3)]
    token, sends = wait(token, sends)
    rest_came = [exchange(s, m) for s, m in zip(sends, xy)]
    home, away = ending(token, stay, hidden_got, near, far, grad_mixed, gain1, dense_rows)
    token, took, away = wait(token, took, away)

    whole = added(lines[0], *took)
    for bit in further:
        whole = added(whole, exchange(whole, bit))
    token, whole = wait(token, whole)
    back_line = [exchange(whole, m) for m in zz]
    away_got = exchange(away, ROW)
    token, rest_came = wait(token, rest_came)

    count = count // 4
    for part in rest_came:
        small = small + one_value(part[count:])
    rest_came = [part[:count].reshape((4,) + rest_keep.shape[1:]) for part in rest_came]
    piece = count // 4
    lines = added(rest_keep[:4], rest_got[:4], *rest_came).reshape(-1, width)
    send = jnp.concatenate([lines[2 * piece :], two_terms(small)])
    token, send = wait(token, send)
    took = exchange(send, line[1])
    token, took = wait(token, took)
    small = small + one_value(took[2 * piece :])
    lines = added(lines[: 2 * piece], took[: 2 * piece])
    send = jnp.concatenate([lines[piece:], two_terms(small)])
    token, send, back_line, away_got = wait(token, send, back_line, away_got)
    took = exchange(send, line[0])

    quarter = jnp.stack([whole] + back_line)
    token, quarter = wait(token, quarter)
    from_y, from_x = exchange(quarter, ROW), exchange(quarter, NEAR_X)
    token, took = wait(token, took)

    small = small + one_value(took[piece:])
    rest = added(lines[:piece], took[:piece])
    for bit in further:
        rest = added(rest, exchange(rest, bit))
        small = small + exchange(small, bit)
    token, rest = wait(token, rest)
    rest_back = [exchange(rest, m) for m in zz]
    token, rest_back, from_y, from_x = wait(token, rest_back, from_y, from_x)
    fourth = jnp.stack([rest] + rest_back)

    sends = [from_x[:2], from_y[2:], fourth, fourth]
    token, sends, quarter = wait(token, sends, quarter)
    far_a, far_b, fourth_y, fourth_x = (exchange(s, m) for s, m in zip(sends, (ROW, NEAR_X, ROW, NEAR_X)))
    other = exchange(quarter, CORE)
    near_pair = jnp.concatenate([from_y, from_x])
    grads = place(token, [(0, quarter), (4, from_y), (8, from_x)], [], width)
    token, grads, other, near_pair, far_a, far_b, fourth_y, fourth_x = wait(token, grads, other, near_pair, far_a, far_b, fourth_y, fourth_x)

    sends = [fourth_x[:2], fourth_y[2:], near_pair, jnp.concatenate([far_a, far_b]), jnp.concatenate([fourth, fourth_y, fourth_x])]
    token, sends = wait(token, sends)
    last_a, last_b, other_near, other_far, pair = (exchange(s, m) for s, m in zip(sends, (ROW, NEAR_X, CORE, CORE, CORE)))
    grads = place(token, [(12, far_a), (14, far_b), (16, other)], grads, width)
    token, grads, last_a, last_b, other_near, other_far, pair = wait(token, grads, last_a, last_b, other_near, other_far, pair)

    ends = exchange(jnp.concatenate([last_a, last_b]), CORE)
    made = sort(token, [(0, fourth), (4, fourth_y), (8, fourth_x), (12, last_a), (14, last_b), (16, pair)], [], width)
    out_back, out_in = place(token, [(20, other_near), (28, other_far)], grads, width)
    token, made, ends = wait(token, made, ends)
    out_out, out_query, out_key, out_value = sort(token, [(28, ends)], made, width)

    pool_mine, pool_other = one_value(home[rows:])[:1], one_value(away_got[rows:])[:1]
    pooled = jnp.where(doc == 0, jnp.concatenate([pool_mine, pool_other]), jnp.concatenate([pool_other, pool_mine]))
    home, away_got = home[:rows], away_got[:rows]
    input_grad = jnp.where(doc == 0, jnp.stack([home, away_got]), jnp.stack([away_got, home]))
    return (
        pooled,
        input_grad,
        out_query,
        out_key,
        out_value,
        out_out,
        out_in,
        out_back,
        small[0],
        small[1],
        small[2],
        small[8:, :BUCKETS].T,
    )

def solution(mesh):
    data = P("dp", "blk", None)
    placed = (data,) + (P(),) * 11 + (P("dp"), P("dp"), P("dp", None))
    return jax.shard_map(local, mesh=mesh, in_specs=placed, out_specs=(P("dp", None), data) + (P(),) * 10, check_vma=False)
```

```python
import functools
import jax, jax.numpy as jnp
from jax import lax
from jax.experimental import pallas as pl
from jax.experimental.pallas import tpu as pltpu
from jax.sharding import PartitionSpec as P

F32, BF16 = jnp.float32, jnp.bfloat16
NEG = -1000000000.0
NT = (((1,), (1,)), ((), ()))
TN = (((0,), (0,)), ((), ()))
NN = (((1,), (0,)), ((), ()))

def dot(a, b, dims=NN):
    return lax.dot_general(a, b, dims, preferred_element_type=F32)

def skew(row, width, dtype=F32):
    return pltpu.roll(jnp.broadcast_to(row, (128, width)), width - 127, 1, stride=1, stride_axis=0)


BUCKETS = 32
EPS = 1e-06
CORE, ROW, NEAR_X = 1, 2, 4

def rms_scale(values):
    return lax.rsqrt(jnp.mean(values * values, axis=-1, keepdims=True) + EPS)

def norm_back(grad_out, values, scale, gain):
    weighted = grad_out * gain
    inner = jnp.mean(weighted * values, axis=-1, keepdims=True)
    grad_in = scale * weighted - scale * scale * scale * values * inner
    return grad_in, jnp.sum(grad_out * values * scale, axis=0, keepdims=True)

def two_terms(value):
    high = value.astype(BF16)
    return jnp.concatenate([high, (value - high.astype(F32)).astype(BF16)])

def one_value(terms):
    return terms[:8].astype(F32) + terms[8:16].astype(F32)

def rows_of(*values):
    count = sum(v.shape[0] for v in values)
    return jnp.concatenate(list(values) + [jnp.zeros((8 - count, values[0].shape[1]), F32)])

def prepare_kernel(ids, mine, other, gain, bias, buckets, pads_h, prefixes_h, wq_h, wk_h, wv_h, hidden, query, keys, values, lines, info,
                   pads, prefixes, wq, wk, wv, sems):
    rows = mine.shape[0]
    load = [pltpu.make_async_copy(a, b, sems.at[i]) for i, (a, b) in enumerate(
        ((pads_h, pads), (prefixes_h, prefixes), (wk_h, wk), (wv_h, wv), (wq_h, wq)))]
    for copy in load:
        copy.start()
    picker = jnp.where(lax.broadcasted_iota(jnp.int32, (BUCKETS, 1), 0) == buckets[...], 1.0, 0.0).astype(BF16)
    left, total = bias[...], None
    for _ in range(3):
        part = left.astype(BF16)
        left = left - part.astype(F32)
        made = dot(part, picker)
        total = made if total is None else total + made
    lines[...] = jnp.zeros_like(lines)
    lines[:, : buckets.shape[1]] = total
    for part, raw in enumerate((mine, other)):
        tokens = raw[...].astype(F32)
        hidden[part * rows : (part + 1) * rows, :] = (tokens * rms_scale(tokens) * gain[...]).astype(BF16)
    h = hidden[...]
    load[2].wait()
    keys[...] = dot(h, wk[...]).astype(BF16)
    load[3].wait()
    values[...] = dot(h, wv[...]).astype(BF16)
    load[4].wait()
    query[...] = dot(h[:rows], wq[...]).astype(BF16)
    load[0].wait()
    load[1].wait()
    doc = ids[6]
    info[0] = 4 * rows - jnp.where(doc == 0, pads[0], pads[1])
    info[5] = jnp.where(doc == 0, prefixes[0], prefixes[1])
    for to, at in enumerate((0, 1, 2, 3)):
        info[1 + to] = ids[at]
    for to, at in enumerate((4, 5, 6)):
        info[6 + to] = ids[at]

def prepare(ids, pads, prefixes, mine, other, wq, wk, wv, gain, bias, buckets):
    rows, width = mine.shape
    span = buckets.shape[1] + 1
    heads = bias.shape[0]
    shape = lambda n: jax.ShapeDtypeStruct((n, width), BF16)
    smem, vmem, far = (pl.BlockSpec(memory_space=m) for m in (pltpu.SMEM, pltpu.VMEM, pltpu.HBM))
    return pl.pallas_call(
        prepare_kernel,
        in_specs=[smem] + [vmem] * 5 + [far] * 5,
        out_specs=[vmem] * 5 + [smem],
        out_shape=[shape(2 * rows), shape(rows), shape(2 * rows), shape(2 * rows),
                   jax.ShapeDtypeStruct((heads, span), F32), jax.ShapeDtypeStruct((16,), jnp.int32)],
        scratch_shapes=[pltpu.SMEM((2,), jnp.int32)] * 2 + [pltpu.VMEM((width, width), BF16)] * 3 + [pltpu.SemaphoreType.DMA((5,))],
        name="prepare", compiler_params=pltpu.CompilerParams(vmem_limit_bytes=14 << 20),
    )(ids, mine, other, gain, bias, buckets, pads, prefixes, wq, wk, wv)

def back_pieces(to, active, low, mine):
    @pl.loop(0, active.shape[1] // 512)
    def _(group):
        made = dot(active[:, pl.ds(pl.multiple_of(group * 512, 512), 512)], low, TN).astype(BF16)
        for b in range(4):
            rows = made[b * 128 : (b + 1) * 128]
            to[(4 * group + b) ^ mine] = jnp.concatenate([rows[:, q * 128 : (q + 1) * 128] for q in range(4)])

def in_pieces(to, slopes, turned, mine):
    @pl.loop(0, slopes.shape[1] // 512)
    def _(group):
        made = dot(turned, slopes[:, pl.ds(pl.multiple_of(group * 512, 512), 512)]).astype(BF16)
        for b in range(4):
            to[(4 * group + b) ^ mine] = made[:, b * 128 : (b + 1) * 128]

def front_kernel(info, far, far_other, near, q_l, k_l, v_l, lines, wq, wk, wv, gain1, gain2, gain3, cots, wo_h, win_h, wback_h,
                 hid_o, q_o, k_o, v_o, expo_o, inv_o, att_o, send_o, active_o, slopes_o, turned_o, mixed_o, steep_o, rows,
                 hid, qs, ks, vs, inv, att, send, active, slopes, turned, mixed, steep, wo, win, wback, expo, scores, skewed, edges, sems):
    count, width = near.shape
    hidden = win.shape[1]
    step = pl.program_id(0)
    late = [pltpu.make_async_copy(a, b, sems.at[i]) for i, (a, b) in enumerate(((wo_h, wo), (win_h, win), (wback_h, wback)))]
    early = [pltpu.make_async_copy(a, b, sems.at[3 + i]) for i, (a, b) in enumerate(((hid, hid_o), (qs, q_o), (ks, k_o), (vs, v_o)))]
    dense = [pltpu.make_async_copy(a, b, sems.at[7 + i]) for i, (a, b) in enumerate((
        (inv, inv_o), (att, att_o), (mixed, mixed_o), (turned, turned_o), (active, active_o), (steep, steep_o), (slopes, slopes_o), (send, send_o)))]
    kept = lambda g: pltpu.make_async_copy(expo, expo_o.at[pl.ds(2 * g, 2)], sems.at[15])

    @pl.when(step == 0)
    def _():
        for copy in late:
            copy.start()
        for part, raw in enumerate((far, far_other)):
            tokens = raw[...].astype(F32)
            hid[part * count : (part + 1) * count, :] = (tokens * rms_scale(tokens) * gain1[...]).astype(BF16)
        h = hid[...]
        qs[...] = dot(h[:count], wq[...]).astype(BF16)
        ks[...] = dot(h, wk[...]).astype(BF16)
        vs[...] = dot(h, wv[...]).astype(BF16)
        for copy in early:
            copy.start()
        column = lax.broadcasted_iota(jnp.int32, (1, 128), 1)
        for b in range(4):
            place = info[1 + b] + lax.broadcasted_iota(jnp.int32, (count, 1), 0)
            gate = jnp.where(place < info[0], 0.0, NEG)
            for head in range(2):
                edges[head, b * count : (b + 1) * count, :] = jnp.where(column == (64 if head == 0 else 0), gate, 0.0).astype(BF16)

    @pl.when(step > 0)
    def _():
        kept(step - 1).wait()

    cols = pl.ds(pl.multiple_of(step * 128, 128), 128)
    lane = lax.broadcasted_iota(jnp.int32, (1, 128), 1)
    first = lane < 64
    limit = info[0]
    starts = [info[1 + b] for b in range(4)]
    keys = [k_l[:count, :], k_l[count:, :], ks[:count, cols], ks[count:, cols]]
    values = jnp.concatenate([v_l[...], vs[:, cols]])
    query = jnp.concatenate([q_l[...], qs[:, cols]])
    made = []
    for head in range(2):
        mine = jnp.where(first if head == 0 else lane >= 64, 1.0, 0.0).astype(BF16)
        one = jnp.where(lane == (64 if head == 0 else 0), 1.0, 0.0).astype(BF16)
        q = query * mine + one
        v = values * mine + one
        skewed[head] = skew(lines[pl.ds(2 * step + head, 1), :], lines.shape[1])
        for b in range(4):
            s = dot(q, keys[b] * mine + edges[head, b * count : (b + 1) * count, :], NT)
            for r in range(4):
                at = starts[b] - starts[2 * (r // 2)] + 896 - 128 * (r % 2)
                part = s[r * 128 : (r + 1) * 128] + skewed[head, :, pl.ds(pl.multiple_of(at, 128), 256)]
                scores[head, r * 128 : (r + 1) * 128, b * 256 : (b + 1) * 256] = part
        for r in range(4):
            rs = slice(r * 128, (r + 1) * 128)
            value = scores[head, rs, :]
            top = jnp.max(value, axis=1, keepdims=True)
            expo[head, rs, :] = jnp.exp(value - top).astype(BF16)
        acc = dot(expo[head], v)
        made.append((acc, 1.0 / (acc[:, 64:65] if head == 0 else acc[:, 0:1])))
    (a0, i0), (a1, i1) = made
    scale = jnp.where(first, i0, i1)
    att[:, cols] = (jnp.where(first, a0, a1) * scale).astype(BF16)
    inv[:, cols] = scale
    kept(step).start()

    @pl.when(step == 3)
    def _():
        for copy in late:
            copy.wait()
        dense[0].start()
        dense[1].start()
        for part, raw in enumerate((near, far)):
            spot = slice(part * count, (part + 1) * count)
            mixed[spot, :] = raw[...].astype(F32) + dot(att[spot, :], wo[...])
        dense[2].start()
        values = mixed[...]
        inner = (values * rms_scale(values) * gain2[...]).astype(BF16)
        turned[...] = inner.T
        dense[3].start()
        total = values
        for at in range(0, hidden, 512):
            lifted = jnp.maximum(dot(inner, win[:, at : at + 512]), 0.0).astype(BF16)
            active[:, at : at + 512] = lifted
            total = total + dot(lifted, wback[at : at + 512, :])
        dense[4].start()
        scale = rms_scale(total)
        place = lax.broadcasted_iota(jnp.int32, (2 * count, 1), 0)
        place = jnp.where(place < count, place + info[1], place + (info[3] - count))
        live = jnp.where((place >= info[5]) & (place < limit), 1.0, 0.0)
        pool = jnp.sum(total * scale * gain3[...] * live, axis=0, keepdims=True)
        cot = jnp.where(info[8] == 0, cots[0:1, :], cots[1:2, :]) / (limit - info[5]).astype(F32)
        slope, grad_end = norm_back(live * cot, total, scale, gain3[...])
        steep[...] = slope
        dense[5].start()
        rows[...] = jnp.concatenate([pool, grad_end, jnp.zeros((6, width), F32)])
        low = slope.astype(BF16)
        for at in range(0, hidden, 512):
            through = dot(low, wback[at : at + 512, :], NT).astype(BF16)
            slopes[:, at : at + 512] = jnp.where(active[:, at : at + 512] > 0, through, jnp.zeros_like(through))
        dense[6].start()
        mine = info[6] & 15

        @pl.when(info[7] == 0)
        def _():
            in_pieces(send, slopes, turned[...], mine)

        @pl.when(info[7] == 1)
        def _():
            back_pieces(send, active, steep[...].astype(BF16), mine)

        dense[7].start()
        for copy in early + dense:
            copy.wait()
        kept(step).wait()

def front(info, far, far_other, near, q_l, k_l, v_l, lines, wq, wk, wv, gain1, gain2, gain3, cots, wo, win, wback):
    count, width = near.shape
    hidden = win.shape[1]
    heads, span = lines.shape
    shape = jax.ShapeDtypeStruct
    smem, free = pl.BlockSpec(memory_space=pltpu.SMEM), pl.BlockSpec(memory_space=pl.ANY)
    whole = lambda *dims: pl.BlockSpec(dims, lambda g: (0,) * len(dims))
    col = lambda n: pl.BlockSpec((n, 128), lambda g: (0, g))
    outs = [shape((2 * count, width), BF16), shape((count, width), BF16), shape((2 * count, width), BF16), shape((2 * count, width), BF16),
            shape((heads, 2 * count, 4 * count), BF16), shape((2 * count, width), F32), shape((2 * count, width), BF16),
            shape((16, width, 128), BF16), shape((2 * count, hidden), BF16), shape((2 * count, hidden), BF16),
            shape((width, 2 * count), BF16), shape((2 * count, width), F32), shape((2 * count, width), F32)]
    return pl.pallas_call(
        front_kernel,
        grid=(heads // 2,),
        in_specs=[smem, whole(count, width), whole(count, width), whole(count, width), col(count), col(2 * count), col(2 * count),
                  whole(heads, span)] + [whole(width, width)] * 3 + [whole(1, width)] * 3
                 + [whole(2, width)] + [pl.BlockSpec(memory_space=pltpu.HBM)] * 3,
        out_specs=[free] * 13 + [whole(8, width)],
        out_shape=outs + [shape((8, width), F32)],
        scratch_shapes=[pltpu.VMEM(o.shape, o.dtype) for o in outs[:4] + outs[5:]]
                       + [pltpu.VMEM(wo.shape, BF16), pltpu.VMEM(win.shape, BF16), pltpu.VMEM(wback.shape, BF16),
                          pltpu.VMEM((2, 2 * count, 4 * count), BF16), pltpu.VMEM((2, 2 * count, 4 * count), F32),
                          pltpu.VMEM((2, 128, span), F32), pltpu.VMEM((2, 4 * count, 128), BF16), pltpu.SemaphoreType.DMA((16,))],
        name="front", compiler_params=pltpu.CompilerParams(vmem_limit_bytes=40 << 20),
    )(info, far, far_other, near, q_l, k_l, v_l, lines, wq, wk, wv, gain1, gain2, gain3, cots, wo, win, wback)

def through_kernel(info, slopes_h, win_h, mixed_h, steep_h, wo_h, att_h, gain2, grad_mixed_o, grad_attended_o, grad_out_o, rows,
                   slopes, win, mixed, steep, wo, att, grad_mixed, grad_attended, grad_out, sems):
    hidden, width = slopes.shape[1], mixed.shape[1]
    chunks = []
    for i, at in enumerate(range(0, hidden, 512)):
        for a, b, s in ((slopes_h, slopes, i), (win_h, win, 4 + i)):
            chunks.append(pltpu.make_async_copy(a.at[:, at : at + 512], b.at[:, at : at + 512], sems.at[s]))
    copies = [pltpu.make_async_copy(a, b, sems.at[8 + i]) for i, (a, b) in enumerate((
        (mixed_h, mixed), (steep_h, steep), (wo_h, wo), (att_h, att)))]
    outs = [pltpu.make_async_copy(a, b, sems.at[12 + i]) for i, (a, b) in enumerate((
        (grad_mixed, grad_mixed_o), (grad_attended, grad_attended_o), (grad_out, grad_out_o)))]
    for copy in chunks + copies:
        copy.start()
    grad_inner = None
    for i, at in enumerate(range(0, hidden, 512)):
        chunks[2 * i].wait()
        chunks[2 * i + 1].wait()
        part = dot(slopes[:, at : at + 512], win[:, at : at + 512], NT)
        grad_inner = part if grad_inner is None else grad_inner + part
    copies[0].wait()
    copies[1].wait()
    values = mixed[...]
    more, grad_two = norm_back(grad_inner, values, rms_scale(values), gain2[...])
    total = steep[...] + more
    grad_mixed[...] = total
    outs[0].start()
    low = total.astype(BF16)
    copies[2].wait()
    grad_attended[...] = dot(low, wo[...], NT).astype(BF16)
    outs[1].start()
    copies[3].wait()
    grad_out[...] = dot(att[...], low, TN).astype(BF16)
    outs[2].start()
    rows[...] = jnp.concatenate([grad_two, jnp.zeros((7, width), F32)])
    for copy in outs:
        copy.wait()

def through(info, slopes, win, mixed, steep, wo, att, gain2):
    n, width = mixed.shape
    smem, vmem, free = (pl.BlockSpec(memory_space=m) for m in (pltpu.SMEM, pltpu.VMEM, pl.ANY))
    shape = jax.ShapeDtypeStruct
    given = (slopes, win, mixed, steep, wo, att)
    outs = [shape((n, width), F32), shape((n, width), BF16), shape((width, width), BF16)]
    return pl.pallas_call(
        through_kernel,
        in_specs=[smem, free, pl.BlockSpec(memory_space=pltpu.HBM)] + [free] * 4 + [vmem],
        out_specs=[free] * 3 + [vmem],
        out_shape=outs + [shape((8, width), F32)],
        scratch_shapes=[pltpu.VMEM(g.shape, g.dtype) for g in given] + [pltpu.VMEM(o.shape, o.dtype) for o in outs] + [pltpu.SemaphoreType.DMA((15,))],
        name="through", compiler_params=pltpu.CompilerParams(vmem_limit_bytes=14 << 20),
    )(info, *given, gain2)

def meet_kernel(info, got_h, active_h, slopes_h, turned_h, steep_h, *refs):
    outs, (got, chunk, turned, steep, blocks, sems) = refs[:4], refs[4:]
    order = (3, 1, 2, 0)
    high, lowest = (info[6] & 15) >> 2, info[6] & 3
    load = [pltpu.make_async_copy(got_h.at[4 * k : 4 * k + 4], got.at[k], sems.at[k]) for k in range(4)]
    save = [pltpu.make_async_copy(blocks.at[k], outs[k], sems.at[4 + k]) for k in range(4)]

    def columns(source, k):
        at = pl.ds(pl.multiple_of((k ^ high) * 512, 512), 512)
        return pltpu.make_async_copy(source.at[:, at], chunk.at[k], sems.at[8 + k])

    for side, source in ((0, active_h), (1, slopes_h)):
        @pl.when(info[7] == side)
        def _(side=side, source=source):
            extra = pltpu.make_async_copy(*((steep_h, steep) if side == 0 else (turned_h, turned)), sems.at[12])
            extra.start()
            for k in order:
                columns(source, k).start()
                load[k].start()
            extra.wait()
            low = steep[...].astype(BF16) if side == 0 else turned[...]
            for k in order:
                columns(source, k).wait()
                made = dot(chunk[k], low, TN) if side == 0 else dot(low, chunk[k])
                load[k].wait()
                for b in range(4):
                    piece = made[:, b * 128 : (b + 1) * 128]
                    if side == 0:
                        piece = made[b * 128 : (b + 1) * 128]
                        piece = jnp.concatenate([piece[:, q * 128 : (q + 1) * 128] for q in range(4)])
                    to = b ^ lowest
                    blocks[k, to] = (piece + got[k, to].astype(F32)).astype(BF16)
                save[k].start()

    for copy in save:
        copy.wait()

def meet(info, got, active, slopes, turned, steep):
    smem, free = pl.BlockSpec(memory_space=pltpu.SMEM), pl.BlockSpec(memory_space=pl.ANY)
    block = (4,) + got.shape[1:]
    n, width = steep.shape
    return pl.pallas_call(
        meet_kernel,
        in_specs=[smem] + [free] * 5,
        out_specs=[free] * 4,
        out_shape=[jax.ShapeDtypeStruct(block, BF16)] * 4,
        scratch_shapes=[pltpu.VMEM((4,) + block, BF16), pltpu.VMEM((4, n, 512), BF16), pltpu.VMEM(turned.shape, BF16), pltpu.VMEM(steep.shape, F32),
                        pltpu.VMEM((4,) + block, BF16), pltpu.SemaphoreType.DMA((13,))],
        name="meet", compiler_params=pltpu.CompilerParams(vmem_limit_bytes=20 << 20),
    )(info, got, active, slopes, turned, steep)

CLASS = {(0, 0): 0, (1, 2): 0, (0, 1): 1, (1, 3): 1, (0, 2): 2, (0, 3): 3, (1, 0): 4, (1, 1): 5}

def back_kernel(info, ql, qr, kl, kr, vl, vr, gout, out, inv, expo, buckets, dense_rows, through_rows,
                hid_l_h, hid_r_h, near_h, near_other_h, far_h, far_other_h, wq_h, wk_h, wv_h, grad_out_h,
                keep_o, send_o, stay_o, leave_o, small,
                hid_l, hid_r, near, near_other, far, far_other, wq, wk, wv, made,
                keep, send, stay, leave, dq, dk, dv, offsets, sums, acc, slopes, sems):
    count, width = near.shape
    step = pl.program_id(0)
    pairs = width // 128
    late = [pltpu.make_async_copy(a, b, sems.at[i]) for i, (a, b) in enumerate((
        (hid_l_h, hid_l), (hid_r_h, hid_r), (near_h, near), (near_other_h, near_other), (far_h, far), (far_other_h, far_other),
        (wq_h, wq), (wk_h, wk), (wv_h, wv), (grad_out_h, made.at[0:width])))]
    done = [pltpu.make_async_copy(a, b, sems.at[10 + i]) for i, (a, b) in enumerate(((send, send_o), (keep, keep_o), (leave, leave_o), (stay, stay_o)))]

    @pl.when(step == 0)
    def _():
        for copy in late:
            copy.start()

    cols = pl.ds(pl.multiple_of(step * 128, 128), 128)
    lane = lax.broadcasted_iota(jnp.int32, (1, 128), 1)
    starts = [info[1 + b] for b in range(4)]
    keys = jnp.concatenate([kl[...], kr[...]])
    values = jnp.concatenate([vl[...], vr[...]])
    query = jnp.concatenate([ql[...], qr[...]])
    scaled = gout[...].astype(F32) * inv[...]
    prod = scaled * out[...].astype(F32)
    low = scaled.astype(BF16)
    query_t, low_t = query.T, low.T
    grads_q, grads_k, grads_v = None, [], []
    for head in range(2):
        mine = (lane < 64) if head == 0 else (lane >= 64)
        base = 64 if head == 0 else 0
        pick = jnp.where(mine, 1.0, 0.0).astype(BF16)
        delta = jnp.sum(jnp.where(mine, prod, 0.0), axis=1, keepdims=True)
        high = delta.astype(BF16).astype(F32)
        extra = jnp.where(lane == base, high, jnp.where(lane == base + 1, delta - high, 0.0)).astype(BF16)
        grad = low * pick + extra
        minus = jnp.where((lane == base) | (lane == base + 1), -1.0, 0.0).astype(BF16)
        for b in range(4):
            spot = slice(b * count, (b + 1) * count)
            ds = dot(grad, values[spot] * pick + minus, NT) * expo[head, :, spot].astype(F32)
            slopes[head, :, spot] = ds.astype(BF16)
            for chunk in range(2):
                upper, lower = (ds[chunk * count + r * 128 : chunk * count + (r + 1) * 128] for r in range(2))
                group = CLASS[chunk, b]
                block = jnp.concatenate([lower[:, :128], lower[:, 128:] + upper[:, :128], upper[:, 128:]], axis=1)
                if (chunk, b) in ((1, 2), (1, 3)):
                    block = block + sums[head, group]
                sums[head, group] = block
        part = dot(slopes[head], keys * pick)
        grads_q = part if grads_q is None else grads_q + part
        half = slice(head * 64, (head + 1) * 64)
        grads_k.append(dot(query_t[half], slopes[head]))
        grads_v.append(dot(low_t[half], expo[head]))
    dq[:, cols] = grads_q.astype(BF16)
    dk[:, cols] = jnp.concatenate(grads_k).astype(BF16).T
    dv[:, cols] = jnp.concatenate(grads_v).astype(BF16).T
    for head in range(2):
        acc[head] = jnp.zeros(acc.shape[1:], F32)
        for (chunk, b), group in CLASS.items():
            if (chunk, b) not in ((1, 2), (1, 3)):
                at = starts[b] - starts[2 * chunk] + 768
                to = pl.ds(pl.multiple_of(at, 128), 384)
                acc[head, :, to] += sums[head, group]
        rest = acc[head]
        n = 64
        while n >= 8:
            rest = rest[:n] + pltpu.roll(rest[n:], 2048 - n, 1)
            n //= 2
        line = rest[7:8]
        for r in range(6, -1, -1):
            line = rest[r : r + 1] + pltpu.roll(line, 2047, 1)
        offsets[pl.ds(2 * step + head, 1), :] = pltpu.roll(line, 127, 1)

    @pl.when(step == pairs - 1)
    def _():
        for copy in late:
            copy.wait()
        made[width : 2 * width, :] = (dot(hid_l[:count, :], dq[:count, :], TN) + dot(hid_r[:count, :], dq[count:, :], TN)).astype(BF16)
        for at, grads in ((2 * width, dk), (3 * width, dv)):
            made[at : at + width, :] = (dot(hid_l[...], grads[: 2 * count, :], TN) + dot(hid_r[...], grads[2 * count :, :], TN)).astype(BF16)
        me = info[6]
        size = made.shape[0] // 32

        @pl.loop(0, 16)
        def _(r):
            keep[r] = made[pl.ds(pl.multiple_of((r ^ me) * size, size), size), :]
            send[pl.ds(pl.multiple_of(r * size, size), size), :] = made[pl.ds(pl.multiple_of(((r + 16) ^ me) * size, size), size), :]

        gain = jnp.zeros((1, width), F32)
        for b, raw in enumerate((near, near_other, far, far_other)):
            spot = slice(b * count, (b + 1) * count)
            grad = dot(dk[spot, :], wk[...], NT) + dot(dv[spot, :], wv[...], NT)
            half = slice((b // 2) * count, (b // 2 + 1) * count)
            if b % 2 == 0:
                grad = grad + dot(dq[half, :], wq[...], NT)
                stay[half, :] = grad
            else:
                leave[half, :] = grad.astype(BF16)
            tokens = raw[...].astype(F32)
            gain = gain + jnp.sum(grad * (tokens * rms_scale(tokens)), axis=0, keepdims=True)
        leave[2 * count :, :] = two_terms(rows_of(dense_rows[0:1, :]))
        picker = jnp.where(lax.broadcasted_iota(jnp.int32, (128, 1), 0) == buckets[...], 1.0, 0.0).astype(BF16)
        left = offsets[...][:, : buckets.shape[1]]
        bias = None
        for _ in range(3):
            part = left.astype(BF16)
            left = left - part.astype(F32)
            bias = dot(part, picker, NT) if bias is None else bias + dot(part, picker, NT)
        bias = jnp.concatenate([bias, jnp.zeros((bias.shape[0], width - 128), F32)], axis=1)
        line = bias[0:1]
        for h in range(1, bias.shape[0]):
            line = line + pltpu.roll(bias[h : h + 1], 32 * h, 1)
        total = rows_of(gain, through_rows[0:1, :], dense_rows[1:2, :], line)
        small[...] = total
        send[16 * size :, :] = two_terms(total)
        for copy in done:
            copy.start()
        for copy in done:
            copy.wait()

def back(info, ql, qr, kl, kr, vl, vr, gout, out, inv, expo, buckets, dense_rows, through_rows,
         hid_l, hid_r, near, near_other, far, far_other, wq, wk, wv, grad_out):
    count, width = near.shape
    smem, free = pl.BlockSpec(memory_space=pltpu.SMEM), pl.BlockSpec(memory_space=pl.ANY)
    whole = lambda *dims: pl.BlockSpec(dims, lambda g: (0,) * len(dims))
    col = lambda n: pl.BlockSpec((n, 128), lambda g: (0, g))
    shape = jax.ShapeDtypeStruct
    size = 4 * width // 32
    outs = [shape((16, size, width), BF16), shape((16 * size + 16, width), BF16), shape((2 * count, width), F32), shape((2 * count + 16, width), BF16)]
    given = (hid_l, hid_r, near, near_other, far, far_other, wq, wk, wv)
    return pl.pallas_call(
        back_kernel,
        grid=(width // 128,),
        in_specs=[smem, col(count), col(count)] + [col(2 * count)] * 7 + [pl.BlockSpec((2, 2 * count, 4 * count), lambda g: (g, 0, 0)),
                  whole(*buckets.shape), whole(8, width), whole(8, width)] + [free] * 10,
        out_specs=[free] * 4 + [whole(8, width)],
        out_shape=outs + [shape((8, width), F32)],
        scratch_shapes=[pltpu.VMEM(g.shape, BF16) for g in given] + [pltpu.VMEM((4 * width, width), BF16)]
                       + [pltpu.VMEM(o.shape, o.dtype) for o in outs]
                       + [pltpu.VMEM((2 * count, width), BF16), pltpu.VMEM((4 * count, width), BF16), pltpu.VMEM((4 * count, width), BF16),
                          pltpu.VMEM((8, 2048), F32), pltpu.VMEM((2, 6, 128, 384), F32), pltpu.VMEM((2, 128, 2048), F32),
                          pltpu.VMEM((2, 2 * count, 4 * count), BF16), pltpu.SemaphoreType.DMA((14,))],
        name="back", compiler_params=pltpu.CompilerParams(vmem_limit_bytes=44 << 20),
    )(info, ql, qr, kl, kr, vl, vr, gout, out, inv, expo, buckets, dense_rows, through_rows, *given, grad_out)

def ending_kernel(info, stay, came, near, far, grad_mixed, gain, dense_rows, home, away):
    count, width = near.shape
    for part, raw in enumerate((near, far)):
        spot = slice(part * count, (part + 1) * count)
        tokens = raw[...].astype(F32)
        grad = stay[spot, :] + came[spot, :].astype(F32)
        more, _ = norm_back(grad, tokens, rms_scale(tokens), gain[...])
        value = (grad_mixed[spot, :] + more).astype(BF16)
        if part == 0:
            home[:count, :] = value
        else:
            away[:count, :] = value
    alive = (info[0] - info[5]).astype(F32)
    pool = two_terms((rows_of(dense_rows[0:1, :]) + one_value(came[2 * count :, :])) / alive)
    home[count:, :] = pool
    away[count:, :] = pool

def ending(info, stay, came, near, far, grad_mixed, gain, dense_rows):
    count, width = near.shape
    smem, vmem = pl.BlockSpec(memory_space=pltpu.SMEM), pl.BlockSpec(memory_space=pltpu.VMEM)
    shape = jax.ShapeDtypeStruct((count + 16, width), BF16)
    return pl.pallas_call(
        ending_kernel, in_specs=[smem] + [vmem] * 7, out_specs=[vmem] * 2, out_shape=[shape, shape], name="ending", compiler_params=pltpu.CompilerParams(vmem_limit_bytes=10 << 20)
    )(info, stay, came, near, far, grad_mixed, gain, dense_rows)

def place_kernel(firsts, info, *refs):
    parts, (back, front, rows, columns, sems) = refs[: len(firsts)], refs[-5:]
    mine = info[6] & 15
    for side in range(2):
        @pl.when(info[7] == side)
        def _(side=side):
            copies, n = [], 0
            for part, first in zip(parts, firsts):
                for i in range(part.shape[0]):
                    r = first + i
                    to = pl.ds(pl.multiple_of(((r & 15) ^ mine) * 128, 128), 128)
                    if (r >= 16) == (side == 1):
                        for q in range(4):
                            rows[n, :, q * 128 : (q + 1) * 128] = part[i, q * 128 : (q + 1) * 128, :].astype(F32)
                        copies.append(pltpu.make_async_copy(rows.at[n], back.at[to, :], sems.at[n]))
                    else:
                        columns[n] = part[i].astype(F32)
                        copies.append(pltpu.make_async_copy(columns.at[n], front.at[:, to], sems.at[n]))
                    copies[-1].start()
                    n += 1
            for copy in copies:
                copy.wait()

def place(info, parts, made, width):
    smem, vmem, far = (pl.BlockSpec(memory_space=m) for m in (pltpu.SMEM, pltpu.VMEM, pltpu.HBM))
    shape = jax.ShapeDtypeStruct
    count = sum(p.shape[0] for _, p in parts)
    return pl.pallas_call(
        functools.partial(place_kernel, [first for first, _ in parts]),
        in_specs=[smem] + [vmem] * len(parts) + [far] * len(made),
        out_specs=[far] * 2,
        out_shape=[shape((16 * 128, width), F32), shape((width, 16 * 128), F32)],
        scratch_shapes=[pltpu.VMEM((count, 128, width), F32), pltpu.VMEM((count, width, 128), F32), pltpu.SemaphoreType.DMA((count,))],
        input_output_aliases={1 + len(parts) + i: i for i in range(len(made))},
        name="place", compiler_params=pltpu.CompilerParams(vmem_limit_bytes=20 << 20),
    )(info, *[p for _, p in parts], *made)

def sort_kernel(firsts, info, *refs):
    parts, made, (tall, sems) = refs[: len(firsts)], refs[-6:-2], refs[-2:]
    size = parts[0].shape[1]
    mine = info[6]
    pieces = []
    for part, first in zip(parts, firsts):
        for i in range(part.shape[0]):
            tall[len(pieces)] = part[i].astype(F32)
            pieces.append(first + i)
    for top in range(4):
        @pl.when((mine >> 3) == top)
        def _(top=top):
            copies = []
            for n, r in enumerate(pieces):
                to = pl.ds(pl.multiple_of(((r ^ mine) & 7) * size, size), size)
                copies.append(pltpu.make_async_copy(tall.at[n], made[top ^ (r >> 3)].at[to, :], sems.at[n]))
                copies[-1].start()
            for copy in copies:
                copy.wait()

def sort(info, parts, made, width):
    smem, vmem, far = (pl.BlockSpec(memory_space=m) for m in (pltpu.SMEM, pltpu.VMEM, pltpu.HBM))
    shape = jax.ShapeDtypeStruct((width, width), F32)
    count = sum(p.shape[0] for _, p in parts)
    return pl.pallas_call(
        functools.partial(sort_kernel, [first for first, _ in parts]),
        in_specs=[smem] + [vmem] * len(parts) + [far] * len(made),
        out_specs=[far] * 4,
        out_shape=[shape] * 4,
        scratch_shapes=[pltpu.VMEM((count,) + parts[0][1].shape[1:], F32), pltpu.SemaphoreType.DMA((count,))],
        input_output_aliases={1 + len(parts) + i: i for i in range(len(made))},
        name="sort", compiler_params=pltpu.CompilerParams(vmem_limit_bytes=12 << 20),
    )(info, *[p for _, p in parts], *made)

def mix_kernel(*refs):
    for k in range(4):
        refs[4 + k][...] = added(*[term[k] for term in refs[:4]])

def mix(terms):
    block = terms[0].shape[1:]
    vmem = pl.BlockSpec(memory_space=pltpu.VMEM)
    return pl.pallas_call(
        mix_kernel, in_specs=[vmem] * 4, out_specs=[vmem] * 4, out_shape=[jax.ShapeDtypeStruct(block, BF16)] * 4, name="mix", compiler_params=pltpu.CompilerParams(vmem_limit_bytes=10 << 20),
    )(*terms)

def exchange(value, bits):
    size = lax.axis_size("dp") * lax.axis_size("blk")
    return lax.ppermute(value, ("dp", "blk"), [(i, i ^ bits) for i in range(size)])

def wait(*values):
    return lax.optimization_barrier(values)

def added(*terms):
    total = terms[0].astype(F32)
    for term in terms[1:]:
        total = total + term.astype(F32)
    return total.astype(BF16)

def local(inputs, w_query, w_key, w_value, w_out, w_in, w_back, norm1_gain, norm2_gain, final_gain, bias_table, bucket_table, prefix_len, pad_len, pooled_grad):
    rows, width = inputs.shape[1:]
    spot, far_off = lax.axis_index("blk"), lax.axis_index("dp")
    doc, core = spot // 2, spot % 2
    block = [doc * 2 + core, doc * 2 + 1 - core, (1 - doc) * 2 + core, (1 - doc) * 2 + 1 - core]
    line = [8, 16]
    further = [32 << b for b in range((lax.axis_size("dp") // 8).bit_length() - 1)]
    piece = core * 16 + doc * 4 + (far_off % 2) * 8 + (far_off // 2) % 4
    near = jnp.where(doc == 0, inputs[0], inputs[1])
    far_send = jnp.where(doc == 0, inputs[1], inputs[0])
    near, far_send = wait(near, far_send)
    far = exchange(far_send, ROW)
    near_other = exchange(near, CORE)
    slot = jnp.arange(8, dtype=jnp.int32)
    ids = jnp.zeros_like(slot)
    for i, value in enumerate([b * rows for b in block] + [piece, core, doc]):
        ids = jnp.where(slot == i, value, ids)
    gain1, gain2, gain3 = norm1_gain[None, :], norm2_gain[None, :], final_gain[None, :]
    buckets = bucket_table[None, :]
    hid_l, q_l, k_l, v_l, lines, info = prepare(ids, pad_len, prefix_len, near, near_other, w_query, w_key, w_value, gain1, bias_table.T, buckets)
    far, info = wait(far, info)
    far_other = exchange(far, CORE)
    (hid_r, q_r, k_r, v_r, expo, inverse, attended, send, active, slopes, turned, mixed, steep, dense_rows) = front(
        info, far, far_other, near, q_l, k_l, v_l, lines, w_query, w_key, w_value, gain1, gain2, gain3, pooled_grad, w_out, w_in, w_back)

    xy = [ROW, NEAR_X, ROW ^ NEAR_X]
    zz = [line[0], line[1], line[0] ^ line[1]]

    token, send = wait(info, send)
    got = exchange(send, CORE)
    grad_mixed, grad_attended, grad_out_w, through_rows = through(token, slopes, w_in, mixed, steep, w_out, attended, gain2)
    token, through_rows, got = wait(token, through_rows, got)
    stays, *sends = meet(token, got, active, slopes, turned, steep)

    token, sends = wait(token, sends)
    came = [exchange(s, m) for s, m in zip(sends, xy)]
    rest_keep, rest_send, stay, leave, small = back(
        token, q_l, q_r, k_l, k_r, v_l, v_r, grad_attended, attended, inverse, expo, buckets, dense_rows, through_rows,
        hid_l, hid_r, near, near_other, far, far_other, w_query, w_key, w_value, grad_out_w)
    token, small, rest_send, leave, came = wait(token, small, rest_send, leave, came)

    rest_got = exchange(rest_send, CORE)
    hidden_got = exchange(leave, CORE)
    lines = mix([stays] + list(came))
    token, lines = wait(token, lines)
    took = [exchange(lines[k + 1], m) for k, m in enumerate(zz)]
    token, rest_got, hidden_got = wait(token, rest_got, hidden_got)

    count = rest_keep.shape[0] * rest_keep.shape[1]
    small = small + one_value(rest_got[count:])
    rest_got = rest_got[:count].reshape(rest_keep.shape)
    terms = two_terms(small)
    sends = [jnp.concatenate([added(rest_keep[4 * k : 4 * k + 4], rest_got[4 * k : 4 * k + 4]).reshape(-1, width), terms]) for k in (1, 2, 3)]
    token, sends = wait(token, sends)
    rest_came = [exchange(s, m) for s, m in zip(sends, xy)]
    home, away = ending(token, stay, hidden_got, near, far, grad_mixed, gain1, dense_rows)
    token, took, away = wait(token, took, away)

    whole = added(lines[0], *took)
    for bit in further:
        whole = added(whole, exchange(whole, bit))
    token, whole = wait(token, whole)
    back_line = [exchange(whole, m) for m in zz]
    away_got = exchange(away, ROW)
    token, rest_came = wait(token, rest_came)

    count = count // 4
    for part in rest_came:
        small = small + one_value(part[count:])
    rest_came = [part[:count].reshape((4,) + rest_keep.shape[1:]) for part in rest_came]
    piece = count // 4
    lines = added(rest_keep[:4], rest_got[:4], *rest_came).reshape(-1, width)
    send = jnp.concatenate([lines[piece : 2 * piece], lines[3 * piece :], two_terms(small)])
    token, send = wait(token, send)
    took = exchange(send, line[0])
    token, took = wait(token, took)
    small = small + one_value(took[2 * piece :])
    send = jnp.concatenate([added(lines[2 * piece : 3 * piece], took[piece : 2 * piece]), two_terms(small)])
    lines = added(lines[:piece], took[:piece])
    token, send, back_line, away_got = wait(token, send, back_line, away_got)
    took = exchange(send, line[1])

    quarter = jnp.stack([whole] + back_line)
    token, quarter = wait(token, quarter)
    from_y, from_x = exchange(quarter, ROW), exchange(quarter, NEAR_X)
    token, took = wait(token, took)

    small = small + one_value(took[piece:])
    rest = added(lines, took[:piece])
    for bit in further:
        rest = added(rest, exchange(rest, bit))
        small = small + exchange(small, bit)
    token, rest = wait(token, rest)
    rest_back = [exchange(rest, m) for m in zz]
    token, rest_back, from_y, from_x = wait(token, rest_back, from_y, from_x)
    fourth = jnp.stack([rest] + rest_back)

    sends = [from_x[:2], from_y[2:], fourth, fourth]
    token, sends, quarter = wait(token, sends, quarter)
    far_a, far_b, fourth_y, fourth_x = (exchange(s, m) for s, m in zip(sends, (ROW, NEAR_X, ROW, NEAR_X)))
    other = exchange(quarter, CORE)
    near_pair = jnp.concatenate([from_y, from_x])
    grads = place(token, [(0, quarter), (4, from_y), (8, from_x)], [], width)
    token, grads, other, near_pair, far_a, far_b, fourth_y, fourth_x = wait(token, grads, other, near_pair, far_a, far_b, fourth_y, fourth_x)

    sends = [fourth_x[:2], fourth_y[2:], near_pair, jnp.concatenate([far_a, far_b]), jnp.concatenate([fourth, fourth_y, fourth_x])]
    token, sends = wait(token, sends)
    last_a, last_b, other_near, other_far, pair = (exchange(s, m) for s, m in zip(sends, (ROW, NEAR_X, CORE, CORE, CORE)))
    grads = place(token, [(12, far_a), (14, far_b), (16, other)], grads, width)
    token, grads, last_a, last_b, other_near, other_far, pair = wait(token, grads, last_a, last_b, other_near, other_far, pair)

    ends = exchange(jnp.concatenate([last_a, last_b]), CORE)
    made = sort(token, [(0, fourth), (4, fourth_y), (8, fourth_x), (12, last_a), (14, last_b), (16, pair)], [], width)
    out_back, out_in = place(token, [(20, other_near), (28, other_far)], grads, width)
    token, made, ends = wait(token, made, ends)
    out_out, out_query, out_key, out_value = sort(token, [(28, ends)], made, width)

    pool_mine, pool_other = one_value(home[rows:])[:1], one_value(away_got[rows:])[:1]
    pooled = jnp.where(doc == 0, jnp.concatenate([pool_mine, pool_other]), jnp.concatenate([pool_other, pool_mine]))
    home, away_got = home[:rows], away_got[:rows]
    input_grad = jnp.where(doc == 0, jnp.stack([home, away_got]), jnp.stack([away_got, home]))
    return (
        pooled,
        input_grad,
        out_query,
        out_key,
        out_value,
        out_out,
        out_in,
        out_back,
        small[0],
        small[1],
        small[2],
        small[3, : bias_table.size].reshape(bias_table.shape[::-1]).T,
    )

def solution(mesh):
    data = P("dp", "blk", None)
    placed = (data,) + (P(),) * 11 + (P("dp"), P("dp"), P("dp", None))
    return jax.shard_map(local, mesh=mesh, in_specs=placed, out_specs=(P("dp", None), data) + (P(),) * 10, check_vma=False)
```

```python
import functools
import jax, jax.numpy as jnp
from jax import lax
from jax.experimental import pallas as pl
from jax.experimental.pallas import tpu as pltpu
from jax.sharding import PartitionSpec as P

F32, BF16 = jnp.float32, jnp.bfloat16
NEG = -1000000000.0
NT = (((1,), (1,)), ((), ()))
TN = (((0,), (0,)), ((), ()))
NN = (((1,), (0,)), ((), ()))

def dot(a, b, dims=NN):
    return lax.dot_general(a, b, dims, preferred_element_type=F32)

def skew(row, width, dtype=F32):
    return pltpu.roll(jnp.broadcast_to(row, (128, width)), width - 127, 1, stride=1, stride_axis=0)


BUCKETS = 32
EPS = 1e-06
CORE, ROW, NEAR_X = 1, 2, 4

def rms_scale(values):
    return lax.rsqrt(jnp.mean(values * values, axis=-1, keepdims=True) + EPS)

def norm_back(grad_out, values, scale, gain):
    weighted = grad_out * gain
    inner = jnp.mean(weighted * values, axis=-1, keepdims=True)
    grad_in = scale * weighted - scale * scale * scale * values * inner
    return grad_in, jnp.sum(grad_out * values * scale, axis=0, keepdims=True)

def two_terms(value):
    high = value.astype(BF16)
    return jnp.concatenate([high, (value - high.astype(F32)).astype(BF16)])

def one_value(terms):
    return terms[:8].astype(F32) + terms[8:16].astype(F32)

def rows_of(*values):
    count = sum(v.shape[0] for v in values)
    return jnp.concatenate(list(values) + [jnp.zeros((8 - count, values[0].shape[1]), F32)])

def prepare_kernel(ids, mine, other, gain, bias, buckets, pads_h, prefixes_h, wq_h, wk_h, wv_h, hidden, query, keys, values, lines, info,
                   pads, prefixes, wq, wk, wv, sems):
    rows = mine.shape[0]
    load = [pltpu.make_async_copy(a, b, sems.at[i]) for i, (a, b) in enumerate(
        ((pads_h, pads), (prefixes_h, prefixes), (wk_h, wk), (wv_h, wv), (wq_h, wq)))]
    for copy in load:
        copy.start()
    picker = jnp.where(lax.broadcasted_iota(jnp.int32, (BUCKETS, 1), 0) == buckets[...], 1.0, 0.0).astype(BF16)
    left, total = bias[...], None
    for _ in range(3):
        part = left.astype(BF16)
        left = left - part.astype(F32)
        made = dot(part, picker)
        total = made if total is None else total + made
    lines[...] = jnp.zeros_like(lines)
    lines[:, : buckets.shape[1]] = total
    for part, raw in enumerate((mine, other)):
        tokens = raw[...].astype(F32)
        hidden[part * rows : (part + 1) * rows, :] = (tokens * rms_scale(tokens) * gain[...]).astype(BF16)
    h = hidden[...]
    load[2].wait()
    keys[...] = dot(h, wk[...]).astype(BF16)
    load[3].wait()
    values[...] = dot(h, wv[...]).astype(BF16)
    load[4].wait()
    query[...] = dot(h[:rows], wq[...]).astype(BF16)
    load[0].wait()
    load[1].wait()
    doc = ids[6]
    info[0] = 4 * rows - jnp.where(doc == 0, pads[0], pads[1])
    info[5] = jnp.where(doc == 0, prefixes[0], prefixes[1])
    for to, at in enumerate((0, 1, 2, 3)):
        info[1 + to] = ids[at]
    for to, at in enumerate((4, 5, 6)):
        info[6 + to] = ids[at]

def prepare(ids, pads, prefixes, mine, other, wq, wk, wv, gain, bias, buckets):
    rows, width = mine.shape
    span = buckets.shape[1] + 1
    heads = bias.shape[0]
    shape = lambda n: jax.ShapeDtypeStruct((n, width), BF16)
    smem, vmem, far = (pl.BlockSpec(memory_space=m) for m in (pltpu.SMEM, pltpu.VMEM, pltpu.HBM))
    return pl.pallas_call(
        prepare_kernel,
        in_specs=[smem] + [vmem] * 5 + [far] * 5,
        out_specs=[vmem] * 5 + [smem],
        out_shape=[shape(2 * rows), shape(rows), shape(2 * rows), shape(2 * rows),
                   jax.ShapeDtypeStruct((heads, span), F32), jax.ShapeDtypeStruct((16,), jnp.int32)],
        scratch_shapes=[pltpu.SMEM((2,), jnp.int32)] * 2 + [pltpu.VMEM((width, width), BF16)] * 3 + [pltpu.SemaphoreType.DMA((5,))],
        name="prepare", compiler_params=pltpu.CompilerParams(vmem_limit_bytes=60 << 20),
    )(ids, mine, other, gain, bias, buckets, pads, prefixes, wq, wk, wv)

def back_pieces(to, active, low, mine):
    @pl.loop(0, active.shape[1] // 512)
    def _(group):
        made = dot(active[:, pl.ds(pl.multiple_of(group * 512, 512), 512)], low, TN).astype(BF16)
        for b in range(4):
            rows = made[b * 128 : (b + 1) * 128]
            to[(4 * group + b) ^ mine] = jnp.concatenate([rows[:, q * 128 : (q + 1) * 128] for q in range(4)])

def in_pieces(to, slopes, turned, mine):
    @pl.loop(0, slopes.shape[1] // 512)
    def _(group):
        made = dot(turned, slopes[:, pl.ds(pl.multiple_of(group * 512, 512), 512)]).astype(BF16)
        for b in range(4):
            to[(4 * group + b) ^ mine] = made[:, b * 128 : (b + 1) * 128]

def front_kernel(info, far, far_other, near, q_l, k_l, v_l, lines, wq, wk, wv, gain1, gain2, gain3, cots, wo_h, win_h, wback_h,
                 hid_o, q_o, k_o, v_o, expo_o, inv_o, att_o, send_o, active_o, slopes_o, turned_o, mixed_o, steep_o, rows,
                 hid, qs, ks, vs, inv, att, send, active, slopes, turned, mixed, steep, wo, win, wback, expo, scores, skewed, edges, sems):
    count, width = near.shape
    hidden = win.shape[1]
    step = pl.program_id(0)
    late = [pltpu.make_async_copy(a, b, sems.at[i]) for i, (a, b) in enumerate(((wo_h, wo), (win_h, win), (wback_h, wback)))]
    early = [pltpu.make_async_copy(a, b, sems.at[3 + i]) for i, (a, b) in enumerate(((hid, hid_o), (qs, q_o), (ks, k_o), (vs, v_o)))]
    dense = [pltpu.make_async_copy(a, b, sems.at[7 + i]) for i, (a, b) in enumerate((
        (inv, inv_o), (att, att_o), (mixed, mixed_o), (turned, turned_o), (active, active_o), (steep, steep_o), (slopes, slopes_o), (send, send_o)))]
    kept = lambda g: pltpu.make_async_copy(expo, expo_o.at[pl.ds(2 * g, 2)], sems.at[15])

    @pl.when(step == 0)
    def _():
        for copy in late:
            copy.start()
        for part, raw in enumerate((far, far_other)):
            tokens = raw[...].astype(F32)
            hid[part * count : (part + 1) * count, :] = (tokens * rms_scale(tokens) * gain1[...]).astype(BF16)
        h = hid[...]
        qs[...] = dot(h[:count], wq[...]).astype(BF16)
        ks[...] = dot(h, wk[...]).astype(BF16)
        vs[...] = dot(h, wv[...]).astype(BF16)
        for copy in early:
            copy.start()
        column = lax.broadcasted_iota(jnp.int32, (1, 128), 1)
        for b in range(4):
            place = info[1 + b] + lax.broadcasted_iota(jnp.int32, (count, 1), 0)
            gate = jnp.where(place < info[0], 0.0, NEG)
            for head in range(2):
                edges[head, b * count : (b + 1) * count, :] = jnp.where(column == (64 if head == 0 else 0), gate, 0.0).astype(BF16)

    @pl.when(step > 0)
    def _():
        kept(step - 1).wait()

    cols = pl.ds(pl.multiple_of(step * 128, 128), 128)
    lane = lax.broadcasted_iota(jnp.int32, (1, 128), 1)
    first = lane < 64
    limit = info[0]
    starts = [info[1 + b] for b in range(4)]
    keys = [k_l[:count, :], k_l[count:, :], ks[:count, cols], ks[count:, cols]]
    values = jnp.concatenate([v_l[...], vs[:, cols]])
    query = jnp.concatenate([q_l[...], qs[:, cols]])
    made = []
    for head in range(2):
        mine = jnp.where(first if head == 0 else lane >= 64, 1.0, 0.0).astype(BF16)
        one = jnp.where(lane == (64 if head == 0 else 0), 1.0, 0.0).astype(BF16)
        q = query * mine + one
        v = values * mine + one
        skewed[head] = skew(lines[pl.ds(2 * step + head, 1), :], lines.shape[1])
        for b in range(4):
            s = dot(q, keys[b] * mine + edges[head, b * count : (b + 1) * count, :], NT)
            for r in range(4):
                at = starts[b] - starts[2 * (r // 2)] + 896 - 128 * (r % 2)
                part = s[r * 128 : (r + 1) * 128] + skewed[head, :, pl.ds(pl.multiple_of(at, 128), 256)]
                scores[head, r * 128 : (r + 1) * 128, b * 256 : (b + 1) * 256] = part
        for r in range(4):
            rs = slice(r * 128, (r + 1) * 128)
            value = scores[head, rs, :]
            top = jnp.max(value, axis=1, keepdims=True)
            expo[head, rs, :] = jnp.exp(value - top).astype(BF16)
        acc = dot(expo[head], v)
        made.append((acc, 1.0 / (acc[:, 64:65] if head == 0 else acc[:, 0:1])))
    (a0, i0), (a1, i1) = made
    scale = jnp.where(first, i0, i1)
    att[:, cols] = (jnp.where(first, a0, a1) * scale).astype(BF16)
    inv[:, cols] = scale
    kept(step).start()

    @pl.when(step == 3)
    def _():
        for copy in late:
            copy.wait()
        dense[0].start()
        dense[1].start()
        for part, raw in enumerate((near, far)):
            spot = slice(part * count, (part + 1) * count)
            mixed[spot, :] = raw[...].astype(F32) + dot(att[spot, :], wo[...])
        dense[2].start()
        values = mixed[...]
        inner = (values * rms_scale(values) * gain2[...]).astype(BF16)
        turned[...] = inner.T
        dense[3].start()
        total = values
        for at in range(0, hidden, 512):
            lifted = jnp.maximum(dot(inner, win[:, at : at + 512]), 0.0).astype(BF16)
            active[:, at : at + 512] = lifted
            total = total + dot(lifted, wback[at : at + 512, :])
        dense[4].start()
        scale = rms_scale(total)
        place = lax.broadcasted_iota(jnp.int32, (2 * count, 1), 0)
        place = jnp.where(place < count, place + info[1], place + (info[3] - count))
        live = jnp.where((place >= info[5]) & (place < limit), 1.0, 0.0)
        pool = jnp.sum(total * scale * gain3[...] * live, axis=0, keepdims=True)
        cot = jnp.where(info[8] == 0, cots[0:1, :], cots[1:2, :]) / (limit - info[5]).astype(F32)
        slope, grad_end = norm_back(live * cot, total, scale, gain3[...])
        steep[...] = slope
        dense[5].start()
        rows[...] = jnp.concatenate([pool, grad_end, jnp.zeros((6, width), F32)])
        low = slope.astype(BF16)
        for at in range(0, hidden, 512):
            through = dot(low, wback[at : at + 512, :], NT).astype(BF16)
            slopes[:, at : at + 512] = jnp.where(active[:, at : at + 512] > 0, through, jnp.zeros_like(through))
        dense[6].start()
        mine = info[6] & 15

        @pl.when(info[7] == 0)
        def _():
            in_pieces(send, slopes, turned[...], mine)

        @pl.when(info[7] == 1)
        def _():
            back_pieces(send, active, steep[...].astype(BF16), mine)

        dense[7].start()
        for copy in early + dense:
            copy.wait()
        kept(step).wait()

def front(info, far, far_other, near, q_l, k_l, v_l, lines, wq, wk, wv, gain1, gain2, gain3, cots, wo, win, wback):
    count, width = near.shape
    hidden = win.shape[1]
    heads, span = lines.shape
    shape = jax.ShapeDtypeStruct
    smem, free = pl.BlockSpec(memory_space=pltpu.SMEM), pl.BlockSpec(memory_space=pl.ANY)
    whole = lambda *dims: pl.BlockSpec(dims, lambda g: (0,) * len(dims))
    col = lambda n: pl.BlockSpec((n, 128), lambda g: (0, g))
    outs = [shape((2 * count, width), BF16), shape((count, width), BF16), shape((2 * count, width), BF16), shape((2 * count, width), BF16),
            shape((heads, 2 * count, 4 * count), BF16), shape((2 * count, width), F32), shape((2 * count, width), BF16),
            shape((16, width, 128), BF16), shape((2 * count, hidden), BF16), shape((2 * count, hidden), BF16),
            shape((width, 2 * count), BF16), shape((2 * count, width), F32), shape((2 * count, width), F32)]
    return pl.pallas_call(
        front_kernel,
        grid=(heads // 2,),
        in_specs=[smem, whole(count, width), whole(count, width), whole(count, width), col(count), col(2 * count), col(2 * count),
                  whole(heads, span)] + [whole(width, width)] * 3 + [whole(1, width)] * 3
                 + [whole(2, width)] + [pl.BlockSpec(memory_space=pltpu.HBM)] * 3,
        out_specs=[free] * 13 + [whole(8, width)],
        out_shape=outs + [shape((8, width), F32)],
        scratch_shapes=[pltpu.VMEM(o.shape, o.dtype) for o in outs[:4] + outs[5:]]
                       + [pltpu.VMEM(wo.shape, BF16), pltpu.VMEM(win.shape, BF16), pltpu.VMEM(wback.shape, BF16),
                          pltpu.VMEM((2, 2 * count, 4 * count), BF16), pltpu.VMEM((2, 2 * count, 4 * count), F32),
                          pltpu.VMEM((2, 128, span), F32), pltpu.VMEM((2, 4 * count, 128), BF16), pltpu.SemaphoreType.DMA((16,))],
        name="front", compiler_params=pltpu.CompilerParams(vmem_limit_bytes=36 << 20),
    )(info, far, far_other, near, q_l, k_l, v_l, lines, wq, wk, wv, gain1, gain2, gain3, cots, wo, win, wback)

def through_kernel(info, slopes_h, win_h, mixed_h, steep_h, wo_h, att_h, gain2, grad_mixed_o, grad_attended_o, grad_out_o, rows,
                   slopes, win, mixed, steep, wo, att, grad_mixed, grad_attended, grad_out, sems):
    hidden, width = slopes.shape[1], mixed.shape[1]
    chunks = []
    for i, at in enumerate(range(0, hidden, 512)):
        for a, b, s in ((slopes_h, slopes, i), (win_h, win, 4 + i)):
            chunks.append(pltpu.make_async_copy(a.at[:, at : at + 512], b.at[:, at : at + 512], sems.at[s]))
    copies = [pltpu.make_async_copy(a, b, sems.at[8 + i]) for i, (a, b) in enumerate((
        (mixed_h, mixed), (steep_h, steep), (wo_h, wo), (att_h, att)))]
    outs = [pltpu.make_async_copy(a, b, sems.at[12 + i]) for i, (a, b) in enumerate((
        (grad_mixed, grad_mixed_o), (grad_attended, grad_attended_o), (grad_out, grad_out_o)))]
    for copy in chunks + copies:
        copy.start()
    grad_inner = None
    for i, at in enumerate(range(0, hidden, 512)):
        chunks[2 * i].wait()
        chunks[2 * i + 1].wait()
        part = dot(slopes[:, at : at + 512], win[:, at : at + 512], NT)
        grad_inner = part if grad_inner is None else grad_inner + part
    copies[0].wait()
    copies[1].wait()
    values = mixed[...]
    more, grad_two = norm_back(grad_inner, values, rms_scale(values), gain2[...])
    total = steep[...] + more
    grad_mixed[...] = total
    outs[0].start()
    low = total.astype(BF16)
    copies[2].wait()
    grad_attended[...] = dot(low, wo[...], NT).astype(BF16)
    outs[1].start()
    copies[3].wait()
    grad_out[...] = dot(att[...], low, TN).astype(BF16)
    outs[2].start()
    rows[...] = jnp.concatenate([grad_two, jnp.zeros((7, width), F32)])
    for copy in outs:
        copy.wait()

def through(info, slopes, win, mixed, steep, wo, att, gain2):
    n, width = mixed.shape
    smem, vmem, free = (pl.BlockSpec(memory_space=m) for m in (pltpu.SMEM, pltpu.VMEM, pl.ANY))
    shape = jax.ShapeDtypeStruct
    given = (slopes, win, mixed, steep, wo, att)
    outs = [shape((n, width), F32), shape((n, width), BF16), shape((width, width), BF16)]
    return pl.pallas_call(
        through_kernel,
        in_specs=[smem, free, pl.BlockSpec(memory_space=pltpu.HBM)] + [free] * 4 + [vmem],
        out_specs=[free] * 3 + [vmem],
        out_shape=outs + [shape((8, width), F32)],
        scratch_shapes=[pltpu.VMEM(g.shape, g.dtype) for g in given] + [pltpu.VMEM(o.shape, o.dtype) for o in outs] + [pltpu.SemaphoreType.DMA((15,))],
        name="through", compiler_params=pltpu.CompilerParams(vmem_limit_bytes=16 << 20),
    )(info, *given, gain2)

def meet_kernel(info, got_h, active_h, slopes_h, turned_h, steep_h, *refs):
    outs, (got, chunk, turned, steep, blocks, sems) = refs[:4], refs[4:]
    order = (3, 1, 2, 0)
    high, lowest = (info[6] & 15) >> 2, info[6] & 3
    load = [pltpu.make_async_copy(got_h.at[4 * k : 4 * k + 4], got.at[k], sems.at[k]) for k in range(4)]
    save = [pltpu.make_async_copy(blocks.at[k], outs[k], sems.at[4 + k]) for k in range(4)]

    def columns(source, k):
        at = pl.ds(pl.multiple_of((k ^ high) * 512, 512), 512)
        return pltpu.make_async_copy(source.at[:, at], chunk.at[k], sems.at[8 + k])

    for side, source in ((0, active_h), (1, slopes_h)):
        @pl.when(info[7] == side)
        def _(side=side, source=source):
            extra = pltpu.make_async_copy(*((steep_h, steep) if side == 0 else (turned_h, turned)), sems.at[12])
            extra.start()
            for k in order:
                columns(source, k).start()
                load[k].start()
            extra.wait()
            low = steep[...].astype(BF16) if side == 0 else turned[...]
            for k in order:
                columns(source, k).wait()
                made = dot(chunk[k], low, TN) if side == 0 else dot(low, chunk[k])
                load[k].wait()
                for b in range(4):
                    piece = made[:, b * 128 : (b + 1) * 128]
                    if side == 0:
                        piece = made[b * 128 : (b + 1) * 128]
                        piece = jnp.concatenate([piece[:, q * 128 : (q + 1) * 128] for q in range(4)])
                    to = b ^ lowest
                    blocks[k, to] = (piece + got[k, to].astype(F32)).astype(BF16)
                save[k].start()

    for copy in save:
        copy.wait()

def meet(info, got, active, slopes, turned, steep):
    smem, free = pl.BlockSpec(memory_space=pltpu.SMEM), pl.BlockSpec(memory_space=pl.ANY)
    block = (4,) + got.shape[1:]
    n, width = steep.shape
    return pl.pallas_call(
        meet_kernel,
        in_specs=[smem] + [free] * 5,
        out_specs=[free] * 4,
        out_shape=[jax.ShapeDtypeStruct(block, BF16)] * 4,
        scratch_shapes=[pltpu.VMEM((4,) + block, BF16), pltpu.VMEM((4, n, 512), BF16), pltpu.VMEM(turned.shape, BF16), pltpu.VMEM(steep.shape, F32),
                        pltpu.VMEM((4,) + block, BF16), pltpu.SemaphoreType.DMA((13,))],
        name="meet", compiler_params=pltpu.CompilerParams(vmem_limit_bytes=20 << 20),
    )(info, got, active, slopes, turned, steep)

CLASS = {(0, 0): 0, (1, 2): 0, (0, 1): 1, (1, 3): 1, (0, 2): 2, (0, 3): 3, (1, 0): 4, (1, 1): 5}

def back_kernel(info, ql, qr, kl, kr, vl, vr, gout, out, inv, expo, buckets, dense_rows, through_rows,
                hid_l_h, hid_r_h, near_h, near_other_h, far_h, far_other_h, wq_h, wk_h, wv_h, grad_out_h,
                keep_o, send_o, stay_o, leave_o, small,
                hid_l, hid_r, near, near_other, far, far_other, wq, wk, wv, made,
                keep, send, stay, leave, dq, dk, dv, offsets, sums, acc, slopes, sems):
    count, width = near.shape
    step = pl.program_id(0)
    pairs = width // 128
    late = [pltpu.make_async_copy(a, b, sems.at[i]) for i, (a, b) in enumerate((
        (hid_l_h, hid_l), (hid_r_h, hid_r), (near_h, near), (near_other_h, near_other), (far_h, far), (far_other_h, far_other),
        (wq_h, wq), (wk_h, wk), (wv_h, wv), (grad_out_h, made.at[0:width])))]
    done = [pltpu.make_async_copy(a, b, sems.at[10 + i]) for i, (a, b) in enumerate(((send, send_o), (keep, keep_o), (leave, leave_o), (stay, stay_o)))]

    @pl.when(step == 0)
    def _():
        for copy in late:
            copy.start()

    cols = pl.ds(pl.multiple_of(step * 128, 128), 128)
    lane = lax.broadcasted_iota(jnp.int32, (1, 128), 1)
    starts = [info[1 + b] for b in range(4)]
    keys = jnp.concatenate([kl[...], kr[...]])
    values = jnp.concatenate([vl[...], vr[...]])
    query = jnp.concatenate([ql[...], qr[...]])
    scaled = gout[...].astype(F32) * inv[...]
    prod = scaled * out[...].astype(F32)
    low = scaled.astype(BF16)
    query_t, low_t = query.T, low.T
    grads_q, grads_k, grads_v = None, [], []
    for head in range(2):
        mine = (lane < 64) if head == 0 else (lane >= 64)
        base = 64 if head == 0 else 0
        pick = jnp.where(mine, 1.0, 0.0).astype(BF16)
        delta = jnp.sum(jnp.where(mine, prod, 0.0), axis=1, keepdims=True)
        high = delta.astype(BF16).astype(F32)
        extra = jnp.where(lane == base, high, jnp.where(lane == base + 1, delta - high, 0.0)).astype(BF16)
        grad = low * pick + extra
        minus = jnp.where((lane == base) | (lane == base + 1), -1.0, 0.0).astype(BF16)
        for b in range(4):
            spot = slice(b * count, (b + 1) * count)
            ds = dot(grad, values[spot] * pick + minus, NT) * expo[head, :, spot].astype(F32)
            slopes[head, :, spot] = ds.astype(BF16)
            for chunk in range(2):
                upper, lower = (ds[chunk * count + r * 128 : chunk * count + (r + 1) * 128] for r in range(2))
                group = CLASS[chunk, b]
                block = jnp.concatenate([lower[:, :128], lower[:, 128:] + upper[:, :128], upper[:, 128:]], axis=1)
                if (chunk, b) in ((1, 2), (1, 3)):
                    block = block + sums[head, group]
                sums[head, group] = block
        part = dot(slopes[head], keys * pick)
        grads_q = part if grads_q is None else grads_q + part
        half = slice(head * 64, (head + 1) * 64)
        grads_k.append(dot(query_t[half], slopes[head]))
        grads_v.append(dot(low_t[half], expo[head]))
    dq[:, cols] = grads_q.astype(BF16)
    dk[:, cols] = jnp.concatenate(grads_k).astype(BF16).T
    dv[:, cols] = jnp.concatenate(grads_v).astype(BF16).T
    for head in range(2):
        acc[head] = jnp.zeros(acc.shape[1:], F32)
        for (chunk, b), group in CLASS.items():
            if (chunk, b) not in ((1, 2), (1, 3)):
                at = starts[b] - starts[2 * chunk] + 768
                to = pl.ds(pl.multiple_of(at, 128), 384)
                acc[head, :, to] += sums[head, group]
        rest = acc[head]
        n = 64
        while n >= 8:
            rest = rest[:n] + pltpu.roll(rest[n:], 2048 - n, 1)
            n //= 2
        line = rest[7:8]
        for r in range(6, -1, -1):
            line = rest[r : r + 1] + pltpu.roll(line, 2047, 1)
        offsets[pl.ds(2 * step + head, 1), :] = pltpu.roll(line, 127, 1)

    @pl.when(step == pairs - 1)
    def _():
        for copy in late:
            copy.wait()
        made[width : 2 * width, :] = (dot(hid_l[:count, :], dq[:count, :], TN) + dot(hid_r[:count, :], dq[count:, :], TN)).astype(BF16)
        for at, grads in ((2 * width, dk), (3 * width, dv)):
            made[at : at + width, :] = (dot(hid_l[...], grads[: 2 * count, :], TN) + dot(hid_r[...], grads[2 * count :, :], TN)).astype(BF16)
        me = info[6]
        size = made.shape[0] // 32

        @pl.loop(0, 16)
        def _(r):
            keep[r] = made[pl.ds(pl.multiple_of((r ^ me) * size, size), size), :]
            send[pl.ds(pl.multiple_of(r * size, size), size), :] = made[pl.ds(pl.multiple_of(((r + 16) ^ me) * size, size), size), :]

        gain = jnp.zeros((1, width), F32)
        for b, raw in enumerate((near, near_other, far, far_other)):
            spot = slice(b * count, (b + 1) * count)
            grad = dot(dk[spot, :], wk[...], NT) + dot(dv[spot, :], wv[...], NT)
            half = slice((b // 2) * count, (b // 2 + 1) * count)
            if b % 2 == 0:
                grad = grad + dot(dq[half, :], wq[...], NT)
                stay[half, :] = grad
            else:
                leave[half, :] = grad.astype(BF16)
            tokens = raw[...].astype(F32)
            gain = gain + jnp.sum(grad * (tokens * rms_scale(tokens)), axis=0, keepdims=True)
        leave[2 * count :, :] = two_terms(rows_of(dense_rows[0:1, :]))
        picker = jnp.where(lax.broadcasted_iota(jnp.int32, (128, 1), 0) == buckets[...], 1.0, 0.0).astype(BF16)
        left = offsets[...][:, : buckets.shape[1]]
        bias = None
        for _ in range(3):
            part = left.astype(BF16)
            left = left - part.astype(F32)
            bias = dot(part, picker, NT) if bias is None else bias + dot(part, picker, NT)
        bias = jnp.concatenate([bias, jnp.zeros((bias.shape[0], width - 128), F32)], axis=1)
        line = bias[0:1]
        for h in range(1, bias.shape[0]):
            line = line + pltpu.roll(bias[h : h + 1], 32 * h, 1)
        total = rows_of(gain, through_rows[0:1, :], dense_rows[1:2, :], line)
        small[...] = total
        send[16 * size :, :] = two_terms(total)
        for copy in done:
            copy.start()
        for copy in done:
            copy.wait()

def back(info, ql, qr, kl, kr, vl, vr, gout, out, inv, expo, buckets, dense_rows, through_rows,
         hid_l, hid_r, near, near_other, far, far_other, wq, wk, wv, grad_out):
    count, width = near.shape
    smem, free = pl.BlockSpec(memory_space=pltpu.SMEM), pl.BlockSpec(memory_space=pl.ANY)
    whole = lambda *dims: pl.BlockSpec(dims, lambda g: (0,) * len(dims))
    col = lambda n: pl.BlockSpec((n, 128), lambda g: (0, g))
    shape = jax.ShapeDtypeStruct
    size = 4 * width // 32
    outs = [shape((16, size, width), BF16), shape((16 * size + 16, width), BF16), shape((2 * count, width), F32), shape((2 * count + 16, width), BF16)]
    given = (hid_l, hid_r, near, near_other, far, far_other, wq, wk, wv)
    return pl.pallas_call(
        back_kernel,
        grid=(width // 128,),
        in_specs=[smem, col(count), col(count)] + [col(2 * count)] * 7 + [pl.BlockSpec((2, 2 * count, 4 * count), lambda g: (g, 0, 0)),
                  whole(*buckets.shape), whole(8, width), whole(8, width)] + [free] * 10,
        out_specs=[free] * 4 + [whole(8, width)],
        out_shape=outs + [shape((8, width), F32)],
        scratch_shapes=[pltpu.VMEM(g.shape, BF16) for g in given] + [pltpu.VMEM((4 * width, width), BF16)]
                       + [pltpu.VMEM(o.shape, o.dtype) for o in outs]
                       + [pltpu.VMEM((2 * count, width), BF16), pltpu.VMEM((4 * count, width), BF16), pltpu.VMEM((4 * count, width), BF16),
                          pltpu.VMEM((8, 2048), F32), pltpu.VMEM((2, 6, 128, 384), F32), pltpu.VMEM((2, 128, 2048), F32),
                          pltpu.VMEM((2, 2 * count, 4 * count), BF16), pltpu.SemaphoreType.DMA((14,))],
        name="back", compiler_params=pltpu.CompilerParams(vmem_limit_bytes=44 << 20),
    )(info, ql, qr, kl, kr, vl, vr, gout, out, inv, expo, buckets, dense_rows, through_rows, *given, grad_out)

def ending_kernel(info, stay, came, near, far, grad_mixed, gain, dense_rows, home, away):
    count, width = near.shape
    for part, raw in enumerate((near, far)):
        spot = slice(part * count, (part + 1) * count)
        tokens = raw[...].astype(F32)
        grad = stay[spot, :] + came[spot, :].astype(F32)
        more, _ = norm_back(grad, tokens, rms_scale(tokens), gain[...])
        value = (grad_mixed[spot, :] + more).astype(BF16)
        if part == 0:
            home[:count, :] = value
        else:
            away[:count, :] = value
    alive = (info[0] - info[5]).astype(F32)
    pool = two_terms((rows_of(dense_rows[0:1, :]) + one_value(came[2 * count :, :])) / alive)
    home[count:, :] = pool
    away[count:, :] = pool

def ending(info, stay, came, near, far, grad_mixed, gain, dense_rows):
    count, width = near.shape
    smem, vmem = pl.BlockSpec(memory_space=pltpu.SMEM), pl.BlockSpec(memory_space=pltpu.VMEM)
    shape = jax.ShapeDtypeStruct((count + 16, width), BF16)
    return pl.pallas_call(
        ending_kernel, in_specs=[smem] + [vmem] * 7, out_specs=[vmem] * 2, out_shape=[shape, shape], name="ending", compiler_params=pltpu.CompilerParams(vmem_limit_bytes=10 << 20)
    )(info, stay, came, near, far, grad_mixed, gain, dense_rows)

def place_kernel(firsts, info, *refs):
    parts, (back, front, rows, columns, sems) = refs[: len(firsts)], refs[-5:]
    mine = info[6] & 15
    for side in range(2):
        @pl.when(info[7] == side)
        def _(side=side):
            copies, n = [], 0
            for part, first in zip(parts, firsts):
                for i in range(part.shape[0]):
                    r = first + i
                    to = pl.ds(pl.multiple_of(((r & 15) ^ mine) * 128, 128), 128)
                    if (r >= 16) == (side == 1):
                        for q in range(4):
                            rows[n, :, q * 128 : (q + 1) * 128] = part[i, q * 128 : (q + 1) * 128, :].astype(F32)
                        copies.append(pltpu.make_async_copy(rows.at[n], back.at[to, :], sems.at[n]))
                    else:
                        columns[n] = part[i].astype(F32)
                        copies.append(pltpu.make_async_copy(columns.at[n], front.at[:, to], sems.at[n]))
                    copies[-1].start()
                    n += 1
            for copy in copies:
                copy.wait()

def place(info, parts, made, width):
    smem, vmem, far = (pl.BlockSpec(memory_space=m) for m in (pltpu.SMEM, pltpu.VMEM, pltpu.HBM))
    shape = jax.ShapeDtypeStruct
    count = sum(p.shape[0] for _, p in parts)
    return pl.pallas_call(
        functools.partial(place_kernel, [first for first, _ in parts]),
        in_specs=[smem] + [vmem] * len(parts) + [far] * len(made),
        out_specs=[far] * 2,
        out_shape=[shape((16 * 128, width), F32), shape((width, 16 * 128), F32)],
        scratch_shapes=[pltpu.VMEM((count, 128, width), F32), pltpu.VMEM((count, width, 128), F32), pltpu.SemaphoreType.DMA((count,))],
        input_output_aliases={1 + len(parts) + i: i for i in range(len(made))},
        name="place", compiler_params=pltpu.CompilerParams(vmem_limit_bytes=24 << 20),
    )(info, *[p for _, p in parts], *made)

def sort_kernel(firsts, info, *refs):
    parts, made, (tall, sems) = refs[: len(firsts)], refs[-6:-2], refs[-2:]
    size = parts[0].shape[1]
    mine = info[6]
    pieces = []
    for part, first in zip(parts, firsts):
        for i in range(part.shape[0]):
            tall[len(pieces)] = part[i].astype(F32)
            pieces.append(first + i)
    for top in range(4):
        @pl.when((mine >> 3) == top)
        def _(top=top):
            copies = []
            for n, r in enumerate(pieces):
                to = pl.ds(pl.multiple_of(((r ^ mine) & 7) * size, size), size)
                copies.append(pltpu.make_async_copy(tall.at[n], made[top ^ (r >> 3)].at[to, :], sems.at[n]))
                copies[-1].start()
            for copy in copies:
                copy.wait()

def sort(info, parts, made, width):
    smem, vmem, far = (pl.BlockSpec(memory_space=m) for m in (pltpu.SMEM, pltpu.VMEM, pltpu.HBM))
    shape = jax.ShapeDtypeStruct((width, width), F32)
    count = sum(p.shape[0] for _, p in parts)
    return pl.pallas_call(
        functools.partial(sort_kernel, [first for first, _ in parts]),
        in_specs=[smem] + [vmem] * len(parts) + [far] * len(made),
        out_specs=[far] * 4,
        out_shape=[shape] * 4,
        scratch_shapes=[pltpu.VMEM((count,) + parts[0][1].shape[1:], F32), pltpu.SemaphoreType.DMA((count,))],
        input_output_aliases={1 + len(parts) + i: i for i in range(len(made))},
        name="sort", compiler_params=pltpu.CompilerParams(vmem_limit_bytes=12 << 20),
    )(info, *[p for _, p in parts], *made)

def mix_kernel(*refs):
    for k in range(4):
        refs[4 + k][...] = added(*[term[k] for term in refs[:4]])

def mix(terms):
    block = terms[0].shape[1:]
    vmem = pl.BlockSpec(memory_space=pltpu.VMEM)
    return pl.pallas_call(
        mix_kernel, in_specs=[vmem] * 4, out_specs=[vmem] * 4, out_shape=[jax.ShapeDtypeStruct(block, BF16)] * 4, name="mix", compiler_params=pltpu.CompilerParams(vmem_limit_bytes=10 << 20),
    )(*terms)

def exchange(value, bits):
    size = lax.axis_size("dp") * lax.axis_size("blk")
    return lax.ppermute(value, ("dp", "blk"), [(i, i ^ bits) for i in range(size)])

def wait(*values):
    return lax.optimization_barrier(values)

def added(*terms):
    total = terms[0].astype(F32)
    for term in terms[1:]:
        total = total + term.astype(F32)
    return total.astype(BF16)

def local(inputs, w_query, w_key, w_value, w_out, w_in, w_back, norm1_gain, norm2_gain, final_gain, bias_table, bucket_table, prefix_len, pad_len, pooled_grad):
    rows, width = inputs.shape[1:]
    spot, far_off = lax.axis_index("blk"), lax.axis_index("dp")
    doc, core = spot // 2, spot % 2
    block = [doc * 2 + core, doc * 2 + 1 - core, (1 - doc) * 2 + core, (1 - doc) * 2 + 1 - core]
    line = [8, 16]
    further = [32 << b for b in range((lax.axis_size("dp") // 8).bit_length() - 1)]
    piece = core * 16 + doc * 4 + (far_off % 2) * 8 + (far_off // 2) % 4
    near = jnp.where(doc == 0, inputs[0], inputs[1])
    far_send = jnp.where(doc == 0, inputs[1], inputs[0])
    near, far_send = wait(near, far_send)
    far = exchange(far_send, ROW)
    near_other = exchange(near, CORE)
    slot = jnp.arange(8, dtype=jnp.int32)
    ids = jnp.zeros_like(slot)
    for i, value in enumerate([b * rows for b in block] + [piece, core, doc]):
        ids = jnp.where(slot == i, value, ids)
    gain1, gain2, gain3 = norm1_gain[None, :], norm2_gain[None, :], final_gain[None, :]
    buckets = bucket_table[None, :]
    hid_l, q_l, k_l, v_l, lines, info = prepare(ids, pad_len, prefix_len, near, near_other, w_query, w_key, w_value, gain1, bias_table.T, buckets)
    far, info = wait(far, info)
    far_other = exchange(far, CORE)
    (hid_r, q_r, k_r, v_r, expo, inverse, attended, send, active, slopes, turned, mixed, steep, dense_rows) = front(
        info, far, far_other, near, q_l, k_l, v_l, lines, w_query, w_key, w_value, gain1, gain2, gain3, pooled_grad, w_out, w_in, w_back)

    xy = [ROW, NEAR_X, ROW ^ NEAR_X]
    zz = [line[0], line[1], line[0] ^ line[1]]

    token, send = wait(info, send)
    got = exchange(send, CORE)
    grad_mixed, grad_attended, grad_out_w, through_rows = through(token, slopes, w_in, mixed, steep, w_out, attended, gain2)
    token, through_rows, got = wait(token, through_rows, got)
    stays, *sends = meet(token, got, active, slopes, turned, steep)

    token, sends = wait(token, sends)
    came = [exchange(s, m) for s, m in zip(sends, xy)]
    rest_keep, rest_send, stay, leave, small = back(
        token, q_l, q_r, k_l, k_r, v_l, v_r, grad_attended, attended, inverse, expo, buckets, dense_rows, through_rows,
        hid_l, hid_r, near, near_other, far, far_other, w_query, w_key, w_value, grad_out_w)
    token, small, rest_send, leave, came = wait(token, small, rest_send, leave, came)

    rest_got = exchange(rest_send, CORE)
    hidden_got = exchange(leave, CORE)
    lines = mix([stays] + list(came))
    token, lines = wait(token, lines)
    took = [exchange(lines[k + 1], m) for k, m in enumerate(zz)]
    token, rest_got, hidden_got = wait(token, rest_got, hidden_got)

    count = rest_keep.shape[0] * rest_keep.shape[1]
    small = small + one_value(rest_got[count:])
    rest_got = rest_got[:count].reshape(rest_keep.shape)
    terms = two_terms(small)
    sends = [jnp.concatenate([added(rest_keep[4 * k : 4 * k + 4], rest_got[4 * k : 4 * k + 4]).reshape(-1, width), terms]) for k in (1, 2, 3)]
    token, sends = wait(token, sends)
    rest_came = [exchange(s, m) for s, m in zip(sends, xy)]
    home, away = ending(token, stay, hidden_got, near, far, grad_mixed, gain1, dense_rows)
    token, took, away = wait(token, took, away)

    whole = added(lines[0], *took)
    for bit in further:
        whole = added(whole, exchange(whole, bit))
    token, whole = wait(token, whole)
    back_line = [exchange(whole, m) for m in zz]
    away_got = exchange(away, ROW)
    token, rest_came = wait(token, rest_came)

    count = count // 4
    for part in rest_came:
        small = small + one_value(part[count:])
    rest_came = [part[:count].reshape((4,) + rest_keep.shape[1:]) for part in rest_came]
    piece = count // 4
    lines = added(rest_keep[:4], rest_got[:4], *rest_came).reshape(-1, width)
    send = jnp.concatenate([lines[piece : 2 * piece], lines[3 * piece :], two_terms(small)])
    token, send = wait(token, send)
    took = exchange(send, line[0])
    token, took = wait(token, took)
    small = small + one_value(took[2 * piece :])
    send = jnp.concatenate([added(lines[2 * piece : 3 * piece], took[piece : 2 * piece]), two_terms(small)])
    lines = added(lines[:piece], took[:piece])
    token, send, back_line, away_got = wait(token, send, back_line, away_got)
    took = exchange(send, line[1])

    quarter = jnp.stack([whole] + back_line)
    token, quarter = wait(token, quarter)
    from_y, from_x = exchange(quarter, ROW), exchange(quarter, NEAR_X)
    pool_mine, pool_other = one_value(home[rows:])[:1], one_value(away_got[rows:])[:1]
    pooled = jnp.where(doc == 0, jnp.concatenate([pool_mine, pool_other]), jnp.concatenate([pool_other, pool_mine]))
    home, away_got = home[:rows], away_got[:rows]
    input_grad = jnp.where(doc == 0, jnp.stack([home, away_got]), jnp.stack([away_got, home]))
    token, took, pooled, input_grad = wait(token, took, pooled, input_grad)

    small = small + one_value(took[piece:])
    rest = added(lines, took[:piece])
    for bit in further:
        rest = added(rest, exchange(rest, bit))
        small = small + exchange(small, bit)
    token, rest = wait(token, rest)
    rest_back = [exchange(rest, m) for m in zz]
    outs = [small[0], small[1], small[2], small[3, : bias_table.size].reshape(bias_table.shape[::-1]).T]
    token, from_y, from_x, outs = wait(token, from_y, from_x, outs)

    sends = [from_x[:2], from_y[2:]]
    token, sends, rest_back = wait(token, sends, rest_back)
    far_a, far_b = exchange(sends[0], ROW), exchange(sends[1], NEAR_X)
    fourth = jnp.stack([rest] + rest_back)
    token, fourth, quarter = wait(token, fourth, quarter)
    fourth_y, fourth_x = exchange(fourth, ROW), exchange(fourth, NEAR_X)
    other = exchange(quarter, CORE)
    near_pair = jnp.concatenate([from_y, from_x])
    grads = place(token, [(0, quarter), (4, from_y), (8, from_x)], [], width)
    token, grads, other, near_pair, far_a, far_b, fourth_y, fourth_x = wait(token, grads, other, near_pair, far_a, far_b, fourth_y, fourth_x)

    sends = [fourth_x[:2], fourth_y[2:], near_pair, jnp.concatenate([far_a, far_b]), jnp.concatenate([fourth, fourth_y, fourth_x])]
    token, sends = wait(token, sends)
    last_a, last_b, other_near, other_far, pair = (exchange(s, m) for s, m in zip(sends, (ROW, NEAR_X, CORE, CORE, CORE)))
    grads = place(token, [(12, far_a), (14, far_b), (16, other)], grads, width)
    token, grads, other_near, other_far = wait(token, grads, other_near, other_far)
    out_back, out_in = place(token, [(20, other_near), (28, other_far)], grads, width)
    token, out_back, out_in, last_a, last_b, pair = wait(token, out_back, out_in, last_a, last_b, pair)

    ends = exchange(jnp.concatenate([last_a, last_b]), CORE)
    made = sort(token, [(0, fourth), (4, fourth_y), (8, fourth_x), (12, last_a), (14, last_b), (16, pair)], [], width)
    token, made, ends = wait(token, made, ends)
    out_out, out_query, out_key, out_value = sort(token, [(28, ends)], made, width)
    return (pooled, input_grad, out_query, out_key, out_value, out_out, out_in, out_back, *outs)

def solution(mesh):
    data = P("dp", "blk", None)
    placed = (data,) + (P(),) * 11 + (P("dp"), P("dp"), P("dp", None))
    return jax.shard_map(local, mesh=mesh, in_specs=placed, out_specs=(P("dp", None), data) + (P(),) * 10, check_vma=False)
```

```python
import functools
import jax, jax.numpy as jnp
from jax import lax
from jax.experimental import pallas as pl
from jax.experimental.pallas import tpu as pltpu
from jax.sharding import PartitionSpec as P

F32, BF16 = jnp.float32, jnp.bfloat16
NEG = -1000000000.0
NT = (((1,), (1,)), ((), ()))
TN = (((0,), (0,)), ((), ()))
NN = (((1,), (0,)), ((), ()))

def dot(a, b, dims=NN):
    return lax.dot_general(a, b, dims, preferred_element_type=F32)

def skew(row, width, dtype=F32):
    return pltpu.roll(jnp.broadcast_to(row, (128, width)), width - 127, 1, stride=1, stride_axis=0)


BUCKETS = 32
EPS = 1e-06
CORE, ROW, NEAR_X = 1, 2, 4

def rms_scale(values):
    return lax.rsqrt(jnp.mean(values * values, axis=-1, keepdims=True) + EPS)

def norm_back(grad_out, values, scale, gain):
    weighted = grad_out * gain
    inner = jnp.mean(weighted * values, axis=-1, keepdims=True)
    grad_in = scale * weighted - scale * scale * scale * values * inner
    return grad_in, jnp.sum(grad_out * values * scale, axis=0, keepdims=True)

def two_terms(value):
    high = value.astype(BF16)
    return jnp.concatenate([high, (value - high.astype(F32)).astype(BF16)])

def one_value(terms):
    return terms[:8].astype(F32) + terms[8:16].astype(F32)

def rows_of(*values):
    count = sum(v.shape[0] for v in values)
    return jnp.concatenate(list(values) + [jnp.zeros((8 - count, values[0].shape[1]), F32)])

def prepare_kernel(mine, other, gain, wq_h, wk_h, wv_h, wo_h, hidden, query, keys, values, wq, wk, wv, wo, sems):
    rows = mine.shape[0]
    load = [pltpu.make_async_copy(a, b, sems.at[i]) for i, (a, b) in enumerate(((wk_h, wk), (wv_h, wv), (wq_h, wq), (wo_h, wo)))]
    for copy in load:
        copy.start()
    for part, raw in enumerate((mine, other)):
        tokens = raw[...].astype(F32)
        hidden[part * rows : (part + 1) * rows, :] = (tokens * rms_scale(tokens) * gain[...]).astype(BF16)
    h = hidden[...]
    load[0].wait()
    keys[...] = dot(h, wk[...]).astype(BF16)
    load[1].wait()
    values[...] = dot(h, wv[...]).astype(BF16)
    load[2].wait()
    query[...] = dot(h[:rows], wq[...]).astype(BF16)
    load[3].wait()

def prepare(mine, other, gain, wq, wk, wv, wo):
    rows, width = mine.shape
    shape = lambda n: jax.ShapeDtypeStruct((n, width), BF16)
    vmem, free = (pl.BlockSpec(memory_space=m) for m in (pltpu.VMEM, pl.ANY))
    return pl.pallas_call(
        prepare_kernel,
        in_specs=[vmem] * 3 + [free] * 4,
        out_specs=[vmem] * 8,
        out_shape=[shape(2 * rows), shape(rows), shape(2 * rows), shape(2 * rows)] + [shape(width)] * 4,
        scratch_shapes=[pltpu.SemaphoreType.DMA((4,))],
        name="prepare", compiler_params=pltpu.CompilerParams(vmem_limit_bytes=14 << 20),
    )(mine, other, gain, wq, wk, wv, wo)

def back_pieces(to, active, low, mine):
    @pl.loop(0, active.shape[1] // 512)
    def _(group):
        made = dot(active[:, pl.ds(pl.multiple_of(group * 512, 512), 512)], low, TN).astype(BF16)
        for b in range(4):
            rows = made[b * 128 : (b + 1) * 128]
            to[(4 * group + b) ^ mine] = jnp.concatenate([rows[:, q * 128 : (q + 1) * 128] for q in range(4)])

def in_pieces(to, slopes, turned, mine):
    @pl.loop(0, slopes.shape[1] // 512)
    def _(group):
        made = dot(turned, slopes[:, pl.ds(pl.multiple_of(group * 512, 512), 512)]).astype(BF16)
        for b in range(4):
            to[(4 * group + b) ^ mine] = made[:, b * 128 : (b + 1) * 128]

def front_kernel(ids, pads, prefixes, far, far_other, near, q_l, k_l, v_l, bias, buckets, wq, wk, wv, gain1, gain2, gain3, cots, wo_h, win_h, wback_h,
                 hid_o, q_o, k_o, v_o, expo_o, inv_o, att_o, send_o, active_o, slopes_o, turned_o, mixed_o, steep_o, rows, info,
                 hid, qs, ks, vs, inv, att, send, active, slopes, turned, mixed, steep, wo, win, wback, expo, scores, skewed, edges, lines, sems):
    count, width = near.shape
    hidden = win.shape[1]
    step = pl.program_id(0)
    late = [pltpu.make_async_copy(a, b, sems.at[i]) for i, (a, b) in enumerate(((wo_h, wo), (win_h, win), (wback_h, wback)))]
    early = [pltpu.make_async_copy(a, b, sems.at[3 + i]) for i, (a, b) in enumerate(((hid, hid_o), (qs, q_o), (ks, k_o), (vs, v_o)))]
    dense = [pltpu.make_async_copy(a, b, sems.at[7 + i]) for i, (a, b) in enumerate((
        (inv, inv_o), (att, att_o), (mixed, mixed_o), (turned, turned_o), (active, active_o), (steep, steep_o), (slopes, slopes_o), (send, send_o)))]
    kept = lambda g: pltpu.make_async_copy(expo, expo_o.at[pl.ds(2 * g, 2)], sems.at[15])

    @pl.when(step == 0)
    def _():
        for copy in late:
            copy.start()
        doc = ids[6]
        info[0] = 4 * count - jnp.where(doc == 0, pads[0], pads[1])
        info[5] = jnp.where(doc == 0, prefixes[0], prefixes[1])
        for to, at in enumerate((0, 1, 2, 3)):
            info[1 + to] = ids[at]
        for to, at in enumerate((4, 5, 6)):
            info[6 + to] = ids[at]
        picker = jnp.where(lax.broadcasted_iota(jnp.int32, (BUCKETS, 1), 0) == buckets[...], 1.0, 0.0).astype(BF16)
        left, total = bias[...], None
        for _ in range(3):
            part = left.astype(BF16)
            left = left - part.astype(F32)
            made = dot(part, picker)
            total = made if total is None else total + made
        lines[...] = jnp.zeros_like(lines)
        lines[:, : buckets.shape[1]] = total
        for part, raw in enumerate((far, far_other)):
            tokens = raw[...].astype(F32)
            hid[part * count : (part + 1) * count, :] = (tokens * rms_scale(tokens) * gain1[...]).astype(BF16)
        h = hid[...]
        qs[...] = dot(h[:count], wq[...]).astype(BF16)
        ks[...] = dot(h, wk[...]).astype(BF16)
        vs[...] = dot(h, wv[...]).astype(BF16)
        for copy in early:
            copy.start()
        column = lax.broadcasted_iota(jnp.int32, (1, 128), 1)
        for b in range(4):
            place = info[1 + b] + lax.broadcasted_iota(jnp.int32, (count, 1), 0)
            gate = jnp.where(place < info[0], 0.0, NEG)
            for head in range(2):
                edges[head, b * count : (b + 1) * count, :] = jnp.where(column == (64 if head == 0 else 0), gate, 0.0).astype(BF16)

    @pl.when(step > 0)
    def _():
        kept(step - 1).wait()

    cols = pl.ds(pl.multiple_of(step * 128, 128), 128)
    lane = lax.broadcasted_iota(jnp.int32, (1, 128), 1)
    first = lane < 64
    limit = info[0]
    starts = [info[1 + b] for b in range(4)]
    keys = [k_l[:count, :], k_l[count:, :], ks[:count, cols], ks[count:, cols]]
    values = jnp.concatenate([v_l[...], vs[:, cols]])
    query = jnp.concatenate([q_l[...], qs[:, cols]])
    made = []
    for head in range(2):
        mine = jnp.where(first if head == 0 else lane >= 64, 1.0, 0.0).astype(BF16)
        one = jnp.where(lane == (64 if head == 0 else 0), 1.0, 0.0).astype(BF16)
        q = query * mine + one
        v = values * mine + one
        skewed[head] = skew(lines[pl.ds(2 * step + head, 1), :], lines.shape[1])
        for b in range(4):
            s = dot(q, keys[b] * mine + edges[head, b * count : (b + 1) * count, :], NT)
            for r in range(4):
                at = starts[b] - starts[2 * (r // 2)] + 896 - 128 * (r % 2)
                part = s[r * 128 : (r + 1) * 128] + skewed[head, :, pl.ds(pl.multiple_of(at, 128), 256)]
                scores[head, r * 128 : (r + 1) * 128, b * 256 : (b + 1) * 256] = part
        for r in range(4):
            rs = slice(r * 128, (r + 1) * 128)
            value = scores[head, rs, :]
            top = jnp.max(value, axis=1, keepdims=True)
            expo[head, rs, :] = jnp.exp(value - top).astype(BF16)
        acc = dot(expo[head], v)
        made.append((acc, 1.0 / (acc[:, 64:65] if head == 0 else acc[:, 0:1])))
    (a0, i0), (a1, i1) = made
    scale = jnp.where(first, i0, i1)
    att[:, cols] = (jnp.where(first, a0, a1) * scale).astype(BF16)
    inv[:, cols] = scale
    kept(step).start()

    @pl.when(step == 3)
    def _():
        for copy in late:
            copy.wait()
        dense[0].start()
        dense[1].start()
        for part, raw in enumerate((near, far)):
            spot = slice(part * count, (part + 1) * count)
            mixed[spot, :] = raw[...].astype(F32) + dot(att[spot, :], wo[...])
        dense[2].start()
        values = mixed[...]
        inner = (values * rms_scale(values) * gain2[...]).astype(BF16)
        turned[...] = inner.T
        dense[3].start()
        total = values
        for at in range(0, hidden, 512):
            lifted = jnp.maximum(dot(inner, win[:, at : at + 512]), 0.0).astype(BF16)
            active[:, at : at + 512] = lifted
            total = total + dot(lifted, wback[at : at + 512, :])
        dense[4].start()
        scale = rms_scale(total)
        place = lax.broadcasted_iota(jnp.int32, (2 * count, 1), 0)
        place = jnp.where(place < count, place + info[1], place + (info[3] - count))
        live = jnp.where((place >= info[5]) & (place < limit), 1.0, 0.0)
        pool = jnp.sum(total * scale * gain3[...] * live, axis=0, keepdims=True)
        cot = jnp.where(info[8] == 0, cots[0:1, :], cots[1:2, :]) / (limit - info[5]).astype(F32)
        slope, grad_end = norm_back(live * cot, total, scale, gain3[...])
        steep[...] = slope
        dense[5].start()
        rows[...] = jnp.concatenate([pool, grad_end, jnp.zeros((6, width), F32)])
        low = slope.astype(BF16)
        for at in range(0, hidden, 512):
            through = dot(low, wback[at : at + 512, :], NT).astype(BF16)
            slopes[:, at : at + 512] = jnp.where(active[:, at : at + 512] > 0, through, jnp.zeros_like(through))
        dense[6].start()
        mine = info[6] & 15

        @pl.when(info[7] == 0)
        def _():
            in_pieces(send, slopes, turned[...], mine)

        @pl.when(info[7] == 1)
        def _():
            back_pieces(send, active, steep[...].astype(BF16), mine)

        dense[7].start()
        for copy in early + dense:
            copy.wait()
        kept(step).wait()

def front(ids, pads, prefixes, far, far_other, near, q_l, k_l, v_l, bias, buckets, wq, wk, wv, gain1, gain2, gain3, cots, wo, win, wback):
    count, width = near.shape
    hidden = win.shape[1]
    heads, span = bias.shape[0], buckets.shape[1] + 1
    shape = jax.ShapeDtypeStruct
    smem, free = pl.BlockSpec(memory_space=pltpu.SMEM), pl.BlockSpec(memory_space=pl.ANY)
    whole = lambda *dims: pl.BlockSpec(dims, lambda g: (0,) * len(dims))
    col = lambda n: pl.BlockSpec((n, 128), lambda g: (0, g))
    outs = [shape((2 * count, width), BF16), shape((count, width), BF16), shape((2 * count, width), BF16), shape((2 * count, width), BF16),
            shape((heads, 2 * count, 4 * count), BF16), shape((2 * count, width), F32), shape((2 * count, width), BF16),
            shape((16, width, 128), BF16), shape((2 * count, hidden), BF16), shape((2 * count, hidden), BF16),
            shape((width, 2 * count), BF16), shape((2 * count, width), F32), shape((2 * count, width), F32)]
    return pl.pallas_call(
        front_kernel,
        grid=(heads // 2,),
        in_specs=[smem] * 3 + [whole(count, width)] * 3 + [col(count), col(2 * count), col(2 * count),
                  whole(*bias.shape), whole(*buckets.shape)] + [whole(width, width)] * 3 + [whole(1, width)] * 3
                 + [whole(2, width)] + [pl.BlockSpec(memory_space=pltpu.HBM)] * 3,
        out_specs=[free] * 13 + [whole(8, width), smem],
        out_shape=outs + [shape((8, width), F32), shape((16,), jnp.int32)],
        scratch_shapes=[pltpu.VMEM(o.shape, o.dtype) for o in outs[:4] + outs[5:]]
                       + [pltpu.VMEM(wo.shape, BF16), pltpu.VMEM(win.shape, BF16), pltpu.VMEM(wback.shape, BF16),
                          pltpu.VMEM((2, 2 * count, 4 * count), BF16), pltpu.VMEM((2, 2 * count, 4 * count), F32),
                          pltpu.VMEM((2, 128, span), F32), pltpu.VMEM((2, 4 * count, 128), BF16), pltpu.VMEM((heads, span), F32),
                          pltpu.SemaphoreType.DMA((16,))],
        name="front", compiler_params=pltpu.CompilerParams(vmem_limit_bytes=34 << 20),
    )(ids, pads, prefixes, far, far_other, near, q_l, k_l, v_l, bias, buckets, wq, wk, wv, gain1, gain2, gain3, cots, wo, win, wback)

def through_kernel(info, slopes_h, win_h, mixed_h, steep_h, wo_h, att_h, gain2, grad_mixed_o, grad_attended_o, grad_out_o, rows,
                   slopes, win, mixed, steep, wo, att, grad_mixed, grad_attended, grad_out, sems):
    hidden, width = slopes.shape[1], mixed.shape[1]
    chunks = []
    for i, at in enumerate(range(0, hidden, 512)):
        for a, b, s in ((slopes_h, slopes, i), (win_h, win, 4 + i)):
            chunks.append(pltpu.make_async_copy(a.at[:, at : at + 512], b.at[:, at : at + 512], sems.at[s]))
    copies = [pltpu.make_async_copy(a, b, sems.at[8 + i]) for i, (a, b) in enumerate((
        (mixed_h, mixed), (steep_h, steep), (wo_h, wo), (att_h, att)))]
    outs = [pltpu.make_async_copy(a, b, sems.at[12 + i]) for i, (a, b) in enumerate((
        (grad_mixed, grad_mixed_o), (grad_attended, grad_attended_o), (grad_out, grad_out_o)))]
    for copy in chunks + copies:
        copy.start()
    grad_inner = None
    for i, at in enumerate(range(0, hidden, 512)):
        chunks[2 * i].wait()
        chunks[2 * i + 1].wait()
        part = dot(slopes[:, at : at + 512], win[:, at : at + 512], NT)
        grad_inner = part if grad_inner is None else grad_inner + part
    copies[0].wait()
    copies[1].wait()
    values = mixed[...]
    more, grad_two = norm_back(grad_inner, values, rms_scale(values), gain2[...])
    total = steep[...] + more
    grad_mixed[...] = total
    outs[0].start()
    low = total.astype(BF16)
    copies[2].wait()
    grad_attended[...] = dot(low, wo[...], NT).astype(BF16)
    outs[1].start()
    copies[3].wait()
    grad_out[...] = dot(att[...], low, TN).astype(BF16)
    outs[2].start()
    rows[...] = jnp.concatenate([grad_two, jnp.zeros((7, width), F32)])
    for copy in outs:
        copy.wait()

def through(info, slopes, win, mixed, steep, wo, att, gain2):
    n, width = mixed.shape
    smem, vmem, free = (pl.BlockSpec(memory_space=m) for m in (pltpu.SMEM, pltpu.VMEM, pl.ANY))
    shape = jax.ShapeDtypeStruct
    given = (slopes, win, mixed, steep, wo, att)
    outs = [shape((n, width), F32), shape((n, width), BF16), shape((width, width), BF16)]
    return pl.pallas_call(
        through_kernel,
        in_specs=[smem, free, pl.BlockSpec(memory_space=pltpu.HBM)] + [free] * 4 + [vmem],
        out_specs=[free] * 3 + [vmem],
        out_shape=outs + [shape((8, width), F32)],
        scratch_shapes=[pltpu.VMEM(g.shape, g.dtype) for g in given] + [pltpu.VMEM(o.shape, o.dtype) for o in outs] + [pltpu.SemaphoreType.DMA((15,))],
        name="through", compiler_params=pltpu.CompilerParams(vmem_limit_bytes=16 << 20),
    )(info, *given, gain2)

def meet_kernel(info, got_h, active_h, slopes_h, turned_h, steep_h, *refs):
    outs, (got, chunk, turned, steep, blocks, sems) = refs[:4], refs[4:]
    order = (3, 1, 2, 0)
    high, lowest = (info[6] & 15) >> 2, info[6] & 3
    load = [pltpu.make_async_copy(got_h.at[4 * k : 4 * k + 4], got.at[k], sems.at[k]) for k in range(4)]
    save = [pltpu.make_async_copy(blocks.at[k], outs[k], sems.at[4 + k]) for k in range(4)]

    def columns(source, k):
        at = pl.ds(pl.multiple_of((k ^ high) * 512, 512), 512)
        return pltpu.make_async_copy(source.at[:, at], chunk.at[k], sems.at[8 + k])

    for side, source in ((0, active_h), (1, slopes_h)):
        @pl.when(info[7] == side)
        def _(side=side, source=source):
            extra = pltpu.make_async_copy(*((steep_h, steep) if side == 0 else (turned_h, turned)), sems.at[12])
            extra.start()
            for k in order:
                columns(source, k).start()
                load[k].start()
            extra.wait()
            low = steep[...].astype(BF16) if side == 0 else turned[...]
            for k in order:
                columns(source, k).wait()
                made = dot(chunk[k], low, TN) if side == 0 else dot(low, chunk[k])
                load[k].wait()
                for b in range(4):
                    piece = made[:, b * 128 : (b + 1) * 128]
                    if side == 0:
                        piece = made[b * 128 : (b + 1) * 128]
                        piece = jnp.concatenate([piece[:, q * 128 : (q + 1) * 128] for q in range(4)])
                    to = b ^ lowest
                    blocks[k, to] = (piece + got[k, to].astype(F32)).astype(BF16)
                save[k].start()

    for copy in save:
        copy.wait()

def meet(info, got, active, slopes, turned, steep):
    smem, free = pl.BlockSpec(memory_space=pltpu.SMEM), pl.BlockSpec(memory_space=pl.ANY)
    block = (4,) + got.shape[1:]
    n, width = steep.shape
    return pl.pallas_call(
        meet_kernel,
        in_specs=[smem] + [free] * 5,
        out_specs=[free] * 4,
        out_shape=[jax.ShapeDtypeStruct(block, BF16)] * 4,
        scratch_shapes=[pltpu.VMEM((4,) + block, BF16), pltpu.VMEM((4, n, 512), BF16), pltpu.VMEM(turned.shape, BF16), pltpu.VMEM(steep.shape, F32),
                        pltpu.VMEM((4,) + block, BF16), pltpu.SemaphoreType.DMA((13,))],
        name="meet", compiler_params=pltpu.CompilerParams(vmem_limit_bytes=20 << 20),
    )(info, got, active, slopes, turned, steep)

CLASS = {(0, 0): 0, (1, 2): 0, (0, 1): 1, (1, 3): 1, (0, 2): 2, (0, 3): 3, (1, 0): 4, (1, 1): 5}

def back_kernel(info, ql, qr, kl, kr, vl, vr, gout, out, inv, expo, buckets, dense_rows, through_rows,
                hid_l_h, hid_r_h, near_h, near_other_h, far_h, far_other_h, wq_h, wk_h, wv_h, grad_out_h,
                keep_o, send_o, stay_o, leave_o, small,
                hid_l, hid_r, near, near_other, far, far_other, wq, wk, wv, made,
                keep, send, stay, leave, dq, dk, dv, offsets, sums, acc, slopes, sems):
    count, width = near.shape
    step = pl.program_id(0)
    pairs = width // 128
    late = [pltpu.make_async_copy(a, b, sems.at[i]) for i, (a, b) in enumerate((
        (hid_l_h, hid_l), (hid_r_h, hid_r), (near_h, near), (near_other_h, near_other), (far_h, far), (far_other_h, far_other),
        (wq_h, wq), (wk_h, wk), (wv_h, wv), (grad_out_h, made.at[0:width])))]
    done = [pltpu.make_async_copy(a, b, sems.at[10 + i]) for i, (a, b) in enumerate(((send, send_o), (keep, keep_o), (leave, leave_o), (stay, stay_o)))]

    @pl.when(step == 0)
    def _():
        for copy in late:
            copy.start()

    cols = pl.ds(pl.multiple_of(step * 128, 128), 128)
    lane = lax.broadcasted_iota(jnp.int32, (1, 128), 1)
    starts = [info[1 + b] for b in range(4)]
    keys = jnp.concatenate([kl[...], kr[...]])
    values = jnp.concatenate([vl[...], vr[...]])
    query = jnp.concatenate([ql[...], qr[...]])
    scaled = gout[...].astype(F32) * inv[...]
    prod = scaled * out[...].astype(F32)
    low = scaled.astype(BF16)
    query_t, low_t = query.T, low.T
    grads_q, grads_k, grads_v = None, [], []
    for head in range(2):
        mine = (lane < 64) if head == 0 else (lane >= 64)
        base = 64 if head == 0 else 0
        pick = jnp.where(mine, 1.0, 0.0).astype(BF16)
        delta = jnp.sum(jnp.where(mine, prod, 0.0), axis=1, keepdims=True)
        high = delta.astype(BF16).astype(F32)
        extra = jnp.where(lane == base, high, jnp.where(lane == base + 1, delta - high, 0.0)).astype(BF16)
        grad = low * pick + extra
        minus = jnp.where((lane == base) | (lane == base + 1), -1.0, 0.0).astype(BF16)
        for b in range(4):
            spot = slice(b * count, (b + 1) * count)
            ds = dot(grad, values[spot] * pick + minus, NT) * expo[head, :, spot].astype(F32)
            slopes[head, :, spot] = ds.astype(BF16)
            for chunk in range(2):
                upper, lower = (ds[chunk * count + r * 128 : chunk * count + (r + 1) * 128] for r in range(2))
                group = CLASS[chunk, b]
                block = jnp.concatenate([lower[:, :128], lower[:, 128:] + upper[:, :128], upper[:, 128:]], axis=1)
                if (chunk, b) in ((1, 2), (1, 3)):
                    block = block + sums[head, group]
                sums[head, group] = block
        part = dot(slopes[head], keys * pick)
        grads_q = part if grads_q is None else grads_q + part
        half = slice(head * 64, (head + 1) * 64)
        grads_k.append(dot(query_t[half], slopes[head]))
        grads_v.append(dot(low_t[half], expo[head]))
    dq[:, cols] = grads_q.astype(BF16)
    dk[:, cols] = jnp.concatenate(grads_k).astype(BF16).T
    dv[:, cols] = jnp.concatenate(grads_v).astype(BF16).T
    for head in range(2):
        acc[head] = jnp.zeros(acc.shape[1:], F32)
        for (chunk, b), group in CLASS.items():
            if (chunk, b) not in ((1, 2), (1, 3)):
                at = starts[b] - starts[2 * chunk] + 768
                to = pl.ds(pl.multiple_of(at, 128), 384)
                acc[head, :, to] += sums[head, group]
        rest = acc[head]
        n = 64
        while n >= 8:
            rest = rest[:n] + pltpu.roll(rest[n:], 2048 - n, 1)
            n //= 2
        line = rest[7:8]
        for r in range(6, -1, -1):
            line = rest[r : r + 1] + pltpu.roll(line, 2047, 1)
        offsets[pl.ds(2 * step + head, 1), :] = pltpu.roll(line, 127, 1)

    @pl.when(step == pairs - 1)
    def _():
        for copy in late:
            copy.wait()
        made[width : 2 * width, :] = (dot(hid_l[:count, :], dq[:count, :], TN) + dot(hid_r[:count, :], dq[count:, :], TN)).astype(BF16)
        for at, grads in ((2 * width, dk), (3 * width, dv)):
            made[at : at + width, :] = (dot(hid_l[...], grads[: 2 * count, :], TN) + dot(hid_r[...], grads[2 * count :, :], TN)).astype(BF16)
        me = info[6]
        size = made.shape[0] // 32

        @pl.loop(0, 16)
        def _(r):
            keep[r] = made[pl.ds(pl.multiple_of((r ^ me) * size, size), size), :]
            send[pl.ds(pl.multiple_of(r * size, size), size), :] = made[pl.ds(pl.multiple_of(((r + 16) ^ me) * size, size), size), :]

        gain = jnp.zeros((1, width), F32)
        for b, raw in enumerate((near, near_other, far, far_other)):
            spot = slice(b * count, (b + 1) * count)
            grad = dot(dk[spot, :], wk[...], NT) + dot(dv[spot, :], wv[...], NT)
            half = slice((b // 2) * count, (b // 2 + 1) * count)
            if b % 2 == 0:
                grad = grad + dot(dq[half, :], wq[...], NT)
                stay[half, :] = grad
            else:
                leave[half, :] = grad.astype(BF16)
            tokens = raw[...].astype(F32)
            gain = gain + jnp.sum(grad * (tokens * rms_scale(tokens)), axis=0, keepdims=True)
        leave[2 * count :, :] = two_terms(rows_of(dense_rows[0:1, :]))
        picker = jnp.where(lax.broadcasted_iota(jnp.int32, (128, 1), 0) == buckets[...], 1.0, 0.0).astype(BF16)
        left = offsets[...][:, : buckets.shape[1]]
        bias = None
        for _ in range(3):
            part = left.astype(BF16)
            left = left - part.astype(F32)
            bias = dot(part, picker, NT) if bias is None else bias + dot(part, picker, NT)
        bias = jnp.concatenate([bias, jnp.zeros((bias.shape[0], width - 128), F32)], axis=1)
        line = bias[0:1]
        for h in range(1, bias.shape[0]):
            line = line + pltpu.roll(bias[h : h + 1], 32 * h, 1)
        total = rows_of(gain, through_rows[0:1, :], dense_rows[1:2, :], line)
        small[...] = total
        send[16 * size :, :] = two_terms(total)
        for copy in done:
            copy.start()
        for copy in done:
            copy.wait()

def back(info, ql, qr, kl, kr, vl, vr, gout, out, inv, expo, buckets, dense_rows, through_rows,
         hid_l, hid_r, near, near_other, far, far_other, wq, wk, wv, grad_out):
    count, width = near.shape
    smem, free = pl.BlockSpec(memory_space=pltpu.SMEM), pl.BlockSpec(memory_space=pl.ANY)
    whole = lambda *dims: pl.BlockSpec(dims, lambda g: (0,) * len(dims))
    col = lambda n: pl.BlockSpec((n, 128), lambda g: (0, g))
    shape = jax.ShapeDtypeStruct
    size = 4 * width // 32
    outs = [shape((16, size, width), BF16), shape((16 * size + 16, width), BF16), shape((2 * count, width), F32), shape((2 * count + 16, width), BF16)]
    given = (hid_l, hid_r, near, near_other, far, far_other, wq, wk, wv)
    return pl.pallas_call(
        back_kernel,
        grid=(width // 128,),
        in_specs=[smem, col(count), col(count)] + [col(2 * count)] * 7 + [pl.BlockSpec((2, 2 * count, 4 * count), lambda g: (g, 0, 0)),
                  whole(*buckets.shape), whole(8, width), whole(8, width)] + [free] * 10,
        out_specs=[free] * 4 + [whole(8, width)],
        out_shape=outs + [shape((8, width), F32)],
        scratch_shapes=[pltpu.VMEM(g.shape, BF16) for g in given] + [pltpu.VMEM((4 * width, width), BF16)]
                       + [pltpu.VMEM(o.shape, o.dtype) for o in outs]
                       + [pltpu.VMEM((2 * count, width), BF16), pltpu.VMEM((4 * count, width), BF16), pltpu.VMEM((4 * count, width), BF16),
                          pltpu.VMEM((8, 2048), F32), pltpu.VMEM((2, 6, 128, 384), F32), pltpu.VMEM((2, 128, 2048), F32),
                          pltpu.VMEM((2, 2 * count, 4 * count), BF16), pltpu.SemaphoreType.DMA((14,))],
        name="back", compiler_params=pltpu.CompilerParams(vmem_limit_bytes=44 << 20),
    )(info, ql, qr, kl, kr, vl, vr, gout, out, inv, expo, buckets, dense_rows, through_rows, *given, grad_out)

def ending_kernel(info, stay, came, near, far, grad_mixed, gain, dense_rows, home, away):
    count, width = near.shape
    for part, raw in enumerate((near, far)):
        spot = slice(part * count, (part + 1) * count)
        tokens = raw[...].astype(F32)
        grad = stay[spot, :] + came[spot, :].astype(F32)
        more, _ = norm_back(grad, tokens, rms_scale(tokens), gain[...])
        value = (grad_mixed[spot, :] + more).astype(BF16)
        if part == 0:
            home[:count, :] = value
        else:
            away[:count, :] = value
    alive = (info[0] - info[5]).astype(F32)
    pool = two_terms((rows_of(dense_rows[0:1, :]) + one_value(came[2 * count :, :])) / alive)
    home[count:, :] = pool
    away[count:, :] = pool

def ending(info, stay, came, near, far, grad_mixed, gain, dense_rows):
    count, width = near.shape
    smem, vmem = pl.BlockSpec(memory_space=pltpu.SMEM), pl.BlockSpec(memory_space=pltpu.VMEM)
    shape = jax.ShapeDtypeStruct((count + 16, width), BF16)
    return pl.pallas_call(
        ending_kernel, in_specs=[smem] + [vmem] * 7, out_specs=[vmem] * 2, out_shape=[shape, shape], name="ending", compiler_params=pltpu.CompilerParams(vmem_limit_bytes=10 << 20)
    )(info, stay, came, near, far, grad_mixed, gain, dense_rows)

def place_kernel(firsts, info, *refs):
    parts, (back, front, rows, columns, sems) = refs[: len(firsts)], refs[-5:]
    mine = info[6] & 15
    for side in range(2):
        @pl.when(info[7] == side)
        def _(side=side):
            copies, n = [], 0
            for part, first in zip(parts, firsts):
                for i in range(part.shape[0]):
                    r = first + i
                    to = pl.ds(pl.multiple_of(((r & 15) ^ mine) * 128, 128), 128)
                    if (r >= 16) == (side == 1):
                        for q in range(4):
                            rows[n, :, q * 128 : (q + 1) * 128] = part[i, q * 128 : (q + 1) * 128, :].astype(F32)
                        copies.append(pltpu.make_async_copy(rows.at[n], back.at[to, :], sems.at[n]))
                    else:
                        columns[n] = part[i].astype(F32)
                        copies.append(pltpu.make_async_copy(columns.at[n], front.at[:, to], sems.at[n]))
                    copies[-1].start()
                    n += 1
            for copy in copies:
                copy.wait()

def place(info, parts, made, width):
    smem, vmem, far = (pl.BlockSpec(memory_space=m) for m in (pltpu.SMEM, pltpu.VMEM, pltpu.HBM))
    shape = jax.ShapeDtypeStruct
    count = sum(p.shape[0] for _, p in parts)
    return pl.pallas_call(
        functools.partial(place_kernel, [first for first, _ in parts]),
        in_specs=[smem] + [vmem] * len(parts) + [far] * len(made),
        out_specs=[far] * 2,
        out_shape=[shape((16 * 128, width), F32), shape((width, 16 * 128), F32)],
        scratch_shapes=[pltpu.VMEM((count, 128, width), F32), pltpu.VMEM((count, width, 128), F32), pltpu.SemaphoreType.DMA((count,))],
        input_output_aliases={1 + len(parts) + i: i for i in range(len(made))},
        name="place", compiler_params=pltpu.CompilerParams(vmem_limit_bytes=24 << 20),
    )(info, *[p for _, p in parts], *made)

def sort_kernel(firsts, info, *refs):
    parts, made, (tall, sems) = refs[: len(firsts)], refs[-6:-2], refs[-2:]
    size = parts[0].shape[1]
    mine = info[6]
    pieces = []
    for part, first in zip(parts, firsts):
        for i in range(part.shape[0]):
            tall[len(pieces)] = part[i].astype(F32)
            pieces.append(first + i)
    for top in range(4):
        @pl.when((mine >> 3) == top)
        def _(top=top):
            copies = []
            for n, r in enumerate(pieces):
                to = pl.ds(pl.multiple_of(((r ^ mine) & 7) * size, size), size)
                copies.append(pltpu.make_async_copy(tall.at[n], made[top ^ (r >> 3)].at[to, :], sems.at[n]))
                copies[-1].start()
            for copy in copies:
                copy.wait()

def sort(info, parts, made, width):
    smem, vmem, far = (pl.BlockSpec(memory_space=m) for m in (pltpu.SMEM, pltpu.VMEM, pltpu.HBM))
    shape = jax.ShapeDtypeStruct((width, width), F32)
    count = sum(p.shape[0] for _, p in parts)
    return pl.pallas_call(
        functools.partial(sort_kernel, [first for first, _ in parts]),
        in_specs=[smem] + [vmem] * len(parts) + [far] * len(made),
        out_specs=[far] * 4,
        out_shape=[shape] * 4,
        scratch_shapes=[pltpu.VMEM((count,) + parts[0][1].shape[1:], F32), pltpu.SemaphoreType.DMA((count,))],
        input_output_aliases={1 + len(parts) + i: i for i in range(len(made))},
        name="sort", compiler_params=pltpu.CompilerParams(vmem_limit_bytes=12 << 20),
    )(info, *[p for _, p in parts], *made)

def mix_kernel(*refs):
    for k in range(4):
        refs[4 + k][...] = added(*[term[k] for term in refs[:4]])

def mix(terms):
    block = terms[0].shape[1:]
    vmem = pl.BlockSpec(memory_space=pltpu.VMEM)
    return pl.pallas_call(
        mix_kernel, in_specs=[vmem] * 4, out_specs=[vmem] * 4, out_shape=[jax.ShapeDtypeStruct(block, BF16)] * 4, name="mix", compiler_params=pltpu.CompilerParams(vmem_limit_bytes=10 << 20),
    )(*terms)

def exchange(value, bits):
    size = lax.axis_size("dp") * lax.axis_size("blk")
    return lax.ppermute(value, ("dp", "blk"), [(i, i ^ bits) for i in range(size)])

def wait(*values):
    return lax.optimization_barrier(values)

def added(*terms):
    total = terms[0].astype(F32)
    for term in terms[1:]:
        total = total + term.astype(F32)
    return total.astype(BF16)

def local(inputs, w_query, w_key, w_value, w_out, w_in, w_back, norm1_gain, norm2_gain, final_gain, bias_table, bucket_table, prefix_len, pad_len, pooled_grad):
    rows, width = inputs.shape[1:]
    spot, far_off = lax.axis_index("blk"), lax.axis_index("dp")
    doc, core = spot // 2, spot % 2
    block = [doc * 2 + core, doc * 2 + 1 - core, (1 - doc) * 2 + core, (1 - doc) * 2 + 1 - core]
    line = [8, 16]
    further = [32 << b for b in range((lax.axis_size("dp") // 8).bit_length() - 1)]
    piece = core * 16 + doc * 4 + (far_off % 2) * 8 + (far_off // 2) % 4
    near = jnp.where(doc == 0, inputs[0], inputs[1])
    far_send = jnp.where(doc == 0, inputs[1], inputs[0])
    near, far_send = wait(near, far_send)
    far = exchange(far_send, ROW)
    near_other = exchange(near, CORE)
    slot = jnp.arange(8, dtype=jnp.int32)
    ids = jnp.zeros_like(slot)
    for i, value in enumerate([b * rows for b in block] + [piece, core, doc]):
        ids = jnp.where(slot == i, value, ids)
    gain1, gain2, gain3 = norm1_gain[None, :], norm2_gain[None, :], final_gain[None, :]
    buckets = bucket_table[None, :]
    hid_l, q_l, k_l, v_l, w_query, w_key, w_value, w_out = prepare(near, near_other, gain1, w_query, w_key, w_value, w_out)
    far, q_l, ids = wait(far, q_l, ids)
    far_other = exchange(far, CORE)
    (hid_r, q_r, k_r, v_r, expo, inverse, attended, send, active, slopes, turned, mixed, steep, dense_rows, info) = front(
        ids, pad_len, prefix_len, far, far_other, near, q_l, k_l, v_l, bias_table.T, buckets, w_query, w_key, w_value,
        gain1, gain2, gain3, pooled_grad, w_out, w_in, w_back)

    xy = [ROW, NEAR_X, ROW ^ NEAR_X]
    zz = [line[0], line[1], line[0] ^ line[1]]

    token, send = wait(info, send)
    got = exchange(send, CORE)
    grad_mixed, grad_attended, grad_out_w, through_rows = through(token, slopes, w_in, mixed, steep, w_out, attended, gain2)
    token, through_rows, got = wait(token, through_rows, got)
    stays, *sends = meet(token, got, active, slopes, turned, steep)

    token, sends = wait(token, sends)
    came = [exchange(s, m) for s, m in zip(sends, xy)]
    rest_keep, rest_send, stay, leave, small = back(
        token, q_l, q_r, k_l, k_r, v_l, v_r, grad_attended, attended, inverse, expo, buckets, dense_rows, through_rows,
        hid_l, hid_r, near, near_other, far, far_other, w_query, w_key, w_value, grad_out_w)
    token, small, rest_send, leave, came = wait(token, small, rest_send, leave, came)

    rest_got = exchange(rest_send, CORE)
    hidden_got = exchange(leave, CORE)
    lines = mix([stays] + list(came))
    token, lines = wait(token, lines)
    took = [exchange(lines[k + 1], m) for k, m in enumerate(zz)]
    token, rest_got, hidden_got = wait(token, rest_got, hidden_got)

    count = rest_keep.shape[0] * rest_keep.shape[1]
    small = small + one_value(rest_got[count:])
    rest_got = rest_got[:count].reshape(rest_keep.shape)
    terms = two_terms(small)
    sends = [jnp.concatenate([added(rest_keep[4 * k : 4 * k + 4], rest_got[4 * k : 4 * k + 4]).reshape(-1, width), terms]) for k in (1, 2, 3)]
    token, sends = wait(token, sends)
    rest_came = [exchange(s, m) for s, m in zip(sends, xy)]
    home, away = ending(token, stay, hidden_got, near, far, grad_mixed, gain1, dense_rows)
    token, took, away = wait(token, took, away)

    whole = added(lines[0], *took)
    for bit in further:
        whole = added(whole, exchange(whole, bit))
    token, whole = wait(token, whole)
    back_line = [exchange(whole, m) for m in zz]
    away_got = exchange(away, ROW)
    token, rest_came = wait(token, rest_came)

    count = count // 4
    for part in rest_came:
        small = small + one_value(part[count:])
    rest_came = [part[:count].reshape((4,) + rest_keep.shape[1:]) for part in rest_came]
    piece = count // 4
    lines = added(rest_keep[:4], rest_got[:4], *rest_came).reshape(-1, width)
    send = jnp.concatenate([lines[piece : 2 * piece], lines[3 * piece :], two_terms(small)])
    token, send = wait(token, send)
    took = exchange(send, line[0])
    token, took = wait(token, took)
    small = small + one_value(took[2 * piece :])
    send = jnp.concatenate([added(lines[2 * piece : 3 * piece], took[piece : 2 * piece]), two_terms(small)])
    lines = added(lines[:piece], took[:piece])
    token, send, back_line, away_got = wait(token, send, back_line, away_got)
    took = exchange(send, line[1])

    quarter = jnp.stack([whole] + back_line)
    token, quarter = wait(token, quarter)
    from_y, from_x = exchange(quarter, ROW), exchange(quarter, NEAR_X)
    pool_mine, pool_other = one_value(home[rows:])[:1], one_value(away_got[rows:])[:1]
    pooled = jnp.where(doc == 0, jnp.concatenate([pool_mine, pool_other]), jnp.concatenate([pool_other, pool_mine]))
    home, away_got = home[:rows], away_got[:rows]
    input_grad = jnp.where(doc == 0, jnp.stack([home, away_got]), jnp.stack([away_got, home]))
    token, took, pooled, input_grad = wait(token, took, pooled, input_grad)

    small = small + one_value(took[piece:])
    rest = added(lines, took[:piece])
    for bit in further:
        rest = added(rest, exchange(rest, bit))
        small = small + exchange(small, bit)
    token, rest = wait(token, rest)
    rest_back = [exchange(rest, m) for m in zz]
    outs = [small[0], small[1], small[2], small[3, : bias_table.size].reshape(bias_table.shape[::-1]).T]
    token, from_y, from_x, outs = wait(token, from_y, from_x, outs)

    sends = [from_x[:2], from_y[2:]]
    token, sends, rest_back = wait(token, sends, rest_back)
    far_a, far_b = exchange(sends[0], ROW), exchange(sends[1], NEAR_X)
    fourth = jnp.stack([rest] + rest_back)
    token, fourth, quarter = wait(token, fourth, quarter)
    fourth_y, fourth_x = exchange(fourth, ROW), exchange(fourth, NEAR_X)
    other = exchange(quarter, CORE)
    near_pair = jnp.concatenate([from_y, from_x])
    grads = place(token, [(0, quarter), (4, from_y), (8, from_x)], [], width)
    token, grads, other, near_pair, far_a, far_b, fourth_y, fourth_x = wait(token, grads, other, near_pair, far_a, far_b, fourth_y, fourth_x)

    sends = [fourth_x[:2], fourth_y[2:], near_pair, jnp.concatenate([far_a, far_b]), jnp.concatenate([fourth, fourth_y, fourth_x])]
    token, sends = wait(token, sends)
    last_a, last_b, other_near, other_far, pair = (exchange(s, m) for s, m in zip(sends, (ROW, NEAR_X, CORE, CORE, CORE)))
    grads = place(token, [(12, far_a), (14, far_b), (16, other)], grads, width)
    token, grads, other_near, other_far = wait(token, grads, other_near, other_far)
    out_back, out_in = place(token, [(20, other_near), (28, other_far)], grads, width)
    token, out_back, out_in, last_a, last_b, pair = wait(token, out_back, out_in, last_a, last_b, pair)

    ends = exchange(jnp.concatenate([last_a, last_b]), CORE)
    made = sort(token, [(0, fourth), (4, fourth_y), (8, fourth_x), (12, last_a), (14, last_b), (16, pair)], [], width)
    token, made, ends = wait(token, made, ends)
    out_out, out_query, out_key, out_value = sort(token, [(28, ends)], made, width)
    return (pooled, input_grad, out_query, out_key, out_value, out_out, out_in, out_back, *outs)

def solution(mesh):
    data = P("dp", "blk", None)
    placed = (data,) + (P(),) * 11 + (P("dp"), P("dp"), P("dp", None))
    return jax.shard_map(local, mesh=mesh, in_specs=placed, out_specs=(P("dp", None), data) + (P(),) * 10, check_vma=False)
```

```python
import functools
import jax, jax.numpy as jnp
from jax import lax
from jax.experimental import pallas as pl
from jax.experimental.pallas import tpu as pltpu
from jax.sharding import PartitionSpec as P

F32, BF16 = jnp.float32, jnp.bfloat16
NEG = -1000000000.0
NT = (((1,), (1,)), ((), ()))
TN = (((0,), (0,)), ((), ()))
NN = (((1,), (0,)), ((), ()))

def dot(a, b, dims=NN):
    return lax.dot_general(a, b, dims, preferred_element_type=F32)

def skew(row, width, dtype=F32):
    return pltpu.roll(jnp.broadcast_to(row, (128, width)), width - 127, 1, stride=1, stride_axis=0)


BUCKETS = 32
EPS = 1e-06
CORE, ROW, NEAR_X = 1, 2, 4

def rms_scale(values):
    return lax.rsqrt(jnp.mean(values * values, axis=-1, keepdims=True) + EPS)

def norm_back(grad_out, values, scale, gain):
    weighted = grad_out * gain
    inner = jnp.mean(weighted * values, axis=-1, keepdims=True)
    grad_in = scale * weighted - scale * scale * scale * values * inner
    return grad_in, jnp.sum(grad_out * values * scale, axis=0, keepdims=True)

def two_terms(value):
    high = value.astype(BF16)
    return jnp.concatenate([high, (value - high.astype(F32)).astype(BF16)])

def one_value(terms):
    return terms[:8].astype(F32) + terms[8:16].astype(F32)

def rows_of(*values):
    count = sum(v.shape[0] for v in values)
    return jnp.concatenate(list(values) + [jnp.zeros((8 - count, values[0].shape[1]), F32)])

def prepare_kernel(mine, other, gain, wq_h, wk_h, wv_h, hidden, query, keys, values, wq, wk, wv, sems):
    rows = mine.shape[0]
    load = [pltpu.make_async_copy(a, b, sems.at[i]) for i, (a, b) in enumerate(((wk_h, wk), (wv_h, wv), (wq_h, wq)))]
    for copy in load:
        copy.start()
    for part, raw in enumerate((mine, other)):
        tokens = raw[...].astype(F32)
        hidden[part * rows : (part + 1) * rows, :] = (tokens * rms_scale(tokens) * gain[...]).astype(BF16)
    h = hidden[...]
    load[0].wait()
    keys[...] = dot(h, wk[...]).astype(BF16)
    load[1].wait()
    values[...] = dot(h, wv[...]).astype(BF16)
    load[2].wait()
    query[...] = dot(h[:rows], wq[...]).astype(BF16)

def prepare(mine, other, gain, wq, wk, wv):
    rows, width = mine.shape
    shape = lambda n: jax.ShapeDtypeStruct((n, width), BF16)
    vmem, free = (pl.BlockSpec(memory_space=m) for m in (pltpu.VMEM, pl.ANY))
    return pl.pallas_call(
        prepare_kernel,
        in_specs=[vmem] * 3 + [free] * 3,
        out_specs=[vmem] * 7,
        out_shape=[shape(2 * rows), shape(rows), shape(2 * rows), shape(2 * rows)] + [shape(width)] * 3,
        scratch_shapes=[pltpu.SemaphoreType.DMA((3,))],
        name="prepare", compiler_params=pltpu.CompilerParams(vmem_limit_bytes=14 << 20),
    )(mine, other, gain, wq, wk, wv)

def tables_kernel(ids, pads, prefixes, bias, buckets, lines, info, *, length):
    doc = ids[6]
    info[0] = length - jnp.where(doc == 0, pads[0], pads[1])
    info[5] = jnp.where(doc == 0, prefixes[0], prefixes[1])
    for to, at in enumerate((0, 1, 2, 3)):
        info[1 + to] = ids[at]
    for to, at in enumerate((4, 5, 6)):
        info[6 + to] = ids[at]
    picker = jnp.where(lax.broadcasted_iota(jnp.int32, (BUCKETS, 1), 0) == buckets[...], 1.0, 0.0).astype(BF16)
    left, total = bias[...], None
    for _ in range(3):
        part = left.astype(BF16)
        left = left - part.astype(F32)
        made = dot(part, picker)
        total = made if total is None else total + made
    lines[...] = jnp.zeros_like(lines)
    lines[:, : buckets.shape[1]] = total

def tables(ids, pads, prefixes, bias, buckets, length):
    smem, vmem = pl.BlockSpec(memory_space=pltpu.SMEM), pl.BlockSpec(memory_space=pltpu.VMEM)
    return pl.pallas_call(
        functools.partial(tables_kernel, length=length),
        in_specs=[smem] * 3 + [vmem] * 2,
        out_specs=[vmem, smem],
        out_shape=[jax.ShapeDtypeStruct((bias.shape[0], buckets.shape[1] + 1), F32), jax.ShapeDtypeStruct((16,), jnp.int32)],
        name="tables", compiler_params=pltpu.CompilerParams(vmem_limit_bytes=4 << 20),
    )(ids, pads, prefixes, bias, buckets)

def back_pieces(to, active, low, mine):
    @pl.loop(0, active.shape[1] // 512)
    def _(group):
        made = dot(active[:, pl.ds(pl.multiple_of(group * 512, 512), 512)], low, TN).astype(BF16)
        for b in range(4):
            rows = made[b * 128 : (b + 1) * 128]
            to[(4 * group + b) ^ mine] = jnp.concatenate([rows[:, q * 128 : (q + 1) * 128] for q in range(4)])

def in_pieces(to, slopes, turned, mine):
    @pl.loop(0, slopes.shape[1] // 512)
    def _(group):
        made = dot(turned, slopes[:, pl.ds(pl.multiple_of(group * 512, 512), 512)]).astype(BF16)
        for b in range(4):
            to[(4 * group + b) ^ mine] = made[:, b * 128 : (b + 1) * 128]

def front_kernel(info, far, far_other, near, q_l, k_l, v_l, lines, wq, wk, wv, gain1, gain2, gain3, cots, wo_h, win_h, wback_h,
                 hid_o, q_o, k_o, v_o, expo_o, inv_o, att_o, send_o, active_o, slopes_o, turned_o, mixed_o, steep_o, rows,
                 hid, qs, ks, vs, inv, att, send, active, slopes, turned, mixed, steep, wo, win, wback, expo, scores, skewed, edges, sems):
    count, width = near.shape
    hidden = win.shape[1]
    step = pl.program_id(0)
    late = [pltpu.make_async_copy(a, b, sems.at[i]) for i, (a, b) in enumerate(((wo_h, wo), (win_h, win), (wback_h, wback)))]
    early = [pltpu.make_async_copy(a, b, sems.at[3 + i]) for i, (a, b) in enumerate(((hid, hid_o), (qs, q_o), (ks, k_o), (vs, v_o)))]
    dense = [pltpu.make_async_copy(a, b, sems.at[7 + i]) for i, (a, b) in enumerate((
        (inv, inv_o), (att, att_o), (mixed, mixed_o), (turned, turned_o), (active, active_o), (steep, steep_o), (slopes, slopes_o), (send, send_o)))]
    kept = lambda g: pltpu.make_async_copy(expo, expo_o.at[pl.ds(2 * g, 2)], sems.at[15])

    @pl.when(step == 0)
    def _():
        for copy in late:
            copy.start()
        for part, raw in enumerate((far, far_other)):
            tokens = raw[...].astype(F32)
            hid[part * count : (part + 1) * count, :] = (tokens * rms_scale(tokens) * gain1[...]).astype(BF16)
        h = hid[...]
        qs[...] = dot(h[:count], wq[...]).astype(BF16)
        ks[...] = dot(h, wk[...]).astype(BF16)
        vs[...] = dot(h, wv[...]).astype(BF16)
        for copy in early:
            copy.start()
        column = lax.broadcasted_iota(jnp.int32, (1, 128), 1)
        for b in range(4):
            place = info[1 + b] + lax.broadcasted_iota(jnp.int32, (count, 1), 0)
            gate = jnp.where(place < info[0], 0.0, NEG)
            for head in range(2):
                edges[head, b * count : (b + 1) * count, :] = jnp.where(column == (64 if head == 0 else 0), gate, 0.0).astype(BF16)

    @pl.when(step > 0)
    def _():
        kept(step - 1).wait()

    cols = pl.ds(pl.multiple_of(step * 128, 128), 128)
    lane = lax.broadcasted_iota(jnp.int32, (1, 128), 1)
    first = lane < 64
    limit = info[0]
    starts = [info[1 + b] for b in range(4)]
    keys = [k_l[:count, :], k_l[count:, :], ks[:count, cols], ks[count:, cols]]
    values = jnp.concatenate([v_l[...], vs[:, cols]])
    query = jnp.concatenate([q_l[...], qs[:, cols]])
    made = []
    for head in range(2):
        mine = jnp.where(first if head == 0 else lane >= 64, 1.0, 0.0).astype(BF16)
        one = jnp.where(lane == (64 if head == 0 else 0), 1.0, 0.0).astype(BF16)
        q = query * mine + one
        v = values * mine + one
        skewed[head] = skew(lines[pl.ds(2 * step + head, 1), :], lines.shape[1])
        for b in range(4):
            s = dot(q, keys[b] * mine + edges[head, b * count : (b + 1) * count, :], NT)
            for r in range(4):
                at = starts[b] - starts[2 * (r // 2)] + 896 - 128 * (r % 2)
                part = s[r * 128 : (r + 1) * 128] + skewed[head, :, pl.ds(pl.multiple_of(at, 128), 256)]
                scores[head, r * 128 : (r + 1) * 128, b * 256 : (b + 1) * 256] = part
        for r in range(4):
            rs = slice(r * 128, (r + 1) * 128)
            value = scores[head, rs, :]
            top = jnp.max(value, axis=1, keepdims=True)
            expo[head, rs, :] = jnp.exp(value - top).astype(BF16)
        acc = dot(expo[head], v)
        made.append((acc, 1.0 / (acc[:, 64:65] if head == 0 else acc[:, 0:1])))
    (a0, i0), (a1, i1) = made
    scale = jnp.where(first, i0, i1)
    att[:, cols] = (jnp.where(first, a0, a1) * scale).astype(BF16)
    inv[:, cols] = scale
    kept(step).start()

    @pl.when(step == 3)
    def _():
        for copy in late:
            copy.wait()
        dense[0].start()
        dense[1].start()
        for part, raw in enumerate((near, far)):
            spot = slice(part * count, (part + 1) * count)
            mixed[spot, :] = raw[...].astype(F32) + dot(att[spot, :], wo[...])
        dense[2].start()
        values = mixed[...]
        inner = (values * rms_scale(values) * gain2[...]).astype(BF16)
        turned[...] = inner.T
        dense[3].start()
        total = values
        for at in range(0, hidden, 512):
            lifted = jnp.maximum(dot(inner, win[:, at : at + 512]), 0.0).astype(BF16)
            active[:, at : at + 512] = lifted
            total = total + dot(lifted, wback[at : at + 512, :])
        dense[4].start()
        scale = rms_scale(total)
        place = lax.broadcasted_iota(jnp.int32, (2 * count, 1), 0)
        place = jnp.where(place < count, place + info[1], place + (info[3] - count))
        live = jnp.where((place >= info[5]) & (place < limit), 1.0, 0.0)
        pool = jnp.sum(total * scale * gain3[...] * live, axis=0, keepdims=True)
        cot = jnp.where(info[8] == 0, cots[0:1, :], cots[1:2, :]) / (limit - info[5]).astype(F32)
        slope, grad_end = norm_back(live * cot, total, scale, gain3[...])
        steep[...] = slope
        dense[5].start()
        rows[...] = jnp.concatenate([pool, grad_end, jnp.zeros((6, width), F32)])
        low = slope.astype(BF16)
        for at in range(0, hidden, 512):
            through = dot(low, wback[at : at + 512, :], NT).astype(BF16)
            slopes[:, at : at + 512] = jnp.where(active[:, at : at + 512] > 0, through, jnp.zeros_like(through))
        dense[6].start()
        mine = info[6] & 15

        @pl.when(info[7] == 0)
        def _():
            in_pieces(send, slopes, turned[...], mine)

        @pl.when(info[7] == 1)
        def _():
            back_pieces(send, active, steep[...].astype(BF16), mine)

        dense[7].start()
        for copy in early + dense:
            copy.wait()
        kept(step).wait()

def front(info, far, far_other, near, q_l, k_l, v_l, lines, wq, wk, wv, gain1, gain2, gain3, cots, wo, win, wback):
    count, width = near.shape
    hidden = win.shape[1]
    heads, span = lines.shape
    shape = jax.ShapeDtypeStruct
    smem, free = pl.BlockSpec(memory_space=pltpu.SMEM), pl.BlockSpec(memory_space=pl.ANY)
    whole = lambda *dims: pl.BlockSpec(dims, lambda g: (0,) * len(dims))
    col = lambda n: pl.BlockSpec((n, 128), lambda g: (0, g))
    outs = [shape((2 * count, width), BF16), shape((count, width), BF16), shape((2 * count, width), BF16), shape((2 * count, width), BF16),
            shape((heads, 2 * count, 4 * count), BF16), shape((2 * count, width), F32), shape((2 * count, width), BF16),
            shape((16, width, 128), BF16), shape((2 * count, hidden), BF16), shape((2 * count, hidden), BF16),
            shape((width, 2 * count), BF16), shape((2 * count, width), F32), shape((2 * count, width), F32)]
    return pl.pallas_call(
        front_kernel,
        grid=(heads // 2,),
        in_specs=[smem] + [whole(count, width)] * 3 + [col(count), col(2 * count), col(2 * count), whole(heads, span)] + [whole(width, width)] * 3 + [whole(1, width)] * 3
                 + [whole(2, width)] + [pl.BlockSpec(memory_space=pltpu.HBM)] * 3,
        out_specs=[free] * 13 + [whole(8, width)],
        out_shape=outs + [shape((8, width), F32)],
        scratch_shapes=[pltpu.VMEM(o.shape, o.dtype) for o in outs[:4] + outs[5:]]
                       + [pltpu.VMEM(wo.shape, BF16), pltpu.VMEM(win.shape, BF16), pltpu.VMEM(wback.shape, BF16),
                          pltpu.VMEM((2, 2 * count, 4 * count), BF16), pltpu.VMEM((2, 2 * count, 4 * count), F32),
                          pltpu.VMEM((2, 128, span), F32), pltpu.VMEM((2, 4 * count, 128), BF16), pltpu.SemaphoreType.DMA((16,))],
        name="front", compiler_params=pltpu.CompilerParams(vmem_limit_bytes=36 << 20),
    )(info, far, far_other, near, q_l, k_l, v_l, lines, wq, wk, wv, gain1, gain2, gain3, cots, wo, win, wback)

def through_kernel(info, slopes_h, win_h, mixed_h, steep_h, wo_h, att_h, gain2, grad_mixed_o, grad_attended_o, grad_out_o, rows,
                   slopes, win, mixed, steep, wo, att, grad_mixed, grad_attended, grad_out, sems):
    hidden, width = slopes.shape[1], mixed.shape[1]
    chunks = []
    for i, at in enumerate(range(0, hidden, 512)):
        for a, b, s in ((slopes_h, slopes, i), (win_h, win, 4 + i)):
            chunks.append(pltpu.make_async_copy(a.at[:, at : at + 512], b.at[:, at : at + 512], sems.at[s]))
    copies = [pltpu.make_async_copy(a, b, sems.at[8 + i]) for i, (a, b) in enumerate((
        (mixed_h, mixed), (steep_h, steep), (wo_h, wo), (att_h, att)))]
    outs = [pltpu.make_async_copy(a, b, sems.at[12 + i]) for i, (a, b) in enumerate((
        (grad_mixed, grad_mixed_o), (grad_attended, grad_attended_o), (grad_out, grad_out_o)))]
    for copy in chunks + copies:
        copy.start()
    grad_inner = None
    for i, at in enumerate(range(0, hidden, 512)):
        chunks[2 * i].wait()
        chunks[2 * i + 1].wait()
        part = dot(slopes[:, at : at + 512], win[:, at : at + 512], NT)
        grad_inner = part if grad_inner is None else grad_inner + part
    copies[0].wait()
    copies[1].wait()
    values = mixed[...]
    more, grad_two = norm_back(grad_inner, values, rms_scale(values), gain2[...])
    total = steep[...] + more
    grad_mixed[...] = total
    outs[0].start()
    low = total.astype(BF16)
    copies[2].wait()
    grad_attended[...] = dot(low, wo[...], NT).astype(BF16)
    outs[1].start()
    copies[3].wait()
    grad_out[...] = dot(att[...], low, TN).astype(BF16)
    outs[2].start()
    rows[...] = jnp.concatenate([grad_two, jnp.zeros((7, width), F32)])
    for copy in outs:
        copy.wait()

def through(info, slopes, win, mixed, steep, wo, att, gain2):
    n, width = mixed.shape
    smem, vmem, free = (pl.BlockSpec(memory_space=m) for m in (pltpu.SMEM, pltpu.VMEM, pl.ANY))
    shape = jax.ShapeDtypeStruct
    given = (slopes, win, mixed, steep, wo, att)
    outs = [shape((n, width), F32), shape((n, width), BF16), shape((width, width), BF16)]
    return pl.pallas_call(
        through_kernel,
        in_specs=[smem, free, pl.BlockSpec(memory_space=pltpu.HBM)] + [free] * 4 + [vmem],
        out_specs=[free] * 3 + [vmem],
        out_shape=outs + [shape((8, width), F32)],
        scratch_shapes=[pltpu.VMEM(g.shape, g.dtype) for g in given] + [pltpu.VMEM(o.shape, o.dtype) for o in outs] + [pltpu.SemaphoreType.DMA((15,))],
        name="through", compiler_params=pltpu.CompilerParams(vmem_limit_bytes=16 << 20),
    )(info, *given, gain2)

def meet_kernel(info, got_h, active_h, slopes_h, turned_h, steep_h, *refs):
    outs, (got, chunk, turned, steep, blocks, sems) = refs[:4], refs[4:]
    order = (3, 1, 2, 0)
    high, lowest = (info[6] & 15) >> 2, info[6] & 3
    load = [pltpu.make_async_copy(got_h.at[4 * k : 4 * k + 4], got.at[k], sems.at[k]) for k in range(4)]
    save = [pltpu.make_async_copy(blocks.at[k], outs[k], sems.at[4 + k]) for k in range(4)]

    def columns(source, k):
        at = pl.ds(pl.multiple_of((k ^ high) * 512, 512), 512)
        return pltpu.make_async_copy(source.at[:, at], chunk.at[k], sems.at[8 + k])

    for side, source in ((0, active_h), (1, slopes_h)):
        @pl.when(info[7] == side)
        def _(side=side, source=source):
            extra = pltpu.make_async_copy(*((steep_h, steep) if side == 0 else (turned_h, turned)), sems.at[12])
            extra.start()
            for k in order:
                columns(source, k).start()
                load[k].start()
            extra.wait()
            low = steep[...].astype(BF16) if side == 0 else turned[...]
            for k in order:
                columns(source, k).wait()
                made = dot(chunk[k], low, TN) if side == 0 else dot(low, chunk[k])
                load[k].wait()
                for b in range(4):
                    piece = made[:, b * 128 : (b + 1) * 128]
                    if side == 0:
                        piece = made[b * 128 : (b + 1) * 128]
                        piece = jnp.concatenate([piece[:, q * 128 : (q + 1) * 128] for q in range(4)])
                    to = b ^ lowest
                    blocks[k, to] = (piece + got[k, to].astype(F32)).astype(BF16)
                save[k].start()

    for copy in save:
        copy.wait()

def meet(info, got, active, slopes, turned, steep):
    smem, free = pl.BlockSpec(memory_space=pltpu.SMEM), pl.BlockSpec(memory_space=pl.ANY)
    block = (4,) + got.shape[1:]
    n, width = steep.shape
    return pl.pallas_call(
        meet_kernel,
        in_specs=[smem] + [free] * 5,
        out_specs=[free] * 4,
        out_shape=[jax.ShapeDtypeStruct(block, BF16)] * 4,
        scratch_shapes=[pltpu.VMEM((4,) + block, BF16), pltpu.VMEM((4, n, 512), BF16), pltpu.VMEM(turned.shape, BF16), pltpu.VMEM(steep.shape, F32),
                        pltpu.VMEM((4,) + block, BF16), pltpu.SemaphoreType.DMA((13,))],
        name="meet", compiler_params=pltpu.CompilerParams(vmem_limit_bytes=20 << 20),
    )(info, got, active, slopes, turned, steep)

CLASS = {(0, 0): 0, (1, 2): 0, (0, 1): 1, (1, 3): 1, (0, 2): 2, (0, 3): 3, (1, 0): 4, (1, 1): 5}

def back_kernel(info, ql, qr, kl, kr, vl, vr, gout, out, inv, expo, buckets, dense_rows, through_rows,
                hid_l_h, hid_r_h, near_h, near_other_h, far_h, far_other_h, wq_h, wk_h, wv_h, grad_out_h,
                keep_o, send_o, stay_o, leave_o, small,
                hid_l, hid_r, near, near_other, far, far_other, wq, wk, wv, made,
                keep, send, stay, leave, dq, dk, dv, offsets, sums, acc, slopes, sems):
    count, width = near.shape
    step = pl.program_id(0)
    pairs = width // 128
    late = [pltpu.make_async_copy(a, b, sems.at[i]) for i, (a, b) in enumerate((
        (hid_l_h, hid_l), (hid_r_h, hid_r), (near_h, near), (near_other_h, near_other), (far_h, far), (far_other_h, far_other),
        (wq_h, wq), (wk_h, wk), (wv_h, wv), (grad_out_h, made.at[0:width])))]
    done = [pltpu.make_async_copy(a, b, sems.at[10 + i]) for i, (a, b) in enumerate(((send, send_o), (keep, keep_o), (leave, leave_o), (stay, stay_o)))]

    @pl.when(step == 0)
    def _():
        for copy in late:
            copy.start()

    cols = pl.ds(pl.multiple_of(step * 128, 128), 128)
    lane = lax.broadcasted_iota(jnp.int32, (1, 128), 1)
    starts = [info[1 + b] for b in range(4)]
    keys = jnp.concatenate([kl[...], kr[...]])
    values = jnp.concatenate([vl[...], vr[...]])
    query = jnp.concatenate([ql[...], qr[...]])
    scaled = gout[...].astype(F32) * inv[...]
    prod = scaled * out[...].astype(F32)
    low = scaled.astype(BF16)
    query_t, low_t = query.T, low.T
    grads_q, grads_k, grads_v = None, [], []
    for head in range(2):
        mine = (lane < 64) if head == 0 else (lane >= 64)
        base = 64 if head == 0 else 0
        pick = jnp.where(mine, 1.0, 0.0).astype(BF16)
        delta = jnp.sum(jnp.where(mine, prod, 0.0), axis=1, keepdims=True)
        high = delta.astype(BF16).astype(F32)
        extra = jnp.where(lane == base, high, jnp.where(lane == base + 1, delta - high, 0.0)).astype(BF16)
        grad = low * pick + extra
        minus = jnp.where((lane == base) | (lane == base + 1), -1.0, 0.0).astype(BF16)
        for b in range(4):
            spot = slice(b * count, (b + 1) * count)
            ds = dot(grad, values[spot] * pick + minus, NT) * expo[head, :, spot].astype(F32)
            slopes[head, :, spot] = ds.astype(BF16)
            for chunk in range(2):
                upper, lower = (ds[chunk * count + r * 128 : chunk * count + (r + 1) * 128] for r in range(2))
                group = CLASS[chunk, b]
                block = jnp.concatenate([lower[:, :128], lower[:, 128:] + upper[:, :128], upper[:, 128:]], axis=1)
                if (chunk, b) in ((1, 2), (1, 3)):
                    block = block + sums[head, group]
                sums[head, group] = block
        part = dot(slopes[head], keys * pick)
        grads_q = part if grads_q is None else grads_q + part
        half = slice(head * 64, (head + 1) * 64)
        grads_k.append(dot(query_t[half], slopes[head]))
        grads_v.append(dot(low_t[half], expo[head]))
    dq[:, cols] = grads_q.astype(BF16)
    dk[:, cols] = jnp.concatenate(grads_k).astype(BF16).T
    dv[:, cols] = jnp.concatenate(grads_v).astype(BF16).T
    for head in range(2):
        acc[head] = jnp.zeros(acc.shape[1:], F32)
        for (chunk, b), group in CLASS.items():
            if (chunk, b) not in ((1, 2), (1, 3)):
                at = starts[b] - starts[2 * chunk] + 768
                to = pl.ds(pl.multiple_of(at, 128), 384)
                acc[head, :, to] += sums[head, group]
        rest = acc[head]
        n = 64
        while n >= 8:
            rest = rest[:n] + pltpu.roll(rest[n:], 2048 - n, 1)
            n //= 2
        line = rest[7:8]
        for r in range(6, -1, -1):
            line = rest[r : r + 1] + pltpu.roll(line, 2047, 1)
        offsets[pl.ds(2 * step + head, 1), :] = pltpu.roll(line, 127, 1)

    @pl.when(step == pairs - 1)
    def _():
        for copy in late:
            copy.wait()
        made[width : 2 * width, :] = (dot(hid_l[:count, :], dq[:count, :], TN) + dot(hid_r[:count, :], dq[count:, :], TN)).astype(BF16)
        for at, grads in ((2 * width, dk), (3 * width, dv)):
            made[at : at + width, :] = (dot(hid_l[...], grads[: 2 * count, :], TN) + dot(hid_r[...], grads[2 * count :, :], TN)).astype(BF16)
        me = info[6]
        size = made.shape[0] // 32

        @pl.loop(0, 16)
        def _(r):
            keep[r] = made[pl.ds(pl.multiple_of((r ^ me) * size, size), size), :]
            send[pl.ds(pl.multiple_of(r * size, size), size), :] = made[pl.ds(pl.multiple_of(((r + 16) ^ me) * size, size), size), :]

        gain = jnp.zeros((1, width), F32)
        for b, raw in enumerate((near, near_other, far, far_other)):
            spot = slice(b * count, (b + 1) * count)
            grad = dot(dk[spot, :], wk[...], NT) + dot(dv[spot, :], wv[...], NT)
            half = slice((b // 2) * count, (b // 2 + 1) * count)
            if b % 2 == 0:
                grad = grad + dot(dq[half, :], wq[...], NT)
                stay[half, :] = grad
            else:
                leave[half, :] = grad.astype(BF16)
            tokens = raw[...].astype(F32)
            gain = gain + jnp.sum(grad * (tokens * rms_scale(tokens)), axis=0, keepdims=True)
        leave[2 * count :, :] = two_terms(rows_of(dense_rows[0:1, :]))
        picker = jnp.where(lax.broadcasted_iota(jnp.int32, (128, 1), 0) == buckets[...], 1.0, 0.0).astype(BF16)
        left = offsets[...][:, : buckets.shape[1]]
        bias = None
        for _ in range(3):
            part = left.astype(BF16)
            left = left - part.astype(F32)
            bias = dot(part, picker, NT) if bias is None else bias + dot(part, picker, NT)
        bias = jnp.concatenate([bias, jnp.zeros((bias.shape[0], width - 128), F32)], axis=1)
        line = bias[0:1]
        for h in range(1, bias.shape[0]):
            line = line + pltpu.roll(bias[h : h + 1], 32 * h, 1)
        total = rows_of(gain, through_rows[0:1, :], dense_rows[1:2, :], line)
        small[...] = total
        send[16 * size :, :] = two_terms(total)
        for copy in done:
            copy.start()
        for copy in done:
            copy.wait()

def back(info, ql, qr, kl, kr, vl, vr, gout, out, inv, expo, buckets, dense_rows, through_rows,
         hid_l, hid_r, near, near_other, far, far_other, wq, wk, wv, grad_out):
    count, width = near.shape
    smem, free = pl.BlockSpec(memory_space=pltpu.SMEM), pl.BlockSpec(memory_space=pl.ANY)
    whole = lambda *dims: pl.BlockSpec(dims, lambda g: (0,) * len(dims))
    col = lambda n: pl.BlockSpec((n, 128), lambda g: (0, g))
    shape = jax.ShapeDtypeStruct
    size = 4 * width // 32
    outs = [shape((16, size, width), BF16), shape((16 * size + 16, width), BF16), shape((2 * count, width), F32), shape((2 * count + 16, width), BF16)]
    given = (hid_l, hid_r, near, near_other, far, far_other, wq, wk, wv)
    return pl.pallas_call(
        back_kernel,
        grid=(width // 128,),
        in_specs=[smem, col(count), col(count)] + [col(2 * count)] * 7 + [pl.BlockSpec((2, 2 * count, 4 * count), lambda g: (g, 0, 0)),
                  whole(*buckets.shape), whole(8, width), whole(8, width)] + [free] * 10,
        out_specs=[free] * 4 + [whole(8, width)],
        out_shape=outs + [shape((8, width), F32)],
        scratch_shapes=[pltpu.VMEM(g.shape, BF16) for g in given] + [pltpu.VMEM((4 * width, width), BF16)]
                       + [pltpu.VMEM(o.shape, o.dtype) for o in outs]
                       + [pltpu.VMEM((2 * count, width), BF16), pltpu.VMEM((4 * count, width), BF16), pltpu.VMEM((4 * count, width), BF16),
                          pltpu.VMEM((8, 2048), F32), pltpu.VMEM((2, 6, 128, 384), F32), pltpu.VMEM((2, 128, 2048), F32),
                          pltpu.VMEM((2, 2 * count, 4 * count), BF16), pltpu.SemaphoreType.DMA((14,))],
        name="back", compiler_params=pltpu.CompilerParams(vmem_limit_bytes=44 << 20),
    )(info, ql, qr, kl, kr, vl, vr, gout, out, inv, expo, buckets, dense_rows, through_rows, *given, grad_out)

def ending_kernel(info, stay, came, near, far, grad_mixed, gain, dense_rows, home, away):
    count, width = near.shape
    for part, raw in enumerate((near, far)):
        spot = slice(part * count, (part + 1) * count)
        tokens = raw[...].astype(F32)
        grad = stay[spot, :] + came[spot, :].astype(F32)
        more, _ = norm_back(grad, tokens, rms_scale(tokens), gain[...])
        value = (grad_mixed[spot, :] + more).astype(BF16)
        if part == 0:
            home[:count, :] = value
        else:
            away[:count, :] = value
    alive = (info[0] - info[5]).astype(F32)
    pool = two_terms((rows_of(dense_rows[0:1, :]) + one_value(came[2 * count :, :])) / alive)
    home[count:, :] = pool
    away[count:, :] = pool

def ending(info, stay, came, near, far, grad_mixed, gain, dense_rows):
    count, width = near.shape
    smem, vmem = pl.BlockSpec(memory_space=pltpu.SMEM), pl.BlockSpec(memory_space=pltpu.VMEM)
    shape = jax.ShapeDtypeStruct((count + 16, width), BF16)
    return pl.pallas_call(
        ending_kernel, in_specs=[smem] + [vmem] * 7, out_specs=[vmem] * 2, out_shape=[shape, shape], name="ending", compiler_params=pltpu.CompilerParams(vmem_limit_bytes=10 << 20)
    )(info, stay, came, near, far, grad_mixed, gain, dense_rows)

def place_kernel(firsts, info, *refs):
    parts, (back, front, rows, columns, sems) = refs[: len(firsts)], refs[-5:]
    mine = info[6] & 15
    for side in range(2):
        @pl.when(info[7] == side)
        def _(side=side):
            copies, n = [], 0
            for part, first in zip(parts, firsts):
                for i in range(part.shape[0]):
                    r = first + i
                    to = pl.ds(pl.multiple_of(((r & 15) ^ mine) * 128, 128), 128)
                    if (r >= 16) == (side == 1):
                        for q in range(4):
                            rows[n, :, q * 128 : (q + 1) * 128] = part[i, q * 128 : (q + 1) * 128, :].astype(F32)
                        copies.append(pltpu.make_async_copy(rows.at[n], back.at[to, :], sems.at[n]))
                    else:
                        columns[n] = part[i].astype(F32)
                        copies.append(pltpu.make_async_copy(columns.at[n], front.at[:, to], sems.at[n]))
                    copies[-1].start()
                    n += 1
            for copy in copies:
                copy.wait()

def place(info, parts, made, width):
    smem, vmem, far = (pl.BlockSpec(memory_space=m) for m in (pltpu.SMEM, pltpu.VMEM, pltpu.HBM))
    shape = jax.ShapeDtypeStruct
    count = sum(p.shape[0] for _, p in parts)
    return pl.pallas_call(
        functools.partial(place_kernel, [first for first, _ in parts]),
        in_specs=[smem] + [vmem] * len(parts) + [far] * len(made),
        out_specs=[far] * 2,
        out_shape=[shape((16 * 128, width), F32), shape((width, 16 * 128), F32)],
        scratch_shapes=[pltpu.VMEM((count, 128, width), F32), pltpu.VMEM((count, width, 128), F32), pltpu.SemaphoreType.DMA((count,))],
        input_output_aliases={1 + len(parts) + i: i for i in range(len(made))},
        name="place", compiler_params=pltpu.CompilerParams(vmem_limit_bytes=24 << 20),
    )(info, *[p for _, p in parts], *made)

def sort_kernel(firsts, info, *refs):
    parts, made, (tall, sems) = refs[: len(firsts)], refs[-6:-2], refs[-2:]
    size = parts[0].shape[1]
    mine = info[6]
    pieces = []
    for part, first in zip(parts, firsts):
        for i in range(part.shape[0]):
            tall[len(pieces)] = part[i].astype(F32)
            pieces.append(first + i)
    for top in range(4):
        @pl.when((mine >> 3) == top)
        def _(top=top):
            copies = []
            for n, r in enumerate(pieces):
                to = pl.ds(pl.multiple_of(((r ^ mine) & 7) * size, size), size)
                copies.append(pltpu.make_async_copy(tall.at[n], made[top ^ (r >> 3)].at[to, :], sems.at[n]))
                copies[-1].start()
            for copy in copies:
                copy.wait()

def sort(info, parts, made, width):
    smem, vmem, far = (pl.BlockSpec(memory_space=m) for m in (pltpu.SMEM, pltpu.VMEM, pltpu.HBM))
    shape = jax.ShapeDtypeStruct((width, width), F32)
    count = sum(p.shape[0] for _, p in parts)
    return pl.pallas_call(
        functools.partial(sort_kernel, [first for first, _ in parts]),
        in_specs=[smem] + [vmem] * len(parts) + [far] * len(made),
        out_specs=[far] * 4,
        out_shape=[shape] * 4,
        scratch_shapes=[pltpu.VMEM((count,) + parts[0][1].shape[1:], F32), pltpu.SemaphoreType.DMA((count,))],
        input_output_aliases={1 + len(parts) + i: i for i in range(len(made))},
        name="sort", compiler_params=pltpu.CompilerParams(vmem_limit_bytes=12 << 20),
    )(info, *[p for _, p in parts], *made)

def mix_kernel(*refs):
    for k in range(4):
        refs[4 + k][...] = added(*[term[k] for term in refs[:4]])

def mix(terms):
    block = terms[0].shape[1:]
    vmem = pl.BlockSpec(memory_space=pltpu.VMEM)
    return pl.pallas_call(
        mix_kernel, in_specs=[vmem] * 4, out_specs=[vmem] * 4, out_shape=[jax.ShapeDtypeStruct(block, BF16)] * 4, name="mix", compiler_params=pltpu.CompilerParams(vmem_limit_bytes=10 << 20),
    )(*terms)

def exchange(value, bits):
    size = lax.axis_size("dp") * lax.axis_size("blk")
    return lax.ppermute(value, ("dp", "blk"), [(i, i ^ bits) for i in range(size)])

def wait(*values):
    return lax.optimization_barrier(values)

def added(*terms):
    total = terms[0].astype(F32)
    for term in terms[1:]:
        total = total + term.astype(F32)
    return total.astype(BF16)

def local(inputs, w_query, w_key, w_value, w_out, w_in, w_back, norm1_gain, norm2_gain, final_gain, bias_table, bucket_table, prefix_len, pad_len, pooled_grad):
    rows, width = inputs.shape[1:]
    spot, far_off = lax.axis_index("blk"), lax.axis_index("dp")
    doc, core = spot // 2, spot % 2
    block = [doc * 2 + core, doc * 2 + 1 - core, (1 - doc) * 2 + core, (1 - doc) * 2 + 1 - core]
    line = [8, 16]
    further = [32 << b for b in range((lax.axis_size("dp") // 8).bit_length() - 1)]
    piece = core * 16 + doc * 4 + (far_off % 2) * 8 + (far_off // 2) % 4
    near = jnp.where(doc == 0, inputs[0], inputs[1])
    far_send = jnp.where(doc == 0, inputs[1], inputs[0])
    near, far_send = wait(near, far_send)
    far = exchange(far_send, ROW)
    near_other = exchange(near, CORE)
    slot = jnp.arange(8, dtype=jnp.int32)
    ids = jnp.zeros_like(slot)
    for i, value in enumerate([b * rows for b in block] + [piece, core, doc]):
        ids = jnp.where(slot == i, value, ids)
    gain1, gain2, gain3 = norm1_gain[None, :], norm2_gain[None, :], final_gain[None, :]
    buckets = bucket_table[None, :]
    hid_l, q_l, k_l, v_l, w_query, w_key, w_value = prepare(near, near_other, gain1, w_query, w_key, w_value)
    far, q_l, ids = wait(far, q_l, ids)
    far_other = exchange(far, CORE)
    lines, info = tables(ids, pad_len, prefix_len, bias_table.T, buckets, 4 * rows)
    (hid_r, q_r, k_r, v_r, expo, inverse, attended, send, active, slopes, turned, mixed, steep, dense_rows) = front(
        info, far, far_other, near, q_l, k_l, v_l, lines, w_query, w_key, w_value,
        gain1, gain2, gain3, pooled_grad, w_out, w_in, w_back)

    xy = [ROW, NEAR_X, ROW ^ NEAR_X]
    zz = [line[0], line[1], line[0] ^ line[1]]

    token, send = wait(info, send)
    got = exchange(send, CORE)
    grad_mixed, grad_attended, grad_out_w, through_rows = through(token, slopes, w_in, mixed, steep, w_out, attended, gain2)
    token, through_rows, got = wait(token, through_rows, got)
    stays, *sends = meet(token, got, active, slopes, turned, steep)

    token, sends = wait(token, sends)
    came = [exchange(s, m) for s, m in zip(sends, xy)]
    rest_keep, rest_send, stay, leave, small = back(
        token, q_l, q_r, k_l, k_r, v_l, v_r, grad_attended, attended, inverse, expo, buckets, dense_rows, through_rows,
        hid_l, hid_r, near, near_other, far, far_other, w_query, w_key, w_value, grad_out_w)
    token, small, rest_send, leave, came = wait(token, small, rest_send, leave, came)

    rest_got = exchange(rest_send, CORE)
    hidden_got = exchange(leave, CORE)
    lines = mix([stays] + list(came))
    token, lines = wait(token, lines)
    took = [exchange(lines[k + 1], m) for k, m in enumerate(zz)]
    token, rest_got, hidden_got = wait(token, rest_got, hidden_got)

    count = rest_keep.shape[0] * rest_keep.shape[1]
    small = small + one_value(rest_got[count:])
    rest_got = rest_got[:count].reshape(rest_keep.shape)
    terms = two_terms(small)
    sends = [jnp.concatenate([added(rest_keep[4 * k : 4 * k + 4], rest_got[4 * k : 4 * k + 4]).reshape(-1, width), terms]) for k in (1, 2, 3)]
    token, sends = wait(token, sends)
    rest_came = [exchange(s, m) for s, m in zip(sends, xy)]
    home, away = ending(token, stay, hidden_got, near, far, grad_mixed, gain1, dense_rows)
    token, took, away = wait(token, took, away)

    whole = added(lines[0], *took)
    for bit in further:
        whole = added(whole, exchange(whole, bit))
    token, whole = wait(token, whole)
    back_line = [exchange(whole, m) for m in zz]
    away_got = exchange(away, ROW)
    token, rest_came = wait(token, rest_came)

    count = count // 4
    for part in rest_came:
        small = small + one_value(part[count:])
    rest_came = [part[:count].reshape((4,) + rest_keep.shape[1:]) for part in rest_came]
    piece = count // 4
    lines = added(rest_keep[:4], rest_got[:4], *rest_came).reshape(-1, width)
    send = jnp.concatenate([lines[piece : 2 * piece], lines[3 * piece :], two_terms(small)])
    token, send = wait(token, send)
    took = exchange(send, line[0])
    token, took = wait(token, took)
    small = small + one_value(took[2 * piece :])
    send = jnp.concatenate([added(lines[2 * piece : 3 * piece], took[piece : 2 * piece]), two_terms(small)])
    lines = added(lines[:piece], took[:piece])
    token, send, back_line, away_got = wait(token, send, back_line, away_got)
    took = exchange(send, line[1])

    quarter = jnp.stack([whole] + back_line)
    token, quarter = wait(token, quarter)
    from_y, from_x = exchange(quarter, ROW), exchange(quarter, NEAR_X)
    pool_mine, pool_other = one_value(home[rows:])[:1], one_value(away_got[rows:])[:1]
    pooled = jnp.where(doc == 0, jnp.concatenate([pool_mine, pool_other]), jnp.concatenate([pool_other, pool_mine]))
    home, away_got = home[:rows], away_got[:rows]
    input_grad = jnp.where(doc == 0, jnp.stack([home, away_got]), jnp.stack([away_got, home]))
    token, took, pooled, input_grad = wait(token, took, pooled, input_grad)

    small = small + one_value(took[piece:])
    rest = added(lines, took[:piece])
    for bit in further:
        rest = added(rest, exchange(rest, bit))
        small = small + exchange(small, bit)
    token, rest = wait(token, rest)
    rest_back = [exchange(rest, m) for m in zz]
    outs = [small[0], small[1], small[2], small[3, : bias_table.size].reshape(bias_table.shape[::-1]).T]
    token, from_y, from_x, outs = wait(token, from_y, from_x, outs)

    sends = [from_x[:2], from_y[2:]]
    token, sends, rest_back = wait(token, sends, rest_back)
    far_a, far_b = exchange(sends[0], ROW), exchange(sends[1], NEAR_X)
    fourth = jnp.stack([rest] + rest_back)
    token, fourth, quarter = wait(token, fourth, quarter)
    fourth_y, fourth_x = exchange(fourth, ROW), exchange(fourth, NEAR_X)
    other = exchange(quarter, CORE)
    near_pair = jnp.concatenate([from_y, from_x])
    grads = place(token, [(0, quarter), (4, from_y), (8, from_x)], [], width)
    token, grads, other, near_pair, far_a, far_b, fourth_y, fourth_x = wait(token, grads, other, near_pair, far_a, far_b, fourth_y, fourth_x)

    sends = [fourth_x[:2], fourth_y[2:], near_pair, jnp.concatenate([far_a, far_b]), jnp.concatenate([fourth, fourth_y, fourth_x])]
    token, sends = wait(token, sends)
    last_a, last_b, other_near, other_far, pair = (exchange(s, m) for s, m in zip(sends, (ROW, NEAR_X, CORE, CORE, CORE)))
    grads = place(token, [(12, far_a), (14, far_b), (16, other)], grads, width)
    token, grads, other_near, other_far = wait(token, grads, other_near, other_far)
    out_back, out_in = place(token, [(20, other_near), (28, other_far)], grads, width)
    token, out_back, out_in, last_a, last_b, pair = wait(token, out_back, out_in, last_a, last_b, pair)

    ends = exchange(jnp.concatenate([last_a, last_b]), CORE)
    made = sort(token, [(0, fourth), (4, fourth_y), (8, fourth_x), (12, last_a), (14, last_b), (16, pair)], [], width)
    token, made, ends = wait(token, made, ends)
    out_out, out_query, out_key, out_value = sort(token, [(28, ends)], made, width)
    return (pooled, input_grad, out_query, out_key, out_value, out_out, out_in, out_back, *outs)

def solution(mesh):
    data = P("dp", "blk", None)
    placed = (data,) + (P(),) * 11 + (P("dp"), P("dp"), P("dp", None))
    return jax.shard_map(local, mesh=mesh, in_specs=placed, out_specs=(P("dp", None), data) + (P(),) * 10, check_vma=False)
```

```python
import functools
import jax, jax.numpy as jnp
from jax import lax
from jax.experimental import pallas as pl
from jax.experimental.pallas import tpu as pltpu
from jax.sharding import PartitionSpec as P

F32, BF16 = jnp.float32, jnp.bfloat16
NEG = -1000000000.0
NT = (((1,), (1,)), ((), ()))
TN = (((0,), (0,)), ((), ()))
NN = (((1,), (0,)), ((), ()))

def dot(a, b, dims=NN):
    return lax.dot_general(a, b, dims, preferred_element_type=F32)

def skew(row, width, dtype=F32):
    return pltpu.roll(jnp.broadcast_to(row, (128, width)), width - 127, 1, stride=1, stride_axis=0)


BUCKETS = 32
EPS = 1e-06
CORE, ROW, NEAR_X = 1, 2, 4

def rms_scale(values):
    return lax.rsqrt(jnp.mean(values * values, axis=-1, keepdims=True) + EPS)

def norm_back(grad_out, values, scale, gain):
    weighted = grad_out * gain
    inner = jnp.mean(weighted * values, axis=-1, keepdims=True)
    grad_in = scale * weighted - scale * scale * scale * values * inner
    return grad_in, jnp.sum(grad_out * values * scale, axis=0, keepdims=True)

def two_terms(value):
    high = value.astype(BF16)
    return jnp.concatenate([high, (value - high.astype(F32)).astype(BF16)])

def one_value(terms):
    return terms[:8].astype(F32) + terms[8:16].astype(F32)

def rows_of(*values):
    count = sum(v.shape[0] for v in values)
    return jnp.concatenate(list(values) + [jnp.zeros((8 - count, values[0].shape[1]), F32)])

def prepare_kernel(mine, other, gain, wq_h, wk_h, wv_h, hidden, query, keys, values, wq, wk, wv, sems):
    rows = mine.shape[0]
    load = [pltpu.make_async_copy(a, b, sems.at[i]) for i, (a, b) in enumerate(((wk_h, wk), (wv_h, wv), (wq_h, wq)))]
    for copy in load:
        copy.start()
    for part, raw in enumerate((mine, other)):
        tokens = raw[...].astype(F32)
        hidden[part * rows : (part + 1) * rows, :] = (tokens * rms_scale(tokens) * gain[...]).astype(BF16)
    h = hidden[...]
    load[0].wait()
    keys[...] = dot(h, wk[...]).astype(BF16)
    load[1].wait()
    values[...] = dot(h, wv[...]).astype(BF16)
    load[2].wait()
    query[...] = dot(h[:rows], wq[...]).astype(BF16)

def prepare(mine, other, gain, wq, wk, wv):
    rows, width = mine.shape
    shape = lambda n: jax.ShapeDtypeStruct((n, width), BF16)
    vmem, free = (pl.BlockSpec(memory_space=m) for m in (pltpu.VMEM, pl.ANY))
    return pl.pallas_call(
        prepare_kernel,
        in_specs=[vmem] * 3 + [free] * 3,
        out_specs=[vmem] * 7,
        out_shape=[shape(2 * rows), shape(rows), shape(2 * rows), shape(2 * rows)] + [shape(width)] * 3,
        scratch_shapes=[pltpu.SemaphoreType.DMA((3,))],
        name="prepare", compiler_params=pltpu.CompilerParams(vmem_limit_bytes=14 << 20),
    )(mine, other, gain, wq, wk, wv)

def tables_kernel(ids, pads, prefixes, bias, buckets, lines, info, *, length):
    doc = ids[6]
    info[0] = length - jnp.where(doc == 0, pads[0], pads[1])
    info[5] = jnp.where(doc == 0, prefixes[0], prefixes[1])
    for to, at in enumerate((0, 1, 2, 3)):
        info[1 + to] = ids[at]
    for to, at in enumerate((4, 5, 6)):
        info[6 + to] = ids[at]
    picker = jnp.where(lax.broadcasted_iota(jnp.int32, (BUCKETS, 1), 0) == buckets[...], 1.0, 0.0).astype(BF16)
    left, total = bias[...], None
    for _ in range(3):
        part = left.astype(BF16)
        left = left - part.astype(F32)
        made = dot(part, picker)
        total = made if total is None else total + made
    lines[...] = jnp.zeros_like(lines)
    lines[:, : buckets.shape[1]] = total

def tables(ids, pads, prefixes, bias, buckets, length):
    smem, vmem = pl.BlockSpec(memory_space=pltpu.SMEM), pl.BlockSpec(memory_space=pltpu.VMEM)
    return pl.pallas_call(
        functools.partial(tables_kernel, length=length),
        in_specs=[smem] * 3 + [vmem] * 2,
        out_specs=[vmem, smem],
        out_shape=[jax.ShapeDtypeStruct((bias.shape[0], buckets.shape[1] + 1), F32), jax.ShapeDtypeStruct((16,), jnp.int32)],
        name="tables", compiler_params=pltpu.CompilerParams(vmem_limit_bytes=4 << 20),
    )(ids, pads, prefixes, bias, buckets)

def back_pieces(to, active, low, mine):
    @pl.loop(0, active.shape[1] // 512)
    def _(group):
        made = dot(active[:, pl.ds(pl.multiple_of(group * 512, 512), 512)], low, TN).astype(BF16)
        for b in range(4):
            rows = made[b * 128 : (b + 1) * 128]
            to[(4 * group + b) ^ mine] = jnp.concatenate([rows[:, q * 128 : (q + 1) * 128] for q in range(4)])

def in_pieces(to, slopes, turned, mine):
    @pl.loop(0, slopes.shape[1] // 512)
    def _(group):
        made = dot(turned, slopes[:, pl.ds(pl.multiple_of(group * 512, 512), 512)]).astype(BF16)
        for b in range(4):
            to[(4 * group + b) ^ mine] = made[:, b * 128 : (b + 1) * 128]

def front_kernel(info, far, far_other, near, q_l, k_l, v_l, lines, wq, wk, wv, gain1, gain2, gain3, cots, wo_h, win_h, wback_h,
                 hid_o, q_o, k_o, v_o, expo_o, inv_o, att_o, send_o, active_o, slopes_o, turned_o, mixed_o, steep_o, rows,
                 hid, qs, ks, vs, inv, att, send, active, slopes, turned, mixed, steep, wo, win, wback, expo, scores, skewed, edges, sems):
    count, width = near.shape
    hidden = win.shape[1]
    step = pl.program_id(0)
    late = [pltpu.make_async_copy(a, b, sems.at[i]) for i, (a, b) in enumerate(((wo_h, wo), (win_h, win), (wback_h, wback)))]
    early = [pltpu.make_async_copy(a, b, sems.at[3 + i]) for i, (a, b) in enumerate(((hid, hid_o), (qs, q_o), (ks, k_o), (vs, v_o)))]
    dense = [pltpu.make_async_copy(a, b, sems.at[7 + i]) for i, (a, b) in enumerate((
        (inv, inv_o), (att, att_o), (mixed, mixed_o), (turned, turned_o), (active, active_o), (steep, steep_o), (slopes, slopes_o), (send, send_o)))]
    kept = lambda g: pltpu.make_async_copy(expo, expo_o.at[pl.ds(2 * g, 2)], sems.at[15])

    @pl.when(step == 0)
    def _():
        for copy in late:
            copy.start()
        for part, raw in enumerate((far, far_other)):
            tokens = raw[...].astype(F32)
            hid[part * count : (part + 1) * count, :] = (tokens * rms_scale(tokens) * gain1[...]).astype(BF16)
        h = hid[...]
        qs[...] = dot(h[:count], wq[...]).astype(BF16)
        ks[...] = dot(h, wk[...]).astype(BF16)
        vs[...] = dot(h, wv[...]).astype(BF16)
        for copy in early:
            copy.start()
        column = lax.broadcasted_iota(jnp.int32, (1, 128), 1)
        for b in range(4):
            place = info[1 + b] + lax.broadcasted_iota(jnp.int32, (count, 1), 0)
            gate = jnp.where(place < info[0], 0.0, NEG)
            for head in range(2):
                edges[head, b * count : (b + 1) * count, :] = jnp.where(column == (64 if head == 0 else 0), gate, 0.0).astype(BF16)

    @pl.when(step > 0)
    def _():
        kept(step - 1).wait()

    cols = pl.ds(pl.multiple_of(step * 128, 128), 128)
    lane = lax.broadcasted_iota(jnp.int32, (1, 128), 1)
    first = lane < 64
    limit = info[0]
    starts = [info[1 + b] for b in range(4)]
    keys = [k_l[:count, :], k_l[count:, :], ks[:count, cols], ks[count:, cols]]
    values = jnp.concatenate([v_l[...], vs[:, cols]])
    query = jnp.concatenate([q_l[...], qs[:, cols]])
    made = []
    for head in range(2):
        mine = jnp.where(first if head == 0 else lane >= 64, 1.0, 0.0).astype(BF16)
        one = jnp.where(lane == (64 if head == 0 else 0), 1.0, 0.0).astype(BF16)
        q = query * mine + one
        v = values * mine + one
        skewed[head] = skew(lines[pl.ds(2 * step + head, 1), :], lines.shape[1])
        k = jnp.concatenate(keys) * mine + edges[head]
        for half in range(2):
            s = dot(q[half * 256 : (half + 1) * 256], k, NT)
            for r in range(2):
                for b in range(4):
                    at = starts[b] - starts[2 * half] + 896 - 128 * r
                    part = s[r * 128 : (r + 1) * 128, b * 256 : (b + 1) * 256] + skewed[head, :, pl.ds(pl.multiple_of(at, 128), 256)]
                    scores[head, half * 256 + r * 128 : half * 256 + (r + 1) * 128, b * 256 : (b + 1) * 256] = part
        accs = []
        for r in range(4):
            rs = slice(r * 128, (r + 1) * 128)
            value = scores[head, rs, :]
            top = jnp.max(value, axis=1, keepdims=True)
            e = jnp.exp(value - top).astype(BF16)
            expo[head, rs, :] = e
            accs.append(dot(e, v))
        acc = jnp.concatenate(accs)
        made.append((acc, 1.0 / (acc[:, 64:65] if head == 0 else acc[:, 0:1])))
    (a0, i0), (a1, i1) = made
    scale = jnp.where(first, i0, i1)
    att[:, cols] = (jnp.where(first, a0, a1) * scale).astype(BF16)
    inv[:, cols] = scale
    kept(step).start()

    @pl.when(step == 3)
    def _():
        for copy in late:
            copy.wait()
        dense[0].start()
        dense[1].start()
        for part, raw in enumerate((near, far)):
            spot = slice(part * count, (part + 1) * count)
            mixed[spot, :] = raw[...].astype(F32) + dot(att[spot, :], wo[...])
        dense[2].start()
        values = mixed[...]
        inner = (values * rms_scale(values) * gain2[...]).astype(BF16)
        turned[...] = inner.T
        dense[3].start()
        total = values
        for at in range(0, hidden, 512):
            lifted = jnp.maximum(dot(inner, win[:, at : at + 512]), 0.0).astype(BF16)
            active[:, at : at + 512] = lifted
            total = total + dot(lifted, wback[at : at + 512, :])
        dense[4].start()
        scale = rms_scale(total)
        place = lax.broadcasted_iota(jnp.int32, (2 * count, 1), 0)
        place = jnp.where(place < count, place + info[1], place + (info[3] - count))
        live = jnp.where((place >= info[5]) & (place < limit), 1.0, 0.0)
        pool = jnp.sum(total * scale * gain3[...] * live, axis=0, keepdims=True)
        cot = jnp.where(info[8] == 0, cots[0:1, :], cots[1:2, :]) / (limit - info[5]).astype(F32)
        slope, grad_end = norm_back(live * cot, total, scale, gain3[...])
        steep[...] = slope
        dense[5].start()
        rows[...] = jnp.concatenate([pool, grad_end, jnp.zeros((6, width), F32)])
        low = slope.astype(BF16)
        for at in range(0, hidden, 512):
            through = dot(low, wback[at : at + 512, :], NT).astype(BF16)
            slopes[:, at : at + 512] = jnp.where(active[:, at : at + 512] > 0, through, jnp.zeros_like(through))
        dense[6].start()
        mine = info[6] & 15

        @pl.when(info[7] == 0)
        def _():
            in_pieces(send, slopes, turned[...], mine)

        @pl.when(info[7] == 1)
        def _():
            back_pieces(send, active, steep[...].astype(BF16), mine)

        dense[7].start()
        for copy in early + dense:
            copy.wait()
        kept(step).wait()

def front(info, far, far_other, near, q_l, k_l, v_l, lines, wq, wk, wv, gain1, gain2, gain3, cots, wo, win, wback):
    count, width = near.shape
    hidden = win.shape[1]
    heads, span = lines.shape
    shape = jax.ShapeDtypeStruct
    smem, free = pl.BlockSpec(memory_space=pltpu.SMEM), pl.BlockSpec(memory_space=pl.ANY)
    whole = lambda *dims: pl.BlockSpec(dims, lambda g: (0,) * len(dims))
    col = lambda n: pl.BlockSpec((n, 128), lambda g: (0, g))
    outs = [shape((2 * count, width), BF16), shape((count, width), BF16), shape((2 * count, width), BF16), shape((2 * count, width), BF16),
            shape((heads, 2 * count, 4 * count), BF16), shape((2 * count, width), F32), shape((2 * count, width), BF16),
            shape((16, width, 128), BF16), shape((2 * count, hidden), BF16), shape((2 * count, hidden), BF16),
            shape((width, 2 * count), BF16), shape((2 * count, width), F32), shape((2 * count, width), F32)]
    return pl.pallas_call(
        front_kernel,
        grid=(heads // 2,),
        in_specs=[smem] + [whole(count, width)] * 3 + [col(count), col(2 * count), col(2 * count), whole(heads, span)] + [whole(width, width)] * 3 + [whole(1, width)] * 3
                 + [whole(2, width)] + [pl.BlockSpec(memory_space=pltpu.HBM)] * 3,
        out_specs=[free] * 13 + [whole(8, width)],
        out_shape=outs + [shape((8, width), F32)],
        scratch_shapes=[pltpu.VMEM(o.shape, o.dtype) for o in outs[:4] + outs[5:]]
                       + [pltpu.VMEM(wo.shape, BF16), pltpu.VMEM(win.shape, BF16), pltpu.VMEM(wback.shape, BF16),
                          pltpu.VMEM((2, 2 * count, 4 * count), BF16), pltpu.VMEM((2, 2 * count, 4 * count), F32),
                          pltpu.VMEM((2, 128, span), F32), pltpu.VMEM((2, 4 * count, 128), BF16), pltpu.SemaphoreType.DMA((16,))],
        name="front", compiler_params=pltpu.CompilerParams(vmem_limit_bytes=36 << 20),
    )(info, far, far_other, near, q_l, k_l, v_l, lines, wq, wk, wv, gain1, gain2, gain3, cots, wo, win, wback)

def through_kernel(info, slopes_h, win_h, mixed_h, steep_h, wo_h, att_h, gain2, grad_mixed_o, grad_attended_o, grad_out_o, rows,
                   slopes, win, mixed, steep, wo, att, grad_mixed, grad_attended, grad_out, sems):
    hidden, width = slopes.shape[1], mixed.shape[1]
    chunks = []
    for i, at in enumerate(range(0, hidden, 512)):
        for a, b, s in ((slopes_h, slopes, i), (win_h, win, 4 + i)):
            chunks.append(pltpu.make_async_copy(a.at[:, at : at + 512], b.at[:, at : at + 512], sems.at[s]))
    copies = [pltpu.make_async_copy(a, b, sems.at[8 + i]) for i, (a, b) in enumerate((
        (mixed_h, mixed), (steep_h, steep), (wo_h, wo), (att_h, att)))]
    outs = [pltpu.make_async_copy(a, b, sems.at[12 + i]) for i, (a, b) in enumerate((
        (grad_mixed, grad_mixed_o), (grad_attended, grad_attended_o), (grad_out, grad_out_o)))]
    for copy in chunks + copies:
        copy.start()
    grad_inner = None
    for i, at in enumerate(range(0, hidden, 512)):
        chunks[2 * i].wait()
        chunks[2 * i + 1].wait()
        part = dot(slopes[:, at : at + 512], win[:, at : at + 512], NT)
        grad_inner = part if grad_inner is None else grad_inner + part
    copies[0].wait()
    copies[1].wait()
    values = mixed[...]
    more, grad_two = norm_back(grad_inner, values, rms_scale(values), gain2[...])
    total = steep[...] + more
    grad_mixed[...] = total
    outs[0].start()
    low = total.astype(BF16)
    copies[2].wait()
    grad_attended[...] = dot(low, wo[...], NT).astype(BF16)
    outs[1].start()
    copies[3].wait()
    grad_out[...] = dot(att[...], low, TN).astype(BF16)
    outs[2].start()
    rows[...] = jnp.concatenate([grad_two, jnp.zeros((7, width), F32)])
    for copy in outs:
        copy.wait()

def through(info, slopes, win, mixed, steep, wo, att, gain2):
    n, width = mixed.shape
    smem, vmem, free = (pl.BlockSpec(memory_space=m) for m in (pltpu.SMEM, pltpu.VMEM, pl.ANY))
    shape = jax.ShapeDtypeStruct
    given = (slopes, win, mixed, steep, wo, att)
    outs = [shape((n, width), F32), shape((n, width), BF16), shape((width, width), BF16)]
    return pl.pallas_call(
        through_kernel,
        in_specs=[smem, free, pl.BlockSpec(memory_space=pltpu.HBM)] + [free] * 4 + [vmem],
        out_specs=[free] * 3 + [vmem],
        out_shape=outs + [shape((8, width), F32)],
        scratch_shapes=[pltpu.VMEM(g.shape, g.dtype) for g in given] + [pltpu.VMEM(o.shape, o.dtype) for o in outs] + [pltpu.SemaphoreType.DMA((15,))],
        name="through", compiler_params=pltpu.CompilerParams(vmem_limit_bytes=16 << 20),
    )(info, *given, gain2)

def meet_kernel(info, got_h, active_h, slopes_h, turned_h, steep_h, *refs):
    outs, (got, chunk, turned, steep, blocks, sems) = refs[:4], refs[4:]
    order = (3, 1, 2, 0)
    high, lowest = (info[6] & 15) >> 2, info[6] & 3
    load = [pltpu.make_async_copy(got_h.at[4 * k : 4 * k + 4], got.at[k], sems.at[k]) for k in range(4)]
    save = [pltpu.make_async_copy(blocks.at[k], outs[k], sems.at[4 + k]) for k in range(4)]

    def columns(source, k):
        at = pl.ds(pl.multiple_of((k ^ high) * 512, 512), 512)
        return pltpu.make_async_copy(source.at[:, at], chunk.at[k], sems.at[8 + k])

    for side, source in ((0, active_h), (1, slopes_h)):
        @pl.when(info[7] == side)
        def _(side=side, source=source):
            extra = pltpu.make_async_copy(*((steep_h, steep) if side == 0 else (turned_h, turned)), sems.at[12])
            extra.start()
            for k in order:
                columns(source, k).start()
                load[k].start()
            extra.wait()
            low = steep[...].astype(BF16) if side == 0 else turned[...]
            for k in order:
                columns(source, k).wait()
                made = dot(chunk[k], low, TN) if side == 0 else dot(low, chunk[k])
                load[k].wait()
                for b in range(4):
                    piece = made[:, b * 128 : (b + 1) * 128]
                    if side == 0:
                        piece = made[b * 128 : (b + 1) * 128]
                        piece = jnp.concatenate([piece[:, q * 128 : (q + 1) * 128] for q in range(4)])
                    to = b ^ lowest
                    blocks[k, to] = (piece + got[k, to].astype(F32)).astype(BF16)
                save[k].start()

    for copy in save:
        copy.wait()

def meet(info, got, active, slopes, turned, steep):
    smem, free = pl.BlockSpec(memory_space=pltpu.SMEM), pl.BlockSpec(memory_space=pl.ANY)
    block = (4,) + got.shape[1:]
    n, width = steep.shape
    return pl.pallas_call(
        meet_kernel,
        in_specs=[smem] + [free] * 5,
        out_specs=[free] * 4,
        out_shape=[jax.ShapeDtypeStruct(block, BF16)] * 4,
        scratch_shapes=[pltpu.VMEM((4,) + block, BF16), pltpu.VMEM((4, n, 512), BF16), pltpu.VMEM(turned.shape, BF16), pltpu.VMEM(steep.shape, F32),
                        pltpu.VMEM((4,) + block, BF16), pltpu.SemaphoreType.DMA((13,))],
        name="meet", compiler_params=pltpu.CompilerParams(vmem_limit_bytes=20 << 20),
    )(info, got, active, slopes, turned, steep)

CLASS = {(0, 0): 0, (1, 2): 0, (0, 1): 1, (1, 3): 1, (0, 2): 2, (0, 3): 3, (1, 0): 4, (1, 1): 5}

def back_kernel(info, ql, qr, kl, kr, vl, vr, gout, out, inv, expo, buckets, dense_rows, through_rows,
                hid_l_h, hid_r_h, near_h, near_other_h, far_h, far_other_h, wq_h, wk_h, wv_h, grad_out_h,
                keep_o, send_o, stay_o, leave_o, small,
                hid_l, hid_r, near, near_other, far, far_other, wq, wk, wv, made,
                keep, send, stay, leave, dq, dk, dv, offsets, sums, acc, slopes, sems):
    count, width = near.shape
    step = pl.program_id(0)
    pairs = width // 128
    late = [pltpu.make_async_copy(a, b, sems.at[i]) for i, (a, b) in enumerate((
        (hid_l_h, hid_l), (hid_r_h, hid_r), (near_h, near), (near_other_h, near_other), (far_h, far), (far_other_h, far_other),
        (wq_h, wq), (wk_h, wk), (wv_h, wv), (grad_out_h, made.at[0:width])))]
    done = [pltpu.make_async_copy(a, b, sems.at[10 + i]) for i, (a, b) in enumerate(((send, send_o), (keep, keep_o), (leave, leave_o), (stay, stay_o)))]

    @pl.when(step == 0)
    def _():
        for copy in late:
            copy.start()

    cols = pl.ds(pl.multiple_of(step * 128, 128), 128)
    lane = lax.broadcasted_iota(jnp.int32, (1, 128), 1)
    starts = [info[1 + b] for b in range(4)]
    keys = jnp.concatenate([kl[...], kr[...]])
    values = jnp.concatenate([vl[...], vr[...]])
    query = jnp.concatenate([ql[...], qr[...]])
    scaled = gout[...].astype(F32) * inv[...]
    prod = scaled * out[...].astype(F32)
    low = scaled.astype(BF16)
    query_t, low_t = query.T, low.T
    grads_q, grads_k, grads_v = None, [], []
    for head in range(2):
        mine = (lane < 64) if head == 0 else (lane >= 64)
        base = 64 if head == 0 else 0
        pick = jnp.where(mine, 1.0, 0.0).astype(BF16)
        delta = jnp.sum(jnp.where(mine, prod, 0.0), axis=1, keepdims=True)
        high = delta.astype(BF16).astype(F32)
        extra = jnp.where(lane == base, high, jnp.where(lane == base + 1, delta - high, 0.0)).astype(BF16)
        grad = low * pick + extra
        minus = jnp.where((lane == base) | (lane == base + 1), -1.0, 0.0).astype(BF16)
        for b in range(4):
            spot = slice(b * count, (b + 1) * count)
            ds = dot(grad, values[spot] * pick + minus, NT) * expo[head, :, spot].astype(F32)
            slopes[head, :, spot] = ds.astype(BF16)
            for chunk in range(2):
                upper, lower = (ds[chunk * count + r * 128 : chunk * count + (r + 1) * 128] for r in range(2))
                group = CLASS[chunk, b]
                block = jnp.concatenate([lower[:, :128], lower[:, 128:] + upper[:, :128], upper[:, 128:]], axis=1)
                if (chunk, b) in ((1, 2), (1, 3)):
                    block = block + sums[head, group]
                sums[head, group] = block
        part = dot(slopes[head], keys * pick)
        grads_q = part if grads_q is None else grads_q + part
        half = slice(head * 64, (head + 1) * 64)
        grads_k.append(dot(query_t[half], slopes[head]))
        grads_v.append(dot(low_t[half], expo[head]))
    dq[:, cols] = grads_q.astype(BF16)
    dk[:, cols] = jnp.concatenate(grads_k).astype(BF16).T
    dv[:, cols] = jnp.concatenate(grads_v).astype(BF16).T
    for head in range(2):
        acc[head] = jnp.zeros(acc.shape[1:], F32)
        for (chunk, b), group in CLASS.items():
            if (chunk, b) not in ((1, 2), (1, 3)):
                at = starts[b] - starts[2 * chunk] + 768
                to = pl.ds(pl.multiple_of(at, 128), 384)
                acc[head, :, to] += sums[head, group]
        rest = acc[head]
        n = 64
        while n >= 8:
            rest = rest[:n] + pltpu.roll(rest[n:], 2048 - n, 1)
            n //= 2
        line = rest[7:8]
        for r in range(6, -1, -1):
            line = rest[r : r + 1] + pltpu.roll(line, 2047, 1)
        offsets[pl.ds(2 * step + head, 1), :] = pltpu.roll(line, 127, 1)

    @pl.when(step == pairs - 1)
    def _():
        for copy in late:
            copy.wait()
        made[width : 2 * width, :] = (dot(hid_l[:count, :], dq[:count, :], TN) + dot(hid_r[:count, :], dq[count:, :], TN)).astype(BF16)
        for at, grads in ((2 * width, dk), (3 * width, dv)):
            made[at : at + width, :] = (dot(hid_l[...], grads[: 2 * count, :], TN) + dot(hid_r[...], grads[2 * count :, :], TN)).astype(BF16)
        me = info[6]
        size = made.shape[0] // 32

        @pl.loop(0, 16)
        def _(r):
            keep[r] = made[pl.ds(pl.multiple_of((r ^ me) * size, size), size), :]
            send[pl.ds(pl.multiple_of(r * size, size), size), :] = made[pl.ds(pl.multiple_of(((r + 16) ^ me) * size, size), size), :]

        gain = jnp.zeros((1, width), F32)
        for b, raw in enumerate((near, near_other, far, far_other)):
            spot = slice(b * count, (b + 1) * count)
            grad = dot(dk[spot, :], wk[...], NT) + dot(dv[spot, :], wv[...], NT)
            half = slice((b // 2) * count, (b // 2 + 1) * count)
            if b % 2 == 0:
                grad = grad + dot(dq[half, :], wq[...], NT)
                stay[half, :] = grad
            else:
                leave[half, :] = grad.astype(BF16)
            tokens = raw[...].astype(F32)
            gain = gain + jnp.sum(grad * (tokens * rms_scale(tokens)), axis=0, keepdims=True)
        leave[2 * count :, :] = two_terms(rows_of(dense_rows[0:1, :]))
        picker = jnp.where(lax.broadcasted_iota(jnp.int32, (128, 1), 0) == buckets[...], 1.0, 0.0).astype(BF16)
        left = offsets[...][:, : buckets.shape[1]]
        bias = None
        for _ in range(3):
            part = left.astype(BF16)
            left = left - part.astype(F32)
            bias = dot(part, picker, NT) if bias is None else bias + dot(part, picker, NT)
        bias = jnp.concatenate([bias, jnp.zeros((bias.shape[0], width - 128), F32)], axis=1)
        line = bias[0:1]
        for h in range(1, bias.shape[0]):
            line = line + pltpu.roll(bias[h : h + 1], 32 * h, 1)
        total = rows_of(gain, through_rows[0:1, :], dense_rows[1:2, :], line)
        small[...] = total
        send[16 * size :, :] = two_terms(total)
        for copy in done:
            copy.start()
        for copy in done:
            copy.wait()

def back(info, ql, qr, kl, kr, vl, vr, gout, out, inv, expo, buckets, dense_rows, through_rows,
         hid_l, hid_r, near, near_other, far, far_other, wq, wk, wv, grad_out):
    count, width = near.shape
    smem, free = pl.BlockSpec(memory_space=pltpu.SMEM), pl.BlockSpec(memory_space=pl.ANY)
    whole = lambda *dims: pl.BlockSpec(dims, lambda g: (0,) * len(dims))
    col = lambda n: pl.BlockSpec((n, 128), lambda g: (0, g))
    shape = jax.ShapeDtypeStruct
    size = 4 * width // 32
    outs = [shape((16, size, width), BF16), shape((16 * size + 16, width), BF16), shape((2 * count, width), F32), shape((2 * count + 16, width), BF16)]
    given = (hid_l, hid_r, near, near_other, far, far_other, wq, wk, wv)
    return pl.pallas_call(
        back_kernel,
        grid=(width // 128,),
        in_specs=[smem, col(count), col(count)] + [col(2 * count)] * 7 + [pl.BlockSpec((2, 2 * count, 4 * count), lambda g: (g, 0, 0)),
                  whole(*buckets.shape), whole(8, width), whole(8, width)] + [free] * 10,
        out_specs=[free] * 4 + [whole(8, width)],
        out_shape=outs + [shape((8, width), F32)],
        scratch_shapes=[pltpu.VMEM(g.shape, BF16) for g in given] + [pltpu.VMEM((4 * width, width), BF16)]
                       + [pltpu.VMEM(o.shape, o.dtype) for o in outs]
                       + [pltpu.VMEM((2 * count, width), BF16), pltpu.VMEM((4 * count, width), BF16), pltpu.VMEM((4 * count, width), BF16),
                          pltpu.VMEM((8, 2048), F32), pltpu.VMEM((2, 6, 128, 384), F32), pltpu.VMEM((2, 128, 2048), F32),
                          pltpu.VMEM((2, 2 * count, 4 * count), BF16), pltpu.SemaphoreType.DMA((14,))],
        name="back", compiler_params=pltpu.CompilerParams(vmem_limit_bytes=44 << 20),
    )(info, ql, qr, kl, kr, vl, vr, gout, out, inv, expo, buckets, dense_rows, through_rows, *given, grad_out)

def ending_kernel(info, stay, came, near, far, grad_mixed, gain, dense_rows, home, away):
    count, width = near.shape
    for part, raw in enumerate((near, far)):
        spot = slice(part * count, (part + 1) * count)
        tokens = raw[...].astype(F32)
        grad = stay[spot, :] + came[spot, :].astype(F32)
        more, _ = norm_back(grad, tokens, rms_scale(tokens), gain[...])
        value = (grad_mixed[spot, :] + more).astype(BF16)
        if part == 0:
            home[:count, :] = value
        else:
            away[:count, :] = value
    alive = (info[0] - info[5]).astype(F32)
    pool = two_terms((rows_of(dense_rows[0:1, :]) + one_value(came[2 * count :, :])) / alive)
    home[count:, :] = pool
    away[count:, :] = pool

def ending(info, stay, came, near, far, grad_mixed, gain, dense_rows):
    count, width = near.shape
    smem, vmem = pl.BlockSpec(memory_space=pltpu.SMEM), pl.BlockSpec(memory_space=pltpu.VMEM)
    shape = jax.ShapeDtypeStruct((count + 16, width), BF16)
    return pl.pallas_call(
        ending_kernel, in_specs=[smem] + [vmem] * 7, out_specs=[vmem] * 2, out_shape=[shape, shape], name="ending", compiler_params=pltpu.CompilerParams(vmem_limit_bytes=10 << 20)
    )(info, stay, came, near, far, grad_mixed, gain, dense_rows)

def place_kernel(firsts, info, *refs):
    parts, (back, front, rows, columns, sems) = refs[: len(firsts)], refs[-5:]
    mine = info[6] & 15
    for side in range(2):
        @pl.when(info[7] == side)
        def _(side=side):
            copies, n = [], 0
            for part, first in zip(parts, firsts):
                for i in range(part.shape[0]):
                    r = first + i
                    to = pl.ds(pl.multiple_of(((r & 15) ^ mine) * 128, 128), 128)
                    if (r >= 16) == (side == 1):
                        for q in range(4):
                            rows[n, :, q * 128 : (q + 1) * 128] = part[i, q * 128 : (q + 1) * 128, :].astype(F32)
                        copies.append(pltpu.make_async_copy(rows.at[n], back.at[to, :], sems.at[n]))
                    else:
                        columns[n] = part[i].astype(F32)
                        copies.append(pltpu.make_async_copy(columns.at[n], front.at[:, to], sems.at[n]))
                    copies[-1].start()
                    n += 1
            for copy in copies:
                copy.wait()

def place(info, parts, made, width):
    smem, vmem, far = (pl.BlockSpec(memory_space=m) for m in (pltpu.SMEM, pltpu.VMEM, pltpu.HBM))
    shape = jax.ShapeDtypeStruct
    count = sum(p.shape[0] for _, p in parts)
    return pl.pallas_call(
        functools.partial(place_kernel, [first for first, _ in parts]),
        in_specs=[smem] + [vmem] * len(parts) + [far] * len(made),
        out_specs=[far] * 2,
        out_shape=[shape((16 * 128, width), F32), shape((width, 16 * 128), F32)],
        scratch_shapes=[pltpu.VMEM((count, 128, width), F32), pltpu.VMEM((count, width, 128), F32), pltpu.SemaphoreType.DMA((count,))],
        input_output_aliases={1 + len(parts) + i: i for i in range(len(made))},
        name="place", compiler_params=pltpu.CompilerParams(vmem_limit_bytes=24 << 20),
    )(info, *[p for _, p in parts], *made)

def sort_kernel(firsts, info, *refs):
    parts, made, (tall, sems) = refs[: len(firsts)], refs[-6:-2], refs[-2:]
    size = parts[0].shape[1]
    mine = info[6]
    pieces = []
    for part, first in zip(parts, firsts):
        for i in range(part.shape[0]):
            tall[len(pieces)] = part[i].astype(F32)
            pieces.append(first + i)
    for top in range(4):
        @pl.when((mine >> 3) == top)
        def _(top=top):
            copies = []
            for n, r in enumerate(pieces):
                to = pl.ds(pl.multiple_of(((r ^ mine) & 7) * size, size), size)
                copies.append(pltpu.make_async_copy(tall.at[n], made[top ^ (r >> 3)].at[to, :], sems.at[n]))
                copies[-1].start()
            for copy in copies:
                copy.wait()

def sort(info, parts, made, width):
    smem, vmem, far = (pl.BlockSpec(memory_space=m) for m in (pltpu.SMEM, pltpu.VMEM, pltpu.HBM))
    shape = jax.ShapeDtypeStruct((width, width), F32)
    count = sum(p.shape[0] for _, p in parts)
    return pl.pallas_call(
        functools.partial(sort_kernel, [first for first, _ in parts]),
        in_specs=[smem] + [vmem] * len(parts) + [far] * len(made),
        out_specs=[far] * 4,
        out_shape=[shape] * 4,
        scratch_shapes=[pltpu.VMEM((count,) + parts[0][1].shape[1:], F32), pltpu.SemaphoreType.DMA((count,))],
        input_output_aliases={1 + len(parts) + i: i for i in range(len(made))},
        name="sort", compiler_params=pltpu.CompilerParams(vmem_limit_bytes=12 << 20),
    )(info, *[p for _, p in parts], *made)

def mix_kernel(*refs):
    for k in range(4):
        refs[4 + k][...] = added(*[term[k] for term in refs[:4]])

def mix(terms):
    block = terms[0].shape[1:]
    vmem = pl.BlockSpec(memory_space=pltpu.VMEM)
    return pl.pallas_call(
        mix_kernel, in_specs=[vmem] * 4, out_specs=[vmem] * 4, out_shape=[jax.ShapeDtypeStruct(block, BF16)] * 4, name="mix", compiler_params=pltpu.CompilerParams(vmem_limit_bytes=10 << 20),
    )(*terms)

def exchange(value, bits):
    size = lax.axis_size("dp") * lax.axis_size("blk")
    return lax.ppermute(value, ("dp", "blk"), [(i, i ^ bits) for i in range(size)])

def wait(*values):
    return lax.optimization_barrier(values)

def added(*terms):
    total = terms[0].astype(F32)
    for term in terms[1:]:
        total = total + term.astype(F32)
    return total.astype(BF16)

def local(inputs, w_query, w_key, w_value, w_out, w_in, w_back, norm1_gain, norm2_gain, final_gain, bias_table, bucket_table, prefix_len, pad_len, pooled_grad):
    rows, width = inputs.shape[1:]
    spot, far_off = lax.axis_index("blk"), lax.axis_index("dp")
    doc, core = spot // 2, spot % 2
    block = [doc * 2 + core, doc * 2 + 1 - core, (1 - doc) * 2 + core, (1 - doc) * 2 + 1 - core]
    line = [8, 16]
    further = [32 << b for b in range((lax.axis_size("dp") // 8).bit_length() - 1)]
    piece = core * 16 + doc * 4 + (far_off % 2) * 8 + (far_off // 2) % 4
    far_send = jnp.where(doc == 0, inputs[1], inputs[0])
    far = exchange(far_send, ROW)
    inputs, _ = wait(inputs, far_send)
    near = jnp.where(doc == 0, inputs[0], inputs[1])
    near_other = exchange(near, CORE)
    slot = jnp.arange(8, dtype=jnp.int32)
    ids = jnp.zeros_like(slot)
    for i, value in enumerate([b * rows for b in block] + [piece, core, doc]):
        ids = jnp.where(slot == i, value, ids)
    gain1, gain2, gain3 = norm1_gain[None, :], norm2_gain[None, :], final_gain[None, :]
    buckets = bucket_table[None, :]
    hid_l, q_l, k_l, v_l, w_query, w_key, w_value = prepare(near, near_other, gain1, w_query, w_key, w_value)
    far, q_l, ids = wait(far, q_l, ids)
    far_other = exchange(far, CORE)
    lines, info = tables(ids, pad_len, prefix_len, bias_table.T, buckets, 4 * rows)
    (hid_r, q_r, k_r, v_r, expo, inverse, attended, send, active, slopes, turned, mixed, steep, dense_rows) = front(
        info, far, far_other, near, q_l, k_l, v_l, lines, w_query, w_key, w_value,
        gain1, gain2, gain3, pooled_grad, w_out, w_in, w_back)

    xy = [ROW, NEAR_X, ROW ^ NEAR_X]
    zz = [line[0], line[1], line[0] ^ line[1]]

    token, send = wait(info, send)
    got = exchange(send, CORE)
    grad_mixed, grad_attended, grad_out_w, through_rows = through(token, slopes, w_in, mixed, steep, w_out, attended, gain2)
    token, through_rows, got = wait(token, through_rows, got)
    stays, *sends = meet(token, got, active, slopes, turned, steep)

    token, sends = wait(token, sends)
    came = [exchange(s, m) for s, m in zip(sends, xy)]
    rest_keep, rest_send, stay, leave, small = back(
        token, q_l, q_r, k_l, k_r, v_l, v_r, grad_attended, attended, inverse, expo, buckets, dense_rows, through_rows,
        hid_l, hid_r, near, near_other, far, far_other, w_query, w_key, w_value, grad_out_w)
    token, small, rest_send, leave, came = wait(token, small, rest_send, leave, came)

    rest_got = exchange(rest_send, CORE)
    hidden_got = exchange(leave, CORE)
    lines = mix([stays] + list(came))
    token, lines = wait(token, lines)
    took = [exchange(lines[k + 1], m) for k, m in enumerate(zz)]
    token, rest_got, hidden_got = wait(token, rest_got, hidden_got)

    count = rest_keep.shape[0] * rest_keep.shape[1]
    small = small + one_value(rest_got[count:])
    rest_got = rest_got[:count].reshape(rest_keep.shape)
    terms = two_terms(small)
    sends = [jnp.concatenate([added(rest_keep[4 * k : 4 * k + 4], rest_got[4 * k : 4 * k + 4]).reshape(-1, width), terms]) for k in (1, 2, 3)]
    token, sends = wait(token, sends)
    rest_came = [exchange(s, m) for s, m in zip(sends, xy)]
    home, away = ending(token, stay, hidden_got, near, far, grad_mixed, gain1, dense_rows)
    token, took, away = wait(token, took, away)

    whole = added(lines[0], *took)
    for bit in further:
        whole = added(whole, exchange(whole, bit))
    token, whole = wait(token, whole)
    back_line = [exchange(whole, m) for m in zz]
    away_got = exchange(away, ROW)
    token, rest_came = wait(token, rest_came)

    count = count // 4
    for part in rest_came:
        small = small + one_value(part[count:])
    rest_came = [part[:count].reshape((4,) + rest_keep.shape[1:]) for part in rest_came]
    piece = count // 4
    lines = added(rest_keep[:4], rest_got[:4], *rest_came).reshape(-1, width)
    send = jnp.concatenate([lines[piece : 2 * piece], lines[3 * piece :], two_terms(small)])
    token, send = wait(token, send)
    took = exchange(send, line[0])
    token, took = wait(token, took)
    small = small + one_value(took[2 * piece :])
    lines = added(jnp.concatenate([lines[:piece], lines[2 * piece : 3 * piece]]), took[: 2 * piece])
    send = jnp.concatenate([lines, two_terms(small)])
    token, send, back_line, away_got = wait(token, send, back_line, away_got)
    took = exchange(send, line[1])

    quarter = jnp.stack([whole] + back_line)
    token, quarter = wait(token, quarter)
    from_y, from_x = exchange(quarter, ROW), exchange(quarter, NEAR_X)
    pool_mine, pool_other = one_value(home[rows:])[:1], one_value(away_got[rows:])[:1]
    pooled = jnp.where(doc == 0, jnp.concatenate([pool_mine, pool_other]), jnp.concatenate([pool_other, pool_mine]))
    home, away_got = home[:rows], away_got[:rows]
    input_grad = jnp.where(doc == 0, jnp.stack([home, away_got]), jnp.stack([away_got, home]))
    token, took, pooled, input_grad = wait(token, took, pooled, input_grad)

    small = small + one_value(took[2 * piece :])
    rest = added(lines, jnp.concatenate([took[piece : 2 * piece], took[:piece]]))
    for bit in further:
        rest = added(rest, exchange(rest, bit))
        small = small + exchange(small, bit)
    token, rest = wait(token, rest)
    rest_back = exchange(rest, line[0])
    outs = [small[0], small[1], small[2], small[3, : bias_table.size].reshape(bias_table.shape[::-1]).T]
    token, from_y, from_x, outs = wait(token, from_y, from_x, outs)

    sends = [from_x[:2], from_y[2:]]
    token, sends, rest_back = wait(token, sends, rest_back)
    far_a, far_b = exchange(sends[0], ROW), exchange(sends[1], NEAR_X)
    fourth = jnp.stack([rest[:piece], rest_back[:piece], rest[piece:], rest_back[piece:]])
    token, fourth, quarter = wait(token, fourth, quarter)
    fourth_y, fourth_x = exchange(fourth, ROW), exchange(fourth, NEAR_X)
    other = exchange(quarter, CORE)
    near_pair = jnp.concatenate([from_y, from_x])
    grads = place(token, [(0, quarter), (4, from_y), (8, from_x)], [], width)
    token, grads, other, near_pair, far_a, far_b, fourth_y, fourth_x = wait(token, grads, other, near_pair, far_a, far_b, fourth_y, fourth_x)

    sends = [fourth_x[:2], fourth_y[2:], near_pair, jnp.concatenate([far_a, far_b]), jnp.concatenate([fourth, fourth_y, fourth_x])]
    token, sends = wait(token, sends)
    last_a, last_b, other_near, other_far, pair = (exchange(s, m) for s, m in zip(sends, (ROW, NEAR_X, CORE, CORE, CORE)))
    grads = place(token, [(12, far_a), (14, far_b), (16, other)], grads, width)
    token, grads, other_near, other_far = wait(token, grads, other_near, other_far)
    out_back, out_in = place(token, [(20, other_near), (28, other_far)], grads, width)
    token, out_back, out_in, last_a, last_b, pair = wait(token, out_back, out_in, last_a, last_b, pair)

    ends = exchange(jnp.concatenate([last_a, last_b]), CORE)
    made = sort(token, [(0, fourth), (4, fourth_y), (8, fourth_x), (12, last_a), (14, last_b), (16, pair)], [], width)
    token, made, ends = wait(token, made, ends)
    out_out, out_query, out_key, out_value = sort(token, [(28, ends)], made, width)
    return (pooled, input_grad, out_query, out_key, out_value, out_out, out_in, out_back, *outs)

def solution(mesh):
    data = P("dp", "blk", None)
    placed = (data,) + (P(),) * 11 + (P("dp"), P("dp"), P("dp", None))
    return jax.shard_map(local, mesh=mesh, in_specs=placed, out_specs=(P("dp", None), data) + (P(),) * 10, check_vma=False)
```

```python
import functools
import jax, jax.numpy as jnp
from jax import lax
from jax.experimental import pallas as pl
from jax.experimental.pallas import tpu as pltpu
from jax.sharding import PartitionSpec as P

F32, BF16 = jnp.float32, jnp.bfloat16
NEG = -1000000000.0
NT = (((1,), (1,)), ((), ()))
TN = (((0,), (0,)), ((), ()))
NN = (((1,), (0,)), ((), ()))

def dot(a, b, dims=NN):
    return lax.dot_general(a, b, dims, preferred_element_type=F32)

def skew(row, width, dtype=F32):
    return pltpu.roll(jnp.broadcast_to(row, (128, width)), width - 127, 1, stride=1, stride_axis=0)


BUCKETS = 32
EPS = 1e-06
CORE, ROW, NEAR_X = 1, 2, 4

def rms_scale(values):
    return lax.rsqrt(jnp.mean(values * values, axis=-1, keepdims=True) + EPS)

def norm_back(grad_out, values, scale, gain):
    weighted = grad_out * gain
    inner = jnp.mean(weighted * values, axis=-1, keepdims=True)
    grad_in = scale * weighted - scale * scale * scale * values * inner
    return grad_in, jnp.sum(grad_out * values * scale, axis=0, keepdims=True)

def two_terms(value):
    high = value.astype(BF16)
    return jnp.concatenate([high, (value - high.astype(F32)).astype(BF16)])

def one_value(terms):
    return terms[:8].astype(F32) + terms[8:16].astype(F32)

def rows_of(*values):
    count = sum(v.shape[0] for v in values)
    return jnp.concatenate(list(values) + [jnp.zeros((8 - count, values[0].shape[1]), F32)])

def prepare_kernel(mine, other, gain, wq_h, wk_h, wv_h, hidden, query, keys, values, wq, wk, wv, sems):
    rows = mine.shape[0]
    load = [pltpu.make_async_copy(a, b, sems.at[i]) for i, (a, b) in enumerate(((wk_h, wk), (wv_h, wv), (wq_h, wq)))]
    for copy in load:
        copy.start()
    for part, raw in enumerate((mine, other)):
        tokens = raw[...].astype(F32)
        hidden[part * rows : (part + 1) * rows, :] = (tokens * rms_scale(tokens) * gain[...]).astype(BF16)
    h = hidden[...]
    load[0].wait()
    keys[...] = dot(h, wk[...]).astype(BF16)
    load[1].wait()
    values[...] = dot(h, wv[...]).astype(BF16)
    load[2].wait()
    query[...] = dot(h[:rows], wq[...]).astype(BF16)

def prepare(mine, other, gain, wq, wk, wv):
    rows, width = mine.shape
    shape = lambda n: jax.ShapeDtypeStruct((n, width), BF16)
    vmem, free = (pl.BlockSpec(memory_space=m) for m in (pltpu.VMEM, pl.ANY))
    return pl.pallas_call(
        prepare_kernel,
        in_specs=[vmem] * 3 + [free] * 3,
        out_specs=[vmem] * 7,
        out_shape=[shape(2 * rows), shape(rows), shape(2 * rows), shape(2 * rows)] + [shape(width)] * 3,
        scratch_shapes=[pltpu.SemaphoreType.DMA((3,))],
        name="prepare", compiler_params=pltpu.CompilerParams(vmem_limit_bytes=14 << 20),
    )(mine, other, gain, wq, wk, wv)

def tables_kernel(ids, pads, prefixes, bias, buckets, lines, info, *, length):
    doc = ids[6]
    info[0] = length - jnp.where(doc == 0, pads[0], pads[1])
    info[5] = jnp.where(doc == 0, prefixes[0], prefixes[1])
    for to, at in enumerate((0, 1, 2, 3)):
        info[1 + to] = ids[at]
    for to, at in enumerate((4, 5, 6)):
        info[6 + to] = ids[at]
    picker = jnp.where(lax.broadcasted_iota(jnp.int32, (BUCKETS, 1), 0) == buckets[...], 1.0, 0.0).astype(BF16)
    left, total = bias[...], None
    for _ in range(3):
        part = left.astype(BF16)
        left = left - part.astype(F32)
        made = dot(part, picker)
        total = made if total is None else total + made
    lines[...] = jnp.zeros_like(lines)
    lines[:, : buckets.shape[1]] = total

def tables(ids, pads, prefixes, bias, buckets, length):
    smem, vmem = pl.BlockSpec(memory_space=pltpu.SMEM), pl.BlockSpec(memory_space=pltpu.VMEM)
    return pl.pallas_call(
        functools.partial(tables_kernel, length=length),
        in_specs=[smem] * 3 + [vmem] * 2,
        out_specs=[vmem, smem],
        out_shape=[jax.ShapeDtypeStruct((bias.shape[0], buckets.shape[1] + 1), F32), jax.ShapeDtypeStruct((16,), jnp.int32)],
        name="tables", compiler_params=pltpu.CompilerParams(vmem_limit_bytes=4 << 20),
    )(ids, pads, prefixes, bias, buckets)

def back_pieces(to, active, low, mine):
    @pl.loop(0, active.shape[1] // 512)
    def _(group):
        made = dot(active[:, pl.ds(pl.multiple_of(group * 512, 512), 512)], low, TN).astype(BF16)
        for b in range(4):
            rows = made[b * 128 : (b + 1) * 128]
            to[(4 * group + b) ^ mine] = jnp.concatenate([rows[:, q * 128 : (q + 1) * 128] for q in range(4)])

def in_pieces(to, slopes, turned, mine):
    @pl.loop(0, slopes.shape[1] // 512)
    def _(group):
        made = dot(turned, slopes[:, pl.ds(pl.multiple_of(group * 512, 512), 512)]).astype(BF16)
        for b in range(4):
            to[(4 * group + b) ^ mine] = made[:, b * 128 : (b + 1) * 128]

def front_kernel(info, far, far_other, near, q_l, k_l, v_l, lines, wq, wk, wv, gain1, gain2, gain3, cots, wo_h, win_h, wback_h,
                 hid_o, q_o, k_o, v_o, expo_o, inv_o, att_o, send_o, active_o, slopes_o, turned_o, mixed_o, steep_o, rows,
                 hid, qs, ks, vs, inv, att, send, active, slopes, turned, mixed, steep, wo, win, wback, expo, scores, skewed, edges, sems):
    count, width = near.shape
    hidden = win.shape[1]
    step = pl.program_id(0)
    late = [pltpu.make_async_copy(a, b, sems.at[i]) for i, (a, b) in enumerate(((wo_h, wo), (win_h, win), (wback_h, wback)))]
    early = [pltpu.make_async_copy(a, b, sems.at[3 + i]) for i, (a, b) in enumerate(((hid, hid_o), (qs, q_o), (ks, k_o), (vs, v_o)))]
    dense = [pltpu.make_async_copy(a, b, sems.at[7 + i]) for i, (a, b) in enumerate((
        (inv, inv_o), (att, att_o), (mixed, mixed_o), (turned, turned_o), (active, active_o), (steep, steep_o), (slopes, slopes_o), (send, send_o)))]
    kept = lambda g: pltpu.make_async_copy(expo, expo_o.at[pl.ds(2 * g, 2)], sems.at[15])

    @pl.when(step == 0)
    def _():
        for copy in late:
            copy.start()
        for part, raw in enumerate((far, far_other)):
            tokens = raw[...].astype(F32)
            hid[part * count : (part + 1) * count, :] = (tokens * rms_scale(tokens) * gain1[...]).astype(BF16)
        h = hid[...]
        qs[...] = dot(h[:count], wq[...]).astype(BF16)
        ks[...] = dot(h, wk[...]).astype(BF16)
        vs[...] = dot(h, wv[...]).astype(BF16)
        for copy in early:
            copy.start()
        column = lax.broadcasted_iota(jnp.int32, (1, 128), 1)
        for b in range(4):
            place = info[1 + b] + lax.broadcasted_iota(jnp.int32, (count, 1), 0)
            gate = jnp.where(place < info[0], 0.0, NEG)
            for head in range(2):
                edges[head, b * count : (b + 1) * count, :] = jnp.where(column == (64 if head == 0 else 0), gate, 0.0).astype(BF16)

    @pl.when(step > 0)
    def _():
        kept(step - 1).wait()

    cols = pl.ds(pl.multiple_of(step * 128, 128), 128)
    lane = lax.broadcasted_iota(jnp.int32, (1, 128), 1)
    first = lane < 64
    limit = info[0]
    starts = [info[1 + b] for b in range(4)]
    keys = [k_l[:count, :], k_l[count:, :], ks[:count, cols], ks[count:, cols]]
    values = jnp.concatenate([v_l[...], vs[:, cols]])
    query = jnp.concatenate([q_l[...], qs[:, cols]])
    made = []
    for head in range(2):
        mine = jnp.where(first if head == 0 else lane >= 64, 1.0, 0.0).astype(BF16)
        one = jnp.where(lane == (64 if head == 0 else 0), 1.0, 0.0).astype(BF16)
        q = query * mine + one
        v = values * mine + one
        skewed[head] = skew(lines[pl.ds(2 * step + head, 1), :], lines.shape[1])
        k = jnp.concatenate(keys) * mine + edges[head]
        for half in range(2):
            s = dot(q[half * 256 : (half + 1) * 256], k, NT)
            for r in range(2):
                for b in range(4):
                    at = starts[b] - starts[2 * half] + 896 - 128 * r
                    part = s[r * 128 : (r + 1) * 128, b * 256 : (b + 1) * 256] + skewed[head, :, pl.ds(pl.multiple_of(at, 128), 256)]
                    scores[head, half * 256 + r * 128 : half * 256 + (r + 1) * 128, b * 256 : (b + 1) * 256] = part
        accs = []
        for r in range(4):
            rs = slice(r * 128, (r + 1) * 128)
            value = scores[head, rs, :]
            top = jnp.max(value, axis=1, keepdims=True)
            e = jnp.exp(value - top).astype(BF16)
            expo[head, rs, :] = e
            accs.append(dot(e, v))
        acc = jnp.concatenate(accs)
        made.append((acc, 1.0 / (acc[:, 64:65] if head == 0 else acc[:, 0:1])))
    (a0, i0), (a1, i1) = made
    scale = jnp.where(first, i0, i1)
    att[:, cols] = (jnp.where(first, a0, a1) * scale).astype(BF16)
    inv[:, cols] = scale
    kept(step).start()

    @pl.when(step == 3)
    def _():
        for copy in late:
            copy.wait()
        dense[0].start()
        dense[1].start()
        for part, raw in enumerate((near, far)):
            spot = slice(part * count, (part + 1) * count)
            mixed[spot, :] = raw[...].astype(F32) + dot(att[spot, :], wo[...])
        dense[2].start()
        values = mixed[...]
        inner = (values * rms_scale(values) * gain2[...]).astype(BF16)
        turned[...] = inner.T
        dense[3].start()
        total = values
        for at in range(0, hidden, 512):
            lifted = jnp.maximum(dot(inner, win[:, at : at + 512]), 0.0).astype(BF16)
            active[:, at : at + 512] = lifted
            total = total + dot(lifted, wback[at : at + 512, :])
        dense[4].start()
        scale = rms_scale(total)
        place = lax.broadcasted_iota(jnp.int32, (2 * count, 1), 0)
        place = jnp.where(place < count, place + info[1], place + (info[3] - count))
        live = jnp.where((place >= info[5]) & (place < limit), 1.0, 0.0)
        pool = jnp.sum(total * scale * gain3[...] * live, axis=0, keepdims=True)
        cot = jnp.where(info[8] == 0, cots[0:1, :], cots[1:2, :]) / (limit - info[5]).astype(F32)
        slope, grad_end = norm_back(live * cot, total, scale, gain3[...])
        steep[...] = slope
        dense[5].start()
        rows[...] = jnp.concatenate([pool, grad_end, jnp.zeros((6, width), F32)])
        low = slope.astype(BF16)
        for at in range(0, hidden, 512):
            through = dot(low, wback[at : at + 512, :], NT).astype(BF16)
            slopes[:, at : at + 512] = jnp.where(active[:, at : at + 512] > 0, through, jnp.zeros_like(through))
        dense[6].start()
        mine = info[6] & 15

        @pl.when(info[7] == 0)
        def _():
            in_pieces(send, slopes, turned[...], mine)

        @pl.when(info[7] == 1)
        def _():
            back_pieces(send, active, steep[...].astype(BF16), mine)

        dense[7].start()
        for copy in early + dense:
            copy.wait()
        kept(step).wait()

def front(info, far, far_other, near, q_l, k_l, v_l, lines, wq, wk, wv, gain1, gain2, gain3, cots, wo, win, wback):
    count, width = near.shape
    hidden = win.shape[1]
    heads, span = lines.shape
    shape = jax.ShapeDtypeStruct
    smem, free = pl.BlockSpec(memory_space=pltpu.SMEM), pl.BlockSpec(memory_space=pl.ANY)
    whole = lambda *dims: pl.BlockSpec(dims, lambda g: (0,) * len(dims))
    col = lambda n: pl.BlockSpec((n, 128), lambda g: (0, g))
    outs = [shape((2 * count, width), BF16), shape((count, width), BF16), shape((2 * count, width), BF16), shape((2 * count, width), BF16),
            shape((heads, 2 * count, 4 * count), BF16), shape((2 * count, width), F32), shape((2 * count, width), BF16),
            shape((16, width, 128), BF16), shape((2 * count, hidden), BF16), shape((2 * count, hidden), BF16),
            shape((width, 2 * count), BF16), shape((2 * count, width), F32), shape((2 * count, width), F32)]
    return pl.pallas_call(
        front_kernel,
        grid=(heads // 2,),
        in_specs=[smem] + [whole(count, width)] * 3 + [col(count), col(2 * count), col(2 * count), whole(heads, span)] + [whole(width, width)] * 3 + [whole(1, width)] * 3
                 + [whole(2, width)] + [pl.BlockSpec(memory_space=pltpu.HBM)] * 3,
        out_specs=[free] * 13 + [whole(8, width)],
        out_shape=outs + [shape((8, width), F32)],
        scratch_shapes=[pltpu.VMEM(o.shape, o.dtype) for o in outs[:4] + outs[5:]]
                       + [pltpu.VMEM(wo.shape, BF16), pltpu.VMEM(win.shape, BF16), pltpu.VMEM(wback.shape, BF16),
                          pltpu.VMEM((2, 2 * count, 4 * count), BF16), pltpu.VMEM((2, 2 * count, 4 * count), F32),
                          pltpu.VMEM((2, 128, span), F32), pltpu.VMEM((2, 4 * count, 128), BF16), pltpu.SemaphoreType.DMA((16,))],
        name="front", compiler_params=pltpu.CompilerParams(vmem_limit_bytes=38 << 20),
    )(info, far, far_other, near, q_l, k_l, v_l, lines, wq, wk, wv, gain1, gain2, gain3, cots, wo, win, wback)

def through_kernel(info, slopes_h, win_h, mixed_h, steep_h, wo_h, att_h, gain2, grad_mixed_o, grad_attended_o, grad_out_o, rows,
                   slopes, win, mixed, steep, wo, att, grad_mixed, grad_attended, grad_out, sems):
    hidden, width = slopes.shape[1], mixed.shape[1]
    chunks = []
    for i, at in enumerate(range(0, hidden, 512)):
        for a, b, s in ((slopes_h, slopes, i), (win_h, win, 4 + i)):
            chunks.append(pltpu.make_async_copy(a.at[:, at : at + 512], b.at[:, at : at + 512], sems.at[s]))
    copies = [pltpu.make_async_copy(a, b, sems.at[8 + i]) for i, (a, b) in enumerate((
        (mixed_h, mixed), (steep_h, steep), (wo_h, wo), (att_h, att)))]
    outs = [pltpu.make_async_copy(a, b, sems.at[12 + i]) for i, (a, b) in enumerate((
        (grad_mixed, grad_mixed_o), (grad_attended, grad_attended_o), (grad_out, grad_out_o)))]
    for copy in chunks + copies:
        copy.start()
    grad_inner = None
    for i, at in enumerate(range(0, hidden, 512)):
        chunks[2 * i].wait()
        chunks[2 * i + 1].wait()
        part = dot(slopes[:, at : at + 512], win[:, at : at + 512], NT)
        grad_inner = part if grad_inner is None else grad_inner + part
    copies[0].wait()
    copies[1].wait()
    values = mixed[...]
    more, grad_two = norm_back(grad_inner, values, rms_scale(values), gain2[...])
    total = steep[...] + more
    grad_mixed[...] = total
    outs[0].start()
    low = total.astype(BF16)
    copies[2].wait()
    grad_attended[...] = dot(low, wo[...], NT).astype(BF16)
    outs[1].start()
    copies[3].wait()
    grad_out[...] = dot(att[...], low, TN).astype(BF16)
    outs[2].start()
    rows[...] = jnp.concatenate([grad_two, jnp.zeros((7, width), F32)])
    for copy in outs:
        copy.wait()

def through(info, slopes, win, mixed, steep, wo, att, gain2):
    n, width = mixed.shape
    smem, vmem, free = (pl.BlockSpec(memory_space=m) for m in (pltpu.SMEM, pltpu.VMEM, pl.ANY))
    shape = jax.ShapeDtypeStruct
    given = (slopes, win, mixed, steep, wo, att)
    outs = [shape((n, width), F32), shape((n, width), BF16), shape((width, width), BF16)]
    return pl.pallas_call(
        through_kernel,
        in_specs=[smem, free, pl.BlockSpec(memory_space=pltpu.HBM)] + [free] * 4 + [vmem],
        out_specs=[free] * 3 + [vmem],
        out_shape=outs + [shape((8, width), F32)],
        scratch_shapes=[pltpu.VMEM(g.shape, g.dtype) for g in given] + [pltpu.VMEM(o.shape, o.dtype) for o in outs] + [pltpu.SemaphoreType.DMA((15,))],
        name="through", compiler_params=pltpu.CompilerParams(vmem_limit_bytes=16 << 20),
    )(info, *given, gain2)

def meet_kernel(info, got_h, active_h, slopes_h, turned_h, steep_h, *refs):
    outs, (got, chunk, turned, steep, blocks, sems) = refs[:4], refs[4:]
    order = (3, 1, 2, 0)
    high, lowest = (info[6] & 15) >> 2, info[6] & 3
    load = [pltpu.make_async_copy(got_h.at[4 * k : 4 * k + 4], got.at[k], sems.at[k]) for k in range(4)]
    save = [pltpu.make_async_copy(blocks.at[k], outs[k], sems.at[4 + k]) for k in range(4)]

    def columns(source, k):
        at = pl.ds(pl.multiple_of((k ^ high) * 512, 512), 512)
        return pltpu.make_async_copy(source.at[:, at], chunk.at[k], sems.at[8 + k])

    for side, source in ((0, active_h), (1, slopes_h)):
        @pl.when(info[7] == side)
        def _(side=side, source=source):
            extra = pltpu.make_async_copy(*((steep_h, steep) if side == 0 else (turned_h, turned)), sems.at[12])
            extra.start()
            for k in order:
                columns(source, k).start()
                load[k].start()
            extra.wait()
            low = steep[...].astype(BF16) if side == 0 else turned[...]
            for k in order:
                columns(source, k).wait()
                made = dot(chunk[k], low, TN) if side == 0 else dot(low, chunk[k])
                load[k].wait()
                for b in range(4):
                    piece = made[:, b * 128 : (b + 1) * 128]
                    if side == 0:
                        piece = made[b * 128 : (b + 1) * 128]
                        piece = jnp.concatenate([piece[:, q * 128 : (q + 1) * 128] for q in range(4)])
                    to = b ^ lowest
                    blocks[k, to] = (piece + got[k, to].astype(F32)).astype(BF16)
                save[k].start()

    for copy in save:
        copy.wait()

def meet(info, got, active, slopes, turned, steep):
    smem, free = pl.BlockSpec(memory_space=pltpu.SMEM), pl.BlockSpec(memory_space=pl.ANY)
    block = (4,) + got.shape[1:]
    n, width = steep.shape
    return pl.pallas_call(
        meet_kernel,
        in_specs=[smem] + [free] * 5,
        out_specs=[free] * 4,
        out_shape=[jax.ShapeDtypeStruct(block, BF16)] * 4,
        scratch_shapes=[pltpu.VMEM((4,) + block, BF16), pltpu.VMEM((4, n, 512), BF16), pltpu.VMEM(turned.shape, BF16), pltpu.VMEM(steep.shape, F32),
                        pltpu.VMEM((4,) + block, BF16), pltpu.SemaphoreType.DMA((13,))],
        name="meet", compiler_params=pltpu.CompilerParams(vmem_limit_bytes=20 << 20),
    )(info, got, active, slopes, turned, steep)

CLASS = {(0, 0): 0, (1, 2): 0, (0, 1): 1, (1, 3): 1, (0, 2): 2, (0, 3): 3, (1, 0): 4, (1, 1): 5}

def back_kernel(info, ql, qr, kl, kr, vl, vr, gout, out, inv, expo, buckets, dense_rows, through_rows,
                hid_l_h, hid_r_h, near_h, near_other_h, far_h, far_other_h, wq_h, wk_h, wv_h, grad_out_h,
                keep_o, send_o, stay_o, leave_o, small,
                hid_l, hid_r, near, near_other, far, far_other, wq, wk, wv, made,
                keep, send, stay, leave, dq, dk, dv, offsets, sums, acc, slopes, sems):
    count, width = near.shape
    step = pl.program_id(0)
    pairs = width // 128
    late = [pltpu.make_async_copy(a, b, sems.at[i]) for i, (a, b) in enumerate((
        (hid_l_h, hid_l), (hid_r_h, hid_r), (near_h, near), (near_other_h, near_other), (far_h, far), (far_other_h, far_other),
        (wq_h, wq), (wk_h, wk), (wv_h, wv), (grad_out_h, made.at[0:width])))]
    done = [pltpu.make_async_copy(a, b, sems.at[10 + i]) for i, (a, b) in enumerate(((send, send_o), (keep, keep_o), (leave, leave_o), (stay, stay_o)))]

    @pl.when(step == 0)
    def _():
        for copy in late:
            copy.start()

    cols = pl.ds(pl.multiple_of(step * 128, 128), 128)
    lane = lax.broadcasted_iota(jnp.int32, (1, 128), 1)
    starts = [info[1 + b] for b in range(4)]
    keys = jnp.concatenate([kl[...], kr[...]])
    values = jnp.concatenate([vl[...], vr[...]])
    query = jnp.concatenate([ql[...], qr[...]])
    scaled = gout[...].astype(F32) * inv[...]
    prod = scaled * out[...].astype(F32)
    low = scaled.astype(BF16)
    query_t, low_t = query.T, low.T
    grads_q, grads_k, grads_v = None, [], []
    for head in range(2):
        mine = (lane < 64) if head == 0 else (lane >= 64)
        base = 64 if head == 0 else 0
        pick = jnp.where(mine, 1.0, 0.0).astype(BF16)
        delta = jnp.sum(jnp.where(mine, prod, 0.0), axis=1, keepdims=True)
        high = delta.astype(BF16).astype(F32)
        extra = jnp.where(lane == base, high, jnp.where(lane == base + 1, delta - high, 0.0)).astype(BF16)
        grad = low * pick + extra
        minus = jnp.where((lane == base) | (lane == base + 1), -1.0, 0.0).astype(BF16)
        for b in range(4):
            spot = slice(b * count, (b + 1) * count)
            ds = dot(grad, values[spot] * pick + minus, NT) * expo[head, :, spot].astype(F32)
            slopes[head, :, spot] = ds.astype(BF16)
            for chunk in range(2):
                upper, lower = (ds[chunk * count + r * 128 : chunk * count + (r + 1) * 128] for r in range(2))
                group = CLASS[chunk, b]
                block = jnp.concatenate([lower[:, :128], lower[:, 128:] + upper[:, :128], upper[:, 128:]], axis=1)
                if (chunk, b) in ((1, 2), (1, 3)):
                    block = block + sums[head, group]
                sums[head, group] = block
        part = dot(slopes[head], keys * pick)
        grads_q = part if grads_q is None else grads_q + part
        half = slice(head * 64, (head + 1) * 64)
        grads_k.append(dot(query_t[half], slopes[head]))
        grads_v.append(dot(low_t[half], expo[head]))
    dq[:, cols] = grads_q.astype(BF16)
    dk[:, cols] = jnp.concatenate(grads_k).astype(BF16).T
    dv[:, cols] = jnp.concatenate(grads_v).astype(BF16).T
    for head in range(2):
        acc[head] = jnp.zeros(acc.shape[1:], F32)
        for (chunk, b), group in CLASS.items():
            if (chunk, b) not in ((1, 2), (1, 3)):
                at = starts[b] - starts[2 * chunk] + 768
                to = pl.ds(pl.multiple_of(at, 128), 384)
                acc[head, :, to] += sums[head, group]
        rest = acc[head]
        n = 64
        while n >= 8:
            rest = rest[:n] + pltpu.roll(rest[n:], 2048 - n, 1)
            n //= 2
        line = rest[7:8]
        for r in range(6, -1, -1):
            line = rest[r : r + 1] + pltpu.roll(line, 2047, 1)
        offsets[pl.ds(2 * step + head, 1), :] = pltpu.roll(line, 127, 1)

    @pl.when(step == pairs - 1)
    def _():
        for copy in late:
            copy.wait()
        made[width : 2 * width, :] = (dot(hid_l[:count, :], dq[:count, :], TN) + dot(hid_r[:count, :], dq[count:, :], TN)).astype(BF16)
        for at, grads in ((2 * width, dk), (3 * width, dv)):
            made[at : at + width, :] = (dot(hid_l[...], grads[: 2 * count, :], TN) + dot(hid_r[...], grads[2 * count :, :], TN)).astype(BF16)
        me = info[6]
        size = made.shape[0] // 32

        @pl.loop(0, 16)
        def _(r):
            keep[r] = made[pl.ds(pl.multiple_of((r ^ me) * size, size), size), :]
            send[pl.ds(pl.multiple_of(r * size, size), size), :] = made[pl.ds(pl.multiple_of(((r + 16) ^ me) * size, size), size), :]

        gain = jnp.zeros((1, width), F32)
        for b, raw in enumerate((near, near_other, far, far_other)):
            spot = slice(b * count, (b + 1) * count)
            grad = dot(dk[spot, :], wk[...], NT) + dot(dv[spot, :], wv[...], NT)
            half = slice((b // 2) * count, (b // 2 + 1) * count)
            if b % 2 == 0:
                grad = grad + dot(dq[half, :], wq[...], NT)
                stay[half, :] = grad
            else:
                leave[half, :] = grad.astype(BF16)
            tokens = raw[...].astype(F32)
            gain = gain + jnp.sum(grad * (tokens * rms_scale(tokens)), axis=0, keepdims=True)
        leave[2 * count :, :] = two_terms(rows_of(dense_rows[0:1, :]))
        picker = jnp.where(lax.broadcasted_iota(jnp.int32, (128, 1), 0) == buckets[...], 1.0, 0.0).astype(BF16)
        left = offsets[...][:, : buckets.shape[1]]
        bias = None
        for _ in range(3):
            part = left.astype(BF16)
            left = left - part.astype(F32)
            bias = dot(part, picker, NT) if bias is None else bias + dot(part, picker, NT)
        bias = jnp.concatenate([bias, jnp.zeros((bias.shape[0], width - 128), F32)], axis=1)
        line = bias[0:1]
        for h in range(1, bias.shape[0]):
            line = line + pltpu.roll(bias[h : h + 1], 32 * h, 1)
        total = rows_of(gain, through_rows[0:1, :], dense_rows[1:2, :], line)
        small[...] = total
        send[16 * size :, :] = two_terms(total)
        for copy in done:
            copy.start()
        for copy in done:
            copy.wait()

def back(info, ql, qr, kl, kr, vl, vr, gout, out, inv, expo, buckets, dense_rows, through_rows,
         hid_l, hid_r, near, near_other, far, far_other, wq, wk, wv, grad_out):
    count, width = near.shape
    smem, free = pl.BlockSpec(memory_space=pltpu.SMEM), pl.BlockSpec(memory_space=pl.ANY)
    whole = lambda *dims: pl.BlockSpec(dims, lambda g: (0,) * len(dims))
    col = lambda n: pl.BlockSpec((n, 128), lambda g: (0, g))
    shape = jax.ShapeDtypeStruct
    size = 4 * width // 32
    outs = [shape((16, size, width), BF16), shape((16 * size + 16, width), BF16), shape((2 * count, width), F32), shape((2 * count + 16, width), BF16)]
    given = (hid_l, hid_r, near, near_other, far, far_other, wq, wk, wv)
    return pl.pallas_call(
        back_kernel,
        grid=(width // 128,),
        in_specs=[smem, col(count), col(count)] + [col(2 * count)] * 7 + [pl.BlockSpec((2, 2 * count, 4 * count), lambda g: (g, 0, 0)),
                  whole(*buckets.shape), whole(8, width), whole(8, width)] + [free] * 10,
        out_specs=[free] * 4 + [whole(8, width)],
        out_shape=outs + [shape((8, width), F32)],
        scratch_shapes=[pltpu.VMEM(g.shape, BF16) for g in given] + [pltpu.VMEM((4 * width, width), BF16)]
                       + [pltpu.VMEM(o.shape, o.dtype) for o in outs]
                       + [pltpu.VMEM((2 * count, width), BF16), pltpu.VMEM((4 * count, width), BF16), pltpu.VMEM((4 * count, width), BF16),
                          pltpu.VMEM((8, 2048), F32), pltpu.VMEM((2, 6, 128, 384), F32), pltpu.VMEM((2, 128, 2048), F32),
                          pltpu.VMEM((2, 2 * count, 4 * count), BF16), pltpu.SemaphoreType.DMA((14,))],
        name="back", compiler_params=pltpu.CompilerParams(vmem_limit_bytes=44 << 20),
    )(info, ql, qr, kl, kr, vl, vr, gout, out, inv, expo, buckets, dense_rows, through_rows, *given, grad_out)

def ending_kernel(info, stay, came, near, far, grad_mixed, gain, dense_rows, home, away):
    count, width = near.shape
    for part, raw in enumerate((near, far)):
        spot = slice(part * count, (part + 1) * count)
        tokens = raw[...].astype(F32)
        grad = stay[spot, :] + came[spot, :].astype(F32)
        more, _ = norm_back(grad, tokens, rms_scale(tokens), gain[...])
        value = (grad_mixed[spot, :] + more).astype(BF16)
        if part == 0:
            home[:count, :] = value
        else:
            away[:count, :] = value
    alive = (info[0] - info[5]).astype(F32)
    pool = two_terms((rows_of(dense_rows[0:1, :]) + one_value(came[2 * count :, :])) / alive)
    home[count:, :] = pool
    away[count:, :] = pool

def ending(info, stay, came, near, far, grad_mixed, gain, dense_rows):
    count, width = near.shape
    smem, vmem = pl.BlockSpec(memory_space=pltpu.SMEM), pl.BlockSpec(memory_space=pltpu.VMEM)
    shape = jax.ShapeDtypeStruct((count + 16, width), BF16)
    return pl.pallas_call(
        ending_kernel, in_specs=[smem] + [vmem] * 7, out_specs=[vmem] * 2, out_shape=[shape, shape], name="ending", compiler_params=pltpu.CompilerParams(vmem_limit_bytes=10 << 20)
    )(info, stay, came, near, far, grad_mixed, gain, dense_rows)

def place_kernel(firsts, info, *refs):
    parts, (back, front, rows, columns, sems) = refs[: len(firsts)], refs[-5:]
    mine = info[6] & 15
    for side in range(2):
        @pl.when(info[7] == side)
        def _(side=side):
            copies, n = [], 0
            for part, first in zip(parts, firsts):
                for i in range(part.shape[0]):
                    r = first + i
                    to = pl.ds(pl.multiple_of(((r & 15) ^ mine) * 128, 128), 128)
                    if (r >= 16) == (side == 1):
                        for q in range(4):
                            rows[n, :, q * 128 : (q + 1) * 128] = part[i, q * 128 : (q + 1) * 128, :].astype(F32)
                        copies.append(pltpu.make_async_copy(rows.at[n], back.at[to, :], sems.at[n]))
                    else:
                        columns[n] = part[i].astype(F32)
                        copies.append(pltpu.make_async_copy(columns.at[n], front.at[:, to], sems.at[n]))
                    copies[-1].start()
                    n += 1
            for copy in copies:
                copy.wait()

def place(info, parts, made, width):
    smem, vmem, far = (pl.BlockSpec(memory_space=m) for m in (pltpu.SMEM, pltpu.VMEM, pltpu.HBM))
    shape = jax.ShapeDtypeStruct
    count = sum(p.shape[0] for _, p in parts)
    return pl.pallas_call(
        functools.partial(place_kernel, [first for first, _ in parts]),
        in_specs=[smem] + [vmem] * len(parts) + [far] * len(made),
        out_specs=[far] * 2,
        out_shape=[shape((16 * 128, width), F32), shape((width, 16 * 128), F32)],
        scratch_shapes=[pltpu.VMEM((count, 128, width), F32), pltpu.VMEM((count, width, 128), F32), pltpu.SemaphoreType.DMA((count,))],
        input_output_aliases={1 + len(parts) + i: i for i in range(len(made))},
        name="place", compiler_params=pltpu.CompilerParams(vmem_limit_bytes=28 << 20),
    )(info, *[p for _, p in parts], *made)

def sort_kernel(firsts, info, *refs):
    parts, made, (tall, sems) = refs[: len(firsts)], refs[-6:-2], refs[-2:]
    size = parts[0].shape[1]
    mine = info[6]
    pieces = []
    for part, first in zip(parts, firsts):
        for i in range(part.shape[0]):
            tall[len(pieces)] = part[i].astype(F32)
            pieces.append(first + i)
    for top in range(4):
        @pl.when((mine >> 3) == top)
        def _(top=top):
            copies = []
            for n, r in enumerate(pieces):
                to = pl.ds(pl.multiple_of(((r ^ mine) & 7) * size, size), size)
                copies.append(pltpu.make_async_copy(tall.at[n], made[top ^ (r >> 3)].at[to, :], sems.at[n]))
                copies[-1].start()
            for copy in copies:
                copy.wait()

def sort(info, parts, made, width):
    smem, vmem, far = (pl.BlockSpec(memory_space=m) for m in (pltpu.SMEM, pltpu.VMEM, pltpu.HBM))
    shape = jax.ShapeDtypeStruct((width, width), F32)
    count = sum(p.shape[0] for _, p in parts)
    return pl.pallas_call(
        functools.partial(sort_kernel, [first for first, _ in parts]),
        in_specs=[smem] + [vmem] * len(parts) + [far] * len(made),
        out_specs=[far] * 4,
        out_shape=[shape] * 4,
        scratch_shapes=[pltpu.VMEM((count,) + parts[0][1].shape[1:], F32), pltpu.SemaphoreType.DMA((count,))],
        input_output_aliases={1 + len(parts) + i: i for i in range(len(made))},
        name="sort", compiler_params=pltpu.CompilerParams(vmem_limit_bytes=12 << 20),
    )(info, *[p for _, p in parts], *made)

def mix_kernel(*refs):
    for k in range(4):
        refs[4 + k][...] = added(*[term[k] for term in refs[:4]])

def mix(terms):
    block = terms[0].shape[1:]
    vmem = pl.BlockSpec(memory_space=pltpu.VMEM)
    return pl.pallas_call(
        mix_kernel, in_specs=[vmem] * 4, out_specs=[vmem] * 4, out_shape=[jax.ShapeDtypeStruct(block, BF16)] * 4, name="mix", compiler_params=pltpu.CompilerParams(vmem_limit_bytes=10 << 20),
    )(*terms)

def exchange(value, bits):
    size = lax.axis_size("dp") * lax.axis_size("blk")
    return lax.ppermute(value, ("dp", "blk"), [(i, i ^ bits) for i in range(size)])

def wait(*values):
    return lax.optimization_barrier(values)

def added(*terms):
    total = terms[0].astype(F32)
    for term in terms[1:]:
        total = total + term.astype(F32)
    return total.astype(BF16)

def local(inputs, w_query, w_key, w_value, w_out, w_in, w_back, norm1_gain, norm2_gain, final_gain, bias_table, bucket_table, prefix_len, pad_len, pooled_grad):
    rows, width = inputs.shape[1:]
    spot, far_off = lax.axis_index("blk"), lax.axis_index("dp")
    doc, core = spot // 2, spot % 2
    block = [doc * 2 + core, doc * 2 + 1 - core, (1 - doc) * 2 + core, (1 - doc) * 2 + 1 - core]
    line = [8, 16]
    further = [32 << b for b in range((lax.axis_size("dp") // 8).bit_length() - 1)]
    piece = core * 16 + doc * 4 + (far_off % 2) * 8 + (far_off // 2) % 4
    near = jnp.where(doc == 0, inputs[0], inputs[1])
    far_send = jnp.where(doc == 0, inputs[1], inputs[0])
    near, far_send = wait(near, far_send)
    far = exchange(far_send, ROW)
    near_other = exchange(near, CORE)
    slot = jnp.arange(8, dtype=jnp.int32)
    ids = jnp.zeros_like(slot)
    for i, value in enumerate([b * rows for b in block] + [piece, core, doc]):
        ids = jnp.where(slot == i, value, ids)
    gain1, gain2, gain3 = norm1_gain[None, :], norm2_gain[None, :], final_gain[None, :]
    buckets = bucket_table[None, :]
    hid_l, q_l, k_l, v_l, w_query, w_key, w_value = prepare(near, near_other, gain1, w_query, w_key, w_value)
    far, q_l, ids = wait(far, q_l, ids)
    far_other = exchange(far, CORE)
    lines, info = tables(ids, pad_len, prefix_len, bias_table.T, buckets, 4 * rows)
    (hid_r, q_r, k_r, v_r, expo, inverse, attended, send, active, slopes, turned, mixed, steep, dense_rows) = front(
        info, far, far_other, near, q_l, k_l, v_l, lines, w_query, w_key, w_value,
        gain1, gain2, gain3, pooled_grad, w_out, w_in, w_back)

    xy = [ROW, NEAR_X, ROW ^ NEAR_X]
    zz = [line[0], line[1], line[0] ^ line[1]]

    token, send = wait(info, send)
    got = exchange(send, CORE)
    grad_mixed, grad_attended, grad_out_w, through_rows = through(token, slopes, w_in, mixed, steep, w_out, attended, gain2)
    token, through_rows, got = wait(token, through_rows, got)
    stays, *sends = meet(token, got, active, slopes, turned, steep)

    token, sends = wait(token, sends)
    came = [exchange(s, m) for s, m in zip(sends, xy)]
    rest_keep, rest_send, stay, leave, small = back(
        token, q_l, q_r, k_l, k_r, v_l, v_r, grad_attended, attended, inverse, expo, buckets, dense_rows, through_rows,
        hid_l, hid_r, near, near_other, far, far_other, w_query, w_key, w_value, grad_out_w)
    token, small, rest_send, leave, came = wait(token, small, rest_send, leave, came)

    rest_got = exchange(rest_send, CORE)
    hidden_got = exchange(leave, CORE)
    lines = mix([stays] + list(came))
    token, lines = wait(token, lines)
    took = [exchange(lines[k + 1], m) for k, m in enumerate(zz)]
    token, rest_got, hidden_got = wait(token, rest_got, hidden_got)

    count = rest_keep.shape[0] * rest_keep.shape[1]
    small = small + one_value(rest_got[count:])
    rest_got = rest_got[:count].reshape(rest_keep.shape)
    terms = two_terms(small)
    sends = [jnp.concatenate([added(rest_keep[4 * k : 4 * k + 4], rest_got[4 * k : 4 * k + 4]).reshape(-1, width), terms]) for k in (1, 2, 3)]
    token, sends = wait(token, sends)
    rest_came = [exchange(s, m) for s, m in zip(sends, xy)]
    home, away = ending(token, stay, hidden_got, near, far, grad_mixed, gain1, dense_rows)
    token, took, away = wait(token, took, away)

    whole = added(lines[0], *took)
    for bit in further:
        whole = added(whole, exchange(whole, bit))
    token, whole = wait(token, whole)
    back_line = [exchange(whole, m) for m in zz]
    away_got = exchange(away, ROW)
    token, rest_came = wait(token, rest_came)

    count = count // 4
    for part in rest_came:
        small = small + one_value(part[count:])
    rest_came = [part[:count].reshape((4,) + rest_keep.shape[1:]) for part in rest_came]
    piece = count // 4
    lines = added(rest_keep[:4], rest_got[:4], *rest_came).reshape(-1, width)
    send = jnp.concatenate([lines[piece : 2 * piece], lines[3 * piece :], two_terms(small)])
    token, send = wait(token, send)
    took = exchange(send, line[0])
    token, took = wait(token, took)
    small = small + one_value(took[2 * piece :])
    lines = added(jnp.concatenate([lines[:piece], lines[2 * piece : 3 * piece]]), took[: 2 * piece])
    send = jnp.concatenate([lines, two_terms(small)])
    token, send, back_line, away_got = wait(token, send, back_line, away_got)
    took = exchange(send, line[1])

    quarter = jnp.stack([whole] + back_line)
    token, quarter = wait(token, quarter)
    from_y, from_x = exchange(quarter, ROW), exchange(quarter, NEAR_X)
    pool_mine, pool_other = one_value(home[rows:])[:1], one_value(away_got[rows:])[:1]
    pooled = jnp.where(doc == 0, jnp.concatenate([pool_mine, pool_other]), jnp.concatenate([pool_other, pool_mine]))
    home, away_got = home[:rows], away_got[:rows]
    input_grad = jnp.where(doc == 0, jnp.stack([home, away_got]), jnp.stack([away_got, home]))
    token, took, pooled, input_grad = wait(token, took, pooled, input_grad)

    small = small + one_value(took[2 * piece :])
    rest = added(lines, jnp.concatenate([took[piece : 2 * piece], took[:piece]]))
    for bit in further:
        rest = added(rest, exchange(rest, bit))
        small = small + exchange(small, bit)
    token, rest = wait(token, rest)
    rest_back = exchange(rest, line[0])
    outs = [small[0], small[1], small[2], small[3, : bias_table.size].reshape(bias_table.shape[::-1]).T]
    token, from_y, from_x, outs = wait(token, from_y, from_x, outs)

    sends = [from_x[:2], from_y[2:]]
    token, sends, rest_back = wait(token, sends, rest_back)
    far_a, far_b = exchange(sends[0], ROW), exchange(sends[1], NEAR_X)
    fourth = jnp.stack([rest[:piece], rest_back[:piece], rest[piece:], rest_back[piece:]])
    token, fourth, quarter = wait(token, fourth, quarter)
    fourth_y, fourth_x = exchange(fourth, ROW), exchange(fourth, NEAR_X)
    other = exchange(quarter, CORE)
    near_pair = jnp.concatenate([from_y, from_x])
    grads = place(token, [(0, quarter), (4, from_y), (8, from_x)], [], width)
    token, grads, other, near_pair, far_a, far_b, fourth_y, fourth_x = wait(token, grads, other, near_pair, far_a, far_b, fourth_y, fourth_x)

    sends = [fourth_x[:2], fourth_y[2:], near_pair, jnp.concatenate([far_a, far_b]), jnp.concatenate([fourth, fourth_y, fourth_x])]
    token, sends = wait(token, sends)
    last_a, last_b, other_near, other_far, pair = (exchange(s, m) for s, m in zip(sends, (ROW, NEAR_X, CORE, CORE, CORE)))
    token, other_near, other_far = wait(token, other_near, other_far)
    out_back, out_in = place(token, [(12, far_a), (14, far_b), (16, other), (20, other_near), (28, other_far)], grads, width)
    token, out_back, out_in, last_a, last_b, pair = wait(token, out_back, out_in, last_a, last_b, pair)

    ends = exchange(jnp.concatenate([last_a, last_b]), CORE)
    made = sort(token, [(0, fourth), (4, fourth_y), (8, fourth_x), (12, last_a), (14, last_b), (16, pair)], [], width)
    token, made, ends = wait(token, made, ends)
    out_out, out_query, out_key, out_value = sort(token, [(28, ends)], made, width)
    return (pooled, input_grad, out_query, out_key, out_value, out_out, out_in, out_back, *outs)

def solution(mesh):
    data = P("dp", "blk", None)
    placed = (data,) + (P(),) * 11 + (P("dp"), P("dp"), P("dp", None))
    return jax.shard_map(local, mesh=mesh, in_specs=placed, out_specs=(P("dp", None), data) + (P(),) * 10, check_vma=False)
```

```python
import functools
import jax, jax.numpy as jnp
from jax import lax
from jax.experimental import pallas as pl
from jax.experimental.pallas import tpu as pltpu
from jax.sharding import PartitionSpec as P

F32, BF16 = jnp.float32, jnp.bfloat16
NEG = -1000000000.0
NT = (((1,), (1,)), ((), ()))
TN = (((0,), (0,)), ((), ()))
NN = (((1,), (0,)), ((), ()))

def dot(a, b, dims=NN):
    return lax.dot_general(a, b, dims, preferred_element_type=F32)

def skew(row, width, dtype=F32):
    return pltpu.roll(jnp.broadcast_to(row, (128, width)), width - 127, 1, stride=1, stride_axis=0)


BUCKETS = 32
EPS = 1e-06
CORE, ROW, NEAR_X = 1, 2, 4

def rms_scale(values):
    return lax.rsqrt(jnp.mean(values * values, axis=-1, keepdims=True) + EPS)

def norm_back(grad_out, values, scale, gain):
    weighted = grad_out * gain
    inner = jnp.mean(weighted * values, axis=-1, keepdims=True)
    grad_in = scale * weighted - scale * scale * scale * values * inner
    return grad_in, jnp.sum(grad_out * values * scale, axis=0, keepdims=True)

def two_terms(value):
    high = value.astype(BF16)
    return jnp.concatenate([high, (value - high.astype(F32)).astype(BF16)])

def one_value(terms):
    return terms[:8].astype(F32) + terms[8:16].astype(F32)

def rows_of(*values):
    count = sum(v.shape[0] for v in values)
    return jnp.concatenate(list(values) + [jnp.zeros((8 - count, values[0].shape[1]), F32)])

def prepare_kernel(mine, other, gain, wq_h, wk_h, wv_h, hidden, query, keys, values, wq, wk, wv, sems):
    rows = mine.shape[0]
    load = [pltpu.make_async_copy(a, b, sems.at[i]) for i, (a, b) in enumerate(((wk_h, wk), (wv_h, wv), (wq_h, wq)))]
    for copy in load:
        copy.start()
    for part, raw in enumerate((mine, other)):
        tokens = raw[...].astype(F32)
        hidden[part * rows : (part + 1) * rows, :] = (tokens * rms_scale(tokens) * gain[...]).astype(BF16)
    h = hidden[...]
    load[0].wait()
    keys[...] = dot(h, wk[...]).astype(BF16)
    load[1].wait()
    values[...] = dot(h, wv[...]).astype(BF16)
    load[2].wait()
    query[...] = dot(h[:rows], wq[...]).astype(BF16)

def prepare(mine, other, gain, wq, wk, wv):
    rows, width = mine.shape
    shape = lambda n: jax.ShapeDtypeStruct((n, width), BF16)
    vmem, free = (pl.BlockSpec(memory_space=m) for m in (pltpu.VMEM, pl.ANY))
    return pl.pallas_call(
        prepare_kernel,
        in_specs=[vmem] * 3 + [free] * 3,
        out_specs=[vmem] * 7,
        out_shape=[shape(2 * rows), shape(rows), shape(2 * rows), shape(2 * rows)] + [shape(width)] * 3,
        scratch_shapes=[pltpu.SemaphoreType.DMA((3,))],
        name="prepare", compiler_params=pltpu.CompilerParams(vmem_limit_bytes=14 << 20),
    )(mine, other, gain, wq, wk, wv)

def tables_kernel(ids, pads, prefixes, bias, buckets, lines, info, *, length):
    doc = ids[6]
    info[0] = length - jnp.where(doc == 0, pads[0], pads[1])
    info[5] = jnp.where(doc == 0, prefixes[0], prefixes[1])
    for to, at in enumerate((0, 1, 2, 3)):
        info[1 + to] = ids[at]
    for to, at in enumerate((4, 5, 6)):
        info[6 + to] = ids[at]
    picker = jnp.where(lax.broadcasted_iota(jnp.int32, (BUCKETS, 1), 0) == buckets[...], 1.0, 0.0).astype(BF16)
    left, total = bias[...], None
    for _ in range(3):
        part = left.astype(BF16)
        left = left - part.astype(F32)
        made = dot(part, picker)
        total = made if total is None else total + made
    lines[...] = jnp.zeros_like(lines)
    lines[:, : buckets.shape[1]] = total

def tables(ids, pads, prefixes, bias, buckets, length):
    smem, vmem = pl.BlockSpec(memory_space=pltpu.SMEM), pl.BlockSpec(memory_space=pltpu.VMEM)
    return pl.pallas_call(
        functools.partial(tables_kernel, length=length),
        in_specs=[smem] * 3 + [vmem] * 2,
        out_specs=[vmem, smem],
        out_shape=[jax.ShapeDtypeStruct((bias.shape[0], buckets.shape[1] + 1), F32), jax.ShapeDtypeStruct((16,), jnp.int32)],
        name="tables", compiler_params=pltpu.CompilerParams(vmem_limit_bytes=4 << 20),
    )(ids, pads, prefixes, bias, buckets)

def back_pieces(to, active, low, mine):
    @pl.loop(0, active.shape[1] // 512)
    def _(group):
        made = dot(active[:, pl.ds(pl.multiple_of(group * 512, 512), 512)], low, TN).astype(BF16)
        for b in range(4):
            rows = made[b * 128 : (b + 1) * 128]
            to[(4 * group + b) ^ mine] = jnp.concatenate([rows[:, q * 128 : (q + 1) * 128] for q in range(4)])

def in_pieces(to, slopes, turned, mine):
    @pl.loop(0, slopes.shape[1] // 512)
    def _(group):
        made = dot(turned, slopes[:, pl.ds(pl.multiple_of(group * 512, 512), 512)]).astype(BF16)
        for b in range(4):
            to[(4 * group + b) ^ mine] = made[:, b * 128 : (b + 1) * 128]

def front_kernel(info, far, far_other, near, q_l, k_l, v_l, lines, wq, wk, wv, gain1, gain2, gain3, cots, wo_h, win_h, wback_h,
                 hid_o, q_o, k_o, v_o, expo_o, inv_o, att_o, send_o, active_o, slopes_o, turned_o, mixed_o, steep_o, rows,
                 hid, qs, ks, vs, inv, att, send, active, slopes, turned, mixed, steep, wo, win, wback, expo, scores, skewed, edges, sems):
    count, width = near.shape
    hidden = win.shape[1]
    step = pl.program_id(0)
    late = [pltpu.make_async_copy(a, b, sems.at[i]) for i, (a, b) in enumerate(((wo_h, wo), (win_h, win), (wback_h, wback)))]
    early = [pltpu.make_async_copy(a, b, sems.at[3 + i]) for i, (a, b) in enumerate(((hid, hid_o), (qs, q_o), (ks, k_o), (vs, v_o)))]
    dense = [pltpu.make_async_copy(a, b, sems.at[7 + i]) for i, (a, b) in enumerate((
        (inv, inv_o), (att, att_o), (mixed, mixed_o), (turned, turned_o), (active, active_o), (steep, steep_o), (slopes, slopes_o), (send, send_o)))]
    kept = lambda g: pltpu.make_async_copy(expo, expo_o.at[pl.ds(2 * g, 2)], sems.at[15])

    @pl.when(step == 0)
    def _():
        for copy in late:
            copy.start()
        for part, raw in enumerate((far, far_other)):
            tokens = raw[...].astype(F32)
            hid[part * count : (part + 1) * count, :] = (tokens * rms_scale(tokens) * gain1[...]).astype(BF16)
        h = hid[...]
        qs[...] = dot(h[:count], wq[...]).astype(BF16)
        ks[...] = dot(h, wk[...]).astype(BF16)
        vs[...] = dot(h, wv[...]).astype(BF16)
        for copy in early:
            copy.start()
        column = lax.broadcasted_iota(jnp.int32, (1, 128), 1)
        for b in range(4):
            place = info[1 + b] + lax.broadcasted_iota(jnp.int32, (count, 1), 0)
            gate = jnp.where(place < info[0], 0.0, NEG)
            for head in range(2):
                edges[head, b * count : (b + 1) * count, :] = jnp.where(column == (64 if head == 0 else 0), gate, 0.0).astype(BF16)

    @pl.when(step > 0)
    def _():
        kept(step - 1).wait()

    cols = pl.ds(pl.multiple_of(step * 128, 128), 128)
    lane = lax.broadcasted_iota(jnp.int32, (1, 128), 1)
    first = lane < 64
    limit = info[0]
    starts = [info[1 + b] for b in range(4)]
    keys = [k_l[:count, :], k_l[count:, :], ks[:count, cols], ks[count:, cols]]
    values = jnp.concatenate([v_l[...], vs[:, cols]])
    query = jnp.concatenate([q_l[...], qs[:, cols]])
    made = []
    for head in range(2):
        mine = jnp.where(first if head == 0 else lane >= 64, 1.0, 0.0).astype(BF16)
        one = jnp.where(lane == (64 if head == 0 else 0), 1.0, 0.0).astype(BF16)
        q = query * mine + one
        v = values * mine + one
        skewed[head] = skew(lines[pl.ds(2 * step + head, 1), :], lines.shape[1])
        k = jnp.concatenate(keys) * mine + edges[head]
        for half in range(2):
            s = dot(q[half * 256 : (half + 1) * 256], k, NT)
            for r in range(2):
                for b in range(4):
                    at = starts[b] - starts[2 * half] + 896 - 128 * r
                    part = s[r * 128 : (r + 1) * 128, b * 256 : (b + 1) * 256] + skewed[head, :, pl.ds(pl.multiple_of(at, 128), 256)]
                    scores[head, half * 256 + r * 128 : half * 256 + (r + 1) * 128, b * 256 : (b + 1) * 256] = part
        accs = []
        for r in range(4):
            rs = slice(r * 128, (r + 1) * 128)
            value = scores[head, rs, :]
            top = jnp.max(value, axis=1, keepdims=True)
            e = jnp.exp(value - top).astype(BF16)
            expo[head, rs, :] = e
            accs.append(dot(e, v))
        acc = jnp.concatenate(accs)
        made.append((acc, 1.0 / (acc[:, 64:65] if head == 0 else acc[:, 0:1])))
    (a0, i0), (a1, i1) = made
    scale = jnp.where(first, i0, i1)
    att[:, cols] = (jnp.where(first, a0, a1) * scale).astype(BF16)
    inv[:, cols] = scale
    kept(step).start()

    @pl.when(step == 3)
    def _():
        for copy in late:
            copy.wait()
        dense[0].start()
        dense[1].start()
        for part, raw in enumerate((near, far)):
            spot = slice(part * count, (part + 1) * count)
            mixed[spot, :] = raw[...].astype(F32) + dot(att[spot, :], wo[...])
        dense[2].start()
        values = mixed[...]
        inner = (values * rms_scale(values) * gain2[...]).astype(BF16)
        turned[...] = inner.T
        dense[3].start()
        total = values
        for at in range(0, hidden, 512):
            lifted = jnp.maximum(dot(inner, win[:, at : at + 512]), 0.0).astype(BF16)
            active[:, at : at + 512] = lifted
            total = total + dot(lifted, wback[at : at + 512, :])
        dense[4].start()
        scale = rms_scale(total)
        place = lax.broadcasted_iota(jnp.int32, (2 * count, 1), 0)
        place = jnp.where(place < count, place + info[1], place + (info[3] - count))
        live = jnp.where((place >= info[5]) & (place < limit), 1.0, 0.0)
        pool = jnp.sum(total * scale * gain3[...] * live, axis=0, keepdims=True)
        cot = jnp.where(info[8] == 0, cots[0:1, :], cots[1:2, :]) / (limit - info[5]).astype(F32)
        slope, grad_end = norm_back(live * cot, total, scale, gain3[...])
        steep[...] = slope
        dense[5].start()
        rows[...] = jnp.concatenate([pool, grad_end, jnp.zeros((6, width), F32)])
        low = slope.astype(BF16)
        for at in range(0, hidden, 512):
            through = dot(low, wback[at : at + 512, :], NT).astype(BF16)
            slopes[:, at : at + 512] = jnp.where(active[:, at : at + 512] > 0, through, jnp.zeros_like(through))
        dense[6].start()
        mine = info[6] & 15

        @pl.when(info[7] == 0)
        def _():
            in_pieces(send, slopes, turned[...], mine)

        @pl.when(info[7] == 1)
        def _():
            back_pieces(send, active, steep[...].astype(BF16), mine)

        dense[7].start()
        for copy in early + dense:
            copy.wait()
        kept(step).wait()

def front(info, far, far_other, near, q_l, k_l, v_l, lines, wq, wk, wv, gain1, gain2, gain3, cots, wo, win, wback):
    count, width = near.shape
    hidden = win.shape[1]
    heads, span = lines.shape
    shape = jax.ShapeDtypeStruct
    smem, free = pl.BlockSpec(memory_space=pltpu.SMEM), pl.BlockSpec(memory_space=pl.ANY)
    whole = lambda *dims: pl.BlockSpec(dims, lambda g: (0,) * len(dims))
    col = lambda n: pl.BlockSpec((n, 128), lambda g: (0, g))
    outs = [shape((2 * count, width), BF16), shape((count, width), BF16), shape((2 * count, width), BF16), shape((2 * count, width), BF16),
            shape((heads, 2 * count, 4 * count), BF16), shape((2 * count, width), F32), shape((2 * count, width), BF16),
            shape((16, width, 128), BF16), shape((2 * count, hidden), BF16), shape((2 * count, hidden), BF16),
            shape((width, 2 * count), BF16), shape((2 * count, width), F32), shape((2 * count, width), F32)]
    return pl.pallas_call(
        front_kernel,
        grid=(heads // 2,),
        in_specs=[smem] + [whole(count, width)] * 3 + [col(count), col(2 * count), col(2 * count), whole(heads, span)] + [whole(width, width)] * 3 + [whole(1, width)] * 3
                 + [whole(2, width)] + [pl.BlockSpec(memory_space=pltpu.HBM)] * 3,
        out_specs=[free] * 13 + [whole(8, width)],
        out_shape=outs + [shape((8, width), F32)],
        scratch_shapes=[pltpu.VMEM(o.shape, o.dtype) for o in outs[:4] + outs[5:]]
                       + [pltpu.VMEM(wo.shape, BF16), pltpu.VMEM(win.shape, BF16), pltpu.VMEM(wback.shape, BF16),
                          pltpu.VMEM((2, 2 * count, 4 * count), BF16), pltpu.VMEM((2, 2 * count, 4 * count), F32),
                          pltpu.VMEM((2, 128, span), F32), pltpu.VMEM((2, 4 * count, 128), BF16), pltpu.SemaphoreType.DMA((16,))],
        name="front", compiler_params=pltpu.CompilerParams(vmem_limit_bytes=38 << 20),
    )(info, far, far_other, near, q_l, k_l, v_l, lines, wq, wk, wv, gain1, gain2, gain3, cots, wo, win, wback)

def through_kernel(info, slopes_h, win_h, mixed_h, steep_h, wo_h, att_h, gain2, grad_mixed_o, grad_attended_o, grad_out_o, rows,
                   slopes, win, mixed, steep, wo, att, grad_mixed, grad_attended, grad_out, sems):
    hidden, width = slopes.shape[1], mixed.shape[1]
    chunks = []
    for i, at in enumerate(range(0, hidden, 512)):
        for a, b, s in ((slopes_h, slopes, i), (win_h, win, 4 + i)):
            chunks.append(pltpu.make_async_copy(a.at[:, at : at + 512], b.at[:, at : at + 512], sems.at[s]))
    copies = [pltpu.make_async_copy(a, b, sems.at[8 + i]) for i, (a, b) in enumerate((
        (mixed_h, mixed), (steep_h, steep), (wo_h, wo), (att_h, att)))]
    outs = [pltpu.make_async_copy(a, b, sems.at[12 + i]) for i, (a, b) in enumerate((
        (grad_mixed, grad_mixed_o), (grad_attended, grad_attended_o), (grad_out, grad_out_o)))]
    for copy in chunks + copies:
        copy.start()
    grad_inner = None
    for i, at in enumerate(range(0, hidden, 512)):
        chunks[2 * i].wait()
        chunks[2 * i + 1].wait()
        part = dot(slopes[:, at : at + 512], win[:, at : at + 512], NT)
        grad_inner = part if grad_inner is None else grad_inner + part
    copies[0].wait()
    copies[1].wait()
    values = mixed[...]
    more, grad_two = norm_back(grad_inner, values, rms_scale(values), gain2[...])
    total = steep[...] + more
    grad_mixed[...] = total
    outs[0].start()
    low = total.astype(BF16)
    copies[2].wait()
    grad_attended[...] = dot(low, wo[...], NT).astype(BF16)
    outs[1].start()
    copies[3].wait()
    grad_out[...] = dot(att[...], low, TN).astype(BF16)
    outs[2].start()
    rows[...] = jnp.concatenate([grad_two, jnp.zeros((7, width), F32)])
    for copy in outs:
        copy.wait()

def through(info, slopes, win, mixed, steep, wo, att, gain2):
    n, width = mixed.shape
    smem, vmem, free = (pl.BlockSpec(memory_space=m) for m in (pltpu.SMEM, pltpu.VMEM, pl.ANY))
    shape = jax.ShapeDtypeStruct
    given = (slopes, win, mixed, steep, wo, att)
    outs = [shape((n, width), F32), shape((n, width), BF16), shape((width, width), BF16)]
    return pl.pallas_call(
        through_kernel,
        in_specs=[smem, free, pl.BlockSpec(memory_space=pltpu.HBM)] + [free] * 4 + [vmem],
        out_specs=[free] * 3 + [vmem],
        out_shape=outs + [shape((8, width), F32)],
        scratch_shapes=[pltpu.VMEM(g.shape, g.dtype) for g in given] + [pltpu.VMEM(o.shape, o.dtype) for o in outs] + [pltpu.SemaphoreType.DMA((15,))],
        name="through", compiler_params=pltpu.CompilerParams(vmem_limit_bytes=16 << 20),
    )(info, *given, gain2)

def meet_kernel(info, got_h, active_h, slopes_h, turned_h, steep_h, *refs):
    outs, (got, chunk, turned, steep, blocks, sems) = refs[:4], refs[4:]
    order = (3, 1, 2, 0)
    high, lowest = (info[6] & 15) >> 2, info[6] & 3
    load = [pltpu.make_async_copy(got_h.at[4 * k : 4 * k + 4], got.at[k], sems.at[k]) for k in range(4)]
    save = [pltpu.make_async_copy(blocks.at[k], outs[k], sems.at[4 + k]) for k in range(4)]

    def columns(source, k):
        at = pl.ds(pl.multiple_of((k ^ high) * 512, 512), 512)
        return pltpu.make_async_copy(source.at[:, at], chunk.at[k], sems.at[8 + k])

    for side, source in ((0, active_h), (1, slopes_h)):
        @pl.when(info[7] == side)
        def _(side=side, source=source):
            extra = pltpu.make_async_copy(*((steep_h, steep) if side == 0 else (turned_h, turned)), sems.at[12])
            extra.start()
            for k in order:
                columns(source, k).start()
                load[k].start()
            extra.wait()
            low = steep[...].astype(BF16) if side == 0 else turned[...]
            for k in order:
                columns(source, k).wait()
                made = dot(chunk[k], low, TN) if side == 0 else dot(low, chunk[k])
                load[k].wait()
                for b in range(4):
                    piece = made[:, b * 128 : (b + 1) * 128]
                    if side == 0:
                        piece = made[b * 128 : (b + 1) * 128]
                        piece = jnp.concatenate([piece[:, q * 128 : (q + 1) * 128] for q in range(4)])
                    to = b ^ lowest
                    blocks[k, to] = (piece + got[k, to].astype(F32)).astype(BF16)
                save[k].start()

    for copy in save:
        copy.wait()

def meet(info, got, active, slopes, turned, steep):
    smem, free = pl.BlockSpec(memory_space=pltpu.SMEM), pl.BlockSpec(memory_space=pl.ANY)
    block = (4,) + got.shape[1:]
    n, width = steep.shape
    return pl.pallas_call(
        meet_kernel,
        in_specs=[smem] + [free] * 5,
        out_specs=[free] * 4,
        out_shape=[jax.ShapeDtypeStruct(block, BF16)] * 4,
        scratch_shapes=[pltpu.VMEM((4,) + block, BF16), pltpu.VMEM((4, n, 512), BF16), pltpu.VMEM(turned.shape, BF16), pltpu.VMEM(steep.shape, F32),
                        pltpu.VMEM((4,) + block, BF16), pltpu.SemaphoreType.DMA((13,))],
        name="meet", compiler_params=pltpu.CompilerParams(vmem_limit_bytes=20 << 20),
    )(info, got, active, slopes, turned, steep)

CLASS = {(0, 0): 0, (1, 2): 0, (0, 1): 1, (1, 3): 1, (0, 2): 2, (0, 3): 3, (1, 0): 4, (1, 1): 5}

def back_kernel(info, ql, qr, kl, kr, vl, vr, gout, out, inv, expo, buckets, dense_rows, through_rows,
                hid_l_h, hid_r_h, near_h, near_other_h, far_h, far_other_h, wq_h, wk_h, wv_h, grad_out_h,
                keep_o, send_o, stay_o, leave_o, small,
                hid_l, hid_r, near, near_other, far, far_other, wq, wk, wv, made,
                keep, send, stay, leave, dq, dk, dv, offsets, sums, acc, slopes, sems):
    count, width = near.shape
    step = pl.program_id(0)
    pairs = width // 128
    late = [pltpu.make_async_copy(a, b, sems.at[i]) for i, (a, b) in enumerate((
        (hid_l_h, hid_l), (hid_r_h, hid_r), (near_h, near), (near_other_h, near_other), (far_h, far), (far_other_h, far_other),
        (wq_h, wq), (wk_h, wk), (wv_h, wv), (grad_out_h, made.at[0:width])))]
    done = [pltpu.make_async_copy(a, b, sems.at[10 + i]) for i, (a, b) in enumerate(((send, send_o), (keep, keep_o), (leave, leave_o), (stay, stay_o)))]

    @pl.when(step == 0)
    def _():
        for copy in late:
            copy.start()

    cols = pl.ds(pl.multiple_of(step * 128, 128), 128)
    lane = lax.broadcasted_iota(jnp.int32, (1, 128), 1)
    starts = [info[1 + b] for b in range(4)]
    keys = jnp.concatenate([kl[...], kr[...]])
    values = jnp.concatenate([vl[...], vr[...]])
    query = jnp.concatenate([ql[...], qr[...]])
    scaled = gout[...].astype(F32) * inv[...]
    prod = scaled * out[...].astype(F32)
    low = scaled.astype(BF16)
    query_t, low_t = query.T, low.T
    grads_q, grads_k, grads_v = None, [], []
    for head in range(2):
        mine = (lane < 64) if head == 0 else (lane >= 64)
        base = 64 if head == 0 else 0
        pick = jnp.where(mine, 1.0, 0.0).astype(BF16)
        delta = jnp.sum(jnp.where(mine, prod, 0.0), axis=1, keepdims=True)
        high = delta.astype(BF16).astype(F32)
        extra = jnp.where(lane == base, high, jnp.where(lane == base + 1, delta - high, 0.0)).astype(BF16)
        grad = low * pick + extra
        minus = jnp.where((lane == base) | (lane == base + 1), -1.0, 0.0).astype(BF16)
        for b in range(4):
            spot = slice(b * count, (b + 1) * count)
            ds = dot(grad, values[spot] * pick + minus, NT) * expo[head, :, spot].astype(F32)
            slopes[head, :, spot] = ds.astype(BF16)
            for chunk in range(2):
                upper, lower = (ds[chunk * count + r * 128 : chunk * count + (r + 1) * 128] for r in range(2))
                group = CLASS[chunk, b]
                block = jnp.concatenate([lower[:, :128], lower[:, 128:] + upper[:, :128], upper[:, 128:]], axis=1)
                if (chunk, b) in ((1, 2), (1, 3)):
                    block = block + sums[head, group]
                sums[head, group] = block
        part = dot(slopes[head], keys * pick)
        grads_q = part if grads_q is None else grads_q + part
        half = slice(head * 64, (head + 1) * 64)
        grads_k.append(dot(query_t[half], slopes[head]))
        grads_v.append(dot(low_t[half], expo[head]))
    dq[:, cols] = grads_q.astype(BF16)
    dk[:, cols] = jnp.concatenate(grads_k).astype(BF16).T
    dv[:, cols] = jnp.concatenate(grads_v).astype(BF16).T
    for head in range(2):
        acc[head] = jnp.zeros(acc.shape[1:], F32)
        for (chunk, b), group in CLASS.items():
            if (chunk, b) not in ((1, 2), (1, 3)):
                at = starts[b] - starts[2 * chunk] + 768
                to = pl.ds(pl.multiple_of(at, 128), 384)
                acc[head, :, to] += sums[head, group]
        rest = acc[head]
        n = 64
        while n >= 8:
            rest = rest[:n] + pltpu.roll(rest[n:], 2048 - n, 1)
            n //= 2
        line = rest[7:8]
        for r in range(6, -1, -1):
            line = rest[r : r + 1] + pltpu.roll(line, 2047, 1)
        offsets[pl.ds(2 * step + head, 1), :] = pltpu.roll(line, 127, 1)

    @pl.when(step == pairs - 1)
    def _():
        for copy in late:
            copy.wait()
        made[width : 2 * width, :] = (dot(hid_l[:count, :], dq[:count, :], TN) + dot(hid_r[:count, :], dq[count:, :], TN)).astype(BF16)
        for at, grads in ((2 * width, dk), (3 * width, dv)):
            made[at : at + width, :] = (dot(hid_l[...], grads[: 2 * count, :], TN) + dot(hid_r[...], grads[2 * count :, :], TN)).astype(BF16)
        me = info[6]
        size = made.shape[0] // 32

        @pl.loop(0, 16)
        def _(r):
            keep[r] = made[pl.ds(pl.multiple_of((r ^ me) * size, size), size), :]
            send[pl.ds(pl.multiple_of(r * size, size), size), :] = made[pl.ds(pl.multiple_of(((r + 16) ^ me) * size, size), size), :]

        gain = jnp.zeros((1, width), F32)
        for b, raw in enumerate((near, near_other, far, far_other)):
            spot = slice(b * count, (b + 1) * count)
            grad = dot(dk[spot, :], wk[...], NT) + dot(dv[spot, :], wv[...], NT)
            half = slice((b // 2) * count, (b // 2 + 1) * count)
            if b % 2 == 0:
                grad = grad + dot(dq[half, :], wq[...], NT)
                stay[half, :] = grad
            else:
                leave[half, :] = grad.astype(BF16)
            tokens = raw[...].astype(F32)
            gain = gain + jnp.sum(grad * (tokens * rms_scale(tokens)), axis=0, keepdims=True)
        leave[2 * count :, :] = two_terms(rows_of(dense_rows[0:1, :]))
        picker = jnp.where(lax.broadcasted_iota(jnp.int32, (128, 1), 0) == buckets[...], 1.0, 0.0).astype(BF16)
        left = offsets[...][:, : buckets.shape[1]]
        bias = None
        for _ in range(3):
            part = left.astype(BF16)
            left = left - part.astype(F32)
            bias = dot(part, picker, NT) if bias is None else bias + dot(part, picker, NT)
        bias = jnp.concatenate([bias, jnp.zeros((bias.shape[0], width - 128), F32)], axis=1)
        line = bias[0:1]
        for h in range(1, bias.shape[0]):
            line = line + pltpu.roll(bias[h : h + 1], 32 * h, 1)
        total = rows_of(gain, through_rows[0:1, :], dense_rows[1:2, :], line)
        small[...] = total
        send[16 * size :, :] = two_terms(total)
        for copy in done:
            copy.start()
        for copy in done:
            copy.wait()

def back(info, ql, qr, kl, kr, vl, vr, gout, out, inv, expo, buckets, dense_rows, through_rows,
         hid_l, hid_r, near, near_other, far, far_other, wq, wk, wv, grad_out):
    count, width = near.shape
    smem, free = pl.BlockSpec(memory_space=pltpu.SMEM), pl.BlockSpec(memory_space=pl.ANY)
    whole = lambda *dims: pl.BlockSpec(dims, lambda g: (0,) * len(dims))
    col = lambda n: pl.BlockSpec((n, 128), lambda g: (0, g))
    shape = jax.ShapeDtypeStruct
    size = 4 * width // 32
    outs = [shape((16, size, width), BF16), shape((16 * size + 16, width), BF16), shape((2 * count, width), F32), shape((2 * count + 16, width), BF16)]
    given = (hid_l, hid_r, near, near_other, far, far_other, wq, wk, wv)
    return pl.pallas_call(
        back_kernel,
        grid=(width // 128,),
        in_specs=[smem, col(count), col(count)] + [col(2 * count)] * 7 + [pl.BlockSpec((2, 2 * count, 4 * count), lambda g: (g, 0, 0)),
                  whole(*buckets.shape), whole(8, width), whole(8, width)] + [free] * 10,
        out_specs=[free] * 4 + [whole(8, width)],
        out_shape=outs + [shape((8, width), F32)],
        scratch_shapes=[pltpu.VMEM(g.shape, BF16) for g in given] + [pltpu.VMEM((4 * width, width), BF16)]
                       + [pltpu.VMEM(o.shape, o.dtype) for o in outs]
                       + [pltpu.VMEM((2 * count, width), BF16), pltpu.VMEM((4 * count, width), BF16), pltpu.VMEM((4 * count, width), BF16),
                          pltpu.VMEM((8, 2048), F32), pltpu.VMEM((2, 6, 128, 384), F32), pltpu.VMEM((2, 128, 2048), F32),
                          pltpu.VMEM((2, 2 * count, 4 * count), BF16), pltpu.SemaphoreType.DMA((14,))],
        name="back", compiler_params=pltpu.CompilerParams(vmem_limit_bytes=44 << 20),
    )(info, ql, qr, kl, kr, vl, vr, gout, out, inv, expo, buckets, dense_rows, through_rows, *given, grad_out)

def ending_kernel(info, stay, came, near, far, grad_mixed, gain, dense_rows, home, away):
    count, width = near.shape
    for part, raw in enumerate((near, far)):
        spot = slice(part * count, (part + 1) * count)
        tokens = raw[...].astype(F32)
        grad = stay[spot, :] + came[spot, :].astype(F32)
        more, _ = norm_back(grad, tokens, rms_scale(tokens), gain[...])
        value = (grad_mixed[spot, :] + more).astype(BF16)
        if part == 0:
            home[:count, :] = value
        else:
            away[:count, :] = value
    alive = (info[0] - info[5]).astype(F32)
    pool = two_terms((rows_of(dense_rows[0:1, :]) + one_value(came[2 * count :, :])) / alive)
    home[count:, :] = pool
    away[count:, :] = pool

def ending(info, stay, came, near, far, grad_mixed, gain, dense_rows):
    count, width = near.shape
    smem, vmem = pl.BlockSpec(memory_space=pltpu.SMEM), pl.BlockSpec(memory_space=pltpu.VMEM)
    shape = jax.ShapeDtypeStruct((count + 16, width), BF16)
    return pl.pallas_call(
        ending_kernel, in_specs=[smem] + [vmem] * 7, out_specs=[vmem] * 2, out_shape=[shape, shape], name="ending", compiler_params=pltpu.CompilerParams(vmem_limit_bytes=10 << 20)
    )(info, stay, came, near, far, grad_mixed, gain, dense_rows)

def place_kernel(firsts, info, *refs):
    parts, (back, front, rows, columns, sems) = refs[: len(firsts)], refs[-5:]
    mine = info[6] & 15
    for side in range(2):
        @pl.when(info[7] == side)
        def _(side=side):
            copies, n = [], 0
            for part, first in zip(parts, firsts):
                for i in range(part.shape[0]):
                    r = first + i
                    to = pl.ds(pl.multiple_of(((r & 15) ^ mine) * 128, 128), 128)
                    if (r >= 16) == (side == 1):
                        for q in range(4):
                            rows[n, :, q * 128 : (q + 1) * 128] = part[i, q * 128 : (q + 1) * 128, :].astype(F32)
                        copies.append(pltpu.make_async_copy(rows.at[n], back.at[to, :], sems.at[n]))
                    else:
                        columns[n] = part[i].astype(F32)
                        copies.append(pltpu.make_async_copy(columns.at[n], front.at[:, to], sems.at[n]))
                    copies[-1].start()
                    n += 1
            for copy in copies:
                copy.wait()

def place(info, parts, made, width):
    smem, vmem, far = (pl.BlockSpec(memory_space=m) for m in (pltpu.SMEM, pltpu.VMEM, pltpu.HBM))
    shape = jax.ShapeDtypeStruct
    count = sum(p.shape[0] for _, p in parts)
    return pl.pallas_call(
        functools.partial(place_kernel, [first for first, _ in parts]),
        in_specs=[smem] + [vmem] * len(parts) + [far] * len(made),
        out_specs=[far] * 2,
        out_shape=[shape((16 * 128, width), F32), shape((width, 16 * 128), F32)],
        scratch_shapes=[pltpu.VMEM((count, 128, width), F32), pltpu.VMEM((count, width, 128), F32), pltpu.SemaphoreType.DMA((count,))],
        input_output_aliases={1 + len(parts) + i: i for i in range(len(made))},
        name="place", compiler_params=pltpu.CompilerParams(vmem_limit_bytes=28 << 20),
    )(info, *[p for _, p in parts], *made)

def sort_kernel(firsts, info, *refs):
    parts, made, (tall, sems) = refs[: len(firsts)], refs[-6:-2], refs[-2:]
    size = parts[0].shape[1]
    mine = info[6]
    pieces = []
    for part, first in zip(parts, firsts):
        for i in range(part.shape[0]):
            tall[len(pieces)] = part[i].astype(F32)
            pieces.append(first + i)
    for top in range(4):
        @pl.when((mine >> 3) == top)
        def _(top=top):
            copies = []
            for n, r in enumerate(pieces):
                to = pl.ds(pl.multiple_of(((r ^ mine) & 7) * size, size), size)
                copies.append(pltpu.make_async_copy(tall.at[n], made[top ^ (r >> 3)].at[to, :], sems.at[n]))
                copies[-1].start()
            for copy in copies:
                copy.wait()

def sort(info, parts, made, width):
    smem, vmem, far = (pl.BlockSpec(memory_space=m) for m in (pltpu.SMEM, pltpu.VMEM, pltpu.HBM))
    shape = jax.ShapeDtypeStruct((width, width), F32)
    count = sum(p.shape[0] for _, p in parts)
    return pl.pallas_call(
        functools.partial(sort_kernel, [first for first, _ in parts]),
        in_specs=[smem] + [vmem] * len(parts) + [far] * len(made),
        out_specs=[far] * 4,
        out_shape=[shape] * 4,
        scratch_shapes=[pltpu.VMEM((count,) + parts[0][1].shape[1:], F32), pltpu.SemaphoreType.DMA((count,))],
        input_output_aliases={1 + len(parts) + i: i for i in range(len(made))},
        name="sort", compiler_params=pltpu.CompilerParams(vmem_limit_bytes=12 << 20),
    )(info, *[p for _, p in parts], *made)

def mix_kernel(*refs):
    for k in range(4):
        refs[4 + k][...] = added(*[term[k] for term in refs[:4]])

def mix(terms):
    block = terms[0].shape[1:]
    vmem = pl.BlockSpec(memory_space=pltpu.VMEM)
    return pl.pallas_call(
        mix_kernel, in_specs=[vmem] * 4, out_specs=[vmem] * 4, out_shape=[jax.ShapeDtypeStruct(block, BF16)] * 4, name="mix", compiler_params=pltpu.CompilerParams(vmem_limit_bytes=10 << 20),
    )(*terms)

def exchange(value, bits):
    size = lax.axis_size("dp") * lax.axis_size("blk")
    return lax.ppermute(value, ("dp", "blk"), [(i, i ^ bits) for i in range(size)])

def wait(*values):
    return lax.optimization_barrier(values)

def added(*terms):
    total = terms[0].astype(F32)
    for term in terms[1:]:
        total = total + term.astype(F32)
    return total.astype(BF16)

def local(inputs, w_query, w_key, w_value, w_out, w_in, w_back, norm1_gain, norm2_gain, final_gain, bias_table, bucket_table, prefix_len, pad_len, pooled_grad):
    rows, width = inputs.shape[1:]
    spot, far_off = lax.axis_index("blk"), lax.axis_index("dp")
    doc, core = spot // 2, spot % 2
    block = [doc * 2 + core, doc * 2 + 1 - core, (1 - doc) * 2 + core, (1 - doc) * 2 + 1 - core]
    line = [8, 16]
    further = [32 << b for b in range((lax.axis_size("dp") // 8).bit_length() - 1)]
    piece = core * 16 + doc * 4 + (far_off % 2) * 8 + (far_off // 2) % 4
    near = jnp.where(doc == 0, inputs[0], inputs[1])
    far_send = jnp.where(doc == 0, inputs[1], inputs[0])
    near, far_send = wait(near, far_send)
    far = exchange(far_send, ROW)
    near_other = exchange(near, CORE)
    slot = jnp.arange(8, dtype=jnp.int32)
    ids = jnp.zeros_like(slot)
    for i, value in enumerate([b * rows for b in block] + [piece, core, doc]):
        ids = jnp.where(slot == i, value, ids)
    gain1, gain2, gain3 = norm1_gain[None, :], norm2_gain[None, :], final_gain[None, :]
    buckets = bucket_table[None, :]
    hid_l, q_l, k_l, v_l, w_query, w_key, w_value = prepare(near, near_other, gain1, w_query, w_key, w_value)
    far, q_l, ids = wait(far, q_l, ids)
    far_other = exchange(far, CORE)
    lines, info = tables(ids, pad_len, prefix_len, bias_table.T, buckets, 4 * rows)
    (hid_r, q_r, k_r, v_r, expo, inverse, attended, send, active, slopes, turned, mixed, steep, dense_rows) = front(
        info, far, far_other, near, q_l, k_l, v_l, lines, w_query, w_key, w_value,
        gain1, gain2, gain3, pooled_grad, w_out, w_in, w_back)

    xy = [ROW, NEAR_X, ROW ^ NEAR_X]
    zz = [line[0], line[1], line[0] ^ line[1]]

    token, send = wait(info, send)
    got = exchange(send, CORE)
    grad_mixed, grad_attended, grad_out_w, through_rows = through(token, slopes, w_in, mixed, steep, w_out, attended, gain2)
    token, through_rows, got = wait(token, through_rows, got)
    stays, *sends = meet(token, got, active, slopes, turned, steep)

    token, sends = wait(token, sends)
    came = [exchange(s, m) for s, m in zip(sends, xy)]
    rest_keep, rest_send, stay, leave, small = back(
        token, q_l, q_r, k_l, k_r, v_l, v_r, grad_attended, attended, inverse, expo, buckets, dense_rows, through_rows,
        hid_l, hid_r, near, near_other, far, far_other, w_query, w_key, w_value, grad_out_w)
    token, small, rest_send, leave, came = wait(token, small, rest_send, leave, came)

    rest_got = exchange(rest_send, CORE)
    hidden_got = exchange(leave, CORE)
    lines = mix([stays] + list(came))
    token, lines = wait(token, lines)
    took = [exchange(lines[k + 1], m) for k, m in enumerate(zz)]
    token, rest_got, hidden_got = wait(token, rest_got, hidden_got)

    count = rest_keep.shape[0] * rest_keep.shape[1]
    small = small + one_value(rest_got[count:])
    rest_got = rest_got[:count].reshape(rest_keep.shape)
    terms = two_terms(small)
    sends = [jnp.concatenate([added(rest_keep[4 * k : 4 * k + 4], rest_got[4 * k : 4 * k + 4]).reshape(-1, width), terms]) for k in (1, 2, 3)]
    token, sends = wait(token, sends)
    rest_came = [exchange(s, m) for s, m in zip(sends, xy)]
    home, away = ending(token, stay, hidden_got, near, far, grad_mixed, gain1, dense_rows)
    token, took, away = wait(token, took, away)

    whole = added(lines[0], *took)
    for bit in further:
        whole = added(whole, exchange(whole, bit))
    token, whole = wait(token, whole)
    back_line = [exchange(whole, m) for m in zz]
    away_got = exchange(away, ROW)
    token, rest_came = wait(token, rest_came)

    count = count // 4
    for part in rest_came:
        small = small + one_value(part[count:])
    rest_came = [part[:count].reshape((4,) + rest_keep.shape[1:]) for part in rest_came]
    piece = count // 4
    lines = added(rest_keep[:4], rest_got[:4], *rest_came).reshape(-1, width)
    send = jnp.concatenate([lines[piece : 2 * piece], lines[3 * piece :], two_terms(small)])
    token, send = wait(token, send)
    took = exchange(send, line[0])
    token, took = wait(token, took)
    small = small + one_value(took[2 * piece :])
    lines = added(jnp.concatenate([lines[:piece], lines[2 * piece : 3 * piece]]), took[: 2 * piece])
    send = jnp.concatenate([lines, two_terms(small)])
    token, send, back_line, away_got = wait(token, send, back_line, away_got)
    took = exchange(send, line[1])

    quarter = jnp.stack([whole] + back_line)
    token, quarter = wait(token, quarter)
    from_y, from_x = exchange(quarter, ROW), exchange(quarter, NEAR_X)
    pool_mine, pool_other = one_value(home[rows:])[:1], one_value(away_got[rows:])[:1]
    pooled = jnp.where(doc == 0, jnp.concatenate([pool_mine, pool_other]), jnp.concatenate([pool_other, pool_mine]))
    home, away_got = home[:rows], away_got[:rows]
    input_grad = jnp.where(doc == 0, jnp.stack([home, away_got]), jnp.stack([away_got, home]))
    token, took, pooled, input_grad = wait(token, took, pooled, input_grad)

    small = small + one_value(took[2 * piece :])
    rest = added(lines, jnp.concatenate([took[piece : 2 * piece], took[:piece]]))
    for bit in further:
        rest = added(rest, exchange(rest, bit))
        small = small + exchange(small, bit)
    token, rest = wait(token, rest)
    rest_back = exchange(rest, line[0])
    outs = [small[0], small[1], small[2], small[3, : bias_table.size].reshape(bias_table.shape[::-1]).T]
    token, from_y, from_x, outs = wait(token, from_y, from_x, outs)

    sends = [from_x[:2], from_y[2:]]
    here = jnp.concatenate([quarter, from_y, from_x])
    token, sends, here = wait(token, sends, here)
    far_a, far_b = exchange(sends[0], ROW), exchange(sends[1], NEAR_X)
    other = exchange(here, CORE)
    grads = place(token, [(0, here)], [], width)
    token, grads, rest_back, far_a, far_b, other = wait(token, grads, rest_back, far_a, far_b, other)

    fourth = jnp.stack([rest[:piece], rest_back[:piece], rest[piece:], rest_back[piece:]])
    far_pair = jnp.concatenate([far_a, far_b])
    token, fourth, far_pair = wait(token, fourth, far_pair)
    fourth_y, fourth_x = exchange(fourth, ROW), exchange(fourth, NEAR_X)
    other_far = exchange(far_pair, CORE)
    grads = place(token, [(12, far_pair), (16, other)], grads, width)
    token, grads, other_far, fourth_y, fourth_x = wait(token, grads, other_far, fourth_y, fourth_x)

    sends = [fourth_x[:2], fourth_y[2:], jnp.concatenate([fourth, fourth_y, fourth_x])]
    token, sends = wait(token, sends)
    last_a, last_b, pair = (exchange(s, m) for s, m in zip(sends, (ROW, NEAR_X, CORE)))
    out_back, out_in = place(token, [(28, other_far)], grads, width)
    token, out_back, out_in, last_a, last_b, pair = wait(token, out_back, out_in, last_a, last_b, pair)

    ends = exchange(jnp.concatenate([last_a, last_b]), CORE)
    made = sort(token, [(0, sends[2]), (12, last_a), (14, last_b), (16, pair)], [], width)
    token, made, ends = wait(token, made, ends)
    out_out, out_query, out_key, out_value = sort(token, [(28, ends)], made, width)
    return (pooled, input_grad, out_query, out_key, out_value, out_out, out_in, out_back, *outs)

def solution(mesh):
    data = P("dp", "blk", None)
    placed = (data,) + (P(),) * 11 + (P("dp"), P("dp"), P("dp", None))
    return jax.shard_map(local, mesh=mesh, in_specs=placed, out_specs=(P("dp", None), data) + (P(),) * 10, check_vma=False)
```

```python
import functools
import jax, jax.numpy as jnp
from jax import lax
from jax.experimental import pallas as pl
from jax.experimental.pallas import tpu as pltpu
from jax.sharding import PartitionSpec as P

F32, BF16 = jnp.float32, jnp.bfloat16
NEG = -1000000000.0
NT = (((1,), (1,)), ((), ()))
TN = (((0,), (0,)), ((), ()))
NN = (((1,), (0,)), ((), ()))

def dot(a, b, dims=NN):
    return lax.dot_general(a, b, dims, preferred_element_type=F32)

def skew(row, width, dtype=F32):
    return pltpu.roll(jnp.broadcast_to(row, (128, width)), width - 127, 1, stride=1, stride_axis=0)


BUCKETS = 32
EPS = 1e-06
CORE, ROW, NEAR_X = 1, 2, 4

def rms_scale(values):
    return lax.rsqrt(jnp.mean(values * values, axis=-1, keepdims=True) + EPS)

def norm_back(grad_out, values, scale, gain):
    weighted = grad_out * gain
    inner = jnp.mean(weighted * values, axis=-1, keepdims=True)
    grad_in = scale * weighted - scale * scale * scale * values * inner
    return grad_in, jnp.sum(grad_out * values * scale, axis=0, keepdims=True)

def two_terms(value):
    high = value.astype(BF16)
    return jnp.concatenate([high, (value - high.astype(F32)).astype(BF16)])

def one_value(terms):
    return terms[:8].astype(F32) + terms[8:16].astype(F32)

def rows_of(*values):
    count = sum(v.shape[0] for v in values)
    return jnp.concatenate(list(values) + [jnp.zeros((8 - count, values[0].shape[1]), F32)])

def prepare_kernel(mine, other, gain, wq_h, wk_h, wv_h, hidden, query, keys, values, wq, wk, wv, sems):
    rows = mine.shape[0]
    load = [pltpu.make_async_copy(a, b, sems.at[i]) for i, (a, b) in enumerate(((wk_h, wk), (wv_h, wv), (wq_h, wq)))]
    for copy in load:
        copy.start()
    for part, raw in enumerate((mine, other)):
        tokens = raw[...].astype(F32)
        hidden[part * rows : (part + 1) * rows, :] = (tokens * rms_scale(tokens) * gain[...]).astype(BF16)
    h = hidden[...]
    load[0].wait()
    keys[...] = dot(h, wk[...]).astype(BF16)
    load[1].wait()
    values[...] = dot(h, wv[...]).astype(BF16)
    load[2].wait()
    query[...] = dot(h[:rows], wq[...]).astype(BF16)

def prepare(mine, other, gain, wq, wk, wv):
    rows, width = mine.shape
    shape = lambda n: jax.ShapeDtypeStruct((n, width), BF16)
    vmem, free = (pl.BlockSpec(memory_space=m) for m in (pltpu.VMEM, pl.ANY))
    return pl.pallas_call(
        prepare_kernel,
        in_specs=[vmem] * 3 + [free] * 3,
        out_specs=[vmem] * 7,
        out_shape=[shape(2 * rows), shape(rows), shape(2 * rows), shape(2 * rows)] + [shape(width)] * 3,
        scratch_shapes=[pltpu.SemaphoreType.DMA((3,))],
        name="prepare", compiler_params=pltpu.CompilerParams(vmem_limit_bytes=14 << 20),
    )(mine, other, gain, wq, wk, wv)

def tables_kernel(ids, pads, prefixes, bias, buckets, lines, info, *, length):
    doc = ids[6]
    info[0] = length - jnp.where(doc == 0, pads[0], pads[1])
    info[5] = jnp.where(doc == 0, prefixes[0], prefixes[1])
    for to, at in enumerate((0, 1, 2, 3)):
        info[1 + to] = ids[at]
    for to, at in enumerate((4, 5, 6)):
        info[6 + to] = ids[at]
    picker = jnp.where(lax.broadcasted_iota(jnp.int32, (BUCKETS, 1), 0) == buckets[...], 1.0, 0.0).astype(BF16)
    left, total = bias[...], None
    for _ in range(3):
        part = left.astype(BF16)
        left = left - part.astype(F32)
        made = dot(part, picker)
        total = made if total is None else total + made
    lines[...] = jnp.zeros_like(lines)
    lines[:, : buckets.shape[1]] = total

def tables(ids, pads, prefixes, bias, buckets, length):
    smem, vmem = pl.BlockSpec(memory_space=pltpu.SMEM), pl.BlockSpec(memory_space=pltpu.VMEM)
    return pl.pallas_call(
        functools.partial(tables_kernel, length=length),
        in_specs=[smem] * 3 + [vmem] * 2,
        out_specs=[vmem, smem],
        out_shape=[jax.ShapeDtypeStruct((bias.shape[0], buckets.shape[1] + 1), F32), jax.ShapeDtypeStruct((16,), jnp.int32)],
        name="tables", compiler_params=pltpu.CompilerParams(vmem_limit_bytes=4 << 20),
    )(ids, pads, prefixes, bias, buckets)

def back_pieces(to, active, low, mine):
    @pl.loop(0, active.shape[1] // 512)
    def _(group):
        made = dot(active[:, pl.ds(pl.multiple_of(group * 512, 512), 512)], low, TN).astype(BF16)
        for b in range(4):
            rows = made[b * 128 : (b + 1) * 128]
            to[(4 * group + b) ^ mine] = jnp.concatenate([rows[:, q * 128 : (q + 1) * 128] for q in range(4)])

def in_pieces(to, slopes, turned, mine):
    @pl.loop(0, slopes.shape[1] // 512)
    def _(group):
        made = dot(turned, slopes[:, pl.ds(pl.multiple_of(group * 512, 512), 512)]).astype(BF16)
        for b in range(4):
            to[(4 * group + b) ^ mine] = made[:, b * 128 : (b + 1) * 128]

def front_kernel(info, far, far_other, near, q_l, k_l, v_l, lines, wq, wk, wv, gain1, gain2, gain3, cots, wo_h, win_h, wback_h,
                 hid_o, q_o, k_o, v_o, expo_o, inv_o, att_o, send_o, active_o, slopes_o, turned_o, mixed_o, steep_o, rows,
                 hid, qs, ks, vs, inv, att, send, active, slopes, turned, mixed, steep, wo, win, wback, expo, scores, skewed, edges, sems):
    count, width = near.shape
    hidden = win.shape[1]
    step = pl.program_id(0)
    late = [pltpu.make_async_copy(a, b, sems.at[i]) for i, (a, b) in enumerate(((wo_h, wo), (win_h, win), (wback_h, wback)))]
    early = [pltpu.make_async_copy(a, b, sems.at[3 + i]) for i, (a, b) in enumerate(((hid, hid_o), (qs, q_o), (ks, k_o), (vs, v_o)))]
    dense = [pltpu.make_async_copy(a, b, sems.at[7 + i]) for i, (a, b) in enumerate((
        (inv, inv_o), (att, att_o), (mixed, mixed_o), (turned, turned_o), (active, active_o), (steep, steep_o), (slopes, slopes_o), (send, send_o)))]
    kept = lambda g: pltpu.make_async_copy(expo, expo_o.at[pl.ds(2 * g, 2)], sems.at[15])

    @pl.when(step == 0)
    def _():
        for copy in late:
            copy.start()
        for part, raw in enumerate((far, far_other)):
            tokens = raw[...].astype(F32)
            hid[part * count : (part + 1) * count, :] = (tokens * rms_scale(tokens) * gain1[...]).astype(BF16)
        h = hid[...]
        qs[...] = dot(h[:count], wq[...]).astype(BF16)
        ks[...] = dot(h, wk[...]).astype(BF16)
        vs[...] = dot(h, wv[...]).astype(BF16)
        for copy in early:
            copy.start()
        column = lax.broadcasted_iota(jnp.int32, (1, 128), 1)
        for b in range(4):
            place = info[1 + b] + lax.broadcasted_iota(jnp.int32, (count, 1), 0)
            gate = jnp.where(place < info[0], 0.0, NEG)
            for head in range(2):
                edges[head, b * count : (b + 1) * count, :] = jnp.where(column == (64 if head == 0 else 0), gate, 0.0).astype(BF16)

    @pl.when(step > 0)
    def _():
        kept(step - 1).wait()

    cols = pl.ds(pl.multiple_of(step * 128, 128), 128)
    lane = lax.broadcasted_iota(jnp.int32, (1, 128), 1)
    first = lane < 64
    limit = info[0]
    starts = [info[1 + b] for b in range(4)]
    keys = [k_l[:count, :], k_l[count:, :], ks[:count, cols], ks[count:, cols]]
    values = jnp.concatenate([v_l[...], vs[:, cols]])
    query = jnp.concatenate([q_l[...], qs[:, cols]])
    made = []
    for head in range(2):
        mine = jnp.where(first if head == 0 else lane >= 64, 1.0, 0.0).astype(BF16)
        one = jnp.where(lane == (64 if head == 0 else 0), 1.0, 0.0).astype(BF16)
        q = query * mine + one
        v = values * mine + one
        skewed[head] = skew(lines[pl.ds(2 * step + head, 1), :], lines.shape[1])
        k = jnp.concatenate(keys) * mine + edges[head]
        for half in range(2):
            s = dot(q[half * 256 : (half + 1) * 256], k, NT)
            for r in range(2):
                for b in range(4):
                    at = starts[b] - starts[2 * half] + 896 - 128 * r
                    part = s[r * 128 : (r + 1) * 128, b * 256 : (b + 1) * 256] + skewed[head, :, pl.ds(pl.multiple_of(at, 128), 256)]
                    scores[head, half * 256 + r * 128 : half * 256 + (r + 1) * 128, b * 256 : (b + 1) * 256] = part
        accs = []
        for r in range(4):
            rs = slice(r * 128, (r + 1) * 128)
            value = scores[head, rs, :]
            top = jnp.max(value, axis=1, keepdims=True)
            e = jnp.exp(value - top).astype(BF16)
            expo[head, rs, :] = e
            accs.append(dot(e, v))
        acc = jnp.concatenate(accs)
        made.append((acc, 1.0 / (acc[:, 64:65] if head == 0 else acc[:, 0:1])))
    (a0, i0), (a1, i1) = made
    scale = jnp.where(first, i0, i1)
    att[:, cols] = (jnp.where(first, a0, a1) * scale).astype(BF16)
    inv[:, cols] = scale
    kept(step).start()

    @pl.when(step == 3)
    def _():
        for copy in late:
            copy.wait()
        dense[0].start()
        dense[1].start()
        for part, raw in enumerate((near, far)):
            spot = slice(part * count, (part + 1) * count)
            mixed[spot, :] = raw[...].astype(F32) + dot(att[spot, :], wo[...])
        dense[2].start()
        values = mixed[...]
        inner = (values * rms_scale(values) * gain2[...]).astype(BF16)
        turned[...] = inner.T
        dense[3].start()
        total = values
        for at in range(0, hidden, 512):
            lifted = jnp.maximum(dot(inner, win[:, at : at + 512]), 0.0).astype(BF16)
            active[:, at : at + 512] = lifted
            total = total + dot(lifted, wback[at : at + 512, :])
        dense[4].start()
        scale = rms_scale(total)
        place = lax.broadcasted_iota(jnp.int32, (2 * count, 1), 0)
        place = jnp.where(place < count, place + info[1], place + (info[3] - count))
        live = jnp.where((place >= info[5]) & (place < limit), 1.0, 0.0)
        pool = jnp.sum(total * scale * gain3[...] * live, axis=0, keepdims=True)
        cot = jnp.where(info[8] == 0, cots[0:1, :], cots[1:2, :]) / (limit - info[5]).astype(F32)
        slope, grad_end = norm_back(live * cot, total, scale, gain3[...])
        steep[...] = slope
        dense[5].start()
        rows[...] = jnp.concatenate([pool, grad_end, jnp.zeros((6, width), F32)])
        low = slope.astype(BF16)
        for at in range(0, hidden, 512):
            through = dot(low, wback[at : at + 512, :], NT).astype(BF16)
            slopes[:, at : at + 512] = jnp.where(active[:, at : at + 512] > 0, through, jnp.zeros_like(through))
        dense[6].start()
        mine = info[6] & 15

        @pl.when(info[7] == 0)
        def _():
            in_pieces(send, slopes, turned[...], mine)

        @pl.when(info[7] == 1)
        def _():
            back_pieces(send, active, steep[...].astype(BF16), mine)

        dense[7].start()
        for copy in early + dense:
            copy.wait()
        kept(step).wait()

def front(info, far, far_other, near, q_l, k_l, v_l, lines, wq, wk, wv, gain1, gain2, gain3, cots, wo, win, wback):
    count, width = near.shape
    hidden = win.shape[1]
    heads, span = lines.shape
    shape = jax.ShapeDtypeStruct
    smem, free = pl.BlockSpec(memory_space=pltpu.SMEM), pl.BlockSpec(memory_space=pl.ANY)
    whole = lambda *dims: pl.BlockSpec(dims, lambda g: (0,) * len(dims))
    col = lambda n: pl.BlockSpec((n, 128), lambda g: (0, g))
    outs = [shape((2 * count, width), BF16), shape((count, width), BF16), shape((2 * count, width), BF16), shape((2 * count, width), BF16),
            shape((heads, 2 * count, 4 * count), BF16), shape((2 * count, width), F32), shape((2 * count, width), BF16),
            shape((16, width, 128), BF16), shape((2 * count, hidden), BF16), shape((2 * count, hidden), BF16),
            shape((width, 2 * count), BF16), shape((2 * count, width), F32), shape((2 * count, width), F32)]
    return pl.pallas_call(
        front_kernel,
        grid=(heads // 2,),
        in_specs=[smem] + [whole(count, width)] * 3 + [col(count), col(2 * count), col(2 * count), whole(heads, span)] + [whole(width, width)] * 3 + [whole(1, width)] * 3
                 + [whole(2, width)] + [pl.BlockSpec(memory_space=pltpu.HBM)] * 3,
        out_specs=[free] * 13 + [whole(8, width)],
        out_shape=outs + [shape((8, width), F32)],
        scratch_shapes=[pltpu.VMEM(o.shape, o.dtype) for o in outs[:4] + outs[5:]]
                       + [pltpu.VMEM(wo.shape, BF16), pltpu.VMEM(win.shape, BF16), pltpu.VMEM(wback.shape, BF16),
                          pltpu.VMEM((2, 2 * count, 4 * count), BF16), pltpu.VMEM((2, 2 * count, 4 * count), F32),
                          pltpu.VMEM((2, 128, span), F32), pltpu.VMEM((2, 4 * count, 128), BF16), pltpu.SemaphoreType.DMA((16,))],
        name="front", compiler_params=pltpu.CompilerParams(vmem_limit_bytes=38 << 20),
    )(info, far, far_other, near, q_l, k_l, v_l, lines, wq, wk, wv, gain1, gain2, gain3, cots, wo, win, wback)

def inner_kernel(info, slopes, win, grad_inner):
    total = None
    for at in range(0, slopes.shape[1], 512):
        part = dot(slopes[:, at : at + 512], win[:, at : at + 512], NT)
        total = part if total is None else total + part
    grad_inner[...] = total

def inner(info, slopes, win):
    smem, vmem = pl.BlockSpec(memory_space=pltpu.SMEM), pl.BlockSpec(memory_space=pltpu.VMEM)
    return pl.pallas_call(
        inner_kernel, in_specs=[smem, vmem, vmem], out_specs=vmem,
        out_shape=jax.ShapeDtypeStruct((slopes.shape[0], win.shape[0]), F32), name="inner", compiler_params=pltpu.CompilerParams(vmem_limit_bytes=10 << 20),
    )(info, slopes, win)

def through_kernel(info, grad_inner, mixed, steep, wo, att, gain2, grad_mixed, grad_attended, grad_out, rows):
    values = mixed[...]
    more, grad_two = norm_back(grad_inner[...], values, rms_scale(values), gain2[...])
    total = steep[...] + more
    grad_mixed[...] = total
    low = total.astype(BF16)
    grad_attended[...] = dot(low, wo[...], NT).astype(BF16)
    grad_out[...] = dot(att[...], low, TN).astype(BF16)
    rows[...] = jnp.concatenate([grad_two, jnp.zeros((7, low.shape[1]), F32)])

def through(info, grad_inner, mixed, steep, wo, att, gain2):
    n, width = mixed.shape
    smem, vmem = pl.BlockSpec(memory_space=pltpu.SMEM), pl.BlockSpec(memory_space=pltpu.VMEM)
    shape = jax.ShapeDtypeStruct
    return pl.pallas_call(
        through_kernel,
        in_specs=[smem] + [vmem] * 6,
        out_specs=[vmem] * 4,
        out_shape=[shape((n, width), F32), shape((n, width), BF16), shape((width, width), BF16), shape((8, width), F32)],
        name="through", compiler_params=pltpu.CompilerParams(vmem_limit_bytes=16 << 20),
    )(info, grad_inner, mixed, steep, wo, att, gain2)

def stay_kernel(info, active, slopes, turned, steep, blocks):
    high, lowest = (info[6] & 15) >> 2, info[6] & 3
    for side in range(2):
        @pl.when(info[7] == side)
        def _(side=side):
            low = steep[...].astype(BF16) if side == 0 else turned[...]
            for k in range(4):
                at = pl.ds(pl.multiple_of((k ^ high) * 512, 512), 512)
                made = dot(active[:, at], low, TN) if side == 0 else dot(low, slopes[:, at])
                for b in range(4):
                    piece = made[:, b * 128 : (b + 1) * 128]
                    if side == 0:
                        piece = made[b * 128 : (b + 1) * 128]
                        piece = jnp.concatenate([piece[:, q * 128 : (q + 1) * 128] for q in range(4)])
                    blocks[k, b ^ lowest] = piece.astype(BF16)

def stay_half(info, active, slopes, turned, steep):
    smem, vmem = pl.BlockSpec(memory_space=pltpu.SMEM), pl.BlockSpec(memory_space=pltpu.VMEM)
    width = steep.shape[1]
    return pl.pallas_call(
        stay_kernel, in_specs=[smem] + [vmem] * 4, out_specs=vmem,
        out_shape=jax.ShapeDtypeStruct((4, 4, width, 128), BF16), name="stay", compiler_params=pltpu.CompilerParams(vmem_limit_bytes=12 << 20),
    )(info, active, slopes, turned, steep)

def meet_kernel(kept, got, *outs):
    for k in (3, 1, 2, 0):
        outs[k][...] = added(kept[k], got[4 * k : 4 * k + 4])

def meet(kept, got):
    vmem = pl.BlockSpec(memory_space=pltpu.VMEM)
    return pl.pallas_call(
        meet_kernel, in_specs=[vmem] * 2, out_specs=[vmem] * 4, out_shape=[jax.ShapeDtypeStruct(kept.shape[1:], BF16)] * 4, name="meet", compiler_params=pltpu.CompilerParams(vmem_limit_bytes=20 << 20),
    )(kept, got)

CLASS = {(0, 0): 0, (1, 2): 0, (0, 1): 1, (1, 3): 1, (0, 2): 2, (0, 3): 3, (1, 0): 4, (1, 1): 5}

def back_kernel(info, ql, qr, kl, kr, vl, vr, gout, out, inv, expo, buckets, dense_rows, through_rows,
                hid_l_h, hid_r_h, near_h, near_other_h, far_h, far_other_h, wq_h, wk_h, wv_h, grad_out_h,
                keep_o, send_o, stay_o, leave_o, small,
                hid_l, hid_r, near, near_other, far, far_other, wq, wk, wv, made,
                keep, send, stay, leave, dq, dk, dv, offsets, sums, acc, slopes, sems):
    count, width = near.shape
    step = pl.program_id(0)
    pairs = width // 128
    late = [pltpu.make_async_copy(a, b, sems.at[i]) for i, (a, b) in enumerate((
        (hid_l_h, hid_l), (hid_r_h, hid_r), (near_h, near), (near_other_h, near_other), (far_h, far), (far_other_h, far_other),
        (wq_h, wq), (wk_h, wk), (wv_h, wv), (grad_out_h, made.at[0:width])))]
    done = [pltpu.make_async_copy(a, b, sems.at[10 + i]) for i, (a, b) in enumerate(((send, send_o), (keep, keep_o), (leave, leave_o), (stay, stay_o)))]

    @pl.when(step == 0)
    def _():
        for copy in late:
            copy.start()

    cols = pl.ds(pl.multiple_of(step * 128, 128), 128)
    lane = lax.broadcasted_iota(jnp.int32, (1, 128), 1)
    starts = [info[1 + b] for b in range(4)]
    keys = jnp.concatenate([kl[...], kr[...]])
    values = jnp.concatenate([vl[...], vr[...]])
    query = jnp.concatenate([ql[...], qr[...]])
    scaled = gout[...].astype(F32) * inv[...]
    prod = scaled * out[...].astype(F32)
    low = scaled.astype(BF16)
    query_t, low_t = query.T, low.T
    grads_q, grads_k, grads_v = None, [], []
    for head in range(2):
        mine = (lane < 64) if head == 0 else (lane >= 64)
        base = 64 if head == 0 else 0
        pick = jnp.where(mine, 1.0, 0.0).astype(BF16)
        delta = jnp.sum(jnp.where(mine, prod, 0.0), axis=1, keepdims=True)
        high = delta.astype(BF16).astype(F32)
        extra = jnp.where(lane == base, high, jnp.where(lane == base + 1, delta - high, 0.0)).astype(BF16)
        grad = low * pick + extra
        minus = jnp.where((lane == base) | (lane == base + 1), -1.0, 0.0).astype(BF16)
        for b in range(4):
            spot = slice(b * count, (b + 1) * count)
            ds = dot(grad, values[spot] * pick + minus, NT) * expo[head, :, spot].astype(F32)
            slopes[head, :, spot] = ds.astype(BF16)
            for chunk in range(2):
                upper, lower = (ds[chunk * count + r * 128 : chunk * count + (r + 1) * 128] for r in range(2))
                group = CLASS[chunk, b]
                block = jnp.concatenate([lower[:, :128], lower[:, 128:] + upper[:, :128], upper[:, 128:]], axis=1)
                if (chunk, b) in ((1, 2), (1, 3)):
                    block = block + sums[head, group]
                sums[head, group] = block
        part = dot(slopes[head], keys * pick)
        grads_q = part if grads_q is None else grads_q + part
        half = slice(head * 64, (head + 1) * 64)
        grads_k.append(dot(query_t[half], slopes[head]))
        grads_v.append(dot(low_t[half], expo[head]))
    dq[:, cols] = grads_q.astype(BF16)
    dk[:, cols] = jnp.concatenate(grads_k).astype(BF16).T
    dv[:, cols] = jnp.concatenate(grads_v).astype(BF16).T
    for head in range(2):
        acc[head] = jnp.zeros(acc.shape[1:], F32)
        for (chunk, b), group in CLASS.items():
            if (chunk, b) not in ((1, 2), (1, 3)):
                at = starts[b] - starts[2 * chunk] + 768
                to = pl.ds(pl.multiple_of(at, 128), 384)
                acc[head, :, to] += sums[head, group]
        rest = acc[head]
        n = 64
        while n >= 8:
            rest = rest[:n] + pltpu.roll(rest[n:], 2048 - n, 1)
            n //= 2
        line = rest[7:8]
        for r in range(6, -1, -1):
            line = rest[r : r + 1] + pltpu.roll(line, 2047, 1)
        offsets[pl.ds(2 * step + head, 1), :] = pltpu.roll(line, 127, 1)

    @pl.when(step == pairs - 1)
    def _():
        for copy in late:
            copy.wait()
        made[width : 2 * width, :] = (dot(hid_l[:count, :], dq[:count, :], TN) + dot(hid_r[:count, :], dq[count:, :], TN)).astype(BF16)
        for at, grads in ((2 * width, dk), (3 * width, dv)):
            made[at : at + width, :] = (dot(hid_l[...], grads[: 2 * count, :], TN) + dot(hid_r[...], grads[2 * count :, :], TN)).astype(BF16)
        me = info[6]
        size = made.shape[0] // 32

        @pl.loop(0, 16)
        def _(r):
            keep[r] = made[pl.ds(pl.multiple_of((r ^ me) * size, size), size), :]
            send[pl.ds(pl.multiple_of(r * size, size), size), :] = made[pl.ds(pl.multiple_of(((r + 16) ^ me) * size, size), size), :]

        gain = jnp.zeros((1, width), F32)
        for b, raw in enumerate((near, near_other, far, far_other)):
            spot = slice(b * count, (b + 1) * count)
            grad = dot(dk[spot, :], wk[...], NT) + dot(dv[spot, :], wv[...], NT)
            half = slice((b // 2) * count, (b // 2 + 1) * count)
            if b % 2 == 0:
                grad = grad + dot(dq[half, :], wq[...], NT)
                stay[half, :] = grad
            else:
                leave[half, :] = grad.astype(BF16)
            tokens = raw[...].astype(F32)
            gain = gain + jnp.sum(grad * (tokens * rms_scale(tokens)), axis=0, keepdims=True)
        leave[2 * count :, :] = two_terms(rows_of(dense_rows[0:1, :]))
        picker = jnp.where(lax.broadcasted_iota(jnp.int32, (128, 1), 0) == buckets[...], 1.0, 0.0).astype(BF16)
        left = offsets[...][:, : buckets.shape[1]]
        bias = None
        for _ in range(3):
            part = left.astype(BF16)
            left = left - part.astype(F32)
            bias = dot(part, picker, NT) if bias is None else bias + dot(part, picker, NT)
        bias = jnp.concatenate([bias, jnp.zeros((bias.shape[0], width - 128), F32)], axis=1)
        line = bias[0:1]
        for h in range(1, bias.shape[0]):
            line = line + pltpu.roll(bias[h : h + 1], 32 * h, 1)
        total = rows_of(gain, through_rows[0:1, :], dense_rows[1:2, :], line)
        small[...] = total
        send[16 * size :, :] = two_terms(total)
        for copy in done:
            copy.start()
        for copy in done:
            copy.wait()

def back(info, ql, qr, kl, kr, vl, vr, gout, out, inv, expo, buckets, dense_rows, through_rows,
         hid_l, hid_r, near, near_other, far, far_other, wq, wk, wv, grad_out):
    count, width = near.shape
    smem, free = pl.BlockSpec(memory_space=pltpu.SMEM), pl.BlockSpec(memory_space=pl.ANY)
    whole = lambda *dims: pl.BlockSpec(dims, lambda g: (0,) * len(dims))
    col = lambda n: pl.BlockSpec((n, 128), lambda g: (0, g))
    shape = jax.ShapeDtypeStruct
    size = 4 * width // 32
    outs = [shape((16, size, width), BF16), shape((16 * size + 16, width), BF16), shape((2 * count, width), F32), shape((2 * count + 16, width), BF16)]
    given = (hid_l, hid_r, near, near_other, far, far_other, wq, wk, wv)
    return pl.pallas_call(
        back_kernel,
        grid=(width // 128,),
        in_specs=[smem, col(count), col(count)] + [col(2 * count)] * 7 + [pl.BlockSpec((2, 2 * count, 4 * count), lambda g: (g, 0, 0)),
                  whole(*buckets.shape), whole(8, width), whole(8, width)] + [free] * 10,
        out_specs=[free] * 4 + [whole(8, width)],
        out_shape=outs + [shape((8, width), F32)],
        scratch_shapes=[pltpu.VMEM(g.shape, BF16) for g in given] + [pltpu.VMEM((4 * width, width), BF16)]
                       + [pltpu.VMEM(o.shape, o.dtype) for o in outs]
                       + [pltpu.VMEM((2 * count, width), BF16), pltpu.VMEM((4 * count, width), BF16), pltpu.VMEM((4 * count, width), BF16),
                          pltpu.VMEM((8, 2048), F32), pltpu.VMEM((2, 6, 128, 384), F32), pltpu.VMEM((2, 128, 2048), F32),
                          pltpu.VMEM((2, 2 * count, 4 * count), BF16), pltpu.SemaphoreType.DMA((14,))],
        name="back", compiler_params=pltpu.CompilerParams(vmem_limit_bytes=44 << 20),
    )(info, ql, qr, kl, kr, vl, vr, gout, out, inv, expo, buckets, dense_rows, through_rows, *given, grad_out)

def ending_kernel(info, stay, came, near, far, grad_mixed, gain, dense_rows, home, away):
    count, width = near.shape
    for part, raw in enumerate((near, far)):
        spot = slice(part * count, (part + 1) * count)
        tokens = raw[...].astype(F32)
        grad = stay[spot, :] + came[spot, :].astype(F32)
        more, _ = norm_back(grad, tokens, rms_scale(tokens), gain[...])
        value = (grad_mixed[spot, :] + more).astype(BF16)
        if part == 0:
            home[:count, :] = value
        else:
            away[:count, :] = value
    alive = (info[0] - info[5]).astype(F32)
    pool = two_terms((rows_of(dense_rows[0:1, :]) + one_value(came[2 * count :, :])) / alive)
    home[count:, :] = pool
    away[count:, :] = pool

def ending(info, stay, came, near, far, grad_mixed, gain, dense_rows):
    count, width = near.shape
    smem, vmem = pl.BlockSpec(memory_space=pltpu.SMEM), pl.BlockSpec(memory_space=pltpu.VMEM)
    shape = jax.ShapeDtypeStruct((count + 16, width), BF16)
    return pl.pallas_call(
        ending_kernel, in_specs=[smem] + [vmem] * 7, out_specs=[vmem] * 2, out_shape=[shape, shape], name="ending", compiler_params=pltpu.CompilerParams(vmem_limit_bytes=10 << 20)
    )(info, stay, came, near, far, grad_mixed, gain, dense_rows)

def place_kernel(firsts, info, *refs):
    parts, (back, front, rows, columns, sems) = refs[: len(firsts)], refs[-5:]
    mine = info[6] & 15
    for side in range(2):
        @pl.when(info[7] == side)
        def _(side=side):
            copies, n = [], 0
            for part, first in zip(parts, firsts):
                for i in range(part.shape[0]):
                    r = first + i
                    to = pl.ds(pl.multiple_of(((r & 15) ^ mine) * 128, 128), 128)
                    if (r >= 16) == (side == 1):
                        for q in range(4):
                            rows[n, :, q * 128 : (q + 1) * 128] = part[i, q * 128 : (q + 1) * 128, :].astype(F32)
                        copies.append(pltpu.make_async_copy(rows.at[n], back.at[to, :], sems.at[n]))
                    else:
                        columns[n] = part[i].astype(F32)
                        copies.append(pltpu.make_async_copy(columns.at[n], front.at[:, to], sems.at[n]))
                    copies[-1].start()
                    n += 1
            for copy in copies:
                copy.wait()

def place(info, parts, made, width):
    smem, vmem, far = (pl.BlockSpec(memory_space=m) for m in (pltpu.SMEM, pltpu.VMEM, pltpu.HBM))
    shape = jax.ShapeDtypeStruct
    count = sum(p.shape[0] for _, p in parts)
    return pl.pallas_call(
        functools.partial(place_kernel, [first for first, _ in parts]),
        in_specs=[smem] + [vmem] * len(parts) + [far] * len(made),
        out_specs=[far] * 2,
        out_shape=[shape((16 * 128, width), F32), shape((width, 16 * 128), F32)],
        scratch_shapes=[pltpu.VMEM((count, 128, width), F32), pltpu.VMEM((count, width, 128), F32), pltpu.SemaphoreType.DMA((count,))],
        input_output_aliases={1 + len(parts) + i: i for i in range(len(made))},
        name="place", compiler_params=pltpu.CompilerParams(vmem_limit_bytes=28 << 20),
    )(info, *[p for _, p in parts], *made)

def sort_kernel(firsts, info, *refs):
    parts, made, (tall, sems) = refs[: len(firsts)], refs[-6:-2], refs[-2:]
    size = parts[0].shape[1]
    mine = info[6]
    pieces = []
    for part, first in zip(parts, firsts):
        for i in range(part.shape[0]):
            tall[len(pieces)] = part[i].astype(F32)
            pieces.append(first + i)
    for top in range(4):
        @pl.when((mine >> 3) == top)
        def _(top=top):
            copies = []
            for n, r in enumerate(pieces):
                to = pl.ds(pl.multiple_of(((r ^ mine) & 7) * size, size), size)
                copies.append(pltpu.make_async_copy(tall.at[n], made[top ^ (r >> 3)].at[to, :], sems.at[n]))
                copies[-1].start()
            for copy in copies:
                copy.wait()

def sort(info, parts, made, width):
    smem, vmem, far = (pl.BlockSpec(memory_space=m) for m in (pltpu.SMEM, pltpu.VMEM, pltpu.HBM))
    shape = jax.ShapeDtypeStruct((width, width), F32)
    count = sum(p.shape[0] for _, p in parts)
    return pl.pallas_call(
        functools.partial(sort_kernel, [first for first, _ in parts]),
        in_specs=[smem] + [vmem] * len(parts) + [far] * len(made),
        out_specs=[far] * 4,
        out_shape=[shape] * 4,
        scratch_shapes=[pltpu.VMEM((count,) + parts[0][1].shape[1:], F32), pltpu.SemaphoreType.DMA((count,))],
        input_output_aliases={1 + len(parts) + i: i for i in range(len(made))},
        name="sort", compiler_params=pltpu.CompilerParams(vmem_limit_bytes=12 << 20),
    )(info, *[p for _, p in parts], *made)

def mix_kernel(*refs):
    for k in range(4):
        refs[4 + k][...] = added(*[term[k] for term in refs[:4]])

def mix(terms):
    block = terms[0].shape[1:]
    vmem = pl.BlockSpec(memory_space=pltpu.VMEM)
    return pl.pallas_call(
        mix_kernel, in_specs=[vmem] * 4, out_specs=[vmem] * 4, out_shape=[jax.ShapeDtypeStruct(block, BF16)] * 4, name="mix", compiler_params=pltpu.CompilerParams(vmem_limit_bytes=10 << 20),
    )(*terms)

def exchange(value, bits):
    size = lax.axis_size("dp") * lax.axis_size("blk")
    return lax.ppermute(value, ("dp", "blk"), [(i, i ^ bits) for i in range(size)])

def wait(*values):
    return lax.optimization_barrier(values)

def added(*terms):
    total = terms[0].astype(F32)
    for term in terms[1:]:
        total = total + term.astype(F32)
    return total.astype(BF16)

def local(inputs, w_query, w_key, w_value, w_out, w_in, w_back, norm1_gain, norm2_gain, final_gain, bias_table, bucket_table, prefix_len, pad_len, pooled_grad):
    rows, width = inputs.shape[1:]
    spot, far_off = lax.axis_index("blk"), lax.axis_index("dp")
    doc, core = spot // 2, spot % 2
    block = [doc * 2 + core, doc * 2 + 1 - core, (1 - doc) * 2 + core, (1 - doc) * 2 + 1 - core]
    line = [8, 16]
    further = [32 << b for b in range((lax.axis_size("dp") // 8).bit_length() - 1)]
    piece = core * 16 + doc * 4 + (far_off % 2) * 8 + (far_off // 2) % 4
    near = jnp.where(doc == 0, inputs[0], inputs[1])
    far_send = jnp.where(doc == 0, inputs[1], inputs[0])
    near, far_send = wait(near, far_send)
    far = exchange(far_send, ROW)
    near_other = exchange(near, CORE)
    slot = jnp.arange(8, dtype=jnp.int32)
    ids = jnp.zeros_like(slot)
    for i, value in enumerate([b * rows for b in block] + [piece, core, doc]):
        ids = jnp.where(slot == i, value, ids)
    gain1, gain2, gain3 = norm1_gain[None, :], norm2_gain[None, :], final_gain[None, :]
    buckets = bucket_table[None, :]
    hid_l, q_l, k_l, v_l, w_query, w_key, w_value = prepare(near, near_other, gain1, w_query, w_key, w_value)
    far, q_l, ids = wait(far, q_l, ids)
    far_other = exchange(far, CORE)
    lines, info = tables(ids, pad_len, prefix_len, bias_table.T, buckets, 4 * rows)
    (hid_r, q_r, k_r, v_r, expo, inverse, attended, send, active, slopes, turned, mixed, steep, dense_rows) = front(
        info, far, far_other, near, q_l, k_l, v_l, lines, w_query, w_key, w_value,
        gain1, gain2, gain3, pooled_grad, w_out, w_in, w_back)

    xy = [ROW, NEAR_X, ROW ^ NEAR_X]
    zz = [line[0], line[1], line[0] ^ line[1]]

    token, send = wait(info, send)
    got = exchange(send, CORE)
    kept = stay_half(token, active, slopes, turned, steep)
    token, kept = wait(token, kept)
    grad_inner = inner(token, slopes, w_in)
    token, grad_inner, got = wait(token, grad_inner, got)
    stays, *sends = meet(kept, got)

    token, sends, grad_inner = wait(token, sends, grad_inner)
    came = [exchange(s, m) for s, m in zip(sends, xy)]
    grad_mixed, grad_attended, grad_out_w, through_rows = through(token, grad_inner, mixed, steep, w_out, attended, gain2)
    token, through_rows = wait(token, through_rows)
    rest_keep, rest_send, stay, leave, small = back(
        token, q_l, q_r, k_l, k_r, v_l, v_r, grad_attended, attended, inverse, expo, buckets, dense_rows, through_rows,
        hid_l, hid_r, near, near_other, far, far_other, w_query, w_key, w_value, grad_out_w)
    token, small, rest_send, leave, came = wait(token, small, rest_send, leave, came)

    rest_got = exchange(rest_send, CORE)
    hidden_got = exchange(leave, CORE)
    lines = mix([stays] + list(came))
    token, lines = wait(token, lines)
    took = [exchange(lines[k + 1], m) for k, m in enumerate(zz)]
    token, rest_got, hidden_got = wait(token, rest_got, hidden_got)

    count = rest_keep.shape[0] * rest_keep.shape[1]
    small = small + one_value(rest_got[count:])
    rest_got = rest_got[:count].reshape(rest_keep.shape)
    terms = two_terms(small)
    sends = [jnp.concatenate([added(rest_keep[4 * k : 4 * k + 4], rest_got[4 * k : 4 * k + 4]).reshape(-1, width), terms]) for k in (1, 2, 3)]
    token, sends = wait(token, sends)
    rest_came = [exchange(s, m) for s, m in zip(sends, xy)]
    home, away = ending(token, stay, hidden_got, near, far, grad_mixed, gain1, dense_rows)
    token, took, away = wait(token, took, away)

    whole = added(lines[0], *took)
    for bit in further:
        whole = added(whole, exchange(whole, bit))
    token, whole = wait(token, whole)
    back_line = [exchange(whole, m) for m in zz]
    away_got = exchange(away, ROW)
    token, rest_came = wait(token, rest_came)

    count = count // 4
    for part in rest_came:
        small = small + one_value(part[count:])
    rest_came = [part[:count].reshape((4,) + rest_keep.shape[1:]) for part in rest_came]
    piece = count // 4
    lines = added(rest_keep[:4], rest_got[:4], *rest_came).reshape(-1, width)
    send = jnp.concatenate([lines[piece : 2 * piece], lines[3 * piece :], two_terms(small)])
    token, send = wait(token, send)
    took = exchange(send, line[0])
    token, took = wait(token, took)
    small = small + one_value(took[2 * piece :])
    lines = added(jnp.concatenate([lines[:piece], lines[2 * piece : 3 * piece]]), took[: 2 * piece])
    send = jnp.concatenate([lines, two_terms(small)])
    token, send, back_line, away_got = wait(token, send, back_line, away_got)
    took = exchange(send, line[1])

    quarter = jnp.stack([whole] + back_line)
    token, quarter = wait(token, quarter)
    from_y, from_x = exchange(quarter, ROW), exchange(quarter, NEAR_X)
    pool_mine, pool_other = one_value(home[rows:])[:1], one_value(away_got[rows:])[:1]
    pooled = jnp.where(doc == 0, jnp.concatenate([pool_mine, pool_other]), jnp.concatenate([pool_other, pool_mine]))
    home, away_got = home[:rows], away_got[:rows]
    input_grad = jnp.where(doc == 0, jnp.stack([home, away_got]), jnp.stack([away_got, home]))
    token, took, pooled, input_grad = wait(token, took, pooled, input_grad)

    small = small + one_value(took[2 * piece :])
    rest = added(lines, jnp.concatenate([took[piece : 2 * piece], took[:piece]]))
    for bit in further:
        rest = added(rest, exchange(rest, bit))
        small = small + exchange(small, bit)
    token, rest = wait(token, rest)
    rest_back = exchange(rest, line[0])
    outs = [small[0], small[1], small[2], small[3, : bias_table.size].reshape(bias_table.shape[::-1]).T]
    token, from_y, from_x, outs = wait(token, from_y, from_x, outs)

    sends = [from_x[:2], from_y[2:]]
    here = jnp.concatenate([quarter, from_y, from_x])
    token, sends, here = wait(token, sends, here)
    far_a, far_b = exchange(sends[0], ROW), exchange(sends[1], NEAR_X)
    other = exchange(here, CORE)
    grads = place(token, [(0, here)], [], width)
    token, grads, rest_back, far_a, far_b, other = wait(token, grads, rest_back, far_a, far_b, other)

    fourth = jnp.stack([rest[:piece], rest_back[:piece], rest[piece:], rest_back[piece:]])
    far_pair = jnp.concatenate([far_a, far_b])
    token, fourth, far_pair = wait(token, fourth, far_pair)
    fourth_y, fourth_x = exchange(fourth, ROW), exchange(fourth, NEAR_X)
    other_far = exchange(far_pair, CORE)
    token, other_far = wait(token, other_far)
    out_back, out_in = place(token, [(12, far_pair), (16, other), (28, other_far)], grads, width)
    token, out_back, out_in, fourth_y, fourth_x = wait(token, out_back, out_in, fourth_y, fourth_x)

    sends = [fourth_x[:2], fourth_y[2:], jnp.concatenate([fourth, fourth_y, fourth_x])]
    token, sends = wait(token, sends)
    last_a, last_b, pair = (exchange(s, m) for s, m in zip(sends, (ROW, NEAR_X, CORE)))
    made = sort(token, [(0, sends[2])], [], width)
    token, made, last_a, last_b, pair = wait(token, made, last_a, last_b, pair)

    ends = exchange(jnp.concatenate([last_a, last_b]), CORE)
    made = sort(token, [(12, last_a), (14, last_b), (16, pair)], made, width)
    token, made, ends = wait(token, made, ends)
    out_out, out_query, out_key, out_value = sort(token, [(28, ends)], made, width)
    return (pooled, input_grad, out_query, out_key, out_value, out_out, out_in, out_back, *outs)

def solution(mesh):
    data = P("dp", "blk", None)
    placed = (data,) + (P(),) * 11 + (P("dp"), P("dp"), P("dp", None))
    return jax.shard_map(local, mesh=mesh, in_specs=placed, out_specs=(P("dp", None), data) + (P(),) * 10, check_vma=False)
```

```python
import functools
import jax, jax.numpy as jnp
from jax import lax
from jax.experimental import pallas as pl
from jax.experimental.pallas import tpu as pltpu
from jax.sharding import PartitionSpec as P

F32, BF16 = jnp.float32, jnp.bfloat16
NEG = -1000000000.0
NT = (((1,), (1,)), ((), ()))
TN = (((0,), (0,)), ((), ()))
NN = (((1,), (0,)), ((), ()))

def dot(a, b, dims=NN):
    return lax.dot_general(a, b, dims, preferred_element_type=F32)

def skew(row, width, dtype=F32):
    return pltpu.roll(jnp.broadcast_to(row, (128, width)), width - 127, 1, stride=1, stride_axis=0)


BUCKETS = 32
EPS = 1e-06
CORE, ROW, NEAR_X = 1, 2, 4

def rms_scale(values):
    return lax.rsqrt(jnp.mean(values * values, axis=-1, keepdims=True) + EPS)

def norm_back(grad_out, values, scale, gain):
    weighted = grad_out * gain
    inner = jnp.mean(weighted * values, axis=-1, keepdims=True)
    grad_in = scale * weighted - scale * scale * scale * values * inner
    return grad_in, jnp.sum(grad_out * values * scale, axis=0, keepdims=True)

def two_terms(value):
    high = value.astype(BF16)
    return jnp.concatenate([high, (value - high.astype(F32)).astype(BF16)])

def one_value(terms):
    return terms[:8].astype(F32) + terms[8:16].astype(F32)

def rows_of(*values):
    count = sum(v.shape[0] for v in values)
    return jnp.concatenate(list(values) + [jnp.zeros((8 - count, values[0].shape[1]), F32)])

def prepare_kernel(mine, other, gain, wq_h, wk_h, wv_h, hidden, query, keys, values, wq, wk, wv, sems):
    rows = mine.shape[0]
    load = [pltpu.make_async_copy(a, b, sems.at[i]) for i, (a, b) in enumerate(((wk_h, wk), (wv_h, wv), (wq_h, wq)))]
    for copy in load:
        copy.start()
    for part, raw in enumerate((mine, other)):
        tokens = raw[...].astype(F32)
        hidden[part * rows : (part + 1) * rows, :] = (tokens * rms_scale(tokens) * gain[...]).astype(BF16)
    h = hidden[...]
    load[0].wait()
    keys[...] = dot(h, wk[...]).astype(BF16)
    load[1].wait()
    values[...] = dot(h, wv[...]).astype(BF16)
    load[2].wait()
    query[...] = dot(h[:rows], wq[...]).astype(BF16)

def prepare(mine, other, gain, wq, wk, wv):
    rows, width = mine.shape
    shape = lambda n: jax.ShapeDtypeStruct((n, width), BF16)
    vmem, free = (pl.BlockSpec(memory_space=m) for m in (pltpu.VMEM, pl.ANY))
    return pl.pallas_call(
        prepare_kernel,
        in_specs=[vmem] * 3 + [free] * 3,
        out_specs=[vmem] * 7,
        out_shape=[shape(2 * rows), shape(rows), shape(2 * rows), shape(2 * rows)] + [shape(width)] * 3,
        scratch_shapes=[pltpu.SemaphoreType.DMA((3,))],
        name="prepare", compiler_params=pltpu.CompilerParams(vmem_limit_bytes=14 << 20),
    )(mine, other, gain, wq, wk, wv)

def tables_kernel(ids, pads, prefixes, bias, buckets, lines, info, *, length):
    doc = ids[6]
    info[0] = length - jnp.where(doc == 0, pads[0], pads[1])
    info[5] = jnp.where(doc == 0, prefixes[0], prefixes[1])
    for to, at in enumerate((0, 1, 2, 3)):
        info[1 + to] = ids[at]
    for to, at in enumerate((4, 5, 6)):
        info[6 + to] = ids[at]
    picker = jnp.where(lax.broadcasted_iota(jnp.int32, (BUCKETS, 1), 0) == buckets[...], 1.0, 0.0).astype(BF16)
    left, total = bias[...], None
    for _ in range(3):
        part = left.astype(BF16)
        left = left - part.astype(F32)
        made = dot(part, picker)
        total = made if total is None else total + made
    lines[...] = jnp.zeros_like(lines)
    lines[:, : buckets.shape[1]] = total

def tables(ids, pads, prefixes, bias, buckets, length):
    smem, vmem = pl.BlockSpec(memory_space=pltpu.SMEM), pl.BlockSpec(memory_space=pltpu.VMEM)
    return pl.pallas_call(
        functools.partial(tables_kernel, length=length),
        in_specs=[smem] * 3 + [vmem] * 2,
        out_specs=[vmem, smem],
        out_shape=[jax.ShapeDtypeStruct((bias.shape[0], buckets.shape[1] + 1), F32), jax.ShapeDtypeStruct((16,), jnp.int32)],
        name="tables", compiler_params=pltpu.CompilerParams(vmem_limit_bytes=4 << 20),
    )(ids, pads, prefixes, bias, buckets)

def back_pieces(to, active, low, mine):
    @pl.loop(0, active.shape[1] // 512)
    def _(group):
        made = dot(active[:, pl.ds(pl.multiple_of(group * 512, 512), 512)], low, TN).astype(BF16)
        for b in range(4):
            rows = made[b * 128 : (b + 1) * 128]
            to[(4 * group + b) ^ mine] = jnp.concatenate([rows[:, q * 128 : (q + 1) * 128] for q in range(4)])

def in_pieces(to, slopes, turned, mine):
    @pl.loop(0, slopes.shape[1] // 512)
    def _(group):
        made = dot(turned, slopes[:, pl.ds(pl.multiple_of(group * 512, 512), 512)]).astype(BF16)
        for b in range(4):
            to[(4 * group + b) ^ mine] = made[:, b * 128 : (b + 1) * 128]

def front_kernel(info, far, far_other, near, q_l, k_l, v_l, lines, wq, wk, wv, gain1, gain2, gain3, cots, wo_h, win_h, wback_h,
                 hid, qs, ks, vs, expo_o, inv, att, send, active, slopes, turned, mixed, steep, rows,
                 wo, win, wback, expo, scores, skewed, edges, sems):
    count, width = near.shape
    hidden = win.shape[1]
    late = [pltpu.make_async_copy(a, b, sems.at[i]) for i, (a, b) in enumerate(((wo_h, wo), (win_h, win), (wback_h, wback)))]
    kept = lambda g: pltpu.make_async_copy(expo, expo_o.at[pl.ds(2 * g, 2)], sems.at[3])

    for copy in late:
        copy.start()
    for part, raw in enumerate((far, far_other)):
        tokens = raw[...].astype(F32)
        hid[part * count : (part + 1) * count, :] = (tokens * rms_scale(tokens) * gain1[...]).astype(BF16)
    h = hid[...]
    qs[...] = dot(h[:count], wq[...]).astype(BF16)
    ks[...] = dot(h, wk[...]).astype(BF16)
    vs[...] = dot(h, wv[...]).astype(BF16)
    column = lax.broadcasted_iota(jnp.int32, (1, 128), 1)
    for b in range(4):
        place = info[1 + b] + lax.broadcasted_iota(jnp.int32, (count, 1), 0)
        gate = jnp.where(place < info[0], 0.0, NEG)
        for head in range(2):
            edges[head, b * count : (b + 1) * count, :] = jnp.where(column == (64 if head == 0 else 0), gate, 0.0).astype(BF16)
    limit = info[0]

    @pl.loop(0, width // 128)
    def _(step):
        @pl.when(step > 0)
        def _():
            kept(step - 1).wait()

        cols = pl.ds(pl.multiple_of(step * 128, 128), 128)
        lane = lax.broadcasted_iota(jnp.int32, (1, 128), 1)
        first = lane < 64
        starts = [info[1 + b] for b in range(4)]
        keys = [k_l[:count, cols], k_l[count:, cols], ks[:count, cols], ks[count:, cols]]
        values = jnp.concatenate([v_l[:, cols], vs[:, cols]])
        query = jnp.concatenate([q_l[:, cols], qs[:, cols]])
        made = []
        for head in range(2):
            mine = jnp.where(first if head == 0 else lane >= 64, 1.0, 0.0).astype(BF16)
            one = jnp.where(lane == (64 if head == 0 else 0), 1.0, 0.0).astype(BF16)
            q = query * mine + one
            v = values * mine + one
            skewed[head] = skew(lines[pl.ds(2 * step + head, 1), :], lines.shape[1])
            k = jnp.concatenate(keys) * mine + edges[head]
            for half in range(2):
                s = dot(q[half * 256 : (half + 1) * 256], k, NT)
                for r in range(2):
                    for b in range(4):
                        at = starts[b] - starts[2 * half] + 896 - 128 * r
                        part = s[r * 128 : (r + 1) * 128, b * 256 : (b + 1) * 256] + skewed[head, :, pl.ds(pl.multiple_of(at, 128), 256)]
                        scores[head, half * 256 + r * 128 : half * 256 + (r + 1) * 128, b * 256 : (b + 1) * 256] = part
            accs = []
            for r in range(4):
                rs = slice(r * 128, (r + 1) * 128)
                value = scores[head, rs, :]
                top = jnp.max(value, axis=1, keepdims=True)
                e = jnp.exp(value - top).astype(BF16)
                expo[head, rs, :] = e
                accs.append(dot(e, v))
            acc = jnp.concatenate(accs)
            made.append((acc, 1.0 / (acc[:, 64:65] if head == 0 else acc[:, 0:1])))
        (a0, i0), (a1, i1) = made
        scale = jnp.where(first, i0, i1)
        att[:, cols] = (jnp.where(first, a0, a1) * scale).astype(BF16)
        inv[:, cols] = scale
        kept(step).start()

    for copy in late:
        copy.wait()
    for part, raw in enumerate((near, far)):
        spot = slice(part * count, (part + 1) * count)
        mixed[spot, :] = raw[...].astype(F32) + dot(att[spot, :], wo[...])
    values = mixed[...]
    inner = (values * rms_scale(values) * gain2[...]).astype(BF16)
    turned[...] = inner.T
    total = values
    for at in range(0, hidden, 512):
        lifted = jnp.maximum(dot(inner, win[:, at : at + 512]), 0.0).astype(BF16)
        active[:, at : at + 512] = lifted
        total = total + dot(lifted, wback[at : at + 512, :])
    scale = rms_scale(total)
    place = lax.broadcasted_iota(jnp.int32, (2 * count, 1), 0)
    place = jnp.where(place < count, place + info[1], place + (info[3] - count))
    live = jnp.where((place >= info[5]) & (place < limit), 1.0, 0.0)
    pool = jnp.sum(total * scale * gain3[...] * live, axis=0, keepdims=True)
    cot = jnp.where(info[8] == 0, cots[0:1, :], cots[1:2, :]) / (limit - info[5]).astype(F32)
    slope, grad_end = norm_back(live * cot, total, scale, gain3[...])
    steep[...] = slope
    rows[...] = jnp.concatenate([pool, grad_end, jnp.zeros((6, width), F32)])
    low = slope.astype(BF16)
    for at in range(0, hidden, 512):
        through = dot(low, wback[at : at + 512, :], NT).astype(BF16)
        slopes[:, at : at + 512] = jnp.where(active[:, at : at + 512] > 0, through, jnp.zeros_like(through))
    mine = info[6] & 15

    @pl.when(info[7] == 0)
    def _():
        in_pieces(send, slopes, turned[...], mine)

    @pl.when(info[7] == 1)
    def _():
        back_pieces(send, active, steep[...].astype(BF16), mine)

    kept(3).wait()


def front(info, far, far_other, near, q_l, k_l, v_l, lines, wq, wk, wv, gain1, gain2, gain3, cots, wo, win, wback):
    count, width = near.shape
    hidden = win.shape[1]
    heads, span = lines.shape
    shape = jax.ShapeDtypeStruct
    smem, vmem, free = (pl.BlockSpec(memory_space=m) for m in (pltpu.SMEM, pltpu.VMEM, pl.ANY))
    outs = [shape((2 * count, width), BF16), shape((count, width), BF16), shape((2 * count, width), BF16), shape((2 * count, width), BF16),
            shape((heads, 2 * count, 4 * count), BF16), shape((2 * count, width), F32), shape((2 * count, width), BF16),
            shape((16, width, 128), BF16), shape((2 * count, hidden), BF16), shape((2 * count, hidden), BF16),
            shape((width, 2 * count), BF16), shape((2 * count, width), F32), shape((2 * count, width), F32)]
    return pl.pallas_call(
        front_kernel,
        in_specs=[smem] + [vmem] * 14 + [free] * 3,
        out_specs=[vmem] * 4 + [free] + [vmem] * 9,
        out_shape=outs + [shape((8, width), F32)],
        scratch_shapes=[pltpu.VMEM(wo.shape, BF16), pltpu.VMEM(win.shape, BF16), pltpu.VMEM(wback.shape, BF16),
                        pltpu.VMEM((2, 2 * count, 4 * count), BF16), pltpu.VMEM((2, 2 * count, 4 * count), F32),
                        pltpu.VMEM((2, 128, span), F32), pltpu.VMEM((2, 4 * count, 128), BF16), pltpu.SemaphoreType.DMA((4,))],
        name="front", compiler_params=pltpu.CompilerParams(vmem_limit_bytes=38 << 20),
    )(info, far, far_other, near, q_l, k_l, v_l, lines, wq, wk, wv, gain1, gain2, gain3, cots, wo, win, wback)

def inner_kernel(info, slopes, win, grad_inner):
    total = None
    for at in range(0, slopes.shape[1], 512):
        part = dot(slopes[:, at : at + 512], win[:, at : at + 512], NT)
        total = part if total is None else total + part
    grad_inner[...] = total

def inner(info, slopes, win):
    smem, vmem = pl.BlockSpec(memory_space=pltpu.SMEM), pl.BlockSpec(memory_space=pltpu.VMEM)
    return pl.pallas_call(
        inner_kernel, in_specs=[smem, vmem, vmem], out_specs=vmem,
        out_shape=jax.ShapeDtypeStruct((slopes.shape[0], win.shape[0]), F32), name="inner", compiler_params=pltpu.CompilerParams(vmem_limit_bytes=10 << 20),
    )(info, slopes, win)

def through_kernel(info, grad_inner, mixed, steep, wo, att, gain2, grad_mixed, grad_attended, grad_out, rows):
    values = mixed[...]
    more, grad_two = norm_back(grad_inner[...], values, rms_scale(values), gain2[...])
    total = steep[...] + more
    grad_mixed[...] = total
    low = total.astype(BF16)
    grad_attended[...] = dot(low, wo[...], NT).astype(BF16)
    grad_out[...] = dot(att[...], low, TN).astype(BF16)
    rows[...] = jnp.concatenate([grad_two, jnp.zeros((7, low.shape[1]), F32)])

def through(info, grad_inner, mixed, steep, wo, att, gain2):
    n, width = mixed.shape
    smem, vmem = pl.BlockSpec(memory_space=pltpu.SMEM), pl.BlockSpec(memory_space=pltpu.VMEM)
    shape = jax.ShapeDtypeStruct
    return pl.pallas_call(
        through_kernel,
        in_specs=[smem] + [vmem] * 6,
        out_specs=[vmem] * 4,
        out_shape=[shape((n, width), F32), shape((n, width), BF16), shape((width, width), BF16), shape((8, width), F32)],
        name="through", compiler_params=pltpu.CompilerParams(vmem_limit_bytes=16 << 20),
    )(info, grad_inner, mixed, steep, wo, att, gain2)

def stay_kernel(info, active, slopes, turned, steep, blocks):
    high, lowest = (info[6] & 15) >> 2, info[6] & 3
    for side in range(2):
        @pl.when(info[7] == side)
        def _(side=side):
            low = steep[...].astype(BF16) if side == 0 else turned[...]
            for k in range(4):
                at = pl.ds(pl.multiple_of((k ^ high) * 512, 512), 512)
                made = dot(active[:, at], low, TN) if side == 0 else dot(low, slopes[:, at])
                for b in range(4):
                    piece = made[:, b * 128 : (b + 1) * 128]
                    if side == 0:
                        piece = made[b * 128 : (b + 1) * 128]
                        piece = jnp.concatenate([piece[:, q * 128 : (q + 1) * 128] for q in range(4)])
                    blocks[k, b ^ lowest] = piece.astype(BF16)

def stay_half(info, active, slopes, turned, steep):
    smem, vmem = pl.BlockSpec(memory_space=pltpu.SMEM), pl.BlockSpec(memory_space=pltpu.VMEM)
    width = steep.shape[1]
    return pl.pallas_call(
        stay_kernel, in_specs=[smem] + [vmem] * 4, out_specs=vmem,
        out_shape=jax.ShapeDtypeStruct((4, 4, width, 128), BF16), name="stay", compiler_params=pltpu.CompilerParams(vmem_limit_bytes=12 << 20),
    )(info, active, slopes, turned, steep)

def meet_kernel(kept, got, *outs):
    for k in (3, 1, 2, 0):
        outs[k][...] = added(kept[k], got[4 * k : 4 * k + 4])

def meet(kept, got):
    vmem = pl.BlockSpec(memory_space=pltpu.VMEM)
    return pl.pallas_call(
        meet_kernel, in_specs=[vmem] * 2, out_specs=[vmem] * 4, out_shape=[jax.ShapeDtypeStruct(kept.shape[1:], BF16)] * 4, name="meet", compiler_params=pltpu.CompilerParams(vmem_limit_bytes=20 << 20),
    )(kept, got)

CLASS = {(0, 0): 0, (1, 2): 0, (0, 1): 1, (1, 3): 1, (0, 2): 2, (0, 3): 3, (1, 0): 4, (1, 1): 5}

def back_kernel(info, ql, qr, kl, kr, vl, vr, gout, out, inv, expo, buckets, dense_rows, through_rows,
                hid_l_h, hid_r_h, near_h, near_other_h, far_h, far_other_h, wq_h, wk_h, wv_h, grad_out_h,
                keep_o, send_o, stay_o, leave_o, small,
                hid_l, hid_r, near, near_other, far, far_other, wq, wk, wv, made,
                keep, send, stay, leave, dq, dk, dv, offsets, sums, acc, slopes, sems):
    count, width = near.shape
    step = pl.program_id(0)
    pairs = width // 128
    late = [pltpu.make_async_copy(a, b, sems.at[i]) for i, (a, b) in enumerate((
        (hid_l_h, hid_l), (hid_r_h, hid_r), (near_h, near), (near_other_h, near_other), (far_h, far), (far_other_h, far_other),
        (wq_h, wq), (wk_h, wk), (wv_h, wv), (grad_out_h, made.at[0:width])))]
    done = [pltpu.make_async_copy(a, b, sems.at[10 + i]) for i, (a, b) in enumerate(((send, send_o), (keep, keep_o), (leave, leave_o), (stay, stay_o)))]

    @pl.when(step == 0)
    def _():
        for copy in late:
            copy.start()

    cols = pl.ds(pl.multiple_of(step * 128, 128), 128)
    lane = lax.broadcasted_iota(jnp.int32, (1, 128), 1)
    starts = [info[1 + b] for b in range(4)]
    keys = jnp.concatenate([kl[...], kr[...]])
    values = jnp.concatenate([vl[...], vr[...]])
    query = jnp.concatenate([ql[...], qr[...]])
    scaled = gout[...].astype(F32) * inv[...]
    prod = scaled * out[...].astype(F32)
    low = scaled.astype(BF16)
    query_t, low_t = query.T, low.T
    grads_q, grads_k, grads_v = None, [], []
    for head in range(2):
        mine = (lane < 64) if head == 0 else (lane >= 64)
        base = 64 if head == 0 else 0
        pick = jnp.where(mine, 1.0, 0.0).astype(BF16)
        delta = jnp.sum(jnp.where(mine, prod, 0.0), axis=1, keepdims=True)
        high = delta.astype(BF16).astype(F32)
        extra = jnp.where(lane == base, high, jnp.where(lane == base + 1, delta - high, 0.0)).astype(BF16)
        grad = low * pick + extra
        minus = jnp.where((lane == base) | (lane == base + 1), -1.0, 0.0).astype(BF16)
        for b in range(4):
            spot = slice(b * count, (b + 1) * count)
            ds = dot(grad, values[spot] * pick + minus, NT) * expo[head, :, spot].astype(F32)
            slopes[head, :, spot] = ds.astype(BF16)
            for chunk in range(2):
                upper, lower = (ds[chunk * count + r * 128 : chunk * count + (r + 1) * 128] for r in range(2))
                group = CLASS[chunk, b]
                block = jnp.concatenate([lower[:, :128], lower[:, 128:] + upper[:, :128], upper[:, 128:]], axis=1)
                if (chunk, b) in ((1, 2), (1, 3)):
                    block = block + sums[head, group]
                sums[head, group] = block
        part = dot(slopes[head], keys * pick)
        grads_q = part if grads_q is None else grads_q + part
        half = slice(head * 64, (head + 1) * 64)
        grads_k.append(dot(query_t[half], slopes[head]))
        grads_v.append(dot(low_t[half], expo[head]))
    dq[:, cols] = grads_q.astype(BF16)
    dk[:, cols] = jnp.concatenate(grads_k).astype(BF16).T
    dv[:, cols] = jnp.concatenate(grads_v).astype(BF16).T
    for head in range(2):
        acc[head] = jnp.zeros(acc.shape[1:], F32)
        for (chunk, b), group in CLASS.items():
            if (chunk, b) not in ((1, 2), (1, 3)):
                at = starts[b] - starts[2 * chunk] + 768
                to = pl.ds(pl.multiple_of(at, 128), 384)
                acc[head, :, to] += sums[head, group]
        rest = acc[head]
        n = 64
        while n >= 8:
            rest = rest[:n] + pltpu.roll(rest[n:], 2048 - n, 1)
            n //= 2
        line = rest[7:8]
        for r in range(6, -1, -1):
            line = rest[r : r + 1] + pltpu.roll(line, 2047, 1)
        offsets[pl.ds(2 * step + head, 1), :] = pltpu.roll(line, 127, 1)

    @pl.when(step == pairs - 1)
    def _():
        for copy in late:
            copy.wait()
        made[width : 2 * width, :] = (dot(hid_l[:count, :], dq[:count, :], TN) + dot(hid_r[:count, :], dq[count:, :], TN)).astype(BF16)
        for at, grads in ((2 * width, dk), (3 * width, dv)):
            made[at : at + width, :] = (dot(hid_l[...], grads[: 2 * count, :], TN) + dot(hid_r[...], grads[2 * count :, :], TN)).astype(BF16)
        me = info[6]
        size = made.shape[0] // 32

        @pl.loop(0, 16)
        def _(r):
            keep[r] = made[pl.ds(pl.multiple_of((r ^ me) * size, size), size), :]
            send[pl.ds(pl.multiple_of(r * size, size), size), :] = made[pl.ds(pl.multiple_of(((r + 16) ^ me) * size, size), size), :]

        gain = jnp.zeros((1, width), F32)
        for b, raw in enumerate((near, near_other, far, far_other)):
            spot = slice(b * count, (b + 1) * count)
            grad = dot(dk[spot, :], wk[...], NT) + dot(dv[spot, :], wv[...], NT)
            half = slice((b // 2) * count, (b // 2 + 1) * count)
            if b % 2 == 0:
                grad = grad + dot(dq[half, :], wq[...], NT)
                stay[half, :] = grad
            else:
                leave[half, :] = grad.astype(BF16)
            tokens = raw[...].astype(F32)
            gain = gain + jnp.sum(grad * (tokens * rms_scale(tokens)), axis=0, keepdims=True)
        leave[2 * count :, :] = two_terms(rows_of(dense_rows[0:1, :]))
        picker = jnp.where(lax.broadcasted_iota(jnp.int32, (128, 1), 0) == buckets[...], 1.0, 0.0).astype(BF16)
        left = offsets[...][:, : buckets.shape[1]]
        bias = None
        for _ in range(3):
            part = left.astype(BF16)
            left = left - part.astype(F32)
            bias = dot(part, picker, NT) if bias is None else bias + dot(part, picker, NT)
        bias = jnp.concatenate([bias, jnp.zeros((bias.shape[0], width - 128), F32)], axis=1)
        line = bias[0:1]
        for h in range(1, bias.shape[0]):
            line = line + pltpu.roll(bias[h : h + 1], 32 * h, 1)
        total = rows_of(gain, through_rows[0:1, :], dense_rows[1:2, :], line)
        small[...] = total
        send[16 * size :, :] = two_terms(total)
        for copy in done:
            copy.start()
        for copy in done:
            copy.wait()

def back(info, ql, qr, kl, kr, vl, vr, gout, out, inv, expo, buckets, dense_rows, through_rows,
         hid_l, hid_r, near, near_other, far, far_other, wq, wk, wv, grad_out):
    count, width = near.shape
    smem, free = pl.BlockSpec(memory_space=pltpu.SMEM), pl.BlockSpec(memory_space=pl.ANY)
    whole = lambda *dims: pl.BlockSpec(dims, lambda g: (0,) * len(dims))
    col = lambda n: pl.BlockSpec((n, 128), lambda g: (0, g))
    shape = jax.ShapeDtypeStruct
    size = 4 * width // 32
    outs = [shape((16, size, width), BF16), shape((16 * size + 16, width), BF16), shape((2 * count, width), F32), shape((2 * count + 16, width), BF16)]
    given = (hid_l, hid_r, near, near_other, far, far_other, wq, wk, wv)
    return pl.pallas_call(
        back_kernel,
        grid=(width // 128,),
        in_specs=[smem, col(count), col(count)] + [col(2 * count)] * 7 + [pl.BlockSpec((2, 2 * count, 4 * count), lambda g: (g, 0, 0)),
                  whole(*buckets.shape), whole(8, width), whole(8, width)] + [free] * 10,
        out_specs=[free] * 4 + [whole(8, width)],
        out_shape=outs + [shape((8, width), F32)],
        scratch_shapes=[pltpu.VMEM(g.shape, BF16) for g in given] + [pltpu.VMEM((4 * width, width), BF16)]
                       + [pltpu.VMEM(o.shape, o.dtype) for o in outs]
                       + [pltpu.VMEM((2 * count, width), BF16), pltpu.VMEM((4 * count, width), BF16), pltpu.VMEM((4 * count, width), BF16),
                          pltpu.VMEM((8, 2048), F32), pltpu.VMEM((2, 6, 128, 384), F32), pltpu.VMEM((2, 128, 2048), F32),
                          pltpu.VMEM((2, 2 * count, 4 * count), BF16), pltpu.SemaphoreType.DMA((14,))],
        name="back", compiler_params=pltpu.CompilerParams(vmem_limit_bytes=44 << 20),
    )(info, ql, qr, kl, kr, vl, vr, gout, out, inv, expo, buckets, dense_rows, through_rows, *given, grad_out)

def ending_kernel(info, stay, came, near, far, grad_mixed, gain, dense_rows, home, away):
    count, width = near.shape
    for part, raw in enumerate((near, far)):
        spot = slice(part * count, (part + 1) * count)
        tokens = raw[...].astype(F32)
        grad = stay[spot, :] + came[spot, :].astype(F32)
        more, _ = norm_back(grad, tokens, rms_scale(tokens), gain[...])
        value = (grad_mixed[spot, :] + more).astype(BF16)
        if part == 0:
            home[:count, :] = value
        else:
            away[:count, :] = value
    alive = (info[0] - info[5]).astype(F32)
    pool = two_terms((rows_of(dense_rows[0:1, :]) + one_value(came[2 * count :, :])) / alive)
    home[count:, :] = pool
    away[count:, :] = pool

def ending(info, stay, came, near, far, grad_mixed, gain, dense_rows):
    count, width = near.shape
    smem, vmem = pl.BlockSpec(memory_space=pltpu.SMEM), pl.BlockSpec(memory_space=pltpu.VMEM)
    shape = jax.ShapeDtypeStruct((count + 16, width), BF16)
    return pl.pallas_call(
        ending_kernel, in_specs=[smem] + [vmem] * 7, out_specs=[vmem] * 2, out_shape=[shape, shape], name="ending", compiler_params=pltpu.CompilerParams(vmem_limit_bytes=10 << 20)
    )(info, stay, came, near, far, grad_mixed, gain, dense_rows)

def place_kernel(firsts, info, *refs):
    parts, (back, front, rows, columns, sems) = refs[: len(firsts)], refs[-5:]
    mine = info[6] & 15
    for side in range(2):
        @pl.when(info[7] == side)
        def _(side=side):
            copies, n = [], 0
            for part, first in zip(parts, firsts):
                for i in range(part.shape[0]):
                    r = first + i
                    to = pl.ds(pl.multiple_of(((r & 15) ^ mine) * 128, 128), 128)
                    if (r >= 16) == (side == 1):
                        for q in range(4):
                            rows[n, :, q * 128 : (q + 1) * 128] = part[i, q * 128 : (q + 1) * 128, :].astype(F32)
                        copies.append(pltpu.make_async_copy(rows.at[n], back.at[to, :], sems.at[n]))
                    else:
                        columns[n] = part[i].astype(F32)
                        copies.append(pltpu.make_async_copy(columns.at[n], front.at[:, to], sems.at[n]))
                    copies[-1].start()
                    n += 1
            for copy in copies:
                copy.wait()

def place(info, parts, made, width):
    smem, vmem, far = (pl.BlockSpec(memory_space=m) for m in (pltpu.SMEM, pltpu.VMEM, pltpu.HBM))
    shape = jax.ShapeDtypeStruct
    count = sum(p.shape[0] for _, p in parts)
    return pl.pallas_call(
        functools.partial(place_kernel, [first for first, _ in parts]),
        in_specs=[smem] + [vmem] * len(parts) + [far] * len(made),
        out_specs=[far] * 2,
        out_shape=[shape((16 * 128, width), F32), shape((width, 16 * 128), F32)],
        scratch_shapes=[pltpu.VMEM((count, 128, width), F32), pltpu.VMEM((count, width, 128), F32), pltpu.SemaphoreType.DMA((count,))],
        input_output_aliases={1 + len(parts) + i: i for i in range(len(made))},
        name="place", compiler_params=pltpu.CompilerParams(vmem_limit_bytes=28 << 20),
    )(info, *[p for _, p in parts], *made)

def sort_kernel(firsts, info, *refs):
    parts, made, (tall, sems) = refs[: len(firsts)], refs[-6:-2], refs[-2:]
    size = parts[0].shape[1]
    mine = info[6]
    pieces = []
    for part, first in zip(parts, firsts):
        for i in range(part.shape[0]):
            tall[len(pieces)] = part[i].astype(F32)
            pieces.append(first + i)
    for top in range(4):
        @pl.when((mine >> 3) == top)
        def _(top=top):
            copies = []
            for n, r in enumerate(pieces):
                to = pl.ds(pl.multiple_of(((r ^ mine) & 7) * size, size), size)
                copies.append(pltpu.make_async_copy(tall.at[n], made[top ^ (r >> 3)].at[to, :], sems.at[n]))
                copies[-1].start()
            for copy in copies:
                copy.wait()

def sort(info, parts, made, width):
    smem, vmem, far = (pl.BlockSpec(memory_space=m) for m in (pltpu.SMEM, pltpu.VMEM, pltpu.HBM))
    shape = jax.ShapeDtypeStruct((width, width), F32)
    count = sum(p.shape[0] for _, p in parts)
    return pl.pallas_call(
        functools.partial(sort_kernel, [first for first, _ in parts]),
        in_specs=[smem] + [vmem] * len(parts) + [far] * len(made),
        out_specs=[far] * 4,
        out_shape=[shape] * 4,
        scratch_shapes=[pltpu.VMEM((count,) + parts[0][1].shape[1:], F32), pltpu.SemaphoreType.DMA((count,))],
        input_output_aliases={1 + len(parts) + i: i for i in range(len(made))},
        name="sort", compiler_params=pltpu.CompilerParams(vmem_limit_bytes=12 << 20),
    )(info, *[p for _, p in parts], *made)

def mix_kernel(*refs):
    for k in range(4):
        refs[4 + k][...] = added(*[term[k] for term in refs[:4]])

def mix(terms):
    block = terms[0].shape[1:]
    vmem = pl.BlockSpec(memory_space=pltpu.VMEM)
    return pl.pallas_call(
        mix_kernel, in_specs=[vmem] * 4, out_specs=[vmem] * 4, out_shape=[jax.ShapeDtypeStruct(block, BF16)] * 4, name="mix", compiler_params=pltpu.CompilerParams(vmem_limit_bytes=10 << 20),
    )(*terms)

def exchange(value, bits):
    size = lax.axis_size("dp") * lax.axis_size("blk")
    return lax.ppermute(value, ("dp", "blk"), [(i, i ^ bits) for i in range(size)])

def wait(*values):
    return lax.optimization_barrier(values)

def added(*terms):
    total = terms[0].astype(F32)
    for term in terms[1:]:
        total = total + term.astype(F32)
    return total.astype(BF16)

def local(inputs, w_query, w_key, w_value, w_out, w_in, w_back, norm1_gain, norm2_gain, final_gain, bias_table, bucket_table, prefix_len, pad_len, pooled_grad):
    rows, width = inputs.shape[1:]
    spot, far_off = lax.axis_index("blk"), lax.axis_index("dp")
    doc, core = spot // 2, spot % 2
    block = [doc * 2 + core, doc * 2 + 1 - core, (1 - doc) * 2 + core, (1 - doc) * 2 + 1 - core]
    line = [8, 16]
    further = [32 << b for b in range((lax.axis_size("dp") // 8).bit_length() - 1)]
    piece = core * 16 + doc * 4 + (far_off % 2) * 8 + (far_off // 2) % 4
    near = jnp.where(doc == 0, inputs[0], inputs[1])
    far_send = jnp.where(doc == 0, inputs[1], inputs[0])
    near, far_send = wait(near, far_send)
    far = exchange(far_send, ROW)
    near_other = exchange(near, CORE)
    slot = jnp.arange(8, dtype=jnp.int32)
    ids = jnp.zeros_like(slot)
    for i, value in enumerate([b * rows for b in block] + [piece, core, doc]):
        ids = jnp.where(slot == i, value, ids)
    gain1, gain2, gain3 = norm1_gain[None, :], norm2_gain[None, :], final_gain[None, :]
    buckets = bucket_table[None, :]
    hid_l, q_l, k_l, v_l, w_query, w_key, w_value = prepare(near, near_other, gain1, w_query, w_key, w_value)
    far, q_l, ids = wait(far, q_l, ids)
    far_other = exchange(far, CORE)
    lines, info = tables(ids, pad_len, prefix_len, bias_table.T, buckets, 4 * rows)
    (hid_r, q_r, k_r, v_r, expo, inverse, attended, send, active, slopes, turned, mixed, steep, dense_rows) = front(
        info, far, far_other, near, q_l, k_l, v_l, lines, w_query, w_key, w_value,
        gain1, gain2, gain3, pooled_grad, w_out, w_in, w_back)

    xy = [ROW, NEAR_X, ROW ^ NEAR_X]
    zz = [line[0], line[1], line[0] ^ line[1]]

    token, send = wait(info, send)
    got = exchange(send, CORE)
    kept = stay_half(token, active, slopes, turned, steep)
    token, kept = wait(token, kept)
    grad_inner = inner(token, slopes, w_in)
    token, grad_inner, got = wait(token, grad_inner, got)
    stays, *sends = meet(kept, got)

    token, sends, grad_inner = wait(token, sends, grad_inner)
    came = [exchange(s, m) for s, m in zip(sends, xy)]
    grad_mixed, grad_attended, grad_out_w, through_rows = through(token, grad_inner, mixed, steep, w_out, attended, gain2)
    token, through_rows = wait(token, through_rows)
    rest_keep, rest_send, stay, leave, small = back(
        token, q_l, q_r, k_l, k_r, v_l, v_r, grad_attended, attended, inverse, expo, buckets, dense_rows, through_rows,
        hid_l, hid_r, near, near_other, far, far_other, w_query, w_key, w_value, grad_out_w)
    token, small, rest_send, leave, came = wait(token, small, rest_send, leave, came)

    rest_got = exchange(rest_send, CORE)
    hidden_got = exchange(leave, CORE)
    lines = mix([stays] + list(came))
    token, lines = wait(token, lines)
    took = [exchange(lines[k + 1], m) for k, m in enumerate(zz)]
    token, rest_got, hidden_got = wait(token, rest_got, hidden_got)

    count = rest_keep.shape[0] * rest_keep.shape[1]
    small = small + one_value(rest_got[count:])
    rest_got = rest_got[:count].reshape(rest_keep.shape)
    terms = two_terms(small)
    sends = [jnp.concatenate([added(rest_keep[4 * k : 4 * k + 4], rest_got[4 * k : 4 * k + 4]).reshape(-1, width), terms]) for k in (1, 2, 3)]
    token, sends = wait(token, sends)
    rest_came = [exchange(s, m) for s, m in zip(sends, xy)]
    home, away = ending(token, stay, hidden_got, near, far, grad_mixed, gain1, dense_rows)
    token, took, away = wait(token, took, away)

    whole = added(lines[0], *took)
    for bit in further:
        whole = added(whole, exchange(whole, bit))
    token, whole = wait(token, whole)
    back_line = [exchange(whole, m) for m in zz]
    away_got = exchange(away, ROW)
    token, rest_came = wait(token, rest_came)

    count = count // 4
    for part in rest_came:
        small = small + one_value(part[count:])
    rest_came = [part[:count].reshape((4,) + rest_keep.shape[1:]) for part in rest_came]
    piece = count // 4
    lines = added(rest_keep[:4], rest_got[:4], *rest_came).reshape(-1, width)
    send = jnp.concatenate([lines[piece : 2 * piece], lines[3 * piece :], two_terms(small)])
    token, send = wait(token, send)
    took = exchange(send, line[0])
    token, took = wait(token, took)
    small = small + one_value(took[2 * piece :])
    lines = added(jnp.concatenate([lines[:piece], lines[2 * piece : 3 * piece]]), took[: 2 * piece])
    send = jnp.concatenate([lines, two_terms(small)])
    token, send, back_line, away_got = wait(token, send, back_line, away_got)
    took = exchange(send, line[1])

    quarter = jnp.stack([whole] + back_line)
    token, quarter = wait(token, quarter)
    from_y, from_x = exchange(quarter, ROW), exchange(quarter, NEAR_X)
    pool_mine, pool_other = one_value(home[rows:])[:1], one_value(away_got[rows:])[:1]
    pooled = jnp.where(doc == 0, jnp.concatenate([pool_mine, pool_other]), jnp.concatenate([pool_other, pool_mine]))
    home, away_got = home[:rows], away_got[:rows]
    input_grad = jnp.where(doc == 0, jnp.stack([home, away_got]), jnp.stack([away_got, home]))
    token, took, pooled, input_grad = wait(token, took, pooled, input_grad)

    small = small + one_value(took[2 * piece :])
    rest = added(lines, jnp.concatenate([took[piece : 2 * piece], took[:piece]]))
    for bit in further:
        rest = added(rest, exchange(rest, bit))
        small = small + exchange(small, bit)
    token, rest = wait(token, rest)
    rest_back = exchange(rest, line[0])
    outs = [small[0], small[1], small[2], small[3, : bias_table.size].reshape(bias_table.shape[::-1]).T]
    token, from_y, from_x, outs = wait(token, from_y, from_x, outs)

    sends = [from_x[:2], from_y[2:]]
    here = jnp.concatenate([quarter, from_y, from_x])
    token, sends, here = wait(token, sends, here)
    far_a, far_b = exchange(sends[0], ROW), exchange(sends[1], NEAR_X)
    other = exchange(here, CORE)
    grads = place(token, [(0, here)], [], width)
    token, grads, rest_back, far_a, far_b, other = wait(token, grads, rest_back, far_a, far_b, other)

    fourth = jnp.stack([rest[:piece], rest_back[:piece], rest[piece:], rest_back[piece:]])
    far_pair = jnp.concatenate([far_a, far_b])
    token, fourth, far_pair = wait(token, fourth, far_pair)
    fourth_y, fourth_x = exchange(fourth, ROW), exchange(fourth, NEAR_X)
    other_far = exchange(far_pair, CORE)
    token, other_far = wait(token, other_far)
    out_back, out_in = place(token, [(12, far_pair), (16, other), (28, other_far)], grads, width)
    token, out_back, out_in, fourth_y, fourth_x = wait(token, out_back, out_in, fourth_y, fourth_x)

    sends = [fourth_x[:2], fourth_y[2:], jnp.concatenate([fourth, fourth_y, fourth_x])]
    token, sends = wait(token, sends)
    last_a, last_b, pair = (exchange(s, m) for s, m in zip(sends, (ROW, NEAR_X, CORE)))
    made = sort(token, [(0, sends[2])], [], width)
    token, made, last_a, last_b, pair = wait(token, made, last_a, last_b, pair)

    ends = exchange(jnp.concatenate([last_a, last_b]), CORE)
    made = sort(token, [(12, last_a), (14, last_b), (16, pair)], made, width)
    token, made, ends = wait(token, made, ends)
    out_out, out_query, out_key, out_value = sort(token, [(28, ends)], made, width)
    return (pooled, input_grad, out_query, out_key, out_value, out_out, out_in, out_back, *outs)

def solution(mesh):
    data = P("dp", "blk", None)
    placed = (data,) + (P(),) * 11 + (P("dp"), P("dp"), P("dp", None))
    return jax.shard_map(local, mesh=mesh, in_specs=placed, out_specs=(P("dp", None), data) + (P(),) * 10, check_vma=False)
```

```python
import functools
import jax, jax.numpy as jnp
from jax import lax
from jax.experimental import pallas as pl
from jax.experimental.pallas import tpu as pltpu
from jax.sharding import PartitionSpec as P

F32, BF16 = jnp.float32, jnp.bfloat16
NEG = -1000000000.0
NT = (((1,), (1,)), ((), ()))
TN = (((0,), (0,)), ((), ()))
NN = (((1,), (0,)), ((), ()))

def dot(a, b, dims=NN):
    return lax.dot_general(a, b, dims, preferred_element_type=F32)

def skew(row, width, dtype=F32):
    return pltpu.roll(jnp.broadcast_to(row, (128, width)), width - 127, 1, stride=1, stride_axis=0)


BUCKETS = 32
EPS = 1e-06
CORE, ROW, NEAR_X = 1, 2, 4

def rms_scale(values):
    return lax.rsqrt(jnp.mean(values * values, axis=-1, keepdims=True) + EPS)

def norm_back(grad_out, values, scale, gain):
    weighted = grad_out * gain
    inner = jnp.mean(weighted * values, axis=-1, keepdims=True)
    grad_in = scale * weighted - scale * scale * scale * values * inner
    return grad_in, jnp.sum(grad_out * values * scale, axis=0, keepdims=True)

def two_terms(value):
    high = value.astype(BF16)
    return jnp.concatenate([high, (value - high.astype(F32)).astype(BF16)])

def one_value(terms):
    return terms[:8].astype(F32) + terms[8:16].astype(F32)

def rows_of(*values):
    count = sum(v.shape[0] for v in values)
    return jnp.concatenate(list(values) + [jnp.zeros((8 - count, values[0].shape[1]), F32)])

def prepare_kernel(mine, other, gain, wq_h, wk_h, wv_h, hidden, query, keys, values, wq, wk, wv, sems):
    rows = mine.shape[0]
    load = [pltpu.make_async_copy(a, b, sems.at[i]) for i, (a, b) in enumerate(((wk_h, wk), (wv_h, wv), (wq_h, wq)))]
    for copy in load:
        copy.start()
    for part, raw in enumerate((mine, other)):
        tokens = raw[...].astype(F32)
        hidden[part * rows : (part + 1) * rows, :] = (tokens * rms_scale(tokens) * gain[...]).astype(BF16)
    h = hidden[...]
    load[0].wait()
    keys[...] = dot(h, wk[...]).astype(BF16)
    load[1].wait()
    values[...] = dot(h, wv[...]).astype(BF16)
    load[2].wait()
    query[...] = dot(h[:rows], wq[...]).astype(BF16)

def prepare(mine, other, gain, wq, wk, wv):
    rows, width = mine.shape
    shape = lambda n: jax.ShapeDtypeStruct((n, width), BF16)
    vmem, free = (pl.BlockSpec(memory_space=m) for m in (pltpu.VMEM, pl.ANY))
    return pl.pallas_call(
        prepare_kernel,
        in_specs=[vmem] * 3 + [free] * 3,
        out_specs=[vmem] * 7,
        out_shape=[shape(2 * rows), shape(rows), shape(2 * rows), shape(2 * rows)] + [shape(width)] * 3,
        scratch_shapes=[pltpu.SemaphoreType.DMA((3,))],
        name="prepare", compiler_params=pltpu.CompilerParams(vmem_limit_bytes=14 << 20),
    )(mine, other, gain, wq, wk, wv)

def tables_kernel(ids, pads, prefixes, bias, buckets, lines, info, *, length):
    doc = ids[6]
    info[0] = length - jnp.where(doc == 0, pads[0], pads[1])
    info[5] = jnp.where(doc == 0, prefixes[0], prefixes[1])
    for to, at in enumerate((0, 1, 2, 3)):
        info[1 + to] = ids[at]
    for to, at in enumerate((4, 5, 6)):
        info[6 + to] = ids[at]
    picker = jnp.where(lax.broadcasted_iota(jnp.int32, (BUCKETS, 1), 0) == buckets[...], 1.0, 0.0).astype(BF16)
    left, total = bias[...], None
    for _ in range(3):
        part = left.astype(BF16)
        left = left - part.astype(F32)
        made = dot(part, picker)
        total = made if total is None else total + made
    lines[...] = jnp.zeros_like(lines)
    lines[:, : buckets.shape[1]] = total

def tables(ids, pads, prefixes, bias, buckets, length):
    smem, vmem = pl.BlockSpec(memory_space=pltpu.SMEM), pl.BlockSpec(memory_space=pltpu.VMEM)
    return pl.pallas_call(
        functools.partial(tables_kernel, length=length),
        in_specs=[smem] * 3 + [vmem] * 2,
        out_specs=[vmem, smem],
        out_shape=[jax.ShapeDtypeStruct((bias.shape[0], buckets.shape[1] + 1), F32), jax.ShapeDtypeStruct((16,), jnp.int32)],
        name="tables", compiler_params=pltpu.CompilerParams(vmem_limit_bytes=4 << 20),
    )(ids, pads, prefixes, bias, buckets)

def back_pieces(to, active, low, mine):
    @pl.loop(0, active.shape[1] // 512)
    def _(group):
        made = dot(active[:, pl.ds(pl.multiple_of(group * 512, 512), 512)], low, TN).astype(BF16)
        for b in range(4):
            rows = made[b * 128 : (b + 1) * 128]
            to[(4 * group + b) ^ mine] = jnp.concatenate([rows[:, q * 128 : (q + 1) * 128] for q in range(4)])

def in_pieces(to, slopes, turned, mine):
    @pl.loop(0, slopes.shape[1] // 512)
    def _(group):
        made = dot(turned, slopes[:, pl.ds(pl.multiple_of(group * 512, 512), 512)]).astype(BF16)
        for b in range(4):
            to[(4 * group + b) ^ mine] = made[:, b * 128 : (b + 1) * 128]

def front_kernel(info, far, far_other, near, q_l, k_l, v_l, lines, wq, wk, wv, gain1, gain2, gain3, cots, wo_h, win_h, wback_h,
                 hid, qs, ks, vs, expo_o, inv, att, send, active, slopes, turned, mixed, steep, rows,
                 wo, win, wback, expo, scores, skewed, edges, sems):
    count, width = near.shape
    hidden = win.shape[1]
    late = [pltpu.make_async_copy(a, b, sems.at[i]) for i, (a, b) in enumerate(((wo_h, wo), (win_h, win), (wback_h, wback)))]
    kept = lambda g: pltpu.make_async_copy(expo, expo_o.at[pl.ds(2 * g, 2)], sems.at[3])

    for copy in late:
        copy.start()
    for part, raw in enumerate((far, far_other)):
        tokens = raw[...].astype(F32)
        hid[part * count : (part + 1) * count, :] = (tokens * rms_scale(tokens) * gain1[...]).astype(BF16)
    h = hid[...]
    qs[...] = dot(h[:count], wq[...]).astype(BF16)
    ks[...] = dot(h, wk[...]).astype(BF16)
    vs[...] = dot(h, wv[...]).astype(BF16)
    column = lax.broadcasted_iota(jnp.int32, (1, 128), 1)
    for b in range(4):
        place = info[1 + b] + lax.broadcasted_iota(jnp.int32, (count, 1), 0)
        gate = jnp.where(place < info[0], 0.0, NEG)
        for head in range(2):
            edges[head, b * count : (b + 1) * count, :] = jnp.where(column == (64 if head == 0 else 0), gate, 0.0).astype(BF16)
    limit = info[0]

    @pl.loop(0, width // 128)
    def _(step):
        @pl.when(step > 0)
        def _():
            kept(step - 1).wait()

        cols = pl.ds(pl.multiple_of(step * 128, 128), 128)
        lane = lax.broadcasted_iota(jnp.int32, (1, 128), 1)
        first = lane < 64
        starts = [info[1 + b] for b in range(4)]
        keys = [k_l[:count, cols], k_l[count:, cols], ks[:count, cols], ks[count:, cols]]
        values = jnp.concatenate([v_l[:, cols], vs[:, cols]])
        query = jnp.concatenate([q_l[:, cols], qs[:, cols]])
        made = []
        for head in range(2):
            mine = jnp.where(first if head == 0 else lane >= 64, 1.0, 0.0).astype(BF16)
            one = jnp.where(lane == (64 if head == 0 else 0), 1.0, 0.0).astype(BF16)
            q = query * mine + one
            v = values * mine + one
            skewed[head] = skew(lines[pl.ds(2 * step + head, 1), :], lines.shape[1])
            k = jnp.concatenate(keys) * mine + edges[head]
            for half in range(2):
                s = dot(q[half * 256 : (half + 1) * 256], k, NT)
                for r in range(2):
                    for b in range(4):
                        at = starts[b] - starts[2 * half] + 896 - 128 * r
                        part = s[r * 128 : (r + 1) * 128, b * 256 : (b + 1) * 256] + skewed[head, :, pl.ds(pl.multiple_of(at, 128), 256)]
                        scores[head, half * 256 + r * 128 : half * 256 + (r + 1) * 128, b * 256 : (b + 1) * 256] = part
            accs = []
            for r in range(4):
                rs = slice(r * 128, (r + 1) * 128)
                value = scores[head, rs, :]
                top = jnp.max(value, axis=1, keepdims=True)
                e = jnp.exp(value - top).astype(BF16)
                expo[head, rs, :] = e
                accs.append(dot(e, v))
            acc = jnp.concatenate(accs)
            made.append((acc, 1.0 / (acc[:, 64:65] if head == 0 else acc[:, 0:1])))
        (a0, i0), (a1, i1) = made
        scale = jnp.where(first, i0, i1)
        att[:, cols] = (jnp.where(first, a0, a1) * scale).astype(BF16)
        inv[:, cols] = scale
        kept(step).start()

    for copy in late:
        copy.wait()
    for part, raw in enumerate((near, far)):
        spot = slice(part * count, (part + 1) * count)
        mixed[spot, :] = raw[...].astype(F32) + dot(att[spot, :], wo[...])
    values = mixed[...]
    inner = (values * rms_scale(values) * gain2[...]).astype(BF16)
    turned[...] = inner.T
    total = values
    for at in range(0, hidden, 512):
        lifted = jnp.maximum(dot(inner, win[:, at : at + 512]), 0.0).astype(BF16)
        active[:, at : at + 512] = lifted
        total = total + dot(lifted, wback[at : at + 512, :])
    scale = rms_scale(total)
    place = lax.broadcasted_iota(jnp.int32, (2 * count, 1), 0)
    place = jnp.where(place < count, place + info[1], place + (info[3] - count))
    live = jnp.where((place >= info[5]) & (place < limit), 1.0, 0.0)
    pool = jnp.sum(total * scale * gain3[...] * live, axis=0, keepdims=True)
    cot = jnp.where(info[8] == 0, cots[0:1, :], cots[1:2, :]) / (limit - info[5]).astype(F32)
    slope, grad_end = norm_back(live * cot, total, scale, gain3[...])
    steep[...] = slope
    rows[...] = jnp.concatenate([pool, grad_end, jnp.zeros((6, width), F32)])
    low = slope.astype(BF16)
    for at in range(0, hidden, 512):
        through = dot(low, wback[at : at + 512, :], NT).astype(BF16)
        slopes[:, at : at + 512] = jnp.where(active[:, at : at + 512] > 0, through, jnp.zeros_like(through))
    mine = info[6] & 15

    @pl.when(info[7] == 0)
    def _():
        in_pieces(send, slopes, turned[...], mine)

    @pl.when(info[7] == 1)
    def _():
        back_pieces(send, active, steep[...].astype(BF16), mine)

    kept(3).wait()


def front(info, far, far_other, near, q_l, k_l, v_l, lines, wq, wk, wv, gain1, gain2, gain3, cots, wo, win, wback):
    count, width = near.shape
    hidden = win.shape[1]
    heads, span = lines.shape
    shape = jax.ShapeDtypeStruct
    smem, vmem, free = (pl.BlockSpec(memory_space=m) for m in (pltpu.SMEM, pltpu.VMEM, pl.ANY))
    outs = [shape((2 * count, width), BF16), shape((count, width), BF16), shape((2 * count, width), BF16), shape((2 * count, width), BF16),
            shape((heads, 2 * count, 4 * count), BF16), shape((2 * count, width), F32), shape((2 * count, width), BF16),
            shape((16, width, 128), BF16), shape((2 * count, hidden), BF16), shape((2 * count, hidden), BF16),
            shape((width, 2 * count), BF16), shape((2 * count, width), F32), shape((2 * count, width), F32)]
    return pl.pallas_call(
        front_kernel,
        in_specs=[smem] + [vmem] * 14 + [free] * 3,
        out_specs=[vmem] * 4 + [free] + [vmem] * 9,
        out_shape=outs + [shape((8, width), F32)],
        scratch_shapes=[pltpu.VMEM(wo.shape, BF16), pltpu.VMEM(win.shape, BF16), pltpu.VMEM(wback.shape, BF16),
                        pltpu.VMEM((2, 2 * count, 4 * count), BF16), pltpu.VMEM((2, 2 * count, 4 * count), F32),
                        pltpu.VMEM((2, 128, span), F32), pltpu.VMEM((2, 4 * count, 128), BF16), pltpu.SemaphoreType.DMA((4,))],
        name="front", compiler_params=pltpu.CompilerParams(vmem_limit_bytes=38 << 20),
    )(info, far, far_other, near, q_l, k_l, v_l, lines, wq, wk, wv, gain1, gain2, gain3, cots, wo, win, wback)

def inner_kernel(info, slopes, win, grad_inner):
    total = None
    for at in range(0, slopes.shape[1], 512):
        part = dot(slopes[:, at : at + 512], win[:, at : at + 512], NT)
        total = part if total is None else total + part
    grad_inner[...] = total

def inner(info, slopes, win):
    smem, vmem = pl.BlockSpec(memory_space=pltpu.SMEM), pl.BlockSpec(memory_space=pltpu.VMEM)
    return pl.pallas_call(
        inner_kernel, in_specs=[smem, vmem, vmem], out_specs=vmem,
        out_shape=jax.ShapeDtypeStruct((slopes.shape[0], win.shape[0]), F32), name="inner", compiler_params=pltpu.CompilerParams(vmem_limit_bytes=10 << 20),
    )(info, slopes, win)

def through_kernel(info, grad_inner, mixed, steep, wo, att, gain2, grad_mixed, grad_attended, grad_out, rows):
    values = mixed[...]
    more, grad_two = norm_back(grad_inner[...], values, rms_scale(values), gain2[...])
    total = steep[...] + more
    grad_mixed[...] = total
    low = total.astype(BF16)
    grad_attended[...] = dot(low, wo[...], NT).astype(BF16)
    grad_out[...] = dot(att[...], low, TN).astype(BF16)
    rows[...] = jnp.concatenate([grad_two, jnp.zeros((7, low.shape[1]), F32)])

def through(info, grad_inner, mixed, steep, wo, att, gain2):
    n, width = mixed.shape
    smem, vmem = pl.BlockSpec(memory_space=pltpu.SMEM), pl.BlockSpec(memory_space=pltpu.VMEM)
    shape = jax.ShapeDtypeStruct
    return pl.pallas_call(
        through_kernel,
        in_specs=[smem] + [vmem] * 6,
        out_specs=[vmem] * 4,
        out_shape=[shape((n, width), F32), shape((n, width), BF16), shape((width, width), BF16), shape((8, width), F32)],
        name="through", compiler_params=pltpu.CompilerParams(vmem_limit_bytes=16 << 20),
    )(info, grad_inner, mixed, steep, wo, att, gain2)

def stay_kernel(info, active, slopes, turned, steep, blocks):
    high, lowest = (info[6] & 15) >> 2, info[6] & 3
    for side in range(2):
        @pl.when(info[7] == side)
        def _(side=side):
            low = steep[...].astype(BF16) if side == 0 else turned[...]
            for k in range(4):
                at = pl.ds(pl.multiple_of((k ^ high) * 512, 512), 512)
                made = dot(active[:, at], low, TN) if side == 0 else dot(low, slopes[:, at])
                for b in range(4):
                    piece = made[:, b * 128 : (b + 1) * 128]
                    if side == 0:
                        piece = made[b * 128 : (b + 1) * 128]
                        piece = jnp.concatenate([piece[:, q * 128 : (q + 1) * 128] for q in range(4)])
                    blocks[k, b ^ lowest] = piece.astype(BF16)

def stay_half(info, active, slopes, turned, steep):
    smem, vmem = pl.BlockSpec(memory_space=pltpu.SMEM), pl.BlockSpec(memory_space=pltpu.VMEM)
    width = steep.shape[1]
    return pl.pallas_call(
        stay_kernel, in_specs=[smem] + [vmem] * 4, out_specs=vmem,
        out_shape=jax.ShapeDtypeStruct((4, 4, width, 128), BF16), name="stay", compiler_params=pltpu.CompilerParams(vmem_limit_bytes=12 << 20),
    )(info, active, slopes, turned, steep)

def meet_kernel(kept, got, *outs):
    for k in (3, 1, 2, 0):
        outs[k][...] = added(kept[k], got[4 * k : 4 * k + 4])

def meet(kept, got):
    vmem = pl.BlockSpec(memory_space=pltpu.VMEM)
    return pl.pallas_call(
        meet_kernel, in_specs=[vmem] * 2, out_specs=[vmem] * 4, out_shape=[jax.ShapeDtypeStruct(kept.shape[1:], BF16)] * 4, name="meet", compiler_params=pltpu.CompilerParams(vmem_limit_bytes=20 << 20),
    )(kept, got)

CLASS = {(0, 0): 0, (1, 2): 0, (0, 1): 1, (1, 3): 1, (0, 2): 2, (0, 3): 3, (1, 0): 4, (1, 1): 5}

def back_kernel(info, ql, qr, kl, kr, vl, vr, gout, out, inv, expo, buckets, dense_rows, through_rows,
                hid_l_h, hid_r_h, near_h, near_other_h, far_h, far_other_h, wq_h, wk_h, wv_h, grad_out_h,
                keep_o, send_o, stay_o, leave_o, small,
                hid_l, hid_r, near, near_other, far, far_other, wq, wk, wv, made,
                keep, send, stay, leave, dq, dk, dv, offsets, sums, acc, slopes, sems):
    count, width = near.shape
    step = pl.program_id(0)
    pairs = width // 128
    late = [pltpu.make_async_copy(a, b, sems.at[i]) for i, (a, b) in enumerate((
        (hid_l_h, hid_l), (hid_r_h, hid_r), (near_h, near), (near_other_h, near_other), (far_h, far), (far_other_h, far_other),
        (wq_h, wq), (wk_h, wk), (wv_h, wv), (grad_out_h, made.at[0:width])))]
    done = [pltpu.make_async_copy(a, b, sems.at[10 + i]) for i, (a, b) in enumerate(((send, send_o), (keep, keep_o), (leave, leave_o), (stay, stay_o)))]

    @pl.when(step == 0)
    def _():
        for copy in late:
            copy.start()

    cols = pl.ds(pl.multiple_of(step * 128, 128), 128)
    lane = lax.broadcasted_iota(jnp.int32, (1, 128), 1)
    starts = [info[1 + b] for b in range(4)]
    keys = jnp.concatenate([kl[...], kr[...]])
    values = jnp.concatenate([vl[...], vr[...]])
    query = jnp.concatenate([ql[...], qr[...]])
    scaled = gout[...].astype(F32) * inv[...]
    prod = scaled * out[...].astype(F32)
    low = scaled.astype(BF16)
    query_t, low_t = query.T, low.T
    grads_q, grads_k, grads_v = None, [], []
    for head in range(2):
        mine = (lane < 64) if head == 0 else (lane >= 64)
        base = 64 if head == 0 else 0
        pick = jnp.where(mine, 1.0, 0.0).astype(BF16)
        delta = jnp.sum(jnp.where(mine, prod, 0.0), axis=1, keepdims=True)
        high = delta.astype(BF16).astype(F32)
        extra = jnp.where(lane == base, high, jnp.where(lane == base + 1, delta - high, 0.0)).astype(BF16)
        grad = low * pick + extra
        minus = jnp.where((lane == base) | (lane == base + 1), -1.0, 0.0).astype(BF16)
        for b in range(4):
            spot = slice(b * count, (b + 1) * count)
            ds = dot(grad, values[spot] * pick + minus, NT) * expo[head, :, spot].astype(F32)
            slopes[head, :, spot] = ds.astype(BF16)
            for chunk in range(2):
                upper, lower = (ds[chunk * count + r * 128 : chunk * count + (r + 1) * 128] for r in range(2))
                group = CLASS[chunk, b]
                block = jnp.concatenate([lower[:, :128], lower[:, 128:] + upper[:, :128], upper[:, 128:]], axis=1)
                if (chunk, b) in ((1, 2), (1, 3)):
                    block = block + sums[head, group]
                sums[head, group] = block
        part = dot(slopes[head], keys * pick)
        grads_q = part if grads_q is None else grads_q + part
        half = slice(head * 64, (head + 1) * 64)
        grads_k.append(dot(query_t[half], slopes[head]))
        grads_v.append(dot(low_t[half], expo[head]))
    dq[:, cols] = grads_q.astype(BF16)
    dk[:, cols] = jnp.concatenate(grads_k).astype(BF16).T
    dv[:, cols] = jnp.concatenate(grads_v).astype(BF16).T
    for head in range(2):
        acc[head] = jnp.zeros(acc.shape[1:], F32)
        for (chunk, b), group in CLASS.items():
            if (chunk, b) not in ((1, 2), (1, 3)):
                at = starts[b] - starts[2 * chunk] + 768
                to = pl.ds(pl.multiple_of(at, 128), 384)
                acc[head, :, to] += sums[head, group]
        rest = acc[head]
        n = 64
        while n >= 8:
            rest = rest[:n] + pltpu.roll(rest[n:], 2048 - n, 1)
            n //= 2
        line = rest[7:8]
        for r in range(6, -1, -1):
            line = rest[r : r + 1] + pltpu.roll(line, 2047, 1)
        offsets[pl.ds(2 * step + head, 1), :] = pltpu.roll(line, 127, 1)

    @pl.when(step == pairs - 1)
    def _():
        for copy in late:
            copy.wait()
        made[width : 2 * width, :] = (dot(hid_l[:count, :], dq[:count, :], TN) + dot(hid_r[:count, :], dq[count:, :], TN)).astype(BF16)
        for at, grads in ((2 * width, dk), (3 * width, dv)):
            made[at : at + width, :] = (dot(hid_l[...], grads[: 2 * count, :], TN) + dot(hid_r[...], grads[2 * count :, :], TN)).astype(BF16)
        me = info[6]
        size = made.shape[0] // 32

        @pl.loop(0, 16)
        def _(r):
            keep[r] = made[pl.ds(pl.multiple_of((r ^ me) * size, size), size), :]
            send[pl.ds(pl.multiple_of(r * size, size), size), :] = made[pl.ds(pl.multiple_of(((r + 16) ^ me) * size, size), size), :]

        gain = jnp.zeros((1, width), F32)
        for b, raw in enumerate((near, near_other, far, far_other)):
            spot = slice(b * count, (b + 1) * count)
            grad = dot(dk[spot, :], wk[...], NT) + dot(dv[spot, :], wv[...], NT)
            half = slice((b // 2) * count, (b // 2 + 1) * count)
            if b % 2 == 0:
                grad = grad + dot(dq[half, :], wq[...], NT)
                stay[half, :] = grad
            else:
                leave[half, :] = grad.astype(BF16)
            tokens = raw[...].astype(F32)
            gain = gain + jnp.sum(grad * (tokens * rms_scale(tokens)), axis=0, keepdims=True)
        leave[2 * count :, :] = two_terms(rows_of(dense_rows[0:1, :]))
        picker = jnp.where(lax.broadcasted_iota(jnp.int32, (128, 1), 0) == buckets[...], 1.0, 0.0).astype(BF16)
        left = offsets[...][:, : buckets.shape[1]]
        bias = None
        for _ in range(3):
            part = left.astype(BF16)
            left = left - part.astype(F32)
            bias = dot(part, picker, NT) if bias is None else bias + dot(part, picker, NT)
        bias = jnp.concatenate([bias, jnp.zeros((bias.shape[0], width - 128), F32)], axis=1)
        line = bias[0:1]
        for h in range(1, bias.shape[0]):
            line = line + pltpu.roll(bias[h : h + 1], 32 * h, 1)
        total = rows_of(gain, through_rows[0:1, :], dense_rows[1:2, :], line)
        small[...] = total
        send[16 * size :, :] = two_terms(total)
        for copy in done:
            copy.start()
        for copy in done:
            copy.wait()

def back(info, ql, qr, kl, kr, vl, vr, gout, out, inv, expo, buckets, dense_rows, through_rows,
         hid_l, hid_r, near, near_other, far, far_other, wq, wk, wv, grad_out):
    count, width = near.shape
    smem, free = pl.BlockSpec(memory_space=pltpu.SMEM), pl.BlockSpec(memory_space=pl.ANY)
    whole = lambda *dims: pl.BlockSpec(dims, lambda g: (0,) * len(dims))
    col = lambda n: pl.BlockSpec((n, 128), lambda g: (0, g))
    shape = jax.ShapeDtypeStruct
    size = 4 * width // 32
    outs = [shape((16, size, width), BF16), shape((16 * size + 16, width), BF16), shape((2 * count, width), F32), shape((2 * count + 16, width), BF16)]
    given = (hid_l, hid_r, near, near_other, far, far_other, wq, wk, wv)
    return pl.pallas_call(
        back_kernel,
        grid=(width // 128,),
        in_specs=[smem, col(count), col(count)] + [col(2 * count)] * 7 + [pl.BlockSpec((2, 2 * count, 4 * count), lambda g: (g, 0, 0)),
                  whole(*buckets.shape), whole(8, width), whole(8, width)] + [free] * 10,
        out_specs=[free] * 4 + [whole(8, width)],
        out_shape=outs + [shape((8, width), F32)],
        scratch_shapes=[pltpu.VMEM(g.shape, BF16) for g in given] + [pltpu.VMEM((4 * width, width), BF16)]
                       + [pltpu.VMEM(o.shape, o.dtype) for o in outs]
                       + [pltpu.VMEM((2 * count, width), BF16), pltpu.VMEM((4 * count, width), BF16), pltpu.VMEM((4 * count, width), BF16),
                          pltpu.VMEM((8, 2048), F32), pltpu.VMEM((2, 6, 128, 384), F32), pltpu.VMEM((2, 128, 2048), F32),
                          pltpu.VMEM((2, 2 * count, 4 * count), BF16), pltpu.SemaphoreType.DMA((14,))],
        name="back", compiler_params=pltpu.CompilerParams(vmem_limit_bytes=44 << 20),
    )(info, ql, qr, kl, kr, vl, vr, gout, out, inv, expo, buckets, dense_rows, through_rows, *given, grad_out)

def ending_kernel(info, stay, came, near, far, grad_mixed, gain, dense_rows, home, away):
    count, width = near.shape
    for part, raw in enumerate((near, far)):
        spot = slice(part * count, (part + 1) * count)
        tokens = raw[...].astype(F32)
        grad = stay[spot, :] + came[spot, :].astype(F32)
        more, _ = norm_back(grad, tokens, rms_scale(tokens), gain[...])
        value = (grad_mixed[spot, :] + more).astype(BF16)
        if part == 0:
            home[:count, :] = value
        else:
            away[:count, :] = value
    alive = (info[0] - info[5]).astype(F32)
    pool = two_terms((rows_of(dense_rows[0:1, :]) + one_value(came[2 * count :, :])) / alive)
    home[count:, :] = pool
    away[count:, :] = pool

def ending(info, stay, came, near, far, grad_mixed, gain, dense_rows):
    count, width = near.shape
    smem, vmem = pl.BlockSpec(memory_space=pltpu.SMEM), pl.BlockSpec(memory_space=pltpu.VMEM)
    shape = jax.ShapeDtypeStruct((count + 16, width), BF16)
    return pl.pallas_call(
        ending_kernel, in_specs=[smem] + [vmem] * 7, out_specs=[vmem] * 2, out_shape=[shape, shape], name="ending", compiler_params=pltpu.CompilerParams(vmem_limit_bytes=10 << 20)
    )(info, stay, came, near, far, grad_mixed, gain, dense_rows)

def place_kernel(firsts, info, *refs):
    parts, (back, front, rows, columns, sems) = refs[: len(firsts)], refs[-5:]
    mine = info[6] & 15
    for side in range(2):
        @pl.when(info[7] == side)
        def _(side=side):
            copies, n = [], 0
            for part, first in zip(parts, firsts):
                for i in range(part.shape[0]):
                    r = first + i
                    to = pl.ds(pl.multiple_of(((r & 15) ^ mine) * 128, 128), 128)
                    if (r >= 16) == (side == 1):
                        for q in range(4):
                            rows[n, :, q * 128 : (q + 1) * 128] = part[i, q * 128 : (q + 1) * 128, :].astype(F32)
                        copies.append(pltpu.make_async_copy(rows.at[n], back.at[to, :], sems.at[n]))
                    else:
                        columns[n] = part[i].astype(F32)
                        copies.append(pltpu.make_async_copy(columns.at[n], front.at[:, to], sems.at[n]))
                    copies[-1].start()
                    n += 1
            for copy in copies:
                copy.wait()

def place(info, parts, made, width):
    smem, vmem, far = (pl.BlockSpec(memory_space=m) for m in (pltpu.SMEM, pltpu.VMEM, pltpu.HBM))
    shape = jax.ShapeDtypeStruct
    count = sum(p.shape[0] for _, p in parts)
    return pl.pallas_call(
        functools.partial(place_kernel, [first for first, _ in parts]),
        in_specs=[smem] + [vmem] * len(parts) + [far] * len(made),
        out_specs=[far] * 2,
        out_shape=[shape((16 * 128, width), F32), shape((width, 16 * 128), F32)],
        scratch_shapes=[pltpu.VMEM((count, 128, width), F32), pltpu.VMEM((count, width, 128), F32), pltpu.SemaphoreType.DMA((count,))],
        input_output_aliases={1 + len(parts) + i: i for i in range(len(made))},
        name="place", compiler_params=pltpu.CompilerParams(vmem_limit_bytes=28 << 20),
    )(info, *[p for _, p in parts], *made)

def sort_kernel(firsts, info, *refs):
    parts, made, (tall, sems) = refs[: len(firsts)], refs[-6:-2], refs[-2:]
    size = parts[0].shape[1]
    mine = info[6]
    pieces = []
    for part, first in zip(parts, firsts):
        for i in range(part.shape[0]):
            tall[len(pieces)] = part[i].astype(F32)
            pieces.append(first + i)
    for top in range(4):
        @pl.when((mine >> 3) == top)
        def _(top=top):
            copies = []
            for n, r in enumerate(pieces):
                to = pl.ds(pl.multiple_of(((r ^ mine) & 7) * size, size), size)
                copies.append(pltpu.make_async_copy(tall.at[n], made[top ^ (r >> 3)].at[to, :], sems.at[n]))
                copies[-1].start()
            for copy in copies:
                copy.wait()

def sort(info, parts, made, width):
    smem, vmem, far = (pl.BlockSpec(memory_space=m) for m in (pltpu.SMEM, pltpu.VMEM, pltpu.HBM))
    shape = jax.ShapeDtypeStruct((width, width), F32)
    count = sum(p.shape[0] for _, p in parts)
    return pl.pallas_call(
        functools.partial(sort_kernel, [first for first, _ in parts]),
        in_specs=[smem] + [vmem] * len(parts) + [far] * len(made),
        out_specs=[far] * 4,
        out_shape=[shape] * 4,
        scratch_shapes=[pltpu.VMEM((count,) + parts[0][1].shape[1:], F32), pltpu.SemaphoreType.DMA((count,))],
        input_output_aliases={1 + len(parts) + i: i for i in range(len(made))},
        name="sort", compiler_params=pltpu.CompilerParams(vmem_limit_bytes=12 << 20),
    )(info, *[p for _, p in parts], *made)

def mix_kernel(*refs):
    for k in range(4):
        refs[4 + k][...] = added(*[term[k] for term in refs[:4]])

def mix(terms):
    block = terms[0].shape[1:]
    vmem = pl.BlockSpec(memory_space=pltpu.VMEM)
    return pl.pallas_call(
        mix_kernel, in_specs=[vmem] * 4, out_specs=[vmem] * 4, out_shape=[jax.ShapeDtypeStruct(block, BF16)] * 4, name="mix", compiler_params=pltpu.CompilerParams(vmem_limit_bytes=10 << 20),
    )(*terms)

def exchange(value, bits):
    size = lax.axis_size("dp") * lax.axis_size("blk")
    return lax.ppermute(value, ("dp", "blk"), [(i, i ^ bits) for i in range(size)])

def wait(*values):
    return lax.optimization_barrier(values)

def added(*terms):
    total = terms[0].astype(F32)
    for term in terms[1:]:
        total = total + term.astype(F32)
    return total.astype(BF16)

def local(inputs, w_query, w_key, w_value, w_out, w_in, w_back, norm1_gain, norm2_gain, final_gain, bias_table, bucket_table, prefix_len, pad_len, pooled_grad):
    rows, width = inputs.shape[1:]
    spot, far_off = lax.axis_index("blk"), lax.axis_index("dp")
    doc, core = spot // 2, spot % 2
    block = [doc * 2 + core, doc * 2 + 1 - core, (1 - doc) * 2 + core, (1 - doc) * 2 + 1 - core]
    line = [8, 16]
    further = [32 << b for b in range((lax.axis_size("dp") // 8).bit_length() - 1)]
    piece = core * 16 + doc * 4 + (far_off % 2) * 8 + (far_off // 2) % 4
    near = jnp.where(doc == 0, inputs[0], inputs[1])
    far_send = jnp.where(doc == 0, inputs[1], inputs[0])
    near, far_send = wait(near, far_send)
    far = exchange(far_send, ROW)
    near_other = exchange(near, CORE)
    slot = jnp.arange(8, dtype=jnp.int32)
    ids = jnp.zeros_like(slot)
    for i, value in enumerate([b * rows for b in block] + [piece, core, doc]):
        ids = jnp.where(slot == i, value, ids)
    gain1, gain2, gain3 = norm1_gain[None, :], norm2_gain[None, :], final_gain[None, :]
    buckets = bucket_table[None, :]
    hid_l, q_l, k_l, v_l, w_query, w_key, w_value = prepare(near, near_other, gain1, w_query, w_key, w_value)
    far, q_l, ids = wait(far, q_l, ids)
    far_other = exchange(far, CORE)
    lines, info = tables(ids, pad_len, prefix_len, bias_table.T, buckets, 4 * rows)
    (hid_r, q_r, k_r, v_r, expo, inverse, attended, send, active, slopes, turned, mixed, steep, dense_rows) = front(
        info, far, far_other, near, q_l, k_l, v_l, lines, w_query, w_key, w_value,
        gain1, gain2, gain3, pooled_grad, w_out, w_in, w_back)

    xy = [ROW, NEAR_X, ROW ^ NEAR_X]
    zz = [line[0], line[1], line[0] ^ line[1]]

    token, send = wait(info, send)
    got = exchange(send, CORE)
    kept = stay_half(token, active, slopes, turned, steep)
    token, kept = wait(token, kept)
    grad_inner = inner(token, slopes, w_in)
    token, grad_inner, got = wait(token, grad_inner, got)
    stays, *sends = meet(kept, got)

    token, sends, grad_inner = wait(token, sends, grad_inner)
    came = [exchange(sends[k], xy[k]) for k in (2, 0, 1)]
    grad_mixed, grad_attended, grad_out_w, through_rows = through(token, grad_inner, mixed, steep, w_out, attended, gain2)
    token, through_rows = wait(token, through_rows)
    rest_keep, rest_send, stay, leave, small = back(
        token, q_l, q_r, k_l, k_r, v_l, v_r, grad_attended, attended, inverse, expo, buckets, dense_rows, through_rows,
        hid_l, hid_r, near, near_other, far, far_other, w_query, w_key, w_value, grad_out_w)
    token, small, rest_send, leave, came = wait(token, small, rest_send, leave, came)

    rest_got = exchange(rest_send, CORE)
    hidden_got = exchange(leave, CORE)
    lines = mix([stays] + list(came))
    token, lines = wait(token, lines)
    took = [exchange(lines[k + 1], m) for k, m in enumerate(zz)]
    token, rest_got, hidden_got = wait(token, rest_got, hidden_got)

    count = rest_keep.shape[0] * rest_keep.shape[1]
    small = small + one_value(rest_got[count:])
    rest_got = rest_got[:count].reshape(rest_keep.shape)
    terms = two_terms(small)
    sends = [jnp.concatenate([added(rest_keep[4 * k : 4 * k + 4], rest_got[4 * k : 4 * k + 4]).reshape(-1, width), terms]) for k in (1, 2, 3)]
    token, sends = wait(token, sends)
    rest_came = [exchange(s, m) for s, m in zip(sends, xy)]
    home, away = ending(token, stay, hidden_got, near, far, grad_mixed, gain1, dense_rows)
    token, took, away = wait(token, took, away)

    whole = added(lines[0], *took)
    for bit in further:
        whole = added(whole, exchange(whole, bit))
    token, whole = wait(token, whole)
    back_line = [exchange(whole, m) for m in zz]
    away_got = exchange(away, ROW)
    token, rest_came = wait(token, rest_came)

    count = count // 4
    for part in rest_came:
        small = small + one_value(part[count:])
    rest_came = [part[:count].reshape((4,) + rest_keep.shape[1:]) for part in rest_came]
    piece = count // 4
    lines = added(rest_keep[:4], rest_got[:4], *rest_came).reshape(-1, width)
    send = jnp.concatenate([lines[piece : 2 * piece], lines[3 * piece :], two_terms(small)])
    token, send = wait(token, send)
    took = exchange(send, line[0])
    token, took = wait(token, took)
    small = small + one_value(took[2 * piece :])
    lines = added(jnp.concatenate([lines[:piece], lines[2 * piece : 3 * piece]]), took[: 2 * piece])
    send = jnp.concatenate([lines, two_terms(small)])
    token, send, back_line, away_got = wait(token, send, back_line, away_got)
    took = exchange(send, line[1])

    quarter = jnp.stack([whole] + back_line)
    token, quarter = wait(token, quarter)
    from_y, from_x = exchange(quarter, ROW), exchange(quarter, NEAR_X)
    pool_mine, pool_other = one_value(home[rows:])[:1], one_value(away_got[rows:])[:1]
    pooled = jnp.where(doc == 0, jnp.concatenate([pool_mine, pool_other]), jnp.concatenate([pool_other, pool_mine]))
    home, away_got = home[:rows], away_got[:rows]
    input_grad = jnp.where(doc == 0, jnp.stack([home, away_got]), jnp.stack([away_got, home]))
    token, took, pooled, input_grad = wait(token, took, pooled, input_grad)

    small = small + one_value(took[2 * piece :])
    rest = added(lines, jnp.concatenate([took[piece : 2 * piece], took[:piece]]))
    for bit in further:
        rest = added(rest, exchange(rest, bit))
        small = small + exchange(small, bit)
    token, rest = wait(token, rest)
    rest_back = exchange(rest, line[0])
    outs = [small[0], small[1], small[2], small[3, : bias_table.size].reshape(bias_table.shape[::-1]).T]
    token, from_y, from_x, outs = wait(token, from_y, from_x, outs)

    sends = [from_x[:2], from_y[2:]]
    here = jnp.concatenate([quarter, from_y, from_x])
    token, sends, here = wait(token, sends, here)
    far_a, far_b = exchange(sends[0], ROW), exchange(sends[1], NEAR_X)
    other = exchange(here, CORE)
    grads = place(token, [(0, here)], [], width)
    token, grads, rest_back, far_a, far_b, other = wait(token, grads, rest_back, far_a, far_b, other)

    fourth = jnp.stack([rest[:piece], rest_back[:piece], rest[piece:], rest_back[piece:]])
    far_pair = jnp.concatenate([far_a, far_b])
    token, fourth, far_pair = wait(token, fourth, far_pair)
    fourth_y, fourth_x = exchange(fourth, ROW), exchange(fourth, NEAR_X)
    other_far = exchange(far_pair, CORE)
    token, other_far = wait(token, other_far)
    out_back, out_in = place(token, [(12, far_pair), (16, other), (28, other_far)], grads, width)
    token, out_back, out_in, fourth_y, fourth_x = wait(token, out_back, out_in, fourth_y, fourth_x)

    sends = [fourth_x[:2], fourth_y[2:], jnp.concatenate([fourth, fourth_y, fourth_x])]
    token, sends = wait(token, sends)
    last_a, last_b, pair = (exchange(s, m) for s, m in zip(sends, (ROW, NEAR_X, CORE)))
    made = sort(token, [(0, sends[2])], [], width)
    token, made, last_a, last_b, pair = wait(token, made, last_a, last_b, pair)

    ends = exchange(jnp.concatenate([last_a, last_b]), CORE)
    made = sort(token, [(12, last_a), (14, last_b), (16, pair)], made, width)
    token, made, ends = wait(token, made, ends)
    out_out, out_query, out_key, out_value = sort(token, [(28, ends)], made, width)
    return (pooled, input_grad, out_query, out_key, out_value, out_out, out_in, out_back, *outs)

def solution(mesh):
    data = P("dp", "blk", None)
    placed = (data,) + (P(),) * 11 + (P("dp"), P("dp"), P("dp", None))
    return jax.shard_map(local, mesh=mesh, in_specs=placed, out_specs=(P("dp", None), data) + (P(),) * 10, check_vma=False)
```

```python
import functools
import jax, jax.numpy as jnp
from jax import lax
from jax.experimental import pallas as pl
from jax.experimental.pallas import tpu as pltpu
from jax.sharding import PartitionSpec as P

F32, BF16 = jnp.float32, jnp.bfloat16
NEG = -1000000000.0
NT = (((1,), (1,)), ((), ()))
TN = (((0,), (0,)), ((), ()))
NN = (((1,), (0,)), ((), ()))

def dot(a, b, dims=NN):
    return lax.dot_general(a, b, dims, preferred_element_type=F32)

def skew(row, width, dtype=F32):
    return pltpu.roll(jnp.broadcast_to(row, (128, width)), width - 127, 1, stride=1, stride_axis=0)


BUCKETS = 32
EPS = 1e-06
CORE, ROW, NEAR_X = 1, 2, 4

def rms_scale(values):
    return lax.rsqrt(jnp.mean(values * values, axis=-1, keepdims=True) + EPS)

def norm_back(grad_out, values, scale, gain):
    weighted = grad_out * gain
    inner = jnp.mean(weighted * values, axis=-1, keepdims=True)
    grad_in = scale * weighted - scale * scale * scale * values * inner
    return grad_in, jnp.sum(grad_out * values * scale, axis=0, keepdims=True)

def two_terms(value):
    high = value.astype(BF16)
    return jnp.concatenate([high, (value - high.astype(F32)).astype(BF16)])

def one_value(terms):
    return terms[:8].astype(F32) + terms[8:16].astype(F32)

def rows_of(*values):
    count = sum(v.shape[0] for v in values)
    return jnp.concatenate(list(values) + [jnp.zeros((8 - count, values[0].shape[1]), F32)])

def prepare_kernel(mine, other, gain, wq_h, wk_h, wv_h, hidden, query, keys, values, wq, wk, wv, sems):
    rows = mine.shape[0]
    load = [pltpu.make_async_copy(a, b, sems.at[i]) for i, (a, b) in enumerate(((wk_h, wk), (wv_h, wv), (wq_h, wq)))]
    for copy in load:
        copy.start()
    for part, raw in enumerate((mine, other)):
        tokens = raw[...].astype(F32)
        hidden[part * rows : (part + 1) * rows, :] = (tokens * rms_scale(tokens) * gain[...]).astype(BF16)
    h = hidden[...]
    load[0].wait()
    keys[...] = dot(h, wk[...]).astype(BF16)
    load[1].wait()
    values[...] = dot(h, wv[...]).astype(BF16)
    load[2].wait()
    query[...] = dot(h[:rows], wq[...]).astype(BF16)

def prepare(mine, other, gain, wq, wk, wv):
    rows, width = mine.shape
    shape = lambda n: jax.ShapeDtypeStruct((n, width), BF16)
    vmem, free = (pl.BlockSpec(memory_space=m) for m in (pltpu.VMEM, pl.ANY))
    return pl.pallas_call(
        prepare_kernel,
        in_specs=[vmem] * 3 + [free] * 3,
        out_specs=[vmem] * 7,
        out_shape=[shape(2 * rows), shape(rows), shape(2 * rows), shape(2 * rows)] + [shape(width)] * 3,
        scratch_shapes=[pltpu.SemaphoreType.DMA((3,))],
        name="prepare", compiler_params=pltpu.CompilerParams(vmem_limit_bytes=14 << 20),
    )(mine, other, gain, wq, wk, wv)

def tables_kernel(ids, pads, prefixes, bias, buckets, lines, info, *, length):
    doc = ids[6]
    info[0] = length - jnp.where(doc == 0, pads[0], pads[1])
    info[5] = jnp.where(doc == 0, prefixes[0], prefixes[1])
    for to, at in enumerate((0, 1, 2, 3)):
        info[1 + to] = ids[at]
    for to, at in enumerate((4, 5, 6)):
        info[6 + to] = ids[at]
    picker = jnp.where(lax.broadcasted_iota(jnp.int32, (BUCKETS, 1), 0) == buckets[...], 1.0, 0.0).astype(BF16)
    left, total = bias[...], None
    for _ in range(3):
        part = left.astype(BF16)
        left = left - part.astype(F32)
        made = dot(part, picker)
        total = made if total is None else total + made
    lines[...] = jnp.zeros_like(lines)
    lines[:, : buckets.shape[1]] = total

def tables(ids, pads, prefixes, bias, buckets, length):
    smem, vmem = pl.BlockSpec(memory_space=pltpu.SMEM), pl.BlockSpec(memory_space=pltpu.VMEM)
    return pl.pallas_call(
        functools.partial(tables_kernel, length=length),
        in_specs=[smem] * 3 + [vmem] * 2,
        out_specs=[vmem, smem],
        out_shape=[jax.ShapeDtypeStruct((bias.shape[0], buckets.shape[1] + 1), F32), jax.ShapeDtypeStruct((16,), jnp.int32)],
        name="tables", compiler_params=pltpu.CompilerParams(vmem_limit_bytes=4 << 20),
    )(ids, pads, prefixes, bias, buckets)

def back_pieces(to, active, low, mine):
    @pl.loop(0, active.shape[1] // 512)
    def _(group):
        made = dot(active[:, pl.ds(pl.multiple_of(group * 512, 512), 512)], low, TN).astype(BF16)
        for b in range(4):
            rows = made[b * 128 : (b + 1) * 128]
            to[(4 * group + b) ^ mine] = jnp.concatenate([rows[:, q * 128 : (q + 1) * 128] for q in range(4)])

def in_pieces(to, slopes, turned, mine):
    @pl.loop(0, slopes.shape[1] // 512)
    def _(group):
        made = dot(turned, slopes[:, pl.ds(pl.multiple_of(group * 512, 512), 512)]).astype(BF16)
        for b in range(4):
            to[(4 * group + b) ^ mine] = made[:, b * 128 : (b + 1) * 128]

def front_kernel(info, far, far_other, near, q_l, k_l, v_l, lines, wq, wk, wv, gain1, gain2, gain3, cots, wo_h, win_h, wback_h,
                 hid, qs, ks, vs, expo_o, inv, att, send, active, slopes, turned, mixed, steep, rows,
                 wo, win, wback, expo, scores, skewed, edges, sems):
    count, width = near.shape
    hidden = win.shape[1]
    late = [pltpu.make_async_copy(a, b, sems.at[i]) for i, (a, b) in enumerate(((wo_h, wo), (win_h, win), (wback_h, wback)))]
    kept = lambda g: pltpu.make_async_copy(expo, expo_o.at[pl.ds(2 * g, 2)], sems.at[3])

    for copy in late:
        copy.start()
    for part, raw in enumerate((far, far_other)):
        tokens = raw[...].astype(F32)
        hid[part * count : (part + 1) * count, :] = (tokens * rms_scale(tokens) * gain1[...]).astype(BF16)
    h = hid[...]
    qs[...] = dot(h[:count], wq[...]).astype(BF16)
    ks[...] = dot(h, wk[...]).astype(BF16)
    vs[...] = dot(h, wv[...]).astype(BF16)
    column = lax.broadcasted_iota(jnp.int32, (1, 128), 1)
    for b in range(4):
        place = info[1 + b] + lax.broadcasted_iota(jnp.int32, (count, 1), 0)
        gate = jnp.where(place < info[0], 0.0, NEG)
        for head in range(2):
            edges[head, b * count : (b + 1) * count, :] = jnp.where(column == (64 if head == 0 else 0), gate, 0.0).astype(BF16)
    limit = info[0]

    @pl.loop(0, width // 128)
    def _(step):
        @pl.when(step > 0)
        def _():
            kept(step - 1).wait()

        cols = pl.ds(pl.multiple_of(step * 128, 128), 128)
        lane = lax.broadcasted_iota(jnp.int32, (1, 128), 1)
        first = lane < 64
        starts = [info[1 + b] for b in range(4)]
        keys = [k_l[:count, cols], k_l[count:, cols], ks[:count, cols], ks[count:, cols]]
        values = jnp.concatenate([v_l[:, cols], vs[:, cols]])
        query = jnp.concatenate([q_l[:, cols], qs[:, cols]])
        made = []
        for head in range(2):
            mine = jnp.where(first if head == 0 else lane >= 64, 1.0, 0.0).astype(BF16)
            one = jnp.where(lane == (64 if head == 0 else 0), 1.0, 0.0).astype(BF16)
            q = query * mine + one
            v = values * mine + one
            skewed[head] = skew(lines[pl.ds(2 * step + head, 1), :], lines.shape[1])
            k = jnp.concatenate(keys) * mine + edges[head]
            for half in range(2):
                s = dot(q[half * 256 : (half + 1) * 256], k, NT)
                for r in range(2):
                    for b in range(4):
                        at = starts[b] - starts[2 * half] + 896 - 128 * r
                        part = s[r * 128 : (r + 1) * 128, b * 256 : (b + 1) * 256] + skewed[head, :, pl.ds(pl.multiple_of(at, 128), 256)]
                        scores[head, half * 256 + r * 128 : half * 256 + (r + 1) * 128, b * 256 : (b + 1) * 256] = part
            accs = []
            for r in range(4):
                rs = slice(r * 128, (r + 1) * 128)
                value = scores[head, rs, :]
                top = jnp.max(value, axis=1, keepdims=True)
                e = jnp.exp(value - top).astype(BF16)
                expo[head, rs, :] = e
                accs.append(dot(e, v))
            acc = jnp.concatenate(accs)
            made.append((acc, 1.0 / (acc[:, 64:65] if head == 0 else acc[:, 0:1])))
        (a0, i0), (a1, i1) = made
        scale = jnp.where(first, i0, i1)
        att[:, cols] = (jnp.where(first, a0, a1) * scale).astype(BF16)
        inv[:, cols] = scale
        kept(step).start()

    for copy in late:
        copy.wait()
    for part, raw in enumerate((near, far)):
        spot = slice(part * count, (part + 1) * count)
        mixed[spot, :] = raw[...].astype(F32) + dot(att[spot, :], wo[...])
    values = mixed[...]
    inner = (values * rms_scale(values) * gain2[...]).astype(BF16)
    turned[...] = inner.T
    total = values
    for at in range(0, hidden, 512):
        lifted = jnp.maximum(dot(inner, win[:, at : at + 512]), 0.0).astype(BF16)
        active[:, at : at + 512] = lifted
        total = total + dot(lifted, wback[at : at + 512, :])
    scale = rms_scale(total)
    place = lax.broadcasted_iota(jnp.int32, (2 * count, 1), 0)
    place = jnp.where(place < count, place + info[1], place + (info[3] - count))
    live = jnp.where((place >= info[5]) & (place < limit), 1.0, 0.0)
    pool = jnp.sum(total * scale * gain3[...] * live, axis=0, keepdims=True)
    cot = jnp.where(info[8] == 0, cots[0:1, :], cots[1:2, :]) / (limit - info[5]).astype(F32)
    slope, grad_end = norm_back(live * cot, total, scale, gain3[...])
    steep[...] = slope
    rows[...] = jnp.concatenate([pool, grad_end, jnp.zeros((6, width), F32)])
    low = slope.astype(BF16)
    for at in range(0, hidden, 512):
        through = dot(low, wback[at : at + 512, :], NT).astype(BF16)
        slopes[:, at : at + 512] = jnp.where(active[:, at : at + 512] > 0, through, jnp.zeros_like(through))
    mine = info[6] & 15

    @pl.when(info[7] == 0)
    def _():
        in_pieces(send, slopes, turned[...], mine)

    @pl.when(info[7] == 1)
    def _():
        back_pieces(send, active, steep[...].astype(BF16), mine)

    kept(3).wait()


def front(info, far, far_other, near, q_l, k_l, v_l, lines, wq, wk, wv, gain1, gain2, gain3, cots, wo, win, wback):
    count, width = near.shape
    hidden = win.shape[1]
    heads, span = lines.shape
    shape = jax.ShapeDtypeStruct
    smem, vmem, free = (pl.BlockSpec(memory_space=m) for m in (pltpu.SMEM, pltpu.VMEM, pl.ANY))
    outs = [shape((2 * count, width), BF16), shape((count, width), BF16), shape((2 * count, width), BF16), shape((2 * count, width), BF16),
            shape((heads, 2 * count, 4 * count), BF16), shape((2 * count, width), F32), shape((2 * count, width), BF16),
            shape((16, width, 128), BF16), shape((2 * count, hidden), BF16), shape((2 * count, hidden), BF16),
            shape((width, 2 * count), BF16), shape((2 * count, width), F32), shape((2 * count, width), F32)]
    return pl.pallas_call(
        front_kernel,
        in_specs=[smem] + [vmem] * 14 + [free] * 3,
        out_specs=[vmem] * 4 + [free] + [vmem] * 9,
        out_shape=outs + [shape((8, width), F32)],
        scratch_shapes=[pltpu.VMEM(wo.shape, BF16), pltpu.VMEM(win.shape, BF16), pltpu.VMEM(wback.shape, BF16),
                        pltpu.VMEM((2, 2 * count, 4 * count), BF16), pltpu.VMEM((2, 2 * count, 4 * count), F32),
                        pltpu.VMEM((2, 128, span), F32), pltpu.VMEM((2, 4 * count, 128), BF16), pltpu.SemaphoreType.DMA((4,))],
        name="front", compiler_params=pltpu.CompilerParams(vmem_limit_bytes=38 << 20),
    )(info, far, far_other, near, q_l, k_l, v_l, lines, wq, wk, wv, gain1, gain2, gain3, cots, wo, win, wback)

def inner_kernel(info, slopes, win, grad_inner):
    total = None
    for at in range(0, slopes.shape[1], 512):
        part = dot(slopes[:, at : at + 512], win[:, at : at + 512], NT)
        total = part if total is None else total + part
    grad_inner[...] = total

def inner(info, slopes, win):
    smem, vmem = pl.BlockSpec(memory_space=pltpu.SMEM), pl.BlockSpec(memory_space=pltpu.VMEM)
    return pl.pallas_call(
        inner_kernel, in_specs=[smem, vmem, vmem], out_specs=vmem,
        out_shape=jax.ShapeDtypeStruct((slopes.shape[0], win.shape[0]), F32), name="inner", compiler_params=pltpu.CompilerParams(vmem_limit_bytes=10 << 20),
    )(info, slopes, win)

def through_kernel(info, grad_inner, mixed, steep, wo, att, gain2, grad_mixed, grad_attended, grad_out, rows):
    values = mixed[...]
    more, grad_two = norm_back(grad_inner[...], values, rms_scale(values), gain2[...])
    total = steep[...] + more
    grad_mixed[...] = total
    low = total.astype(BF16)
    grad_attended[...] = dot(low, wo[...], NT).astype(BF16)
    grad_out[...] = dot(att[...], low, TN).astype(BF16)
    rows[...] = jnp.concatenate([grad_two, jnp.zeros((7, low.shape[1]), F32)])

def through(info, grad_inner, mixed, steep, wo, att, gain2):
    n, width = mixed.shape
    smem, vmem = pl.BlockSpec(memory_space=pltpu.SMEM), pl.BlockSpec(memory_space=pltpu.VMEM)
    shape = jax.ShapeDtypeStruct
    return pl.pallas_call(
        through_kernel,
        in_specs=[smem] + [vmem] * 6,
        out_specs=[vmem] * 4,
        out_shape=[shape((n, width), F32), shape((n, width), BF16), shape((width, width), BF16), shape((8, width), F32)],
        name="through", compiler_params=pltpu.CompilerParams(vmem_limit_bytes=16 << 20),
    )(info, grad_inner, mixed, steep, wo, att, gain2)

def stay_kernel(info, active, slopes, turned, steep, blocks):
    high, lowest = (info[6] & 15) >> 2, info[6] & 3
    for side in range(2):
        @pl.when(info[7] == side)
        def _(side=side):
            low = steep[...].astype(BF16) if side == 0 else turned[...]
            for k in range(4):
                at = pl.ds(pl.multiple_of((k ^ high) * 512, 512), 512)
                made = dot(active[:, at], low, TN) if side == 0 else dot(low, slopes[:, at])
                for b in range(4):
                    piece = made[:, b * 128 : (b + 1) * 128]
                    if side == 0:
                        piece = made[b * 128 : (b + 1) * 128]
                        piece = jnp.concatenate([piece[:, q * 128 : (q + 1) * 128] for q in range(4)])
                    blocks[k, b ^ lowest] = piece.astype(BF16)

def stay_half(info, active, slopes, turned, steep):
    smem, vmem = pl.BlockSpec(memory_space=pltpu.SMEM), pl.BlockSpec(memory_space=pltpu.VMEM)
    width = steep.shape[1]
    return pl.pallas_call(
        stay_kernel, in_specs=[smem] + [vmem] * 4, out_specs=vmem,
        out_shape=jax.ShapeDtypeStruct((4, 4, width, 128), BF16), name="stay", compiler_params=pltpu.CompilerParams(vmem_limit_bytes=12 << 20),
    )(info, active, slopes, turned, steep)

def meet_kernel(kept, got, *outs):
    for k in (3, 1, 2, 0):
        outs[k][...] = added(kept[k], got[4 * k : 4 * k + 4])

def meet(kept, got):
    vmem = pl.BlockSpec(memory_space=pltpu.VMEM)
    return pl.pallas_call(
        meet_kernel, in_specs=[vmem] * 2, out_specs=[vmem] * 4, out_shape=[jax.ShapeDtypeStruct(kept.shape[1:], BF16)] * 4, name="meet", compiler_params=pltpu.CompilerParams(vmem_limit_bytes=20 << 20),
    )(kept, got)

CLASS = {(0, 0): 0, (1, 2): 0, (0, 1): 1, (1, 3): 1, (0, 2): 2, (0, 3): 3, (1, 0): 4, (1, 1): 5}

def back_kernel(info, ql, qr, kl, kr, vl, vr, gout, out, inv, expo, buckets, dense_rows, through_rows,
                hid_l_h, hid_r_h, near_h, near_other_h, far_h, far_other_h, wq_h, wk_h, wv_h, grad_out_h,
                keep_o, send_o, stay_o, leave_o, small,
                hid_l, hid_r, near, near_other, far, far_other, wq, wk, wv, made,
                keep, send, stay, leave, dq, dk, dv, offsets, sums, acc, slopes, sems):
    count, width = near.shape
    step = pl.program_id(0)
    pairs = width // 128
    late = [pltpu.make_async_copy(a, b, sems.at[i]) for i, (a, b) in enumerate((
        (hid_l_h, hid_l), (hid_r_h, hid_r), (near_h, near), (near_other_h, near_other), (far_h, far), (far_other_h, far_other),
        (wq_h, wq), (wk_h, wk), (wv_h, wv), (grad_out_h, made.at[0:width])))]
    done = [pltpu.make_async_copy(a, b, sems.at[10 + i]) for i, (a, b) in enumerate(((send, send_o), (keep, keep_o), (leave, leave_o), (stay, stay_o)))]

    @pl.when(step == 0)
    def _():
        for copy in late:
            copy.start()

    cols = pl.ds(pl.multiple_of(step * 128, 128), 128)
    lane = lax.broadcasted_iota(jnp.int32, (1, 128), 1)
    starts = [info[1 + b] for b in range(4)]
    keys = jnp.concatenate([kl[...], kr[...]])
    values = jnp.concatenate([vl[...], vr[...]])
    query = jnp.concatenate([ql[...], qr[...]])
    scaled = gout[...].astype(F32) * inv[...]
    prod = scaled * out[...].astype(F32)
    low = scaled.astype(BF16)
    query_t, low_t = query.T, low.T
    grads_q, grads_k, grads_v = None, [], []
    for head in range(2):
        mine = (lane < 64) if head == 0 else (lane >= 64)
        base = 64 if head == 0 else 0
        pick = jnp.where(mine, 1.0, 0.0).astype(BF16)
        delta = jnp.sum(jnp.where(mine, prod, 0.0), axis=1, keepdims=True)
        high = delta.astype(BF16).astype(F32)
        extra = jnp.where(lane == base, high, jnp.where(lane == base + 1, delta - high, 0.0)).astype(BF16)
        grad = low * pick + extra
        minus = jnp.where((lane == base) | (lane == base + 1), -1.0, 0.0).astype(BF16)
        for b in range(4):
            spot = slice(b * count, (b + 1) * count)
            ds = dot(grad, values[spot] * pick + minus, NT) * expo[head, :, spot].astype(F32)
            slopes[head, :, spot] = ds.astype(BF16)
            for chunk in range(2):
                upper, lower = (ds[chunk * count + r * 128 : chunk * count + (r + 1) * 128] for r in range(2))
                group = CLASS[chunk, b]
                block = jnp.concatenate([lower[:, :128], lower[:, 128:] + upper[:, :128], upper[:, 128:]], axis=1)
                if (chunk, b) in ((1, 2), (1, 3)):
                    block = block + sums[head, group]
                sums[head, group] = block
        part = dot(slopes[head], keys * pick)
        grads_q = part if grads_q is None else grads_q + part
        half = slice(head * 64, (head + 1) * 64)
        grads_k.append(dot(query_t[half], slopes[head]))
        grads_v.append(dot(low_t[half], expo[head]))
    dq[:, cols] = grads_q.astype(BF16)
    dk[:, cols] = jnp.concatenate(grads_k).astype(BF16).T
    dv[:, cols] = jnp.concatenate(grads_v).astype(BF16).T
    for head in range(2):
        acc[head] = jnp.zeros(acc.shape[1:], F32)
        for (chunk, b), group in CLASS.items():
            if (chunk, b) not in ((1, 2), (1, 3)):
                at = starts[b] - starts[2 * chunk] + 768
                to = pl.ds(pl.multiple_of(at, 128), 384)
                acc[head, :, to] += sums[head, group]
        rest = acc[head]
        n = 64
        while n >= 8:
            rest = rest[:n] + pltpu.roll(rest[n:], 2048 - n, 1)
            n //= 2
        line = rest[7:8]
        for r in range(6, -1, -1):
            line = rest[r : r + 1] + pltpu.roll(line, 2047, 1)
        offsets[pl.ds(2 * step + head, 1), :] = pltpu.roll(line, 127, 1)

    @pl.when(step == pairs - 1)
    def _():
        for copy in late:
            copy.wait()
        made[width : 2 * width, :] = (dot(hid_l[:count, :], dq[:count, :], TN) + dot(hid_r[:count, :], dq[count:, :], TN)).astype(BF16)
        for at, grads in ((2 * width, dk), (3 * width, dv)):
            made[at : at + width, :] = (dot(hid_l[...], grads[: 2 * count, :], TN) + dot(hid_r[...], grads[2 * count :, :], TN)).astype(BF16)
        me = info[6]
        size = made.shape[0] // 32

        @pl.loop(0, 16)
        def _(r):
            keep[r] = made[pl.ds(pl.multiple_of((r ^ me) * size, size), size), :]
            send[pl.ds(pl.multiple_of(r * size, size), size), :] = made[pl.ds(pl.multiple_of(((r + 16) ^ me) * size, size), size), :]

        gain = jnp.zeros((1, width), F32)
        for b, raw in enumerate((near, near_other, far, far_other)):
            spot = slice(b * count, (b + 1) * count)
            grad = dot(dk[spot, :], wk[...], NT) + dot(dv[spot, :], wv[...], NT)
            half = slice((b // 2) * count, (b // 2 + 1) * count)
            if b % 2 == 0:
                grad = grad + dot(dq[half, :], wq[...], NT)
                stay[half, :] = grad
            else:
                leave[half, :] = grad.astype(BF16)
            tokens = raw[...].astype(F32)
            gain = gain + jnp.sum(grad * (tokens * rms_scale(tokens)), axis=0, keepdims=True)
        leave[2 * count :, :] = two_terms(rows_of(dense_rows[0:1, :]))
        picker = jnp.where(lax.broadcasted_iota(jnp.int32, (128, 1), 0) == buckets[...], 1.0, 0.0).astype(BF16)
        left = offsets[...][:, : buckets.shape[1]]
        bias = None
        for _ in range(3):
            part = left.astype(BF16)
            left = left - part.astype(F32)
            bias = dot(part, picker, NT) if bias is None else bias + dot(part, picker, NT)
        bias = jnp.concatenate([bias, jnp.zeros((bias.shape[0], width - 128), F32)], axis=1)
        line = bias[0:1]
        for h in range(1, bias.shape[0]):
            line = line + pltpu.roll(bias[h : h + 1], 32 * h, 1)
        total = rows_of(gain, through_rows[0:1, :], dense_rows[1:2, :], line)
        small[...] = total
        send[16 * size :, :] = two_terms(total)
        for copy in done:
            copy.start()
        for copy in done:
            copy.wait()

def back(info, ql, qr, kl, kr, vl, vr, gout, out, inv, expo, buckets, dense_rows, through_rows,
         hid_l, hid_r, near, near_other, far, far_other, wq, wk, wv, grad_out):
    count, width = near.shape
    smem, free = pl.BlockSpec(memory_space=pltpu.SMEM), pl.BlockSpec(memory_space=pl.ANY)
    whole = lambda *dims: pl.BlockSpec(dims, lambda g: (0,) * len(dims))
    col = lambda n: pl.BlockSpec((n, 128), lambda g: (0, g))
    shape = jax.ShapeDtypeStruct
    size = 4 * width // 32
    outs = [shape((16, size, width), BF16), shape((16 * size + 16, width), BF16), shape((2 * count, width), F32), shape((2 * count + 16, width), BF16)]
    given = (hid_l, hid_r, near, near_other, far, far_other, wq, wk, wv)
    return pl.pallas_call(
        back_kernel,
        grid=(width // 128,),
        in_specs=[smem, col(count), col(count)] + [col(2 * count)] * 7 + [pl.BlockSpec((2, 2 * count, 4 * count), lambda g: (g, 0, 0)),
                  whole(*buckets.shape), whole(8, width), whole(8, width)] + [free] * 10,
        out_specs=[free] * 4 + [whole(8, width)],
        out_shape=outs + [shape((8, width), F32)],
        scratch_shapes=[pltpu.VMEM(g.shape, BF16) for g in given] + [pltpu.VMEM((4 * width, width), BF16)]
                       + [pltpu.VMEM(o.shape, o.dtype) for o in outs]
                       + [pltpu.VMEM((2 * count, width), BF16), pltpu.VMEM((4 * count, width), BF16), pltpu.VMEM((4 * count, width), BF16),
                          pltpu.VMEM((8, 2048), F32), pltpu.VMEM((2, 6, 128, 384), F32), pltpu.VMEM((2, 128, 2048), F32),
                          pltpu.VMEM((2, 2 * count, 4 * count), BF16), pltpu.SemaphoreType.DMA((14,))],
        name="back", compiler_params=pltpu.CompilerParams(vmem_limit_bytes=44 << 20),
    )(info, ql, qr, kl, kr, vl, vr, gout, out, inv, expo, buckets, dense_rows, through_rows, *given, grad_out)

def ending_kernel(info, stay, came, near, far, grad_mixed, gain, dense_rows, home, away):
    count, width = near.shape
    for part, raw in enumerate((near, far)):
        spot = slice(part * count, (part + 1) * count)
        tokens = raw[...].astype(F32)
        grad = stay[spot, :] + came[spot, :].astype(F32)
        more, _ = norm_back(grad, tokens, rms_scale(tokens), gain[...])
        value = (grad_mixed[spot, :] + more).astype(BF16)
        if part == 0:
            home[:count, :] = value
        else:
            away[:count, :] = value
    alive = (info[0] - info[5]).astype(F32)
    pool = two_terms((rows_of(dense_rows[0:1, :]) + one_value(came[2 * count :, :])) / alive)
    home[count:, :] = pool
    away[count:, :] = pool

def ending(info, stay, came, near, far, grad_mixed, gain, dense_rows):
    count, width = near.shape
    smem, vmem = pl.BlockSpec(memory_space=pltpu.SMEM), pl.BlockSpec(memory_space=pltpu.VMEM)
    shape = jax.ShapeDtypeStruct((count + 16, width), BF16)
    return pl.pallas_call(
        ending_kernel, in_specs=[smem] + [vmem] * 7, out_specs=[vmem] * 2, out_shape=[shape, shape], name="ending", compiler_params=pltpu.CompilerParams(vmem_limit_bytes=10 << 20)
    )(info, stay, came, near, far, grad_mixed, gain, dense_rows)

def place_kernel(firsts, info, *refs):
    parts, (back, front, rows, columns, sems) = refs[: len(firsts)], refs[-5:]
    mine = info[6] & 15
    for side in range(2):
        @pl.when(info[7] == side)
        def _(side=side):
            copies, n = [], 0
            for part, first in zip(parts, firsts):
                for i in range(part.shape[0]):
                    r = first + i
                    to = pl.ds(pl.multiple_of(((r & 15) ^ mine) * 128, 128), 128)
                    if (r >= 16) == (side == 1):
                        for q in range(4):
                            rows[n, :, q * 128 : (q + 1) * 128] = part[i, q * 128 : (q + 1) * 128, :].astype(F32)
                        copies.append(pltpu.make_async_copy(rows.at[n], back.at[to, :], sems.at[n]))
                    else:
                        columns[n] = part[i].astype(F32)
                        copies.append(pltpu.make_async_copy(columns.at[n], front.at[:, to], sems.at[n]))
                    copies[-1].start()
                    n += 1
            for copy in copies:
                copy.wait()

def place(info, parts, made, width):
    smem, vmem, far = (pl.BlockSpec(memory_space=m) for m in (pltpu.SMEM, pltpu.VMEM, pltpu.HBM))
    shape = jax.ShapeDtypeStruct
    count = sum(p.shape[0] for _, p in parts)
    return pl.pallas_call(
        functools.partial(place_kernel, [first for first, _ in parts]),
        in_specs=[smem] + [vmem] * len(parts) + [far] * len(made),
        out_specs=[far] * 2,
        out_shape=[shape((16 * 128, width), F32), shape((width, 16 * 128), F32)],
        scratch_shapes=[pltpu.VMEM((count, 128, width), F32), pltpu.VMEM((count, width, 128), F32), pltpu.SemaphoreType.DMA((count,))],
        input_output_aliases={1 + len(parts) + i: i for i in range(len(made))},
        name="place", compiler_params=pltpu.CompilerParams(vmem_limit_bytes=28 << 20),
    )(info, *[p for _, p in parts], *made)

def sort_kernel(firsts, info, *refs):
    parts, made, (tall, sems) = refs[: len(firsts)], refs[-6:-2], refs[-2:]
    size = parts[0].shape[1]
    mine = info[6]
    pieces = []
    for part, first in zip(parts, firsts):
        for i in range(part.shape[0]):
            tall[len(pieces)] = part[i].astype(F32)
            pieces.append(first + i)
    for top in range(4):
        @pl.when((mine >> 3) == top)
        def _(top=top):
            copies = []
            for n, r in enumerate(pieces):
                to = pl.ds(pl.multiple_of(((r ^ mine) & 7) * size, size), size)
                copies.append(pltpu.make_async_copy(tall.at[n], made[top ^ (r >> 3)].at[to, :], sems.at[n]))
                copies[-1].start()
            for copy in copies:
                copy.wait()

def sort(info, parts, made, width):
    smem, vmem, far = (pl.BlockSpec(memory_space=m) for m in (pltpu.SMEM, pltpu.VMEM, pltpu.HBM))
    shape = jax.ShapeDtypeStruct((width, width), F32)
    count = sum(p.shape[0] for _, p in parts)
    return pl.pallas_call(
        functools.partial(sort_kernel, [first for first, _ in parts]),
        in_specs=[smem] + [vmem] * len(parts) + [far] * len(made),
        out_specs=[far] * 4,
        out_shape=[shape] * 4,
        scratch_shapes=[pltpu.VMEM((count,) + parts[0][1].shape[1:], F32), pltpu.SemaphoreType.DMA((count,))],
        input_output_aliases={1 + len(parts) + i: i for i in range(len(made))},
        name="sort", compiler_params=pltpu.CompilerParams(vmem_limit_bytes=12 << 20),
    )(info, *[p for _, p in parts], *made)

def mix_kernel(*refs):
    for k in range(4):
        refs[4 + k][...] = added(*[term[k] for term in refs[:4]])

def mix(terms):
    block = terms[0].shape[1:]
    vmem = pl.BlockSpec(memory_space=pltpu.VMEM)
    return pl.pallas_call(
        mix_kernel, in_specs=[vmem] * 4, out_specs=[vmem] * 4, out_shape=[jax.ShapeDtypeStruct(block, BF16)] * 4, name="mix", compiler_params=pltpu.CompilerParams(vmem_limit_bytes=10 << 20),
    )(*terms)

def exchange(value, bits):
    size = lax.axis_size("dp") * lax.axis_size("blk")
    return lax.ppermute(value, ("dp", "blk"), [(i, i ^ bits) for i in range(size)])

def wait(*values):
    return lax.optimization_barrier(values)

def added(*terms):
    total = terms[0].astype(F32)
    for term in terms[1:]:
        total = total + term.astype(F32)
    return total.astype(BF16)

def local(inputs, w_query, w_key, w_value, w_out, w_in, w_back, norm1_gain, norm2_gain, final_gain, bias_table, bucket_table, prefix_len, pad_len, pooled_grad):
    rows, width = inputs.shape[1:]
    spot, far_off = lax.axis_index("blk"), lax.axis_index("dp")
    doc, core = spot // 2, spot % 2
    block = [doc * 2 + core, doc * 2 + 1 - core, (1 - doc) * 2 + core, (1 - doc) * 2 + 1 - core]
    line = [8, 16]
    further = [32 << b for b in range((lax.axis_size("dp") // 8).bit_length() - 1)]
    piece = core * 16 + doc * 4 + (far_off % 2) * 8 + (far_off // 2) % 4
    near = jnp.where(doc == 0, inputs[0], inputs[1])
    far_send = jnp.where(doc == 0, inputs[1], inputs[0])
    near, far_send = wait(near, far_send)
    far = exchange(far_send, ROW)
    near_other = exchange(near, CORE)
    slot = jnp.arange(8, dtype=jnp.int32)
    ids = jnp.zeros_like(slot)
    for i, value in enumerate([b * rows for b in block] + [piece, core, doc]):
        ids = jnp.where(slot == i, value, ids)
    gain1, gain2, gain3 = norm1_gain[None, :], norm2_gain[None, :], final_gain[None, :]
    buckets = bucket_table[None, :]
    hid_l, q_l, k_l, v_l, w_query, w_key, w_value = prepare(near, near_other, gain1, w_query, w_key, w_value)
    far, q_l, ids = wait(far, q_l, ids)
    far_other = exchange(far, CORE)
    lines, info = tables(ids, pad_len, prefix_len, bias_table.T, buckets, 4 * rows)
    (hid_r, q_r, k_r, v_r, expo, inverse, attended, send, active, slopes, turned, mixed, steep, dense_rows) = front(
        info, far, far_other, near, q_l, k_l, v_l, lines, w_query, w_key, w_value,
        gain1, gain2, gain3, pooled_grad, w_out, w_in, w_back)

    xy = [ROW, NEAR_X, ROW ^ NEAR_X]
    zz = [line[0], line[1], line[0] ^ line[1]]

    token, send = wait(info, send)
    got = exchange(send, CORE)
    kept = stay_half(token, active, slopes, turned, steep)
    token, kept = wait(token, kept)
    grad_inner = inner(token, slopes, w_in)
    token, grad_inner, got = wait(token, grad_inner, got)
    stays, *sends = meet(kept, got)

    token, sends, grad_inner = wait(token, sends, grad_inner)
    came = [exchange(sends[k], xy[k]) for k in (2, 0, 1)]
    grad_mixed, grad_attended, grad_out_w, through_rows = through(token, grad_inner, mixed, steep, w_out, attended, gain2)
    token, through_rows = wait(token, through_rows)
    rest_keep, rest_send, stay, leave, small = back(
        token, q_l, q_r, k_l, k_r, v_l, v_r, grad_attended, attended, inverse, expo, buckets, dense_rows, through_rows,
        hid_l, hid_r, near, near_other, far, far_other, w_query, w_key, w_value, grad_out_w)
    token, small, rest_send, leave, came = wait(token, small, rest_send, leave, came)

    rest_got = exchange(rest_send, CORE)
    hidden_got = exchange(leave, CORE)
    lines = mix([stays] + list(came))
    token, lines = wait(token, lines)
    took = [exchange(lines[k + 1], m) for k, m in enumerate(zz)]
    token, rest_got, hidden_got = wait(token, rest_got, hidden_got)

    count = rest_keep.shape[0] * rest_keep.shape[1]
    small = small + one_value(rest_got[count:])
    rest_got = rest_got[:count].reshape(rest_keep.shape)
    terms = two_terms(small)
    sends = [jnp.concatenate([added(rest_keep[4 * k : 4 * k + 4], rest_got[4 * k : 4 * k + 4]).reshape(-1, width), terms]) for k in (1, 2, 3)]
    token, sends = wait(token, sends)
    rest_came = [exchange(s, m) for s, m in zip(sends, xy)]
    home, away = ending(token, stay, hidden_got, near, far, grad_mixed, gain1, dense_rows)
    token, took, away = wait(token, took, away)

    whole = added(lines[0], *took)
    for bit in further:
        whole = added(whole, exchange(whole, bit))
    token, whole = wait(token, whole)
    back_line = [exchange(whole, m) for m in zz]
    away_got = exchange(away, ROW)
    token, rest_came = wait(token, rest_came)

    count = count // 4
    for part in rest_came:
        small = small + one_value(part[count:])
    rest_came = [part[:count].reshape((4,) + rest_keep.shape[1:]) for part in rest_came]
    piece = count // 4
    lines = added(rest_keep[:4], rest_got[:4], *rest_came).reshape(-1, width)
    send = jnp.concatenate([lines[piece : 2 * piece], lines[3 * piece :], two_terms(small)])
    token, send = wait(token, send)
    took = exchange(send, line[0])
    token, took = wait(token, took)
    small = small + one_value(took[2 * piece :])
    lines = added(jnp.concatenate([lines[:piece], lines[2 * piece : 3 * piece]]), took[: 2 * piece])
    send = jnp.concatenate([lines, two_terms(small)])
    token, send, back_line, away_got = wait(token, send, back_line, away_got)
    took = exchange(send, line[1])

    quarter = jnp.stack([whole] + back_line)
    token, quarter = wait(token, quarter)
    from_y, from_x = exchange(quarter, ROW), exchange(quarter, NEAR_X)
    pool_mine, pool_other = one_value(home[rows:])[:1], one_value(away_got[rows:])[:1]
    pooled = jnp.where(doc == 0, jnp.concatenate([pool_mine, pool_other]), jnp.concatenate([pool_other, pool_mine]))
    home, away_got = home[:rows], away_got[:rows]
    input_grad = jnp.where(doc == 0, jnp.stack([home, away_got]), jnp.stack([away_got, home]))
    token, took, pooled, input_grad = wait(token, took, pooled, input_grad)

    small = small + one_value(took[2 * piece :])
    rest = added(lines, jnp.concatenate([took[piece : 2 * piece], took[:piece]]))
    for bit in further:
        rest = added(rest, exchange(rest, bit))
        small = small + exchange(small, bit)
    token, rest = wait(token, rest)
    rest_back = exchange(rest, line[0])
    outs = [small[0], small[1], small[2], small[3, : bias_table.size].reshape(bias_table.shape[::-1]).T]
    token, from_y, from_x, outs = wait(token, from_y, from_x, outs)

    sends = [from_x[:2], from_y[2:]]
    far_a, far_b = exchange(sends[0], ROW), exchange(sends[1], NEAR_X)
    quarter, from_y, from_x, _ = wait(quarter, from_y, from_x, sends)
    here = jnp.concatenate([quarter, from_y, from_x])
    token, here = wait(token, here)
    other = exchange(here, CORE)
    grads = place(token, [(0, here)], [], width)
    token, grads, rest_back, far_a, far_b, other = wait(token, grads, rest_back, far_a, far_b, other)

    fourth = jnp.stack([rest[:piece], rest_back[:piece], rest[piece:], rest_back[piece:]])
    far_pair = jnp.concatenate([far_a, far_b])
    token, fourth, far_pair = wait(token, fourth, far_pair)
    fourth_y, fourth_x = exchange(fourth, ROW), exchange(fourth, NEAR_X)
    other_far = exchange(far_pair, CORE)
    token, other_far = wait(token, other_far)
    out_back, out_in = place(token, [(12, far_pair), (16, other), (28, other_far)], grads, width)
    token, out_back, out_in, fourth_y, fourth_x = wait(token, out_back, out_in, fourth_y, fourth_x)

    sends = [fourth_x[:2], fourth_y[2:], jnp.concatenate([fourth, fourth_y, fourth_x])]
    token, sends = wait(token, sends)
    last_a, last_b, pair = (exchange(s, m) for s, m in zip(sends, (ROW, NEAR_X, CORE)))
    token, pair = wait(token, pair)
    made = sort(token, [(0, sends[2]), (16, pair)], [], width)
    token, made, last_a, last_b = wait(token, made, last_a, last_b)

    ends = exchange(jnp.concatenate([last_a, last_b]), CORE)
    made = sort(token, [(12, last_a), (14, last_b)], made, width)
    token, made, ends = wait(token, made, ends)
    out_out, out_query, out_key, out_value = sort(token, [(28, ends)], made, width)
    return (pooled, input_grad, out_query, out_key, out_value, out_out, out_in, out_back, *outs)

def solution(mesh):
    data = P("dp", "blk", None)
    placed = (data,) + (P(),) * 11 + (P("dp"), P("dp"), P("dp", None))
    return jax.shard_map(local, mesh=mesh, in_specs=placed, out_specs=(P("dp", None), data) + (P(),) * 10, check_vma=False)
```

```python
import functools
import jax, jax.numpy as jnp
from jax import lax
from jax.experimental import pallas as pl
from jax.experimental.pallas import tpu as pltpu
from jax.sharding import PartitionSpec as P

F32, BF16 = jnp.float32, jnp.bfloat16
NEG = -1000000000.0
NT = (((1,), (1,)), ((), ()))
TN = (((0,), (0,)), ((), ()))
NN = (((1,), (0,)), ((), ()))

def dot(a, b, dims=NN):
    return lax.dot_general(a, b, dims, preferred_element_type=F32)

def skew(row, width, dtype=F32):
    return pltpu.roll(jnp.broadcast_to(row, (128, width)), width - 127, 1, stride=1, stride_axis=0)


BUCKETS = 32
EPS = 1e-06
CORE, ROW, NEAR_X = 1, 2, 4

def rms_scale(values):
    return lax.rsqrt(jnp.mean(values * values, axis=-1, keepdims=True) + EPS)

def norm_back(grad_out, values, scale, gain):
    weighted = grad_out * gain
    inner = jnp.mean(weighted * values, axis=-1, keepdims=True)
    grad_in = scale * weighted - scale * scale * scale * values * inner
    return grad_in, jnp.sum(grad_out * values * scale, axis=0, keepdims=True)

def two_terms(value):
    high = value.astype(BF16)
    return jnp.concatenate([high, (value - high.astype(F32)).astype(BF16)])

def one_value(terms):
    return terms[:8].astype(F32) + terms[8:16].astype(F32)

def rows_of(*values):
    count = sum(v.shape[0] for v in values)
    return jnp.concatenate(list(values) + [jnp.zeros((8 - count, values[0].shape[1]), F32)])

def prepare_kernel(mine, other, gain, wq_h, wk_h, wv_h, hidden, query, keys, values, wq, wk, wv, sems):
    rows = mine.shape[0]
    load = [pltpu.make_async_copy(a, b, sems.at[i]) for i, (a, b) in enumerate(((wk_h, wk), (wv_h, wv), (wq_h, wq)))]
    for copy in load:
        copy.start()
    for part, raw in enumerate((mine, other)):
        tokens = raw[...].astype(F32)
        hidden[part * rows : (part + 1) * rows, :] = (tokens * rms_scale(tokens) * gain[...]).astype(BF16)
    h = hidden[...]
    load[0].wait()
    keys[...] = dot(h, wk[...]).astype(BF16)
    load[1].wait()
    values[...] = dot(h, wv[...]).astype(BF16)
    load[2].wait()
    query[...] = dot(h[:rows], wq[...]).astype(BF16)

def prepare(mine, other, gain, wq, wk, wv):
    rows, width = mine.shape
    shape = lambda n: jax.ShapeDtypeStruct((n, width), BF16)
    vmem, free = (pl.BlockSpec(memory_space=m) for m in (pltpu.VMEM, pl.ANY))
    return pl.pallas_call(
        prepare_kernel,
        in_specs=[vmem] * 3 + [free] * 3,
        out_specs=[vmem] * 7,
        out_shape=[shape(2 * rows), shape(rows), shape(2 * rows), shape(2 * rows)] + [shape(width)] * 3,
        scratch_shapes=[pltpu.SemaphoreType.DMA((3,))],
        name="prepare", compiler_params=pltpu.CompilerParams(vmem_limit_bytes=14 << 20),
    )(mine, other, gain, wq, wk, wv)

def tables_kernel(ids, pads, prefixes, bias, buckets, lines, info, *, length):
    doc = ids[6]
    info[0] = length - jnp.where(doc == 0, pads[0], pads[1])
    info[5] = jnp.where(doc == 0, prefixes[0], prefixes[1])
    for to, at in enumerate((0, 1, 2, 3)):
        info[1 + to] = ids[at]
    for to, at in enumerate((4, 5, 6)):
        info[6 + to] = ids[at]
    picker = jnp.where(lax.broadcasted_iota(jnp.int32, (BUCKETS, 1), 0) == buckets[...], 1.0, 0.0).astype(BF16)
    left, total = bias[...], None
    for _ in range(3):
        part = left.astype(BF16)
        left = left - part.astype(F32)
        made = dot(part, picker)
        total = made if total is None else total + made
    lines[...] = jnp.zeros_like(lines)
    lines[:, : buckets.shape[1]] = total

def tables(ids, pads, prefixes, bias, buckets, length):
    smem, vmem = pl.BlockSpec(memory_space=pltpu.SMEM), pl.BlockSpec(memory_space=pltpu.VMEM)
    return pl.pallas_call(
        functools.partial(tables_kernel, length=length),
        in_specs=[smem] * 3 + [vmem] * 2,
        out_specs=[vmem, smem],
        out_shape=[jax.ShapeDtypeStruct((bias.shape[0], buckets.shape[1] + 1), F32), jax.ShapeDtypeStruct((16,), jnp.int32)],
        name="tables", compiler_params=pltpu.CompilerParams(vmem_limit_bytes=4 << 20),
    )(ids, pads, prefixes, bias, buckets)

def back_pieces(to, active, low, mine):
    @pl.loop(0, active.shape[1] // 512)
    def _(group):
        made = dot(active[:, pl.ds(pl.multiple_of(group * 512, 512), 512)], low, TN).astype(BF16)
        for b in range(4):
            rows = made[b * 128 : (b + 1) * 128]
            to[(4 * group + b) ^ mine] = jnp.concatenate([rows[:, q * 128 : (q + 1) * 128] for q in range(4)])

def in_pieces(to, slopes, turned, mine):
    @pl.loop(0, slopes.shape[1] // 512)
    def _(group):
        made = dot(turned, slopes[:, pl.ds(pl.multiple_of(group * 512, 512), 512)]).astype(BF16)
        for b in range(4):
            to[(4 * group + b) ^ mine] = made[:, b * 128 : (b + 1) * 128]

def front_kernel(info, far, far_other, near, q_l, k_l, v_l, lines, wq, wk, wv, gain1, gain2, gain3, cots, wo_h, win_h, wback_h,
                 hid, qs, ks, vs, expo_o, inv, att, send, active, slopes, turned, mixed, steep, rows,
                 wo, win, wback, expo, scores, skewed, edges, sems):
    count, width = near.shape
    hidden = win.shape[1]
    late = [pltpu.make_async_copy(a, b, sems.at[i]) for i, (a, b) in enumerate(((wo_h, wo), (win_h, win), (wback_h, wback)))]
    kept = lambda g: pltpu.make_async_copy(expo, expo_o.at[pl.ds(2 * g, 2)], sems.at[3])

    for copy in late:
        copy.start()
    for part, raw in enumerate((far, far_other)):
        tokens = raw[...].astype(F32)
        hid[part * count : (part + 1) * count, :] = (tokens * rms_scale(tokens) * gain1[...]).astype(BF16)
    h = hid[...]
    qs[...] = dot(h[:count], wq[...]).astype(BF16)
    ks[...] = dot(h, wk[...]).astype(BF16)
    vs[...] = dot(h, wv[...]).astype(BF16)
    column = lax.broadcasted_iota(jnp.int32, (1, 128), 1)
    for b in range(4):
        place = info[1 + b] + lax.broadcasted_iota(jnp.int32, (count, 1), 0)
        gate = jnp.where(place < info[0], 0.0, NEG)
        for head in range(2):
            edges[head, b * count : (b + 1) * count, :] = jnp.where(column == (64 if head == 0 else 0), gate, 0.0).astype(BF16)
    limit = info[0]

    @pl.loop(0, width // 128)
    def _(step):
        @pl.when(step > 0)
        def _():
            kept(step - 1).wait()

        cols = pl.ds(pl.multiple_of(step * 128, 128), 128)
        lane = lax.broadcasted_iota(jnp.int32, (1, 128), 1)
        first = lane < 64
        starts = [info[1 + b] for b in range(4)]
        keys = [k_l[:count, cols], k_l[count:, cols], ks[:count, cols], ks[count:, cols]]
        values = jnp.concatenate([v_l[:, cols], vs[:, cols]])
        query = jnp.concatenate([q_l[:, cols], qs[:, cols]])
        made = []
        for head in range(2):
            mine = jnp.where(first if head == 0 else lane >= 64, 1.0, 0.0).astype(BF16)
            one = jnp.where(lane == (64 if head == 0 else 0), 1.0, 0.0).astype(BF16)
            q = query * mine + one
            v = values * mine + one
            skewed[head] = skew(lines[pl.ds(2 * step + head, 1), :], lines.shape[1])
            k = jnp.concatenate(keys) * mine + edges[head]
            for half in range(2):
                s = dot(q[half * 256 : (half + 1) * 256], k, NT)
                for r in range(2):
                    for b in range(4):
                        at = starts[b] - starts[2 * half] + 896 - 128 * r
                        part = s[r * 128 : (r + 1) * 128, b * 256 : (b + 1) * 256] + skewed[head, :, pl.ds(pl.multiple_of(at, 128), 256)]
                        scores[head, half * 256 + r * 128 : half * 256 + (r + 1) * 128, b * 256 : (b + 1) * 256] = part
            accs = []
            for r in range(4):
                rs = slice(r * 128, (r + 1) * 128)
                value = scores[head, rs, :]
                top = jnp.max(value, axis=1, keepdims=True)
                e = jnp.exp(value - top).astype(BF16)
                expo[head, rs, :] = e
                accs.append(dot(e, v))
            acc = jnp.concatenate(accs)
            made.append((acc, 1.0 / (acc[:, 64:65] if head == 0 else acc[:, 0:1])))
        (a0, i0), (a1, i1) = made
        scale = jnp.where(first, i0, i1)
        att[:, cols] = (jnp.where(first, a0, a1) * scale).astype(BF16)
        inv[:, cols] = scale
        kept(step).start()

    for copy in late:
        copy.wait()
    for part, raw in enumerate((near, far)):
        spot = slice(part * count, (part + 1) * count)
        mixed[spot, :] = raw[...].astype(F32) + dot(att[spot, :], wo[...])
    values = mixed[...]
    inner = (values * rms_scale(values) * gain2[...]).astype(BF16)
    turned[...] = inner.T
    total = values
    for at in range(0, hidden, 512):
        lifted = jnp.maximum(dot(inner, win[:, at : at + 512]), 0.0).astype(BF16)
        active[:, at : at + 512] = lifted
        total = total + dot(lifted, wback[at : at + 512, :])
    scale = rms_scale(total)
    place = lax.broadcasted_iota(jnp.int32, (2 * count, 1), 0)
    place = jnp.where(place < count, place + info[1], place + (info[3] - count))
    live = jnp.where((place >= info[5]) & (place < limit), 1.0, 0.0)
    pool = jnp.sum(total * scale * gain3[...] * live, axis=0, keepdims=True)
    cot = jnp.where(info[8] == 0, cots[0:1, :], cots[1:2, :]) / (limit - info[5]).astype(F32)
    slope, grad_end = norm_back(live * cot, total, scale, gain3[...])
    steep[...] = slope
    rows[...] = jnp.concatenate([pool, grad_end, jnp.zeros((6, width), F32)])
    low = slope.astype(BF16)
    for at in range(0, hidden, 512):
        through = dot(low, wback[at : at + 512, :], NT).astype(BF16)
        slopes[:, at : at + 512] = jnp.where(active[:, at : at + 512] > 0, through, jnp.zeros_like(through))
    mine = info[6] & 15

    @pl.when(info[7] == 0)
    def _():
        in_pieces(send, slopes, turned[...], mine)

    @pl.when(info[7] == 1)
    def _():
        back_pieces(send, active, steep[...].astype(BF16), mine)

    kept(3).wait()


def front(info, far, far_other, near, q_l, k_l, v_l, lines, wq, wk, wv, gain1, gain2, gain3, cots, wo, win, wback):
    count, width = near.shape
    hidden = win.shape[1]
    heads, span = lines.shape
    shape = jax.ShapeDtypeStruct
    smem, vmem, free = (pl.BlockSpec(memory_space=m) for m in (pltpu.SMEM, pltpu.VMEM, pl.ANY))
    outs = [shape((2 * count, width), BF16), shape((count, width), BF16), shape((2 * count, width), BF16), shape((2 * count, width), BF16),
            shape((heads, 2 * count, 4 * count), BF16), shape((2 * count, width), F32), shape((2 * count, width), BF16),
            shape((16, width, 128), BF16), shape((2 * count, hidden), BF16), shape((2 * count, hidden), BF16),
            shape((width, 2 * count), BF16), shape((2 * count, width), F32), shape((2 * count, width), F32)]
    return pl.pallas_call(
        front_kernel,
        in_specs=[smem] + [vmem] * 14 + [free] * 3,
        out_specs=[vmem] * 4 + [free] + [vmem] * 9,
        out_shape=outs + [shape((8, width), F32)],
        scratch_shapes=[pltpu.VMEM(wo.shape, BF16), pltpu.VMEM(win.shape, BF16), pltpu.VMEM(wback.shape, BF16),
                        pltpu.VMEM((2, 2 * count, 4 * count), BF16), pltpu.VMEM((2, 2 * count, 4 * count), F32),
                        pltpu.VMEM((2, 128, span), F32), pltpu.VMEM((2, 4 * count, 128), BF16), pltpu.SemaphoreType.DMA((4,))],
        name="front", compiler_params=pltpu.CompilerParams(vmem_limit_bytes=38 << 20),
    )(info, far, far_other, near, q_l, k_l, v_l, lines, wq, wk, wv, gain1, gain2, gain3, cots, wo, win, wback)

def inner_kernel(info, slopes, win, grad_inner):
    total = None
    for at in range(0, slopes.shape[1], 512):
        part = dot(slopes[:, at : at + 512], win[:, at : at + 512], NT)
        total = part if total is None else total + part
    grad_inner[...] = total

def inner(info, slopes, win):
    smem, vmem = pl.BlockSpec(memory_space=pltpu.SMEM), pl.BlockSpec(memory_space=pltpu.VMEM)
    return pl.pallas_call(
        inner_kernel, in_specs=[smem, vmem, vmem], out_specs=vmem,
        out_shape=jax.ShapeDtypeStruct((slopes.shape[0], win.shape[0]), F32), name="inner", compiler_params=pltpu.CompilerParams(vmem_limit_bytes=10 << 20),
    )(info, slopes, win)

def through_kernel(info, grad_inner, mixed, steep, wo, att, gain2, grad_mixed, grad_attended, grad_out, rows):
    values = mixed[...]
    more, grad_two = norm_back(grad_inner[...], values, rms_scale(values), gain2[...])
    total = steep[...] + more
    grad_mixed[...] = total
    low = total.astype(BF16)
    grad_attended[...] = dot(low, wo[...], NT).astype(BF16)
    grad_out[...] = dot(att[...], low, TN).astype(BF16)
    rows[...] = jnp.concatenate([grad_two, jnp.zeros((7, low.shape[1]), F32)])

def through(info, grad_inner, mixed, steep, wo, att, gain2):
    n, width = mixed.shape
    smem, vmem = pl.BlockSpec(memory_space=pltpu.SMEM), pl.BlockSpec(memory_space=pltpu.VMEM)
    shape = jax.ShapeDtypeStruct
    return pl.pallas_call(
        through_kernel,
        in_specs=[smem] + [vmem] * 6,
        out_specs=[vmem] * 4,
        out_shape=[shape((n, width), F32), shape((n, width), BF16), shape((width, width), BF16), shape((8, width), F32)],
        name="through", compiler_params=pltpu.CompilerParams(vmem_limit_bytes=16 << 20),
    )(info, grad_inner, mixed, steep, wo, att, gain2)

def stay_kernel(info, active, slopes, turned, steep, blocks):
    high, lowest = (info[6] & 15) >> 2, info[6] & 3
    for side in range(2):
        @pl.when(info[7] == side)
        def _(side=side):
            low = steep[...].astype(BF16) if side == 0 else turned[...]
            for k in range(4):
                at = pl.ds(pl.multiple_of((k ^ high) * 512, 512), 512)
                made = dot(active[:, at], low, TN) if side == 0 else dot(low, slopes[:, at])
                for b in range(4):
                    piece = made[:, b * 128 : (b + 1) * 128]
                    if side == 0:
                        piece = made[b * 128 : (b + 1) * 128]
                        piece = jnp.concatenate([piece[:, q * 128 : (q + 1) * 128] for q in range(4)])
                    blocks[k, b ^ lowest] = piece.astype(BF16)

def stay_half(info, active, slopes, turned, steep):
    smem, vmem = pl.BlockSpec(memory_space=pltpu.SMEM), pl.BlockSpec(memory_space=pltpu.VMEM)
    width = steep.shape[1]
    return pl.pallas_call(
        stay_kernel, in_specs=[smem] + [vmem] * 4, out_specs=vmem,
        out_shape=jax.ShapeDtypeStruct((4, 4, width, 128), BF16), name="stay", compiler_params=pltpu.CompilerParams(vmem_limit_bytes=12 << 20),
    )(info, active, slopes, turned, steep)

def meet_kernel(kept, got, *outs):
    for k in (3, 1, 2, 0):
        outs[k][...] = added(kept[k], got[4 * k : 4 * k + 4])

def meet(kept, got):
    vmem = pl.BlockSpec(memory_space=pltpu.VMEM)
    return pl.pallas_call(
        meet_kernel, in_specs=[vmem] * 2, out_specs=[vmem] * 4, out_shape=[jax.ShapeDtypeStruct(kept.shape[1:], BF16)] * 4, name="meet", compiler_params=pltpu.CompilerParams(vmem_limit_bytes=20 << 20),
    )(kept, got)

CLASS = {(0, 0): 0, (1, 2): 0, (0, 1): 1, (1, 3): 1, (0, 2): 2, (0, 3): 3, (1, 0): 4, (1, 1): 5}

def back_kernel(info, ql, qr, kl, kr, vl, vr, gout, out, inv, expo, buckets, dense_rows, through_rows,
                hid_l_h, hid_r_h, near_h, near_other_h, far_h, far_other_h, wq_h, wk_h, wv_h, grad_out_h,
                keep_o, send_o, stay_o, leave_o, small,
                hid_l, hid_r, near, near_other, far, far_other, wq, wk, wv, made,
                keep, send, stay, leave, dq, dk, dv, offsets, sums, acc, slopes, sems):
    count, width = near.shape
    step = pl.program_id(0)
    pairs = width // 128
    late = [pltpu.make_async_copy(a, b, sems.at[i]) for i, (a, b) in enumerate((
        (hid_l_h, hid_l), (hid_r_h, hid_r), (near_h, near), (near_other_h, near_other), (far_h, far), (far_other_h, far_other),
        (wq_h, wq), (wk_h, wk), (wv_h, wv), (grad_out_h, made.at[0:width])))]
    done = [pltpu.make_async_copy(a, b, sems.at[10 + i]) for i, (a, b) in enumerate(((send, send_o), (keep, keep_o), (leave, leave_o), (stay, stay_o)))]

    @pl.when(step == 0)
    def _():
        for copy in late:
            copy.start()

    cols = pl.ds(pl.multiple_of(step * 128, 128), 128)
    lane = lax.broadcasted_iota(jnp.int32, (1, 128), 1)
    starts = [info[1 + b] for b in range(4)]
    keys = jnp.concatenate([kl[...], kr[...]])
    values = jnp.concatenate([vl[...], vr[...]])
    query = jnp.concatenate([ql[...], qr[...]])
    scaled = gout[...].astype(F32) * inv[...]
    prod = scaled * out[...].astype(F32)
    low = scaled.astype(BF16)
    query_t, low_t = query.T, low.T
    grads_q, grads_k, grads_v = None, [], []
    for head in range(2):
        mine = (lane < 64) if head == 0 else (lane >= 64)
        base = 64 if head == 0 else 0
        pick = jnp.where(mine, 1.0, 0.0).astype(BF16)
        delta = jnp.sum(jnp.where(mine, prod, 0.0), axis=1, keepdims=True)
        high = delta.astype(BF16).astype(F32)
        extra = jnp.where(lane == base, high, jnp.where(lane == base + 1, delta - high, 0.0)).astype(BF16)
        grad = low * pick + extra
        minus = jnp.where((lane == base) | (lane == base + 1), -1.0, 0.0).astype(BF16)
        for b in range(4):
            spot = slice(b * count, (b + 1) * count)
            ds = dot(grad, values[spot] * pick + minus, NT) * expo[head, :, spot].astype(F32)
            slopes[head, :, spot] = ds.astype(BF16)
            for chunk in range(2):
                upper, lower = (ds[chunk * count + r * 128 : chunk * count + (r + 1) * 128] for r in range(2))
                group = CLASS[chunk, b]
                block = jnp.concatenate([lower[:, :128], lower[:, 128:] + upper[:, :128], upper[:, 128:]], axis=1)
                if (chunk, b) in ((1, 2), (1, 3)):
                    block = block + sums[head, group]
                sums[head, group] = block
        part = dot(slopes[head], keys * pick)
        grads_q = part if grads_q is None else grads_q + part
        half = slice(head * 64, (head + 1) * 64)
        grads_k.append(dot(query_t[half], slopes[head]))
        grads_v.append(dot(low_t[half], expo[head]))
    dq[:, cols] = grads_q.astype(BF16)
    dk[:, cols] = jnp.concatenate(grads_k).astype(BF16).T
    dv[:, cols] = jnp.concatenate(grads_v).astype(BF16).T
    for head in range(2):
        acc[head] = jnp.zeros(acc.shape[1:], F32)
        for (chunk, b), group in CLASS.items():
            if (chunk, b) not in ((1, 2), (1, 3)):
                at = starts[b] - starts[2 * chunk] + 768
                to = pl.ds(pl.multiple_of(at, 128), 384)
                acc[head, :, to] += sums[head, group]
        rest = acc[head]
        n = 64
        while n >= 8:
            rest = rest[:n] + pltpu.roll(rest[n:], 2048 - n, 1)
            n //= 2
        line = rest[7:8]
        for r in range(6, -1, -1):
            line = rest[r : r + 1] + pltpu.roll(line, 2047, 1)
        offsets[pl.ds(2 * step + head, 1), :] = pltpu.roll(line, 127, 1)

    @pl.when(step == pairs - 1)
    def _():
        for copy in late:
            copy.wait()
        made[width : 2 * width, :] = (dot(hid_l[:count, :], dq[:count, :], TN) + dot(hid_r[:count, :], dq[count:, :], TN)).astype(BF16)
        for at, grads in ((2 * width, dk), (3 * width, dv)):
            made[at : at + width, :] = (dot(hid_l[...], grads[: 2 * count, :], TN) + dot(hid_r[...], grads[2 * count :, :], TN)).astype(BF16)
        me = info[6]
        size = made.shape[0] // 32

        @pl.loop(0, 16)
        def _(r):
            keep[r] = made[pl.ds(pl.multiple_of((r ^ me) * size, size), size), :]
            send[pl.ds(pl.multiple_of(r * size, size), size), :] = made[pl.ds(pl.multiple_of(((r + 16) ^ me) * size, size), size), :]

        gain = jnp.zeros((1, width), F32)
        for b, raw in enumerate((near, near_other, far, far_other)):
            spot = slice(b * count, (b + 1) * count)
            grad = dot(dk[spot, :], wk[...], NT) + dot(dv[spot, :], wv[...], NT)
            half = slice((b // 2) * count, (b // 2 + 1) * count)
            if b % 2 == 0:
                grad = grad + dot(dq[half, :], wq[...], NT)
                stay[half, :] = grad
            else:
                leave[half, :] = grad.astype(BF16)
            tokens = raw[...].astype(F32)
            gain = gain + jnp.sum(grad * (tokens * rms_scale(tokens)), axis=0, keepdims=True)
        leave[2 * count :, :] = two_terms(rows_of(dense_rows[0:1, :]))
        picker = jnp.where(lax.broadcasted_iota(jnp.int32, (128, 1), 0) == buckets[...], 1.0, 0.0).astype(BF16)
        left = offsets[...][:, : buckets.shape[1]]
        bias = None
        for _ in range(3):
            part = left.astype(BF16)
            left = left - part.astype(F32)
            bias = dot(part, picker, NT) if bias is None else bias + dot(part, picker, NT)
        bias = jnp.concatenate([bias, jnp.zeros((bias.shape[0], width - 128), F32)], axis=1)
        line = bias[0:1]
        for h in range(1, bias.shape[0]):
            line = line + pltpu.roll(bias[h : h + 1], 32 * h, 1)
        total = rows_of(gain, through_rows[0:1, :], dense_rows[1:2, :], line)
        small[...] = total
        send[16 * size :, :] = two_terms(total)
        for copy in done:
            copy.start()
        for copy in done:
            copy.wait()

def back(info, ql, qr, kl, kr, vl, vr, gout, out, inv, expo, buckets, dense_rows, through_rows,
         hid_l, hid_r, near, near_other, far, far_other, wq, wk, wv, grad_out):
    count, width = near.shape
    smem, free = pl.BlockSpec(memory_space=pltpu.SMEM), pl.BlockSpec(memory_space=pl.ANY)
    whole = lambda *dims: pl.BlockSpec(dims, lambda g: (0,) * len(dims))
    col = lambda n: pl.BlockSpec((n, 128), lambda g: (0, g))
    shape = jax.ShapeDtypeStruct
    size = 4 * width // 32
    outs = [shape((16, size, width), BF16), shape((16 * size + 16, width), BF16), shape((2 * count, width), F32), shape((2 * count + 16, width), BF16)]
    given = (hid_l, hid_r, near, near_other, far, far_other, wq, wk, wv)
    return pl.pallas_call(
        back_kernel,
        grid=(width // 128,),
        in_specs=[smem, col(count), col(count)] + [col(2 * count)] * 7 + [pl.BlockSpec((2, 2 * count, 4 * count), lambda g: (g, 0, 0)),
                  whole(*buckets.shape), whole(8, width), whole(8, width)] + [free] * 10,
        out_specs=[free] * 4 + [whole(8, width)],
        out_shape=outs + [shape((8, width), F32)],
        scratch_shapes=[pltpu.VMEM(g.shape, BF16) for g in given] + [pltpu.VMEM((4 * width, width), BF16)]
                       + [pltpu.VMEM(o.shape, o.dtype) for o in outs]
                       + [pltpu.VMEM((2 * count, width), BF16), pltpu.VMEM((4 * count, width), BF16), pltpu.VMEM((4 * count, width), BF16),
                          pltpu.VMEM((8, 2048), F32), pltpu.VMEM((2, 6, 128, 384), F32), pltpu.VMEM((2, 128, 2048), F32),
                          pltpu.VMEM((2, 2 * count, 4 * count), BF16), pltpu.SemaphoreType.DMA((14,))],
        name="back", compiler_params=pltpu.CompilerParams(vmem_limit_bytes=44 << 20),
    )(info, ql, qr, kl, kr, vl, vr, gout, out, inv, expo, buckets, dense_rows, through_rows, *given, grad_out)

def ending_kernel(info, stay, came, near, far, grad_mixed, gain, dense_rows, home, away):
    count, width = near.shape
    for part, raw in enumerate((near, far)):
        spot = slice(part * count, (part + 1) * count)
        tokens = raw[...].astype(F32)
        grad = stay[spot, :] + came[spot, :].astype(F32)
        more, _ = norm_back(grad, tokens, rms_scale(tokens), gain[...])
        value = (grad_mixed[spot, :] + more).astype(BF16)
        if part == 0:
            home[:count, :] = value
        else:
            away[:count, :] = value
    alive = (info[0] - info[5]).astype(F32)
    pool = two_terms((rows_of(dense_rows[0:1, :]) + one_value(came[2 * count :, :])) / alive)
    home[count:, :] = pool
    away[count:, :] = pool

def ending(info, stay, came, near, far, grad_mixed, gain, dense_rows):
    count, width = near.shape
    smem, vmem = pl.BlockSpec(memory_space=pltpu.SMEM), pl.BlockSpec(memory_space=pltpu.VMEM)
    shape = jax.ShapeDtypeStruct((count + 16, width), BF16)
    return pl.pallas_call(
        ending_kernel, in_specs=[smem] + [vmem] * 7, out_specs=[vmem] * 2, out_shape=[shape, shape], name="ending", compiler_params=pltpu.CompilerParams(vmem_limit_bytes=10 << 20)
    )(info, stay, came, near, far, grad_mixed, gain, dense_rows)

def place_kernel(firsts, info, *refs):
    parts, (back, front, rows, columns, sems) = refs[: len(firsts)], refs[-5:]
    mine = info[6] & 15
    for side in range(2):
        @pl.when(info[7] == side)
        def _(side=side):
            copies, n = [], 0
            for part, first in zip(parts, firsts):
                for i in range(part.shape[0]):
                    r = first + i
                    to = pl.ds(pl.multiple_of(((r & 15) ^ mine) * 128, 128), 128)
                    if (r >= 16) == (side == 1):
                        for q in range(4):
                            rows[n, :, q * 128 : (q + 1) * 128] = part[i, q * 128 : (q + 1) * 128, :].astype(F32)
                        copies.append(pltpu.make_async_copy(rows.at[n], back.at[to, :], sems.at[n]))
                    else:
                        columns[n] = part[i].astype(F32)
                        copies.append(pltpu.make_async_copy(columns.at[n], front.at[:, to], sems.at[n]))
                    copies[-1].start()
                    n += 1
            for copy in copies:
                copy.wait()

def place(info, parts, made, width):
    smem, vmem, far = (pl.BlockSpec(memory_space=m) for m in (pltpu.SMEM, pltpu.VMEM, pltpu.HBM))
    shape = jax.ShapeDtypeStruct
    count = sum(p.shape[0] for _, p in parts)
    return pl.pallas_call(
        functools.partial(place_kernel, [first for first, _ in parts]),
        in_specs=[smem] + [vmem] * len(parts) + [far] * len(made),
        out_specs=[far] * 2,
        out_shape=[shape((16 * 128, width), F32), shape((width, 16 * 128), F32)],
        scratch_shapes=[pltpu.VMEM((count, 128, width), F32), pltpu.VMEM((count, width, 128), F32), pltpu.SemaphoreType.DMA((count,))],
        input_output_aliases={1 + len(parts) + i: i for i in range(len(made))},
        name="place", compiler_params=pltpu.CompilerParams(vmem_limit_bytes=28 << 20),
    )(info, *[p for _, p in parts], *made)

def sort_kernel(firsts, info, *refs):
    parts, made, (tall, sems) = refs[: len(firsts)], refs[-6:-2], refs[-2:]
    size = parts[0].shape[1]
    mine = info[6]
    pieces = []
    for part, first in zip(parts, firsts):
        for i in range(part.shape[0]):
            tall[len(pieces)] = part[i].astype(F32)
            pieces.append(first + i)
    for top in range(4):
        @pl.when((mine >> 3) == top)
        def _(top=top):
            copies = []
            for n, r in enumerate(pieces):
                to = pl.ds(pl.multiple_of(((r ^ mine) & 7) * size, size), size)
                copies.append(pltpu.make_async_copy(tall.at[n], made[top ^ (r >> 3)].at[to, :], sems.at[n]))
                copies[-1].start()
            for copy in copies:
                copy.wait()

def sort(info, parts, made, width):
    smem, vmem, far = (pl.BlockSpec(memory_space=m) for m in (pltpu.SMEM, pltpu.VMEM, pltpu.HBM))
    shape = jax.ShapeDtypeStruct((width, width), F32)
    count = sum(p.shape[0] for _, p in parts)
    return pl.pallas_call(
        functools.partial(sort_kernel, [first for first, _ in parts]),
        in_specs=[smem] + [vmem] * len(parts) + [far] * len(made),
        out_specs=[far] * 4,
        out_shape=[shape] * 4,
        scratch_shapes=[pltpu.VMEM((count,) + parts[0][1].shape[1:], F32), pltpu.SemaphoreType.DMA((count,))],
        input_output_aliases={1 + len(parts) + i: i for i in range(len(made))},
        name="sort", compiler_params=pltpu.CompilerParams(vmem_limit_bytes=12 << 20),
    )(info, *[p for _, p in parts], *made)

def mix_kernel(*refs):
    for k in range(4):
        refs[4 + k][...] = added(*[term[k] for term in refs[:4]])

def mix(terms):
    block = terms[0].shape[1:]
    vmem = pl.BlockSpec(memory_space=pltpu.VMEM)
    return pl.pallas_call(
        mix_kernel, in_specs=[vmem] * 4, out_specs=[vmem] * 4, out_shape=[jax.ShapeDtypeStruct(block, BF16)] * 4, name="mix", compiler_params=pltpu.CompilerParams(vmem_limit_bytes=10 << 20),
    )(*terms)

def exchange(value, bits):
    size = lax.axis_size("dp") * lax.axis_size("blk")
    return lax.ppermute(value, ("dp", "blk"), [(i, i ^ bits) for i in range(size)])

def wait(*values):
    return lax.optimization_barrier(values)

def added(*terms):
    total = terms[0].astype(F32)
    for term in terms[1:]:
        total = total + term.astype(F32)
    return total.astype(BF16)

def local(inputs, w_query, w_key, w_value, w_out, w_in, w_back, norm1_gain, norm2_gain, final_gain, bias_table, bucket_table, prefix_len, pad_len, pooled_grad):
    rows, width = inputs.shape[1:]
    spot, far_off = lax.axis_index("blk"), lax.axis_index("dp")
    doc, core = spot // 2, spot % 2
    block = [doc * 2 + core, doc * 2 + 1 - core, (1 - doc) * 2 + core, (1 - doc) * 2 + 1 - core]
    line = [8, 16]
    further = [32 << b for b in range((lax.axis_size("dp") // 8).bit_length() - 1)]
    piece = core * 16 + doc * 4 + (far_off % 2) * 8 + (far_off // 2) % 4
    near = jnp.where(doc == 0, inputs[0], inputs[1])
    far_send = jnp.where(doc == 0, inputs[1], inputs[0])
    near, far_send = wait(near, far_send)
    far = exchange(far_send, ROW)
    near_other = exchange(near, CORE)
    slot = jnp.arange(8, dtype=jnp.int32)
    ids = jnp.zeros_like(slot)
    for i, value in enumerate([b * rows for b in block] + [piece, core, doc]):
        ids = jnp.where(slot == i, value, ids)
    gain1, gain2, gain3 = norm1_gain[None, :], norm2_gain[None, :], final_gain[None, :]
    buckets = bucket_table[None, :]
    hid_l, q_l, k_l, v_l, w_query, w_key, w_value = prepare(near, near_other, gain1, w_query, w_key, w_value)
    far, q_l, ids = wait(far, q_l, ids)
    far_other = exchange(far, CORE)
    lines, info = tables(ids, pad_len, prefix_len, bias_table.T, buckets, 4 * rows)
    (hid_r, q_r, k_r, v_r, expo, inverse, attended, send, active, slopes, turned, mixed, steep, dense_rows) = front(
        info, far, far_other, near, q_l, k_l, v_l, lines, w_query, w_key, w_value,
        gain1, gain2, gain3, pooled_grad, w_out, w_in, w_back)

    xy = [ROW, NEAR_X, ROW ^ NEAR_X]
    zz = [line[0], line[1], line[0] ^ line[1]]

    token, send = wait(info, send)
    got = exchange(send, CORE)
    kept = stay_half(token, active, slopes, turned, steep)
    token, kept = wait(token, kept)
    grad_inner = inner(token, slopes, w_in)
    token, grad_inner, got = wait(token, grad_inner, got)
    stays, *sends = meet(kept, got)

    token, sends, grad_inner = wait(token, sends, grad_inner)
    came = [exchange(sends[k], xy[k]) for k in (2, 0, 1)]
    grad_mixed, grad_attended, grad_out_w, through_rows = through(token, grad_inner, mixed, steep, w_out, attended, gain2)
    token, through_rows = wait(token, through_rows)
    rest_keep, rest_send, stay, leave, small = back(
        token, q_l, q_r, k_l, k_r, v_l, v_r, grad_attended, attended, inverse, expo, buckets, dense_rows, through_rows,
        hid_l, hid_r, near, near_other, far, far_other, w_query, w_key, w_value, grad_out_w)
    token, small, rest_send, leave, came = wait(token, small, rest_send, leave, came)

    rest_got = exchange(rest_send, CORE)
    hidden_got = exchange(leave, CORE)
    lines = mix([stays] + list(came))
    token, lines = wait(token, lines)
    took = [exchange(lines[k + 1], m) for k, m in enumerate(zz)]
    token, rest_got, hidden_got = wait(token, rest_got, hidden_got)

    count = rest_keep.shape[0] * rest_keep.shape[1]
    small = small + one_value(rest_got[count:])
    rest_got = rest_got[:count].reshape(rest_keep.shape)
    terms = two_terms(small)
    sends = [jnp.concatenate([added(rest_keep[4 * k : 4 * k + 4], rest_got[4 * k : 4 * k + 4]).reshape(-1, width), terms]) for k in (1, 2, 3)]
    token, sends = wait(token, sends)
    rest_came = [exchange(s, m) for s, m in zip(sends, xy)]
    home, away = ending(token, stay, hidden_got, near, far, grad_mixed, gain1, dense_rows)
    token, took, away = wait(token, took, away)

    whole = added(lines[0], *took)
    for bit in further:
        whole = added(whole, exchange(whole, bit))
    token, whole = wait(token, whole)
    back_line = [exchange(whole, m) for m in zz]
    away_got = exchange(away, ROW)
    token, rest_came = wait(token, rest_came)

    count = count // 4
    for part in rest_came:
        small = small + one_value(part[count:])
    rest_came = [part[:count].reshape((4,) + rest_keep.shape[1:]) for part in rest_came]
    piece = count // 4
    lines = added(rest_keep[:4], rest_got[:4], *rest_came).reshape(-1, width)
    send = jnp.concatenate([lines[piece : 2 * piece], lines[3 * piece :], two_terms(small)])
    token, send = wait(token, send)
    took = exchange(send, line[0])
    token, took = wait(token, took)
    small = small + one_value(took[2 * piece :])
    lines = added(jnp.concatenate([lines[:piece], lines[2 * piece : 3 * piece]]), took[: 2 * piece])
    send = jnp.concatenate([lines, two_terms(small)])
    token, send, back_line, away_got = wait(token, send, back_line, away_got)
    took = exchange(send, line[1])

    quarter = jnp.stack([whole] + back_line)
    token, quarter = wait(token, quarter)
    from_y, from_x = exchange(quarter, ROW), exchange(quarter, NEAR_X)
    pool_mine, pool_other = one_value(home[rows:])[:1], one_value(away_got[rows:])[:1]
    pooled = jnp.where(doc == 0, jnp.concatenate([pool_mine, pool_other]), jnp.concatenate([pool_other, pool_mine]))
    home, away_got = home[:rows], away_got[:rows]
    input_grad = jnp.where(doc == 0, jnp.stack([home, away_got]), jnp.stack([away_got, home]))
    token, took, pooled, input_grad = wait(token, took, pooled, input_grad)

    small = small + one_value(took[2 * piece :])
    rest = added(lines, jnp.concatenate([took[piece : 2 * piece], took[:piece]]))
    for bit in further:
        rest = added(rest, exchange(rest, bit))
        small = small + exchange(small, bit)
    token, rest = wait(token, rest)
    rest_back = exchange(rest, line[0])
    outs = [small[0], small[1], small[2], small[3, : bias_table.size].reshape(bias_table.shape[::-1]).T]
    token, from_y, from_x, outs = wait(token, from_y, from_x, outs)

    sends = [from_x[:2], from_y[2:]]
    far_a, far_b = exchange(sends[0], ROW), exchange(sends[1], NEAR_X)
    quarter, from_y, from_x, _ = wait(quarter, from_y, from_x, sends)
    here = jnp.concatenate([quarter, from_y, from_x])
    token, here = wait(token, here)
    other = exchange(here, CORE)
    grads = place(token, [(0, here)], [], width)
    token, grads, rest_back, far_a, far_b, other = wait(token, grads, rest_back, far_a, far_b, other)

    fourth = jnp.stack([rest[:piece], rest_back[:piece], rest[piece:], rest_back[piece:]])
    far_pair = jnp.concatenate([far_a, far_b])
    token, fourth, far_pair = wait(token, fourth, far_pair)
    fourths = [exchange(fourth, xy[k]) for k in (2, 0, 1)]
    other_far = exchange(far_pair, CORE)
    token, other_far = wait(token, other_far)
    other_fourth = exchange(fourth, CORE)
    out_back, out_in = place(token, [(12, far_pair), (16, other), (28, other_far)], grads, width)
    token, out_back, out_in, other_fourth, fourths = wait(token, out_back, out_in, other_fourth, fourths)

    three = jnp.concatenate([fourths[1], fourths[2], fourths[0]])
    token, three = wait(token, three)
    others = exchange(three, CORE)
    made = sort(token, [(0, fourth), (4, three), (16, other_fourth)], [], width)
    token, made, others = wait(token, made, others)
    out_out, out_query, out_key, out_value = sort(token, [(20, others)], made, width)
    return (pooled, input_grad, out_query, out_key, out_value, out_out, out_in, out_back, *outs)

def solution(mesh):
    data = P("dp", "blk", None)
    placed = (data,) + (P(),) * 11 + (P("dp"), P("dp"), P("dp", None))
    return jax.shard_map(local, mesh=mesh, in_specs=placed, out_specs=(P("dp", None), data) + (P(),) * 10, check_vma=False)
```

```python
import functools
import jax, jax.numpy as jnp
from jax import lax
from jax.experimental import pallas as pl
from jax.experimental.pallas import tpu as pltpu
from jax.sharding import PartitionSpec as P

F32, BF16 = jnp.float32, jnp.bfloat16
NEG = -1000000000.0
NT = (((1,), (1,)), ((), ()))
TN = (((0,), (0,)), ((), ()))
NN = (((1,), (0,)), ((), ()))

def dot(a, b, dims=NN):
    return lax.dot_general(a, b, dims, preferred_element_type=F32)

def skew(row, width, dtype=F32):
    return pltpu.roll(jnp.broadcast_to(row, (128, width)), width - 127, 1, stride=1, stride_axis=0)


BUCKETS = 32
EPS = 1e-06
CORE, ROW, NEAR_X = 1, 2, 4

def rms_scale(values):
    return lax.rsqrt(jnp.mean(values * values, axis=-1, keepdims=True) + EPS)

def norm_back(grad_out, values, scale, gain):
    weighted = grad_out * gain
    inner = jnp.mean(weighted * values, axis=-1, keepdims=True)
    grad_in = scale * weighted - scale * scale * scale * values * inner
    return grad_in, jnp.sum(grad_out * values * scale, axis=0, keepdims=True)

def two_terms(value):
    high = value.astype(BF16)
    return jnp.concatenate([high, (value - high.astype(F32)).astype(BF16)])

def one_value(terms):
    return terms[:8].astype(F32) + terms[8:16].astype(F32)

def rows_of(*values):
    count = sum(v.shape[0] for v in values)
    return jnp.concatenate(list(values) + [jnp.zeros((8 - count, values[0].shape[1]), F32)])

def prepare_kernel(mine, other, gain, wq_h, wk_h, wv_h, hidden, query, keys, values, wq, wk, wv, sems):
    rows = mine.shape[0]
    load = [pltpu.make_async_copy(a, b, sems.at[i]) for i, (a, b) in enumerate(((wk_h, wk), (wv_h, wv), (wq_h, wq)))]
    for copy in load:
        copy.start()
    for part, raw in enumerate((mine, other)):
        tokens = raw[...].astype(F32)
        hidden[part * rows : (part + 1) * rows, :] = (tokens * rms_scale(tokens) * gain[...]).astype(BF16)
    h = hidden[...]
    load[0].wait()
    keys[...] = dot(h, wk[...]).astype(BF16)
    load[1].wait()
    values[...] = dot(h, wv[...]).astype(BF16)
    load[2].wait()
    query[...] = dot(h[:rows], wq[...]).astype(BF16)

def prepare(mine, other, gain, wq, wk, wv):
    rows, width = mine.shape
    shape = lambda n: jax.ShapeDtypeStruct((n, width), BF16)
    vmem, free = (pl.BlockSpec(memory_space=m) for m in (pltpu.VMEM, pl.ANY))
    return pl.pallas_call(
        prepare_kernel,
        in_specs=[vmem] * 3 + [free] * 3,
        out_specs=[vmem] * 7,
        out_shape=[shape(2 * rows), shape(rows), shape(2 * rows), shape(2 * rows)] + [shape(width)] * 3,
        scratch_shapes=[pltpu.SemaphoreType.DMA((3,))],
        name="prepare", compiler_params=pltpu.CompilerParams(vmem_limit_bytes=14 << 20),
    )(mine, other, gain, wq, wk, wv)

def tables_kernel(ids, pads, prefixes, bias, buckets, lines, info, *, length):
    doc = ids[6]
    info[0] = length - jnp.where(doc == 0, pads[0], pads[1])
    info[5] = jnp.where(doc == 0, prefixes[0], prefixes[1])
    for to, at in enumerate((0, 1, 2, 3)):
        info[1 + to] = ids[at]
    for to, at in enumerate((4, 5, 6)):
        info[6 + to] = ids[at]
    picker = jnp.where(lax.broadcasted_iota(jnp.int32, (BUCKETS, 1), 0) == buckets[...], 1.0, 0.0).astype(BF16)
    left, total = bias[...], None
    for _ in range(3):
        part = left.astype(BF16)
        left = left - part.astype(F32)
        made = dot(part, picker)
        total = made if total is None else total + made
    lines[...] = jnp.zeros_like(lines)
    lines[:, : buckets.shape[1]] = total

def tables(ids, pads, prefixes, bias, buckets, length):
    smem, vmem = pl.BlockSpec(memory_space=pltpu.SMEM), pl.BlockSpec(memory_space=pltpu.VMEM)
    return pl.pallas_call(
        functools.partial(tables_kernel, length=length),
        in_specs=[smem] * 3 + [vmem] * 2,
        out_specs=[vmem, smem],
        out_shape=[jax.ShapeDtypeStruct((bias.shape[0], buckets.shape[1] + 1), F32), jax.ShapeDtypeStruct((16,), jnp.int32)],
        name="tables", compiler_params=pltpu.CompilerParams(vmem_limit_bytes=4 << 20),
    )(ids, pads, prefixes, bias, buckets)

def back_pieces(to, active, low, mine):
    @pl.loop(0, active.shape[1] // 512)
    def _(group):
        made = dot(active[:, pl.ds(pl.multiple_of(group * 512, 512), 512)], low, TN).astype(BF16)
        for b in range(4):
            rows = made[b * 128 : (b + 1) * 128]
            to[(4 * group + b) ^ mine] = jnp.concatenate([rows[:, q * 128 : (q + 1) * 128] for q in range(4)])

def in_pieces(to, slopes, turned, mine):
    @pl.loop(0, slopes.shape[1] // 512)
    def _(group):
        made = dot(turned, slopes[:, pl.ds(pl.multiple_of(group * 512, 512), 512)]).astype(BF16)
        for b in range(4):
            to[(4 * group + b) ^ mine] = made[:, b * 128 : (b + 1) * 128]

def front_kernel(info, far, far_other, near, q_l, k_l, v_l, lines, wq, wk, wv, gain1, gain2, gain3, cots, wo_h, win_h, wback_h,
                 hid, qs, ks, vs, expo_o, inv, att, send, active, slopes, turned, mixed, steep, rows,
                 wo, win, wback, expo, scores, skewed, edges, sems):
    count, width = near.shape
    hidden = win.shape[1]
    late = [pltpu.make_async_copy(a, b, sems.at[i]) for i, (a, b) in enumerate(((wo_h, wo), (win_h, win), (wback_h, wback)))]
    kept = lambda g: pltpu.make_async_copy(expo, expo_o.at[pl.ds(2 * g, 2)], sems.at[3])

    for copy in late:
        copy.start()
    for part, raw in enumerate((far, far_other)):
        tokens = raw[...].astype(F32)
        hid[part * count : (part + 1) * count, :] = (tokens * rms_scale(tokens) * gain1[...]).astype(BF16)
    h = hid[...]
    qs[...] = dot(h[:count], wq[...]).astype(BF16)
    ks[...] = dot(h, wk[...]).astype(BF16)
    vs[...] = dot(h, wv[...]).astype(BF16)
    column = lax.broadcasted_iota(jnp.int32, (1, 128), 1)
    for b in range(4):
        place = info[1 + b] + lax.broadcasted_iota(jnp.int32, (count, 1), 0)
        gate = jnp.where(place < info[0], 0.0, NEG)
        for head in range(2):
            edges[head, b * count : (b + 1) * count, :] = jnp.where(column == (64 if head == 0 else 0), gate, 0.0).astype(BF16)
    limit = info[0]

    @pl.loop(0, width // 128)
    def _(step):
        @pl.when(step > 0)
        def _():
            kept(step - 1).wait()

        cols = pl.ds(pl.multiple_of(step * 128, 128), 128)
        lane = lax.broadcasted_iota(jnp.int32, (1, 128), 1)
        first = lane < 64
        starts = [info[1 + b] for b in range(4)]
        keys = [k_l[:count, cols], k_l[count:, cols], ks[:count, cols], ks[count:, cols]]
        values = jnp.concatenate([v_l[:, cols], vs[:, cols]])
        query = jnp.concatenate([q_l[:, cols], qs[:, cols]])
        made = []
        for head in range(2):
            mine = jnp.where(first if head == 0 else lane >= 64, 1.0, 0.0).astype(BF16)
            one = jnp.where(lane == (64 if head == 0 else 0), 1.0, 0.0).astype(BF16)
            q = query * mine + one
            v = values * mine + one
            skewed[head] = skew(lines[pl.ds(2 * step + head, 1), :], lines.shape[1])
            k = jnp.concatenate(keys) * mine + edges[head]
            for half in range(2):
                s = dot(q[half * 256 : (half + 1) * 256], k, NT)
                for r in range(2):
                    for b in range(4):
                        at = starts[b] - starts[2 * half] + 896 - 128 * r
                        part = s[r * 128 : (r + 1) * 128, b * 256 : (b + 1) * 256] + skewed[head, :, pl.ds(pl.multiple_of(at, 128), 256)]
                        scores[head, half * 256 + r * 128 : half * 256 + (r + 1) * 128, b * 256 : (b + 1) * 256] = part
            accs = []
            for r in range(4):
                rs = slice(r * 128, (r + 1) * 128)
                value = scores[head, rs, :]
                top = jnp.max(value, axis=1, keepdims=True)
                e = jnp.exp(value - top).astype(BF16)
                expo[head, rs, :] = e
                accs.append(dot(e, v))
            acc = jnp.concatenate(accs)
            made.append((acc, 1.0 / (acc[:, 64:65] if head == 0 else acc[:, 0:1])))
        (a0, i0), (a1, i1) = made
        scale = jnp.where(first, i0, i1)
        att[:, cols] = (jnp.where(first, a0, a1) * scale).astype(BF16)
        inv[:, cols] = scale
        kept(step).start()

    for copy in late:
        copy.wait()
    for part, raw in enumerate((near, far)):
        spot = slice(part * count, (part + 1) * count)
        mixed[spot, :] = raw[...].astype(F32) + dot(att[spot, :], wo[...])
    values = mixed[...]
    inner = (values * rms_scale(values) * gain2[...]).astype(BF16)
    turned[...] = inner.T
    total = values
    for at in range(0, hidden, 512):
        lifted = jnp.maximum(dot(inner, win[:, at : at + 512]), 0.0).astype(BF16)
        active[:, at : at + 512] = lifted
        total = total + dot(lifted, wback[at : at + 512, :])
    scale = rms_scale(total)
    place = lax.broadcasted_iota(jnp.int32, (2 * count, 1), 0)
    place = jnp.where(place < count, place + info[1], place + (info[3] - count))
    live = jnp.where((place >= info[5]) & (place < limit), 1.0, 0.0)
    pool = jnp.sum(total * scale * gain3[...] * live, axis=0, keepdims=True)
    cot = jnp.where(info[8] == 0, cots[0:1, :], cots[1:2, :]) / (limit - info[5]).astype(F32)
    slope, grad_end = norm_back(live * cot, total, scale, gain3[...])
    steep[...] = slope
    rows[...] = jnp.concatenate([pool, grad_end, jnp.zeros((6, width), F32)])
    low = slope.astype(BF16)
    for at in range(0, hidden, 512):
        through = dot(low, wback[at : at + 512, :], NT).astype(BF16)
        slopes[:, at : at + 512] = jnp.where(active[:, at : at + 512] > 0, through, jnp.zeros_like(through))
    mine = info[6] & 15

    @pl.when(info[7] == 0)
    def _():
        in_pieces(send, slopes, turned[...], mine)

    @pl.when(info[7] == 1)
    def _():
        back_pieces(send, active, steep[...].astype(BF16), mine)

    kept(3).wait()


def front(info, far, far_other, near, q_l, k_l, v_l, lines, wq, wk, wv, gain1, gain2, gain3, cots, wo, win, wback):
    count, width = near.shape
    hidden = win.shape[1]
    heads, span = lines.shape
    shape = jax.ShapeDtypeStruct
    smem, vmem, free = (pl.BlockSpec(memory_space=m) for m in (pltpu.SMEM, pltpu.VMEM, pl.ANY))
    outs = [shape((2 * count, width), BF16), shape((count, width), BF16), shape((2 * count, width), BF16), shape((2 * count, width), BF16),
            shape((heads, 2 * count, 4 * count), BF16), shape((2 * count, width), F32), shape((2 * count, width), BF16),
            shape((16, width, 128), BF16), shape((2 * count, hidden), BF16), shape((2 * count, hidden), BF16),
            shape((width, 2 * count), BF16), shape((2 * count, width), F32), shape((2 * count, width), F32)]
    return pl.pallas_call(
        front_kernel,
        in_specs=[smem] + [vmem] * 14 + [free] * 3,
        out_specs=[vmem] * 4 + [free] + [vmem] * 9,
        out_shape=outs + [shape((8, width), F32)],
        scratch_shapes=[pltpu.VMEM(wo.shape, BF16), pltpu.VMEM(win.shape, BF16), pltpu.VMEM(wback.shape, BF16),
                        pltpu.VMEM((2, 2 * count, 4 * count), BF16), pltpu.VMEM((2, 2 * count, 4 * count), F32),
                        pltpu.VMEM((2, 128, span), F32), pltpu.VMEM((2, 4 * count, 128), BF16), pltpu.SemaphoreType.DMA((4,))],
        name="front", compiler_params=pltpu.CompilerParams(vmem_limit_bytes=38 << 20),
    )(info, far, far_other, near, q_l, k_l, v_l, lines, wq, wk, wv, gain1, gain2, gain3, cots, wo, win, wback)

def inner_kernel(info, slopes, win, grad_inner):
    total = None
    for at in range(0, slopes.shape[1], 512):
        part = dot(slopes[:, at : at + 512], win[:, at : at + 512], NT)
        total = part if total is None else total + part
    grad_inner[...] = total

def inner(info, slopes, win):
    smem, vmem = pl.BlockSpec(memory_space=pltpu.SMEM), pl.BlockSpec(memory_space=pltpu.VMEM)
    return pl.pallas_call(
        inner_kernel, in_specs=[smem, vmem, vmem], out_specs=vmem,
        out_shape=jax.ShapeDtypeStruct((slopes.shape[0], win.shape[0]), F32), name="inner", compiler_params=pltpu.CompilerParams(vmem_limit_bytes=10 << 20),
    )(info, slopes, win)

def through_kernel(info, grad_inner, mixed, steep, wo, att, gain2, grad_mixed, grad_attended, grad_out, rows):
    values = mixed[...]
    more, grad_two = norm_back(grad_inner[...], values, rms_scale(values), gain2[...])
    total = steep[...] + more
    grad_mixed[...] = total
    low = total.astype(BF16)
    grad_attended[...] = dot(low, wo[...], NT).astype(BF16)
    grad_out[...] = dot(att[...], low, TN).astype(BF16)
    rows[...] = jnp.concatenate([grad_two, jnp.zeros((7, low.shape[1]), F32)])

def through(info, grad_inner, mixed, steep, wo, att, gain2):
    n, width = mixed.shape
    smem, vmem = pl.BlockSpec(memory_space=pltpu.SMEM), pl.BlockSpec(memory_space=pltpu.VMEM)
    shape = jax.ShapeDtypeStruct
    return pl.pallas_call(
        through_kernel,
        in_specs=[smem] + [vmem] * 6,
        out_specs=[vmem] * 4,
        out_shape=[shape((n, width), F32), shape((n, width), BF16), shape((width, width), BF16), shape((8, width), F32)],
        name="through", compiler_params=pltpu.CompilerParams(vmem_limit_bytes=16 << 20),
    )(info, grad_inner, mixed, steep, wo, att, gain2)

def stay_kernel(info, active, slopes, turned, steep, blocks):
    high, lowest = (info[6] & 15) >> 2, info[6] & 3
    for side in range(2):
        @pl.when(info[7] == side)
        def _(side=side):
            low = steep[...].astype(BF16) if side == 0 else turned[...]
            for k in range(4):
                at = pl.ds(pl.multiple_of((k ^ high) * 512, 512), 512)
                made = dot(active[:, at], low, TN) if side == 0 else dot(low, slopes[:, at])
                for b in range(4):
                    piece = made[:, b * 128 : (b + 1) * 128]
                    if side == 0:
                        piece = made[b * 128 : (b + 1) * 128]
                        piece = jnp.concatenate([piece[:, q * 128 : (q + 1) * 128] for q in range(4)])
                    blocks[k, b ^ lowest] = piece.astype(BF16)

def stay_half(info, active, slopes, turned, steep):
    smem, vmem = pl.BlockSpec(memory_space=pltpu.SMEM), pl.BlockSpec(memory_space=pltpu.VMEM)
    width = steep.shape[1]
    return pl.pallas_call(
        stay_kernel, in_specs=[smem] + [vmem] * 4, out_specs=vmem,
        out_shape=jax.ShapeDtypeStruct((4, 4, width, 128), BF16), name="stay", compiler_params=pltpu.CompilerParams(vmem_limit_bytes=12 << 20),
    )(info, active, slopes, turned, steep)

def meet_kernel(kept, got, *outs):
    for k in (3, 1, 2, 0):
        outs[k][...] = added(kept[k], got[4 * k : 4 * k + 4])

def meet(kept, got):
    vmem = pl.BlockSpec(memory_space=pltpu.VMEM)
    return pl.pallas_call(
        meet_kernel, in_specs=[vmem] * 2, out_specs=[vmem] * 4, out_shape=[jax.ShapeDtypeStruct(kept.shape[1:], BF16)] * 4, name="meet", compiler_params=pltpu.CompilerParams(vmem_limit_bytes=20 << 20),
    )(kept, got)

CLASS = {(0, 0): 0, (1, 2): 0, (0, 1): 1, (1, 3): 1, (0, 2): 2, (0, 3): 3, (1, 0): 4, (1, 1): 5}

def back_kernel(info, ql, qr, kl, kr, vl, vr, gout, out, inv, expo, buckets, dense_rows, through_rows,
                hid_l_h, hid_r_h, near_h, near_other_h, far_h, far_other_h, wq_h, wk_h, wv_h, grad_out_h,
                keep_o, send_o, stay_o, leave_o, small,
                hid_l, hid_r, near, near_other, far, far_other, wq, wk, wv, made,
                keep, send, stay, leave, dq, dk, dv, offsets, sums, acc, slopes, sems):
    count, width = near.shape
    step = pl.program_id(0)
    pairs = width // 128
    late = [pltpu.make_async_copy(a, b, sems.at[i]) for i, (a, b) in enumerate((
        (hid_l_h, hid_l), (hid_r_h, hid_r), (near_h, near), (near_other_h, near_other), (far_h, far), (far_other_h, far_other),
        (wq_h, wq), (wk_h, wk), (wv_h, wv), (grad_out_h, made.at[0:width])))]
    done = [pltpu.make_async_copy(a, b, sems.at[10 + i]) for i, (a, b) in enumerate(((send, send_o), (keep, keep_o), (leave, leave_o), (stay, stay_o)))]

    @pl.when(step == 0)
    def _():
        for copy in late:
            copy.start()

    cols = pl.ds(pl.multiple_of(step * 128, 128), 128)
    lane = lax.broadcasted_iota(jnp.int32, (1, 128), 1)
    starts = [info[1 + b] for b in range(4)]
    keys = jnp.concatenate([kl[...], kr[...]])
    values = jnp.concatenate([vl[...], vr[...]])
    query = jnp.concatenate([ql[...], qr[...]])
    scaled = gout[...].astype(F32) * inv[...]
    prod = scaled * out[...].astype(F32)
    low = scaled.astype(BF16)
    query_t, low_t = query.T, low.T
    grads_q, grads_k, grads_v = None, [], []
    for head in range(2):
        mine = (lane < 64) if head == 0 else (lane >= 64)
        base = 64 if head == 0 else 0
        pick = jnp.where(mine, 1.0, 0.0).astype(BF16)
        delta = jnp.sum(jnp.where(mine, prod, 0.0), axis=1, keepdims=True)
        high = delta.astype(BF16).astype(F32)
        extra = jnp.where(lane == base, high, jnp.where(lane == base + 1, delta - high, 0.0)).astype(BF16)
        grad = low * pick + extra
        minus = jnp.where((lane == base) | (lane == base + 1), -1.0, 0.0).astype(BF16)
        for b in range(4):
            spot = slice(b * count, (b + 1) * count)
            ds = dot(grad, values[spot] * pick + minus, NT) * expo[head, :, spot].astype(F32)
            slopes[head, :, spot] = ds.astype(BF16)
            for chunk in range(2):
                upper, lower = (ds[chunk * count + r * 128 : chunk * count + (r + 1) * 128] for r in range(2))
                group = CLASS[chunk, b]
                block = jnp.concatenate([lower[:, :128], lower[:, 128:] + upper[:, :128], upper[:, 128:]], axis=1)
                if (chunk, b) in ((1, 2), (1, 3)):
                    block = block + sums[head, group]
                sums[head, group] = block
        part = dot(slopes[head], keys * pick)
        grads_q = part if grads_q is None else grads_q + part
        half = slice(head * 64, (head + 1) * 64)
        grads_k.append(dot(query_t[half], slopes[head]))
        grads_v.append(dot(low_t[half], expo[head]))
    dq[:, cols] = grads_q.astype(BF16)
    dk[:, cols] = jnp.concatenate(grads_k).astype(BF16).T
    dv[:, cols] = jnp.concatenate(grads_v).astype(BF16).T
    for head in range(2):
        acc[head] = jnp.zeros(acc.shape[1:], F32)
        for (chunk, b), group in CLASS.items():
            if (chunk, b) not in ((1, 2), (1, 3)):
                at = starts[b] - starts[2 * chunk] + 768
                to = pl.ds(pl.multiple_of(at, 128), 384)
                acc[head, :, to] += sums[head, group]
        rest = acc[head]
        n = 64
        while n >= 8:
            rest = rest[:n] + pltpu.roll(rest[n:], 2048 - n, 1)
            n //= 2
        line = rest[7:8]
        for r in range(6, -1, -1):
            line = rest[r : r + 1] + pltpu.roll(line, 2047, 1)
        offsets[pl.ds(2 * step + head, 1), :] = pltpu.roll(line, 127, 1)

    @pl.when(step == pairs - 1)
    def _():
        for copy in late:
            copy.wait()
        made[width : 2 * width, :] = (dot(hid_l[:count, :], dq[:count, :], TN) + dot(hid_r[:count, :], dq[count:, :], TN)).astype(BF16)
        for at, grads in ((2 * width, dk), (3 * width, dv)):
            made[at : at + width, :] = (dot(hid_l[...], grads[: 2 * count, :], TN) + dot(hid_r[...], grads[2 * count :, :], TN)).astype(BF16)
        me = info[6]
        size = made.shape[0] // 32

        @pl.loop(0, 16)
        def _(r):
            keep[r] = made[pl.ds(pl.multiple_of((r ^ me) * size, size), size), :]
            send[pl.ds(pl.multiple_of(r * size, size), size), :] = made[pl.ds(pl.multiple_of(((r + 16) ^ me) * size, size), size), :]

        gain = jnp.zeros((1, width), F32)
        for b, raw in enumerate((near, near_other, far, far_other)):
            spot = slice(b * count, (b + 1) * count)
            grad = dot(dk[spot, :], wk[...], NT) + dot(dv[spot, :], wv[...], NT)
            half = slice((b // 2) * count, (b // 2 + 1) * count)
            if b % 2 == 0:
                grad = grad + dot(dq[half, :], wq[...], NT)
                stay[half, :] = grad
            else:
                leave[half, :] = grad.astype(BF16)
            tokens = raw[...].astype(F32)
            gain = gain + jnp.sum(grad * (tokens * rms_scale(tokens)), axis=0, keepdims=True)
        leave[2 * count :, :] = two_terms(rows_of(dense_rows[0:1, :]))
        picker = jnp.where(lax.broadcasted_iota(jnp.int32, (128, 1), 0) == buckets[...], 1.0, 0.0).astype(BF16)
        left = offsets[...][:, : buckets.shape[1]]
        bias = None
        for _ in range(3):
            part = left.astype(BF16)
            left = left - part.astype(F32)
            bias = dot(part, picker, NT) if bias is None else bias + dot(part, picker, NT)
        bias = jnp.concatenate([bias, jnp.zeros((bias.shape[0], width - 128), F32)], axis=1)
        line = bias[0:1]
        for h in range(1, bias.shape[0]):
            line = line + pltpu.roll(bias[h : h + 1], 32 * h, 1)
        total = rows_of(gain, through_rows[0:1, :], dense_rows[1:2, :], line)
        small[...] = total
        send[16 * size :, :] = two_terms(total)
        for copy in done:
            copy.start()
        for copy in done:
            copy.wait()

def back(info, ql, qr, kl, kr, vl, vr, gout, out, inv, expo, buckets, dense_rows, through_rows,
         hid_l, hid_r, near, near_other, far, far_other, wq, wk, wv, grad_out):
    count, width = near.shape
    smem, free = pl.BlockSpec(memory_space=pltpu.SMEM), pl.BlockSpec(memory_space=pl.ANY)
    whole = lambda *dims: pl.BlockSpec(dims, lambda g: (0,) * len(dims))
    col = lambda n: pl.BlockSpec((n, 128), lambda g: (0, g))
    shape = jax.ShapeDtypeStruct
    size = 4 * width // 32
    outs = [shape((16, size, width), BF16), shape((16 * size + 16, width), BF16), shape((2 * count, width), F32), shape((2 * count + 16, width), BF16)]
    given = (hid_l, hid_r, near, near_other, far, far_other, wq, wk, wv)
    return pl.pallas_call(
        back_kernel,
        grid=(width // 128,),
        in_specs=[smem, col(count), col(count)] + [col(2 * count)] * 7 + [pl.BlockSpec((2, 2 * count, 4 * count), lambda g: (g, 0, 0)),
                  whole(*buckets.shape), whole(8, width), whole(8, width)] + [free] * 10,
        out_specs=[free] * 4 + [whole(8, width)],
        out_shape=outs + [shape((8, width), F32)],
        scratch_shapes=[pltpu.VMEM(g.shape, BF16) for g in given] + [pltpu.VMEM((4 * width, width), BF16)]
                       + [pltpu.VMEM(o.shape, o.dtype) for o in outs]
                       + [pltpu.VMEM((2 * count, width), BF16), pltpu.VMEM((4 * count, width), BF16), pltpu.VMEM((4 * count, width), BF16),
                          pltpu.VMEM((8, 2048), F32), pltpu.VMEM((2, 6, 128, 384), F32), pltpu.VMEM((2, 128, 2048), F32),
                          pltpu.VMEM((2, 2 * count, 4 * count), BF16), pltpu.SemaphoreType.DMA((14,))],
        name="back", compiler_params=pltpu.CompilerParams(vmem_limit_bytes=40 << 20),
    )(info, ql, qr, kl, kr, vl, vr, gout, out, inv, expo, buckets, dense_rows, through_rows, *given, grad_out)

def ending_kernel(info, stay, came, near, far, grad_mixed, gain, dense_rows, home, away):
    count, width = near.shape
    for part, raw in enumerate((near, far)):
        spot = slice(part * count, (part + 1) * count)
        tokens = raw[...].astype(F32)
        grad = stay[spot, :] + came[spot, :].astype(F32)
        more, _ = norm_back(grad, tokens, rms_scale(tokens), gain[...])
        value = (grad_mixed[spot, :] + more).astype(BF16)
        if part == 0:
            home[:count, :] = value
        else:
            away[:count, :] = value
    alive = (info[0] - info[5]).astype(F32)
    pool = two_terms((rows_of(dense_rows[0:1, :]) + one_value(came[2 * count :, :])) / alive)
    home[count:, :] = pool
    away[count:, :] = pool

def ending(info, stay, came, near, far, grad_mixed, gain, dense_rows):
    count, width = near.shape
    smem, vmem = pl.BlockSpec(memory_space=pltpu.SMEM), pl.BlockSpec(memory_space=pltpu.VMEM)
    shape = jax.ShapeDtypeStruct((count + 16, width), BF16)
    return pl.pallas_call(
        ending_kernel, in_specs=[smem] + [vmem] * 7, out_specs=[vmem] * 2, out_shape=[shape, shape], name="ending", compiler_params=pltpu.CompilerParams(vmem_limit_bytes=10 << 20)
    )(info, stay, came, near, far, grad_mixed, gain, dense_rows)

def place_kernel(firsts, info, *refs):
    parts, (back, front, rows, columns, sems) = refs[: len(firsts)], refs[-5:]
    mine = info[6] & 15
    for side in range(2):
        @pl.when(info[7] == side)
        def _(side=side):
            copies, n = [], 0
            for part, first in zip(parts, firsts):
                for i in range(part.shape[0]):
                    r = first + i
                    to = pl.ds(pl.multiple_of(((r & 15) ^ mine) * 128, 128), 128)
                    if (r >= 16) == (side == 1):
                        for q in range(4):
                            rows[n, :, q * 128 : (q + 1) * 128] = part[i, q * 128 : (q + 1) * 128, :].astype(F32)
                        copies.append(pltpu.make_async_copy(rows.at[n], back.at[to, :], sems.at[n]))
                    else:
                        columns[n] = part[i].astype(F32)
                        copies.append(pltpu.make_async_copy(columns.at[n], front.at[:, to], sems.at[n]))
                    copies[-1].start()
                    n += 1
            for copy in copies:
                copy.wait()

def place(info, parts, made, width):
    smem, vmem, far = (pl.BlockSpec(memory_space=m) for m in (pltpu.SMEM, pltpu.VMEM, pltpu.HBM))
    shape = jax.ShapeDtypeStruct
    count = sum(p.shape[0] for _, p in parts)
    return pl.pallas_call(
        functools.partial(place_kernel, [first for first, _ in parts]),
        in_specs=[smem] + [vmem] * len(parts) + [far] * len(made),
        out_specs=[far] * 2,
        out_shape=[shape((16 * 128, width), F32), shape((width, 16 * 128), F32)],
        scratch_shapes=[pltpu.VMEM((count, 128, width), F32), pltpu.VMEM((count, width, 128), F32), pltpu.SemaphoreType.DMA((count,))],
        input_output_aliases={1 + len(parts) + i: i for i in range(len(made))},
        name="place", compiler_params=pltpu.CompilerParams(vmem_limit_bytes=28 << 20),
    )(info, *[p for _, p in parts], *made)

def sort_kernel(firsts, info, *refs):
    parts, made, (tall, sems) = refs[: len(firsts)], refs[-6:-2], refs[-2:]
    size = parts[0].shape[1]
    mine = info[6]
    pieces = []
    for part, first in zip(parts, firsts):
        for i in range(part.shape[0]):
            tall[len(pieces)] = part[i].astype(F32)
            pieces.append(first + i)
    for top in range(4):
        @pl.when((mine >> 3) == top)
        def _(top=top):
            copies = []
            for n, r in enumerate(pieces):
                to = pl.ds(pl.multiple_of(((r ^ mine) & 7) * size, size), size)
                copies.append(pltpu.make_async_copy(tall.at[n], made[top ^ (r >> 3)].at[to, :], sems.at[n]))
                copies[-1].start()
            for copy in copies:
                copy.wait()

def sort(info, parts, made, width):
    smem, vmem, far = (pl.BlockSpec(memory_space=m) for m in (pltpu.SMEM, pltpu.VMEM, pltpu.HBM))
    shape = jax.ShapeDtypeStruct((width, width), F32)
    count = sum(p.shape[0] for _, p in parts)
    return pl.pallas_call(
        functools.partial(sort_kernel, [first for first, _ in parts]),
        in_specs=[smem] + [vmem] * len(parts) + [far] * len(made),
        out_specs=[far] * 4,
        out_shape=[shape] * 4,
        scratch_shapes=[pltpu.VMEM((count,) + parts[0][1].shape[1:], F32), pltpu.SemaphoreType.DMA((count,))],
        input_output_aliases={1 + len(parts) + i: i for i in range(len(made))},
        name="sort", compiler_params=pltpu.CompilerParams(vmem_limit_bytes=12 << 20),
    )(info, *[p for _, p in parts], *made)

def mix_kernel(*refs):
    for k in range(4):
        refs[4 + k][...] = added(*[term[k] for term in refs[:4]])

def mix(terms):
    block = terms[0].shape[1:]
    vmem = pl.BlockSpec(memory_space=pltpu.VMEM)
    return pl.pallas_call(
        mix_kernel, in_specs=[vmem] * 4, out_specs=[vmem] * 4, out_shape=[jax.ShapeDtypeStruct(block, BF16)] * 4, name="mix", compiler_params=pltpu.CompilerParams(vmem_limit_bytes=10 << 20),
    )(*terms)

def exchange(value, bits):
    size = lax.axis_size("dp") * lax.axis_size("blk")
    return lax.ppermute(value, ("dp", "blk"), [(i, i ^ bits) for i in range(size)])

def wait(*values):
    return lax.optimization_barrier(values)

def added(*terms):
    total = terms[0].astype(F32)
    for term in terms[1:]:
        total = total + term.astype(F32)
    return total.astype(BF16)

def local(inputs, w_query, w_key, w_value, w_out, w_in, w_back, norm1_gain, norm2_gain, final_gain, bias_table, bucket_table, prefix_len, pad_len, pooled_grad):
    rows, width = inputs.shape[1:]
    spot, far_off = lax.axis_index("blk"), lax.axis_index("dp")
    doc, core = spot // 2, spot % 2
    block = [doc * 2 + core, doc * 2 + 1 - core, (1 - doc) * 2 + core, (1 - doc) * 2 + 1 - core]
    line = [8, 16]
    further = [32 << b for b in range((lax.axis_size("dp") // 8).bit_length() - 1)]
    piece = core * 16 + doc * 4 + (far_off % 2) * 8 + (far_off // 2) % 4
    near = jnp.where(doc == 0, inputs[0], inputs[1])
    far_send = jnp.where(doc == 0, inputs[1], inputs[0])
    near, far_send = wait(near, far_send)
    far = exchange(far_send, ROW)
    near_other = exchange(near, CORE)
    slot = jnp.arange(8, dtype=jnp.int32)
    ids = jnp.zeros_like(slot)
    for i, value in enumerate([b * rows for b in block] + [piece, core, doc]):
        ids = jnp.where(slot == i, value, ids)
    gain1, gain2, gain3 = norm1_gain[None, :], norm2_gain[None, :], final_gain[None, :]
    buckets = bucket_table[None, :]
    hid_l, q_l, k_l, v_l, w_query, w_key, w_value = prepare(near, near_other, gain1, w_query, w_key, w_value)
    far, q_l, ids = wait(far, q_l, ids)
    far_other = exchange(far, CORE)
    lines, info = tables(ids, pad_len, prefix_len, bias_table.T, buckets, 4 * rows)
    (hid_r, q_r, k_r, v_r, expo, inverse, attended, send, active, slopes, turned, mixed, steep, dense_rows) = front(
        info, far, far_other, near, q_l, k_l, v_l, lines, w_query, w_key, w_value,
        gain1, gain2, gain3, pooled_grad, w_out, w_in, w_back)

    xy = [ROW, NEAR_X, ROW ^ NEAR_X]
    zz = [line[0], line[1], line[0] ^ line[1]]

    token, send = wait(info, send)
    got = exchange(send, CORE)
    kept = stay_half(token, active, slopes, turned, steep)
    token, kept = wait(token, kept)
    grad_inner = inner(token, slopes, w_in)
    token, grad_inner, got = wait(token, grad_inner, got)
    stays, *sends = meet(kept, got)

    token, sends, grad_inner = wait(token, sends, grad_inner)
    came = [exchange(sends[k], xy[k]) for k in (2, 0, 1)]
    grad_mixed, grad_attended, grad_out_w, through_rows = through(token, grad_inner, mixed, steep, w_out, attended, gain2)
    token, through_rows = wait(token, through_rows)
    rest_keep, rest_send, stay, leave, small = back(
        token, q_l, q_r, k_l, k_r, v_l, v_r, grad_attended, attended, inverse, expo, buckets, dense_rows, through_rows,
        hid_l, hid_r, near, near_other, far, far_other, w_query, w_key, w_value, grad_out_w)
    token, small, rest_send, leave, came = wait(token, small, rest_send, leave, came)

    rest_got = exchange(rest_send, CORE)
    hidden_got = exchange(leave, CORE)
    lines = mix([stays] + list(came))
    token, lines = wait(token, lines)
    took = [exchange(lines[k + 1], m) for k, m in enumerate(zz)]
    token, rest_got, hidden_got = wait(token, rest_got, hidden_got)

    count = rest_keep.shape[0] * rest_keep.shape[1]
    small = small + one_value(rest_got[count:])
    rest_got = rest_got[:count].reshape(rest_keep.shape)
    terms = two_terms(small)
    sends = [jnp.concatenate([added(rest_keep[4 * k : 4 * k + 4], rest_got[4 * k : 4 * k + 4]).reshape(-1, width), terms]) for k in (1, 2, 3)]
    token, sends = wait(token, sends)
    rest_came = [exchange(s, m) for s, m in zip(sends, xy)]
    home, away = ending(token, stay, hidden_got, near, far, grad_mixed, gain1, dense_rows)
    token, took, away = wait(token, took, away)

    whole = added(lines[0], *took)
    for bit in further:
        whole = added(whole, exchange(whole, bit))
    token, whole = wait(token, whole)
    back_line = [exchange(whole, m) for m in zz]
    away_got = exchange(away, ROW)
    token, rest_came = wait(token, rest_came)

    count = count // 4
    for part in rest_came:
        small = small + one_value(part[count:])
    rest_came = [part[:count].reshape((4,) + rest_keep.shape[1:]) for part in rest_came]
    piece = count // 4
    lines = added(rest_keep[:4], rest_got[:4], *rest_came).reshape(-1, width)
    send = jnp.concatenate([lines[piece : 2 * piece], lines[3 * piece :], two_terms(small)])
    token, send = wait(token, send)
    took = exchange(send, line[0])
    token, took = wait(token, took)
    small = small + one_value(took[2 * piece :])
    lines = added(jnp.concatenate([lines[:piece], lines[2 * piece : 3 * piece]]), took[: 2 * piece])
    send = jnp.concatenate([lines, two_terms(small)])
    token, send, back_line, away_got = wait(token, send, back_line, away_got)
    took = exchange(send, line[1])

    quarter = jnp.stack([whole] + back_line)
    token, quarter = wait(token, quarter)
    from_y, from_x = exchange(quarter, ROW), exchange(quarter, NEAR_X)
    pool_mine, pool_other = one_value(home[rows:])[:1], one_value(away_got[rows:])[:1]
    pooled = jnp.where(doc == 0, jnp.concatenate([pool_mine, pool_other]), jnp.concatenate([pool_other, pool_mine]))
    home, away_got = home[:rows], away_got[:rows]
    input_grad = jnp.where(doc == 0, jnp.stack([home, away_got]), jnp.stack([away_got, home]))
    token, took, pooled, input_grad = wait(token, took, pooled, input_grad)

    small = small + one_value(took[2 * piece :])
    rest = added(lines, jnp.concatenate([took[piece : 2 * piece], took[:piece]]))
    for bit in further:
        rest = added(rest, exchange(rest, bit))
        small = small + exchange(small, bit)
    token, rest = wait(token, rest)
    rest_back = exchange(rest, line[0])
    outs = [small[0], small[1], small[2], small[3, : bias_table.size].reshape(bias_table.shape[::-1]).T]
    token, from_y, from_x, outs = wait(token, from_y, from_x, outs)

    sends = [from_x[:2], from_y[2:]]
    far_a, far_b = exchange(sends[0], ROW), exchange(sends[1], NEAR_X)
    quarter, from_y, from_x, _ = wait(quarter, from_y, from_x, sends)
    here = jnp.concatenate([quarter, from_y, from_x])
    token, here = wait(token, here)
    other = exchange(here, CORE)
    grads = place(token, [(0, here)], [], width)
    token, grads, rest_back, far_a, far_b, other = wait(token, grads, rest_back, far_a, far_b, other)

    fourth = jnp.stack([rest[:piece], rest_back[:piece], rest[piece:], rest_back[piece:]])
    far_pair = jnp.concatenate([far_a, far_b])
    token, fourth, far_pair = wait(token, fourth, far_pair)
    fourth_y, fourth_x = exchange(fourth, ROW), exchange(fourth, NEAR_X)
    other_far = exchange(far_pair, CORE)
    token, other_far = wait(token, other_far)
    out_back, out_in = place(token, [(12, far_pair), (16, other), (28, other_far)], grads, width)
    token, out_back, out_in, fourth_y, fourth_x = wait(token, out_back, out_in, fourth_y, fourth_x)

    sends = [fourth_x[:2], fourth_y[2:], jnp.concatenate([fourth, fourth_y, fourth_x])]
    token, sends = wait(token, sends)
    last_a, last_b, pair = (exchange(s, m) for s, m in zip(sends, (ROW, NEAR_X, CORE)))
    token, pair = wait(token, pair)
    made = sort(token, [(0, sends[2]), (16, pair)], [], width)
    token, made, last_a, last_b = wait(token, made, last_a, last_b)

    ends = exchange(jnp.concatenate([last_a, last_b]), CORE)
    made = sort(token, [(12, last_a), (14, last_b)], made, width)
    token, made, ends = wait(token, made, ends)
    out_out, out_query, out_key, out_value = sort(token, [(28, ends)], made, width)
    return (pooled, input_grad, out_query, out_key, out_value, out_out, out_in, out_back, *outs)

def solution(mesh):
    data = P("dp", "blk", None)
    placed = (data,) + (P(),) * 11 + (P("dp"), P("dp"), P("dp", None))
    return jax.shard_map(local, mesh=mesh, in_specs=placed, out_specs=(P("dp", None), data) + (P(),) * 10, check_vma=False)
```

```python
import functools
import jax, jax.numpy as jnp
from jax import lax
from jax.experimental import pallas as pl
from jax.experimental.pallas import tpu as pltpu
from jax.sharding import PartitionSpec as P

F32, BF16 = jnp.float32, jnp.bfloat16
NEG = -1000000000.0
NT = (((1,), (1,)), ((), ()))
TN = (((0,), (0,)), ((), ()))
NN = (((1,), (0,)), ((), ()))

def dot(a, b, dims=NN):
    return lax.dot_general(a, b, dims, preferred_element_type=F32)

def skew(row, width, dtype=F32):
    return pltpu.roll(jnp.broadcast_to(row, (128, width)), width - 127, 1, stride=1, stride_axis=0)


BUCKETS = 32
EPS = 1e-06
CORE, ROW, NEAR_X = 1, 2, 4

def rms_scale(values):
    return lax.rsqrt(jnp.mean(values * values, axis=-1, keepdims=True) + EPS)

def norm_back(grad_out, values, scale, gain):
    weighted = grad_out * gain
    inner = jnp.mean(weighted * values, axis=-1, keepdims=True)
    grad_in = scale * weighted - scale * scale * scale * values * inner
    return grad_in, jnp.sum(grad_out * values * scale, axis=0, keepdims=True)

def two_terms(value):
    high = value.astype(BF16)
    return jnp.concatenate([high, (value - high.astype(F32)).astype(BF16)])

def one_value(terms):
    return terms[:8].astype(F32) + terms[8:16].astype(F32)

def rows_of(*values):
    count = sum(v.shape[0] for v in values)
    return jnp.concatenate(list(values) + [jnp.zeros((8 - count, values[0].shape[1]), F32)])

def prepare_kernel(mine, other, gain, wq_h, wk_h, wv_h, hidden, query, keys, values, wq, wk, wv, sems):
    rows = mine.shape[0]
    load = [pltpu.make_async_copy(a, b, sems.at[i]) for i, (a, b) in enumerate(((wk_h, wk), (wv_h, wv), (wq_h, wq)))]
    for copy in load:
        copy.start()
    for part, raw in enumerate((mine, other)):
        tokens = raw[...].astype(F32)
        hidden[part * rows : (part + 1) * rows, :] = (tokens * rms_scale(tokens) * gain[...]).astype(BF16)
    h = hidden[...]
    load[0].wait()
    keys[...] = dot(h, wk[...]).astype(BF16)
    load[1].wait()
    values[...] = dot(h, wv[...]).astype(BF16)
    load[2].wait()
    query[...] = dot(h[:rows], wq[...]).astype(BF16)

def prepare(mine, other, gain, wq, wk, wv):
    rows, width = mine.shape
    shape = lambda n: jax.ShapeDtypeStruct((n, width), BF16)
    vmem, free = (pl.BlockSpec(memory_space=m) for m in (pltpu.VMEM, pl.ANY))
    return pl.pallas_call(
        prepare_kernel,
        in_specs=[vmem] * 3 + [free] * 3,
        out_specs=[vmem] * 7,
        out_shape=[shape(2 * rows), shape(rows), shape(2 * rows), shape(2 * rows)] + [shape(width)] * 3,
        scratch_shapes=[pltpu.SemaphoreType.DMA((3,))],
        name="prepare", compiler_params=pltpu.CompilerParams(vmem_limit_bytes=14 << 20),
    )(mine, other, gain, wq, wk, wv)

def tables_kernel(ids, pads, prefixes, bias, buckets, lines, info, *, length):
    doc = ids[6]
    info[0] = length - jnp.where(doc == 0, pads[0], pads[1])
    info[5] = jnp.where(doc == 0, prefixes[0], prefixes[1])
    for to, at in enumerate((0, 1, 2, 3)):
        info[1 + to] = ids[at]
    for to, at in enumerate((4, 5, 6)):
        info[6 + to] = ids[at]
    picker = jnp.where(lax.broadcasted_iota(jnp.int32, (BUCKETS, 1), 0) == buckets[...], 1.0, 0.0).astype(BF16)
    left, total = bias[...], None
    for _ in range(3):
        part = left.astype(BF16)
        left = left - part.astype(F32)
        made = dot(part, picker)
        total = made if total is None else total + made
    lines[...] = jnp.zeros_like(lines)
    lines[:, : buckets.shape[1]] = total

def tables(ids, pads, prefixes, bias, buckets, length):
    smem, vmem = pl.BlockSpec(memory_space=pltpu.SMEM), pl.BlockSpec(memory_space=pltpu.VMEM)
    return pl.pallas_call(
        functools.partial(tables_kernel, length=length),
        in_specs=[smem] * 3 + [vmem] * 2,
        out_specs=[vmem, smem],
        out_shape=[jax.ShapeDtypeStruct((bias.shape[0], buckets.shape[1] + 1), F32), jax.ShapeDtypeStruct((16,), jnp.int32)],
        name="tables", compiler_params=pltpu.CompilerParams(vmem_limit_bytes=4 << 20),
    )(ids, pads, prefixes, bias, buckets)

def back_pieces(to, active, low, mine):
    @pl.loop(0, active.shape[1] // 512)
    def _(group):
        made = dot(active[:, pl.ds(pl.multiple_of(group * 512, 512), 512)], low, TN).astype(BF16)
        for b in range(4):
            rows = made[b * 128 : (b + 1) * 128]
            to[(4 * group + b) ^ mine] = jnp.concatenate([rows[:, q * 128 : (q + 1) * 128] for q in range(4)])

def in_pieces(to, slopes, turned, mine):
    @pl.loop(0, slopes.shape[1] // 512)
    def _(group):
        made = dot(turned, slopes[:, pl.ds(pl.multiple_of(group * 512, 512), 512)]).astype(BF16)
        for b in range(4):
            to[(4 * group + b) ^ mine] = made[:, b * 128 : (b + 1) * 128]

def front_kernel(info, far, far_other, near, q_l, k_l, v_l, lines, wq, wk, wv, gain1, gain2, gain3, cots, wo_h, win_h, wback_h,
                 hid, qs, ks, vs, expo_o, inv, att, send, active, slopes, turned, mixed, steep, rows,
                 wo, win, wback, expo, scores, skewed, edges, sems):
    count, width = near.shape
    hidden = win.shape[1]
    late = [pltpu.make_async_copy(a, b, sems.at[i]) for i, (a, b) in enumerate(((wo_h, wo), (win_h, win), (wback_h, wback)))]
    kept = lambda g: pltpu.make_async_copy(expo, expo_o.at[pl.ds(2 * g, 2)], sems.at[3])

    for copy in late:
        copy.start()
    for part, raw in enumerate((far, far_other)):
        tokens = raw[...].astype(F32)
        hid[part * count : (part + 1) * count, :] = (tokens * rms_scale(tokens) * gain1[...]).astype(BF16)
    h = hid[...]
    qs[...] = dot(h[:count], wq[...]).astype(BF16)
    ks[...] = dot(h, wk[...]).astype(BF16)
    vs[...] = dot(h, wv[...]).astype(BF16)
    column = lax.broadcasted_iota(jnp.int32, (1, 128), 1)
    for b in range(4):
        place = info[1 + b] + lax.broadcasted_iota(jnp.int32, (count, 1), 0)
        gate = jnp.where(place < info[0], 0.0, NEG)
        for head in range(2):
            edges[head, b * count : (b + 1) * count, :] = jnp.where(column == (64 if head == 0 else 0), gate, 0.0).astype(BF16)
    limit = info[0]

    @pl.loop(0, width // 128)
    def _(step):
        @pl.when(step > 0)
        def _():
            kept(step - 1).wait()

        cols = pl.ds(pl.multiple_of(step * 128, 128), 128)
        lane = lax.broadcasted_iota(jnp.int32, (1, 128), 1)
        first = lane < 64
        starts = [info[1 + b] for b in range(4)]
        keys = [k_l[:count, cols], k_l[count:, cols], ks[:count, cols], ks[count:, cols]]
        values = jnp.concatenate([v_l[:, cols], vs[:, cols]])
        query = jnp.concatenate([q_l[:, cols], qs[:, cols]])
        made = []
        for head in range(2):
            mine = jnp.where(first if head == 0 else lane >= 64, 1.0, 0.0).astype(BF16)
            one = jnp.where(lane == (64 if head == 0 else 0), 1.0, 0.0).astype(BF16)
            q = query * mine + one
            v = values * mine + one
            skewed[head] = skew(lines[pl.ds(2 * step + head, 1), :], lines.shape[1])
            k = jnp.concatenate(keys) * mine + edges[head]
            for half in range(2):
                s = dot(q[half * 256 : (half + 1) * 256], k, NT)
                for r in range(2):
                    for b in range(4):
                        at = starts[b] - starts[2 * half] + 896 - 128 * r
                        part = s[r * 128 : (r + 1) * 128, b * 256 : (b + 1) * 256] + skewed[head, :, pl.ds(pl.multiple_of(at, 128), 256)]
                        scores[head, half * 256 + r * 128 : half * 256 + (r + 1) * 128, b * 256 : (b + 1) * 256] = part
            accs = []
            for r in range(4):
                rs = slice(r * 128, (r + 1) * 128)
                value = scores[head, rs, :]
                top = jnp.max(value, axis=1, keepdims=True)
                e = jnp.exp(value - top).astype(BF16)
                expo[head, rs, :] = e
                accs.append(dot(e, v))
            acc = jnp.concatenate(accs)
            made.append((acc, 1.0 / (acc[:, 64:65] if head == 0 else acc[:, 0:1])))
        (a0, i0), (a1, i1) = made
        scale = jnp.where(first, i0, i1)
        att[:, cols] = (jnp.where(first, a0, a1) * scale).astype(BF16)
        inv[:, cols] = scale
        kept(step).start()

    for copy in late:
        copy.wait()
    for part, raw in enumerate((near, far)):
        spot = slice(part * count, (part + 1) * count)
        mixed[spot, :] = raw[...].astype(F32) + dot(att[spot, :], wo[...])
    values = mixed[...]
    inner = (values * rms_scale(values) * gain2[...]).astype(BF16)
    turned[...] = inner.T
    total = values
    for at in range(0, hidden, 1024):
        lifted = jnp.maximum(dot(inner, win[:, at : at + 1024]), 0.0).astype(BF16)
        active[:, at : at + 1024] = lifted
        total = total + dot(lifted, wback[at : at + 1024, :])
    scale = rms_scale(total)
    place = lax.broadcasted_iota(jnp.int32, (2 * count, 1), 0)
    place = jnp.where(place < count, place + info[1], place + (info[3] - count))
    live = jnp.where((place >= info[5]) & (place < limit), 1.0, 0.0)
    pool = jnp.sum(total * scale * gain3[...] * live, axis=0, keepdims=True)
    cot = jnp.where(info[8] == 0, cots[0:1, :], cots[1:2, :]) / (limit - info[5]).astype(F32)
    slope, grad_end = norm_back(live * cot, total, scale, gain3[...])
    steep[...] = slope
    rows[...] = jnp.concatenate([pool, grad_end, jnp.zeros((6, width), F32)])
    low = slope.astype(BF16)
    for at in range(0, hidden, 1024):
        through = dot(low, wback[at : at + 1024, :], NT).astype(BF16)
        slopes[:, at : at + 1024] = jnp.where(active[:, at : at + 1024] > 0, through, jnp.zeros_like(through))
    mine = info[6] & 15

    @pl.when(info[7] == 0)
    def _():
        in_pieces(send, slopes, turned[...], mine)

    @pl.when(info[7] == 1)
    def _():
        back_pieces(send, active, steep[...].astype(BF16), mine)

    kept(3).wait()


def front(info, far, far_other, near, q_l, k_l, v_l, lines, wq, wk, wv, gain1, gain2, gain3, cots, wo, win, wback):
    count, width = near.shape
    hidden = win.shape[1]
    heads, span = lines.shape
    shape = jax.ShapeDtypeStruct
    smem, vmem, free = (pl.BlockSpec(memory_space=m) for m in (pltpu.SMEM, pltpu.VMEM, pl.ANY))
    outs = [shape((2 * count, width), BF16), shape((count, width), BF16), shape((2 * count, width), BF16), shape((2 * count, width), BF16),
            shape((heads, 2 * count, 4 * count), BF16), shape((2 * count, width), F32), shape((2 * count, width), BF16),
            shape((16, width, 128), BF16), shape((2 * count, hidden), BF16), shape((2 * count, hidden), BF16),
            shape((width, 2 * count), BF16), shape((2 * count, width), F32), shape((2 * count, width), F32)]
    return pl.pallas_call(
        front_kernel,
        in_specs=[smem] + [vmem] * 14 + [free] * 3,
        out_specs=[vmem] * 4 + [free] + [vmem] * 9,
        out_shape=outs + [shape((8, width), F32)],
        scratch_shapes=[pltpu.VMEM(wo.shape, BF16), pltpu.VMEM(win.shape, BF16), pltpu.VMEM(wback.shape, BF16),
                        pltpu.VMEM((2, 2 * count, 4 * count), BF16), pltpu.VMEM((2, 2 * count, 4 * count), F32),
                        pltpu.VMEM((2, 128, span), F32), pltpu.VMEM((2, 4 * count, 128), BF16), pltpu.SemaphoreType.DMA((4,))],
        name="front", compiler_params=pltpu.CompilerParams(vmem_limit_bytes=38 << 20),
    )(info, far, far_other, near, q_l, k_l, v_l, lines, wq, wk, wv, gain1, gain2, gain3, cots, wo, win, wback)

def inner_kernel(info, slopes, win, grad_inner):
    total = None
    for at in range(0, slopes.shape[1], 512):
        part = dot(slopes[:, at : at + 512], win[:, at : at + 512], NT)
        total = part if total is None else total + part
    grad_inner[...] = total

def inner(info, slopes, win):
    smem, vmem = pl.BlockSpec(memory_space=pltpu.SMEM), pl.BlockSpec(memory_space=pltpu.VMEM)
    return pl.pallas_call(
        inner_kernel, in_specs=[smem, vmem, vmem], out_specs=vmem,
        out_shape=jax.ShapeDtypeStruct((slopes.shape[0], win.shape[0]), F32), name="inner", compiler_params=pltpu.CompilerParams(vmem_limit_bytes=10 << 20),
    )(info, slopes, win)

def through_kernel(info, grad_inner, mixed, steep, wo, att, gain2, grad_mixed, grad_attended, grad_out, rows):
    values = mixed[...]
    more, grad_two = norm_back(grad_inner[...], values, rms_scale(values), gain2[...])
    total = steep[...] + more
    grad_mixed[...] = total
    low = total.astype(BF16)
    grad_attended[...] = dot(low, wo[...], NT).astype(BF16)
    grad_out[...] = dot(att[...], low, TN).astype(BF16)
    rows[...] = jnp.concatenate([grad_two, jnp.zeros((7, low.shape[1]), F32)])

def through(info, grad_inner, mixed, steep, wo, att, gain2):
    n, width = mixed.shape
    smem, vmem = pl.BlockSpec(memory_space=pltpu.SMEM), pl.BlockSpec(memory_space=pltpu.VMEM)
    shape = jax.ShapeDtypeStruct
    return pl.pallas_call(
        through_kernel,
        in_specs=[smem] + [vmem] * 6,
        out_specs=[vmem] * 4,
        out_shape=[shape((n, width), F32), shape((n, width), BF16), shape((width, width), BF16), shape((8, width), F32)],
        name="through", compiler_params=pltpu.CompilerParams(vmem_limit_bytes=16 << 20),
    )(info, grad_inner, mixed, steep, wo, att, gain2)

def stay_kernel(info, active, slopes, turned, steep, blocks):
    high, lowest = (info[6] & 15) >> 2, info[6] & 3
    for side in range(2):
        @pl.when(info[7] == side)
        def _(side=side):
            low = steep[...].astype(BF16) if side == 0 else turned[...]
            for k in range(4):
                at = pl.ds(pl.multiple_of((k ^ high) * 512, 512), 512)
                made = dot(active[:, at], low, TN) if side == 0 else dot(low, slopes[:, at])
                for b in range(4):
                    piece = made[:, b * 128 : (b + 1) * 128]
                    if side == 0:
                        piece = made[b * 128 : (b + 1) * 128]
                        piece = jnp.concatenate([piece[:, q * 128 : (q + 1) * 128] for q in range(4)])
                    blocks[k, b ^ lowest] = piece.astype(BF16)

def stay_half(info, active, slopes, turned, steep):
    smem, vmem = pl.BlockSpec(memory_space=pltpu.SMEM), pl.BlockSpec(memory_space=pltpu.VMEM)
    width = steep.shape[1]
    return pl.pallas_call(
        stay_kernel, in_specs=[smem] + [vmem] * 4, out_specs=vmem,
        out_shape=jax.ShapeDtypeStruct((4, 4, width, 128), BF16), name="stay", compiler_params=pltpu.CompilerParams(vmem_limit_bytes=12 << 20),
    )(info, active, slopes, turned, steep)

def meet_kernel(kept, got, *outs):
    for k in (3, 1, 2, 0):
        outs[k][...] = added(kept[k], got[4 * k : 4 * k + 4])

def meet(kept, got):
    vmem = pl.BlockSpec(memory_space=pltpu.VMEM)
    return pl.pallas_call(
        meet_kernel, in_specs=[vmem] * 2, out_specs=[vmem] * 4, out_shape=[jax.ShapeDtypeStruct(kept.shape[1:], BF16)] * 4, name="meet", compiler_params=pltpu.CompilerParams(vmem_limit_bytes=20 << 20),
    )(kept, got)

CLASS = {(0, 0): 0, (1, 2): 0, (0, 1): 1, (1, 3): 1, (0, 2): 2, (0, 3): 3, (1, 0): 4, (1, 1): 5}

def back_kernel(info, ql, qr, kl, kr, vl, vr, gout, out, inv, expo, buckets, dense_rows, through_rows,
                hid_l_h, hid_r_h, near_h, near_other_h, far_h, far_other_h, wq_h, wk_h, wv_h, grad_out_h,
                keep_o, send_o, stay_o, leave_o, small,
                hid_l, hid_r, near, near_other, far, far_other, wq, wk, wv, made,
                keep, send, stay, leave, dq, dk, dv, offsets, sums, acc, slopes, sems):
    count, width = near.shape
    step = pl.program_id(0)
    pairs = width // 128
    late = [pltpu.make_async_copy(a, b, sems.at[i]) for i, (a, b) in enumerate((
        (hid_l_h, hid_l), (hid_r_h, hid_r), (near_h, near), (near_other_h, near_other), (far_h, far), (far_other_h, far_other),
        (wq_h, wq), (wk_h, wk), (wv_h, wv), (grad_out_h, made.at[0:width])))]
    done = [pltpu.make_async_copy(a, b, sems.at[10 + i]) for i, (a, b) in enumerate(((send, send_o), (keep, keep_o), (leave, leave_o), (stay, stay_o)))]

    @pl.when(step == 0)
    def _():
        for copy in late:
            copy.start()

    cols = pl.ds(pl.multiple_of(step * 128, 128), 128)
    lane = lax.broadcasted_iota(jnp.int32, (1, 128), 1)
    starts = [info[1 + b] for b in range(4)]
    keys = jnp.concatenate([kl[...], kr[...]])
    values = jnp.concatenate([vl[...], vr[...]])
    query = jnp.concatenate([ql[...], qr[...]])
    scaled = gout[...].astype(F32) * inv[...]
    prod = scaled * out[...].astype(F32)
    low = scaled.astype(BF16)
    query_t, low_t = query.T, low.T
    grads_q, grads_k, grads_v = None, [], []
    for head in range(2):
        mine = (lane < 64) if head == 0 else (lane >= 64)
        base = 64 if head == 0 else 0
        pick = jnp.where(mine, 1.0, 0.0).astype(BF16)
        delta = jnp.sum(jnp.where(mine, prod, 0.0), axis=1, keepdims=True)
        high = delta.astype(BF16).astype(F32)
        extra = jnp.where(lane == base, high, jnp.where(lane == base + 1, delta - high, 0.0)).astype(BF16)
        grad = low * pick + extra
        minus = jnp.where((lane == base) | (lane == base + 1), -1.0, 0.0).astype(BF16)
        for b in range(4):
            spot = slice(b * count, (b + 1) * count)
            ds = dot(grad, values[spot] * pick + minus, NT) * expo[head, :, spot].astype(F32)
            slopes[head, :, spot] = ds.astype(BF16)
            for chunk in range(2):
                upper, lower = (ds[chunk * count + r * 128 : chunk * count + (r + 1) * 128] for r in range(2))
                group = CLASS[chunk, b]
                block = jnp.concatenate([lower[:, :128], lower[:, 128:] + upper[:, :128], upper[:, 128:]], axis=1)
                if (chunk, b) in ((1, 2), (1, 3)):
                    block = block + sums[head, group]
                sums[head, group] = block
        part = dot(slopes[head], keys * pick)
        grads_q = part if grads_q is None else grads_q + part
        half = slice(head * 64, (head + 1) * 64)
        grads_k.append(dot(query_t[half], slopes[head]))
        grads_v.append(dot(low_t[half], expo[head]))
    dq[:, cols] = grads_q.astype(BF16)
    dk[:, cols] = jnp.concatenate(grads_k).astype(BF16).T
    dv[:, cols] = jnp.concatenate(grads_v).astype(BF16).T
    for head in range(2):
        acc[head] = jnp.zeros(acc.shape[1:], F32)
        for (chunk, b), group in CLASS.items():
            if (chunk, b) not in ((1, 2), (1, 3)):
                at = starts[b] - starts[2 * chunk] + 768
                to = pl.ds(pl.multiple_of(at, 128), 384)
                acc[head, :, to] += sums[head, group]
        rest = acc[head]
        n = 64
        while n >= 8:
            rest = rest[:n] + pltpu.roll(rest[n:], 2048 - n, 1)
            n //= 2
        line = rest[7:8]
        for r in range(6, -1, -1):
            line = rest[r : r + 1] + pltpu.roll(line, 2047, 1)
        offsets[pl.ds(2 * step + head, 1), :] = pltpu.roll(line, 127, 1)

    @pl.when(step == pairs - 1)
    def _():
        for copy in late:
            copy.wait()
        made[width : 2 * width, :] = (dot(hid_l[:count, :], dq[:count, :], TN) + dot(hid_r[:count, :], dq[count:, :], TN)).astype(BF16)
        for at, grads in ((2 * width, dk), (3 * width, dv)):
            made[at : at + width, :] = (dot(hid_l[...], grads[: 2 * count, :], TN) + dot(hid_r[...], grads[2 * count :, :], TN)).astype(BF16)
        me = info[6]
        size = made.shape[0] // 32

        @pl.loop(0, 16)
        def _(r):
            keep[r] = made[pl.ds(pl.multiple_of((r ^ me) * size, size), size), :]
            send[pl.ds(pl.multiple_of(r * size, size), size), :] = made[pl.ds(pl.multiple_of(((r + 16) ^ me) * size, size), size), :]

        gain = jnp.zeros((1, width), F32)
        for b, raw in enumerate((near, near_other, far, far_other)):
            spot = slice(b * count, (b + 1) * count)
            grad = dot(dk[spot, :], wk[...], NT) + dot(dv[spot, :], wv[...], NT)
            half = slice((b // 2) * count, (b // 2 + 1) * count)
            if b % 2 == 0:
                grad = grad + dot(dq[half, :], wq[...], NT)
                stay[half, :] = grad
            else:
                leave[half, :] = grad.astype(BF16)
            tokens = raw[...].astype(F32)
            gain = gain + jnp.sum(grad * (tokens * rms_scale(tokens)), axis=0, keepdims=True)
        leave[2 * count :, :] = two_terms(rows_of(dense_rows[0:1, :]))
        picker = jnp.where(lax.broadcasted_iota(jnp.int32, (128, 1), 0) == buckets[...], 1.0, 0.0).astype(BF16)
        left = offsets[...][:, : buckets.shape[1]]
        bias = None
        for _ in range(3):
            part = left.astype(BF16)
            left = left - part.astype(F32)
            bias = dot(part, picker, NT) if bias is None else bias + dot(part, picker, NT)
        bias = jnp.concatenate([bias, jnp.zeros((bias.shape[0], width - 128), F32)], axis=1)
        line = bias[0:1]
        for h in range(1, bias.shape[0]):
            line = line + pltpu.roll(bias[h : h + 1], 32 * h, 1)
        total = rows_of(gain, through_rows[0:1, :], dense_rows[1:2, :], line)
        small[...] = total
        send[16 * size :, :] = two_terms(total)
        for copy in done:
            copy.start()
        for copy in done:
            copy.wait()

def back(info, ql, qr, kl, kr, vl, vr, gout, out, inv, expo, buckets, dense_rows, through_rows,
         hid_l, hid_r, near, near_other, far, far_other, wq, wk, wv, grad_out):
    count, width = near.shape
    smem, free = pl.BlockSpec(memory_space=pltpu.SMEM), pl.BlockSpec(memory_space=pl.ANY)
    whole = lambda *dims: pl.BlockSpec(dims, lambda g: (0,) * len(dims))
    col = lambda n: pl.BlockSpec((n, 128), lambda g: (0, g))
    shape = jax.ShapeDtypeStruct
    size = 4 * width // 32
    outs = [shape((16, size, width), BF16), shape((16 * size + 16, width), BF16), shape((2 * count, width), F32), shape((2 * count + 16, width), BF16)]
    given = (hid_l, hid_r, near, near_other, far, far_other, wq, wk, wv)
    return pl.pallas_call(
        back_kernel,
        grid=(width // 128,),
        in_specs=[smem, col(count), col(count)] + [col(2 * count)] * 7 + [pl.BlockSpec((2, 2 * count, 4 * count), lambda g: (g, 0, 0)),
                  whole(*buckets.shape), whole(8, width), whole(8, width)] + [free] * 10,
        out_specs=[free] * 4 + [whole(8, width)],
        out_shape=outs + [shape((8, width), F32)],
        scratch_shapes=[pltpu.VMEM(g.shape, BF16) for g in given] + [pltpu.VMEM((4 * width, width), BF16)]
                       + [pltpu.VMEM(o.shape, o.dtype) for o in outs]
                       + [pltpu.VMEM((2 * count, width), BF16), pltpu.VMEM((4 * count, width), BF16), pltpu.VMEM((4 * count, width), BF16),
                          pltpu.VMEM((8, 2048), F32), pltpu.VMEM((2, 6, 128, 384), F32), pltpu.VMEM((2, 128, 2048), F32),
                          pltpu.VMEM((2, 2 * count, 4 * count), BF16), pltpu.SemaphoreType.DMA((14,))],
        name="back", compiler_params=pltpu.CompilerParams(vmem_limit_bytes=40 << 20),
    )(info, ql, qr, kl, kr, vl, vr, gout, out, inv, expo, buckets, dense_rows, through_rows, *given, grad_out)

def ending_kernel(info, stay, came, near, far, grad_mixed, gain, dense_rows, home, away):
    count, width = near.shape
    for part, raw in enumerate((near, far)):
        spot = slice(part * count, (part + 1) * count)
        tokens = raw[...].astype(F32)
        grad = stay[spot, :] + came[spot, :].astype(F32)
        more, _ = norm_back(grad, tokens, rms_scale(tokens), gain[...])
        value = (grad_mixed[spot, :] + more).astype(BF16)
        if part == 0:
            home[:count, :] = value
        else:
            away[:count, :] = value
    alive = (info[0] - info[5]).astype(F32)
    pool = two_terms((rows_of(dense_rows[0:1, :]) + one_value(came[2 * count :, :])) / alive)
    home[count:, :] = pool
    away[count:, :] = pool

def ending(info, stay, came, near, far, grad_mixed, gain, dense_rows):
    count, width = near.shape
    smem, vmem = pl.BlockSpec(memory_space=pltpu.SMEM), pl.BlockSpec(memory_space=pltpu.VMEM)
    shape = jax.ShapeDtypeStruct((count + 16, width), BF16)
    return pl.pallas_call(
        ending_kernel, in_specs=[smem] + [vmem] * 7, out_specs=[vmem] * 2, out_shape=[shape, shape], name="ending", compiler_params=pltpu.CompilerParams(vmem_limit_bytes=10 << 20)
    )(info, stay, came, near, far, grad_mixed, gain, dense_rows)

def place_kernel(firsts, info, *refs):
    parts, (back, front, rows, columns, sems) = refs[: len(firsts)], refs[-5:]
    mine = info[6] & 15
    for side in range(2):
        @pl.when(info[7] == side)
        def _(side=side):
            copies, n = [], 0
            for part, first in zip(parts, firsts):
                for i in range(part.shape[0]):
                    r = first + i
                    to = pl.ds(pl.multiple_of(((r & 15) ^ mine) * 128, 128), 128)
                    if (r >= 16) == (side == 1):
                        for q in range(4):
                            rows[n, :, q * 128 : (q + 1) * 128] = part[i, q * 128 : (q + 1) * 128, :].astype(F32)
                        copies.append(pltpu.make_async_copy(rows.at[n], back.at[to, :], sems.at[n]))
                    else:
                        columns[n] = part[i].astype(F32)
                        copies.append(pltpu.make_async_copy(columns.at[n], front.at[:, to], sems.at[n]))
                    copies[-1].start()
                    n += 1
            for copy in copies:
                copy.wait()

def place(info, parts, made, width):
    smem, vmem, far = (pl.BlockSpec(memory_space=m) for m in (pltpu.SMEM, pltpu.VMEM, pltpu.HBM))
    shape = jax.ShapeDtypeStruct
    count = sum(p.shape[0] for _, p in parts)
    return pl.pallas_call(
        functools.partial(place_kernel, [first for first, _ in parts]),
        in_specs=[smem] + [vmem] * len(parts) + [far] * len(made),
        out_specs=[far] * 2,
        out_shape=[shape((16 * 128, width), F32), shape((width, 16 * 128), F32)],
        scratch_shapes=[pltpu.VMEM((count, 128, width), F32), pltpu.VMEM((count, width, 128), F32), pltpu.SemaphoreType.DMA((count,))],
        input_output_aliases={1 + len(parts) + i: i for i in range(len(made))},
        name="place", compiler_params=pltpu.CompilerParams(vmem_limit_bytes=28 << 20),
    )(info, *[p for _, p in parts], *made)

def sort_kernel(firsts, info, *refs):
    parts, made, (tall, sems) = refs[: len(firsts)], refs[-6:-2], refs[-2:]
    size = parts[0].shape[1]
    mine = info[6]
    pieces = []
    for part, first in zip(parts, firsts):
        for i in range(part.shape[0]):
            tall[len(pieces)] = part[i].astype(F32)
            pieces.append(first + i)
    for top in range(4):
        @pl.when((mine >> 3) == top)
        def _(top=top):
            copies = []
            for n, r in enumerate(pieces):
                to = pl.ds(pl.multiple_of(((r ^ mine) & 7) * size, size), size)
                copies.append(pltpu.make_async_copy(tall.at[n], made[top ^ (r >> 3)].at[to, :], sems.at[n]))
                copies[-1].start()
            for copy in copies:
                copy.wait()

def sort(info, parts, made, width):
    smem, vmem, far = (pl.BlockSpec(memory_space=m) for m in (pltpu.SMEM, pltpu.VMEM, pltpu.HBM))
    shape = jax.ShapeDtypeStruct((width, width), F32)
    count = sum(p.shape[0] for _, p in parts)
    return pl.pallas_call(
        functools.partial(sort_kernel, [first for first, _ in parts]),
        in_specs=[smem] + [vmem] * len(parts) + [far] * len(made),
        out_specs=[far] * 4,
        out_shape=[shape] * 4,
        scratch_shapes=[pltpu.VMEM((count,) + parts[0][1].shape[1:], F32), pltpu.SemaphoreType.DMA((count,))],
        input_output_aliases={1 + len(parts) + i: i for i in range(len(made))},
        name="sort", compiler_params=pltpu.CompilerParams(vmem_limit_bytes=12 << 20),
    )(info, *[p for _, p in parts], *made)

def mix_kernel(*refs):
    for k in range(4):
        refs[4 + k][...] = added(*[term[k] for term in refs[:4]])

def mix(terms):
    block = terms[0].shape[1:]
    vmem = pl.BlockSpec(memory_space=pltpu.VMEM)
    return pl.pallas_call(
        mix_kernel, in_specs=[vmem] * 4, out_specs=[vmem] * 4, out_shape=[jax.ShapeDtypeStruct(block, BF16)] * 4, name="mix", compiler_params=pltpu.CompilerParams(vmem_limit_bytes=10 << 20),
    )(*terms)

def exchange(value, bits):
    size = lax.axis_size("dp") * lax.axis_size("blk")
    return lax.ppermute(value, ("dp", "blk"), [(i, i ^ bits) for i in range(size)])

def wait(*values):
    return lax.optimization_barrier(values)

def added(*terms):
    total = terms[0].astype(F32)
    for term in terms[1:]:
        total = total + term.astype(F32)
    return total.astype(BF16)

def local(inputs, w_query, w_key, w_value, w_out, w_in, w_back, norm1_gain, norm2_gain, final_gain, bias_table, bucket_table, prefix_len, pad_len, pooled_grad):
    rows, width = inputs.shape[1:]
    spot, far_off = lax.axis_index("blk"), lax.axis_index("dp")
    doc, core = spot // 2, spot % 2
    block = [doc * 2 + core, doc * 2 + 1 - core, (1 - doc) * 2 + core, (1 - doc) * 2 + 1 - core]
    line = [8, 16]
    further = [32 << b for b in range((lax.axis_size("dp") // 8).bit_length() - 1)]
    piece = core * 16 + doc * 4 + (far_off % 2) * 8 + (far_off // 2) % 4
    near = jnp.where(doc == 0, inputs[0], inputs[1])
    far_send = jnp.where(doc == 0, inputs[1], inputs[0])
    near, far_send = wait(near, far_send)
    far = exchange(far_send, ROW)
    near_other = exchange(near, CORE)
    slot = jnp.arange(8, dtype=jnp.int32)
    ids = jnp.zeros_like(slot)
    for i, value in enumerate([b * rows for b in block] + [piece, core, doc]):
        ids = jnp.where(slot == i, value, ids)
    gain1, gain2, gain3 = norm1_gain[None, :], norm2_gain[None, :], final_gain[None, :]
    buckets = bucket_table[None, :]
    hid_l, q_l, k_l, v_l, w_query, w_key, w_value = prepare(near, near_other, gain1, w_query, w_key, w_value)
    far, q_l, ids = wait(far, q_l, ids)
    far_other = exchange(far, CORE)
    lines, info = tables(ids, pad_len, prefix_len, bias_table.T, buckets, 4 * rows)
    (hid_r, q_r, k_r, v_r, expo, inverse, attended, send, active, slopes, turned, mixed, steep, dense_rows) = front(
        info, far, far_other, near, q_l, k_l, v_l, lines, w_query, w_key, w_value,
        gain1, gain2, gain3, pooled_grad, w_out, w_in, w_back)

    xy = [ROW, NEAR_X, ROW ^ NEAR_X]
    zz = [line[0], line[1], line[0] ^ line[1]]

    token, send = wait(info, send)
    got = exchange(send, CORE)
    kept = stay_half(token, active, slopes, turned, steep)
    token, kept = wait(token, kept)
    grad_inner = inner(token, slopes, w_in)
    token, grad_inner, got = wait(token, grad_inner, got)
    stays, *sends = meet(kept, got)

    token, sends, grad_inner = wait(token, sends, grad_inner)
    came = [exchange(sends[k], xy[k]) for k in (2, 0, 1)]
    grad_mixed, grad_attended, grad_out_w, through_rows = through(token, grad_inner, mixed, steep, w_out, attended, gain2)
    token, through_rows = wait(token, through_rows)
    rest_keep, rest_send, stay, leave, small = back(
        token, q_l, q_r, k_l, k_r, v_l, v_r, grad_attended, attended, inverse, expo, buckets, dense_rows, through_rows,
        hid_l, hid_r, near, near_other, far, far_other, w_query, w_key, w_value, grad_out_w)
    token, small, rest_send, leave, came = wait(token, small, rest_send, leave, came)

    rest_got = exchange(rest_send, CORE)
    hidden_got = exchange(leave, CORE)
    lines = mix([stays] + list(came))
    token, lines = wait(token, lines)
    took = [exchange(lines[k + 1], m) for k, m in enumerate(zz)]
    token, rest_got, hidden_got = wait(token, rest_got, hidden_got)

    count = rest_keep.shape[0] * rest_keep.shape[1]
    small = small + one_value(rest_got[count:])
    rest_got = rest_got[:count].reshape(rest_keep.shape)
    terms = two_terms(small)
    sends = [jnp.concatenate([added(rest_keep[4 * k : 4 * k + 4], rest_got[4 * k : 4 * k + 4]).reshape(-1, width), terms]) for k in (1, 2, 3)]
    token, sends = wait(token, sends)
    rest_came = [exchange(s, m) for s, m in zip(sends, xy)]
    home, away = ending(token, stay, hidden_got, near, far, grad_mixed, gain1, dense_rows)
    token, took, away = wait(token, took, away)

    whole = added(lines[0], *took)
    for bit in further:
        whole = added(whole, exchange(whole, bit))
    token, whole = wait(token, whole)
    back_line = [exchange(whole, m) for m in zz]
    away_got = exchange(away, ROW)
    token, rest_came = wait(token, rest_came)

    count = count // 4
    for part in rest_came:
        small = small + one_value(part[count:])
    rest_came = [part[:count].reshape((4,) + rest_keep.shape[1:]) for part in rest_came]
    piece = count // 4
    lines = added(rest_keep[:4], rest_got[:4], *rest_came).reshape(-1, width)
    send = jnp.concatenate([lines[piece : 2 * piece], lines[3 * piece :], two_terms(small)])
    token, send = wait(token, send)
    took = exchange(send, line[0])
    token, took = wait(token, took)
    small = small + one_value(took[2 * piece :])
    lines = added(jnp.concatenate([lines[:piece], lines[2 * piece : 3 * piece]]), took[: 2 * piece])
    send = jnp.concatenate([lines, two_terms(small)])
    token, send, back_line, away_got = wait(token, send, back_line, away_got)
    took = exchange(send, line[1])

    quarter = jnp.stack([whole] + back_line)
    token, quarter = wait(token, quarter)
    from_y, from_x = exchange(quarter, ROW), exchange(quarter, NEAR_X)
    pool_mine, pool_other = one_value(home[rows:])[:1], one_value(away_got[rows:])[:1]
    pooled = jnp.where(doc == 0, jnp.concatenate([pool_mine, pool_other]), jnp.concatenate([pool_other, pool_mine]))
    home, away_got = home[:rows], away_got[:rows]
    input_grad = jnp.where(doc == 0, jnp.stack([home, away_got]), jnp.stack([away_got, home]))
    token, took, pooled, input_grad = wait(token, took, pooled, input_grad)

    small = small + one_value(took[2 * piece :])
    rest = added(lines, jnp.concatenate([took[piece : 2 * piece], took[:piece]]))
    for bit in further:
        rest = added(rest, exchange(rest, bit))
        small = small + exchange(small, bit)
    token, rest = wait(token, rest)
    rest_back = exchange(rest, line[0])
    outs = [small[0], small[1], small[2], small[3, : bias_table.size].reshape(bias_table.shape[::-1]).T]
    token, from_y, from_x, outs = wait(token, from_y, from_x, outs)

    sends = [from_x[:2], from_y[2:]]
    far_a, far_b = exchange(sends[0], ROW), exchange(sends[1], NEAR_X)
    quarter, from_y, from_x, _ = wait(quarter, from_y, from_x, sends)
    here = jnp.concatenate([quarter, from_y, from_x])
    token, here = wait(token, here)
    other = exchange(here, CORE)
    grads = place(token, [(0, here)], [], width)
    token, grads, rest_back, far_a, far_b, other = wait(token, grads, rest_back, far_a, far_b, other)

    fourth = jnp.stack([rest[:piece], rest_back[:piece], rest[piece:], rest_back[piece:]])
    far_pair = jnp.concatenate([far_a, far_b])
    token, fourth, far_pair = wait(token, fourth, far_pair)
    fourth_y, fourth_x = exchange(fourth, ROW), exchange(fourth, NEAR_X)
    other_far = exchange(far_pair, CORE)
    token, other_far = wait(token, other_far)
    out_back, out_in = place(token, [(12, far_pair), (16, other), (28, other_far)], grads, width)
    token, out_back, out_in, fourth_y, fourth_x = wait(token, out_back, out_in, fourth_y, fourth_x)

    sends = [fourth_x[:2], fourth_y[2:], jnp.concatenate([fourth, fourth_y, fourth_x])]
    token, sends = wait(token, sends)
    last_a, last_b, pair = (exchange(s, m) for s, m in zip(sends, (ROW, NEAR_X, CORE)))
    token, pair = wait(token, pair)
    made = sort(token, [(0, sends[2]), (16, pair)], [], width)
    token, made, last_a, last_b = wait(token, made, last_a, last_b)

    ends = exchange(jnp.concatenate([last_a, last_b]), CORE)
    made = sort(token, [(12, last_a), (14, last_b)], made, width)
    token, made, ends = wait(token, made, ends)
    out_out, out_query, out_key, out_value = sort(token, [(28, ends)], made, width)
    return (pooled, input_grad, out_query, out_key, out_value, out_out, out_in, out_back, *outs)

def solution(mesh):
    data = P("dp", "blk", None)
    placed = (data,) + (P(),) * 11 + (P("dp"), P("dp"), P("dp", None))
    return jax.shard_map(local, mesh=mesh, in_specs=placed, out_specs=(P("dp", None), data) + (P(),) * 10, check_vma=False)
```
